32 devices in a mesh: section: 2 (over core), ctx: 4 (over z), fsdp: 4 (over y, x).
Axes of the slice: x: 2, y: 2, z: 4, core: 2. Of those that a mesh axis runs over, the one named last changes fastest.
Arguments:
- inputs: bfloat16 [8, 1024, 1024], P('fsdp', 'ctx'), may hold values from -6 to 6
- cotangent: bfloat16 [8, 1024, 1024], P('fsdp', 'ctx'), may hold values from -6 to 6
- lengths: int32 [8], replicated, may hold values from 512 to 1024, as said below
- norm_gains: float32 [4, 1024], replicated, may hold values from 0.5 to 1.5
- conv_in: bfloat16 [1024, 3072], P('fsdp'), may hold values from -0.1875 to 0.1875
- conv_kernel: float32 [3, 1024], replicated, may hold values from -3.5 to 3.5
- conv_out: bfloat16 [1024, 1024], P('fsdp'), may hold values from -0.1875 to 0.1875
- attn_q: bfloat16 [1024, 1024], P('fsdp'), may hold values from -0.1875 to 0.1875
- attn_k: bfloat16 [1024, 512], P('fsdp'), may hold values from -0.1875 to 0.1875
- attn_v: bfloat16 [1024, 512], P('fsdp'), may hold values from -0.1875 to 0.1875
- attn_out: bfloat16 [1024, 1024], P('fsdp'), may hold values from -6 to 6
- head_gains: float32 [2, 64], replicated, may hold values from 0.5 to 1.5
- ffn_gate: bfloat16 [2, 1024, 4608], P('section', 'fsdp'), may hold values from -0.1875 to 0.1875
- ffn_up: bfloat16 [2, 1024, 4608], P('section', 'fsdp'), may hold values from -0.1875 to 0.1875
- ffn_down: bfloat16 [2, 4608, 1024], P('section', 'fsdp'), may hold values from -0.09375 to 0.09375
Outputs:
- ends: bfloat16 [2, 8, 1024, 1024], P('section', 'fsdp', 'ctx')
- grad_norm_gains: float32 [3, 1024], P(None, 'fsdp')
- grad_ffn_norm: float32 [1024], P('fsdp')
- grad_conv_in: float32 [1024, 3072], P('fsdp')
- grad_conv_kernel: float32 [3, 1024], P(None, 'fsdp')
- grad_conv_out: float32 [1024, 1024], P('fsdp')
- grad_attn_q: float32 [1024, 1024], P('fsdp')
- grad_attn_k: float32 [1024, 512], P('fsdp')
- grad_attn_v: float32 [1024, 512], P('fsdp')
- grad_attn_out: float32 [1024, 1024], P('fsdp')
- grad_head_gains: float32 [2, 64], P(None, 'fsdp')
- grad_ffn_gate: float32 [2, 1024, 4608], P('section', 'fsdp')
- grad_ffn_up: float32 [2, 1024, 4608], P('section', 'fsdp')
- grad_ffn_down: float32 [2, 4608, 1024], P('section', 'fsdp')
- rms: float32 [8], P('fsdp')
The draws below stay inside these ranges and needn't reach their ends.
Inputs may be any that keep to these rules, and one draw needn't show every extreme that they name: `lengths`: in each group of 2 consecutive sequences (those of one index of fsdp) one sequence has length 1024.
All inputs are finite; a program needn't handle non-finite values.
Results may differ from the reference program's by a relative error of at most 0.025.
Values may be sent and summed in bfloat16 or wider, within the bound.
A program may use at most 576 MiB of HBM per device.

```python
import math
import jax
import jax.numpy as jnp
from jax import lax

D = 1024
FF = 4608
HEADS = 16
KV_HEADS = 8
HEAD = 64
MICRO = 2
SEQ = 1024
SEQS = 8


def draw_lengths(key, part):
    first_key, second_key = jax.random.split(key)
    base = jax.random.randint(first_key, (SEQS,), SEQ // 2, SEQ + 1)
    chosen = jax.random.randint(second_key, (SEQS // MICRO,), 0, MICRO)
    member = jnp.arange(SEQS) % MICRO
    group_of = jnp.arange(SEQS) // MICRO
    longest = member == chosen[group_of]
    return jnp.where(longest, SEQ, base).astype(jnp.int32)


def steps_of(rng, extent, cuts, smallest, largest):
    gain, own = 1.0, jax.random.fold_in(rng, 6)
    for dim, shards_of in cuts:
        draws = jnp.exp(jax.random.uniform(jax.random.fold_in(own, dim), (shards_of,), jnp.float32, smallest / len(cuts), largest / len(cuts)))
        gain = gain * jnp.repeat(draws, extent[dim] // shards_of).reshape([-1 if axis == dim else 1 for axis in range(len(extent))])
    return gain


def gaussian(key, dims, width, bound, pieces=(), kind=jnp.bfloat16):
    level = steps_of(key, dims, pieces, -0.22, 0.18) if pieces else 1.0
    values = jax.random.normal(key, dims, jnp.float32) * width * level
    return jnp.minimum(jnp.maximum(values, -bound), bound).astype(kind)


def setup_inputs(seed: int = 0) -> dict:
    key_of = jax.random.split(jax.random.key(seed), 16)
    inputs = gaussian(key_of[0], (SEQS, SEQ, D), 1.0, 6.0, ((0, 4), (1, 4)))
    cotangent = gaussian(key_of[1], (SEQS, SEQ, D), 1.0, 6.0, ((0, 4), (1, 4)))
    lengths = draw_lengths(jax.random.fold_in(key_of[15], 71), 0)
    norm_gains = jnp.clip(1.0 + 0.1 * jax.random.normal(key_of[3], (4, D), jnp.float32), 0.5, 1.5)
    conv_in = gaussian(key_of[4], (D, 3 * D), D ** -0.5, 0.1875, ((0, 4),))
    conv_kernel = gaussian(key_of[5], (3, D), 3 ** -0.5, 3.5, (), jnp.float32)
    conv_out = gaussian(key_of[6], (D, D), D ** -0.5, 0.1875, ((0, 4),))
    attn_q = gaussian(key_of[7], (D, HEADS * HEAD), D ** -0.5, 0.1875, ((0, 4),))
    attn_k = gaussian(key_of[8], (D, KV_HEADS * HEAD), D ** -0.5, 0.1875, ((0, 4),))
    attn_v = gaussian(key_of[9], (D, KV_HEADS * HEAD), D ** -0.5, 0.1875, ((0, 4),))
    attn_out = gaussian(key_of[10], (HEADS * HEAD, D), 1 ** -0.5, 6.0, ((0, 4),))
    head_gains = jnp.clip(1.0 + 0.1 * jax.random.normal(key_of[11], (2, HEAD), jnp.float32), 0.5, 1.5)
    ffn_gate = gaussian(key_of[12], (2, D, FF), D ** -0.5, 0.1875, ((0, 2), (1, 4)))
    ffn_up = gaussian(key_of[13], (2, D, FF), D ** -0.5, 0.1875, ((0, 2), (1, 4)))
    ffn_down = gaussian(key_of[14], (2, FF, D), FF ** -0.5, 0.09375, ((0, 2), (1, 4)))
    return dict(inputs=inputs, cotangent=cotangent, lengths=lengths, norm_gains=norm_gains, conv_in=conv_in, conv_kernel=conv_kernel, conv_out=conv_out, attn_q=attn_q, attn_k=attn_k, attn_v=attn_v, attn_out=attn_out, head_gains=head_gains, ffn_gate=ffn_gate, ffn_up=ffn_up, ffn_down=ffn_down)


EPSILON = 1e-05
NEGATIVE = -1e+30
HIGHEST = lax.Precision.HIGHEST

@jax.custom_vjp
def low(v):
    return lax.optimization_barrier(v.astype(jnp.bfloat16)).astype(jnp.float32)

@jax.custom_vjp
def low_back(v):
    return v

def low_keep(v):
    return (low(v), None)

def low_pass(kept, grad):
    return (grad,)

def back_keep(v):
    return (v, None)

def back_low(kept, grad):
    return (low(grad),)
low.defvjp(low_keep, low_pass)
low_back.defvjp(back_keep, back_low)

def product(left_op, right_op):
    return jnp.dot(left_op, right_op, precision=HIGHEST, preferred_element_type=jnp.float32)

def norm_rows(values):
    return values * lax.rsqrt(lax.optimization_barrier(jnp.mean(values * values, axis=-1, keepdims=True)) + EPSILON)

def feed_forward(residual, norm_gain, w_gate, w_up, w_down):
    normed_low = low(norm_rows(residual) * norm_gain)
    gate_pre = low_back(product(normed_low, w_gate))
    up_pre = low_back(product(normed_low, w_up))
    hidden = low(jax.nn.silu(gate_pre) * up_pre)
    return product(hidden, w_down)

def mixer_conv(x_rows, norm_gain, w_in, kernel, w_out):
    normed_low = low(norm_rows(x_rows) * norm_gain)
    projected = low_back(product(normed_low, w_in))
    b_gate, c_gate, x_value = jnp.split(projected, 3, axis=-1)
    b_product = low_back(low(b_gate * x_value))
    padded = jnp.pad(b_product, ((2, 0), (0, 0)))
    convolved = kernel[0] * padded[:-2] + kernel[1] * padded[1:-1] + kernel[2] * padded[2:]
    z_low = low(c_gate * convolved)
    return low_back(product(z_low, w_out))

def attention(queries, keys_in, values_in, length):
    group_size = HEADS // KV_HEADS
    keys_rep = jnp.repeat(keys_in, group_size, axis=1)
    values_rep = jnp.repeat(values_in, group_size, axis=1)
    block_rows = math.gcd(SEQ, 512)
    key_pos = jnp.arange(SEQ)

    def per_block(seq_pair):
        query_block, start_at = seq_pair
        query_pos = start_at + jnp.arange(block_rows)
        scores = low_back(jnp.einsum('qhd,khd->hqk', query_block, keys_rep, precision=HIGHEST) * HEAD ** (-0.5))
        allowed = (key_pos[None, :] <= query_pos[:, None]) & (key_pos[None, :] < length)
        scores = jnp.where(allowed[None], scores, NEGATIVE)
        weights = low(jax.nn.softmax(scores, axis=-1))
        return jnp.einsum('hqk,khd->qhd', weights, values_rep, precision=HIGHEST)
    blocks = queries.reshape(SEQ // block_rows, block_rows, HEADS, HEAD)
    starts = jnp.arange(SEQ // block_rows, dtype=jnp.int32) * block_rows
    return lax.map(jax.checkpoint(per_block), (blocks, starts)).reshape(SEQ, HEADS, HEAD)

def mixer_attention(x_rows, norm_gain, w_q, w_k, w_v, w_o, head_gains, length):
    normed_low = low(norm_rows(x_rows) * norm_gain)
    query_pre = low_back(product(normed_low, w_q)).reshape(SEQ, HEADS, HEAD)
    key_pre = low_back(product(normed_low, w_k)).reshape(SEQ, KV_HEADS, HEAD)
    value_pre = product(normed_low, w_v).reshape(SEQ, KV_HEADS, HEAD)
    query_low = low_back(low(norm_rows(query_pre) * head_gains[0]))
    key_low = low_back(low(norm_rows(key_pre) * head_gains[1]))
    value_low = low_back(low(value_pre))
    attended = attention(query_low, key_low, value_low, length)
    attended_low = low_back(low(attended.reshape(SEQ, HEADS * HEAD)))
    return low_back(product(attended_low, w_o))

def one_sequence(x_rows, length, weights):
    norm_gains, conv_in, conv_kernel, conv_out, attn_q, attn_k, attn_v, attn_out, head_gains, ffn_gate, ffn_up, ffn_down = weights
    row_mask = (jnp.arange(SEQ) < length).astype(jnp.float32)[:, None]
    mixer_one = mixer_conv(x_rows, norm_gains[0], conv_in, conv_kernel, conv_out)
    residual = x_rows + mixer_one
    ffn_one = feed_forward(residual, norm_gains[1], ffn_gate[0], ffn_up[0], ffn_down[0])
    passed = low_back(low(residual + ffn_one))
    attn_rows = mixer_attention(passed, norm_gains[2], attn_q, attn_k, attn_v, attn_out, head_gains, length)
    residual_two = passed + attn_rows
    ffn_two = feed_forward(residual_two, norm_gains[3], ffn_gate[1], ffn_up[1], ffn_down[1])
    result = (residual_two + ffn_two) * row_mask
    parts = (x_rows, mixer_one, ffn_one, passed, attn_rows, residual_two, ffn_two, result)
    squares = jnp.stack([jnp.sum(row_mask * part * part) for part in parts])
    return (result, squares)

def reference(inputs, cotangent, lengths, norm_gains, conv_in, conv_kernel, conv_out, attn_q, attn_k, attn_v, attn_out, head_gains, ffn_gate, ffn_up, ffn_down):
    weights = tuple((item.astype(jnp.float32) for item in (norm_gains, conv_in, conv_kernel, conv_out, attn_q, attn_k, attn_v, attn_out, head_gains, ffn_gate, ffn_up, ffn_down)))

    def forward(weights_in, sequences):

        def per_sequence(seq_pair):
            return jax.checkpoint(one_sequence)(seq_pair[0], seq_pair[1], weights_in)
        return lax.map(per_sequence, (sequences, lengths))
    (outputs, squares), pullback = jax.vjp(forward, weights, inputs.astype(jnp.float32))
    weight_grads, input_grads = pullback((cotangent.astype(jnp.float32), jnp.zeros_like(squares)))
    token_total = jnp.sum(lengths).astype(jnp.float32) * D
    rms = jnp.sqrt(lax.optimization_barrier(jnp.sum(squares, axis=0)) / token_total)
    ends = jnp.stack([input_grads, outputs]).astype(jnp.bfloat16)
    gain_grads = weight_grads[0]
    return (ends, gain_grads[:3], gain_grads[3], weight_grads[1], weight_grads[2], weight_grads[3], weight_grads[4], weight_grads[5], weight_grads[6], weight_grads[7], weight_grads[8], weight_grads[9], weight_grads[10], weight_grads[11], rms)
```

```python
import functools

import jax
import jax.numpy as jnp
from jax import lax
from jax.experimental import pallas as pl
from jax.experimental.pallas import tpu as pltpu
from jax.sharding import PartitionSpec as P

EPSILON = 1e-05
NEGATIVE = -1e30
MESH = pl.DeviceIdType.MESH
F32 = jnp.float32
BF16 = jnp.bfloat16


def passed_along(block, axis, distance):
    devices = range(lax.axis_size(axis))
    route = [(i - distance, i) for i in devices if i - distance in devices]
    return lax.ppermute(block, axis, route)


def swapped(block, axis):
    return lax.ppermute(block, axis, [(0, 1), (1, 0)])


def rounded(values):
    return lax.optimization_barrier(values.astype(BF16)).astype(F32)


def matmul(left_op, right_op):
    return jnp.dot(left_op, right_op, preferred_element_type=F32)


def matmul_left(left_op, right_op):
    return lax.dot_general(left_op, right_op, (((0,), (0,)), ((), ())), preferred_element_type=F32)


def matmul_right(left_op, right_op):
    return lax.dot_general(left_op, right_op, (((1,), (1,)), ((), ())), preferred_element_type=F32)


def norm_rows(values):
    inv_rms = lax.rsqrt(jnp.mean(values * values, axis=-1, keepdims=True) + EPSILON)
    return (values * inv_rms, inv_rms)


def norm_back(dnormed, normed, inv_rms):
    return inv_rms * dnormed - normed * inv_rms * jnp.mean(dnormed * normed, axis=-1, keepdims=True)


def greet(axis, count):
    me = lax.axis_index(axis)
    barrier = pltpu.get_barrier_semaphore()
    for step in range(1, count):
        pl.semaphore_signal(
            barrier,
            inc=1,
            device_id={axis: lax.rem(me + step, count)},
            device_id_type=MESH,
        )
    pl.semaphore_wait(barrier, count - 1)


def gather_kernel(axis, count, rows, block, whole, send_sem, recv_sem, own_sem):
    me = lax.axis_index(axis)
    greet(axis, count)
    own_rows = pl.ds(pl.multiple_of(me * rows, rows), rows)
    copies = []
    for step in range(1, count):
        copy = pltpu.make_async_remote_copy(
            src_ref=block,
            dst_ref=whole.at[own_rows],
            send_sem=send_sem.at[step],
            recv_sem=recv_sem.at[step],
            device_id={axis: lax.rem(me + step, count)},
            device_id_type=MESH,
        )
        copy.start()
        copies.append(copy)
    own = pltpu.make_async_copy(block, whole.at[own_rows], own_sem)
    own.start()
    own.wait()
    for copy in copies:
        copy.wait()


def swap_kernel(axis, count, rows, blocks, whole, send_sem, recv_sem, own_sem):
    me = lax.axis_index(axis)
    greet(axis, count)
    own_rows = pl.ds(pl.multiple_of(me * rows, rows), rows)
    copies = []
    for step in range(1, count):
        target = lax.rem(me + step, count)
        copy = pltpu.make_async_remote_copy(
            src_ref=blocks.at[pl.ds(pl.multiple_of(target * rows, rows), rows)],
            dst_ref=whole.at[own_rows],
            send_sem=send_sem.at[step],
            recv_sem=recv_sem.at[step],
            device_id={axis: target},
            device_id_type=MESH,
        )
        copy.start()
        copies.append(copy)
    own = pltpu.make_async_copy(blocks.at[own_rows], whole.at[own_rows], own_sem)
    own.start()
    own.wait()
    for copy in copies:
        copy.wait()


def exchange(kernel, axis, array, rows, collective_id):
    count = lax.axis_size(axis)
    return pl.pallas_call(
        functools.partial(kernel, axis, count, rows),
        out_shape=jax.ShapeDtypeStruct((count * rows,) + array.shape[1:], array.dtype),
        in_specs=[pl.BlockSpec(memory_space=pl.ANY)],
        out_specs=pl.BlockSpec(memory_space=pl.ANY),
        scratch_shapes=[
            pltpu.SemaphoreType.DMA((count,)),
            pltpu.SemaphoreType.DMA((count,)),
            pltpu.SemaphoreType.DMA,
        ],
        compiler_params=pltpu.CompilerParams(
            collective_id=collective_id, has_side_effects=True, vmem_limit_bytes=8 << 20
        ),
    )(array)


def gathered(array, axis, collective_id):
    return exchange(gather_kernel, axis, array, array.shape[0], collective_id)


def swapped_blocks(array, axis, collective_id):
    return exchange(swap_kernel, axis, array, array.shape[0] // lax.axis_size(axis), collective_id)


def reduced(partial, axis, collective_id):
    count = lax.axis_size(axis)
    terms = swapped_blocks(partial.astype(BF16), axis, collective_id)
    return jnp.sum(terms.reshape(count, -1, partial.shape[1]).astype(F32), axis=0)


def attend(query, key_all, value_all, allowed):
    kv_heads = key_all.shape[1]
    rows, q_heads, head = query.shape
    grouped = query.reshape(rows, kv_heads, q_heads // kv_heads, head)
    scores = jnp.einsum("qghd,kgd->ghqk", grouped, key_all, preferred_element_type=F32) * head ** (-0.5)
    scores = jnp.where(allowed, scores, NEGATIVE)
    peak = jnp.max(scores, axis=-1, keepdims=True)
    weights = jnp.where(allowed, jnp.exp(scores - peak), 0.0)
    total = jnp.sum(weights, axis=-1, keepdims=True)
    log_total = peak + jnp.log(total)
    prob = (weights / total).astype(BF16)
    out = jnp.einsum("ghqk,kgd->qghd", prob, value_all, preferred_element_type=F32)
    return out.reshape(rows, q_heads * head), log_total


def attend_back(query, key_all, value_all, allowed, log_total, attended, d_out):
    kv_heads = key_all.shape[1]
    rows, q_heads, head = query.shape
    scale = head ** (-0.5)
    grouped = query.reshape(rows, kv_heads, q_heads // kv_heads, head)
    d_group = d_out.reshape(rows, kv_heads, q_heads // kv_heads, head)
    delta = jnp.sum(d_group.astype(F32) * attended.reshape(d_group.shape), axis=-1)
    scores = jnp.einsum("qghd,kgd->ghqk", grouped, key_all, preferred_element_type=F32) * scale
    prob = jnp.where(allowed, jnp.exp(scores - log_total), 0.0)
    d_prob = jnp.einsum("qghd,kgd->ghqk", d_group, value_all, preferred_element_type=F32)
    d_scores = (prob * (d_prob - delta.transpose(1, 2, 0)[..., None])).astype(BF16)
    d_query = jnp.einsum("ghqk,kgd->qghd", d_scores, key_all, preferred_element_type=F32) * scale
    d_key = jnp.einsum("ghqk,qghd->kgd", d_scores, grouped, preferred_element_type=F32) * scale
    d_value = jnp.einsum("ghqk,qghd->kgd", prob.astype(BF16), d_group, preferred_element_type=F32)
    return d_query.reshape(rows, q_heads, head), d_key, d_value


def ffn_forward(residual, gain, w_gate, w_up, w_down):
    normed, inv_rms = norm_rows(residual)
    act = gathered((normed * gain).astype(BF16), "fsdp", 0)
    gate_pre = matmul(act, w_gate)
    up_pre = matmul(act, w_up)
    hidden = (jax.nn.silu(gate_pre) * up_pre).astype(BF16)
    out = reduced(matmul(hidden, w_down), "fsdp", 1)
    return out, (normed, inv_rms, act, gate_pre, up_pre, hidden)


def ffn_backward(d_low, kept, gain, w_gate, w_up, w_down):
    normed, inv_rms, act, gate_pre, up_pre, hidden = kept
    d_all = gathered(d_low, "fsdp", 0)
    d_hidden = matmul_right(d_all, w_down)
    sigmoid = jax.nn.sigmoid(gate_pre)
    d_up = (d_hidden * gate_pre * sigmoid).astype(BF16)
    d_gate = (d_hidden * up_pre * sigmoid * (1.0 + gate_pre * (1.0 - sigmoid))).astype(BF16)
    d_act = reduced(matmul_right(d_gate, w_gate) + matmul_right(d_up, w_up), "fsdp", 1)
    grad_gate = matmul_left(act, d_gate).astype(BF16)
    grad_up = matmul_left(act, d_up).astype(BF16)
    grad_down = matmul_left(hidden, d_all).astype(BF16)
    grad_gain = jnp.sum(d_act * normed, axis=0)
    return norm_back(d_act * gain, normed, inv_rms), grad_gain, (grad_gate, grad_up, grad_down)


def shards(
    inputs,
    cotangent,
    lengths,
    norm_gains,
    conv_in,
    conv_kernel,
    conv_out,
    attn_q,
    attn_k,
    attn_v,
    attn_out,
    head_gains,
    ffn_gate,
    ffn_up,
    ffn_down,
):
    micro, rows, width = inputs.shape
    section = lax.axis_index("section")
    group = lax.axis_index("fsdp")
    fsdp = lax.axis_size("fsdp")
    assert micro == lax.axis_size("section")
    head = head_gains.shape[1]
    q_width, kv_width = attn_q.shape[1], attn_k.shape[1]
    q_heads, kv_heads = q_width // head, kv_width // head
    positions = lax.axis_index("ctx") * rows + jnp.arange(rows)
    length = lax.dynamic_index_in_dim(lengths, group * micro + section, keepdims=False)
    mask = (positions < length).astype(F32)[:, None]

    def whole_rows(weight):
        half = weight.shape[0] // micro
        mine = lax.dynamic_slice_in_dim(weight, section * half, half, 0)
        return lax.all_gather(mine, ("fsdp", "section"), axis=0, tiled=True)

    def to_columns(weight):
        deep, wide = weight.shape
        blocks = weight.reshape(deep, fsdp, wide // fsdp).transpose(1, 0, 2)
        return swapped_blocks(blocks.reshape(fsdp * deep, wide // fsdp), "fsdp", 2)

    def both(weight):
        other = swapped(weight, "section")
        first = section == 0
        return jnp.where(first, weight, other), jnp.where(first, other, weight)

    in_full = whole_rows(conv_in)
    out_full = whole_rows(conv_out)
    gate_up = to_columns(jnp.concatenate([ffn_gate[0], ffn_up[0]], axis=0))
    part = ffn_gate.shape[1]
    gate_up = gate_up.reshape(fsdp, 2, part, -1)
    gates = both(gate_up[:, 0].reshape(fsdp * part, -1))
    ups = both(gate_up[:, 1].reshape(fsdp * part, -1))
    downs = both(ffn_down[0])
    query_full, key_full, value_full, proj_full = (
        whole_rows(attn_q),
        whole_rows(attn_k),
        whole_rows(attn_v),
        whole_rows(attn_out),
    )

    x = lax.dynamic_index_in_dim(inputs, section, keepdims=False).astype(F32)
    normed0, inv0 = norm_rows(x)
    act1 = (normed0 * norm_gains[0]).astype(BF16)
    projected = matmul(act1, in_full)
    b_gate, c_gate, x_value = (
        projected[:, :width],
        projected[:, width : 2 * width],
        projected[:, 2 * width :],
    )
    b_product = (b_gate * x_value).astype(BF16)
    rim = passed_along(b_product[-2:], "ctx", 1)
    extended = jnp.concatenate([rim, b_product], axis=0).astype(F32)
    convolved = (
        conv_kernel[0] * extended[:-2]
        + conv_kernel[1] * extended[1:-1]
        + conv_kernel[2] * extended[2:]
    )
    z_low = (c_gate * convolved).astype(BF16)
    mixed = matmul(z_low, out_full)
    res1 = x + mixed
    ffn1, kept1 = ffn_forward(res1, norm_gains[1], gates[0], ups[0], downs[0])
    h_low = (res1 + ffn1).astype(BF16)

    h = h_low.astype(F32)
    normed2, inv2 = norm_rows(h)
    act2 = (normed2 * norm_gains[2]).astype(BF16)
    q_normed, q_inv = norm_rows(matmul(act2, query_full).reshape(rows, q_heads, head))
    k_normed, k_inv = norm_rows(matmul(act2, key_full).reshape(rows, kv_heads, head))
    query = (q_normed * head_gains[0]).astype(BF16)
    key = (k_normed * head_gains[1]).astype(BF16)
    value = matmul(act2, value_full).astype(BF16)
    kv_all = gathered(jnp.concatenate([key.reshape(rows, kv_width), value], axis=1), "ctx", 3)
    key_all = kv_all[:, :kv_width].reshape(-1, kv_heads, head)
    value_all = kv_all[:, kv_width:].reshape(-1, kv_heads, head)
    key_pos = jnp.arange(kv_all.shape[0])
    allowed = (key_pos[None, :] <= positions[:, None]) & (key_pos[None, :] < length)
    attended, log_total = attend(query, key_all, value_all, allowed)
    attended_low = attended.astype(BF16)
    attn_rows = matmul(attended_low, proj_full)
    res2 = h + attn_rows
    ffn2, kept2 = ffn_forward(res2, norm_gains[3], gates[1], ups[1], downs[1])
    result = (res2 + ffn2) * mask

    def square(values):
        return jnp.sum(mask * values * values)

    squares = jnp.stack(
        [square(v) for v in (x, mixed, ffn1, h, attn_rows, res2, ffn2, result)]
    )

    d_sum_low = (lax.dynamic_index_in_dim(cotangent, section, keepdims=False).astype(F32) * mask).astype(BF16)
    d_sum = d_sum_low.astype(F32)
    d_ffn, gain3, grads2 = ffn_backward(d_sum_low, kept2, norm_gains[3], gates[1], ups[1], downs[1])
    d_res2 = d_sum + d_ffn
    d_attn = d_res2.astype(BF16)
    grad_proj = matmul_left(attended_low, d_attn)
    d_att = matmul_right(d_attn, proj_full).astype(BF16)
    d_query, d_key_all, d_value_all = attend_back(
        query, key_all, value_all, allowed, log_total, attended, d_att
    )
    d_kv = reduced(
        jnp.concatenate(
            [d_key_all.reshape(-1, kv_width), d_value_all.reshape(-1, kv_width)], axis=1
        ),
        "ctx",
        4,
    )
    d_qn = rounded(d_query)
    grad_qgain = jnp.sum(d_qn * q_normed, axis=(0, 1))
    d_qpre = norm_back(d_qn * head_gains[0], q_normed, q_inv).reshape(rows, -1).astype(BF16)
    d_kn = rounded(d_kv[:, :kv_width]).reshape(rows, kv_heads, head)
    grad_kgain = jnp.sum(d_kn * k_normed, axis=(0, 1))
    d_kpre = norm_back(d_kn * head_gains[1], k_normed, k_inv).reshape(rows, -1).astype(BF16)
    d_vpre = d_kv[:, kv_width:].astype(BF16)
    grad_query = matmul_left(act2, d_qpre)
    grad_key = matmul_left(act2, d_kpre)
    grad_value = matmul_left(act2, d_vpre)
    d_act2 = (
        matmul_right(d_qpre, query_full)
        + matmul_right(d_kpre, key_full)
        + matmul_right(d_vpre, value_full)
    )
    gain2 = jnp.sum(d_act2 * normed2, axis=0)
    d_h_low = (d_res2 + norm_back(d_act2 * norm_gains[2], normed2, inv2)).astype(BF16)

    d_ffn1, gain1, grads1 = ffn_backward(d_h_low, kept1, norm_gains[1], gates[0], ups[0], downs[0])
    d_res1 = d_h_low.astype(F32) + d_ffn1
    d_mixed = d_res1.astype(BF16)
    grad_out = matmul_left(z_low, d_mixed)
    d_z = matmul_right(d_mixed, out_full)
    d_cgate = d_z * convolved
    d_conv = d_z * c_gate
    grad_kernel = jnp.stack(
        [
            jnp.sum(d_conv * extended[:-2], axis=0),
            jnp.sum(d_conv * extended[1:-1], axis=0),
            jnp.sum(d_conv * extended[2:], axis=0),
        ]
    )
    d_extended = (
        jnp.pad(d_conv * conv_kernel[0], ((0, 2), (0, 0)))
        + jnp.pad(d_conv * conv_kernel[1], ((1, 1), (0, 0)))
        + jnp.pad(d_conv * conv_kernel[2], ((2, 0), (0, 0)))
    )
    from_next = passed_along(d_extended[:2], "ctx", -1)
    d_bproduct = rounded(d_extended[2:] + jnp.pad(from_next, ((rows - 2, 0), (0, 0))))
    d_projected = jnp.concatenate(
        [d_bproduct * x_value, d_cgate, d_bproduct * b_gate], axis=1
    ).astype(BF16)
    grad_in = matmul_left(act1, d_projected)
    d_act1 = matmul_right(d_projected, in_full)
    gain0 = jnp.sum(d_act1 * normed0, axis=0)
    d_x = (d_res1 + norm_back(d_act1 * norm_gains[0], normed0, inv0)).astype(BF16)

    y_low = result.astype(BF16)
    is_first = section == 0
    other_end = swapped(jnp.where(is_first, y_low, d_x), "section")
    ends = jnp.where(is_first, jnp.stack([d_x, other_end]), jnp.stack([other_end, y_low]))[None]

    def own_rows(grad):
        share = lax.psum_scatter(
            grad.astype(BF16), ("fsdp", "section"), scatter_dimension=0, tiled=True
        )
        total = lax.psum(share, "ctx")
        return lax.all_gather(total, "section", axis=0, tiled=True).astype(F32)

    conv_grads = own_rows(jnp.concatenate([grad_in, grad_out], axis=1))
    attn_grads = own_rows(jnp.concatenate([grad_query, grad_key, grad_value, grad_proj], axis=1))

    def own_section(first, second):
        mine = jnp.where(is_first, first, second)
        other = swapped(jnp.where(is_first, second, first), "section")
        return (mine.astype(F32) + other.astype(F32)).astype(BF16)

    ffn_grads = lax.psum(tuple(own_section(a, b) for a, b in zip(grads1, grads2)), "ctx")

    def to_rows(grad):
        return swapped_blocks(grad, "fsdp", 5).reshape(fsdp, part, -1).transpose(1, 0, 2).reshape(part, -1)

    small = jnp.concatenate(
        [
            jnp.stack([gain0, gain1, gain2, gain3]).reshape(-1),
            grad_kernel.reshape(-1),
            grad_qgain,
            grad_kgain,
            squares,
            jnp.zeros((width - 2 * head - squares.shape[0],), F32),
        ]
    ).reshape(-1, width)
    small = lax.psum(small, ("section", "ctx", "fsdp"))
    cut = width // fsdp
    mine = lax.dynamic_slice_in_dim(small, group * cut, cut, 1)
    head_cut = head // fsdp
    heads = lax.dynamic_slice_in_dim(small[7, : 2 * head].reshape(2, head), group * head_cut, head_cut, 1)
    token_total = jnp.sum(lengths).astype(F32) * width
    rms_all = jnp.sqrt(small[7, 2 * head : 2 * head + 8] / token_total)
    rms = lax.dynamic_slice_in_dim(rms_all, group * (8 // fsdp), 8 // fsdp)
    return (
        ends,
        mine[:3],
        mine[3],
        conv_grads[:, : 3 * width],
        mine[4:7],
        conv_grads[:, 3 * width :],
        attn_grads[:, :q_width],
        attn_grads[:, q_width : q_width + kv_width],
        attn_grads[:, q_width + kv_width : q_width + 2 * kv_width],
        attn_grads[:, q_width + 2 * kv_width :],
        heads,
        to_rows(ffn_grads[0])[None].astype(F32),
        to_rows(ffn_grads[1])[None].astype(F32),
        ffn_grads[2][None].astype(F32),
        rms,
    )


def solution(mesh):
    return jax.shard_map(
        shards,
        mesh=mesh,
        in_specs=(
            P("fsdp", "ctx", None),
            P("fsdp", "ctx", None),
            P(),
            P(),
            P("fsdp", None),
            P(),
            P("fsdp", None),
            P("fsdp", None),
            P("fsdp", None),
            P("fsdp", None),
            P("fsdp", None),
            P(),
            P("section", "fsdp", None),
            P("section", "fsdp", None),
            P("section", "fsdp", None),
        ),
        out_specs=(
            P("section", "fsdp", "ctx", None),
            P(None, "fsdp"),
            P("fsdp"),
            P("fsdp", None),
            P(None, "fsdp"),
            P("fsdp", None),
            P("fsdp", None),
            P("fsdp", None),
            P("fsdp", None),
            P("fsdp", None),
            P(None, "fsdp"),
            P("section", "fsdp", None),
            P("section", "fsdp", None),
            P("section", "fsdp", None),
            P("fsdp"),
        ),
        check_vma=False,
    )
```

```python
import functools

import jax
import jax.numpy as jnp
from jax import lax
from jax.experimental import pallas as pl
from jax.experimental.pallas import tpu as pltpu
from jax.sharding import PartitionSpec as P

EPSILON = 1e-05
NEGATIVE = -1e30
MESH = pl.DeviceIdType.MESH
F32 = jnp.float32
BF16 = jnp.bfloat16


def passed_along(block, axis, distance):
    devices = range(lax.axis_size(axis))
    route = [(i - distance, i) for i in devices if i - distance in devices]
    return lax.ppermute(block, axis, route)


def swapped(block, axis):
    return lax.ppermute(block, axis, [(0, 1), (1, 0)])


def rounded(values):
    return lax.optimization_barrier(values.astype(BF16)).astype(F32)


def matmul(left_op, right_op):
    return jnp.dot(left_op, right_op, preferred_element_type=F32)


def matmul_left(left_op, right_op):
    return lax.dot_general(left_op, right_op, (((0,), (0,)), ((), ())), preferred_element_type=F32)


def matmul_right(left_op, right_op):
    return lax.dot_general(left_op, right_op, (((1,), (1,)), ((), ())), preferred_element_type=F32)


def norm_rows(values):
    inv_rms = lax.rsqrt(jnp.mean(values * values, axis=-1, keepdims=True) + EPSILON)
    return (values * inv_rms, inv_rms)


def norm_back(dnormed, normed, inv_rms):
    return inv_rms * dnormed - normed * inv_rms * jnp.mean(dnormed * normed, axis=-1, keepdims=True)


def greet(axis, count):
    me = lax.axis_index(axis)
    barrier = pltpu.get_barrier_semaphore()
    for step in range(1, count):
        pl.semaphore_signal(
            barrier,
            inc=1,
            device_id={axis: lax.rem(me + step, count)},
            device_id_type=MESH,
        )
    pl.semaphore_wait(barrier, count - 1)


def gather_kernel(axis, count, rows, block, whole, send_sem, recv_sem, own_sem):
    me = lax.axis_index(axis)
    greet(axis, count)
    own_rows = pl.ds(pl.multiple_of(me * rows, rows), rows)
    copies = []
    for step in range(1, count):
        copy = pltpu.make_async_remote_copy(
            src_ref=block,
            dst_ref=whole.at[own_rows],
            send_sem=send_sem.at[step],
            recv_sem=recv_sem.at[step],
            device_id={axis: lax.rem(me + step, count)},
            device_id_type=MESH,
        )
        copy.start()
        copies.append(copy)
    own = pltpu.make_async_copy(block, whole.at[own_rows], own_sem)
    own.start()
    own.wait()
    for copy in copies:
        copy.wait()


def swap_kernel(axis, count, rows, blocks, whole, send_sem, recv_sem, own_sem):
    me = lax.axis_index(axis)
    greet(axis, count)
    own_rows = pl.ds(pl.multiple_of(me * rows, rows), rows)
    copies = []
    for step in range(1, count):
        target = lax.rem(me + step, count)
        copy = pltpu.make_async_remote_copy(
            src_ref=blocks.at[pl.ds(pl.multiple_of(target * rows, rows), rows)],
            dst_ref=whole.at[own_rows],
            send_sem=send_sem.at[step],
            recv_sem=recv_sem.at[step],
            device_id={axis: target},
            device_id_type=MESH,
        )
        copy.start()
        copies.append(copy)
    own = pltpu.make_async_copy(blocks.at[own_rows], whole.at[own_rows], own_sem)
    own.start()
    own.wait()
    for copy in copies:
        copy.wait()


def exchange(kernel, axis, array, rows, collective_id):
    count = lax.axis_size(axis)
    return pl.pallas_call(
        functools.partial(kernel, axis, count, rows),
        out_shape=jax.ShapeDtypeStruct((count * rows,) + array.shape[1:], array.dtype),
        in_specs=[pl.BlockSpec(memory_space=pl.ANY)],
        out_specs=pl.BlockSpec(memory_space=pl.ANY),
        scratch_shapes=[
            pltpu.SemaphoreType.DMA((count,)),
            pltpu.SemaphoreType.DMA((count,)),
            pltpu.SemaphoreType.DMA,
        ],
        compiler_params=pltpu.CompilerParams(
            collective_id=collective_id, has_side_effects=True, vmem_limit_bytes=8 << 20
        ),
    )(array)


def gathered(array, axis, collective_id):
    return exchange(gather_kernel, axis, array, array.shape[0], collective_id)


def swapped_blocks(array, axis, collective_id):
    return exchange(swap_kernel, axis, array, array.shape[0] // lax.axis_size(axis), collective_id)


def reduced(partial, axis, collective_id):
    count = lax.axis_size(axis)
    terms = swapped_blocks(partial.astype(BF16), axis, collective_id)
    return jnp.sum(terms.reshape(count, -1, partial.shape[1]).astype(F32), axis=0)


def tail_kernel(
    counts,
    gate_in,
    up_in,
    down_in,
    attn_in,
    conv_b_in,
    conv_c_in,
    conv_x_in,
    conv_o_in,
    small_in,
    second_gu_in,
    second_down_in,
    gu_out,
    down_out,
    rest_out,
    a_own,
    a_other,
    a_sum,
    a_done,
    b_own,
    b_other,
    b_sum,
    b_done,
    c_own,
    c_other,
    c_got,
    own_sem,
    pair_send,
    pair_recv,
    c_own_sem,
    c_pair_send,
    c_pair_recv,
    c_send,
    c_recv,
    a_up_send,
    a_up_recv,
    a_back_send,
    a_back_recv,
    a_out_send,
    b_up_send,
    b_up_recv,
    b_back_send,
    b_back_recv,
    b_out_send,
    b_keep_sem,
    gu_recv,
    down_recv,
    rest_recv,
    second_send,
):
    n_ctx, n_fsdp = counts
    section = lax.axis_index("section")
    place = lax.axis_index("ctx")
    group = lax.axis_index("fsdp")
    other = 1 - section
    a_chunks, a_rows, a_width = a_own.shape
    b_chunks, b_rows, b_width = b_own.shape
    half = gate_in.shape[0] // n_fsdp // 2
    subs = half // a_rows
    per_kind = n_fsdp * subs
    down_half = down_in.shape[0] // 2
    down_chunks = down_half // b_rows
    attn_rows = attn_in.shape[0]
    attn_chunks = attn_rows // b_rows
    conv_start = down_chunks + attn_chunks
    c_rows = c_own.shape[1]
    conv_chunks = c_rows // b_rows
    ticks = a_chunks // 2
    tail = 2 * (n_ctx - 1)

    barrier = pltpu.get_barrier_semaphore()
    for step in range(1, 2 * n_fsdp):
        flat = lax.rem(section * n_fsdp + group + step, 2 * n_fsdp)
        pl.semaphore_signal(
            barrier,
            inc=1,
            device_id={"section": flat // n_fsdp, "fsdp": lax.rem(flat, n_fsdp)},
            device_id_type=MESH,
        )

    @pl.when(place > 0)
    def _():
        pl.semaphore_signal(barrier, inc=1, device_id={"ctx": place - 1}, device_id_type=MESH)

    @pl.when(place < n_ctx - 1)
    def _():
        pl.semaphore_signal(barrier, inc=1, device_id={"ctx": place + 1}, device_id_type=MESH)

    at_edge = (place == 0) | (place == n_ctx - 1)

    @pl.when(at_edge)
    def _():
        pl.semaphore_wait(barrier, 2 * n_fsdp)

    @pl.when(jnp.logical_not(at_edge))
    def _():
        pl.semaphore_wait(barrier, 2 * n_fsdp + 1)

    def half_rows(owner, which):
        return pl.ds(pl.multiple_of(owner * (2 * half) + which * half, half), half)

    local, pair = [], []
    for kind, source in enumerate((gate_in, up_in)):
        for owner in range(n_fsdp):
            index = kind * n_fsdp + owner
            slot = pl.ds(index * subs, subs)
            for sub in range(subs):
                src_own = source.at[pl.ds(pl.multiple_of(owner * (2 * half) + section * half + sub * a_rows, a_rows), a_rows)]
                src_other = source.at[pl.ds(pl.multiple_of(owner * (2 * half) + other * half + sub * a_rows, a_rows), a_rows)]
                spot = index * subs + sub
                local.append(pltpu.make_async_copy(src_own, a_own.at[spot], own_sem.at[spot]))
                pair.append(
                    pltpu.make_async_remote_copy(
                        src_ref=src_other,
                        dst_ref=a_other.at[spot],
                        send_sem=pair_send.at[spot],
                        recv_sem=pair_recv.at[spot],
                        device_id={"section": other},
                        device_id_type=MESH,
                    )
                )
    for chunk in range(down_chunks):
        spot = a_chunks + chunk
        src_own = down_in.at[pl.ds(pl.multiple_of(section * down_half + chunk * b_rows, b_rows), b_rows)]
        src_other = down_in.at[pl.ds(pl.multiple_of(other * down_half + chunk * b_rows, b_rows), b_rows)]
        local.append(pltpu.make_async_copy(src_own, b_own.at[chunk], own_sem.at[spot]))
        pair.append(
            pltpu.make_async_remote_copy(
                src_ref=src_other,
                dst_ref=b_other.at[chunk],
                send_sem=pair_send.at[spot],
                recv_sem=pair_recv.at[spot],
                device_id={"section": other},
                device_id_type=MESH,
            )
        )
    for chunk in range(attn_chunks):
        local.append(
            pltpu.make_async_copy(
                attn_in.at[pl.ds(chunk * b_rows, b_rows)],
                b_own.at[down_chunks + chunk],
                own_sem.at[a_chunks + down_chunks + chunk],
            )
        )
    for copy in pair:
        copy.start()
    for copy in local:
        copy.start()
    c_local, c_pair = [], []
    for owner in range(n_fsdp):
        for kind, source in enumerate((conv_b_in, conv_c_in, conv_x_in, conv_o_in)):
            index = owner * 5 + kind
            place_at = pl.ds(kind * half, half)
            c_local.append(
                pltpu.make_async_copy(
                    source.at[half_rows(owner, section)], c_own.at[owner, place_at], c_own_sem.at[index]
                )
            )
            c_pair.append(
                pltpu.make_async_remote_copy(
                    src_ref=source.at[half_rows(owner, other)],
                    dst_ref=c_other.at[owner, place_at],
                    send_sem=c_pair_send.at[index],
                    recv_sem=c_pair_recv.at[index],
                    device_id={"section": other},
                    device_id_type=MESH,
                )
            )
        small_at = pl.ds(4 * half, c_rows - 4 * half)
        index = owner * 5 + 4
        c_local.append(
            pltpu.make_async_copy(small_in.at[owner, section], c_own.at[owner, small_at], c_own_sem.at[index])
        )
        c_pair.append(
            pltpu.make_async_remote_copy(
                src_ref=small_in.at[owner, other],
                dst_ref=c_other.at[owner, small_at],
                send_sem=c_pair_send.at[index],
                recv_sem=c_pair_recv.at[index],
                device_id={"section": other},
                device_id_type=MESH,
            )
        )
    for copy in c_pair:
        copy.start()
    for copy in c_local:
        copy.start()
    b_own[b_chunks - 1] = jnp.zeros((b_rows, b_width), BF16)
    for copy in local:
        copy.wait()
    for copy in pair:
        copy.wait_recv()

    def conv_copy(step):
        target = lax.rem(group + step, n_fsdp)
        return pltpu.make_async_remote_copy(
            src_ref=c_own.at[target],
            dst_ref=c_got.at[step - 1],
            send_sem=c_send.at[step],
            recv_sem=c_recv.at[step],
            device_id={"fsdp": target},
            device_id_type=MESH,
        )

    def conv_out_step():
        for copy in c_local:
            copy.wait()
        for copy in c_pair:
            copy.wait_recv()

        def add(index, carry):
            owner = index // conv_chunks
            at = pl.ds(pl.multiple_of(lax.rem(index, conv_chunks) * b_rows, b_rows), b_rows)
            c_own[owner, at] = (c_own[owner, at].astype(F32) + c_other[owner, at].astype(F32)).astype(BF16)
            return carry

        lax.fori_loop(0, n_fsdp * conv_chunks, add, 0)
        for step in range(1, n_fsdp):
            conv_copy(step).start()

    def conv_in_step():
        for step in range(1, n_fsdp):
            conv_copy(step).wait_recv()

        def add(index, carry):
            at = pl.ds(pl.multiple_of(index * b_rows, b_rows), b_rows)
            total = c_own[group, at].astype(F32)
            for step in range(1, n_fsdp):
                total = total + c_got[step - 1, at].astype(F32)
            b_own[conv_start + index] = total.astype(BF16)
            return carry

        lax.fori_loop(0, conv_chunks, add, 0)

    def second_start():
        for kind in range(2):
            for owner in range(n_fsdp):
                index = kind * n_fsdp + owner
                src = second_gu_in.at[kind, owner]
                dst = gu_out.at[
                    kind,
                    pl.ds(pl.multiple_of(section * half, half), half),
                    pl.ds(pl.multiple_of(group * a_width, 128), a_width),
                ]
                is_mine = (section == 1) & (group == owner)

                @pl.when(is_mine)
                def _(src=src, dst=dst, index=index):
                    pltpu.make_async_copy(src, dst, second_send.at[index]).start()

                @pl.when(jnp.logical_not(is_mine))
                def _(src=src, dst=dst, index=index, kind=kind, owner=owner):
                    pltpu.make_async_remote_copy(
                        src_ref=src,
                        dst_ref=dst,
                        send_sem=second_send.at[index],
                        recv_sem=gu_recv.at[kind, section * n_fsdp + group],
                        device_id={"section": 1, "fsdp": owner},
                        device_id_type=MESH,
                    ).start()

        down_at = down_out.at[pl.ds(pl.multiple_of(section * down_half, b_rows), down_half)]

        @pl.when(section == 1)
        def _():
            pltpu.make_async_copy(second_down_in, down_at, second_send.at[2 * n_fsdp]).start()

        @pl.when(section == 0)
        def _():
            pltpu.make_async_remote_copy(
                src_ref=second_down_in,
                dst_ref=down_at,
                send_sem=second_send.at[2 * n_fsdp],
                recv_sem=down_recv,
                device_id={"section": 1},
                device_id_type=MESH,
            ).start()

    def a_target(k):
        kind = k // per_kind
        rest = lax.rem(k, per_kind)
        owner = rest // subs
        sub = lax.rem(rest, subs)
        spot = gu_out.at[
            kind,
            pl.ds(pl.multiple_of(section * half + sub * a_rows, a_rows), a_rows),
            pl.ds(pl.multiple_of(group * a_width, 128), a_width),
        ]
        return kind, owner, spot

    def hand_out(k):
        kind, owner, spot = a_target(k)
        is_mine = (section == 0) & (group == owner)

        @pl.when(is_mine)
        def _():
            pltpu.make_async_copy(a_done.at[k], spot, a_out_send.at[k]).start()

        @pl.when(jnp.logical_not(is_mine))
        def _():
            pltpu.make_async_remote_copy(
                src_ref=a_done.at[k],
                dst_ref=spot,
                send_sem=a_out_send.at[k],
                recv_sem=gu_recv.at[kind, section * n_fsdp + group],
                device_id={"section": 0, "fsdp": owner},
                device_id_type=MESH,
            ).start()

        @pl.when(k < down_chunks)
        def _():
            at = down_out.at[pl.ds(pl.multiple_of(section * down_half + k * b_rows, b_rows), b_rows)]

            @pl.when(section == 0)
            def _():
                pltpu.make_async_copy(b_done.at[k], at, b_out_send.at[k]).start()

            @pl.when(section == 1)
            def _():
                pltpu.make_async_remote_copy(
                    src_ref=b_done.at[k],
                    dst_ref=at,
                    send_sem=b_out_send.at[k],
                    recv_sem=down_recv,
                    device_id={"section": 0},
                    device_id_type=MESH,
                ).start()

        @pl.when(k >= down_chunks)
        def _():
            at = rest_out.at[section, pl.ds(pl.multiple_of((k - down_chunks) * b_rows, b_rows), b_rows)]
            pltpu.make_async_copy(b_done.at[k], at, b_keep_sem.at[k]).start()
            pltpu.make_async_remote_copy(
                src_ref=b_done.at[k],
                dst_ref=at,
                send_sem=b_out_send.at[k],
                recv_sem=rest_recv,
                device_id={"section": other},
                device_id_type=MESH,
            ).start()

    def up_copies(k, target):
        return (
            pltpu.make_async_remote_copy(
                src_ref=a_sum.at[k],
                dst_ref=a_sum.at[k],
                send_sem=a_up_send.at[k],
                recv_sem=a_up_recv.at[k],
                device_id={"ctx": target},
                device_id_type=MESH,
            ),
            pltpu.make_async_remote_copy(
                src_ref=b_sum.at[k],
                dst_ref=b_sum.at[k],
                send_sem=b_up_send.at[k],
                recv_sem=b_up_recv.at[k],
                device_id={"ctx": target},
                device_id_type=MESH,
            ),
        )

    def back_copies(k, target):
        return (
            pltpu.make_async_remote_copy(
                src_ref=a_done.at[k],
                dst_ref=a_done.at[k],
                send_sem=a_back_send.at[k],
                recv_sem=a_back_recv.at[k],
                device_id={"ctx": target},
                device_id_type=MESH,
            ),
            pltpu.make_async_remote_copy(
                src_ref=b_done.at[k],
                dst_ref=b_done.at[k],
                send_sem=b_back_send.at[k],
                recv_sem=b_back_recv.at[k],
                device_id={"ctx": target},
                device_id_type=MESH,
            ),
        )

    def own_term(k):
        @pl.when(k < down_chunks)
        def _():
            b_own[k] = (b_own[k].astype(F32) + b_other[k].astype(F32)).astype(BF16)

        return a_own[k].astype(F32) + a_other[k].astype(F32)

    lanes = []
    for way in range(2):
        rank = place if way == 0 else n_ctx - 1 - place
        ahead = place + 1 if way == 0 else place - 1
        behind = place - 1 if way == 0 else place + 1
        lanes.append((way, rank, ahead, behind))

    def tick_step(tick, carry):
        @pl.when(tick == 1)
        def _():
            conv_out_step()

        @pl.when(tick == ticks // 2)
        def _():
            second_start()

        @pl.when(tick == conv_start // 2)
        def _():
            conv_in_step()

        for way, rank, ahead, behind in lanes:
            step = tick - rank
            k = 2 * jnp.clip(step, 0, ticks - 1) + way

            @pl.when((step >= 0) & (step < ticks))
            def _(k=k, rank=rank, ahead=ahead, behind=behind):
                term = own_term(k)

                @pl.when(rank == 0)
                def _():
                    a_sum[k] = term.astype(BF16)
                    b_sum[k] = b_own[k]

                @pl.when(rank > 0)
                def _():
                    for copy in up_copies(k, behind):
                        copy.wait_recv()

                @pl.when((rank > 0) & (rank < n_ctx - 1))
                def _():
                    a_sum[k] = (term + a_sum[k].astype(F32)).astype(BF16)
                    b_sum[k] = (b_own[k].astype(F32) + b_sum[k].astype(F32)).astype(BF16)

                @pl.when(rank < n_ctx - 1)
                def _():
                    for copy in up_copies(k, ahead):
                        copy.start()

                @pl.when(rank == n_ctx - 1)
                def _():
                    a_done[k] = (term + a_sum[k].astype(F32)).astype(BF16)
                    b_done[k] = (b_own[k].astype(F32) + b_sum[k].astype(F32)).astype(BF16)
                    for copy in back_copies(k, behind):
                        copy.start()
                    hand_out(k)

            late = tick - (tail - rank)
            j = 2 * jnp.clip(late, 0, ticks - 1) + way

            @pl.when((late >= 0) & (late < ticks) & (rank < n_ctx - 1))
            def _(j=j, rank=rank, ahead=ahead, behind=behind):
                for copy in back_copies(j, ahead):
                    copy.wait_recv()

                @pl.when(rank > 0)
                def _():
                    for copy in back_copies(j, behind):
                        copy.start()

                hand_out(j)

        return carry

    lax.fori_loop(0, ticks + tail, tick_step, 0)

    for copy in pair:
        copy.wait_send()
    for copy in c_pair:
        copy.wait_send()
    for step in range(1, n_fsdp):
        conv_copy(step).wait_send()

    def settle(step, carry):
        for way, rank, ahead, behind in lanes:
            k = 2 * step + way

            @pl.when(rank < n_ctx - 1)
            def _(k=k, ahead=ahead):
                for copy in up_copies(k, ahead):
                    copy.wait_send()

            @pl.when(rank > 0)
            def _(k=k, behind=behind):
                for copy in back_copies(k, behind):
                    copy.wait_send()

            _, _, spot = a_target(k)
            pltpu.make_async_copy(a_done.at[k], spot, a_out_send.at[k]).wait()
            pltpu.make_async_copy(b_done.at[k], b_own.at[k], b_out_send.at[k]).wait()

            @pl.when(k >= down_chunks)
            def _(k=k):
                pltpu.make_async_copy(b_done.at[k], b_own.at[k], b_keep_sem.at[k]).wait()

        return carry

    lax.fori_loop(0, ticks, settle, 0)
    for kind in range(2):
        for owner in range(n_fsdp):
            src = second_gu_in.at[kind, owner]
            pltpu.make_async_copy(src, src, second_send.at[kind * n_fsdp + owner]).wait()
    pltpu.make_async_copy(second_down_in, second_down_in, second_send.at[2 * n_fsdp]).wait()
    for kind in range(2):
        for source in range(2 * n_fsdp):

            @pl.when(section * n_fsdp + group != source)
            def _(kind=kind, source=source):
                region = gu_out.at[
                    kind,
                    pl.ds((source // n_fsdp) * half, half),
                    pl.ds((source % n_fsdp) * a_width, a_width),
                ]
                pltpu.make_async_copy(region, region, gu_recv.at[kind, source]).wait()

    region = down_out.at[pl.ds(pl.multiple_of(other * down_half, b_rows), down_half)]
    pltpu.make_async_copy(region, region, down_recv).wait()
    region = rest_out.at[other]
    pltpu.make_async_copy(region, region, rest_recv).wait()


def summed_gradients(first, attn_half, conv_grads, small, second_gu, second_down):
    n_ctx, n_fsdp = lax.axis_size("ctx"), lax.axis_size("fsdp")
    gate, up, down = first
    half = gate.shape[0] // n_fsdp // 2
    a_rows, b_rows = half // 4, half * 3 // 8
    a_chunks = 2 * n_fsdp * 4
    a_width, b_width = gate.shape[1], down.shape[1]
    c_rows = 4 * half + small.shape[2]
    down_chunks = down.shape[0] // 2 // b_rows
    attn_chunks = attn_half.shape[0] // b_rows
    conv_chunks = c_rows // b_rows
    b_chunks = down_chunks + attn_chunks + conv_chunks + 1
    assert a_chunks == b_chunks and c_rows % b_rows == 0
    rest = b_chunks - down_chunks
    dma = pltpu.SemaphoreType.DMA
    loads = a_chunks + down_chunks + attn_chunks
    return pl.pallas_call(
        functools.partial(tail_kernel, (n_ctx, n_fsdp)),
        out_shape=(
            jax.ShapeDtypeStruct((2, 2 * half, n_fsdp * a_width), BF16),
            jax.ShapeDtypeStruct(down.shape, BF16),
            jax.ShapeDtypeStruct((2, rest * b_rows, b_width), BF16),
        ),
        in_specs=[pl.BlockSpec(memory_space=pl.ANY)] * 11,
        out_specs=[pl.BlockSpec(memory_space=pl.ANY)] * 3,
        scratch_shapes=[
            pltpu.VMEM((a_chunks, a_rows, a_width), BF16),
            pltpu.VMEM((a_chunks, a_rows, a_width), BF16),
            pltpu.VMEM((a_chunks, a_rows, a_width), BF16),
            pltpu.VMEM((a_chunks, a_rows, a_width), BF16),
            pltpu.VMEM((b_chunks, b_rows, b_width), BF16),
            pltpu.VMEM((down_chunks, b_rows, b_width), BF16),
            pltpu.VMEM((b_chunks, b_rows, b_width), BF16),
            pltpu.VMEM((b_chunks, b_rows, b_width), BF16),
            pltpu.VMEM((n_fsdp, c_rows, b_width), BF16),
            pltpu.VMEM((n_fsdp, c_rows, b_width), BF16),
            pltpu.VMEM((n_fsdp - 1, c_rows, b_width), BF16),
            dma((loads,)),
            dma((loads,)),
            dma((loads,)),
            dma((n_fsdp * 5,)),
            dma((n_fsdp * 5,)),
            dma((n_fsdp * 5,)),
            dma((n_fsdp,)),
            dma((n_fsdp,)),
            dma((a_chunks,)),
            dma((a_chunks,)),
            dma((a_chunks,)),
            dma((a_chunks,)),
            dma((a_chunks,)),
            dma((b_chunks,)),
            dma((b_chunks,)),
            dma((b_chunks,)),
            dma((b_chunks,)),
            dma((b_chunks,)),
            dma((b_chunks,)),
            dma((2, 2 * n_fsdp)),
            dma,
            dma,
            dma((2 * n_fsdp + 1,)),
        ],
        compiler_params=pltpu.CompilerParams(
            collective_id=6, has_side_effects=True, vmem_limit_bytes=56 << 20
        ),
    )(gate, up, down, attn_half, *conv_grads, small, second_gu, second_down)


def attend(query, key_all, value_all, allowed):
    kv_heads = key_all.shape[1]
    rows, q_heads, head = query.shape
    grouped = query.reshape(rows, kv_heads, q_heads // kv_heads, head)
    scores = jnp.einsum("qghd,kgd->ghqk", grouped, key_all, preferred_element_type=F32) * head ** (-0.5)
    scores = jnp.where(allowed, scores, NEGATIVE)
    peak = jnp.max(scores, axis=-1, keepdims=True)
    weights = jnp.where(allowed, jnp.exp(scores - peak), 0.0)
    total = jnp.sum(weights, axis=-1, keepdims=True)
    log_total = peak + jnp.log(total)
    prob = (weights / total).astype(BF16)
    out = jnp.einsum("ghqk,kgd->qghd", prob, value_all, preferred_element_type=F32)
    return out.reshape(rows, q_heads * head), log_total


def attend_back(query, key_all, value_all, allowed, log_total, attended, d_out):
    kv_heads = key_all.shape[1]
    rows, q_heads, head = query.shape
    scale = head ** (-0.5)
    grouped = query.reshape(rows, kv_heads, q_heads // kv_heads, head)
    d_group = d_out.reshape(rows, kv_heads, q_heads // kv_heads, head)
    delta = jnp.sum(d_group.astype(F32) * attended.reshape(d_group.shape), axis=-1)
    scores = jnp.einsum("qghd,kgd->ghqk", grouped, key_all, preferred_element_type=F32) * scale
    prob = jnp.where(allowed, jnp.exp(scores - log_total), 0.0)
    d_prob = jnp.einsum("qghd,kgd->ghqk", d_group, value_all, preferred_element_type=F32)
    d_scores = (prob * (d_prob - delta.transpose(1, 2, 0)[..., None])).astype(BF16)
    d_query = jnp.einsum("ghqk,kgd->qghd", d_scores, key_all, preferred_element_type=F32) * scale
    d_key = jnp.einsum("ghqk,qghd->kgd", d_scores, grouped, preferred_element_type=F32) * scale
    d_value = jnp.einsum("ghqk,qghd->kgd", prob.astype(BF16), d_group, preferred_element_type=F32)
    return d_query.reshape(rows, q_heads, head), d_key, d_value


def ffn_forward(residual, gain, w_gate, w_up, w_down):
    normed, inv_rms = norm_rows(residual)
    act = gathered((normed * gain).astype(BF16), "fsdp", 0)
    gate_pre = matmul(act, w_gate)
    up_pre = matmul(act, w_up)
    hidden = (jax.nn.silu(gate_pre) * up_pre).astype(BF16)
    out = reduced(matmul(hidden, w_down), "fsdp", 1)
    return out, (normed, inv_rms, act, gate_pre, up_pre, hidden)


def ffn_backward(d_low, kept, gain, w_gate, w_up, w_down):
    normed, inv_rms, act, gate_pre, up_pre, hidden = kept
    d_all = gathered(d_low, "fsdp", 0)
    d_hidden = matmul_right(d_all, w_down)
    sigmoid = jax.nn.sigmoid(gate_pre)
    d_up = (d_hidden * gate_pre * sigmoid).astype(BF16)
    d_gate = (d_hidden * up_pre * sigmoid * (1.0 + gate_pre * (1.0 - sigmoid))).astype(BF16)
    d_act = reduced(matmul_right(d_gate, w_gate) + matmul_right(d_up, w_up), "fsdp", 1)
    grad_gate = matmul_left(act, d_gate).astype(BF16)
    grad_up = matmul_left(act, d_up).astype(BF16)
    grad_down = matmul_left(hidden, d_all).astype(BF16)
    grad_gain = jnp.sum(d_act * normed, axis=0)
    return norm_back(d_act * gain, normed, inv_rms), grad_gain, (grad_gate, grad_up, grad_down)


def shards(
    inputs,
    cotangent,
    lengths,
    norm_gains,
    conv_in,
    conv_kernel,
    conv_out,
    attn_q,
    attn_k,
    attn_v,
    attn_out,
    head_gains,
    ffn_gate,
    ffn_up,
    ffn_down,
):
    micro, rows, width = inputs.shape
    section = lax.axis_index("section")
    group = lax.axis_index("fsdp")
    fsdp = lax.axis_size("fsdp")
    assert micro == lax.axis_size("section")
    head = head_gains.shape[1]
    q_width, kv_width = attn_q.shape[1], attn_k.shape[1]
    q_heads, kv_heads = q_width // head, kv_width // head
    positions = lax.axis_index("ctx") * rows + jnp.arange(rows)
    length = lax.dynamic_index_in_dim(lengths, group * micro + section, keepdims=False)
    mask = (positions < length).astype(F32)[:, None]

    def whole_rows(weight):
        half = weight.shape[0] // micro
        mine = lax.dynamic_slice_in_dim(weight, section * half, half, 0)
        return lax.all_gather(mine, ("fsdp", "section"), axis=0, tiled=True)

    def to_columns(weight):
        deep, wide = weight.shape
        blocks = weight.reshape(deep, fsdp, wide // fsdp).transpose(1, 0, 2)
        return swapped_blocks(blocks.reshape(fsdp * deep, wide // fsdp), "fsdp", 2)

    def both(weight):
        other = swapped(weight, "section")
        first = section == 0
        return jnp.where(first, weight, other), jnp.where(first, other, weight)

    in_full = whole_rows(conv_in)
    out_full = whole_rows(conv_out)
    gate_up = to_columns(jnp.concatenate([ffn_gate[0], ffn_up[0]], axis=0))
    part = ffn_gate.shape[1]
    gate_up = gate_up.reshape(fsdp, 2, part, -1)
    gates = both(gate_up[:, 0].reshape(fsdp * part, -1))
    ups = both(gate_up[:, 1].reshape(fsdp * part, -1))
    downs = both(ffn_down[0])
    query_full, key_full, value_full, proj_full = (
        whole_rows(attn_q),
        whole_rows(attn_k),
        whole_rows(attn_v),
        whole_rows(attn_out),
    )

    x = lax.dynamic_index_in_dim(inputs, section, keepdims=False).astype(F32)
    normed0, inv0 = norm_rows(x)
    act1 = (normed0 * norm_gains[0]).astype(BF16)
    projected = matmul(act1, in_full)
    b_gate, c_gate, x_value = (
        projected[:, :width],
        projected[:, width : 2 * width],
        projected[:, 2 * width :],
    )
    b_product = (b_gate * x_value).astype(BF16)
    rim = passed_along(b_product[-2:], "ctx", 1)
    extended = jnp.concatenate([rim, b_product], axis=0).astype(F32)
    convolved = (
        conv_kernel[0] * extended[:-2]
        + conv_kernel[1] * extended[1:-1]
        + conv_kernel[2] * extended[2:]
    )
    z_low = (c_gate * convolved).astype(BF16)
    mixed = matmul(z_low, out_full)
    res1 = x + mixed
    ffn1, kept1 = ffn_forward(res1, norm_gains[1], gates[0], ups[0], downs[0])
    h_low = (res1 + ffn1).astype(BF16)

    h = h_low.astype(F32)
    normed2, inv2 = norm_rows(h)
    act2 = (normed2 * norm_gains[2]).astype(BF16)
    q_normed, q_inv = norm_rows(matmul(act2, query_full).reshape(rows, q_heads, head))
    k_normed, k_inv = norm_rows(matmul(act2, key_full).reshape(rows, kv_heads, head))
    query = (q_normed * head_gains[0]).astype(BF16)
    key = (k_normed * head_gains[1]).astype(BF16)
    value = matmul(act2, value_full).astype(BF16)
    kv_all = gathered(jnp.concatenate([key.reshape(rows, kv_width), value], axis=1), "ctx", 3)
    key_all = kv_all[:, :kv_width].reshape(-1, kv_heads, head)
    value_all = kv_all[:, kv_width:].reshape(-1, kv_heads, head)
    key_pos = jnp.arange(kv_all.shape[0])
    allowed = (key_pos[None, :] <= positions[:, None]) & (key_pos[None, :] < length)
    attended, log_total = attend(query, key_all, value_all, allowed)
    attended_low = attended.astype(BF16)
    attn_rows = matmul(attended_low, proj_full)
    res2 = h + attn_rows
    ffn2, kept2 = ffn_forward(res2, norm_gains[3], gates[1], ups[1], downs[1])
    result = (res2 + ffn2) * mask

    def square(values):
        return jnp.sum(mask * values * values)

    squares = jnp.stack(
        [square(v) for v in (x, mixed, ffn1, h, attn_rows, res2, ffn2, result)]
    )

    d_sum_low = (lax.dynamic_index_in_dim(cotangent, section, keepdims=False).astype(F32) * mask).astype(BF16)
    d_sum = d_sum_low.astype(F32)
    d_ffn, gain3, grads2 = ffn_backward(d_sum_low, kept2, norm_gains[3], gates[1], ups[1], downs[1])
    d_res2 = d_sum + d_ffn
    d_attn = d_res2.astype(BF16)
    grad_proj = matmul_left(attended_low, d_attn)
    d_att = matmul_right(d_attn, proj_full).astype(BF16)
    d_query, d_key_all, d_value_all = attend_back(
        query, key_all, value_all, allowed, log_total, attended, d_att
    )
    d_kv = reduced(
        jnp.concatenate(
            [d_key_all.reshape(-1, kv_width), d_value_all.reshape(-1, kv_width)], axis=1
        ),
        "ctx",
        4,
    )
    d_qn = rounded(d_query)
    grad_qgain = jnp.sum(d_qn * q_normed, axis=(0, 1))
    d_qpre = norm_back(d_qn * head_gains[0], q_normed, q_inv).reshape(rows, -1).astype(BF16)
    d_kn = rounded(d_kv[:, :kv_width]).reshape(rows, kv_heads, head)
    grad_kgain = jnp.sum(d_kn * k_normed, axis=(0, 1))
    d_kpre = norm_back(d_kn * head_gains[1], k_normed, k_inv).reshape(rows, -1).astype(BF16)
    d_vpre = d_kv[:, kv_width:].astype(BF16)
    grad_query = matmul_left(act2, d_qpre)
    grad_key = matmul_left(act2, d_kpre)
    grad_value = matmul_left(act2, d_vpre)
    d_act2 = (
        matmul_right(d_qpre, query_full)
        + matmul_right(d_kpre, key_full)
        + matmul_right(d_vpre, value_full)
    )
    gain2 = jnp.sum(d_act2 * normed2, axis=0)
    d_h_low = (d_res2 + norm_back(d_act2 * norm_gains[2], normed2, inv2)).astype(BF16)

    d_ffn1, gain1, grads1 = ffn_backward(d_h_low, kept1, norm_gains[1], gates[0], ups[0], downs[0])
    d_res1 = d_h_low.astype(F32) + d_ffn1
    d_mixed = d_res1.astype(BF16)
    grad_out = matmul_left(z_low, d_mixed)
    d_z = matmul_right(d_mixed, out_full)
    d_cgate = d_z * convolved
    d_conv = d_z * c_gate
    grad_kernel = jnp.stack(
        [
            jnp.sum(d_conv * extended[:-2], axis=0),
            jnp.sum(d_conv * extended[1:-1], axis=0),
            jnp.sum(d_conv * extended[2:], axis=0),
        ]
    )
    d_extended = (
        jnp.pad(d_conv * conv_kernel[0], ((0, 2), (0, 0)))
        + jnp.pad(d_conv * conv_kernel[1], ((1, 1), (0, 0)))
        + jnp.pad(d_conv * conv_kernel[2], ((2, 0), (0, 0)))
    )
    from_next = passed_along(d_extended[:2], "ctx", -1)
    d_bproduct = rounded(d_extended[2:] + jnp.pad(from_next, ((rows - 2, 0), (0, 0))))
    d_projected = jnp.concatenate(
        [d_bproduct * x_value, d_cgate, d_bproduct * b_gate], axis=1
    ).astype(BF16)
    d_act1 = matmul_right(d_projected, in_full)
    gain0 = jnp.sum(d_act1 * normed0, axis=0)
    d_x = (d_res1 + norm_back(d_act1 * norm_gains[0], normed0, inv0)).astype(BF16)

    y_low = result.astype(BF16)
    is_first = section == 0
    other_end = swapped(jnp.where(is_first, y_low, d_x), "section")
    ends = jnp.where(is_first, jnp.stack([d_x, other_end]), jnp.stack([other_end, y_low]))[None]

    grad_parts = [
        matmul_left(act1, d_projected[:, i * width : (i + 1) * width]).astype(BF16) for i in range(3)
    ]
    attn_half = lax.psum_scatter(
        jnp.concatenate([grad_query, grad_key, grad_value, grad_proj], axis=1).astype(BF16),
        ("fsdp", "section"),
        scatter_dimension=0,
        tiled=True,
    )
    attn_half = jnp.concatenate(
        [attn_half[:, i * width : (i + 1) * width] for i in range(attn_half.shape[1] // width)], axis=0
    )

    half = part // 2

    def shared_halves(grad, lead):
        pieces = grad.reshape(lead, 2, -1, grad.shape[1])
        mine = lax.dynamic_index_in_dim(pieces, section, 1, keepdims=False)
        other = swapped(lax.dynamic_index_in_dim(pieces, 1 - section, 1, keepdims=False), "section")
        return (mine.astype(F32) + other.astype(F32)).astype(BF16)

    second = lax.psum(
        (
            shared_halves(grads2[0], fsdp),
            shared_halves(grads2[1], fsdp),
            shared_halves(grads2[2], 1)[0],
        ),
        "ctx",
    )
    cut = width // fsdp
    head_cut = head // fsdp
    square_cut = squares.shape[0] // fsdp
    by_owner = jnp.concatenate(
        [
            jnp.concatenate([jnp.stack([gain0, gain1, gain2, gain3]), grad_kernel])
            .reshape(7, fsdp, cut)
            .transpose(1, 0, 2)
            .reshape(fsdp, 7 * cut),
            jnp.stack([grad_qgain, grad_kgain])
            .reshape(2, fsdp, head_cut)
            .transpose(1, 0, 2)
            .reshape(fsdp, 2 * head_cut),
            squares.reshape(fsdp, square_cut),
            jnp.zeros((fsdp, cut - 2 * head_cut - square_cut), F32),
        ],
        axis=1,
    ).reshape(fsdp, 1, -1, width)
    small = jnp.pad(by_owner, ((0, 0), (0, 1), (0, 16 - by_owner.shape[2]), (0, 0))).astype(BF16)
    gu_sum, down_sum, rest_sum = summed_gradients(
        grads1,
        attn_half,
        grad_parts + [grad_out.astype(BF16)],
        small,
        jnp.stack([second[0], second[1]]),
        second[2],
    )
    rest_sum = rest_sum.astype(F32)

    def block(index):
        rows_at = slice(index * half, (index + 1) * half)
        return rest_sum[:, rows_at].reshape(2 * half, width)

    attn_blocks = [block(i) for i in range(3)]
    conv_blocks = [block(3 + i) for i in range(4)]
    small_sum = rest_sum[0, 7 * half : 7 * half + 2].reshape(-1)
    mine = small_sum[: 7 * cut].reshape(7, cut)
    heads = small_sum[7 * cut : 7 * cut + 2 * head_cut].reshape(2, head_cut)
    square_sum = small_sum[7 * cut + 2 * head_cut : 7 * cut + 2 * head_cut + square_cut]
    token_total = jnp.sum(lengths).astype(F32) * width
    rms = jnp.sqrt(square_sum / token_total)
    return (
        ends,
        mine[:3],
        mine[3],
        jnp.concatenate(conv_blocks[:3], axis=1),
        mine[4:7],
        conv_blocks[3],
        attn_blocks[0],
        attn_blocks[1][:, :kv_width],
        attn_blocks[1][:, kv_width:],
        attn_blocks[2],
        heads,
        gu_sum[0][None].astype(F32),
        gu_sum[1][None].astype(F32),
        down_sum[None].astype(F32),
        rms,
    )


def solution(mesh):
    return jax.shard_map(
        shards,
        mesh=mesh,
        in_specs=(
            P("fsdp", "ctx", None),
            P("fsdp", "ctx", None),
            P(),
            P(),
            P("fsdp", None),
            P(),
            P("fsdp", None),
            P("fsdp", None),
            P("fsdp", None),
            P("fsdp", None),
            P("fsdp", None),
            P(),
            P("section", "fsdp", None),
            P("section", "fsdp", None),
            P("section", "fsdp", None),
        ),
        out_specs=(
            P("section", "fsdp", "ctx", None),
            P(None, "fsdp"),
            P("fsdp"),
            P("fsdp", None),
            P(None, "fsdp"),
            P("fsdp", None),
            P("fsdp", None),
            P("fsdp", None),
            P("fsdp", None),
            P("fsdp", None),
            P(None, "fsdp"),
            P("section", "fsdp", None),
            P("section", "fsdp", None),
            P("section", "fsdp", None),
            P("fsdp"),
        ),
        check_vma=False,
    )
```

```python
import functools

import jax
import jax.numpy as jnp
from jax import lax
from jax.experimental import pallas as pl
from jax.experimental.pallas import tpu as pltpu
from jax.sharding import PartitionSpec as P

EPSILON = 1e-05
NEGATIVE = -1e30
MESH = pl.DeviceIdType.MESH
F32 = jnp.float32
BF16 = jnp.bfloat16


def passed_along(block, axis, distance):
    devices = range(lax.axis_size(axis))
    route = [(i - distance, i) for i in devices if i - distance in devices]
    return lax.ppermute(block, axis, route)


def swapped(block, axis):
    return lax.ppermute(block, axis, [(0, 1), (1, 0)])


def rounded(values):
    return lax.optimization_barrier(values.astype(BF16)).astype(F32)


def matmul(left_op, right_op):
    return jnp.dot(left_op, right_op, preferred_element_type=F32)


def matmul_left(left_op, right_op):
    return lax.dot_general(left_op, right_op, (((0,), (0,)), ((), ())), preferred_element_type=F32)


def matmul_right(left_op, right_op):
    return lax.dot_general(left_op, right_op, (((1,), (1,)), ((), ())), preferred_element_type=F32)


def norm_rows(values):
    inv_rms = lax.rsqrt(jnp.mean(values * values, axis=-1, keepdims=True) + EPSILON)
    return (values * inv_rms, inv_rms)


def norm_back(dnormed, normed, inv_rms):
    return inv_rms * dnormed - normed * inv_rms * jnp.mean(dnormed * normed, axis=-1, keepdims=True)


def greet(axis, count):
    me = lax.axis_index(axis)
    barrier = pltpu.get_barrier_semaphore()
    for step in range(1, count):
        pl.semaphore_signal(
            barrier,
            inc=1,
            device_id={axis: lax.rem(me + step, count)},
            device_id_type=MESH,
        )
    pl.semaphore_wait(barrier, count - 1)


def gather_kernel(axis, count, rows, block, whole, send_sem, recv_sem, own_sem):
    me = lax.axis_index(axis)
    greet(axis, count)
    own_rows = pl.ds(pl.multiple_of(me * rows, rows), rows)
    copies = []
    for step in range(1, count):
        copy = pltpu.make_async_remote_copy(
            src_ref=block,
            dst_ref=whole.at[own_rows],
            send_sem=send_sem.at[step],
            recv_sem=recv_sem.at[step],
            device_id={axis: lax.rem(me + step, count)},
            device_id_type=MESH,
        )
        copy.start()
        copies.append(copy)
    own = pltpu.make_async_copy(block, whole.at[own_rows], own_sem)
    own.start()
    own.wait()
    for copy in copies:
        copy.wait()


def swap_kernel(axis, count, rows, blocks, whole, send_sem, recv_sem, own_sem):
    me = lax.axis_index(axis)
    greet(axis, count)
    own_rows = pl.ds(pl.multiple_of(me * rows, rows), rows)
    copies = []
    for step in range(1, count):
        target = lax.rem(me + step, count)
        copy = pltpu.make_async_remote_copy(
            src_ref=blocks.at[pl.ds(pl.multiple_of(target * rows, rows), rows)],
            dst_ref=whole.at[own_rows],
            send_sem=send_sem.at[step],
            recv_sem=recv_sem.at[step],
            device_id={axis: target},
            device_id_type=MESH,
        )
        copy.start()
        copies.append(copy)
    own = pltpu.make_async_copy(blocks.at[own_rows], whole.at[own_rows], own_sem)
    own.start()
    own.wait()
    for copy in copies:
        copy.wait()


def exchange(kernel, axis, array, rows, collective_id):
    count = lax.axis_size(axis)
    return pl.pallas_call(
        functools.partial(kernel, axis, count, rows),
        out_shape=jax.ShapeDtypeStruct((count * rows,) + array.shape[1:], array.dtype),
        in_specs=[pl.BlockSpec(memory_space=pl.ANY)],
        out_specs=pl.BlockSpec(memory_space=pl.ANY),
        scratch_shapes=[
            pltpu.SemaphoreType.DMA((count,)),
            pltpu.SemaphoreType.DMA((count,)),
            pltpu.SemaphoreType.DMA,
        ],
        compiler_params=pltpu.CompilerParams(
            collective_id=collective_id, has_side_effects=True, vmem_limit_bytes=8 << 20
        ),
    )(array)


def gathered(array, axis, collective_id):
    return exchange(gather_kernel, axis, array, array.shape[0], collective_id)


def swapped_blocks(array, axis, collective_id):
    return exchange(swap_kernel, axis, array, array.shape[0] // lax.axis_size(axis), collective_id)


def reduced(partial, axis, collective_id):
    count = lax.axis_size(axis)
    terms = swapped_blocks(partial.astype(BF16), axis, collective_id)
    return jnp.sum(terms.reshape(count, -1, partial.shape[1]).astype(F32), axis=0)


def tail_kernel(
    counts,
    gate_in,
    up_in,
    down_in,
    query_in,
    kv_in,
    proj_in,
    conv_b_in,
    conv_c_in,
    conv_x_in,
    conv_o_in,
    small_in,
    second_gu_in,
    second_down_in,
    gu_out,
    down_out,
    rest_out,
    a_own,
    a_other,
    a_sum,
    a_done,
    b_own,
    b_other,
    b_sum,
    b_done,
    c_own,
    c_other,
    c_got,
    own_sem,
    pair_send,
    pair_recv,
    c_own_sem,
    c_pair_send,
    c_pair_recv,
    c_send,
    c_recv,
    a_up_send,
    a_up_recv,
    a_back_send,
    a_back_recv,
    a_out_send,
    b_up_send,
    b_up_recv,
    b_back_send,
    b_back_recv,
    b_out_send,
    b_keep_sem,
    gu_recv,
    down_recv,
    rest_recv,
    second_send,
):
    n_ctx, n_fsdp = counts
    section = lax.axis_index("section")
    place = lax.axis_index("ctx")
    group = lax.axis_index("fsdp")
    other = 1 - section
    a_chunks, a_rows, a_width = a_own.shape
    b_chunks, b_rows, b_width = b_own.shape
    half = gate_in.shape[0] // n_fsdp // 2
    subs = half // a_rows
    per_kind = n_fsdp * subs
    down_half = down_in.shape[0] // 2
    down_chunks = down_half // b_rows
    c_rows = c_own.shape[1]
    mixers = (query_in, kv_in, proj_in, conv_b_in, conv_c_in, conv_x_in, conv_o_in)
    n_mix = len(mixers)
    cut = 3 * half // b_rows
    c_parts = ((0, cut), (cut, c_rows // b_rows))
    ticks = a_chunks // 2
    tail = 2 * (n_ctx - 1)

    barrier = pltpu.get_barrier_semaphore()
    for step in range(1, 2 * n_fsdp):
        flat = lax.rem(section * n_fsdp + group + step, 2 * n_fsdp)
        pl.semaphore_signal(
            barrier,
            inc=1,
            device_id={"section": flat // n_fsdp, "fsdp": lax.rem(flat, n_fsdp)},
            device_id_type=MESH,
        )

    @pl.when(place > 0)
    def _():
        pl.semaphore_signal(barrier, inc=1, device_id={"ctx": place - 1}, device_id_type=MESH)

    @pl.when(place < n_ctx - 1)
    def _():
        pl.semaphore_signal(barrier, inc=1, device_id={"ctx": place + 1}, device_id_type=MESH)

    at_edge = (place == 0) | (place == n_ctx - 1)

    @pl.when(at_edge)
    def _():
        pl.semaphore_wait(barrier, 2 * n_fsdp)

    @pl.when(jnp.logical_not(at_edge))
    def _():
        pl.semaphore_wait(barrier, 2 * n_fsdp + 1)

    def half_rows(owner, which):
        return pl.ds(pl.multiple_of(owner * (2 * half) + which * half, half), half)

    local, pair = [], []
    for kind, source in enumerate((gate_in, up_in)):
        for owner in range(n_fsdp):
            index = kind * n_fsdp + owner
            slot = pl.ds(index * subs, subs)
            for sub in range(subs):
                src_own = source.at[pl.ds(pl.multiple_of(owner * (2 * half) + section * half + sub * a_rows, a_rows), a_rows)]
                src_other = source.at[pl.ds(pl.multiple_of(owner * (2 * half) + other * half + sub * a_rows, a_rows), a_rows)]
                spot = index * subs + sub
                local.append(pltpu.make_async_copy(src_own, a_own.at[spot], own_sem.at[spot]))
                pair.append(
                    pltpu.make_async_remote_copy(
                        src_ref=src_other,
                        dst_ref=a_other.at[spot],
                        send_sem=pair_send.at[spot],
                        recv_sem=pair_recv.at[spot],
                        device_id={"section": other},
                        device_id_type=MESH,
                    )
                )
    for chunk in range(down_chunks):
        spot = a_chunks + chunk
        src_own = down_in.at[pl.ds(pl.multiple_of(section * down_half + chunk * b_rows, b_rows), b_rows)]
        src_other = down_in.at[pl.ds(pl.multiple_of(other * down_half + chunk * b_rows, b_rows), b_rows)]
        local.append(pltpu.make_async_copy(src_own, b_own.at[chunk], own_sem.at[spot]))
        pair.append(
            pltpu.make_async_remote_copy(
                src_ref=src_other,
                dst_ref=b_other.at[chunk],
                send_sem=pair_send.at[spot],
                recv_sem=pair_recv.at[spot],
                device_id={"section": other},
                device_id_type=MESH,
            )
        )
    for copy in pair:
        copy.start()
    for copy in local:
        copy.start()
    c_local, c_pair = ([], []), ([], [])
    for kind, source in enumerate(mixers):
        part = 0 if kind < 3 else 1
        for owner in range(n_fsdp):
            index = owner * (n_mix + 1) + kind
            place_at = pl.ds(kind * half, half)
            c_local[part].append(
                pltpu.make_async_copy(
                    source.at[half_rows(owner, section)], c_own.at[owner, place_at], c_own_sem.at[index]
                )
            )
            c_pair[part].append(
                pltpu.make_async_remote_copy(
                    src_ref=source.at[half_rows(owner, other)],
                    dst_ref=c_other.at[owner, place_at],
                    send_sem=c_pair_send.at[index],
                    recv_sem=c_pair_recv.at[index],
                    device_id={"section": other},
                    device_id_type=MESH,
                )
            )
    for owner in range(n_fsdp):
        small_at = pl.ds(n_mix * half, c_rows - n_mix * half)
        index = owner * (n_mix + 1) + n_mix
        c_local[1].append(
            pltpu.make_async_copy(small_in.at[owner, section], c_own.at[owner, small_at], c_own_sem.at[index])
        )
        c_pair[1].append(
            pltpu.make_async_remote_copy(
                src_ref=small_in.at[owner, other],
                dst_ref=c_other.at[owner, small_at],
                send_sem=c_pair_send.at[index],
                recv_sem=c_pair_recv.at[index],
                device_id={"section": other},
                device_id_type=MESH,
            )
        )
    for part in range(2):
        for copy in c_pair[part]:
            copy.start()
        for copy in c_local[part]:
            copy.start()
    b_own[b_chunks - 1] = jnp.zeros((b_rows, b_width), BF16)
    for copy in local:
        copy.wait()
    for copy in pair:
        copy.wait_recv()

    def mixer_copy(part, step):
        target = lax.rem(group + step, n_fsdp)
        first, last = c_parts[part]
        at = pl.ds(first * b_rows, (last - first) * b_rows)
        return pltpu.make_async_remote_copy(
            src_ref=c_own.at[target, at],
            dst_ref=c_got.at[step - 1, at],
            send_sem=c_send.at[part, step],
            recv_sem=c_recv.at[part, step],
            device_id={"fsdp": target},
            device_id_type=MESH,
        )

    def mixer_out(part):
        for copy in c_local[part]:
            copy.wait()
        for copy in c_pair[part]:
            copy.wait_recv()
        first, last = c_parts[part]
        size = last - first

        def add(index, carry):
            owner = index // size
            at = pl.ds(pl.multiple_of((first + lax.rem(index, size)) * b_rows, b_rows), b_rows)
            c_own[owner, at] = (c_own[owner, at].astype(F32) + c_other[owner, at].astype(F32)).astype(BF16)
            return carry

        lax.fori_loop(0, n_fsdp * size, add, 0)
        for step in range(1, n_fsdp):
            mixer_copy(part, step).start()

    def mixer_in(part):
        for step in range(1, n_fsdp):
            mixer_copy(part, step).wait_recv()
        first, last = c_parts[part]

        def add(index, carry):
            at = pl.ds(pl.multiple_of(index * b_rows, b_rows), b_rows)
            total = c_own[group, at].astype(F32)
            for step in range(1, n_fsdp):
                total = total + c_got[step - 1, at].astype(F32)
            b_own[down_chunks + index] = total.astype(BF16)
            return carry

        lax.fori_loop(first, last, add, 0)

    def second_start():
        for kind in range(2):
            for owner in range(n_fsdp):
                index = kind * n_fsdp + owner
                src = second_gu_in.at[kind, owner]
                dst = gu_out.at[
                    kind,
                    pl.ds(pl.multiple_of(section * half, half), half),
                    pl.ds(pl.multiple_of(group * a_width, 128), a_width),
                ]
                is_mine = (section == 1) & (group == owner)

                @pl.when(is_mine)
                def _(src=src, dst=dst, index=index):
                    pltpu.make_async_copy(src, dst, second_send.at[index]).start()

                @pl.when(jnp.logical_not(is_mine))
                def _(src=src, dst=dst, index=index, kind=kind, owner=owner):
                    pltpu.make_async_remote_copy(
                        src_ref=src,
                        dst_ref=dst,
                        send_sem=second_send.at[index],
                        recv_sem=gu_recv.at[kind, section * n_fsdp + group],
                        device_id={"section": 1, "fsdp": owner},
                        device_id_type=MESH,
                    ).start()

        down_at = down_out.at[pl.ds(pl.multiple_of(section * down_half, b_rows), down_half)]

        @pl.when(section == 1)
        def _():
            pltpu.make_async_copy(second_down_in, down_at, second_send.at[2 * n_fsdp]).start()

        @pl.when(section == 0)
        def _():
            pltpu.make_async_remote_copy(
                src_ref=second_down_in,
                dst_ref=down_at,
                send_sem=second_send.at[2 * n_fsdp],
                recv_sem=down_recv,
                device_id={"section": 1},
                device_id_type=MESH,
            ).start()

    def a_target(k):
        kind = k // per_kind
        rest = lax.rem(k, per_kind)
        owner = rest // subs
        sub = lax.rem(rest, subs)
        spot = gu_out.at[
            kind,
            pl.ds(pl.multiple_of(section * half + sub * a_rows, a_rows), a_rows),
            pl.ds(pl.multiple_of(group * a_width, 128), a_width),
        ]
        return kind, owner, spot

    def hand_out(k):
        kind, owner, spot = a_target(k)
        is_mine = (section == 0) & (group == owner)

        @pl.when(is_mine)
        def _():
            pltpu.make_async_copy(a_done.at[k], spot, a_out_send.at[k]).start()

        @pl.when(jnp.logical_not(is_mine))
        def _():
            pltpu.make_async_remote_copy(
                src_ref=a_done.at[k],
                dst_ref=spot,
                send_sem=a_out_send.at[k],
                recv_sem=gu_recv.at[kind, section * n_fsdp + group],
                device_id={"section": 0, "fsdp": owner},
                device_id_type=MESH,
            ).start()

        @pl.when(k < down_chunks)
        def _():
            at = down_out.at[pl.ds(pl.multiple_of(section * down_half + k * b_rows, b_rows), b_rows)]

            @pl.when(section == 0)
            def _():
                pltpu.make_async_copy(b_done.at[k], at, b_out_send.at[k]).start()

            @pl.when(section == 1)
            def _():
                pltpu.make_async_remote_copy(
                    src_ref=b_done.at[k],
                    dst_ref=at,
                    send_sem=b_out_send.at[k],
                    recv_sem=down_recv,
                    device_id={"section": 0},
                    device_id_type=MESH,
                ).start()

        @pl.when(k >= down_chunks)
        def _():
            at = rest_out.at[section, pl.ds(pl.multiple_of((k - down_chunks) * b_rows, b_rows), b_rows)]
            pltpu.make_async_copy(b_done.at[k], at, b_keep_sem.at[k]).start()
            pltpu.make_async_remote_copy(
                src_ref=b_done.at[k],
                dst_ref=at,
                send_sem=b_out_send.at[k],
                recv_sem=rest_recv,
                device_id={"section": other},
                device_id_type=MESH,
            ).start()

    def up_copies(k, target):
        return (
            pltpu.make_async_remote_copy(
                src_ref=a_sum.at[k],
                dst_ref=a_sum.at[k],
                send_sem=a_up_send.at[k],
                recv_sem=a_up_recv.at[k],
                device_id={"ctx": target},
                device_id_type=MESH,
            ),
            pltpu.make_async_remote_copy(
                src_ref=b_sum.at[k],
                dst_ref=b_sum.at[k],
                send_sem=b_up_send.at[k],
                recv_sem=b_up_recv.at[k],
                device_id={"ctx": target},
                device_id_type=MESH,
            ),
        )

    def back_copies(k, target):
        return (
            pltpu.make_async_remote_copy(
                src_ref=a_done.at[k],
                dst_ref=a_done.at[k],
                send_sem=a_back_send.at[k],
                recv_sem=a_back_recv.at[k],
                device_id={"ctx": target},
                device_id_type=MESH,
            ),
            pltpu.make_async_remote_copy(
                src_ref=b_done.at[k],
                dst_ref=b_done.at[k],
                send_sem=b_back_send.at[k],
                recv_sem=b_back_recv.at[k],
                device_id={"ctx": target},
                device_id_type=MESH,
            ),
        )

    def own_term(k):
        @pl.when(k < down_chunks)
        def _():
            b_own[k] = (b_own[k].astype(F32) + b_other[k].astype(F32)).astype(BF16)

        return a_own[k].astype(F32) + a_other[k].astype(F32)

    lanes = []
    for way in range(2):
        rank = place if way == 0 else n_ctx - 1 - place
        ahead = place + 1 if way == 0 else place - 1
        behind = place - 1 if way == 0 else place + 1
        lanes.append((way, rank, ahead, behind))

    def tick_step(tick, carry):
        @pl.when(tick == 0)
        def _():
            mixer_out(0)

        @pl.when(tick == 2)
        def _():
            mixer_out(1)

        @pl.when(tick == down_chunks // 2)
        def _():
            mixer_in(0)

        @pl.when(tick == (down_chunks + cut) // 2)
        def _():
            mixer_in(1)
            second_start()

        for way, rank, ahead, behind in lanes:
            step = tick - rank
            k = 2 * jnp.clip(step, 0, ticks - 1) + way

            @pl.when((step >= 0) & (step < ticks))
            def _(k=k, rank=rank, ahead=ahead, behind=behind):
                term = own_term(k)

                @pl.when(rank == 0)
                def _():
                    a_sum[k] = term.astype(BF16)
                    b_sum[k] = b_own[k]

                @pl.when(rank > 0)
                def _():
                    for copy in up_copies(k, behind):
                        copy.wait_recv()

                @pl.when((rank > 0) & (rank < n_ctx - 1))
                def _():
                    a_sum[k] = (term + a_sum[k].astype(F32)).astype(BF16)
                    b_sum[k] = (b_own[k].astype(F32) + b_sum[k].astype(F32)).astype(BF16)

                @pl.when(rank < n_ctx - 1)
                def _():
                    for copy in up_copies(k, ahead):
                        copy.start()

                @pl.when(rank == n_ctx - 1)
                def _():
                    a_done[k] = (term + a_sum[k].astype(F32)).astype(BF16)
                    b_done[k] = (b_own[k].astype(F32) + b_sum[k].astype(F32)).astype(BF16)
                    for copy in back_copies(k, behind):
                        copy.start()
                    hand_out(k)

            late = tick - (tail - rank)
            j = 2 * jnp.clip(late, 0, ticks - 1) + way

            @pl.when((late >= 0) & (late < ticks) & (rank < n_ctx - 1))
            def _(j=j, rank=rank, ahead=ahead, behind=behind):
                for copy in back_copies(j, ahead):
                    copy.wait_recv()

                @pl.when(rank > 0)
                def _():
                    for copy in back_copies(j, behind):
                        copy.start()

                hand_out(j)

        return carry

    lax.fori_loop(0, ticks + tail, tick_step, 0)

    for copy in pair:
        copy.wait_send()
    for part in range(2):
        for copy in c_pair[part]:
            copy.wait_send()
        for step in range(1, n_fsdp):
            mixer_copy(part, step).wait_send()

    def settle(step, carry):
        for way, rank, ahead, behind in lanes:
            k = 2 * step + way

            @pl.when(rank < n_ctx - 1)
            def _(k=k, ahead=ahead):
                for copy in up_copies(k, ahead):
                    copy.wait_send()

            @pl.when(rank > 0)
            def _(k=k, behind=behind):
                for copy in back_copies(k, behind):
                    copy.wait_send()

            _, _, spot = a_target(k)
            pltpu.make_async_copy(a_done.at[k], spot, a_out_send.at[k]).wait()
            pltpu.make_async_copy(b_done.at[k], b_own.at[k], b_out_send.at[k]).wait()

            @pl.when(k >= down_chunks)
            def _(k=k):
                pltpu.make_async_copy(b_done.at[k], b_own.at[k], b_keep_sem.at[k]).wait()

        return carry

    lax.fori_loop(0, ticks, settle, 0)
    for kind in range(2):
        for owner in range(n_fsdp):
            src = second_gu_in.at[kind, owner]
            pltpu.make_async_copy(src, src, second_send.at[kind * n_fsdp + owner]).wait()
    pltpu.make_async_copy(second_down_in, second_down_in, second_send.at[2 * n_fsdp]).wait()
    for kind in range(2):
        for source in range(2 * n_fsdp):

            @pl.when(section * n_fsdp + group != source)
            def _(kind=kind, source=source):
                region = gu_out.at[
                    kind,
                    pl.ds((source // n_fsdp) * half, half),
                    pl.ds((source % n_fsdp) * a_width, a_width),
                ]
                pltpu.make_async_copy(region, region, gu_recv.at[kind, source]).wait()

    region = down_out.at[pl.ds(pl.multiple_of(other * down_half, b_rows), down_half)]
    pltpu.make_async_copy(region, region, down_recv).wait()
    region = rest_out.at[other]
    pltpu.make_async_copy(region, region, rest_recv).wait()


def summed_gradients(first, mixers, small, second_gu, second_down):
    n_ctx, n_fsdp = lax.axis_size("ctx"), lax.axis_size("fsdp")
    gate, up, down = first
    half = gate.shape[0] // n_fsdp // 2
    a_rows, b_rows = half // 4, half * 3 // 8
    a_chunks = 2 * n_fsdp * 4
    a_width, b_width = gate.shape[1], down.shape[1]
    c_rows = len(mixers) * half + small.shape[2]
    down_chunks = down.shape[0] // 2 // b_rows
    b_chunks = down_chunks + c_rows // b_rows + 1
    assert a_chunks == b_chunks and c_rows % b_rows == 0
    rest = b_chunks - down_chunks
    dma = pltpu.SemaphoreType.DMA
    loads = a_chunks + down_chunks
    pieces = n_fsdp * (len(mixers) + 1)
    return pl.pallas_call(
        functools.partial(tail_kernel, (n_ctx, n_fsdp)),
        out_shape=(
            jax.ShapeDtypeStruct((2, 2 * half, n_fsdp * a_width), BF16),
            jax.ShapeDtypeStruct(down.shape, BF16),
            jax.ShapeDtypeStruct((2, rest * b_rows, b_width), BF16),
        ),
        in_specs=[pl.BlockSpec(memory_space=pl.ANY)] * (6 + len(mixers)),
        out_specs=[pl.BlockSpec(memory_space=pl.ANY)] * 3,
        scratch_shapes=[
            pltpu.VMEM((a_chunks, a_rows, a_width), BF16),
            pltpu.VMEM((a_chunks, a_rows, a_width), BF16),
            pltpu.VMEM((a_chunks, a_rows, a_width), BF16),
            pltpu.VMEM((a_chunks, a_rows, a_width), BF16),
            pltpu.VMEM((b_chunks, b_rows, b_width), BF16),
            pltpu.VMEM((down_chunks, b_rows, b_width), BF16),
            pltpu.VMEM((b_chunks, b_rows, b_width), BF16),
            pltpu.VMEM((b_chunks, b_rows, b_width), BF16),
            pltpu.VMEM((n_fsdp, c_rows, b_width), BF16),
            pltpu.VMEM((n_fsdp, c_rows, b_width), BF16),
            pltpu.VMEM((n_fsdp - 1, c_rows, b_width), BF16),
            dma((loads,)),
            dma((loads,)),
            dma((loads,)),
            dma((pieces,)),
            dma((pieces,)),
            dma((pieces,)),
            dma((2, n_fsdp)),
            dma((2, n_fsdp)),
            dma((a_chunks,)),
            dma((a_chunks,)),
            dma((a_chunks,)),
            dma((a_chunks,)),
            dma((a_chunks,)),
            dma((b_chunks,)),
            dma((b_chunks,)),
            dma((b_chunks,)),
            dma((b_chunks,)),
            dma((b_chunks,)),
            dma((b_chunks,)),
            dma((2, 2 * n_fsdp)),
            dma,
            dma,
            dma((2 * n_fsdp + 1,)),
        ],
        compiler_params=pltpu.CompilerParams(
            collective_id=6, has_side_effects=True, vmem_limit_bytes=56 << 20
        ),
    )(gate, up, down, *mixers, small, second_gu, second_down)


def mixer_weights_kernel(count, first_in, second_in, first_out, second_out, send_sem, recv_sem, pair_send, pair_recv, own_sem):
    section = lax.axis_index("section")
    me = lax.axis_index("fsdp")
    other = 1 - section
    beside = me + 1 - 2 * lax.rem(me, 2)
    across = lax.rem(me + 2, count)
    opposite = lax.rem(beside + 2, count)
    rows = first_in.shape[0]
    half = rows // 2
    quarter = half // 2
    barrier = pltpu.get_barrier_semaphore()
    for target in ({"fsdp": beside}, {"fsdp": across}, {"section": other}):
        pl.semaphore_signal(barrier, inc=1, device_id=target, device_id_type=MESH)
    pl.semaphore_wait(barrier, 3)
    arrays = ((first_in, first_out), (second_in, second_out))

    def at_rows(owner, extra, size):
        return pl.ds(pl.multiple_of(owner * rows + extra, quarter), size)

    def remote(slot, sems, src, dst, target):
        return pltpu.make_async_remote_copy(
            src_ref=src,
            dst_ref=dst,
            send_sem=sems[0].at[slot],
            recv_sem=sems[1].at[slot],
            device_id=target,
            device_id_type=MESH,
        )

    hop, pair = (send_sem, recv_sem), (pair_send, pair_recv)
    waiting = []
    direct = []
    for index, (source, out) in enumerate(arrays):
        mine = source.at[pl.ds(pl.multiple_of(section * half, half), half)]
        spot = out.at[at_rows(me, section * half, half)]
        copies = [
            remote(index * 4, hop, mine, spot, {"fsdp": beside}),
            remote(index * 4 + 1, hop, mine, spot, {"fsdp": across}),
        ]
        for copy in copies:
            copy.start()
        direct.append(copies)
    own = [
        pltpu.make_async_copy(source, out.at[at_rows(me, 0, rows)], own_sem.at[index])
        for index, (source, out) in enumerate(arrays)
    ]
    for copy in own:
        copy.start()

    def arrived(owner, size, extra):
        return lambda out: out.at[at_rows(owner, section * half + extra, size)]

    onward = []
    for index, (source, out) in enumerate(arrays):
        direct[index][0].wait_recv()
        part = arrived(beside, quarter, 0)(out)
        onward.append(remote(index * 4 + 2, hop, part, part, {"fsdp": across}))
        onward[-1].start()
        whole = arrived(beside, half, 0)(out)
        waiting.append(remote(index * 4, pair, whole, whole, {"section": other}))
        waiting[-1].start()
        direct[index][1].wait_recv()
        part = arrived(across, quarter, quarter)(out)
        onward.append(remote(index * 4 + 3, hop, part, part, {"fsdp": beside}))
        onward[-1].start()
        whole = arrived(across, half, 0)(out)
        waiting.append(remote(index * 4 + 1, pair, whole, whole, {"section": other}))
        waiting[-1].start()
    for index, (source, out) in enumerate(arrays):
        for turn in range(2):
            onward[2 * index + turn].wait_recv()
            part = arrived(opposite, quarter, turn * quarter)(out)
            waiting.append(remote(index * 4 + 2 + turn, pair, part, part, {"section": other}))
            waiting[-1].start()
    for copy in own:
        copy.wait()
    for copies in direct:
        for copy in copies:
            copy.wait_send()
    for copy in onward:
        copy.wait_send()
    for copy in waiting:
        copy.wait()


def mixer_weights(first, second, collective_id):
    count = lax.axis_size("fsdp")
    dma = pltpu.SemaphoreType.DMA
    return pl.pallas_call(
        functools.partial(mixer_weights_kernel, count),
        out_shape=tuple(
            jax.ShapeDtypeStruct((count * w.shape[0], w.shape[1]), w.dtype) for w in (first, second)
        ),
        in_specs=[pl.BlockSpec(memory_space=pl.ANY)] * 2,
        out_specs=[pl.BlockSpec(memory_space=pl.ANY)] * 2,
        scratch_shapes=[dma((8,)), dma((8,)), dma((8,)), dma((8,)), dma((2,))],
        compiler_params=pltpu.CompilerParams(
            collective_id=collective_id, has_side_effects=True, vmem_limit_bytes=8 << 20
        ),
    )(first, second)


def column_weights_kernel(count, holder, n_ctx, *refs):
    if n_ctx > 1:
        kv_in, refs = refs[0], refs[1:]
    gate_in, up_in, down_in, gate_out, up_out, down_out = refs[:6]
    refs = refs[6:]
    if n_ctx > 1:
        kv_out, refs = refs[0], refs[1:]
    send_sem, recv_sem, pair_send, pair_recv, own_sem = refs[:5]
    section = lax.axis_index("section")
    me = lax.axis_index("fsdp")
    place = lax.axis_index("ctx")
    other = 1 - section
    rows = gate_in.shape[0]
    wide = gate_out.shape[1]
    barrier = pltpu.get_barrier_semaphore()
    for step in range(1, count):
        pl.semaphore_signal(
            barrier, inc=1, device_id={"fsdp": lax.rem(me + step, count)}, device_id_type=MESH
        )
    pl.semaphore_signal(barrier, inc=1, device_id={"section": other}, device_id_type=MESH)
    for step in range(1, n_ctx):
        pl.semaphore_signal(
            barrier, inc=1, device_id={"ctx": lax.rem(place + step, n_ctx)}, device_id_type=MESH
        )
    pl.semaphore_wait(barrier, count + n_ctx - 1)
    kv_copies = []
    if n_ctx > 1:
        kv_send, kv_recv, kv_own = refs[5:]
        kv_rows = kv_in.shape[0]
        spot = kv_out.at[pl.ds(pl.multiple_of(place * kv_rows, kv_rows), kv_rows)]
        for step in range(1, n_ctx):
            kv_copies.append(
                pltpu.make_async_remote_copy(
                    src_ref=kv_in,
                    dst_ref=spot,
                    send_sem=kv_send.at[step],
                    recv_sem=kv_recv.at[step],
                    device_id={"ctx": lax.rem(place + step, n_ctx)},
                    device_id_type=MESH,
                )
            )
            kv_copies[-1].start()
        kv_keep = pltpu.make_async_copy(kv_in, spot, kv_own)
        kv_keep.start()
    arrays = ((gate_in, gate_out), (up_in, up_out))

    def at_rows(out, owner):
        return out.at[pl.ds(pl.multiple_of(owner * rows, rows), rows)]

    def crossing(kind, step):
        source, out = arrays[kind]
        target = lax.rem(me + step, count)
        return pltpu.make_async_remote_copy(
            src_ref=source.at[:, pl.ds(pl.multiple_of(target * wide, 128), wide)],
            dst_ref=at_rows(out, me),
            send_sem=send_sem.at[kind, step],
            recv_sem=recv_sem.at[kind, step],
            device_id={"fsdp": target},
            device_id_type=MESH,
        )

    def handed(kind, step):
        source, out = arrays[kind]
        origin = lax.rem(me + count - step, count)
        if step == 0:
            src = source.at[:, pl.ds(pl.multiple_of(me * wide, 128), wide)]
        else:
            src = at_rows(out, origin)
        return pltpu.make_async_remote_copy(
            src_ref=src,
            dst_ref=at_rows(out, origin),
            send_sem=pair_send.at[kind, step],
            recv_sem=pair_recv.at[kind, step],
            device_id={"section": other},
            device_id_type=MESH,
        )

    down_copy = pltpu.make_async_remote_copy(
        src_ref=down_in,
        dst_ref=down_out,
        send_sem=pair_send.at[2, 0],
        recv_sem=pair_recv.at[2, 0],
        device_id={"section": other},
        device_id_type=MESH,
    )
    kinds = range(2)

    @pl.when(section == holder)
    def _():
        for step in range(1, count):
            for kind in kinds:
                crossing(kind, step).start()
        for kind in kinds:
            handed(kind, 0).start()
        down_copy.start()
        keep = [
            pltpu.make_async_copy(
                arrays[kind][0].at[:, pl.ds(pl.multiple_of(me * wide, 128), wide)],
                at_rows(arrays[kind][1], me),
                own_sem.at[kind],
            )
            for kind in kinds
        ] + [pltpu.make_async_copy(down_in, down_out, own_sem.at[2])]
        for copy in keep:
            copy.start()
        for step in range(1, count):
            for kind in kinds:
                crossing(kind, step).wait_recv()
                handed(kind, step).start()
        for copy in keep:
            copy.wait()
        for step in range(1, count):
            for kind in kinds:
                crossing(kind, step).wait_send()
        for step in range(count):
            for kind in kinds:
                handed(kind, step).wait_send()
        down_copy.wait_send()

    @pl.when(section != holder)
    def _():
        for step in range(count):
            for kind in kinds:
                handed(kind, step).wait_recv()
        down_copy.wait_recv()

    if n_ctx > 1:
        kv_keep.wait()
        for copy in kv_copies:
            copy.wait()


def column_weights(gate, up, down, holder, collective_id, kv=None):
    count = lax.axis_size("fsdp")
    n_ctx = 1 if kv is None else lax.axis_size("ctx")
    dma = pltpu.SemaphoreType.DMA
    column = jax.ShapeDtypeStruct((count * gate.shape[0], gate.shape[1] // count), gate.dtype)
    outs = [column, column, jax.ShapeDtypeStruct(down.shape, down.dtype)]
    ins = [gate, up, down]
    sems = [dma((2, count)), dma((2, count)), dma((3, count)), dma((3, count)), dma((3,))]
    if kv is not None:
        ins = [kv] + ins
        outs.append(jax.ShapeDtypeStruct((n_ctx * kv.shape[0], kv.shape[1]), kv.dtype))
        sems += [dma((n_ctx,)), dma((n_ctx,)), dma]
    return pl.pallas_call(
        functools.partial(column_weights_kernel, count, holder, n_ctx),
        out_shape=tuple(outs),
        in_specs=[pl.BlockSpec(memory_space=pl.ANY)] * len(ins),
        out_specs=[pl.BlockSpec(memory_space=pl.ANY)] * len(outs),
        scratch_shapes=sems,
        compiler_params=pltpu.CompilerParams(
            collective_id=collective_id, has_side_effects=True, vmem_limit_bytes=8 << 20
        ),
    )(*ins)


def attend(query, key_all, value_all, allowed):
    kv_heads = key_all.shape[1]
    rows, q_heads, head = query.shape
    grouped = query.reshape(rows, kv_heads, q_heads // kv_heads, head)
    scores = jnp.einsum("qghd,kgd->ghqk", grouped, key_all, preferred_element_type=F32) * head ** (-0.5)
    scores = jnp.where(allowed, scores, NEGATIVE)
    peak = jnp.max(scores, axis=-1, keepdims=True)
    weights = jnp.where(allowed, jnp.exp(scores - peak), 0.0)
    total = jnp.sum(weights, axis=-1, keepdims=True)
    log_total = peak + jnp.log(total)
    prob = (weights / total).astype(BF16)
    out = jnp.einsum("ghqk,kgd->qghd", prob, value_all, preferred_element_type=F32)
    return out.reshape(rows, q_heads * head), log_total


def attend_back(query, key_all, value_all, allowed, log_total, attended, d_out):
    kv_heads = key_all.shape[1]
    rows, q_heads, head = query.shape
    scale = head ** (-0.5)
    grouped = query.reshape(rows, kv_heads, q_heads // kv_heads, head)
    d_group = d_out.reshape(rows, kv_heads, q_heads // kv_heads, head)
    delta = jnp.sum(d_group.astype(F32) * attended.reshape(d_group.shape), axis=-1)
    scores = jnp.einsum("qghd,kgd->ghqk", grouped, key_all, preferred_element_type=F32) * scale
    prob = jnp.where(allowed, jnp.exp(scores - log_total), 0.0)
    d_prob = jnp.einsum("qghd,kgd->ghqk", d_group, value_all, preferred_element_type=F32)
    d_scores = (prob * (d_prob - delta.transpose(1, 2, 0)[..., None])).astype(BF16)
    d_query = jnp.einsum("ghqk,kgd->qghd", d_scores, key_all, preferred_element_type=F32) * scale
    d_key = jnp.einsum("ghqk,qghd->kgd", d_scores, grouped, preferred_element_type=F32) * scale
    d_value = jnp.einsum("ghqk,qghd->kgd", prob.astype(BF16), d_group, preferred_element_type=F32)
    return d_query.reshape(rows, q_heads, head), d_key, d_value


def ffn_forward(residual, gain, w_gate, w_up, w_down):
    normed, inv_rms = norm_rows(residual)
    act = gathered((normed * gain).astype(BF16), "fsdp", 0)
    gate_pre = matmul(act, w_gate)
    up_pre = matmul(act, w_up)
    hidden = (jax.nn.silu(gate_pre) * up_pre).astype(BF16)
    out = reduced(matmul(hidden, w_down), "fsdp", 1)
    return out, (normed, inv_rms, act, gate_pre, up_pre, hidden)


def ffn_backward(d_low, kept, gain, w_gate, w_up, w_down):
    normed, inv_rms, act, gate_pre, up_pre, hidden = kept
    d_all = gathered(d_low, "fsdp", 0)
    d_hidden = matmul_right(d_all, w_down)
    sigmoid = jax.nn.sigmoid(gate_pre)
    d_up = (d_hidden * gate_pre * sigmoid).astype(BF16)
    d_gate = (d_hidden * up_pre * sigmoid * (1.0 + gate_pre * (1.0 - sigmoid))).astype(BF16)
    d_act = reduced(matmul_right(d_gate, w_gate) + matmul_right(d_up, w_up), "fsdp", 1)
    grad_gate = matmul_left(act, d_gate).astype(BF16)
    grad_up = matmul_left(act, d_up).astype(BF16)
    grad_down = matmul_left(hidden, d_all).astype(BF16)
    grad_gain = jnp.sum(d_act * normed, axis=0)
    return norm_back(d_act * gain, normed, inv_rms), grad_gain, (grad_gate, grad_up, grad_down)


def shards(
    inputs,
    cotangent,
    lengths,
    norm_gains,
    conv_in,
    conv_kernel,
    conv_out,
    attn_q,
    attn_k,
    attn_v,
    attn_out,
    head_gains,
    ffn_gate,
    ffn_up,
    ffn_down,
):
    micro, rows, width = inputs.shape
    section = lax.axis_index("section")
    group = lax.axis_index("fsdp")
    fsdp = lax.axis_size("fsdp")
    assert micro == lax.axis_size("section")
    head = head_gains.shape[1]
    q_width, kv_width = attn_q.shape[1], attn_k.shape[1]
    q_heads, kv_heads = q_width // head, kv_width // head
    positions = lax.axis_index("ctx") * rows + jnp.arange(rows)
    length = lax.dynamic_index_in_dim(lengths, group * micro + section, keepdims=False)
    mask = (positions < length).astype(F32)[:, None]

    def whole_rows(weight):
        half = weight.shape[0] // micro
        mine = lax.dynamic_slice_in_dim(weight, section * half, half, 0)
        return lax.all_gather(mine, ("fsdp", "section"), axis=0, tiled=True)

    part = ffn_gate.shape[1]
    in_full, out_full = mixer_weights(conv_in, conv_out, 2)
    gate1, up1, down1 = column_weights(ffn_gate[0], ffn_up[0], ffn_down[0], 0, 7)
    query_full, key_full, value_full, proj_full = (
        whole_rows(attn_q),
        whole_rows(attn_k),
        whole_rows(attn_v),
        whole_rows(attn_out),
    )

    x = lax.dynamic_index_in_dim(inputs, section, keepdims=False).astype(F32)
    normed0, inv0 = norm_rows(x)
    act1 = (normed0 * norm_gains[0]).astype(BF16)
    projected = matmul(act1, in_full)
    b_gate, c_gate, x_value = (
        projected[:, :width],
        projected[:, width : 2 * width],
        projected[:, 2 * width :],
    )
    b_product = (b_gate * x_value).astype(BF16)
    rim = passed_along(b_product[-2:], "ctx", 1)
    extended = jnp.concatenate([rim, b_product], axis=0).astype(F32)
    convolved = (
        conv_kernel[0] * extended[:-2]
        + conv_kernel[1] * extended[1:-1]
        + conv_kernel[2] * extended[2:]
    )
    z_low = (c_gate * convolved).astype(BF16)
    mixed = matmul(z_low, out_full)
    res1 = x + mixed
    ffn1, kept1 = ffn_forward(res1, norm_gains[1], gate1, up1, down1)
    h_low = (res1 + ffn1).astype(BF16)

    h = h_low.astype(F32)
    normed2, inv2 = norm_rows(h)
    act2 = (normed2 * norm_gains[2]).astype(BF16)
    q_normed, q_inv = norm_rows(matmul(act2, query_full).reshape(rows, q_heads, head))
    k_normed, k_inv = norm_rows(matmul(act2, key_full).reshape(rows, kv_heads, head))
    query = (q_normed * head_gains[0]).astype(BF16)
    key = (k_normed * head_gains[1]).astype(BF16)
    value = matmul(act2, value_full).astype(BF16)
    gate2, up2, down2, kv_all = column_weights(
        ffn_gate[0],
        ffn_up[0],
        ffn_down[0],
        1,
        3,
        jnp.concatenate([key.reshape(rows, kv_width), value], axis=1),
    )
    key_all = kv_all[:, :kv_width].reshape(-1, kv_heads, head)
    value_all = kv_all[:, kv_width:].reshape(-1, kv_heads, head)
    key_pos = jnp.arange(kv_all.shape[0])
    allowed = (key_pos[None, :] <= positions[:, None]) & (key_pos[None, :] < length)
    attended, log_total = attend(query, key_all, value_all, allowed)
    attended_low = attended.astype(BF16)
    attn_rows = matmul(attended_low, proj_full)
    res2 = h + attn_rows
    ffn2, kept2 = ffn_forward(res2, norm_gains[3], gate2, up2, down2)
    result = (res2 + ffn2) * mask

    def square(values):
        return jnp.sum(mask * values * values)

    squares = jnp.stack(
        [square(v) for v in (x, mixed, ffn1, h, attn_rows, res2, ffn2, result)]
    )

    d_sum_low = (lax.dynamic_index_in_dim(cotangent, section, keepdims=False).astype(F32) * mask).astype(BF16)
    d_sum = d_sum_low.astype(F32)
    d_ffn, gain3, grads2 = ffn_backward(d_sum_low, kept2, norm_gains[3], gate2, up2, down2)
    d_res2 = d_sum + d_ffn
    d_attn = d_res2.astype(BF16)
    grad_proj = matmul_left(attended_low, d_attn)
    d_att = matmul_right(d_attn, proj_full).astype(BF16)
    d_query, d_key_all, d_value_all = attend_back(
        query, key_all, value_all, allowed, log_total, attended, d_att
    )
    d_kv = reduced(
        jnp.concatenate(
            [d_key_all.reshape(-1, kv_width), d_value_all.reshape(-1, kv_width)], axis=1
        ),
        "ctx",
        4,
    )
    d_qn = rounded(d_query)
    grad_qgain = jnp.sum(d_qn * q_normed, axis=(0, 1))
    d_qpre = norm_back(d_qn * head_gains[0], q_normed, q_inv).reshape(rows, -1).astype(BF16)
    d_kn = rounded(d_kv[:, :kv_width]).reshape(rows, kv_heads, head)
    grad_kgain = jnp.sum(d_kn * k_normed, axis=(0, 1))
    d_kpre = norm_back(d_kn * head_gains[1], k_normed, k_inv).reshape(rows, -1).astype(BF16)
    d_vpre = d_kv[:, kv_width:].astype(BF16)
    d_act2 = (
        matmul_right(d_qpre, query_full)
        + matmul_right(d_kpre, key_full)
        + matmul_right(d_vpre, value_full)
    )
    gain2 = jnp.sum(d_act2 * normed2, axis=0)
    d_h_low = (d_res2 + norm_back(d_act2 * norm_gains[2], normed2, inv2)).astype(BF16)

    d_ffn1, gain1, grads1 = ffn_backward(d_h_low, kept1, norm_gains[1], gate1, up1, down1)
    d_res1 = d_h_low.astype(F32) + d_ffn1
    d_mixed = d_res1.astype(BF16)
    grad_out = matmul_left(z_low, d_mixed)
    d_z = matmul_right(d_mixed, out_full)
    d_cgate = d_z * convolved
    d_conv = d_z * c_gate
    grad_kernel = jnp.stack(
        [
            jnp.sum(d_conv * extended[:-2], axis=0),
            jnp.sum(d_conv * extended[1:-1], axis=0),
            jnp.sum(d_conv * extended[2:], axis=0),
        ]
    )
    d_extended = (
        jnp.pad(d_conv * conv_kernel[0], ((0, 2), (0, 0)))
        + jnp.pad(d_conv * conv_kernel[1], ((1, 1), (0, 0)))
        + jnp.pad(d_conv * conv_kernel[2], ((2, 0), (0, 0)))
    )
    from_next = passed_along(d_extended[:2], "ctx", -1)
    d_bproduct = rounded(d_extended[2:] + jnp.pad(from_next, ((rows - 2, 0), (0, 0))))
    d_projected = jnp.concatenate(
        [d_bproduct * x_value, d_cgate, d_bproduct * b_gate], axis=1
    ).astype(BF16)
    d_act1 = matmul_right(d_projected, in_full)
    gain0 = jnp.sum(d_act1 * normed0, axis=0)
    d_x = (d_res1 + norm_back(d_act1 * norm_gains[0], normed0, inv0)).astype(BF16)

    y_low = result.astype(BF16)
    is_first = section == 0
    other_end = swapped(jnp.where(is_first, y_low, d_x), "section")
    ends = jnp.where(is_first, jnp.stack([d_x, other_end]), jnp.stack([other_end, y_low]))[None]

    grad_parts = [
        matmul_left(act1, d_projected[:, i * width : (i + 1) * width]).astype(BF16) for i in range(3)
    ]
    mixers = [
        matmul_left(act2, d_qpre).astype(BF16),
        matmul_left(act2, jnp.concatenate([d_kpre, d_vpre], axis=1)).astype(BF16),
        grad_proj.astype(BF16),
    ] + grad_parts + [grad_out.astype(BF16)]

    half = part // 2

    def shared_halves(grad, lead):
        pieces = grad.reshape(lead, 2, -1, grad.shape[1])
        mine = lax.dynamic_index_in_dim(pieces, section, 1, keepdims=False)
        other = swapped(lax.dynamic_index_in_dim(pieces, 1 - section, 1, keepdims=False), "section")
        return (mine.astype(F32) + other.astype(F32)).astype(BF16)

    second = lax.psum(
        (
            shared_halves(grads2[0], fsdp),
            shared_halves(grads2[1], fsdp),
            shared_halves(grads2[2], 1)[0],
        ),
        "ctx",
    )
    cut = width // fsdp
    head_cut = head // fsdp
    square_cut = squares.shape[0] // fsdp
    by_owner = jnp.concatenate(
        [
            jnp.concatenate([jnp.stack([gain0, gain1, gain2, gain3]), grad_kernel])
            .reshape(7, fsdp, cut)
            .transpose(1, 0, 2)
            .reshape(fsdp, 7 * cut),
            jnp.stack([grad_qgain, grad_kgain])
            .reshape(2, fsdp, head_cut)
            .transpose(1, 0, 2)
            .reshape(fsdp, 2 * head_cut),
            squares.reshape(fsdp, square_cut),
            jnp.zeros((fsdp, cut - 2 * head_cut - square_cut), F32),
        ],
        axis=1,
    ).reshape(fsdp, 1, -1, width)
    small = jnp.pad(by_owner, ((0, 0), (0, 1), (0, 16 - by_owner.shape[2]), (0, 0))).astype(BF16)
    gu_sum, down_sum, rest_sum = summed_gradients(
        grads1,
        mixers,
        small,
        jnp.stack([second[0], second[1]]),
        second[2],
    )
    rest_sum = rest_sum.astype(F32)

    def block(index):
        rows_at = slice(index * half, (index + 1) * half)
        return rest_sum[:, rows_at].reshape(2 * half, width)

    attn_blocks = [block(i) for i in range(3)]
    conv_blocks = [block(3 + i) for i in range(4)]
    small_sum = rest_sum[0, 7 * half : 7 * half + 2].reshape(-1)
    mine = small_sum[: 7 * cut].reshape(7, cut)
    heads = small_sum[7 * cut : 7 * cut + 2 * head_cut].reshape(2, head_cut)
    square_sum = small_sum[7 * cut + 2 * head_cut : 7 * cut + 2 * head_cut + square_cut]
    token_total = jnp.sum(lengths).astype(F32) * width
    rms = jnp.sqrt(square_sum / token_total)
    return (
        ends,
        mine[:3],
        mine[3],
        jnp.concatenate(conv_blocks[:3], axis=1),
        mine[4:7],
        conv_blocks[3],
        attn_blocks[0],
        attn_blocks[1][:, :kv_width],
        attn_blocks[1][:, kv_width:],
        attn_blocks[2],
        heads,
        gu_sum[0][None].astype(F32),
        gu_sum[1][None].astype(F32),
        down_sum[None].astype(F32),
        rms,
    )


def solution(mesh):
    return jax.shard_map(
        shards,
        mesh=mesh,
        in_specs=(
            P("fsdp", "ctx", None),
            P("fsdp", "ctx", None),
            P(),
            P(),
            P("fsdp", None),
            P(),
            P("fsdp", None),
            P("fsdp", None),
            P("fsdp", None),
            P("fsdp", None),
            P("fsdp", None),
            P(),
            P("section", "fsdp", None),
            P("section", "fsdp", None),
            P("section", "fsdp", None),
        ),
        out_specs=(
            P("section", "fsdp", "ctx", None),
            P(None, "fsdp"),
            P("fsdp"),
            P("fsdp", None),
            P(None, "fsdp"),
            P("fsdp", None),
            P("fsdp", None),
            P("fsdp", None),
            P("fsdp", None),
            P("fsdp", None),
            P(None, "fsdp"),
            P("section", "fsdp", None),
            P("section", "fsdp", None),
            P("section", "fsdp", None),
            P("fsdp"),
        ),
        check_vma=False,
    )
```

```python
import functools

import jax
import jax.numpy as jnp
from jax import lax
from jax.experimental import pallas as pl
from jax.experimental.pallas import tpu as pltpu
from jax.sharding import PartitionSpec as P

EPSILON = 1e-05
NEGATIVE = -1e30
MESH = pl.DeviceIdType.MESH
F32 = jnp.float32
BF16 = jnp.bfloat16


def passed_along(block, axis, distance):
    devices = range(lax.axis_size(axis))
    route = [(i - distance, i) for i in devices if i - distance in devices]
    return lax.ppermute(block, axis, route)


def swapped(block, axis):
    return lax.ppermute(block, axis, [(0, 1), (1, 0)])


def rounded(values):
    return lax.optimization_barrier(values.astype(BF16)).astype(F32)


def matmul(left_op, right_op):
    return jnp.dot(left_op, right_op, preferred_element_type=F32)


def matmul_left(left_op, right_op):
    return lax.dot_general(left_op, right_op, (((0,), (0,)), ((), ())), preferred_element_type=F32)


def matmul_right(left_op, right_op):
    return lax.dot_general(left_op, right_op, (((1,), (1,)), ((), ())), preferred_element_type=F32)


def norm_rows(values):
    inv_rms = lax.rsqrt(jnp.mean(values * values, axis=-1, keepdims=True) + EPSILON)
    return (values * inv_rms, inv_rms)


def norm_back(dnormed, normed, inv_rms):
    return inv_rms * dnormed - normed * inv_rms * jnp.mean(dnormed * normed, axis=-1, keepdims=True)


def greet(axis, count):
    me = lax.axis_index(axis)
    barrier = pltpu.get_barrier_semaphore()
    for step in range(1, count):
        pl.semaphore_signal(
            barrier,
            inc=1,
            device_id={axis: lax.rem(me + step, count)},
            device_id_type=MESH,
        )
    pl.semaphore_wait(barrier, count - 1)


def busy(microseconds):
    return pl.CostEstimate(flops=int(microseconds), bytes_accessed=1 << 16, transcendentals=0)


def swap_kernel(axis, count, rows, blocks, whole, send_sem, recv_sem, own_sem):
    me = lax.axis_index(axis)
    greet(axis, count)
    own_rows = pl.ds(pl.multiple_of(me * rows, rows), rows)
    copies = []
    for step in range(1, count):
        target = lax.rem(me + step, count)
        copy = pltpu.make_async_remote_copy(
            src_ref=blocks.at[pl.ds(pl.multiple_of(target * rows, rows), rows)],
            dst_ref=whole.at[own_rows],
            send_sem=send_sem.at[step],
            recv_sem=recv_sem.at[step],
            device_id={axis: target},
            device_id_type=MESH,
        )
        copy.start()
        copies.append(copy)
    own = pltpu.make_async_copy(blocks.at[own_rows], whole.at[own_rows], own_sem)
    own.start()
    own.wait()
    for copy in copies:
        copy.wait()


def swapped_blocks(array, axis, collective_id):
    count = lax.axis_size(axis)
    rows = array.shape[0] // count
    return pl.pallas_call(
        functools.partial(swap_kernel, axis, count, rows),
        out_shape=jax.ShapeDtypeStruct((count * rows,) + array.shape[1:], array.dtype),
        in_specs=[pl.BlockSpec(memory_space=pl.ANY)],
        out_specs=pl.BlockSpec(memory_space=pl.ANY),
        scratch_shapes=[
            pltpu.SemaphoreType.DMA((count,)),
            pltpu.SemaphoreType.DMA((count,)),
            pltpu.SemaphoreType.DMA,
        ],
        compiler_params=pltpu.CompilerParams(
            collective_id=collective_id, has_side_effects=True, vmem_limit_bytes=8 << 20
        ),
        cost_estimate=busy(40),
    )(array)


def corners():
    me = lax.axis_index("fsdp")
    beside = me + 1 - 2 * lax.rem(me, 2)
    across = lax.rem(me + 2, 4)
    return me, beside, across, lax.rem(beside + 2, 4)


def greet_sides():
    _, beside, across, _ = corners()
    barrier = pltpu.get_barrier_semaphore()
    for target in (beside, across):
        pl.semaphore_signal(barrier, inc=1, device_id={"fsdp": target}, device_id_type=MESH)
    pl.semaphore_wait(barrier, 2)


def to_side(src, dst, send_sem, recv_sem, target):
    return pltpu.make_async_remote_copy(
        src_ref=src,
        dst_ref=dst,
        send_sem=send_sem,
        recv_sem=recv_sem,
        device_id={"fsdp": target},
        device_id_type=MESH,
    )


def gather_kernel(block, whole, send_sem, recv_sem, own_sem):
    me, beside, across, _ = corners()
    rows = block.shape[0]
    half = rows // 2

    def part(owner, start, size):
        return whole.at[pl.ds(pl.multiple_of(owner * rows + start, half), size)]

    greet_sides()
    first = to_side(block, part(me, 0, rows), send_sem.at[0], recv_sem.at[0], beside)
    second = to_side(block, part(me, 0, rows), send_sem.at[1], recv_sem.at[1], across)
    first.start()
    second.start()
    own = pltpu.make_async_copy(block, part(me, 0, rows), own_sem)
    own.start()
    first.wait_recv()
    at = part(beside, 0, half)
    third = to_side(at, at, send_sem.at[2], recv_sem.at[2], across)
    third.start()
    second.wait_recv()
    at = part(across, half, half)
    fourth = to_side(at, at, send_sem.at[3], recv_sem.at[3], beside)
    fourth.start()
    own.wait()
    for copy in (first, second):
        copy.wait_send()
    for copy in (third, fourth):
        copy.wait()


def gathered(array, collective_id):
    rows, width = array.shape
    assert lax.axis_size("fsdp") == 4
    dma = pltpu.SemaphoreType.DMA
    return pl.pallas_call(
        gather_kernel,
        out_shape=jax.ShapeDtypeStruct((4 * rows, width), array.dtype),
        in_specs=[pl.BlockSpec(memory_space=pltpu.VMEM)],
        out_specs=pl.BlockSpec(memory_space=pltpu.VMEM),
        scratch_shapes=[dma((4,)), dma((4,)), dma],
        compiler_params=pltpu.CompilerParams(
            collective_id=collective_id, has_side_effects=True, vmem_limit_bytes=8 << 20
        ),
        cost_estimate=busy(25),
    )(array)


def reduce_kernel(blocks, total, beside_got, across_got, passed, passed_got, send_sem, recv_sem):
    me, beside, across, opposite = corners()
    rows = total.shape[0]
    half = rows // 2

    def part(owner, turn):
        return pl.ds(pl.multiple_of(owner * rows + turn * half, half), half)

    greet_sides()
    copies = []
    for index, (turn, target, got) in enumerate(((0, beside, beside_got), (1, across, across_got))):
        for slot, owner in ((1, opposite), (0, target)):
            copies.append(
                to_side(
                    blocks.at[part(owner, turn)],
                    got.at[slot],
                    send_sem.at[2 * index + slot],
                    recv_sem.at[2 * index + slot],
                    target,
                )
            )
    for copy in (copies[0], copies[2], copies[1], copies[3]):
        copy.start()
    onward = []
    for turn, owner, copy, got in ((0, across, copies[0], beside_got), (1, beside, copies[2], across_got)):
        copy.wait_recv()
        passed[turn] = (blocks[part(owner, turn)].astype(F32) + got[1].astype(F32)).astype(BF16)
        onward.append(
            to_side(passed.at[turn], passed_got.at[turn], send_sem.at[4 + turn], recv_sem.at[4 + turn], owner)
        )
        onward[-1].start()
    for turn, copy, got in ((0, copies[1], beside_got), (1, copies[3], across_got)):
        copy.wait_recv()
        total[pl.ds(turn * half, half)] = blocks[part(me, turn)].astype(F32) + got[0].astype(F32)
    for turn in range(2):
        onward[turn].wait_recv()
        at = pl.ds(turn * half, half)
        total[at] = total[at] + passed_got[turn].astype(F32)
    for copy in copies + onward:
        copy.wait_send()


def reduced(partial, collective_id):
    rows, width = partial.shape[0] // 4, partial.shape[1]
    assert lax.axis_size("fsdp") == 4
    dma = pltpu.SemaphoreType.DMA
    pair = pltpu.VMEM((2, rows // 2, width), BF16)
    return pl.pallas_call(
        reduce_kernel,
        out_shape=jax.ShapeDtypeStruct((rows, width), F32),
        in_specs=[pl.BlockSpec(memory_space=pltpu.VMEM)],
        out_specs=pl.BlockSpec(memory_space=pltpu.VMEM),
        scratch_shapes=[pair, pair, pair, pair, dma((6,)), dma((6,))],
        compiler_params=pltpu.CompilerParams(
            collective_id=collective_id, has_side_effects=True, vmem_limit_bytes=16 << 20
        ),
        cost_estimate=busy(25),
    )(partial.astype(BF16))


def tail_kernel(
    counts,
    gate_in,
    up_in,
    down_in,
    query_in,
    kv_in,
    proj_in,
    conv_b_in,
    conv_c_in,
    conv_x_in,
    conv_o_in,
    small_in,
    second_gu_in,
    second_down_in,
    gu_out,
    down_out,
    rest_out,
    a_own,
    a_other,
    a_sum,
    a_done,
    b_own,
    b_other,
    b_sum,
    b_done,
    c_own,
    c_other,
    c_got,
    own_sem,
    pair_send,
    pair_recv,
    c_own_sem,
    c_pair_send,
    c_pair_recv,
    c_send,
    c_recv,
    a_up_send,
    a_up_recv,
    a_back_send,
    a_back_recv,
    a_out_send,
    b_up_send,
    b_up_recv,
    b_back_send,
    b_back_recv,
    b_out_send,
    b_keep_sem,
    gu_recv,
    down_recv,
    rest_recv,
    second_send,
):
    n_ctx, n_fsdp = counts
    section = lax.axis_index("section")
    place = lax.axis_index("ctx")
    group = lax.axis_index("fsdp")
    other = 1 - section
    a_chunks, a_rows, a_width = a_own.shape
    b_chunks, b_rows, b_width = b_own.shape
    half = gate_in.shape[0] // n_fsdp // 2
    subs = half // a_rows
    per_kind = n_fsdp * subs
    down_half = down_in.shape[0] // 2
    down_chunks = down_half // b_rows
    c_rows = c_own.shape[1]
    mixers = (query_in, kv_in, proj_in, conv_b_in, conv_c_in, conv_x_in, conv_o_in)
    n_mix = len(mixers)
    cut = 3 * half // b_rows
    c_parts = ((0, cut), (cut, c_rows // b_rows))
    ticks = a_chunks // 2
    tail = 2 * (n_ctx - 1)

    barrier = pltpu.get_barrier_semaphore()
    for step in range(1, 2 * n_fsdp):
        flat = lax.rem(section * n_fsdp + group + step, 2 * n_fsdp)
        pl.semaphore_signal(
            barrier,
            inc=1,
            device_id={"section": flat // n_fsdp, "fsdp": lax.rem(flat, n_fsdp)},
            device_id_type=MESH,
        )

    @pl.when(place > 0)
    def _():
        pl.semaphore_signal(barrier, inc=1, device_id={"ctx": place - 1}, device_id_type=MESH)

    @pl.when(place < n_ctx - 1)
    def _():
        pl.semaphore_signal(barrier, inc=1, device_id={"ctx": place + 1}, device_id_type=MESH)

    at_edge = (place == 0) | (place == n_ctx - 1)

    @pl.when(at_edge)
    def _():
        pl.semaphore_wait(barrier, 2 * n_fsdp)

    @pl.when(jnp.logical_not(at_edge))
    def _():
        pl.semaphore_wait(barrier, 2 * n_fsdp + 1)

    def half_rows(owner, which):
        return pl.ds(pl.multiple_of(owner * (2 * half) + which * half, half), half)

    local, pair = [], []
    for kind, source in enumerate((gate_in, up_in)):
        for owner in range(n_fsdp):
            index = kind * n_fsdp + owner
            slot = pl.ds(index * subs, subs)
            for sub in range(subs):
                src_own = source.at[pl.ds(pl.multiple_of(owner * (2 * half) + section * half + sub * a_rows, a_rows), a_rows)]
                src_other = source.at[pl.ds(pl.multiple_of(owner * (2 * half) + other * half + sub * a_rows, a_rows), a_rows)]
                spot = index * subs + sub
                local.append(pltpu.make_async_copy(src_own, a_own.at[spot], own_sem.at[spot]))
                pair.append(
                    pltpu.make_async_remote_copy(
                        src_ref=src_other,
                        dst_ref=a_other.at[spot],
                        send_sem=pair_send.at[spot],
                        recv_sem=pair_recv.at[spot],
                        device_id={"section": other},
                        device_id_type=MESH,
                    )
                )
    for chunk in range(down_chunks):
        spot = a_chunks + chunk
        src_own = down_in.at[pl.ds(pl.multiple_of(section * down_half + chunk * b_rows, b_rows), b_rows)]
        src_other = down_in.at[pl.ds(pl.multiple_of(other * down_half + chunk * b_rows, b_rows), b_rows)]
        local.append(pltpu.make_async_copy(src_own, b_own.at[chunk], own_sem.at[spot]))
        pair.append(
            pltpu.make_async_remote_copy(
                src_ref=src_other,
                dst_ref=b_other.at[chunk],
                send_sem=pair_send.at[spot],
                recv_sem=pair_recv.at[spot],
                device_id={"section": other},
                device_id_type=MESH,
            )
        )
    for copy in pair:
        copy.start()
    for copy in local:
        copy.start()
    c_local, c_pair = ([], []), ([], [])
    for kind, source in enumerate(mixers):
        part = 0 if kind < 3 else 1
        for owner in range(n_fsdp):
            index = owner * (n_mix + 1) + kind
            place_at = pl.ds(kind * half, half)
            c_local[part].append(
                pltpu.make_async_copy(
                    source.at[half_rows(owner, section)], c_own.at[owner, place_at], c_own_sem.at[index]
                )
            )
            c_pair[part].append(
                pltpu.make_async_remote_copy(
                    src_ref=source.at[half_rows(owner, other)],
                    dst_ref=c_other.at[owner, place_at],
                    send_sem=c_pair_send.at[index],
                    recv_sem=c_pair_recv.at[index],
                    device_id={"section": other},
                    device_id_type=MESH,
                )
            )
    for owner in range(n_fsdp):
        small_at = pl.ds(n_mix * half, c_rows - n_mix * half)
        index = owner * (n_mix + 1) + n_mix
        c_local[1].append(
            pltpu.make_async_copy(small_in.at[owner, section], c_own.at[owner, small_at], c_own_sem.at[index])
        )
        c_pair[1].append(
            pltpu.make_async_remote_copy(
                src_ref=small_in.at[owner, other],
                dst_ref=c_other.at[owner, small_at],
                send_sem=c_pair_send.at[index],
                recv_sem=c_pair_recv.at[index],
                device_id={"section": other},
                device_id_type=MESH,
            )
        )
    for part in range(2):
        for copy in c_pair[part]:
            copy.start()
        for copy in c_local[part]:
            copy.start()
    b_own[b_chunks - 1] = jnp.zeros((b_rows, b_width), BF16)
    for copy in local:
        copy.wait()
    for copy in pair:
        copy.wait_recv()

    def mixer_copy(part, step):
        target = lax.rem(group + step, n_fsdp)
        first, last = c_parts[part]
        at = pl.ds(first * b_rows, (last - first) * b_rows)
        return pltpu.make_async_remote_copy(
            src_ref=c_own.at[target, at],
            dst_ref=c_got.at[step - 1, at],
            send_sem=c_send.at[part, step],
            recv_sem=c_recv.at[part, step],
            device_id={"fsdp": target},
            device_id_type=MESH,
        )

    def mixer_out(part):
        for copy in c_local[part]:
            copy.wait()
        for copy in c_pair[part]:
            copy.wait_recv()
        first, last = c_parts[part]
        size = last - first

        def add(index, carry):
            owner = index // size
            at = pl.ds(pl.multiple_of((first + lax.rem(index, size)) * b_rows, b_rows), b_rows)
            c_own[owner, at] = (c_own[owner, at].astype(F32) + c_other[owner, at].astype(F32)).astype(BF16)
            return carry

        lax.fori_loop(0, n_fsdp * size, add, 0)
        for step in range(1, n_fsdp):
            mixer_copy(part, step).start()

    def mixer_in(part):
        for step in range(1, n_fsdp):
            mixer_copy(part, step).wait_recv()
        first, last = c_parts[part]

        def add(index, carry):
            at = pl.ds(pl.multiple_of(index * b_rows, b_rows), b_rows)
            total = c_own[group, at].astype(F32)
            for step in range(1, n_fsdp):
                total = total + c_got[step - 1, at].astype(F32)
            b_own[down_chunks + index] = total.astype(BF16)
            return carry

        lax.fori_loop(first, last, add, 0)

    def second_start():
        for kind in range(2):
            for owner in range(n_fsdp):
                index = kind * n_fsdp + owner
                src = second_gu_in.at[kind, owner]
                dst = gu_out.at[
                    kind,
                    pl.ds(pl.multiple_of(section * half, half), half),
                    pl.ds(pl.multiple_of(group * a_width, 128), a_width),
                ]
                is_mine = (section == 1) & (group == owner)

                @pl.when(is_mine)
                def _(src=src, dst=dst, index=index):
                    pltpu.make_async_copy(src, dst, second_send.at[index]).start()

                @pl.when(jnp.logical_not(is_mine))
                def _(src=src, dst=dst, index=index, kind=kind, owner=owner):
                    pltpu.make_async_remote_copy(
                        src_ref=src,
                        dst_ref=dst,
                        send_sem=second_send.at[index],
                        recv_sem=gu_recv.at[kind, section * n_fsdp + group],
                        device_id={"section": 1, "fsdp": owner},
                        device_id_type=MESH,
                    ).start()

        down_at = down_out.at[pl.ds(pl.multiple_of(section * down_half, b_rows), down_half)]

        @pl.when(section == 1)
        def _():
            pltpu.make_async_copy(second_down_in, down_at, second_send.at[2 * n_fsdp]).start()

        @pl.when(section == 0)
        def _():
            pltpu.make_async_remote_copy(
                src_ref=second_down_in,
                dst_ref=down_at,
                send_sem=second_send.at[2 * n_fsdp],
                recv_sem=down_recv,
                device_id={"section": 1},
                device_id_type=MESH,
            ).start()

    def a_target(k):
        kind = k // per_kind
        rest = lax.rem(k, per_kind)
        owner = rest // subs
        sub = lax.rem(rest, subs)
        spot = gu_out.at[
            kind,
            pl.ds(pl.multiple_of(section * half + sub * a_rows, a_rows), a_rows),
            pl.ds(pl.multiple_of(group * a_width, 128), a_width),
        ]
        return kind, owner, spot

    def hand_out(k):
        kind, owner, spot = a_target(k)
        is_mine = (section == 0) & (group == owner)

        @pl.when(is_mine)
        def _():
            pltpu.make_async_copy(a_done.at[k], spot, a_out_send.at[k]).start()

        @pl.when(jnp.logical_not(is_mine))
        def _():
            pltpu.make_async_remote_copy(
                src_ref=a_done.at[k],
                dst_ref=spot,
                send_sem=a_out_send.at[k],
                recv_sem=gu_recv.at[kind, section * n_fsdp + group],
                device_id={"section": 0, "fsdp": owner},
                device_id_type=MESH,
            ).start()

        @pl.when(k < down_chunks)
        def _():
            at = down_out.at[pl.ds(pl.multiple_of(section * down_half + k * b_rows, b_rows), b_rows)]

            @pl.when(section == 0)
            def _():
                pltpu.make_async_copy(b_done.at[k], at, b_out_send.at[k]).start()

            @pl.when(section == 1)
            def _():
                pltpu.make_async_remote_copy(
                    src_ref=b_done.at[k],
                    dst_ref=at,
                    send_sem=b_out_send.at[k],
                    recv_sem=down_recv,
                    device_id={"section": 0},
                    device_id_type=MESH,
                ).start()

        @pl.when(k >= down_chunks)
        def _():
            at = rest_out.at[section, pl.ds(pl.multiple_of((k - down_chunks) * b_rows, b_rows), b_rows)]
            pltpu.make_async_copy(b_done.at[k], at, b_keep_sem.at[k]).start()
            pltpu.make_async_remote_copy(
                src_ref=b_done.at[k],
                dst_ref=at,
                send_sem=b_out_send.at[k],
                recv_sem=rest_recv,
                device_id={"section": other},
                device_id_type=MESH,
            ).start()

    def up_copies(k, target):
        return (
            pltpu.make_async_remote_copy(
                src_ref=a_sum.at[k],
                dst_ref=a_sum.at[k],
                send_sem=a_up_send.at[k],
                recv_sem=a_up_recv.at[k],
                device_id={"ctx": target},
                device_id_type=MESH,
            ),
            pltpu.make_async_remote_copy(
                src_ref=b_sum.at[k],
                dst_ref=b_sum.at[k],
                send_sem=b_up_send.at[k],
                recv_sem=b_up_recv.at[k],
                device_id={"ctx": target},
                device_id_type=MESH,
            ),
        )

    def back_copies(k, target):
        return (
            pltpu.make_async_remote_copy(
                src_ref=a_done.at[k],
                dst_ref=a_done.at[k],
                send_sem=a_back_send.at[k],
                recv_sem=a_back_recv.at[k],
                device_id={"ctx": target},
                device_id_type=MESH,
            ),
            pltpu.make_async_remote_copy(
                src_ref=b_done.at[k],
                dst_ref=b_done.at[k],
                send_sem=b_back_send.at[k],
                recv_sem=b_back_recv.at[k],
                device_id={"ctx": target},
                device_id_type=MESH,
            ),
        )

    def own_term(k):
        @pl.when(k < down_chunks)
        def _():
            b_own[k] = (b_own[k].astype(F32) + b_other[k].astype(F32)).astype(BF16)

        return a_own[k].astype(F32) + a_other[k].astype(F32)

    lanes = []
    for way in range(2):
        rank = place if way == 0 else n_ctx - 1 - place
        ahead = place + 1 if way == 0 else place - 1
        behind = place - 1 if way == 0 else place + 1
        lanes.append((way, rank, ahead, behind))

    def tick_step(tick, carry):
        @pl.when(tick == 0)
        def _():
            mixer_out(0)

        @pl.when(tick == 2)
        def _():
            mixer_out(1)

        @pl.when(tick == down_chunks // 2)
        def _():
            mixer_in(0)

        @pl.when(tick == (down_chunks + cut) // 2)
        def _():
            mixer_in(1)
            second_start()

        for way, rank, ahead, behind in lanes:
            step = tick - rank
            k = 2 * jnp.clip(step, 0, ticks - 1) + way

            @pl.when((step >= 0) & (step < ticks))
            def _(k=k, rank=rank, ahead=ahead, behind=behind):
                term = own_term(k)

                @pl.when(rank == 0)
                def _():
                    a_sum[k] = term.astype(BF16)
                    b_sum[k] = b_own[k]

                @pl.when(rank > 0)
                def _():
                    for copy in up_copies(k, behind):
                        copy.wait_recv()

                @pl.when((rank > 0) & (rank < n_ctx - 1))
                def _():
                    a_sum[k] = (term + a_sum[k].astype(F32)).astype(BF16)
                    b_sum[k] = (b_own[k].astype(F32) + b_sum[k].astype(F32)).astype(BF16)

                @pl.when(rank < n_ctx - 1)
                def _():
                    for copy in up_copies(k, ahead):
                        copy.start()

                @pl.when(rank == n_ctx - 1)
                def _():
                    a_done[k] = (term + a_sum[k].astype(F32)).astype(BF16)
                    b_done[k] = (b_own[k].astype(F32) + b_sum[k].astype(F32)).astype(BF16)
                    for copy in back_copies(k, behind):
                        copy.start()
                    hand_out(k)

            late = tick - (tail - rank)
            j = 2 * jnp.clip(late, 0, ticks - 1) + way

            @pl.when((late >= 0) & (late < ticks) & (rank < n_ctx - 1))
            def _(j=j, rank=rank, ahead=ahead, behind=behind):
                for copy in back_copies(j, ahead):
                    copy.wait_recv()

                @pl.when(rank > 0)
                def _():
                    for copy in back_copies(j, behind):
                        copy.start()

                hand_out(j)

        return carry

    lax.fori_loop(0, ticks + tail, tick_step, 0)

    for copy in pair:
        copy.wait_send()
    for part in range(2):
        for copy in c_pair[part]:
            copy.wait_send()
        for step in range(1, n_fsdp):
            mixer_copy(part, step).wait_send()

    def settle(step, carry):
        for way, rank, ahead, behind in lanes:
            k = 2 * step + way

            @pl.when(rank < n_ctx - 1)
            def _(k=k, ahead=ahead):
                for copy in up_copies(k, ahead):
                    copy.wait_send()

            @pl.when(rank > 0)
            def _(k=k, behind=behind):
                for copy in back_copies(k, behind):
                    copy.wait_send()

            _, _, spot = a_target(k)
            pltpu.make_async_copy(a_done.at[k], spot, a_out_send.at[k]).wait()
            pltpu.make_async_copy(b_done.at[k], b_own.at[k], b_out_send.at[k]).wait()

            @pl.when(k >= down_chunks)
            def _(k=k):
                pltpu.make_async_copy(b_done.at[k], b_own.at[k], b_keep_sem.at[k]).wait()

        return carry

    lax.fori_loop(0, ticks, settle, 0)
    for kind in range(2):
        for owner in range(n_fsdp):
            src = second_gu_in.at[kind, owner]
            pltpu.make_async_copy(src, src, second_send.at[kind * n_fsdp + owner]).wait()
    pltpu.make_async_copy(second_down_in, second_down_in, second_send.at[2 * n_fsdp]).wait()
    for kind in range(2):
        for source in range(2 * n_fsdp):

            @pl.when(section * n_fsdp + group != source)
            def _(kind=kind, source=source):
                region = gu_out.at[
                    kind,
                    pl.ds((source // n_fsdp) * half, half),
                    pl.ds((source % n_fsdp) * a_width, a_width),
                ]
                pltpu.make_async_copy(region, region, gu_recv.at[kind, source]).wait()

    region = down_out.at[pl.ds(pl.multiple_of(other * down_half, b_rows), down_half)]
    pltpu.make_async_copy(region, region, down_recv).wait()
    region = rest_out.at[other]
    pltpu.make_async_copy(region, region, rest_recv).wait()


def summed_gradients(first, mixers, small, second_gu, second_down):
    n_ctx, n_fsdp = lax.axis_size("ctx"), lax.axis_size("fsdp")
    gate, up, down = first
    half = gate.shape[0] // n_fsdp // 2
    a_rows, b_rows = half // 4, half * 3 // 8
    a_chunks = 2 * n_fsdp * 4
    a_width, b_width = gate.shape[1], down.shape[1]
    c_rows = len(mixers) * half + small.shape[2]
    down_chunks = down.shape[0] // 2 // b_rows
    b_chunks = down_chunks + c_rows // b_rows + 1
    assert a_chunks == b_chunks and c_rows % b_rows == 0
    rest = b_chunks - down_chunks
    dma = pltpu.SemaphoreType.DMA
    loads = a_chunks + down_chunks
    pieces = n_fsdp * (len(mixers) + 1)
    return pl.pallas_call(
        functools.partial(tail_kernel, (n_ctx, n_fsdp)),
        out_shape=(
            jax.ShapeDtypeStruct((2, 2 * half, n_fsdp * a_width), BF16),
            jax.ShapeDtypeStruct(down.shape, BF16),
            jax.ShapeDtypeStruct((2, rest * b_rows, b_width), BF16),
        ),
        in_specs=[pl.BlockSpec(memory_space=pl.ANY)] * (6 + len(mixers)),
        out_specs=[pl.BlockSpec(memory_space=pl.ANY)] * 3,
        scratch_shapes=[
            pltpu.VMEM((a_chunks, a_rows, a_width), BF16),
            pltpu.VMEM((a_chunks, a_rows, a_width), BF16),
            pltpu.VMEM((a_chunks, a_rows, a_width), BF16),
            pltpu.VMEM((a_chunks, a_rows, a_width), BF16),
            pltpu.VMEM((b_chunks, b_rows, b_width), BF16),
            pltpu.VMEM((down_chunks, b_rows, b_width), BF16),
            pltpu.VMEM((b_chunks, b_rows, b_width), BF16),
            pltpu.VMEM((b_chunks, b_rows, b_width), BF16),
            pltpu.VMEM((n_fsdp, c_rows, b_width), BF16),
            pltpu.VMEM((n_fsdp, c_rows, b_width), BF16),
            pltpu.VMEM((n_fsdp - 1, c_rows, b_width), BF16),
            dma((loads,)),
            dma((loads,)),
            dma((loads,)),
            dma((pieces,)),
            dma((pieces,)),
            dma((pieces,)),
            dma((2, n_fsdp)),
            dma((2, n_fsdp)),
            dma((a_chunks,)),
            dma((a_chunks,)),
            dma((a_chunks,)),
            dma((a_chunks,)),
            dma((a_chunks,)),
            dma((b_chunks,)),
            dma((b_chunks,)),
            dma((b_chunks,)),
            dma((b_chunks,)),
            dma((b_chunks,)),
            dma((b_chunks,)),
            dma((2, 2 * n_fsdp)),
            dma,
            dma,
            dma((2 * n_fsdp + 1,)),
        ],
        compiler_params=pltpu.CompilerParams(
            collective_id=6, has_side_effects=True, vmem_limit_bytes=56 << 20
        ),
        cost_estimate=busy(160),
    )(gate, up, down, *mixers, small, second_gu, second_down)


def mixer_weights_kernel(count, first_in, second_in, first_out, second_out, send_sem, recv_sem, pair_send, pair_recv, own_sem):
    section = lax.axis_index("section")
    me = lax.axis_index("fsdp")
    other = 1 - section
    beside = me + 1 - 2 * lax.rem(me, 2)
    across = lax.rem(me + 2, count)
    opposite = lax.rem(beside + 2, count)
    rows = first_in.shape[0]
    half = rows // 2
    quarter = half // 2
    barrier = pltpu.get_barrier_semaphore()
    for target in ({"fsdp": beside}, {"fsdp": across}, {"section": other}):
        pl.semaphore_signal(barrier, inc=1, device_id=target, device_id_type=MESH)
    pl.semaphore_wait(barrier, 3)
    arrays = ((first_in, first_out), (second_in, second_out))

    def at_rows(owner, extra, size):
        return pl.ds(pl.multiple_of(owner * rows + extra, quarter), size)

    def remote(slot, sems, src, dst, target):
        return pltpu.make_async_remote_copy(
            src_ref=src,
            dst_ref=dst,
            send_sem=sems[0].at[slot],
            recv_sem=sems[1].at[slot],
            device_id=target,
            device_id_type=MESH,
        )

    hop, pair = (send_sem, recv_sem), (pair_send, pair_recv)
    waiting = []
    direct = []
    for index, (source, out) in enumerate(arrays):
        mine = source.at[pl.ds(pl.multiple_of(section * half, half), half)]
        spot = out.at[at_rows(me, section * half, half)]
        copies = [
            remote(index * 4, hop, mine, spot, {"fsdp": beside}),
            remote(index * 4 + 1, hop, mine, spot, {"fsdp": across}),
        ]
        for copy in copies:
            copy.start()
        direct.append(copies)
    own = [
        pltpu.make_async_copy(source, out.at[at_rows(me, 0, rows)], own_sem.at[index])
        for index, (source, out) in enumerate(arrays)
    ]
    for copy in own:
        copy.start()

    def arrived(owner, size, extra):
        return lambda out: out.at[at_rows(owner, section * half + extra, size)]

    onward = []
    for index, (source, out) in enumerate(arrays):
        direct[index][0].wait_recv()
        part = arrived(beside, quarter, 0)(out)
        onward.append(remote(index * 4 + 2, hop, part, part, {"fsdp": across}))
        onward[-1].start()
        whole = arrived(beside, half, 0)(out)
        waiting.append(remote(index * 4, pair, whole, whole, {"section": other}))
        waiting[-1].start()
        direct[index][1].wait_recv()
        part = arrived(across, quarter, quarter)(out)
        onward.append(remote(index * 4 + 3, hop, part, part, {"fsdp": beside}))
        onward[-1].start()
        whole = arrived(across, half, 0)(out)
        waiting.append(remote(index * 4 + 1, pair, whole, whole, {"section": other}))
        waiting[-1].start()
    for index, (source, out) in enumerate(arrays):
        for turn in range(2):
            onward[2 * index + turn].wait_recv()
            part = arrived(opposite, quarter, turn * quarter)(out)
            waiting.append(remote(index * 4 + 2 + turn, pair, part, part, {"section": other}))
            waiting[-1].start()
    for copy in own:
        copy.wait()
    for copies in direct:
        for copy in copies:
            copy.wait_send()
    for copy in onward:
        copy.wait_send()
    for copy in waiting:
        copy.wait()


def mixer_weights(first, second, collective_id):
    count = lax.axis_size("fsdp")
    dma = pltpu.SemaphoreType.DMA
    return pl.pallas_call(
        functools.partial(mixer_weights_kernel, count),
        out_shape=tuple(
            jax.ShapeDtypeStruct((count * w.shape[0], w.shape[1]), w.dtype) for w in (first, second)
        ),
        in_specs=[pl.BlockSpec(memory_space=pl.ANY)] * 2,
        out_specs=[pl.BlockSpec(memory_space=pl.ANY)] * 2,
        scratch_shapes=[dma((8,)), dma((8,)), dma((8,)), dma((8,)), dma((2,))],
        compiler_params=pltpu.CompilerParams(
            collective_id=collective_id, has_side_effects=True, vmem_limit_bytes=8 << 20
        ),
        cost_estimate=busy(45),
    )(first, second)


def column_weights_kernel(count, holder, n_ctx, *refs):
    if n_ctx > 1:
        kv_in, refs = refs[0], refs[1:]
    gate_in, up_in, down_in, gate_out, up_out, down_out = refs[:6]
    refs = refs[6:]
    if n_ctx > 1:
        kv_out, refs = refs[0], refs[1:]
    send_sem, recv_sem, pair_send, pair_recv, own_sem = refs[:5]
    section = lax.axis_index("section")
    me = lax.axis_index("fsdp")
    place = lax.axis_index("ctx")
    other = 1 - section
    rows = gate_in.shape[0]
    wide = gate_out.shape[1]
    barrier = pltpu.get_barrier_semaphore()
    for step in range(1, count):
        pl.semaphore_signal(
            barrier, inc=1, device_id={"fsdp": lax.rem(me + step, count)}, device_id_type=MESH
        )
    pl.semaphore_signal(barrier, inc=1, device_id={"section": other}, device_id_type=MESH)
    for step in range(1, n_ctx):
        pl.semaphore_signal(
            barrier, inc=1, device_id={"ctx": lax.rem(place + step, n_ctx)}, device_id_type=MESH
        )
    pl.semaphore_wait(barrier, count + n_ctx - 1)
    kv_copies = []
    if n_ctx > 1:
        kv_send, kv_recv, kv_own = refs[5:]
        kv_rows = kv_in.shape[0]
        spot = kv_out.at[pl.ds(pl.multiple_of(place * kv_rows, kv_rows), kv_rows)]
        for step in range(1, n_ctx):
            kv_copies.append(
                pltpu.make_async_remote_copy(
                    src_ref=kv_in,
                    dst_ref=spot,
                    send_sem=kv_send.at[step],
                    recv_sem=kv_recv.at[step],
                    device_id={"ctx": lax.rem(place + step, n_ctx)},
                    device_id_type=MESH,
                )
            )
            kv_copies[-1].start()
        kv_keep = pltpu.make_async_copy(kv_in, spot, kv_own)
        kv_keep.start()
    arrays = ((gate_in, gate_out), (up_in, up_out))

    def at_rows(out, owner):
        return out.at[pl.ds(pl.multiple_of(owner * rows, rows), rows)]

    def crossing(kind, step):
        source, out = arrays[kind]
        target = lax.rem(me + step, count)
        return pltpu.make_async_remote_copy(
            src_ref=source.at[:, pl.ds(pl.multiple_of(target * wide, 128), wide)],
            dst_ref=at_rows(out, me),
            send_sem=send_sem.at[kind, step],
            recv_sem=recv_sem.at[kind, step],
            device_id={"fsdp": target},
            device_id_type=MESH,
        )

    def handed(kind, step):
        source, out = arrays[kind]
        origin = lax.rem(me + count - step, count)
        if step == 0:
            src = source.at[:, pl.ds(pl.multiple_of(me * wide, 128), wide)]
        else:
            src = at_rows(out, origin)
        return pltpu.make_async_remote_copy(
            src_ref=src,
            dst_ref=at_rows(out, origin),
            send_sem=pair_send.at[kind, step],
            recv_sem=pair_recv.at[kind, step],
            device_id={"section": other},
            device_id_type=MESH,
        )

    down_copy = pltpu.make_async_remote_copy(
        src_ref=down_in,
        dst_ref=down_out,
        send_sem=pair_send.at[2, 0],
        recv_sem=pair_recv.at[2, 0],
        device_id={"section": other},
        device_id_type=MESH,
    )
    kinds = range(2)

    @pl.when(section == holder)
    def _():
        for step in range(1, count):
            for kind in kinds:
                crossing(kind, step).start()
        for kind in kinds:
            handed(kind, 0).start()
        down_copy.start()
        keep = [
            pltpu.make_async_copy(
                arrays[kind][0].at[:, pl.ds(pl.multiple_of(me * wide, 128), wide)],
                at_rows(arrays[kind][1], me),
                own_sem.at[kind],
            )
            for kind in kinds
        ] + [pltpu.make_async_copy(down_in, down_out, own_sem.at[2])]
        for copy in keep:
            copy.start()
        for step in range(1, count):
            for kind in kinds:
                crossing(kind, step).wait_recv()
                handed(kind, step).start()
        for copy in keep:
            copy.wait()
        for step in range(1, count):
            for kind in kinds:
                crossing(kind, step).wait_send()
        for step in range(count):
            for kind in kinds:
                handed(kind, step).wait_send()
        down_copy.wait_send()

    @pl.when(section != holder)
    def _():
        for step in range(count):
            for kind in kinds:
                handed(kind, step).wait_recv()
        down_copy.wait_recv()

    if n_ctx > 1:
        kv_keep.wait()
        for copy in kv_copies:
            copy.wait()


def column_weights(gate, up, down, holder, collective_id, kv=None):
    count = lax.axis_size("fsdp")
    n_ctx = 1 if kv is None else lax.axis_size("ctx")
    dma = pltpu.SemaphoreType.DMA
    column = jax.ShapeDtypeStruct((count * gate.shape[0], gate.shape[1] // count), gate.dtype)
    outs = [column, column, jax.ShapeDtypeStruct(down.shape, down.dtype)]
    ins = [gate, up, down]
    sems = [dma((2, count)), dma((2, count)), dma((3, count)), dma((3, count)), dma((3,))]
    if kv is not None:
        ins = [kv] + ins
        outs.append(jax.ShapeDtypeStruct((n_ctx * kv.shape[0], kv.shape[1]), kv.dtype))
        sems += [dma((n_ctx,)), dma((n_ctx,)), dma]
    return pl.pallas_call(
        functools.partial(column_weights_kernel, count, holder, n_ctx),
        out_shape=tuple(outs),
        in_specs=[pl.BlockSpec(memory_space=pl.ANY)] * len(ins),
        out_specs=[pl.BlockSpec(memory_space=pl.ANY)] * len(outs),
        scratch_shapes=sems,
        compiler_params=pltpu.CompilerParams(
            collective_id=collective_id, has_side_effects=True, vmem_limit_bytes=8 << 20
        ),
        cost_estimate=busy(40),
    )(*ins)


def attend(query, key_all, value_all, allowed):
    kv_heads = key_all.shape[1]
    rows, q_heads, head = query.shape
    grouped = query.reshape(rows, kv_heads, q_heads // kv_heads, head)
    scores = jnp.einsum("qghd,kgd->ghqk", grouped, key_all, preferred_element_type=F32) * head ** (-0.5)
    scores = jnp.where(allowed, scores, NEGATIVE)
    peak = jnp.max(scores, axis=-1, keepdims=True)
    weights = jnp.where(allowed, jnp.exp(scores - peak), 0.0)
    total = jnp.sum(weights, axis=-1, keepdims=True)
    log_total = peak + jnp.log(total)
    prob = (weights / total).astype(BF16)
    out = jnp.einsum("ghqk,kgd->qghd", prob, value_all, preferred_element_type=F32)
    return out.reshape(rows, q_heads * head), log_total


def attend_back(query, key_all, value_all, allowed, log_total, attended, d_out):
    kv_heads = key_all.shape[1]
    rows, q_heads, head = query.shape
    scale = head ** (-0.5)
    grouped = query.reshape(rows, kv_heads, q_heads // kv_heads, head)
    d_group = d_out.reshape(rows, kv_heads, q_heads // kv_heads, head)
    delta = jnp.sum(d_group.astype(F32) * attended.reshape(d_group.shape), axis=-1)
    scores = jnp.einsum("qghd,kgd->ghqk", grouped, key_all, preferred_element_type=F32) * scale
    prob = jnp.where(allowed, jnp.exp(scores - log_total), 0.0)
    d_prob = jnp.einsum("qghd,kgd->ghqk", d_group, value_all, preferred_element_type=F32)
    d_scores = (prob * (d_prob - delta.transpose(1, 2, 0)[..., None])).astype(BF16)
    d_query = jnp.einsum("ghqk,kgd->qghd", d_scores, key_all, preferred_element_type=F32) * scale
    d_key = jnp.einsum("ghqk,qghd->kgd", d_scores, grouped, preferred_element_type=F32) * scale
    d_value = jnp.einsum("ghqk,qghd->kgd", prob.astype(BF16), d_group, preferred_element_type=F32)
    return d_query.reshape(rows, q_heads, head), d_key, d_value


def ffn_forward(residual, gain, w_gate, w_up, w_down):
    normed, inv_rms = norm_rows(residual)
    act = gathered((normed * gain).astype(BF16), 0)
    gate_pre = matmul(act, w_gate)
    up_pre = matmul(act, w_up)
    hidden = (jax.nn.silu(gate_pre) * up_pre).astype(BF16)
    out = reduced(matmul(hidden, w_down), 1)
    return out, (normed, inv_rms, act, gate_pre, up_pre, hidden)


def ffn_backward(d_low, kept, gain, w_gate, w_up, w_down, settled=None):
    normed, inv_rms, act, gate_pre, up_pre, hidden = kept
    d_all = gathered(d_low, 0)
    if settled is not None:
        d_all, settled = lax.optimization_barrier((d_all, settled))
    d_hidden = matmul_right(d_all, w_down)
    sigmoid = jax.nn.sigmoid(gate_pre)
    d_up = (d_hidden * gate_pre * sigmoid).astype(BF16)
    d_gate = (d_hidden * up_pre * sigmoid * (1.0 + gate_pre * (1.0 - sigmoid))).astype(BF16)
    d_act = reduced(matmul_right(d_gate, w_gate) + matmul_right(d_up, w_up), 1)
    grad_gate = matmul_left(act, d_gate).astype(BF16)
    grad_up = matmul_left(act, d_up).astype(BF16)
    grad_down = matmul_left(hidden, d_all).astype(BF16)
    grad_gain = jnp.sum(d_act * normed, axis=0)
    return norm_back(d_act * gain, normed, inv_rms), grad_gain, (grad_gate, grad_up, grad_down), settled


def shards(
    inputs,
    cotangent,
    lengths,
    norm_gains,
    conv_in,
    conv_kernel,
    conv_out,
    attn_q,
    attn_k,
    attn_v,
    attn_out,
    head_gains,
    ffn_gate,
    ffn_up,
    ffn_down,
):
    micro, rows, width = inputs.shape
    section = lax.axis_index("section")
    group = lax.axis_index("fsdp")
    fsdp = lax.axis_size("fsdp")
    assert micro == lax.axis_size("section")
    head = head_gains.shape[1]
    q_width, kv_width = attn_q.shape[1], attn_k.shape[1]
    q_heads, kv_heads = q_width // head, kv_width // head
    positions = lax.axis_index("ctx") * rows + jnp.arange(rows)
    length = lax.dynamic_index_in_dim(lengths, group * micro + section, keepdims=False)
    mask = (positions < length).astype(F32)[:, None]

    def whole_rows(weight):
        half = weight.shape[0] // micro
        mine = lax.dynamic_slice_in_dim(weight, section * half, half, 0)
        return lax.all_gather(mine, ("fsdp", "section"), axis=0, tiled=True)

    part = ffn_gate.shape[1]
    in_full, out_full = mixer_weights(conv_in, conv_out, 2)
    gate1, up1, down1 = column_weights(ffn_gate[0], ffn_up[0], ffn_down[0], 0, 7)
    query_full, key_full, value_full, proj_full = (
        whole_rows(attn_q),
        whole_rows(attn_k),
        whole_rows(attn_v),
        whole_rows(attn_out),
    )

    x = lax.dynamic_index_in_dim(inputs, section, keepdims=False).astype(F32)
    normed0, inv0 = norm_rows(x)
    act1 = (normed0 * norm_gains[0]).astype(BF16)
    projected = matmul(act1, in_full)
    b_gate, c_gate, x_value = (
        projected[:, :width],
        projected[:, width : 2 * width],
        projected[:, 2 * width :],
    )
    b_product = (b_gate * x_value).astype(BF16)
    rim = passed_along(b_product[-2:], "ctx", 1)
    extended = jnp.concatenate([rim, b_product], axis=0).astype(F32)
    convolved = (
        conv_kernel[0] * extended[:-2]
        + conv_kernel[1] * extended[1:-1]
        + conv_kernel[2] * extended[2:]
    )
    z_low = (c_gate * convolved).astype(BF16)
    mixed = matmul(z_low, out_full)
    res1 = x + mixed
    ffn1, kept1 = ffn_forward(res1, norm_gains[1], gate1, up1, down1)
    h_low = (res1 + ffn1).astype(BF16)

    h = h_low.astype(F32)
    normed2, inv2 = norm_rows(h)
    act2 = (normed2 * norm_gains[2]).astype(BF16)
    q_normed, q_inv = norm_rows(matmul(act2, query_full).reshape(rows, q_heads, head))
    k_normed, k_inv = norm_rows(matmul(act2, key_full).reshape(rows, kv_heads, head))
    query = (q_normed * head_gains[0]).astype(BF16)
    key = (k_normed * head_gains[1]).astype(BF16)
    value = matmul(act2, value_full).astype(BF16)
    gate2, up2, down2, kv_all = column_weights(
        ffn_gate[0],
        ffn_up[0],
        ffn_down[0],
        1,
        3,
        jnp.concatenate([key.reshape(rows, kv_width), value], axis=1),
    )
    key_all = kv_all[:, :kv_width].reshape(-1, kv_heads, head)
    value_all = kv_all[:, kv_width:].reshape(-1, kv_heads, head)
    key_pos = jnp.arange(kv_all.shape[0])
    allowed = (key_pos[None, :] <= positions[:, None]) & (key_pos[None, :] < length)
    attended, log_total = attend(query, key_all, value_all, allowed)
    attended_low = attended.astype(BF16)
    attn_rows = matmul(attended_low, proj_full)
    res2 = h + attn_rows
    ffn2, kept2 = ffn_forward(res2, norm_gains[3], gate2, up2, down2)
    result = (res2 + ffn2) * mask

    def square(values):
        return jnp.sum(mask * values * values)

    squares = jnp.stack(
        [square(v) for v in (x, mixed, ffn1, h, attn_rows, res2, ffn2, result)]
    )

    d_sum_low = (lax.dynamic_index_in_dim(cotangent, section, keepdims=False).astype(F32) * mask).astype(BF16)
    d_sum = d_sum_low.astype(F32)
    d_ffn, gain3, grads2, _ = ffn_backward(d_sum_low, kept2, norm_gains[3], gate2, up2, down2)
    d_res2 = d_sum + d_ffn
    d_attn = d_res2.astype(BF16)
    grad_proj = matmul_left(attended_low, d_attn)
    d_att = matmul_right(d_attn, proj_full).astype(BF16)
    d_query, d_key_all, d_value_all = attend_back(
        query, key_all, value_all, allowed, log_total, attended, d_att
    )
    half = part // 2

    def shared_halves(grad, lead):
        pieces = grad.reshape(lead, 2, -1, grad.shape[1])
        mine = lax.dynamic_index_in_dim(pieces, section, 1, keepdims=False)
        other = swapped(lax.dynamic_index_in_dim(pieces, 1 - section, 1, keepdims=False), "section")
        return (mine.astype(F32) + other.astype(F32)).astype(BF16)

    d_kv_terms = jnp.concatenate(
        [d_key_all.reshape(-1, kv_width), d_value_all.reshape(-1, kv_width)], axis=1
    ).astype(BF16)
    d_kv_terms, second = lax.optimization_barrier(
        (
            d_kv_terms,
            (
                shared_halves(jnp.concatenate(grads2[:2], axis=0), 2 * fsdp),
                shared_halves(grads2[2], 1)[0],
            ),
        )
    )
    second = tuple(
        lax.psum_scatter(term.reshape(-1, term.shape[-1]), "ctx", scatter_dimension=0, tiled=True)
        for term in second
    )
    d_kv = jnp.sum(
        swapped_blocks(d_kv_terms, "ctx", 4).reshape(lax.axis_size("ctx"), rows, -1).astype(F32), axis=0
    )
    d_qn = rounded(d_query)
    grad_qgain = jnp.sum(d_qn * q_normed, axis=(0, 1))
    d_qpre = norm_back(d_qn * head_gains[0], q_normed, q_inv).reshape(rows, -1).astype(BF16)
    d_kn = rounded(d_kv[:, :kv_width]).reshape(rows, kv_heads, head)
    grad_kgain = jnp.sum(d_kn * k_normed, axis=(0, 1))
    d_kpre = norm_back(d_kn * head_gains[1], k_normed, k_inv).reshape(rows, -1).astype(BF16)
    d_vpre = d_kv[:, kv_width:].astype(BF16)
    d_act2 = (
        matmul_right(d_qpre, query_full)
        + matmul_right(d_kpre, key_full)
        + matmul_right(d_vpre, value_full)
    )
    gain2 = jnp.sum(d_act2 * normed2, axis=0)
    d_h_low = (d_res2 + norm_back(d_act2 * norm_gains[2], normed2, inv2)).astype(BF16)

    d_ffn1, gain1, grads1, second = ffn_backward(
        d_h_low, kept1, norm_gains[1], gate1, up1, down1, second
    )
    second = tuple(lax.all_gather(term, "ctx", axis=0, tiled=True) for term in second)
    d_res1 = d_h_low.astype(F32) + d_ffn1
    d_mixed = d_res1.astype(BF16)
    grad_out = matmul_left(z_low, d_mixed)
    d_z = matmul_right(d_mixed, out_full)
    d_cgate = d_z * convolved
    d_conv = d_z * c_gate
    grad_kernel = jnp.stack(
        [
            jnp.sum(d_conv * extended[:-2], axis=0),
            jnp.sum(d_conv * extended[1:-1], axis=0),
            jnp.sum(d_conv * extended[2:], axis=0),
        ]
    )
    d_extended = (
        jnp.pad(d_conv * conv_kernel[0], ((0, 2), (0, 0)))
        + jnp.pad(d_conv * conv_kernel[1], ((1, 1), (0, 0)))
        + jnp.pad(d_conv * conv_kernel[2], ((2, 0), (0, 0)))
    )
    from_next, second_gu = lax.optimization_barrier(
        (passed_along(d_extended[:2], "ctx", -1), second[0])
    )
    d_bproduct = rounded(d_extended[2:] + jnp.pad(from_next, ((rows - 2, 0), (0, 0))))
    d_projected = jnp.concatenate(
        [d_bproduct * x_value, d_cgate, d_bproduct * b_gate], axis=1
    ).astype(BF16)
    d_act1 = matmul_right(d_projected, in_full)
    gain0 = jnp.sum(d_act1 * normed0, axis=0)
    d_x = (d_res1 + norm_back(d_act1 * norm_gains[0], normed0, inv0)).astype(BF16)

    y_low = result.astype(BF16)
    is_first = section == 0
    other_end = swapped(jnp.where(is_first, y_low, d_x), "section")
    ends = jnp.where(is_first, jnp.stack([d_x, other_end]), jnp.stack([other_end, y_low]))[None]

    grad_parts = [
        matmul_left(act1, d_projected[:, i * width : (i + 1) * width]).astype(BF16) for i in range(3)
    ]
    mixers = [
        matmul_left(act2, d_qpre).astype(BF16),
        matmul_left(act2, jnp.concatenate([d_kpre, d_vpre], axis=1)).astype(BF16),
        grad_proj.astype(BF16),
    ] + grad_parts + [grad_out.astype(BF16)]

    cut = width // fsdp
    head_cut = head // fsdp
    square_cut = squares.shape[0] // fsdp
    by_owner = jnp.concatenate(
        [
            jnp.concatenate([jnp.stack([gain0, gain1, gain2, gain3]), grad_kernel])
            .reshape(7, fsdp, cut)
            .transpose(1, 0, 2)
            .reshape(fsdp, 7 * cut),
            jnp.stack([grad_qgain, grad_kgain])
            .reshape(2, fsdp, head_cut)
            .transpose(1, 0, 2)
            .reshape(fsdp, 2 * head_cut),
            squares.reshape(fsdp, square_cut),
            jnp.zeros((fsdp, cut - 2 * head_cut - square_cut), F32),
        ],
        axis=1,
    ).reshape(fsdp, 1, -1, width)
    small = jnp.pad(by_owner, ((0, 0), (0, 1), (0, 16 - by_owner.shape[2]), (0, 0))).astype(BF16)
    gu_sum, down_sum, rest_sum = summed_gradients(
        grads1,
        mixers,
        small,
        second_gu.reshape(2, fsdp, part // 2, -1),
        second[1],
    )
    rest_sum = rest_sum.astype(F32)

    def block(index):
        rows_at = slice(index * half, (index + 1) * half)
        return rest_sum[:, rows_at].reshape(2 * half, width)

    attn_blocks = [block(i) for i in range(3)]
    conv_blocks = [block(3 + i) for i in range(4)]
    small_sum = rest_sum[0, 7 * half : 7 * half + 2].reshape(-1)
    mine = small_sum[: 7 * cut].reshape(7, cut)
    heads = small_sum[7 * cut : 7 * cut + 2 * head_cut].reshape(2, head_cut)
    square_sum = small_sum[7 * cut + 2 * head_cut : 7 * cut + 2 * head_cut + square_cut]
    token_total = jnp.sum(lengths).astype(F32) * width
    rms = jnp.sqrt(square_sum / token_total)
    return (
        ends,
        mine[:3],
        mine[3],
        jnp.concatenate(conv_blocks[:3], axis=1),
        mine[4:7],
        conv_blocks[3],
        attn_blocks[0],
        attn_blocks[1][:, :kv_width],
        attn_blocks[1][:, kv_width:],
        attn_blocks[2],
        heads,
        gu_sum[0][None].astype(F32),
        gu_sum[1][None].astype(F32),
        down_sum[None].astype(F32),
        rms,
    )


def solution(mesh):
    return jax.shard_map(
        shards,
        mesh=mesh,
        in_specs=(
            P("fsdp", "ctx", None),
            P("fsdp", "ctx", None),
            P(),
            P(),
            P("fsdp", None),
            P(),
            P("fsdp", None),
            P("fsdp", None),
            P("fsdp", None),
            P("fsdp", None),
            P("fsdp", None),
            P(),
            P("section", "fsdp", None),
            P("section", "fsdp", None),
            P("section", "fsdp", None),
        ),
        out_specs=(
            P("section", "fsdp", "ctx", None),
            P(None, "fsdp"),
            P("fsdp"),
            P("fsdp", None),
            P(None, "fsdp"),
            P("fsdp", None),
            P("fsdp", None),
            P("fsdp", None),
            P("fsdp", None),
            P("fsdp", None),
            P(None, "fsdp"),
            P("section", "fsdp", None),
            P("section", "fsdp", None),
            P("section", "fsdp", None),
            P("fsdp"),
        ),
        check_vma=False,
    )
```

```python
import functools

import jax
import jax.numpy as jnp
from jax import lax
from jax.experimental import pallas as pl
from jax.experimental.pallas import tpu as pltpu
from jax.sharding import PartitionSpec as P

EPSILON = 1e-05
NEGATIVE = -1e30
MESH = pl.DeviceIdType.MESH
F32 = jnp.float32
BF16 = jnp.bfloat16


def passed_along(block, axis, distance):
    devices = range(lax.axis_size(axis))
    route = [(i - distance, i) for i in devices if i - distance in devices]
    return lax.ppermute(block, axis, route)


def swapped(block, axis):
    return lax.ppermute(block, axis, [(0, 1), (1, 0)])


def rounded(values):
    return lax.optimization_barrier(values.astype(BF16)).astype(F32)


def matmul(left_op, right_op):
    return jnp.dot(left_op, right_op, preferred_element_type=F32)


def matmul_left(left_op, right_op):
    return lax.dot_general(left_op, right_op, (((0,), (0,)), ((), ())), preferred_element_type=F32)


def matmul_right(left_op, right_op):
    return lax.dot_general(left_op, right_op, (((1,), (1,)), ((), ())), preferred_element_type=F32)


def norm_rows(values):
    inv_rms = lax.rsqrt(jnp.mean(values * values, axis=-1, keepdims=True) + EPSILON)
    return (values * inv_rms, inv_rms)


def norm_back(dnormed, normed, inv_rms):
    return inv_rms * dnormed - normed * inv_rms * jnp.mean(dnormed * normed, axis=-1, keepdims=True)


def busy(microseconds):
    return pl.CostEstimate(flops=int(microseconds), bytes_accessed=1 << 16, transcendentals=0)


def corners():
    me = lax.axis_index("fsdp")
    beside = me + 1 - 2 * lax.rem(me, 2)
    across = lax.rem(me + 2, 4)
    return me, beside, across, lax.rem(beside + 2, 4)


def greet_sides():
    _, beside, across, _ = corners()
    barrier = pltpu.get_barrier_semaphore()
    for target in (beside, across):
        pl.semaphore_signal(barrier, inc=1, device_id={"fsdp": target}, device_id_type=MESH)
    pl.semaphore_wait(barrier, 2)


def to_side(src, dst, send_sem, recv_sem, target):
    return pltpu.make_async_remote_copy(
        src_ref=src,
        dst_ref=dst,
        send_sem=send_sem,
        recv_sem=recv_sem,
        device_id={"fsdp": target},
        device_id_type=MESH,
    )


class SideGather:
    def __init__(self, block, whole, send_sem, recv_sem, own_sem):
        me, beside, across, _ = corners()
        rows = block.shape[0]
        half = rows // 2

        def part(owner, start, size):
            return whole.at[pl.ds(pl.multiple_of(owner * rows + start, half), size)]

        self.first = to_side(block, part(me, 0, rows), send_sem.at[0], recv_sem.at[0], beside)
        self.second = to_side(block, part(me, 0, rows), send_sem.at[1], recv_sem.at[1], across)
        at = part(beside, 0, half)
        self.third = to_side(at, at, send_sem.at[2], recv_sem.at[2], across)
        at = part(across, half, half)
        self.fourth = to_side(at, at, send_sem.at[3], recv_sem.at[3], beside)
        self.own = pltpu.make_async_copy(block, part(me, 0, rows), own_sem)

    def start(self):
        self.first.start()
        self.second.start()
        self.own.start()

    def relay(self):
        self.first.wait_recv()
        self.third.start()
        self.second.wait_recv()
        self.fourth.start()

    def finish(self):
        self.own.wait()
        self.first.wait_send()
        self.second.wait_send()
        self.third.wait()
        self.fourth.wait()


def gather_kernel(block, whole, send_sem, recv_sem, own_sem):
    greet_sides()
    gather = SideGather(block, whole, send_sem, recv_sem, own_sem)
    gather.start()
    gather.relay()
    gather.finish()


def gathered(array, collective_id):
    rows, width = array.shape
    assert lax.axis_size("fsdp") == 4
    dma = pltpu.SemaphoreType.DMA
    return pl.pallas_call(
        gather_kernel,
        out_shape=jax.ShapeDtypeStruct((4 * rows, width), array.dtype),
        in_specs=[pl.BlockSpec(memory_space=pltpu.VMEM)],
        out_specs=pl.BlockSpec(memory_space=pltpu.VMEM),
        scratch_shapes=[dma((4,)), dma((4,)), dma],
        compiler_params=pltpu.CompilerParams(
            collective_id=collective_id, has_side_effects=True, vmem_limit_bytes=8 << 20
        ),
        cost_estimate=busy(25),
    )(array)


class SideReduce:
    def __init__(self, blocks, total, beside_got, across_got, passed, passed_got, send_sem, recv_sem):
        self.refs = blocks, total, beside_got, across_got, passed, passed_got
        me, beside, across, opposite = corners()
        self.me, self.beside, self.across = me, beside, across
        self.copies = []
        for index, (turn, target, got) in enumerate(((0, beside, beside_got), (1, across, across_got))):
            for slot, owner in ((1, opposite), (0, target)):
                self.copies.append(
                    to_side(
                        blocks.at[self.part(owner, turn)],
                        got.at[slot],
                        send_sem.at[2 * index + slot],
                        recv_sem.at[2 * index + slot],
                        target,
                    )
                )
        self.onward = [
            to_side(passed.at[turn], passed_got.at[turn], send_sem.at[4 + turn], recv_sem.at[4 + turn], owner)
            for turn, owner in ((0, across), (1, beside))
        ]

    def part(self, owner, turn):
        half = self.refs[1].shape[0] // 2
        return pl.ds(pl.multiple_of(owner * 2 * half + turn * half, half), half)

    def start(self):
        for index in (0, 2, 1, 3):
            self.copies[index].start()

    def relay(self):
        blocks, _, beside_got, across_got, passed, _ = self.refs
        for turn, owner, index, got in ((0, self.across, 0, beside_got), (1, self.beside, 2, across_got)):
            self.copies[index].wait_recv()
            passed[turn] = (blocks[self.part(owner, turn)].astype(F32) + got[1].astype(F32)).astype(BF16)
            self.onward[turn].start()

    def finish(self):
        blocks, total, beside_got, across_got, _, passed_got = self.refs
        half = total.shape[0] // 2
        for turn, index, got in ((0, 1, beside_got), (1, 3, across_got)):
            self.copies[index].wait_recv()
            total[pl.ds(turn * half, half)] = blocks[self.part(self.me, turn)].astype(F32) + got[0].astype(F32)
        for turn in range(2):
            self.onward[turn].wait_recv()
            at = pl.ds(turn * half, half)
            total[at] = total[at] + passed_got[turn].astype(F32)
        for copy in self.copies + self.onward:
            copy.wait_send()


def reduce_kernel(blocks, total, beside_got, across_got, passed, passed_got, send_sem, recv_sem):
    greet_sides()
    reduction = SideReduce(blocks, total, beside_got, across_got, passed, passed_got, send_sem, recv_sem)
    reduction.start()
    reduction.relay()
    reduction.finish()


def reduced(partial, collective_id):
    rows, width = partial.shape[0] // 4, partial.shape[1]
    assert lax.axis_size("fsdp") == 4
    dma = pltpu.SemaphoreType.DMA
    pair = pltpu.VMEM((2, rows // 2, width), BF16)
    return pl.pallas_call(
        reduce_kernel,
        out_shape=jax.ShapeDtypeStruct((rows, width), F32),
        in_specs=[pl.BlockSpec(memory_space=pltpu.VMEM)],
        out_specs=pl.BlockSpec(memory_space=pltpu.VMEM),
        scratch_shapes=[pair, pair, pair, pair, dma((6,)), dma((6,))],
        compiler_params=pltpu.CompilerParams(
            collective_id=collective_id, has_side_effects=True, vmem_limit_bytes=16 << 20
        ),
        cost_estimate=busy(25),
    )(partial.astype(BF16))


def tail_kernel(
    counts,
    gate_in,
    up_in,
    down_in,
    query_in,
    kv_in,
    proj_in,
    conv_b_in,
    conv_c_in,
    conv_x_in,
    conv_o_in,
    small_in,
    second_gu_in,
    second_down_in,
    gu_out,
    down_out,
    rest_out,
    a_own,
    a_other,
    a_sum,
    a_done,
    b_own,
    b_other,
    b_sum,
    b_done,
    c_own,
    c_other,
    c_got,
    own_sem,
    pair_send,
    pair_recv,
    c_own_sem,
    c_pair_send,
    c_pair_recv,
    c_send,
    c_recv,
    a_up_send,
    a_up_recv,
    a_back_send,
    a_back_recv,
    a_out_send,
    b_up_send,
    b_up_recv,
    b_back_send,
    b_back_recv,
    b_out_send,
    b_keep_sem,
    gu_recv,
    down_recv,
    rest_recv,
    second_send,
):
    n_ctx, n_fsdp = counts
    section = lax.axis_index("section")
    place = lax.axis_index("ctx")
    group = lax.axis_index("fsdp")
    other = 1 - section
    a_chunks, a_rows, a_width = a_own.shape
    b_chunks, b_rows, b_width = b_own.shape
    half = gate_in.shape[0] // n_fsdp // 2
    subs = half // a_rows
    per_kind = n_fsdp * subs
    down_half = down_in.shape[0] // 2
    down_chunks = down_half // b_rows
    c_rows = c_own.shape[1]
    mixers = (query_in, kv_in, proj_in, conv_b_in, conv_c_in, conv_x_in, conv_o_in)
    n_mix = len(mixers)
    cut = 3 * half // b_rows
    c_parts = ((0, cut), (cut, c_rows // b_rows))
    ticks = a_chunks // 2
    tail = 2 * (n_ctx - 1)

    barrier = pltpu.get_barrier_semaphore()
    for step in range(1, 2 * n_fsdp):
        flat = lax.rem(section * n_fsdp + group + step, 2 * n_fsdp)
        pl.semaphore_signal(
            barrier,
            inc=1,
            device_id={"section": flat // n_fsdp, "fsdp": lax.rem(flat, n_fsdp)},
            device_id_type=MESH,
        )

    @pl.when(place > 0)
    def _():
        pl.semaphore_signal(barrier, inc=1, device_id={"ctx": place - 1}, device_id_type=MESH)

    @pl.when(place < n_ctx - 1)
    def _():
        pl.semaphore_signal(barrier, inc=1, device_id={"ctx": place + 1}, device_id_type=MESH)

    at_edge = (place == 0) | (place == n_ctx - 1)

    @pl.when(at_edge)
    def _():
        pl.semaphore_wait(barrier, 2 * n_fsdp)

    @pl.when(jnp.logical_not(at_edge))
    def _():
        pl.semaphore_wait(barrier, 2 * n_fsdp + 1)

    def half_rows(owner, which):
        return pl.ds(pl.multiple_of(owner * (2 * half) + which * half, half), half)

    local, pair = [], []
    for kind, source in enumerate((gate_in, up_in)):
        for owner in range(n_fsdp):
            index = kind * n_fsdp + owner
            slot = pl.ds(index * subs, subs)
            for sub in range(subs):
                src_own = source.at[pl.ds(pl.multiple_of(owner * (2 * half) + section * half + sub * a_rows, a_rows), a_rows)]
                src_other = source.at[pl.ds(pl.multiple_of(owner * (2 * half) + other * half + sub * a_rows, a_rows), a_rows)]
                spot = index * subs + sub
                local.append(pltpu.make_async_copy(src_own, a_own.at[spot], own_sem.at[spot]))
                pair.append(
                    pltpu.make_async_remote_copy(
                        src_ref=src_other,
                        dst_ref=a_other.at[spot],
                        send_sem=pair_send.at[spot],
                        recv_sem=pair_recv.at[spot],
                        device_id={"section": other},
                        device_id_type=MESH,
                    )
                )
    for chunk in range(down_chunks):
        spot = a_chunks + chunk
        src_own = down_in.at[pl.ds(pl.multiple_of(section * down_half + chunk * b_rows, b_rows), b_rows)]
        src_other = down_in.at[pl.ds(pl.multiple_of(other * down_half + chunk * b_rows, b_rows), b_rows)]
        local.append(pltpu.make_async_copy(src_own, b_own.at[chunk], own_sem.at[spot]))
        pair.append(
            pltpu.make_async_remote_copy(
                src_ref=src_other,
                dst_ref=b_other.at[chunk],
                send_sem=pair_send.at[spot],
                recv_sem=pair_recv.at[spot],
                device_id={"section": other},
                device_id_type=MESH,
            )
        )
    for copy in pair:
        copy.start()
    for copy in local:
        copy.start()
    c_local, c_pair = ([], []), ([], [])
    for kind, source in enumerate(mixers):
        part = 0 if kind < 3 else 1
        for owner in range(n_fsdp):
            index = owner * (n_mix + 1) + kind
            place_at = pl.ds(kind * half, half)
            c_local[part].append(
                pltpu.make_async_copy(
                    source.at[half_rows(owner, section)], c_own.at[owner, place_at], c_own_sem.at[index]
                )
            )
            c_pair[part].append(
                pltpu.make_async_remote_copy(
                    src_ref=source.at[half_rows(owner, other)],
                    dst_ref=c_other.at[owner, place_at],
                    send_sem=c_pair_send.at[index],
                    recv_sem=c_pair_recv.at[index],
                    device_id={"section": other},
                    device_id_type=MESH,
                )
            )
    for owner in range(n_fsdp):
        small_at = pl.ds(n_mix * half, c_rows - n_mix * half)
        index = owner * (n_mix + 1) + n_mix
        c_local[1].append(
            pltpu.make_async_copy(small_in.at[owner, section], c_own.at[owner, small_at], c_own_sem.at[index])
        )
        c_pair[1].append(
            pltpu.make_async_remote_copy(
                src_ref=small_in.at[owner, other],
                dst_ref=c_other.at[owner, small_at],
                send_sem=c_pair_send.at[index],
                recv_sem=c_pair_recv.at[index],
                device_id={"section": other},
                device_id_type=MESH,
            )
        )
    for part in range(2):
        for copy in c_pair[part]:
            copy.start()
        for copy in c_local[part]:
            copy.start()
    b_own[b_chunks - 1] = jnp.zeros((b_rows, b_width), BF16)
    for copy in local:
        copy.wait()
    for copy in pair:
        copy.wait_recv()

    def mixer_copy(part, step):
        target = lax.rem(group + step, n_fsdp)
        first, last = c_parts[part]
        at = pl.ds(first * b_rows, (last - first) * b_rows)
        return pltpu.make_async_remote_copy(
            src_ref=c_own.at[target, at],
            dst_ref=c_got.at[step - 1, at],
            send_sem=c_send.at[part, step],
            recv_sem=c_recv.at[part, step],
            device_id={"fsdp": target},
            device_id_type=MESH,
        )

    def mixer_out(part):
        for copy in c_local[part]:
            copy.wait()
        for copy in c_pair[part]:
            copy.wait_recv()
        first, last = c_parts[part]
        size = last - first

        def add(index, carry):
            owner = index // size
            at = pl.ds(pl.multiple_of((first + lax.rem(index, size)) * b_rows, b_rows), b_rows)
            c_own[owner, at] = (c_own[owner, at].astype(F32) + c_other[owner, at].astype(F32)).astype(BF16)
            return carry

        lax.fori_loop(0, n_fsdp * size, add, 0)
        for step in range(1, n_fsdp):
            mixer_copy(part, step).start()

    def mixer_in(part):
        for step in range(1, n_fsdp):
            mixer_copy(part, step).wait_recv()
        first, last = c_parts[part]

        def add(index, carry):
            at = pl.ds(pl.multiple_of(index * b_rows, b_rows), b_rows)
            total = c_own[group, at].astype(F32)
            for step in range(1, n_fsdp):
                total = total + c_got[step - 1, at].astype(F32)
            b_own[down_chunks + index] = total.astype(BF16)
            return carry

        lax.fori_loop(first, last, add, 0)

    def second_start():
        for kind in range(2):
            for owner in range(n_fsdp):
                index = kind * n_fsdp + owner
                src = second_gu_in.at[kind, owner]
                dst = gu_out.at[
                    kind,
                    pl.ds(pl.multiple_of(section * half, half), half),
                    pl.ds(pl.multiple_of(group * a_width, 128), a_width),
                ]
                is_mine = (section == 1) & (group == owner)

                @pl.when(is_mine)
                def _(src=src, dst=dst, index=index):
                    pltpu.make_async_copy(src, dst, second_send.at[index]).start()

                @pl.when(jnp.logical_not(is_mine))
                def _(src=src, dst=dst, index=index, kind=kind, owner=owner):
                    pltpu.make_async_remote_copy(
                        src_ref=src,
                        dst_ref=dst,
                        send_sem=second_send.at[index],
                        recv_sem=gu_recv.at[kind, section * n_fsdp + group],
                        device_id={"section": 1, "fsdp": owner},
                        device_id_type=MESH,
                    ).start()

        down_at = down_out.at[pl.ds(pl.multiple_of(section * down_half, b_rows), down_half)]

        @pl.when(section == 1)
        def _():
            pltpu.make_async_copy(second_down_in, down_at, second_send.at[2 * n_fsdp]).start()

        @pl.when(section == 0)
        def _():
            pltpu.make_async_remote_copy(
                src_ref=second_down_in,
                dst_ref=down_at,
                send_sem=second_send.at[2 * n_fsdp],
                recv_sem=down_recv,
                device_id={"section": 1},
                device_id_type=MESH,
            ).start()

    def a_target(k):
        kind = k // per_kind
        rest = lax.rem(k, per_kind)
        owner = rest // subs
        sub = lax.rem(rest, subs)
        spot = gu_out.at[
            kind,
            pl.ds(pl.multiple_of(section * half + sub * a_rows, a_rows), a_rows),
            pl.ds(pl.multiple_of(group * a_width, 128), a_width),
        ]
        return kind, owner, spot

    def hand_out(k):
        kind, owner, spot = a_target(k)
        is_mine = (section == 0) & (group == owner)

        @pl.when(is_mine)
        def _():
            pltpu.make_async_copy(a_done.at[k], spot, a_out_send.at[k]).start()

        @pl.when(jnp.logical_not(is_mine))
        def _():
            pltpu.make_async_remote_copy(
                src_ref=a_done.at[k],
                dst_ref=spot,
                send_sem=a_out_send.at[k],
                recv_sem=gu_recv.at[kind, section * n_fsdp + group],
                device_id={"section": 0, "fsdp": owner},
                device_id_type=MESH,
            ).start()

        @pl.when(k < down_chunks)
        def _():
            at = down_out.at[pl.ds(pl.multiple_of(section * down_half + k * b_rows, b_rows), b_rows)]

            @pl.when(section == 0)
            def _():
                pltpu.make_async_copy(b_done.at[k], at, b_out_send.at[k]).start()

            @pl.when(section == 1)
            def _():
                pltpu.make_async_remote_copy(
                    src_ref=b_done.at[k],
                    dst_ref=at,
                    send_sem=b_out_send.at[k],
                    recv_sem=down_recv,
                    device_id={"section": 0},
                    device_id_type=MESH,
                ).start()

        @pl.when(k >= down_chunks)
        def _():
            at = rest_out.at[section, pl.ds(pl.multiple_of((k - down_chunks) * b_rows, b_rows), b_rows)]
            pltpu.make_async_copy(b_done.at[k], at, b_keep_sem.at[k]).start()
            pltpu.make_async_remote_copy(
                src_ref=b_done.at[k],
                dst_ref=at,
                send_sem=b_out_send.at[k],
                recv_sem=rest_recv,
                device_id={"section": other},
                device_id_type=MESH,
            ).start()

    def up_copies(k, target):
        return (
            pltpu.make_async_remote_copy(
                src_ref=a_sum.at[k],
                dst_ref=a_sum.at[k],
                send_sem=a_up_send.at[k],
                recv_sem=a_up_recv.at[k],
                device_id={"ctx": target},
                device_id_type=MESH,
            ),
            pltpu.make_async_remote_copy(
                src_ref=b_sum.at[k],
                dst_ref=b_sum.at[k],
                send_sem=b_up_send.at[k],
                recv_sem=b_up_recv.at[k],
                device_id={"ctx": target},
                device_id_type=MESH,
            ),
        )

    def back_copies(k, target):
        return (
            pltpu.make_async_remote_copy(
                src_ref=a_done.at[k],
                dst_ref=a_done.at[k],
                send_sem=a_back_send.at[k],
                recv_sem=a_back_recv.at[k],
                device_id={"ctx": target},
                device_id_type=MESH,
            ),
            pltpu.make_async_remote_copy(
                src_ref=b_done.at[k],
                dst_ref=b_done.at[k],
                send_sem=b_back_send.at[k],
                recv_sem=b_back_recv.at[k],
                device_id={"ctx": target},
                device_id_type=MESH,
            ),
        )

    def own_term(k):
        @pl.when(k < down_chunks)
        def _():
            b_own[k] = (b_own[k].astype(F32) + b_other[k].astype(F32)).astype(BF16)

        return a_own[k].astype(F32) + a_other[k].astype(F32)

    lanes = []
    for way in range(2):
        rank = place if way == 0 else n_ctx - 1 - place
        ahead = place + 1 if way == 0 else place - 1
        behind = place - 1 if way == 0 else place + 1
        lanes.append((way, rank, ahead, behind))

    def tick_step(tick, carry):
        @pl.when(tick == 0)
        def _():
            mixer_out(0)

        @pl.when(tick == 2)
        def _():
            mixer_out(1)

        @pl.when(tick == down_chunks // 2)
        def _():
            mixer_in(0)

        @pl.when(tick == (down_chunks + cut) // 2)
        def _():
            mixer_in(1)
            second_start()

        for way, rank, ahead, behind in lanes:
            step = tick - rank
            k = 2 * jnp.clip(step, 0, ticks - 1) + way

            @pl.when((step >= 0) & (step < ticks))
            def _(k=k, rank=rank, ahead=ahead, behind=behind):
                term = own_term(k)

                @pl.when(rank == 0)
                def _():
                    a_sum[k] = term.astype(BF16)
                    b_sum[k] = b_own[k]

                @pl.when(rank > 0)
                def _():
                    for copy in up_copies(k, behind):
                        copy.wait_recv()

                @pl.when((rank > 0) & (rank < n_ctx - 1))
                def _():
                    a_sum[k] = (term + a_sum[k].astype(F32)).astype(BF16)
                    b_sum[k] = (b_own[k].astype(F32) + b_sum[k].astype(F32)).astype(BF16)

                @pl.when(rank < n_ctx - 1)
                def _():
                    for copy in up_copies(k, ahead):
                        copy.start()

                @pl.when(rank == n_ctx - 1)
                def _():
                    a_done[k] = (term + a_sum[k].astype(F32)).astype(BF16)
                    b_done[k] = (b_own[k].astype(F32) + b_sum[k].astype(F32)).astype(BF16)
                    for copy in back_copies(k, behind):
                        copy.start()
                    hand_out(k)

            late = tick - (tail - rank)
            j = 2 * jnp.clip(late, 0, ticks - 1) + way

            @pl.when((late >= 0) & (late < ticks) & (rank < n_ctx - 1))
            def _(j=j, rank=rank, ahead=ahead, behind=behind):
                for copy in back_copies(j, ahead):
                    copy.wait_recv()

                @pl.when(rank > 0)
                def _():
                    for copy in back_copies(j, behind):
                        copy.start()

                hand_out(j)

        return carry

    lax.fori_loop(0, ticks + tail, tick_step, 0)

    for copy in pair:
        copy.wait_send()
    for part in range(2):
        for copy in c_pair[part]:
            copy.wait_send()
        for step in range(1, n_fsdp):
            mixer_copy(part, step).wait_send()

    def settle(step, carry):
        for way, rank, ahead, behind in lanes:
            k = 2 * step + way

            @pl.when(rank < n_ctx - 1)
            def _(k=k, ahead=ahead):
                for copy in up_copies(k, ahead):
                    copy.wait_send()

            @pl.when(rank > 0)
            def _(k=k, behind=behind):
                for copy in back_copies(k, behind):
                    copy.wait_send()

            _, _, spot = a_target(k)
            pltpu.make_async_copy(a_done.at[k], spot, a_out_send.at[k]).wait()
            pltpu.make_async_copy(b_done.at[k], b_own.at[k], b_out_send.at[k]).wait()

            @pl.when(k >= down_chunks)
            def _(k=k):
                pltpu.make_async_copy(b_done.at[k], b_own.at[k], b_keep_sem.at[k]).wait()

        return carry

    lax.fori_loop(0, ticks, settle, 0)
    for kind in range(2):
        for owner in range(n_fsdp):
            src = second_gu_in.at[kind, owner]
            pltpu.make_async_copy(src, src, second_send.at[kind * n_fsdp + owner]).wait()
    pltpu.make_async_copy(second_down_in, second_down_in, second_send.at[2 * n_fsdp]).wait()
    for kind in range(2):
        for source in range(2 * n_fsdp):

            @pl.when(section * n_fsdp + group != source)
            def _(kind=kind, source=source):
                region = gu_out.at[
                    kind,
                    pl.ds((source // n_fsdp) * half, half),
                    pl.ds((source % n_fsdp) * a_width, a_width),
                ]
                pltpu.make_async_copy(region, region, gu_recv.at[kind, source]).wait()

    region = down_out.at[pl.ds(pl.multiple_of(other * down_half, b_rows), down_half)]
    pltpu.make_async_copy(region, region, down_recv).wait()
    region = rest_out.at[other]
    pltpu.make_async_copy(region, region, rest_recv).wait()


def summed_gradients(first, mixers, small, second_gu, second_down):
    n_ctx, n_fsdp = lax.axis_size("ctx"), lax.axis_size("fsdp")
    gate, up, down = first
    half = gate.shape[0] // n_fsdp // 2
    a_rows, b_rows = half // 4, half * 3 // 8
    a_chunks = 2 * n_fsdp * 4
    a_width, b_width = gate.shape[1], down.shape[1]
    c_rows = len(mixers) * half + small.shape[2]
    down_chunks = down.shape[0] // 2 // b_rows
    b_chunks = down_chunks + c_rows // b_rows + 1
    assert a_chunks == b_chunks and c_rows % b_rows == 0
    rest = b_chunks - down_chunks
    dma = pltpu.SemaphoreType.DMA
    loads = a_chunks + down_chunks
    pieces = n_fsdp * (len(mixers) + 1)
    return pl.pallas_call(
        functools.partial(tail_kernel, (n_ctx, n_fsdp)),
        out_shape=(
            jax.ShapeDtypeStruct((2, 2 * half, n_fsdp * a_width), BF16),
            jax.ShapeDtypeStruct(down.shape, BF16),
            jax.ShapeDtypeStruct((2, rest * b_rows, b_width), BF16),
        ),
        in_specs=[pl.BlockSpec(memory_space=pl.ANY)] * (6 + len(mixers)),
        out_specs=[pl.BlockSpec(memory_space=pl.ANY)] * 3,
        scratch_shapes=[
            pltpu.VMEM((a_chunks, a_rows, a_width), BF16),
            pltpu.VMEM((a_chunks, a_rows, a_width), BF16),
            pltpu.VMEM((a_chunks, a_rows, a_width), BF16),
            pltpu.VMEM((a_chunks, a_rows, a_width), BF16),
            pltpu.VMEM((b_chunks, b_rows, b_width), BF16),
            pltpu.VMEM((down_chunks, b_rows, b_width), BF16),
            pltpu.VMEM((b_chunks, b_rows, b_width), BF16),
            pltpu.VMEM((b_chunks, b_rows, b_width), BF16),
            pltpu.VMEM((n_fsdp, c_rows, b_width), BF16),
            pltpu.VMEM((n_fsdp, c_rows, b_width), BF16),
            pltpu.VMEM((n_fsdp - 1, c_rows, b_width), BF16),
            dma((loads,)),
            dma((loads,)),
            dma((loads,)),
            dma((pieces,)),
            dma((pieces,)),
            dma((pieces,)),
            dma((2, n_fsdp)),
            dma((2, n_fsdp)),
            dma((a_chunks,)),
            dma((a_chunks,)),
            dma((a_chunks,)),
            dma((a_chunks,)),
            dma((a_chunks,)),
            dma((b_chunks,)),
            dma((b_chunks,)),
            dma((b_chunks,)),
            dma((b_chunks,)),
            dma((b_chunks,)),
            dma((b_chunks,)),
            dma((2, 2 * n_fsdp)),
            dma,
            dma,
            dma((2 * n_fsdp + 1,)),
        ],
        compiler_params=pltpu.CompilerParams(
            collective_id=6, has_side_effects=True, vmem_limit_bytes=56 << 20
        ),
        cost_estimate=busy(160),
    )(gate, up, down, *mixers, small, second_gu, second_down)


def mixer_weights_kernel(count, first_in, second_in, first_out, second_out, send_sem, recv_sem, pair_send, pair_recv, own_sem):
    section = lax.axis_index("section")
    me = lax.axis_index("fsdp")
    other = 1 - section
    beside = me + 1 - 2 * lax.rem(me, 2)
    across = lax.rem(me + 2, count)
    opposite = lax.rem(beside + 2, count)
    rows = first_in.shape[0]
    half = rows // 2
    quarter = half // 2
    barrier = pltpu.get_barrier_semaphore()
    for target in ({"fsdp": beside}, {"fsdp": across}, {"section": other}):
        pl.semaphore_signal(barrier, inc=1, device_id=target, device_id_type=MESH)
    pl.semaphore_wait(barrier, 3)
    arrays = ((first_in, first_out), (second_in, second_out))

    def at_rows(owner, extra, size):
        return pl.ds(pl.multiple_of(owner * rows + extra, quarter), size)

    def remote(slot, sems, src, dst, target):
        return pltpu.make_async_remote_copy(
            src_ref=src,
            dst_ref=dst,
            send_sem=sems[0].at[slot],
            recv_sem=sems[1].at[slot],
            device_id=target,
            device_id_type=MESH,
        )

    hop, pair = (send_sem, recv_sem), (pair_send, pair_recv)
    waiting = []
    direct = []
    for index, (source, out) in enumerate(arrays):
        mine = source.at[pl.ds(pl.multiple_of(section * half, half), half)]
        spot = out.at[at_rows(me, section * half, half)]
        copies = [
            remote(index * 4, hop, mine, spot, {"fsdp": beside}),
            remote(index * 4 + 1, hop, mine, spot, {"fsdp": across}),
        ]
        for copy in copies:
            copy.start()
        direct.append(copies)
    own = [
        pltpu.make_async_copy(source, out.at[at_rows(me, 0, rows)], own_sem.at[index])
        for index, (source, out) in enumerate(arrays)
    ]
    for copy in own:
        copy.start()

    def arrived(owner, size, extra):
        return lambda out: out.at[at_rows(owner, section * half + extra, size)]

    onward = []
    for index, (source, out) in enumerate(arrays):
        direct[index][0].wait_recv()
        part = arrived(beside, quarter, 0)(out)
        onward.append(remote(index * 4 + 2, hop, part, part, {"fsdp": across}))
        onward[-1].start()
        whole = arrived(beside, half, 0)(out)
        waiting.append(remote(index * 4, pair, whole, whole, {"section": other}))
        waiting[-1].start()
        direct[index][1].wait_recv()
        part = arrived(across, quarter, quarter)(out)
        onward.append(remote(index * 4 + 3, hop, part, part, {"fsdp": beside}))
        onward[-1].start()
        whole = arrived(across, half, 0)(out)
        waiting.append(remote(index * 4 + 1, pair, whole, whole, {"section": other}))
        waiting[-1].start()
    for index, (source, out) in enumerate(arrays):
        for turn in range(2):
            onward[2 * index + turn].wait_recv()
            part = arrived(opposite, quarter, turn * quarter)(out)
            waiting.append(remote(index * 4 + 2 + turn, pair, part, part, {"section": other}))
            waiting[-1].start()
    for copy in own:
        copy.wait()
    for copies in direct:
        for copy in copies:
            copy.wait_send()
    for copy in onward:
        copy.wait_send()
    for copy in waiting:
        copy.wait()


def mixer_weights(first, second, collective_id):
    count = lax.axis_size("fsdp")
    dma = pltpu.SemaphoreType.DMA
    return pl.pallas_call(
        functools.partial(mixer_weights_kernel, count),
        out_shape=tuple(
            jax.ShapeDtypeStruct((count * w.shape[0], w.shape[1]), w.dtype) for w in (first, second)
        ),
        in_specs=[pl.BlockSpec(memory_space=pl.ANY)] * 2,
        out_specs=[pl.BlockSpec(memory_space=pl.ANY)] * 2,
        scratch_shapes=[dma((8,)), dma((8,)), dma((8,)), dma((8,)), dma((2,))],
        compiler_params=pltpu.CompilerParams(
            collective_id=collective_id, has_side_effects=True, vmem_limit_bytes=8 << 20
        ),
        cost_estimate=busy(45),
    )(first, second)


class Columns:
    def __init__(self, holder, sources, targets, send_sem, recv_sem, pair_send, pair_recv, own_sem):
        self.count = 4
        self.holder = holder
        self.section = lax.axis_index("section")
        self.me = lax.axis_index("fsdp")
        self.sources, self.targets = sources, targets
        self.sems = send_sem, recv_sem, pair_send, pair_recv, own_sem
        self.rows = sources[0].shape[0]
        self.wide = targets[0].shape[1]
        self.steps = [(step, kind) for step in range(1, self.count) for kind in range(2)]

    def at_rows(self, out, owner):
        return out.at[pl.ds(pl.multiple_of(owner * self.rows, self.rows), self.rows)]

    def at_columns(self, source, owner):
        return source.at[:, pl.ds(pl.multiple_of(owner * self.wide, 128), self.wide)]

    def crossing(self, step, kind):
        target = lax.rem(self.me + step, self.count)
        return to_side(
            self.at_columns(self.sources[kind], target),
            self.at_rows(self.targets[kind], self.me),
            self.sems[0].at[kind, step],
            self.sems[1].at[kind, step],
            target,
        )

    def handed(self, step, kind):
        if kind == 2:
            src, dst = self.sources[2], self.targets[2]
        else:
            origin = lax.rem(self.me + self.count - step, self.count)
            dst = self.at_rows(self.targets[kind], origin)
            src = self.at_columns(self.sources[kind], self.me) if step == 0 else dst
        return pltpu.make_async_remote_copy(
            src_ref=src,
            dst_ref=dst,
            send_sem=self.sems[2].at[kind, step],
            recv_sem=self.sems[3].at[kind, step],
            device_id={"section": 1 - self.section},
            device_id_type=MESH,
        )

    def kept(self, kind):
        if kind == 2:
            return pltpu.make_async_copy(self.sources[2], self.targets[2], self.sems[4].at[2])
        return pltpu.make_async_copy(
            self.at_columns(self.sources[kind], self.me),
            self.at_rows(self.targets[kind], self.me),
            self.sems[4].at[kind],
        )

    def start(self):
        @pl.when(self.section == self.holder)
        def _():
            for step, kind in self.steps:
                self.crossing(step, kind).start()
            for kind in range(3):
                self.handed(0, kind).start()
            for kind in range(3):
                self.kept(kind).start()

    def relay(self):
        @pl.when(self.section == self.holder)
        def _():
            for step, kind in self.steps:
                self.crossing(step, kind).wait_recv()
                self.handed(step, kind).start()

    def finish(self):
        every = [(0, kind) for kind in range(3)] + self.steps

        @pl.when(self.section == self.holder)
        def _():
            for kind in range(3):
                self.kept(kind).wait()
            for step, kind in self.steps:
                self.crossing(step, kind).wait_send()
            for step, kind in every:
                self.handed(step, kind).wait_send()

        @pl.when(self.section != self.holder)
        def _():
            for step, kind in every:
                self.handed(step, kind).wait_recv()


def column_weights_kernel(holder, *refs):
    section = lax.axis_index("section")
    _, beside, across, opposite = corners()
    barrier = pltpu.get_barrier_semaphore()
    for target in ({"fsdp": beside}, {"fsdp": across}, {"fsdp": opposite}, {"section": 1 - section}):
        pl.semaphore_signal(barrier, inc=1, device_id=target, device_id_type=MESH)
    pl.semaphore_wait(barrier, 4)
    columns = Columns(holder, refs[:3], refs[3:6], *refs[6:])
    columns.start()
    columns.relay()
    columns.finish()


def column_weights(gate, up, down, holder, collective_id):
    count = lax.axis_size("fsdp")
    assert count == 4
    dma = pltpu.SemaphoreType.DMA
    column = jax.ShapeDtypeStruct((count * gate.shape[0], gate.shape[1] // count), gate.dtype)
    return pl.pallas_call(
        functools.partial(column_weights_kernel, holder),
        out_shape=(column, column, jax.ShapeDtypeStruct(down.shape, down.dtype)),
        in_specs=[pl.BlockSpec(memory_space=pl.ANY)] * 3,
        out_specs=[pl.BlockSpec(memory_space=pl.ANY)] * 3,
        scratch_shapes=[dma((2, count)), dma((2, count)), dma((3, count)), dma((3, count)), dma((3,))],
        compiler_params=pltpu.CompilerParams(
            collective_id=collective_id, has_side_effects=True, vmem_limit_bytes=8 << 20
        ),
        cost_estimate=busy(40),
    )(gate, up, down)


class Chain:
    def __init__(self, count):
        self.count = count
        self.place = lax.axis_index("ctx")
        self.has_next = self.place < count - 1
        self.has_last = self.place > 0


def greet_mixed(chain, targets):
    barrier = pltpu.get_barrier_semaphore()
    for target in targets:
        pl.semaphore_signal(barrier, inc=1, device_id=target, device_id_type=MESH)

    @pl.when(chain.has_last)
    def _():
        pl.semaphore_signal(barrier, inc=1, device_id={"ctx": chain.place - 1}, device_id_type=MESH)

    @pl.when(chain.has_next)
    def _():
        pl.semaphore_signal(barrier, inc=1, device_id={"ctx": chain.place + 1}, device_id_type=MESH)

    inner = chain.has_last & chain.has_next

    @pl.when(inner)
    def _():
        pl.semaphore_wait(barrier, len(targets) + 2)

    @pl.when(jnp.logical_not(inner))
    def _():
        pl.semaphore_wait(barrier, len(targets) + 1)


def along(src, dst, send_sem, recv_sem, place):
    return pltpu.make_async_remote_copy(
        src_ref=src,
        dst_ref=dst,
        send_sem=send_sem,
        recv_sem=recv_sem,
        device_id={"ctx": place},
        device_id_type=MESH,
    )


def spread_heads(source, spread):
    rows = source.shape[0]
    low = lax.broadcasted_iota(jnp.int32, (rows, 128), 1) < 64
    for pair in range(source.shape[1] // 256):
        first = source[:, pair * 256 : pair * 256 + 128].astype(F32)
        second = source[:, pair * 256 + 128 : pair * 256 + 256].astype(F32)
        spread[4 * pair] = jnp.where(low, first, 0.0).astype(BF16)
        spread[4 * pair + 1] = jnp.where(low, pltpu.roll(first, 64, 1), 0.0).astype(BF16)
        spread[4 * pair + 2] = jnp.where(low, 0.0, pltpu.roll(second, 64, 1)).astype(BF16)
        spread[4 * pair + 3] = jnp.where(low, 0.0, second).astype(BF16)


def join_heads(spread, target):
    rows = target.shape[0]
    low = lax.broadcasted_iota(jnp.int32, (rows, 128), 1) < 64
    for pair in range(target.shape[1] // 256):
        parts = [spread(4 * pair + i).T for i in range(4)]
        target[:, pair * 256 : pair * 256 + 128] = jnp.where(low, parts[0], pltpu.roll(parts[1], 64, 1))
        target[:, pair * 256 + 128 : pair * 256 + 256] = jnp.where(low, pltpu.roll(parts[2], 64, 1), parts[3])


def mask_block(bias, length, place, block):
    rows = bias.shape[0]
    key_at = block * rows + lax.broadcasted_iota(jnp.int32, bias.shape, 0)
    query_at = place * rows + lax.broadcasted_iota(jnp.int32, bias.shape, 1)
    bias[...] = jnp.where((key_at <= query_at) & (key_at < length), 0.0, NEGATIVE)


def dot_right(left, right):
    return lax.dot_general(left, right, (((1,), (1,)), ((), ())), preferred_element_type=F32)


def dot_plain(left, right):
    return jnp.dot(left, right, preferred_element_type=F32)


def attend_kernel(
    n_ctx,
    length_ref,
    query,
    kv,
    d_block,
    gate_in,
    up_in,
    down_in,
    attended,
    log_total,
    kv_all,
    d_all,
    gate_out,
    up_out,
    down_out,
    spread,
    bias,
    peak,
    total,
    out_t,
    kv_send,
    kv_recv,
    d_send,
    d_recv,
    d_own,
    send_sem,
    recv_sem,
    pair_send,
    pair_recv,
    own_sem,
):
    chain = Chain(n_ctx)
    place = chain.place
    section = lax.axis_index("section")
    me, beside, across, opposite = corners()
    greet_mixed(
        chain,
        [{"fsdp": beside}, {"fsdp": across}, {"fsdp": opposite}, {"section": 1 - section}],
    )
    rows = query.shape[0]
    half_width = kv.shape[1] // 2

    def block_rows(block):
        return pl.ds(pl.multiple_of(block * rows, rows), rows)

    def upward(step, src):
        return along(
            src,
            kv_all.at[block_rows(place - step)],
            kv_send.at[step],
            kv_recv.at[step + 1],
            place + 1,
        )

    def arriving(step):
        at = kv_all.at[block_rows(place - step)]
        return along(at, at, kv_send.at[step], kv_recv.at[step], place)

    @pl.when(chain.has_next)
    def _():
        upward(0, kv).start()

    gather = SideGather(d_block, d_all, d_send, d_recv, d_own)
    gather.start()
    columns = Columns(
        1, (gate_in, up_in, down_in), (gate_out, up_out, down_out), send_sem, recv_sem, pair_send, pair_recv, own_sem
    )
    columns.start()
    kv_all[block_rows(place)] = kv[...]
    spread_heads(query, spread)
    peak[...] = jnp.full(peak.shape, NEGATIVE, F32)
    total[...] = jnp.zeros(total.shape, F32)
    out_t[...] = jnp.zeros(out_t.shape, F32)
    length = length_ref[0]
    scale = 64 ** (-0.5)

    def attend_block(block):
        mask_block(bias, length, place, block)
        for pair in range(half_width // 128):
            key = kv_all[block_rows(block), pair * 128 : pair * 128 + 128]
            value_t = kv_all[block_rows(block), half_width + pair * 128 : half_width + pair * 128 + 128].T
            for index in range(4):
                head = 4 * pair + index
                scores = dot_right(key, spread[head]) * scale + bias[...]
                before = peak[head]
                now = jnp.maximum(before, jnp.max(scores, axis=0, keepdims=True))
                weights = jnp.exp(scores - now)
                fade = jnp.exp(before - now)
                peak[head] = now
                total[head] = total[head] * fade + jnp.sum(weights, axis=0, keepdims=True)
                out_t[head] = out_t[head] * fade + dot_plain(value_t, weights.astype(BF16))

    attend_block(place)
    gather.relay()

    def step_on(step, carry):
        @pl.when(step <= place)
        def _():
            arriving(step).wait_recv()

            @pl.when(chain.has_next)
            def _():
                upward(step, kv_all.at[block_rows(place - step)]).start()

            attend_block(place - step)

        return carry

    lax.fori_loop(1, n_ctx, step_on, 0)
    join_heads(lambda head: out_t[head] / total[head], attended)
    for head in range(spread.shape[0]):
        log_total[head] = peak[head] + jnp.log(total[head])
    columns.relay()
    gather.finish()
    columns.finish()

    def settle(step, carry):
        @pl.when((step <= place) & chain.has_next)
        def _():
            upward(step, kv_all.at[block_rows(place - step)]).wait_send()

        return carry

    lax.fori_loop(0, n_ctx, settle, 0)


def attend(length, query, kv, d_block, gate, up, down, collective_id):
    n_ctx, count = lax.axis_size("ctx"), lax.axis_size("fsdp")
    rows, width = query.shape
    heads = width // 64
    dma = pltpu.SemaphoreType.DMA
    vmem = pl.BlockSpec(memory_space=pltpu.VMEM)
    hbm = pl.BlockSpec(memory_space=pl.ANY)
    column = jax.ShapeDtypeStruct((count * gate.shape[0], gate.shape[1] // count), gate.dtype)
    return pl.pallas_call(
        functools.partial(attend_kernel, n_ctx),
        out_shape=(
            jax.ShapeDtypeStruct((rows, width), F32),
            jax.ShapeDtypeStruct((heads, 1, rows), F32),
            jax.ShapeDtypeStruct((n_ctx * rows, kv.shape[1]), BF16),
            jax.ShapeDtypeStruct((count * rows, d_block.shape[1]), BF16),
            column,
            column,
            jax.ShapeDtypeStruct(down.shape, down.dtype),
        ),
        in_specs=[pl.BlockSpec(memory_space=pltpu.SMEM), vmem, vmem, vmem, hbm, hbm, hbm],
        out_specs=[vmem, vmem, vmem, vmem, hbm, hbm, hbm],
        scratch_shapes=[
            pltpu.VMEM((heads, rows, 128), BF16),
            pltpu.VMEM((rows, rows), F32),
            pltpu.VMEM((heads, 1, rows), F32),
            pltpu.VMEM((heads, 1, rows), F32),
            pltpu.VMEM((heads, 128, rows), F32),
            dma((n_ctx + 1,)),
            dma((n_ctx + 1,)),
            dma((4,)),
            dma((4,)),
            dma,
            dma((2, count)),
            dma((2, count)),
            dma((3, count)),
            dma((3, count)),
            dma((3,)),
        ],
        compiler_params=pltpu.CompilerParams(
            collective_id=collective_id, has_side_effects=True, vmem_limit_bytes=40 << 20
        ),
        cost_estimate=busy(50),
    )(length, query, kv, d_block, gate, up, down)


def attend_back_kernel(
    n_ctx,
    length_ref,
    query,
    kv_all,
    d_out,
    log_total,
    delta,
    blocks,
    d_query,
    d_kv,
    reduced_out,
    spread,
    d_spread,
    bias,
    d_query_t,
    term,
    leaving,
    coming,
    kv_send,
    kv_recv,
    beside_got,
    across_got,
    passed,
    passed_got,
    send_sem,
    recv_sem,
):
    chain = Chain(n_ctx)
    place = chain.place
    _, beside, across, _ = corners()
    greet_mixed(chain, [{"fsdp": beside}, {"fsdp": across}])
    rows = query.shape[0]
    half_width = kv_all.shape[1] // 2
    reduction = SideReduce(blocks, reduced_out, beside_got, across_got, passed, passed_got, send_sem, recv_sem)
    reduction.start()
    spread_heads(query, spread)
    spread_heads(d_out, d_spread)
    d_query_t[...] = jnp.zeros(d_query_t.shape, F32)
    length = length_ref[0]
    scale = 64 ** (-0.5)

    def downward(block):
        return along(leaving.at[block], coming.at[block], kv_send.at[block], kv_recv.at[block], place - 1)

    def step_on(block, carry):
        @pl.when(block <= place)
        def _():
            mask_block(bias, length, place, block)
            at = pl.ds(pl.multiple_of(block * rows, rows), rows)
            for pair in range(half_width // 128):
                lanes = slice(pair * 128, pair * 128 + 128)
                more = slice(half_width + pair * 128, half_width + pair * 128 + 128)
                key = kv_all[at, lanes]
                value = kv_all[at, more]
                key_t = key.T
                d_key = jnp.zeros((rows, 128), F32)
                d_value = jnp.zeros((rows, 128), F32)
                for index in range(4):
                    head = 4 * pair + index
                    scores = dot_right(key, spread[head]) * scale + bias[...]
                    prob = jnp.exp(scores - log_total[head])
                    d_prob = dot_right(value, d_spread[head])
                    d_scores = (prob * (d_prob - delta[head])).astype(BF16)
                    d_value = d_value + dot_plain(prob.astype(BF16), d_spread[head])
                    d_key = d_key + dot_plain(d_scores, spread[head])
                    d_query_t[head] = d_query_t[head] + dot_plain(key_t, d_scores)
                term[:, lanes] = d_key * scale
                term[:, more] = d_value

            @pl.when(chain.has_next)
            def _():
                along(
                    leaving.at[block], coming.at[block], kv_send.at[block], kv_recv.at[block], place
                ).wait_recv()
                term[...] = term[...] + coming[block].astype(F32)

            @pl.when(block < place)
            def _():
                leaving[block] = term[...].astype(BF16)
                downward(block).start()

            @pl.when(block == place)
            def _():
                d_kv[...] = term[...]

        @pl.when(block == 0)
        def _():
            reduction.relay()

        return carry

    lax.fori_loop(0, n_ctx, step_on, 0)
    join_heads(lambda head: d_query_t[head] * scale, d_query)
    reduction.finish()

    def settle(block, carry):
        @pl.when(block < place)
        def _():
            downward(block).wait_send()

        return carry

    lax.fori_loop(0, n_ctx, settle, 0)


def attend_back(length, query, kv_all, d_out, log_total, delta, blocks, collective_id):
    n_ctx = lax.axis_size("ctx")
    rows, width = query.shape
    heads = width // 64
    dma = pltpu.SemaphoreType.DMA
    vmem = pl.BlockSpec(memory_space=pltpu.VMEM)
    wide = jax.ShapeDtypeStruct((rows, width), F32)
    pair = pltpu.VMEM((2, rows // 2, blocks.shape[1]), BF16)
    return pl.pallas_call(
        functools.partial(attend_back_kernel, n_ctx),
        out_shape=(wide, jax.ShapeDtypeStruct((rows, kv_all.shape[1]), F32), wide),
        in_specs=[pl.BlockSpec(memory_space=pltpu.SMEM)] + [vmem] * 6,
        out_specs=[vmem] * 3,
        scratch_shapes=[
            pltpu.VMEM((heads, rows, 128), BF16),
            pltpu.VMEM((heads, rows, 128), BF16),
            pltpu.VMEM((rows, rows), F32),
            pltpu.VMEM((heads, 128, rows), F32),
            pltpu.VMEM((rows, kv_all.shape[1]), F32),
            pltpu.VMEM((n_ctx, rows, kv_all.shape[1]), BF16),
            pltpu.VMEM((n_ctx, rows, kv_all.shape[1]), BF16),
            dma((n_ctx,)),
            dma((n_ctx,)),
            pair,
            pair,
            pair,
            pair,
            dma((6,)),
            dma((6,)),
        ],
        compiler_params=pltpu.CompilerParams(
            collective_id=collective_id, has_side_effects=True, vmem_limit_bytes=56 << 20
        ),
        cost_estimate=busy(50),
    )(length, query, kv_all, d_out, log_total, delta, blocks)


def ffn_forward(residual, gain, w_gate, w_up, w_down):
    normed, inv_rms = norm_rows(residual)
    act = gathered((normed * gain).astype(BF16), 0)
    gate_pre = matmul(act, w_gate)
    up_pre = matmul(act, w_up)
    hidden = (jax.nn.silu(gate_pre) * up_pre).astype(BF16)
    return matmul(hidden, w_down).astype(BF16), (normed, inv_rms, act, gate_pre, up_pre, hidden)


def ffn_backward(d_all, kept, gain, w_gate, w_up, w_down):
    normed, inv_rms, act, gate_pre, up_pre, hidden = kept
    d_hidden = matmul_right(d_all, w_down)
    sigmoid = jax.nn.sigmoid(gate_pre)
    d_up = (d_hidden * gate_pre * sigmoid).astype(BF16)
    d_gate = (d_hidden * up_pre * sigmoid * (1.0 + gate_pre * (1.0 - sigmoid))).astype(BF16)
    d_act = reduced(matmul_right(d_gate, w_gate) + matmul_right(d_up, w_up), 1)
    grad_gate = matmul_left(act, d_gate).astype(BF16)
    grad_up = matmul_left(act, d_up).astype(BF16)
    grad_down = matmul_left(hidden, d_all).astype(BF16)
    grad_gain = jnp.sum(d_act * normed, axis=0)
    return norm_back(d_act * gain, normed, inv_rms), grad_gain, (grad_gate, grad_up, grad_down)


def shards(
    inputs,
    cotangent,
    lengths,
    norm_gains,
    conv_in,
    conv_kernel,
    conv_out,
    attn_q,
    attn_k,
    attn_v,
    attn_out,
    head_gains,
    ffn_gate,
    ffn_up,
    ffn_down,
):
    micro, rows, width = inputs.shape
    section = lax.axis_index("section")
    group = lax.axis_index("fsdp")
    fsdp = lax.axis_size("fsdp")
    assert micro == lax.axis_size("section")
    head = head_gains.shape[1]
    q_width, kv_width = attn_q.shape[1], attn_k.shape[1]
    q_heads, kv_heads = q_width // head, kv_width // head
    positions = lax.axis_index("ctx") * rows + jnp.arange(rows)
    length = lax.dynamic_index_in_dim(lengths, group * micro + section, keepdims=False)
    mask = (positions < length).astype(F32)[:, None]

    def whole_rows(weight):
        half = weight.shape[0] // micro
        mine = lax.dynamic_slice_in_dim(weight, section * half, half, 0)
        return lax.all_gather(mine, ("fsdp", "section"), axis=0, tiled=True)

    part = ffn_gate.shape[1]
    in_full, out_full = mixer_weights(conv_in, conv_out, 2)
    gate1, up1, down1 = column_weights(ffn_gate[0], ffn_up[0], ffn_down[0], 0, 7)
    query_full, key_full, value_full, proj_full = (
        whole_rows(attn_q),
        whole_rows(attn_k),
        whole_rows(attn_v),
        whole_rows(attn_out),
    )

    x = lax.dynamic_index_in_dim(inputs, section, keepdims=False).astype(F32)
    normed0, inv0 = norm_rows(x)
    act1 = (normed0 * norm_gains[0]).astype(BF16)
    projected = matmul(act1, in_full)
    b_gate, c_gate, x_value = (
        projected[:, :width],
        projected[:, width : 2 * width],
        projected[:, 2 * width :],
    )
    b_product = (b_gate * x_value).astype(BF16)
    rim = passed_along(b_product[-2:], "ctx", 1)
    extended = jnp.concatenate([rim, b_product], axis=0).astype(F32)
    convolved = (
        conv_kernel[0] * extended[:-2]
        + conv_kernel[1] * extended[1:-1]
        + conv_kernel[2] * extended[2:]
    )
    z_low = (c_gate * convolved).astype(BF16)
    mixed = matmul(z_low, out_full)
    res1 = x + mixed
    terms1, kept1 = ffn_forward(res1, norm_gains[1], gate1, up1, down1)
    ffn1 = reduced(terms1, 1)
    h_low = (res1 + ffn1).astype(BF16)

    h = h_low.astype(F32)
    normed2, inv2 = norm_rows(h)
    act2 = (normed2 * norm_gains[2]).astype(BF16)
    q_normed, q_inv = norm_rows(matmul(act2, query_full).reshape(rows, q_heads, head))
    k_normed, k_inv = norm_rows(matmul(act2, key_full).reshape(rows, kv_heads, head))
    query = (q_normed * head_gains[0]).astype(BF16).reshape(rows, q_width)
    key = (k_normed * head_gains[1]).astype(BF16).reshape(rows, kv_width)
    value = matmul(act2, value_full).astype(BF16)
    d_sum_low = (lax.dynamic_index_in_dim(cotangent, section, keepdims=False).astype(F32) * mask).astype(BF16)
    attended, log_total, kv_all, d_sum_all, gate2, up2, down2 = attend(
        length.reshape(1),
        query,
        jnp.concatenate([key, value], axis=1),
        d_sum_low,
        ffn_gate[0],
        ffn_up[0],
        ffn_down[0],
        3,
    )
    attended_low = attended.astype(BF16)
    attn_rows = matmul(attended_low, proj_full)
    res2 = h + attn_rows
    terms2, kept2 = ffn_forward(res2, norm_gains[3], gate2, up2, down2)

    d_sum = d_sum_low.astype(F32)
    d_ffn, gain3, grads2 = ffn_backward(d_sum_all, kept2, norm_gains[3], gate2, up2, down2)
    d_res2 = d_sum + d_ffn
    d_attn = d_res2.astype(BF16)
    grad_proj = matmul_left(attended_low, d_attn)
    d_att = matmul_right(d_attn, proj_full).astype(BF16)
    half = part // 2

    def shared_halves(grad, lead):
        pieces = grad.reshape(lead, 2, -1, grad.shape[1])
        mine = lax.dynamic_index_in_dim(pieces, section, 1, keepdims=False)
        other = swapped(lax.dynamic_index_in_dim(pieces, 1 - section, 1, keepdims=False), "section")
        return (mine.astype(F32) + other.astype(F32)).astype(BF16)

    delta = jnp.sum((d_att.astype(F32) * attended).reshape(rows, q_heads, head), axis=-1)
    d_query, d_kv, ffn2 = attend_back(
        length.reshape(1), query, kv_all, d_att, log_total, delta.T.reshape(q_heads, 1, rows), terms2, 4
    )
    result = (res2 + ffn2) * mask

    def square(values):
        return jnp.sum(mask * values * values)

    squares = jnp.stack(
        [square(v) for v in (x, mixed, ffn1, h, attn_rows, res2, ffn2, result)]
    )
    second = (
        shared_halves(jnp.concatenate(grads2[:2], axis=0), 2 * fsdp),
        shared_halves(grads2[2], 1)[0],
    )
    second = tuple(
        lax.psum_scatter(term.reshape(-1, term.shape[-1]), "ctx", scatter_dimension=0, tiled=True)
        for term in second
    )
    d_qn = rounded(d_query).reshape(rows, q_heads, head)
    grad_qgain = jnp.sum(d_qn * q_normed, axis=(0, 1))
    d_qpre = norm_back(d_qn * head_gains[0], q_normed, q_inv).reshape(rows, -1).astype(BF16)
    d_kn = rounded(d_kv[:, :kv_width]).reshape(rows, kv_heads, head)
    grad_kgain = jnp.sum(d_kn * k_normed, axis=(0, 1))
    d_kpre = norm_back(d_kn * head_gains[1], k_normed, k_inv).reshape(rows, -1).astype(BF16)
    d_vpre = d_kv[:, kv_width:].astype(BF16)
    d_act2 = (
        matmul_right(d_qpre, query_full)
        + matmul_right(d_kpre, key_full)
        + matmul_right(d_vpre, value_full)
    )
    gain2 = jnp.sum(d_act2 * normed2, axis=0)
    d_h_low = (d_res2 + norm_back(d_act2 * norm_gains[2], normed2, inv2)).astype(BF16)

    d_h_all, second = lax.optimization_barrier((gathered(d_h_low, 0), second))
    d_ffn1, gain1, grads1 = ffn_backward(d_h_all, kept1, norm_gains[1], gate1, up1, down1)
    second = tuple(lax.all_gather(term, "ctx", axis=0, tiled=True) for term in second)
    d_res1 = d_h_low.astype(F32) + d_ffn1
    d_mixed = d_res1.astype(BF16)
    grad_out = matmul_left(z_low, d_mixed)
    d_z = matmul_right(d_mixed, out_full)
    d_cgate = d_z * convolved
    d_conv = d_z * c_gate
    grad_kernel = jnp.stack(
        [
            jnp.sum(d_conv * extended[:-2], axis=0),
            jnp.sum(d_conv * extended[1:-1], axis=0),
            jnp.sum(d_conv * extended[2:], axis=0),
        ]
    )
    d_extended = (
        jnp.pad(d_conv * conv_kernel[0], ((0, 2), (0, 0)))
        + jnp.pad(d_conv * conv_kernel[1], ((1, 1), (0, 0)))
        + jnp.pad(d_conv * conv_kernel[2], ((2, 0), (0, 0)))
    )
    from_next, second_gu = lax.optimization_barrier(
        (passed_along(d_extended[:2], "ctx", -1), second[0])
    )
    d_bproduct = rounded(d_extended[2:] + jnp.pad(from_next, ((rows - 2, 0), (0, 0))))
    d_projected = jnp.concatenate(
        [d_bproduct * x_value, d_cgate, d_bproduct * b_gate], axis=1
    ).astype(BF16)
    d_act1 = matmul_right(d_projected, in_full)
    gain0 = jnp.sum(d_act1 * normed0, axis=0)
    d_x = (d_res1 + norm_back(d_act1 * norm_gains[0], normed0, inv0)).astype(BF16)

    y_low = result.astype(BF16)
    is_first = section == 0
    other_end = swapped(jnp.where(is_first, y_low, d_x), "section")
    ends = jnp.where(is_first, jnp.stack([d_x, other_end]), jnp.stack([other_end, y_low]))[None]

    grad_parts = [
        matmul_left(act1, d_projected[:, i * width : (i + 1) * width]).astype(BF16) for i in range(3)
    ]
    mixers = [
        matmul_left(act2, d_qpre).astype(BF16),
        matmul_left(act2, jnp.concatenate([d_kpre, d_vpre], axis=1)).astype(BF16),
        grad_proj.astype(BF16),
    ] + grad_parts + [grad_out.astype(BF16)]

    cut = width // fsdp
    head_cut = head // fsdp
    square_cut = squares.shape[0] // fsdp
    by_owner = jnp.concatenate(
        [
            jnp.concatenate([jnp.stack([gain0, gain1, gain2, gain3]), grad_kernel])
            .reshape(7, fsdp, cut)
            .transpose(1, 0, 2)
            .reshape(fsdp, 7 * cut),
            jnp.stack([grad_qgain, grad_kgain])
            .reshape(2, fsdp, head_cut)
            .transpose(1, 0, 2)
            .reshape(fsdp, 2 * head_cut),
            squares.reshape(fsdp, square_cut),
            jnp.zeros((fsdp, cut - 2 * head_cut - square_cut), F32),
        ],
        axis=1,
    ).reshape(fsdp, 1, -1, width)
    small = jnp.pad(by_owner, ((0, 0), (0, 1), (0, 16 - by_owner.shape[2]), (0, 0))).astype(BF16)
    gu_sum, down_sum, rest_sum = summed_gradients(
        grads1,
        mixers,
        small,
        second_gu.reshape(2, fsdp, part // 2, -1),
        second[1],
    )
    rest_sum = rest_sum.astype(F32)

    def block(index):
        rows_at = slice(index * half, (index + 1) * half)
        return rest_sum[:, rows_at].reshape(2 * half, width)

    attn_blocks = [block(i) for i in range(3)]
    conv_blocks = [block(3 + i) for i in range(4)]
    small_sum = rest_sum[0, 7 * half : 7 * half + 2].reshape(-1)
    mine = small_sum[: 7 * cut].reshape(7, cut)
    heads = small_sum[7 * cut : 7 * cut + 2 * head_cut].reshape(2, head_cut)
    square_sum = small_sum[7 * cut + 2 * head_cut : 7 * cut + 2 * head_cut + square_cut]
    token_total = jnp.sum(lengths).astype(F32) * width
    rms = jnp.sqrt(square_sum / token_total)
    return (
        ends,
        mine[:3],
        mine[3],
        jnp.concatenate(conv_blocks[:3], axis=1),
        mine[4:7],
        conv_blocks[3],
        attn_blocks[0],
        attn_blocks[1][:, :kv_width],
        attn_blocks[1][:, kv_width:],
        attn_blocks[2],
        heads,
        gu_sum[0][None].astype(F32),
        gu_sum[1][None].astype(F32),
        down_sum[None].astype(F32),
        rms,
    )


def solution(mesh):
    return jax.shard_map(
        shards,
        mesh=mesh,
        in_specs=(
            P("fsdp", "ctx", None),
            P("fsdp", "ctx", None),
            P(),
            P(),
            P("fsdp", None),
            P(),
            P("fsdp", None),
            P("fsdp", None),
            P("fsdp", None),
            P("fsdp", None),
            P("fsdp", None),
            P(),
            P("section", "fsdp", None),
            P("section", "fsdp", None),
            P("section", "fsdp", None),
        ),
        out_specs=(
            P("section", "fsdp", "ctx", None),
            P(None, "fsdp"),
            P("fsdp"),
            P("fsdp", None),
            P(None, "fsdp"),
            P("fsdp", None),
            P("fsdp", None),
            P("fsdp", None),
            P("fsdp", None),
            P("fsdp", None),
            P(None, "fsdp"),
            P("section", "fsdp", None),
            P("section", "fsdp", None),
            P("section", "fsdp", None),
            P("fsdp"),
        ),
        check_vma=False,
    )
```

```python
import functools

import jax
import jax.numpy as jnp
from jax import lax
from jax.experimental import pallas as pl
from jax.experimental.pallas import tpu as pltpu
from jax.sharding import PartitionSpec as P

EPSILON = 1e-05
NEGATIVE = -1e30
MESH = pl.DeviceIdType.MESH
F32 = jnp.float32
BF16 = jnp.bfloat16


def passed_along(block, axis, distance):
    devices = range(lax.axis_size(axis))
    route = [(i - distance, i) for i in devices if i - distance in devices]
    return lax.ppermute(block, axis, route)


def swapped(block, axis):
    return lax.ppermute(block, axis, [(0, 1), (1, 0)])


def rounded(values):
    return lax.optimization_barrier(values.astype(BF16)).astype(F32)


def matmul(left_op, right_op):
    return jnp.dot(left_op, right_op, preferred_element_type=F32)


def matmul_left(left_op, right_op):
    return lax.dot_general(left_op, right_op, (((0,), (0,)), ((), ())), preferred_element_type=F32)


def matmul_right(left_op, right_op):
    return lax.dot_general(left_op, right_op, (((1,), (1,)), ((), ())), preferred_element_type=F32)


def norm_rows(values):
    inv_rms = lax.rsqrt(jnp.mean(values * values, axis=-1, keepdims=True) + EPSILON)
    return (values * inv_rms, inv_rms)


def norm_back(dnormed, normed, inv_rms):
    return inv_rms * dnormed - normed * inv_rms * jnp.mean(dnormed * normed, axis=-1, keepdims=True)


def head_sums(values, head):
    heads = values.shape[1] // head
    owner = (jnp.arange(values.shape[1])[:, None] // head == jnp.arange(heads)[None, :]).astype(F32)
    sums = jnp.dot(values, owner, precision=lax.Precision.HIGHEST, preferred_element_type=F32)
    return jnp.dot(sums, owner.T, precision=lax.Precision.HIGHEST, preferred_element_type=F32)


def norm_heads(values, head):
    inv_rms = lax.rsqrt(head_sums(values * values, head) / head + EPSILON)
    return (values * inv_rms, inv_rms)


def norm_heads_back(dnormed, normed, inv_rms, head):
    return inv_rms * dnormed - normed * inv_rms * (head_sums(dnormed * normed, head) / head)


def busy(microseconds):
    return pl.CostEstimate(flops=int(microseconds), bytes_accessed=1 << 16, transcendentals=0)


def corners():
    me = lax.axis_index("fsdp")
    beside = me + 1 - 2 * lax.rem(me, 2)
    across = lax.rem(me + 2, 4)
    return me, beside, across, lax.rem(beside + 2, 4)


def greet_sides():
    _, beside, across, _ = corners()
    barrier = pltpu.get_barrier_semaphore()
    for target in (beside, across):
        pl.semaphore_signal(barrier, inc=1, device_id={"fsdp": target}, device_id_type=MESH)
    pl.semaphore_wait(barrier, 2)


def to_side(src, dst, send_sem, recv_sem, target):
    return pltpu.make_async_remote_copy(
        src_ref=src,
        dst_ref=dst,
        send_sem=send_sem,
        recv_sem=recv_sem,
        device_id={"fsdp": target},
        device_id_type=MESH,
    )


class SideGather:
    def __init__(self, block, whole, send_sem, recv_sem, own_sem):
        me, beside, across, _ = corners()
        rows = block.shape[0]
        half = rows // 2

        def part(owner, start, size):
            return whole.at[pl.ds(pl.multiple_of(owner * rows + start, half), size)]

        self.first = to_side(block, part(me, 0, rows), send_sem.at[0], recv_sem.at[0], beside)
        self.second = to_side(block, part(me, 0, rows), send_sem.at[1], recv_sem.at[1], across)
        at = part(beside, 0, half)
        self.third = to_side(at, at, send_sem.at[2], recv_sem.at[2], across)
        at = part(across, half, half)
        self.fourth = to_side(at, at, send_sem.at[3], recv_sem.at[3], beside)
        self.own = pltpu.make_async_copy(block, part(me, 0, rows), own_sem)

    def start(self):
        self.first.start()
        self.second.start()
        self.own.start()

    def relay(self):
        self.first.wait_recv()
        self.third.start()
        self.second.wait_recv()
        self.fourth.start()

    def finish(self):
        self.own.wait()
        self.first.wait_send()
        self.second.wait_send()
        self.third.wait()
        self.fourth.wait()


def gather_kernel(block, whole, send_sem, recv_sem, own_sem):
    greet_sides()
    gather = SideGather(block, whole, send_sem, recv_sem, own_sem)
    gather.start()
    gather.relay()
    gather.finish()


def gathered(array, collective_id):
    rows, width = array.shape
    assert lax.axis_size("fsdp") == 4
    dma = pltpu.SemaphoreType.DMA
    return pl.pallas_call(
        gather_kernel,
        out_shape=jax.ShapeDtypeStruct((4 * rows, width), array.dtype),
        in_specs=[pl.BlockSpec(memory_space=pltpu.VMEM)],
        out_specs=pl.BlockSpec(memory_space=pltpu.VMEM),
        scratch_shapes=[dma((4,)), dma((4,)), dma],
        compiler_params=pltpu.CompilerParams(
            collective_id=collective_id, has_side_effects=True, vmem_limit_bytes=8 << 20
        ),
        cost_estimate=busy(25),
    )(array)


def gather_swap_kernel(block, pieces, whole, swapped_out, send_sem, recv_sem, own_sem, cross_send, cross_recv, keep_sem):
    me, beside, across, opposite = corners()
    barrier = pltpu.get_barrier_semaphore()
    for target in (beside, across, opposite):
        pl.semaphore_signal(barrier, inc=1, device_id={"fsdp": target}, device_id_type=MESH)
    pl.semaphore_wait(barrier, 3)
    gather = SideGather(block, whole, send_sem, recv_sem, own_sem)
    gather.start()
    crossing = []
    for step in range(1, 4):
        target = lax.rem(me + step, 4)
        crossing.append(
            to_side(pieces.at[target], swapped_out.at[me], cross_send.at[step], cross_recv.at[step], target)
        )
        crossing[-1].start()
    keep = pltpu.make_async_copy(pieces.at[me], swapped_out.at[me], keep_sem)
    keep.start()
    gather.relay()
    gather.finish()
    keep.wait()
    for copy in crossing:
        copy.wait()


def gathered_swapped(array, pieces, collective_id):
    rows, width = array.shape
    dma = pltpu.SemaphoreType.DMA
    vmem = pl.BlockSpec(memory_space=pltpu.VMEM)
    hbm = pl.BlockSpec(memory_space=pl.ANY)
    return pl.pallas_call(
        gather_swap_kernel,
        out_shape=(
            jax.ShapeDtypeStruct((4 * rows, width), array.dtype),
            jax.ShapeDtypeStruct(pieces.shape, pieces.dtype),
        ),
        in_specs=[vmem, hbm],
        out_specs=[vmem, hbm],
        scratch_shapes=[dma((4,)), dma((4,)), dma, dma((4,)), dma((4,)), dma],
        compiler_params=pltpu.CompilerParams(
            collective_id=collective_id, has_side_effects=True, vmem_limit_bytes=56 << 20
        ),
        cost_estimate=busy(25),
    )(array, pieces)


class SideReduce:
    def __init__(self, blocks, total, beside_got, across_got, passed, passed_got, send_sem, recv_sem):
        self.refs = blocks, total, beside_got, across_got, passed, passed_got
        me, beside, across, opposite = corners()
        self.me, self.beside, self.across = me, beside, across
        self.copies = []
        for index, (turn, target, got) in enumerate(((0, beside, beside_got), (1, across, across_got))):
            for slot, owner in ((1, opposite), (0, target)):
                self.copies.append(
                    to_side(
                        blocks.at[self.part(owner, turn)],
                        got.at[slot],
                        send_sem.at[2 * index + slot],
                        recv_sem.at[2 * index + slot],
                        target,
                    )
                )
        self.onward = [
            to_side(passed.at[turn], passed_got.at[turn], send_sem.at[4 + turn], recv_sem.at[4 + turn], owner)
            for turn, owner in ((0, across), (1, beside))
        ]

    def part(self, owner, turn):
        half = self.refs[1].shape[0] // 2
        return pl.ds(pl.multiple_of(owner * 2 * half + turn * half, half), half)

    def start(self):
        for index in (0, 2, 1, 3):
            self.copies[index].start()

    def relay(self):
        blocks, _, beside_got, across_got, passed, _ = self.refs
        for turn, owner, index, got in ((0, self.across, 0, beside_got), (1, self.beside, 2, across_got)):
            self.copies[index].wait_recv()
            passed[turn] = (blocks[self.part(owner, turn)].astype(F32) + got[1].astype(F32)).astype(BF16)
            self.onward[turn].start()

    def finish(self):
        blocks, total, beside_got, across_got, _, passed_got = self.refs
        half = total.shape[0] // 2
        for turn, index, got in ((0, 1, beside_got), (1, 3, across_got)):
            self.copies[index].wait_recv()
            total[pl.ds(turn * half, half)] = blocks[self.part(self.me, turn)].astype(F32) + got[0].astype(F32)
        for turn in range(2):
            self.onward[turn].wait_recv()
            at = pl.ds(turn * half, half)
            total[at] = total[at] + passed_got[turn].astype(F32)
        for copy in self.copies + self.onward:
            copy.wait_send()


def reduce_kernel(blocks, total, beside_got, across_got, passed, passed_got, send_sem, recv_sem):
    greet_sides()
    reduction = SideReduce(blocks, total, beside_got, across_got, passed, passed_got, send_sem, recv_sem)
    reduction.start()
    reduction.relay()
    reduction.finish()


def reduced(partial, collective_id):
    rows, width = partial.shape[0] // 4, partial.shape[1]
    assert lax.axis_size("fsdp") == 4
    dma = pltpu.SemaphoreType.DMA
    pair = pltpu.VMEM((2, rows // 2, width), BF16)
    return pl.pallas_call(
        reduce_kernel,
        out_shape=jax.ShapeDtypeStruct((rows, width), F32),
        in_specs=[pl.BlockSpec(memory_space=pltpu.VMEM)],
        out_specs=pl.BlockSpec(memory_space=pltpu.VMEM),
        scratch_shapes=[pair, pair, pair, pair, dma((6,)), dma((6,))],
        compiler_params=pltpu.CompilerParams(
            collective_id=collective_id, has_side_effects=True, vmem_limit_bytes=16 << 20
        ),
        cost_estimate=busy(25),
    )(partial.astype(BF16))


def tail_kernel(
    counts,
    gate_in,
    up_in,
    down_in,
    query_in,
    kv_in,
    proj_in,
    conv_b_in,
    conv_c_in,
    conv_x_in,
    conv_o_in,
    small_in,
    second_gu_in,
    second_down_in,
    gu_out,
    down_out,
    rest_out,
    a_own,
    a_other,
    a_sum,
    a_done,
    b_own,
    b_other,
    b_sum,
    b_done,
    c_own,
    c_other,
    c_got,
    own_sem,
    pair_send,
    pair_recv,
    c_own_sem,
    c_pair_send,
    c_pair_recv,
    c_send,
    c_recv,
    a_up_send,
    a_up_recv,
    a_back_send,
    a_back_recv,
    a_out_send,
    b_up_send,
    b_up_recv,
    b_back_send,
    b_back_recv,
    b_out_send,
    b_keep_sem,
    gu_recv,
    down_recv,
    rest_recv,
    second_send,
    second_recv,
):
    n_ctx, n_fsdp = counts
    section = lax.axis_index("section")
    place = lax.axis_index("ctx")
    group = lax.axis_index("fsdp")
    other = 1 - section
    a_chunks, a_rows, a_width = a_own.shape
    b_chunks, b_rows, b_width = b_own.shape
    half = gate_in.shape[0] // n_fsdp // 2
    subs = half // a_rows
    per_kind = n_fsdp * subs
    down_half = down_in.shape[0] // 2
    down_chunks = down_half // b_rows
    c_rows = c_own.shape[1]
    mixers = (query_in, kv_in, proj_in, conv_b_in, conv_c_in, conv_x_in, conv_o_in)
    n_mix = len(mixers)
    cut = 3 * half // b_rows
    c_parts = ((0, cut), (cut, c_rows // b_rows))
    ticks = a_chunks // 2
    tail = 2 * (n_ctx - 1)

    barrier = pltpu.get_barrier_semaphore()
    for step in range(1, 2 * n_fsdp):
        flat = lax.rem(section * n_fsdp + group + step, 2 * n_fsdp)
        pl.semaphore_signal(
            barrier,
            inc=1,
            device_id={"section": flat // n_fsdp, "fsdp": lax.rem(flat, n_fsdp)},
            device_id_type=MESH,
        )

    @pl.when(place > 0)
    def _():
        pl.semaphore_signal(barrier, inc=1, device_id={"ctx": place - 1}, device_id_type=MESH)

    @pl.when(place < n_ctx - 1)
    def _():
        pl.semaphore_signal(barrier, inc=1, device_id={"ctx": place + 1}, device_id_type=MESH)

    at_edge = (place == 0) | (place == n_ctx - 1)

    @pl.when(at_edge)
    def _():
        pl.semaphore_wait(barrier, 2 * n_fsdp)

    @pl.when(jnp.logical_not(at_edge))
    def _():
        pl.semaphore_wait(barrier, 2 * n_fsdp + 1)

    def half_rows(owner, which):
        return pl.ds(pl.multiple_of(owner * (2 * half) + which * half, half), half)

    local, pair = [], []
    for kind, source in enumerate((gate_in, up_in)):
        for owner in range(n_fsdp):
            index = kind * n_fsdp + owner
            slot = pl.ds(index * subs, subs)
            for sub in range(subs):
                src_own = source.at[pl.ds(pl.multiple_of(owner * (2 * half) + section * half + sub * a_rows, a_rows), a_rows)]
                src_other = source.at[pl.ds(pl.multiple_of(owner * (2 * half) + other * half + sub * a_rows, a_rows), a_rows)]
                spot = index * subs + sub
                local.append(pltpu.make_async_copy(src_own, a_own.at[spot], own_sem.at[spot]))
                pair.append(
                    pltpu.make_async_remote_copy(
                        src_ref=src_other,
                        dst_ref=a_other.at[spot],
                        send_sem=pair_send.at[spot],
                        recv_sem=pair_recv.at[spot],
                        device_id={"section": other},
                        device_id_type=MESH,
                    )
                )
    for chunk in range(down_chunks):
        spot = a_chunks + chunk
        src_own = down_in.at[pl.ds(pl.multiple_of(section * down_half + chunk * b_rows, b_rows), b_rows)]
        src_other = down_in.at[pl.ds(pl.multiple_of(other * down_half + chunk * b_rows, b_rows), b_rows)]
        local.append(pltpu.make_async_copy(src_own, b_own.at[chunk], own_sem.at[spot]))
        pair.append(
            pltpu.make_async_remote_copy(
                src_ref=src_other,
                dst_ref=b_other.at[chunk],
                send_sem=pair_send.at[spot],
                recv_sem=pair_recv.at[spot],
                device_id={"section": other},
                device_id_type=MESH,
            )
        )
    for index in range(a_chunks):
        order = [index] + ([a_chunks + index] if index < down_chunks else [])
        for spot in order:
            pair[spot].start()
            local[spot].start()
    c_local, c_pair = ([], []), ([], [])
    for kind, source in enumerate(mixers):
        part = 0 if kind < 3 else 1
        for owner in range(n_fsdp):
            index = owner * (n_mix + 1) + kind
            place_at = pl.ds(kind * half, half)
            c_local[part].append(
                pltpu.make_async_copy(
                    source.at[half_rows(owner, section)], c_own.at[owner, place_at], c_own_sem.at[index]
                )
            )
            c_pair[part].append(
                pltpu.make_async_remote_copy(
                    src_ref=source.at[half_rows(owner, other)],
                    dst_ref=c_other.at[owner, place_at],
                    send_sem=c_pair_send.at[index],
                    recv_sem=c_pair_recv.at[index],
                    device_id={"section": other},
                    device_id_type=MESH,
                )
            )
    for owner in range(n_fsdp):
        small_at = pl.ds(n_mix * half, c_rows - n_mix * half)
        index = owner * (n_mix + 1) + n_mix
        c_local[1].append(
            pltpu.make_async_copy(small_in.at[section], c_own.at[owner, small_at], c_own_sem.at[index])
        )
        c_pair[1].append(
            pltpu.make_async_remote_copy(
                src_ref=small_in.at[other],
                dst_ref=c_other.at[owner, small_at],
                send_sem=c_pair_send.at[index],
                recv_sem=c_pair_recv.at[index],
                device_id={"section": other},
                device_id_type=MESH,
            )
        )
    for part in range(2):
        for copy in c_pair[part]:
            copy.start()
        for copy in c_local[part]:
            copy.start()
    b_own[b_chunks - 1] = jnp.zeros((b_rows, b_width), BF16)
    _, beside, across, opposite = corners()

    def span(first, last):
        return pl.ds(first * b_rows, (last - first) * b_rows)

    def mixer_spans(part):
        first, last = c_parts[part]
        middle = (first + last) // 2
        return (first, middle, beside, across), (middle, last, across, beside)

    def mixer_copies(part):
        opening, onward = [], []
        for turn, (first, last, near, far) in enumerate(mixer_spans(part)):
            at = span(first, last)
            for slot, owner in ((0, opposite), (1, near)):
                opening.append(
                    to_side(
                        c_own.at[owner, at],
                        c_got.at[slot, at],
                        c_send.at[part, 3 * turn + slot],
                        c_recv.at[part, 3 * turn + slot],
                        near,
                    )
                )
            onward.append(
                to_side(
                    c_own.at[far, at],
                    c_got.at[2, at],
                    c_send.at[part, 3 * turn + 2],
                    c_recv.at[part, 3 * turn + 2],
                    far,
                )
            )
        return opening, onward

    def mixer_out(part):
        for copy in c_local[part]:
            copy.wait()
        for copy in c_pair[part]:
            copy.wait_recv()
        first, last = c_parts[part]
        size = last - first

        def add(index, carry):
            owner = index // size
            at = pl.ds(pl.multiple_of((first + lax.rem(index, size)) * b_rows, b_rows), b_rows)
            c_own[owner, at] = (c_own[owner, at].astype(F32) + c_other[owner, at].astype(F32)).astype(BF16)
            return carry

        lax.fori_loop(0, n_fsdp * size, add, 0)
        opening, _ = mixer_copies(part)
        for index in (0, 2, 1, 3):
            opening[index].start()

    def mixer_on(part):
        opening, onward = mixer_copies(part)
        for turn, (first, last, near, far) in enumerate(mixer_spans(part)):
            opening[2 * turn].wait_recv()

            def add(index, carry, far=far):
                at = pl.ds(pl.multiple_of(index * b_rows, b_rows), b_rows)
                c_own[far, at] = (c_own[far, at].astype(F32) + c_got[0, at].astype(F32)).astype(BF16)
                return carry

            lax.fori_loop(first, last, add, 0)
            onward[turn].start()

    def mixer_in(part):
        opening, onward = mixer_copies(part)
        for turn in range(2):
            opening[2 * turn + 1].wait_recv()
            onward[turn].wait_recv()
        first, last = c_parts[part]

        def add(index, carry):
            at = pl.ds(pl.multiple_of(index * b_rows, b_rows), b_rows)
            total = c_own[group, at].astype(F32) + c_got[1, at].astype(F32) + c_got[2, at].astype(F32)
            b_own[down_chunks + index] = total.astype(BF16)
            return carry

        lax.fori_loop(first, last, add, 0)

    strip = half // n_ctx

    def second_copies(remote):
        for index in range(n_ctx * n_fsdp * 2):
            source, kind = index // 2, index % 2
            turn, owner = source // n_fsdp, source % n_fsdp
            src = second_gu_in.at[turn, owner, kind]
            dst = gu_out.at[
                kind,
                pl.ds(pl.multiple_of(section * half + turn * strip, strip), strip),
                pl.ds(owner * a_width, a_width),
            ]
            if remote:
                pltpu.make_async_remote_copy(
                    src_ref=src,
                    dst_ref=dst,
                    send_sem=second_send.at[0],
                    recv_sem=second_recv,
                    device_id={"section": 1},
                    device_id_type=MESH,
                ).start()
            else:
                pltpu.make_async_copy(src, dst, second_send.at[0]).start()

    def second_start():
        down_at = down_out.at[pl.ds(pl.multiple_of(section * down_half, b_rows), down_half)]

        @pl.when(section == 1)
        def _():
            second_copies(False)
            pltpu.make_async_copy(second_down_in, down_at, second_send.at[1]).start()

        @pl.when(section == 0)
        def _():
            second_copies(True)
            pltpu.make_async_remote_copy(
                src_ref=second_down_in,
                dst_ref=down_at,
                send_sem=second_send.at[1],
                recv_sem=down_recv,
                device_id={"section": 1},
                device_id_type=MESH,
            ).start()

    def a_target(k):
        kind = k // per_kind
        rest = lax.rem(k, per_kind)
        owner = rest // subs
        sub = lax.rem(rest, subs)
        spot = gu_out.at[
            kind,
            pl.ds(pl.multiple_of(section * half + sub * a_rows, a_rows), a_rows),
            pl.ds(pl.multiple_of(group * a_width, 128), a_width),
        ]
        return kind, owner, spot

    def hand_out(k):
        kind, owner, spot = a_target(k)
        is_mine = (section == 0) & (group == owner)

        @pl.when(is_mine)
        def _():
            pltpu.make_async_copy(a_done.at[k], spot, a_out_send.at[k]).start()

        @pl.when(jnp.logical_not(is_mine))
        def _():
            pltpu.make_async_remote_copy(
                src_ref=a_done.at[k],
                dst_ref=spot,
                send_sem=a_out_send.at[k],
                recv_sem=gu_recv.at[kind, section * n_fsdp + group],
                device_id={"section": 0, "fsdp": owner},
                device_id_type=MESH,
            ).start()

        @pl.when(k < down_chunks)
        def _():
            at = down_out.at[pl.ds(pl.multiple_of(section * down_half + k * b_rows, b_rows), b_rows)]

            @pl.when(section == 0)
            def _():
                pltpu.make_async_copy(b_done.at[k], at, b_out_send.at[k]).start()

            @pl.when(section == 1)
            def _():
                pltpu.make_async_remote_copy(
                    src_ref=b_done.at[k],
                    dst_ref=at,
                    send_sem=b_out_send.at[k],
                    recv_sem=down_recv,
                    device_id={"section": 0},
                    device_id_type=MESH,
                ).start()

        @pl.when(k >= down_chunks)
        def _():
            at = rest_out.at[section, pl.ds(pl.multiple_of((k - down_chunks) * b_rows, b_rows), b_rows)]
            pltpu.make_async_copy(b_done.at[k], at, b_keep_sem.at[k]).start()
            pltpu.make_async_remote_copy(
                src_ref=b_done.at[k],
                dst_ref=at,
                send_sem=b_out_send.at[k],
                recv_sem=rest_recv,
                device_id={"section": other},
                device_id_type=MESH,
            ).start()

    def up_copies(k, target):
        return (
            pltpu.make_async_remote_copy(
                src_ref=a_sum.at[k],
                dst_ref=a_sum.at[k],
                send_sem=a_up_send.at[k],
                recv_sem=a_up_recv.at[k],
                device_id={"ctx": target},
                device_id_type=MESH,
            ),
            pltpu.make_async_remote_copy(
                src_ref=b_sum.at[k],
                dst_ref=b_sum.at[k],
                send_sem=b_up_send.at[k],
                recv_sem=b_up_recv.at[k],
                device_id={"ctx": target},
                device_id_type=MESH,
            ),
        )

    def back_copies(k, target):
        return (
            pltpu.make_async_remote_copy(
                src_ref=a_done.at[k],
                dst_ref=a_done.at[k],
                send_sem=a_back_send.at[k],
                recv_sem=a_back_recv.at[k],
                device_id={"ctx": target},
                device_id_type=MESH,
            ),
            pltpu.make_async_remote_copy(
                src_ref=b_done.at[k],
                dst_ref=b_done.at[k],
                send_sem=b_back_send.at[k],
                recv_sem=b_back_recv.at[k],
                device_id={"ctx": target},
                device_id_type=MESH,
            ),
        )

    def own_term(k):
        pltpu.make_async_copy(a_own.at[k], a_other.at[k], own_sem.at[k]).wait()
        pltpu.make_async_copy(a_own.at[k], a_other.at[k], pair_recv.at[k]).wait()

        @pl.when(k < down_chunks)
        def _():
            pltpu.make_async_copy(b_own.at[k], b_sum.at[k], own_sem.at[a_chunks + k]).wait()
            pltpu.make_async_copy(b_own.at[k], b_sum.at[k], pair_recv.at[a_chunks + k]).wait()
            b_own[k] = (b_own[k].astype(F32) + b_other[k].astype(F32)).astype(BF16)

        return a_own[k].astype(F32) + a_other[k].astype(F32)

    lanes = []
    for way in range(2):
        rank = place if way == 0 else n_ctx - 1 - place
        ahead = place + 1 if way == 0 else place - 1
        behind = place - 1 if way == 0 else place + 1
        lanes.append((way, rank, ahead, behind))

    def tick_step(tick, carry):
        events = (
            (1, mixer_out, 0),
            (2, mixer_out, 1),
            (3, mixer_on, 0),
            (down_chunks // 2 - 1, mixer_on, 1),
            (down_chunks // 2, mixer_in, 0),
            ((down_chunks + cut) // 2, mixer_in, 1),
        )
        for moment, action, part in events:

            @pl.when(tick == moment)
            def _(action=action, part=part):
                action(part)

        @pl.when(tick == 4)
        def _():
            second_start()

        for way, rank, ahead, behind in lanes:
            step = tick - rank
            k = 2 * jnp.clip(step, 0, ticks - 1) + way

            @pl.when((step >= 0) & (step < ticks))
            def _(k=k, rank=rank, ahead=ahead, behind=behind):
                term = own_term(k)

                @pl.when(rank == 0)
                def _():
                    a_sum[k] = term.astype(BF16)
                    b_sum[k] = b_own[k]

                @pl.when(rank > 0)
                def _():
                    for copy in up_copies(k, behind):
                        copy.wait_recv()

                @pl.when((rank > 0) & (rank < n_ctx - 1))
                def _():
                    a_sum[k] = (term + a_sum[k].astype(F32)).astype(BF16)
                    b_sum[k] = (b_own[k].astype(F32) + b_sum[k].astype(F32)).astype(BF16)

                @pl.when(rank < n_ctx - 1)
                def _():
                    for copy in up_copies(k, ahead):
                        copy.start()

                @pl.when(rank == n_ctx - 1)
                def _():
                    a_done[k] = (term + a_sum[k].astype(F32)).astype(BF16)
                    b_done[k] = (b_own[k].astype(F32) + b_sum[k].astype(F32)).astype(BF16)
                    for copy in back_copies(k, behind):
                        copy.start()
                    hand_out(k)

            late = tick - (tail - rank)
            j = 2 * jnp.clip(late, 0, ticks - 1) + way

            @pl.when((late >= 0) & (late < ticks) & (rank < n_ctx - 1))
            def _(j=j, rank=rank, ahead=ahead, behind=behind):
                for copy in back_copies(j, ahead):
                    copy.wait_recv()

                @pl.when(rank > 0)
                def _():
                    for copy in back_copies(j, behind):
                        copy.start()

                hand_out(j)

        return carry

    lax.fori_loop(0, ticks + tail, tick_step, 0)

    for copy in pair:
        copy.wait_send()
    for part in range(2):
        for copy in c_pair[part]:
            copy.wait_send()
        opening, onward = mixer_copies(part)
        for copy in opening + onward:
            copy.wait_send()

    def settle(step, carry):
        for way, rank, ahead, behind in lanes:
            k = 2 * step + way

            @pl.when(rank < n_ctx - 1)
            def _(k=k, ahead=ahead):
                for copy in up_copies(k, ahead):
                    copy.wait_send()

            @pl.when(rank > 0)
            def _(k=k, behind=behind):
                for copy in back_copies(k, behind):
                    copy.wait_send()

            _, _, spot = a_target(k)
            pltpu.make_async_copy(a_done.at[k], spot, a_out_send.at[k]).wait()
            pltpu.make_async_copy(b_done.at[k], b_own.at[k], b_out_send.at[k]).wait()

            @pl.when(k >= down_chunks)
            def _(k=k):
                pltpu.make_async_copy(b_done.at[k], b_own.at[k], b_keep_sem.at[k]).wait()

        return carry

    lax.fori_loop(0, ticks, settle, 0)
    pltpu.make_async_copy(second_gu_in, second_gu_in, second_send.at[0]).wait()
    pltpu.make_async_copy(second_down_in, second_down_in, second_send.at[1]).wait()

    @pl.when(section == 0)
    def _():
        for kind in range(2):
            for source in range(2 * n_fsdp):

                @pl.when(group != source)
                def _(kind=kind, source=source):
                    region = gu_out.at[
                        kind,
                        pl.ds((source // n_fsdp) * half, half),
                        pl.ds((source % n_fsdp) * a_width, a_width),
                    ]
                    pltpu.make_async_copy(region, region, gu_recv.at[kind, source]).wait()

    @pl.when(section == 1)
    def _():
        pltpu.make_async_copy(second_gu_in, second_gu_in, second_recv).wait()

    region = down_out.at[pl.ds(pl.multiple_of(other * down_half, b_rows), down_half)]
    pltpu.make_async_copy(region, region, down_recv).wait()
    region = rest_out.at[other]
    pltpu.make_async_copy(region, region, rest_recv).wait()


def summed_gradients(first, mixers, small, second_gu, second_down):
    n_ctx, n_fsdp = lax.axis_size("ctx"), lax.axis_size("fsdp")
    gate, up, down = first
    half = gate.shape[0] // n_fsdp // 2
    a_rows, b_rows = half // 4, half * 3 // 8
    a_chunks = 2 * n_fsdp * 4
    a_width, b_width = gate.shape[1], down.shape[1]
    c_rows = len(mixers) * half + small.shape[1]
    down_chunks = down.shape[0] // 2 // b_rows
    b_chunks = down_chunks + c_rows // b_rows + 1
    assert a_chunks == b_chunks and c_rows % b_rows == 0
    rest = b_chunks - down_chunks
    dma = pltpu.SemaphoreType.DMA
    loads = a_chunks + down_chunks
    pieces = n_fsdp * (len(mixers) + 1)
    return pl.pallas_call(
        functools.partial(tail_kernel, (n_ctx, n_fsdp)),
        out_shape=(
            jax.ShapeDtypeStruct((2, 2 * half, n_fsdp * a_width), BF16),
            jax.ShapeDtypeStruct(down.shape, BF16),
            jax.ShapeDtypeStruct((2, rest * b_rows, b_width), BF16),
        ),
        in_specs=[pl.BlockSpec(memory_space=pl.ANY)] * (6 + len(mixers)),
        out_specs=[pl.BlockSpec(memory_space=pl.ANY)] * 3,
        scratch_shapes=[
            pltpu.VMEM((a_chunks, a_rows, a_width), BF16),
            pltpu.VMEM((a_chunks, a_rows, a_width), BF16),
            pltpu.VMEM((a_chunks, a_rows, a_width), BF16),
            pltpu.VMEM((a_chunks, a_rows, a_width), BF16),
            pltpu.VMEM((b_chunks, b_rows, b_width), BF16),
            pltpu.VMEM((down_chunks, b_rows, b_width), BF16),
            pltpu.VMEM((b_chunks, b_rows, b_width), BF16),
            pltpu.VMEM((b_chunks, b_rows, b_width), BF16),
            pltpu.VMEM((n_fsdp, c_rows, b_width), BF16),
            pltpu.VMEM((n_fsdp, c_rows, b_width), BF16),
            pltpu.VMEM((n_fsdp - 1, c_rows, b_width), BF16),
            dma((loads,)),
            dma((loads,)),
            dma((loads,)),
            dma((pieces,)),
            dma((pieces,)),
            dma((pieces,)),
            dma((2, 6)),
            dma((2, 6)),
            dma((a_chunks,)),
            dma((a_chunks,)),
            dma((a_chunks,)),
            dma((a_chunks,)),
            dma((a_chunks,)),
            dma((b_chunks,)),
            dma((b_chunks,)),
            dma((b_chunks,)),
            dma((b_chunks,)),
            dma((b_chunks,)),
            dma((b_chunks,)),
            dma((2, 2 * n_fsdp)),
            dma,
            dma,
            dma((2,)),
            dma,
        ],
        compiler_params=pltpu.CompilerParams(
            collective_id=6, has_side_effects=True, vmem_limit_bytes=56 << 20
        ),
        cost_estimate=busy(160),
    )(gate, up, down, *mixers, small, second_gu, second_down)


def mixer_weights_kernel(count, first_in, second_in, first_out, second_out, send_sem, recv_sem, pair_send, pair_recv, own_sem):
    section = lax.axis_index("section")
    me = lax.axis_index("fsdp")
    other = 1 - section
    beside = me + 1 - 2 * lax.rem(me, 2)
    across = lax.rem(me + 2, count)
    opposite = lax.rem(beside + 2, count)
    rows = first_in.shape[0]
    half = rows // 2
    quarter = half // 2
    barrier = pltpu.get_barrier_semaphore()
    for target in ({"fsdp": beside}, {"fsdp": across}, {"section": other}):
        pl.semaphore_signal(barrier, inc=1, device_id=target, device_id_type=MESH)
    pl.semaphore_wait(barrier, 3)
    arrays = ((first_in, first_out), (second_in, second_out))

    def at_rows(owner, extra, size):
        return pl.ds(pl.multiple_of(owner * rows + extra, quarter), size)

    def remote(slot, sems, src, dst, target):
        return pltpu.make_async_remote_copy(
            src_ref=src,
            dst_ref=dst,
            send_sem=sems[0].at[slot],
            recv_sem=sems[1].at[slot],
            device_id=target,
            device_id_type=MESH,
        )

    hop, pair = (send_sem, recv_sem), (pair_send, pair_recv)
    waiting = []
    direct = []
    for index, (source, out) in enumerate(arrays):
        mine = source.at[pl.ds(pl.multiple_of(section * half, half), half)]
        spot = out.at[at_rows(me, section * half, half)]
        copies = [
            remote(index * 4, hop, mine, spot, {"fsdp": beside}),
            remote(index * 4 + 1, hop, mine, spot, {"fsdp": across}),
        ]
        for copy in copies:
            copy.start()
        direct.append(copies)
    own = [
        pltpu.make_async_copy(source, out.at[at_rows(me, 0, rows)], own_sem.at[index])
        for index, (source, out) in enumerate(arrays)
    ]
    for copy in own:
        copy.start()

    def arrived(owner, size, extra):
        return lambda out: out.at[at_rows(owner, section * half + extra, size)]

    onward = []
    for index, (source, out) in enumerate(arrays):
        direct[index][0].wait_recv()
        part = arrived(beside, quarter, 0)(out)
        onward.append(remote(index * 4 + 2, hop, part, part, {"fsdp": across}))
        onward[-1].start()
        whole = arrived(beside, half, 0)(out)
        waiting.append(remote(index * 4, pair, whole, whole, {"section": other}))
        waiting[-1].start()
        direct[index][1].wait_recv()
        part = arrived(across, quarter, quarter)(out)
        onward.append(remote(index * 4 + 3, hop, part, part, {"fsdp": beside}))
        onward[-1].start()
        whole = arrived(across, half, 0)(out)
        waiting.append(remote(index * 4 + 1, pair, whole, whole, {"section": other}))
        waiting[-1].start()
    for index, (source, out) in enumerate(arrays):
        for turn in range(2):
            onward[2 * index + turn].wait_recv()
            part = arrived(opposite, quarter, turn * quarter)(out)
            waiting.append(remote(index * 4 + 2 + turn, pair, part, part, {"section": other}))
            waiting[-1].start()
    for copy in own:
        copy.wait()
    for copies in direct:
        for copy in copies:
            copy.wait_send()
    for copy in onward:
        copy.wait_send()
    for copy in waiting:
        copy.wait()


def mixer_weights(first, second, collective_id):
    count = lax.axis_size("fsdp")
    dma = pltpu.SemaphoreType.DMA
    return pl.pallas_call(
        functools.partial(mixer_weights_kernel, count),
        out_shape=tuple(
            jax.ShapeDtypeStruct((count * w.shape[0], w.shape[1]), w.dtype) for w in (first, second)
        ),
        in_specs=[pl.BlockSpec(memory_space=pl.ANY)] * 2,
        out_specs=[pl.BlockSpec(memory_space=pl.ANY)] * 2,
        scratch_shapes=[dma((8,)), dma((8,)), dma((8,)), dma((8,)), dma((2,))],
        compiler_params=pltpu.CompilerParams(
            collective_id=collective_id, has_side_effects=True, vmem_limit_bytes=56 << 20
        ),
        cost_estimate=busy(45),
    )(first, second)


class Columns:
    def __init__(self, holder, sources, targets, send_sem, recv_sem, pair_send, pair_recv, own_sem):
        self.count = 4
        self.holder = holder
        self.section = lax.axis_index("section")
        self.me = lax.axis_index("fsdp")
        self.sources, self.targets = sources, targets
        self.sems = send_sem, recv_sem, pair_send, pair_recv, own_sem
        self.rows = sources[0].shape[0]
        self.wide = targets[0].shape[1]
        self.steps = [(step, kind) for step in range(1, self.count) for kind in range(2)]

    def at_rows(self, out, owner):
        return out.at[pl.ds(pl.multiple_of(owner * self.rows, self.rows), self.rows)]

    def at_columns(self, source, owner):
        return source.at[:, pl.ds(pl.multiple_of(owner * self.wide, 128), self.wide)]

    def crossing(self, step, kind):
        target = lax.rem(self.me + step, self.count)
        return to_side(
            self.at_columns(self.sources[kind], target),
            self.at_rows(self.targets[kind], self.me),
            self.sems[0].at[kind, step],
            self.sems[1].at[kind, step],
            target,
        )

    def handed(self, step, kind):
        if kind == 2:
            src, dst = self.sources[2], self.targets[2]
        else:
            origin = lax.rem(self.me + self.count - step, self.count)
            dst = self.at_rows(self.targets[kind], origin)
            src = self.at_columns(self.sources[kind], self.me) if step == 0 else dst
        return pltpu.make_async_remote_copy(
            src_ref=src,
            dst_ref=dst,
            send_sem=self.sems[2].at[kind, step],
            recv_sem=self.sems[3].at[kind, step],
            device_id={"section": 1 - self.section},
            device_id_type=MESH,
        )

    def kept(self, kind):
        if kind == 2:
            return pltpu.make_async_copy(self.sources[2], self.targets[2], self.sems[4].at[2])
        return pltpu.make_async_copy(
            self.at_columns(self.sources[kind], self.me),
            self.at_rows(self.targets[kind], self.me),
            self.sems[4].at[kind],
        )

    def start(self):
        @pl.when(self.section == self.holder)
        def _():
            for step, kind in self.steps:
                self.crossing(step, kind).start()
            for kind in range(3):
                self.handed(0, kind).start()
            for kind in range(3):
                self.kept(kind).start()

    def relay(self):
        @pl.when(self.section == self.holder)
        def _():
            for step, kind in self.steps:
                self.crossing(step, kind).wait_recv()
                self.handed(step, kind).start()

    def finish(self):
        every = [(0, kind) for kind in range(3)] + self.steps

        @pl.when(self.section == self.holder)
        def _():
            for kind in range(3):
                self.kept(kind).wait()
            for step, kind in self.steps:
                self.crossing(step, kind).wait_send()
            for step, kind in every:
                self.handed(step, kind).wait_send()

        @pl.when(self.section != self.holder)
        def _():
            for step, kind in every:
                self.handed(step, kind).wait_recv()


def column_weights_kernel(holder, *refs):
    section = lax.axis_index("section")
    _, beside, across, opposite = corners()
    barrier = pltpu.get_barrier_semaphore()
    for target in ({"fsdp": beside}, {"fsdp": across}, {"fsdp": opposite}, {"section": 1 - section}):
        pl.semaphore_signal(barrier, inc=1, device_id=target, device_id_type=MESH)
    pl.semaphore_wait(barrier, 4)
    columns = Columns(holder, refs[:3], refs[3:6], *refs[6:])
    columns.start()
    columns.relay()
    columns.finish()


def column_weights(gate, up, down, holder, collective_id):
    count = lax.axis_size("fsdp")
    assert count == 4
    dma = pltpu.SemaphoreType.DMA
    column = jax.ShapeDtypeStruct((count * gate.shape[0], gate.shape[1] // count), gate.dtype)
    return pl.pallas_call(
        functools.partial(column_weights_kernel, holder),
        out_shape=(column, column, jax.ShapeDtypeStruct(down.shape, down.dtype)),
        in_specs=[pl.BlockSpec(memory_space=pl.ANY)] * 3,
        out_specs=[pl.BlockSpec(memory_space=pl.ANY)] * 3,
        scratch_shapes=[dma((2, count)), dma((2, count)), dma((3, count)), dma((3, count)), dma((3,))],
        compiler_params=pltpu.CompilerParams(
            collective_id=collective_id, has_side_effects=True, vmem_limit_bytes=56 << 20
        ),
        cost_estimate=busy(40),
    )(gate, up, down)


class Chain:
    def __init__(self, count):
        self.count = count
        self.place = lax.axis_index("ctx")
        self.has_next = self.place < count - 1
        self.has_last = self.place > 0


def greet_mixed(chain, targets):
    barrier = pltpu.get_barrier_semaphore()
    for target in targets:
        pl.semaphore_signal(barrier, inc=1, device_id=target, device_id_type=MESH)

    @pl.when(chain.has_last)
    def _():
        pl.semaphore_signal(barrier, inc=1, device_id={"ctx": chain.place - 1}, device_id_type=MESH)

    @pl.when(chain.has_next)
    def _():
        pl.semaphore_signal(barrier, inc=1, device_id={"ctx": chain.place + 1}, device_id_type=MESH)

    inner = chain.has_last & chain.has_next

    @pl.when(inner)
    def _():
        pl.semaphore_wait(barrier, len(targets) + 2)

    @pl.when(jnp.logical_not(inner))
    def _():
        pl.semaphore_wait(barrier, len(targets) + 1)


def along(src, dst, send_sem, recv_sem, place):
    return pltpu.make_async_remote_copy(
        src_ref=src,
        dst_ref=dst,
        send_sem=send_sem,
        recv_sem=recv_sem,
        device_id={"ctx": place},
        device_id_type=MESH,
    )


def spread_heads(source, spread):
    rows = source.shape[0]
    low = lax.broadcasted_iota(jnp.int32, (rows, 128), 1) < 64
    for pair in range(source.shape[1] // 256):
        first = source[:, pair * 256 : pair * 256 + 128].astype(F32)
        second = source[:, pair * 256 + 128 : pair * 256 + 256].astype(F32)
        spread[4 * pair] = jnp.where(low, first, 0.0).astype(BF16)
        spread[4 * pair + 1] = jnp.where(low, pltpu.roll(first, 64, 1), 0.0).astype(BF16)
        spread[4 * pair + 2] = jnp.where(low, 0.0, pltpu.roll(second, 64, 1)).astype(BF16)
        spread[4 * pair + 3] = jnp.where(low, 0.0, second).astype(BF16)


def join_heads(spread, target):
    rows = target.shape[0]
    low = lax.broadcasted_iota(jnp.int32, (rows, 128), 1) < 64
    for pair in range(target.shape[1] // 256):
        parts = [spread(4 * pair + i).T for i in range(4)]
        target[:, pair * 256 : pair * 256 + 128] = jnp.where(low, parts[0], pltpu.roll(parts[1], 64, 1))
        target[:, pair * 256 + 128 : pair * 256 + 256] = jnp.where(low, pltpu.roll(parts[2], 64, 1), parts[3])


def mask_block(bias, length, place, block):
    rows = bias.shape[0]
    key_at = block * rows + lax.broadcasted_iota(jnp.int32, bias.shape, 0)
    query_at = place * rows + lax.broadcasted_iota(jnp.int32, bias.shape, 1)
    bias[...] = jnp.where((key_at <= query_at) & (key_at < length), 0.0, NEGATIVE)


def dot_right(left, right):
    return lax.dot_general(left, right, (((1,), (1,)), ((), ())), preferred_element_type=F32)


def dot_plain(left, right):
    return jnp.dot(left, right, preferred_element_type=F32)


def attend_kernel(
    n_ctx,
    length_ref,
    query,
    kv,
    d_block,
    gate_in,
    up_in,
    down_in,
    attended,
    log_total,
    kv_all,
    d_all,
    gate_out,
    up_out,
    down_out,
    spread,
    bias,
    peak,
    total,
    out_t,
    kv_send,
    kv_recv,
    d_send,
    d_recv,
    d_own,
    send_sem,
    recv_sem,
    pair_send,
    pair_recv,
    own_sem,
):
    chain = Chain(n_ctx)
    place = chain.place
    section = lax.axis_index("section")
    me, beside, across, opposite = corners()
    greet_mixed(
        chain,
        [{"fsdp": beside}, {"fsdp": across}, {"fsdp": opposite}, {"section": 1 - section}],
    )
    rows = query.shape[0]
    half_width = kv.shape[1] // 2

    def block_rows(block):
        return pl.ds(pl.multiple_of(block * rows, rows), rows)

    def upward(step, src):
        return along(
            src,
            kv_all.at[block_rows(place - step)],
            kv_send.at[step],
            kv_recv.at[step + 1],
            place + 1,
        )

    def arriving(step):
        at = kv_all.at[block_rows(place - step)]
        return along(at, at, kv_send.at[step], kv_recv.at[step], place)

    @pl.when(chain.has_next)
    def _():
        upward(0, kv).start()

    gather = SideGather(d_block, d_all, d_send, d_recv, d_own)
    gather.start()
    columns = Columns(
        1, (gate_in, up_in, down_in), (gate_out, up_out, down_out), send_sem, recv_sem, pair_send, pair_recv, own_sem
    )
    columns.start()
    kv_all[block_rows(place)] = kv[...]
    spread_heads(query, spread)
    peak[...] = jnp.full(peak.shape, NEGATIVE, F32)
    total[...] = jnp.zeros(total.shape, F32)
    out_t[...] = jnp.zeros(out_t.shape, F32)
    length = length_ref[0]
    scale = 64 ** (-0.5)

    def attend_block(block):
        mask_block(bias, length, place, block)
        for pair in range(half_width // 128):
            key = kv_all[block_rows(block), pair * 128 : pair * 128 + 128]
            value_t = kv_all[block_rows(block), half_width + pair * 128 : half_width + pair * 128 + 128].T
            for index in range(4):
                head = 4 * pair + index
                scores = dot_right(key, spread[head]) * scale + bias[...]
                before = peak[head]
                now = jnp.maximum(before, jnp.max(scores, axis=0, keepdims=True))
                weights = jnp.exp(scores - now)
                fade = jnp.exp(before - now)
                peak[head] = now
                total[head] = total[head] * fade + jnp.sum(weights, axis=0, keepdims=True)
                out_t[head] = out_t[head] * fade + dot_plain(value_t, weights.astype(BF16))

    attend_block(place)
    gather.relay()

    def step_on(step, carry):
        @pl.when(step <= place)
        def _():
            arriving(step).wait_recv()

            @pl.when(chain.has_next)
            def _():
                upward(step, kv_all.at[block_rows(place - step)]).start()

            attend_block(place - step)

        return carry

    lax.fori_loop(1, n_ctx, step_on, 0)
    join_heads(lambda head: out_t[head] / total[head], attended)
    for head in range(spread.shape[0]):
        log_total[head] = peak[head] + jnp.log(total[head])
    columns.relay()
    gather.finish()
    columns.finish()

    def settle(step, carry):
        @pl.when((step <= place) & chain.has_next)
        def _():
            upward(step, kv_all.at[block_rows(place - step)]).wait_send()

        return carry

    lax.fori_loop(0, n_ctx, settle, 0)


def attend(length, query, kv, d_block, gate, up, down, collective_id):
    n_ctx, count = lax.axis_size("ctx"), lax.axis_size("fsdp")
    rows, width = query.shape
    heads = width // 64
    dma = pltpu.SemaphoreType.DMA
    vmem = pl.BlockSpec(memory_space=pltpu.VMEM)
    hbm = pl.BlockSpec(memory_space=pl.ANY)
    column = jax.ShapeDtypeStruct((count * gate.shape[0], gate.shape[1] // count), gate.dtype)
    return pl.pallas_call(
        functools.partial(attend_kernel, n_ctx),
        out_shape=(
            jax.ShapeDtypeStruct((rows, width), F32),
            jax.ShapeDtypeStruct((heads, 1, rows), F32),
            jax.ShapeDtypeStruct((n_ctx * rows, kv.shape[1]), BF16),
            jax.ShapeDtypeStruct((count * rows, d_block.shape[1]), BF16),
            column,
            column,
            jax.ShapeDtypeStruct(down.shape, down.dtype),
        ),
        in_specs=[pl.BlockSpec(memory_space=pltpu.SMEM), vmem, vmem, vmem, hbm, hbm, hbm],
        out_specs=[vmem, vmem, vmem, vmem, hbm, hbm, hbm],
        scratch_shapes=[
            pltpu.VMEM((heads, rows, 128), BF16),
            pltpu.VMEM((rows, rows), F32),
            pltpu.VMEM((heads, 1, rows), F32),
            pltpu.VMEM((heads, 1, rows), F32),
            pltpu.VMEM((heads, 128, rows), F32),
            dma((n_ctx + 1,)),
            dma((n_ctx + 1,)),
            dma((4,)),
            dma((4,)),
            dma,
            dma((2, count)),
            dma((2, count)),
            dma((3, count)),
            dma((3, count)),
            dma((3,)),
        ],
        compiler_params=pltpu.CompilerParams(
            collective_id=collective_id, has_side_effects=True, vmem_limit_bytes=56 << 20
        ),
        cost_estimate=busy(50),
    )(length, query, kv, d_block, gate, up, down)


def attend_back_kernel(
    n_ctx,
    length_ref,
    query,
    kv_all,
    d_out,
    log_total,
    delta,
    blocks,
    d_query,
    d_kv,
    reduced_out,
    spread,
    d_spread,
    bias,
    d_query_t,
    term,
    leaving,
    coming,
    kv_send,
    kv_recv,
    beside_got,
    across_got,
    passed,
    passed_got,
    send_sem,
    recv_sem,
):
    chain = Chain(n_ctx)
    place = chain.place
    _, beside, across, _ = corners()
    greet_mixed(chain, [{"fsdp": beside}, {"fsdp": across}])
    rows = query.shape[0]
    half_width = kv_all.shape[1] // 2
    reduction = SideReduce(blocks, reduced_out, beside_got, across_got, passed, passed_got, send_sem, recv_sem)
    reduction.start()
    spread_heads(query, spread)
    spread_heads(d_out, d_spread)
    d_query_t[...] = jnp.zeros(d_query_t.shape, F32)
    length = length_ref[0]
    scale = 64 ** (-0.5)

    def downward(block):
        return along(leaving.at[block], coming.at[block], kv_send.at[block], kv_recv.at[block], place - 1)

    def step_on(block, carry):
        @pl.when(block <= place)
        def _():
            mask_block(bias, length, place, block)
            at = pl.ds(pl.multiple_of(block * rows, rows), rows)
            for pair in range(half_width // 128):
                lanes = slice(pair * 128, pair * 128 + 128)
                more = slice(half_width + pair * 128, half_width + pair * 128 + 128)
                key = kv_all[at, lanes]
                value = kv_all[at, more]
                key_t = key.T
                d_key = jnp.zeros((rows, 128), F32)
                d_value = jnp.zeros((rows, 128), F32)
                for index in range(4):
                    head = 4 * pair + index
                    scores = dot_right(key, spread[head]) * scale + bias[...]
                    prob = jnp.exp(scores - log_total[head])
                    d_prob = dot_right(value, d_spread[head])
                    d_scores = (prob * (d_prob - delta[head])).astype(BF16)
                    d_value = d_value + dot_plain(prob.astype(BF16), d_spread[head])
                    d_key = d_key + dot_plain(d_scores, spread[head])
                    d_query_t[head] = d_query_t[head] + dot_plain(key_t, d_scores)
                term[:, lanes] = d_key * scale
                term[:, more] = d_value

            @pl.when(chain.has_next)
            def _():
                along(
                    leaving.at[block], coming.at[block], kv_send.at[block], kv_recv.at[block], place
                ).wait_recv()
                term[...] = term[...] + coming[block].astype(F32)

            @pl.when(block < place)
            def _():
                leaving[block] = term[...].astype(BF16)
                downward(block).start()

            @pl.when(block == place)
            def _():
                d_kv[...] = term[...]

        @pl.when(block == 0)
        def _():
            reduction.relay()

        return carry

    lax.fori_loop(0, n_ctx, step_on, 0)
    join_heads(lambda head: d_query_t[head] * scale, d_query)
    reduction.finish()

    def settle(block, carry):
        @pl.when(block < place)
        def _():
            downward(block).wait_send()

        return carry

    lax.fori_loop(0, n_ctx, settle, 0)


def attend_back(length, query, kv_all, d_out, log_total, delta, blocks, collective_id):
    n_ctx = lax.axis_size("ctx")
    rows, width = query.shape
    heads = width // 64
    dma = pltpu.SemaphoreType.DMA
    vmem = pl.BlockSpec(memory_space=pltpu.VMEM)
    wide = jax.ShapeDtypeStruct((rows, width), F32)
    pair = pltpu.VMEM((2, rows // 2, blocks.shape[1]), BF16)
    return pl.pallas_call(
        functools.partial(attend_back_kernel, n_ctx),
        out_shape=(wide, jax.ShapeDtypeStruct((rows, kv_all.shape[1]), F32), wide),
        in_specs=[pl.BlockSpec(memory_space=pltpu.SMEM)] + [vmem] * 6,
        out_specs=[vmem] * 3,
        scratch_shapes=[
            pltpu.VMEM((heads, rows, 128), BF16),
            pltpu.VMEM((heads, rows, 128), BF16),
            pltpu.VMEM((rows, rows), F32),
            pltpu.VMEM((heads, 128, rows), F32),
            pltpu.VMEM((rows, kv_all.shape[1]), F32),
            pltpu.VMEM((n_ctx, rows, kv_all.shape[1]), BF16),
            pltpu.VMEM((n_ctx, rows, kv_all.shape[1]), BF16),
            dma((n_ctx,)),
            dma((n_ctx,)),
            pair,
            pair,
            pair,
            pair,
            dma((6,)),
            dma((6,)),
        ],
        compiler_params=pltpu.CompilerParams(
            collective_id=collective_id, has_side_effects=True, vmem_limit_bytes=56 << 20
        ),
        cost_estimate=busy(50),
    )(length, query, kv_all, d_out, log_total, delta, blocks)


def ffn_forward(residual, gain, w_gate, w_up, w_down):
    normed, inv_rms = norm_rows(residual)
    act = gathered((normed * gain).astype(BF16), 0)
    gate_pre = matmul(act, w_gate)
    up_pre = matmul(act, w_up)
    hidden = (jax.nn.silu(gate_pre) * up_pre).astype(BF16)
    return matmul(hidden, w_down).astype(BF16), (normed, inv_rms, act, gate_pre, up_pre, hidden)


def ffn_backward(d_all, kept, gain, w_gate, w_up, w_down):
    normed, inv_rms, act, gate_pre, up_pre, hidden = kept
    d_hidden = matmul_right(d_all, w_down)
    sigmoid = jax.nn.sigmoid(gate_pre)
    d_up = (d_hidden * gate_pre * sigmoid).astype(BF16)
    d_gate = (d_hidden * up_pre * sigmoid * (1.0 + gate_pre * (1.0 - sigmoid))).astype(BF16)
    d_act = reduced(matmul_right(d_gate, w_gate) + matmul_right(d_up, w_up), 1)
    grad_gate = matmul_left(act, d_gate).astype(BF16)
    grad_up = matmul_left(act, d_up).astype(BF16)
    grad_down = matmul_left(hidden, d_all).astype(BF16)
    grad_gain = jnp.sum(d_act * normed, axis=0)
    return norm_back(d_act * gain, normed, inv_rms), grad_gain, (grad_gate, grad_up, grad_down)


def shards(
    inputs,
    cotangent,
    lengths,
    norm_gains,
    conv_in,
    conv_kernel,
    conv_out,
    attn_q,
    attn_k,
    attn_v,
    attn_out,
    head_gains,
    ffn_gate,
    ffn_up,
    ffn_down,
):
    micro, rows, width = inputs.shape
    section = lax.axis_index("section")
    group = lax.axis_index("fsdp")
    fsdp = lax.axis_size("fsdp")
    assert micro == lax.axis_size("section")
    head = head_gains.shape[1]
    q_width, kv_width = attn_q.shape[1], attn_k.shape[1]
    q_heads, kv_heads = q_width // head, kv_width // head
    positions = lax.axis_index("ctx") * rows + jnp.arange(rows)
    length = lax.dynamic_index_in_dim(lengths, group * micro + section, keepdims=False)
    mask = (positions < length).astype(F32)[:, None]

    def whole_rows(weight):
        half = weight.shape[0] // micro
        mine = lax.dynamic_slice_in_dim(weight, section * half, half, 0)
        return lax.all_gather(mine, ("fsdp", "section"), axis=0, tiled=True)

    part = ffn_gate.shape[1]
    in_full, out_full = mixer_weights(conv_in, conv_out, 2)
    gate1, up1, down1 = column_weights(ffn_gate[0], ffn_up[0], ffn_down[0], 0, 7)
    query_full, key_full, value_full, proj_full = (
        whole_rows(attn_q),
        whole_rows(attn_k),
        whole_rows(attn_v),
        whole_rows(attn_out),
    )

    x = lax.dynamic_index_in_dim(inputs, section, keepdims=False).astype(F32)
    normed0, inv0 = norm_rows(x)
    act1 = (normed0 * norm_gains[0]).astype(BF16)
    projected = matmul(act1, in_full)
    b_gate, c_gate, x_value = (
        projected[:, :width],
        projected[:, width : 2 * width],
        projected[:, 2 * width :],
    )
    b_product = (b_gate * x_value).astype(BF16)
    rim = passed_along(b_product[-2:], "ctx", 1)
    extended = jnp.concatenate([rim, b_product], axis=0).astype(F32)
    convolved = (
        conv_kernel[0] * extended[:-2]
        + conv_kernel[1] * extended[1:-1]
        + conv_kernel[2] * extended[2:]
    )
    z_low = (c_gate * convolved).astype(BF16)
    mixed = matmul(z_low, out_full)
    res1 = x + mixed
    terms1, kept1 = ffn_forward(res1, norm_gains[1], gate1, up1, down1)
    ffn1 = reduced(terms1, 1)
    h_low = (res1 + ffn1).astype(BF16)

    h = h_low.astype(F32)
    normed2, inv2 = norm_rows(h)
    act2 = (normed2 * norm_gains[2]).astype(BF16)
    q_normed, q_inv = norm_heads(matmul(act2, query_full), head)
    k_normed, k_inv = norm_heads(matmul(act2, key_full), head)
    q_gain = jnp.tile(head_gains[0], q_heads)
    k_gain = jnp.tile(head_gains[1], kv_heads)
    query = (q_normed * q_gain).astype(BF16)
    key = (k_normed * k_gain).astype(BF16)
    value = matmul(act2, value_full).astype(BF16)
    d_sum_low = (lax.dynamic_index_in_dim(cotangent, section, keepdims=False).astype(F32) * mask).astype(BF16)
    attended, log_total, kv_all, d_sum_all, gate2, up2, down2 = attend(
        length.reshape(1),
        query,
        jnp.concatenate([key, value], axis=1),
        d_sum_low,
        ffn_gate[0],
        ffn_up[0],
        ffn_down[0],
        3,
    )
    attended_low = attended.astype(BF16)
    attn_rows = matmul(attended_low, proj_full)
    res2 = h + attn_rows
    terms2, kept2 = ffn_forward(res2, norm_gains[3], gate2, up2, down2)

    d_sum = d_sum_low.astype(F32)
    d_ffn, gain3, grads2 = ffn_backward(d_sum_all, kept2, norm_gains[3], gate2, up2, down2)
    d_res2 = d_sum + d_ffn
    d_attn = d_res2.astype(BF16)
    grad_proj = matmul_left(attended_low, d_attn)
    d_att = matmul_right(d_attn, proj_full).astype(BF16)
    half = part // 2
    strip = half // lax.axis_size("ctx")

    def shared(mine, theirs):
        return (mine.astype(F32) + swapped(theirs, "section").astype(F32)).astype(BF16)

    def column_half(which):
        pieces = jnp.stack(grads2[:2]).reshape(2, fsdp, 2, half // strip, strip, -1)
        pieces = lax.dynamic_index_in_dim(pieces, which, 2, keepdims=False)
        return pieces.transpose(2, 1, 0, 3, 4).reshape(2 * fsdp * half, -1)

    def down_half(which):
        size = grads2[2].shape[0] // 2
        return lax.dynamic_slice_in_dim(grads2[2], which * size, size, 0)

    delta = jnp.sum((d_att.astype(F32) * attended).reshape(rows, q_heads, head), axis=-1)
    d_query, d_kv, ffn2 = attend_back(
        length.reshape(1), query, kv_all, d_att, log_total, delta.T.reshape(q_heads, 1, rows), terms2, 4
    )
    result = (res2 + ffn2) * mask

    def square(values):
        return jnp.sum(mask * values * values)

    squares = jnp.stack(
        [square(v) for v in (x, mixed, ffn1, h, attn_rows, res2, ffn2, result)]
    )
    second_gu, second_down = (
        lax.psum_scatter(
            shared(pick(section), pick(1 - section)), "ctx", scatter_dimension=0, tiled=True
        )
        for pick in (column_half, down_half)
    )
    d_qn = rounded(d_query)
    grad_qgain = jnp.sum(jnp.sum(d_qn * q_normed, axis=0).reshape(q_heads, head), axis=0)
    d_qpre = norm_heads_back(d_qn * q_gain, q_normed, q_inv, head).astype(BF16)
    d_kn = rounded(d_kv[:, :kv_width])
    grad_kgain = jnp.sum(jnp.sum(d_kn * k_normed, axis=0).reshape(kv_heads, head), axis=0)
    d_kpre = norm_heads_back(d_kn * k_gain, k_normed, k_inv, head).astype(BF16)
    d_vpre = d_kv[:, kv_width:].astype(BF16)
    d_act2 = (
        matmul_right(d_qpre, query_full)
        + matmul_right(d_kpre, key_full)
        + matmul_right(d_vpre, value_full)
    )
    gain2 = jnp.sum(d_act2 * normed2, axis=0)
    d_h_low = (d_res2 + norm_back(d_act2 * norm_gains[2], normed2, inv2)).astype(BF16)

    d_h_all, second_gu = gathered_swapped(d_h_low, second_gu.reshape(fsdp, 2 * strip, -1), 5)
    second_gu = lax.all_gather(second_gu, "ctx", axis=0)
    second_down = lax.all_gather(second_down, "ctx", axis=0, tiled=True)
    d_ffn1, gain1, grads1 = ffn_backward(d_h_all, kept1, norm_gains[1], gate1, up1, down1)
    d_ffn1, second_gu = lax.optimization_barrier((d_ffn1, second_gu))
    d_res1 = d_h_low.astype(F32) + d_ffn1
    d_mixed = d_res1.astype(BF16)
    grad_out = matmul_left(z_low, d_mixed)
    d_z = matmul_right(d_mixed, out_full)
    d_cgate = d_z * convolved
    d_conv = d_z * c_gate
    grad_kernel = jnp.stack(
        [
            jnp.sum(d_conv * extended[:-2], axis=0),
            jnp.sum(d_conv * extended[1:-1], axis=0),
            jnp.sum(d_conv * extended[2:], axis=0),
        ]
    )
    d_extended = (
        jnp.pad(d_conv * conv_kernel[0], ((0, 2), (0, 0)))
        + jnp.pad(d_conv * conv_kernel[1], ((1, 1), (0, 0)))
        + jnp.pad(d_conv * conv_kernel[2], ((2, 0), (0, 0)))
    )
    from_next, second_down = lax.optimization_barrier(
        (passed_along(d_extended[:2], "ctx", -1), second_down)
    )
    d_bproduct = rounded(d_extended[2:] + jnp.pad(from_next, ((rows - 2, 0), (0, 0))))
    d_projected = jnp.concatenate(
        [d_bproduct * x_value, d_cgate, d_bproduct * b_gate], axis=1
    ).astype(BF16)
    d_act1 = matmul_right(d_projected, in_full)
    gain0 = jnp.sum(d_act1 * normed0, axis=0)
    d_x = (d_res1 + norm_back(d_act1 * norm_gains[0], normed0, inv0)).astype(BF16)

    y_low = result.astype(BF16)
    is_first = section == 0
    other_end = swapped(jnp.where(is_first, y_low, d_x), "section")
    ends = jnp.where(is_first, jnp.stack([d_x, other_end]), jnp.stack([other_end, y_low]))[None]

    grad_parts = [
        matmul_left(act1, d_projected[:, i * width : (i + 1) * width]).astype(BF16) for i in range(3)
    ]
    mixers = [
        matmul_left(act2, d_qpre).astype(BF16),
        matmul_left(act2, jnp.concatenate([d_kpre, d_vpre], axis=1)).astype(BF16),
        grad_proj.astype(BF16),
    ] + grad_parts + [grad_out.astype(BF16)]

    last_row = jnp.concatenate(
        [grad_qgain, grad_kgain, squares, jnp.zeros((width - 2 * head - squares.shape[0],), F32)]
    )
    small = jnp.concatenate(
        [
            jnp.stack([gain0, gain1, gain2, gain3]),
            grad_kernel,
            last_row[None],
            jnp.zeros((24, width), F32),
        ]
    ).astype(BF16)
    small = small.reshape(2, 16, width)
    gu_sum, down_sum, rest_sum = summed_gradients(
        grads1,
        mixers,
        small,
        second_gu.reshape(-1, fsdp, 2, strip, second_gu.shape[-1]),
        second_down,
    )
    rest_sum = rest_sum.astype(F32)

    def block(index):
        rows_at = slice(index * half, (index + 1) * half)
        return rest_sum[:, rows_at].reshape(2 * half, width)

    attn_blocks = [block(i) for i in range(3)]
    conv_blocks = [block(3 + i) for i in range(4)]
    small_sum = rest_sum[0, 7 * half : 7 * half + 8]
    cut = width // fsdp
    mine = lax.dynamic_slice_in_dim(small_sum[:7], group * cut, cut, 1)
    head_cut = head // fsdp
    heads = lax.dynamic_slice_in_dim(
        small_sum[7, : 2 * head].reshape(2, head), group * head_cut, head_cut, 1
    )
    square_cut = squares.shape[0] // fsdp
    square_sum = lax.dynamic_slice_in_dim(small_sum[7], 2 * head + group * square_cut, square_cut)
    token_total = jnp.sum(lengths).astype(F32) * width
    rms = jnp.sqrt(square_sum / token_total)
    return (
        ends,
        mine[:3],
        mine[3],
        jnp.concatenate(conv_blocks[:3], axis=1),
        mine[4:7],
        conv_blocks[3],
        attn_blocks[0],
        attn_blocks[1][:, :kv_width],
        attn_blocks[1][:, kv_width:],
        attn_blocks[2],
        heads,
        gu_sum[0][None].astype(F32),
        gu_sum[1][None].astype(F32),
        down_sum[None].astype(F32),
        rms,
    )


def solution(mesh):
    return jax.shard_map(
        shards,
        mesh=mesh,
        in_specs=(
            P("fsdp", "ctx", None),
            P("fsdp", "ctx", None),
            P(),
            P(),
            P("fsdp", None),
            P(),
            P("fsdp", None),
            P("fsdp", None),
            P("fsdp", None),
            P("fsdp", None),
            P("fsdp", None),
            P(),
            P("section", "fsdp", None),
            P("section", "fsdp", None),
            P("section", "fsdp", None),
        ),
        out_specs=(
            P("section", "fsdp", "ctx", None),
            P(None, "fsdp"),
            P("fsdp"),
            P("fsdp", None),
            P(None, "fsdp"),
            P("fsdp", None),
            P("fsdp", None),
            P("fsdp", None),
            P("fsdp", None),
            P("fsdp", None),
            P(None, "fsdp"),
            P("section", "fsdp", None),
            P("section", "fsdp", None),
            P("section", "fsdp", None),
            P("fsdp"),
        ),
        check_vma=False,
    )
```

```python
import functools

import jax
import jax.numpy as jnp
from jax import lax
from jax.experimental import pallas as pl
from jax.experimental.pallas import tpu as pltpu
from jax.sharding import PartitionSpec as P

EPSILON = 1e-05
NEGATIVE = -1e30
MESH = pl.DeviceIdType.MESH
F32 = jnp.float32
BF16 = jnp.bfloat16


def passed_along(block, axis, distance):
    devices = range(lax.axis_size(axis))
    route = [(i - distance, i) for i in devices if i - distance in devices]
    return lax.ppermute(block, axis, route)


def swapped(block, axis):
    return lax.ppermute(block, axis, [(0, 1), (1, 0)])


def rounded(values):
    return lax.optimization_barrier(values.astype(BF16)).astype(F32)


def matmul(left_op, right_op):
    return jnp.dot(left_op, right_op, preferred_element_type=F32)


def matmul_left(left_op, right_op):
    return lax.dot_general(left_op, right_op, (((0,), (0,)), ((), ())), preferred_element_type=F32)


def matmul_right(left_op, right_op):
    return lax.dot_general(left_op, right_op, (((1,), (1,)), ((), ())), preferred_element_type=F32)


def norm_rows(values):
    inv_rms = lax.rsqrt(jnp.mean(values * values, axis=-1, keepdims=True) + EPSILON)
    return (values * inv_rms, inv_rms)


def norm_back(dnormed, normed, inv_rms):
    return inv_rms * dnormed - normed * inv_rms * jnp.mean(dnormed * normed, axis=-1, keepdims=True)


def head_sums(values, head):
    heads = values.shape[1] // head
    owner = (jnp.arange(values.shape[1])[:, None] // head == jnp.arange(heads)[None, :]).astype(F32)
    sums = jnp.dot(values, owner, precision=lax.Precision.HIGHEST, preferred_element_type=F32)
    return jnp.dot(sums, owner.T, precision=lax.Precision.HIGHEST, preferred_element_type=F32)


def norm_heads(values, head):
    inv_rms = lax.rsqrt(head_sums(values * values, head) / head + EPSILON)
    return (values * inv_rms, inv_rms)


def norm_heads_back(dnormed, normed, inv_rms, head):
    return inv_rms * dnormed - normed * inv_rms * (head_sums(dnormed * normed, head) / head)


def busy(microseconds):
    return pl.CostEstimate(flops=int(microseconds), bytes_accessed=1 << 16, transcendentals=0)


def corners():
    me = lax.axis_index("fsdp")
    beside = me + 1 - 2 * lax.rem(me, 2)
    across = lax.rem(me + 2, 4)
    return me, beside, across, lax.rem(beside + 2, 4)


def greet_sides():
    _, beside, across, _ = corners()
    barrier = pltpu.get_barrier_semaphore()
    for target in (beside, across):
        pl.semaphore_signal(barrier, inc=1, device_id={"fsdp": target}, device_id_type=MESH)
    pl.semaphore_wait(barrier, 2)


def to_side(src, dst, send_sem, recv_sem, target):
    return pltpu.make_async_remote_copy(
        src_ref=src,
        dst_ref=dst,
        send_sem=send_sem,
        recv_sem=recv_sem,
        device_id={"fsdp": target},
        device_id_type=MESH,
    )


class SideGather:
    def __init__(self, block, whole, send_sem, recv_sem, own_sem):
        me, beside, across, _ = corners()
        rows = block.shape[0]
        half = rows // 2

        def part(owner, start, size):
            return whole.at[pl.ds(pl.multiple_of(owner * rows + start, half), size)]

        self.first = to_side(block, part(me, 0, rows), send_sem.at[0], recv_sem.at[0], beside)
        self.second = to_side(block, part(me, 0, rows), send_sem.at[1], recv_sem.at[1], across)
        at = part(beside, 0, half)
        self.third = to_side(at, at, send_sem.at[2], recv_sem.at[2], across)
        at = part(across, half, half)
        self.fourth = to_side(at, at, send_sem.at[3], recv_sem.at[3], beside)
        self.own = pltpu.make_async_copy(block, part(me, 0, rows), own_sem)

    def start(self):
        self.first.start()
        self.second.start()
        self.own.start()

    def relay(self):
        self.first.wait_recv()
        self.third.start()
        self.second.wait_recv()
        self.fourth.start()

    def finish(self):
        self.own.wait()
        self.first.wait_send()
        self.second.wait_send()
        self.third.wait()
        self.fourth.wait()


def gather_kernel(block, whole, send_sem, recv_sem, own_sem):
    greet_sides()
    gather = SideGather(block, whole, send_sem, recv_sem, own_sem)
    gather.start()
    gather.relay()
    gather.finish()


def gathered(array, collective_id):
    rows, width = array.shape
    assert lax.axis_size("fsdp") == 4
    dma = pltpu.SemaphoreType.DMA
    return pl.pallas_call(
        gather_kernel,
        out_shape=jax.ShapeDtypeStruct((4 * rows, width), array.dtype),
        in_specs=[pl.BlockSpec(memory_space=pltpu.VMEM)],
        out_specs=pl.BlockSpec(memory_space=pltpu.VMEM),
        scratch_shapes=[dma((4,)), dma((4,)), dma],
        compiler_params=pltpu.CompilerParams(
            collective_id=collective_id, has_side_effects=True, vmem_limit_bytes=8 << 20
        ),
        cost_estimate=busy(25),
    )(array)


def gather_swap_kernel(block, pieces, whole, swapped_out, send_sem, recv_sem, own_sem, cross_send, cross_recv, keep_sem):
    me, beside, across, opposite = corners()
    barrier = pltpu.get_barrier_semaphore()
    for target in (beside, across, opposite):
        pl.semaphore_signal(barrier, inc=1, device_id={"fsdp": target}, device_id_type=MESH)
    pl.semaphore_wait(barrier, 3)
    gather = SideGather(block, whole, send_sem, recv_sem, own_sem)
    gather.start()
    crossing = []
    for step in range(1, 4):
        target = lax.rem(me + step, 4)
        crossing.append(
            to_side(pieces.at[target], swapped_out.at[me], cross_send.at[step], cross_recv.at[step], target)
        )
        crossing[-1].start()
    keep = pltpu.make_async_copy(pieces.at[me], swapped_out.at[me], keep_sem)
    keep.start()
    gather.relay()
    gather.finish()
    keep.wait()
    for copy in crossing:
        copy.wait()


def gathered_swapped(array, pieces, collective_id):
    rows, width = array.shape
    dma = pltpu.SemaphoreType.DMA
    vmem = pl.BlockSpec(memory_space=pltpu.VMEM)
    hbm = pl.BlockSpec(memory_space=pl.ANY)
    return pl.pallas_call(
        gather_swap_kernel,
        out_shape=(
            jax.ShapeDtypeStruct((4 * rows, width), array.dtype),
            jax.ShapeDtypeStruct(pieces.shape, pieces.dtype),
        ),
        in_specs=[vmem, hbm],
        out_specs=[vmem, hbm],
        scratch_shapes=[dma((4,)), dma((4,)), dma, dma((4,)), dma((4,)), dma],
        compiler_params=pltpu.CompilerParams(
            collective_id=collective_id, has_side_effects=True, vmem_limit_bytes=8 << 20
        ),
        cost_estimate=busy(25),
    )(array, pieces)


class SideReduce:
    def __init__(self, blocks, total, beside_got, across_got, passed, passed_got, send_sem, recv_sem):
        self.refs = blocks, total, beside_got, across_got, passed, passed_got
        me, beside, across, opposite = corners()
        self.me, self.beside, self.across = me, beside, across
        self.copies = []
        for index, (turn, target, got) in enumerate(((0, beside, beside_got), (1, across, across_got))):
            for slot, owner in ((1, opposite), (0, target)):
                self.copies.append(
                    to_side(
                        blocks.at[self.part(owner, turn)],
                        got.at[slot],
                        send_sem.at[2 * index + slot],
                        recv_sem.at[2 * index + slot],
                        target,
                    )
                )
        self.onward = [
            to_side(passed.at[turn], passed_got.at[turn], send_sem.at[4 + turn], recv_sem.at[4 + turn], owner)
            for turn, owner in ((0, across), (1, beside))
        ]

    def part(self, owner, turn):
        half = self.refs[1].shape[0] // 2
        return pl.ds(pl.multiple_of(owner * 2 * half + turn * half, half), half)

    def start(self):
        for index in (0, 2, 1, 3):
            self.copies[index].start()

    def relay(self):
        blocks, _, beside_got, across_got, passed, _ = self.refs
        for turn, owner, index, got in ((0, self.across, 0, beside_got), (1, self.beside, 2, across_got)):
            self.copies[index].wait_recv()
            passed[turn] = (blocks[self.part(owner, turn)].astype(F32) + got[1].astype(F32)).astype(BF16)
            self.onward[turn].start()

    def finish(self):
        blocks, total, beside_got, across_got, _, passed_got = self.refs
        half = total.shape[0] // 2
        for turn, index, got in ((0, 1, beside_got), (1, 3, across_got)):
            self.copies[index].wait_recv()
            total[pl.ds(turn * half, half)] = blocks[self.part(self.me, turn)].astype(F32) + got[0].astype(F32)
        for turn in range(2):
            self.onward[turn].wait_recv()
            at = pl.ds(turn * half, half)
            total[at] = total[at] + passed_got[turn].astype(F32)
        for copy in self.copies + self.onward:
            copy.wait_send()


def reduce_kernel(blocks, total, beside_got, across_got, passed, passed_got, send_sem, recv_sem):
    greet_sides()
    reduction = SideReduce(blocks, total, beside_got, across_got, passed, passed_got, send_sem, recv_sem)
    reduction.start()
    reduction.relay()
    reduction.finish()


def reduce_pair_kernel(
    blocks,
    give_a,
    give_b,
    total,
    got_a,
    got_b,
    beside_got,
    across_got,
    passed,
    passed_got,
    send_sem,
    recv_sem,
    pair_send,
    pair_recv,
):
    other = {"section": 1 - lax.axis_index("section")}
    _, beside, across, _ = corners()
    barrier = pltpu.get_barrier_semaphore()
    for target in ({"fsdp": beside}, {"fsdp": across}, other):
        pl.semaphore_signal(barrier, inc=1, device_id=target, device_id_type=MESH)
    pl.semaphore_wait(barrier, 3)
    reduction = SideReduce(blocks, total, beside_got, across_got, passed, passed_got, send_sem, recv_sem)
    reduction.start()
    pairs = [
        pltpu.make_async_remote_copy(
            src_ref=src,
            dst_ref=dst,
            send_sem=pair_send.at[index],
            recv_sem=pair_recv.at[index],
            device_id=other,
            device_id_type=MESH,
        )
        for index, (src, dst) in enumerate(((give_a, got_a), (give_b, got_b)))
    ]
    for copy in pairs:
        copy.start()
    reduction.relay()
    reduction.finish()
    for copy in pairs:
        copy.wait()


def reduced_swapping(partial, give_a, give_b, collective_id):
    rows, width = partial.shape[0] // 4, partial.shape[1]
    dma = pltpu.SemaphoreType.DMA
    pair = pltpu.VMEM((2, rows // 2, width), BF16)
    vmem = pl.BlockSpec(memory_space=pltpu.VMEM)
    hbm = pl.BlockSpec(memory_space=pl.ANY)
    return pl.pallas_call(
        reduce_pair_kernel,
        out_shape=(
            jax.ShapeDtypeStruct((rows, width), F32),
            jax.ShapeDtypeStruct(give_a.shape, BF16),
            jax.ShapeDtypeStruct(give_b.shape, BF16),
        ),
        in_specs=[vmem, hbm, hbm],
        out_specs=[vmem, hbm, hbm],
        scratch_shapes=[pair, pair, pair, pair, dma((6,)), dma((6,)), dma((2,)), dma((2,))],
        compiler_params=pltpu.CompilerParams(
            collective_id=collective_id, has_side_effects=True, vmem_limit_bytes=16 << 20
        ),
        cost_estimate=busy(25),
    )(partial.astype(BF16), give_a, give_b)


def reduced(partial, collective_id):
    rows, width = partial.shape[0] // 4, partial.shape[1]
    assert lax.axis_size("fsdp") == 4
    dma = pltpu.SemaphoreType.DMA
    pair = pltpu.VMEM((2, rows // 2, width), BF16)
    return pl.pallas_call(
        reduce_kernel,
        out_shape=jax.ShapeDtypeStruct((rows, width), F32),
        in_specs=[pl.BlockSpec(memory_space=pltpu.VMEM)],
        out_specs=pl.BlockSpec(memory_space=pltpu.VMEM),
        scratch_shapes=[pair, pair, pair, pair, dma((6,)), dma((6,))],
        compiler_params=pltpu.CompilerParams(
            collective_id=collective_id, has_side_effects=True, vmem_limit_bytes=16 << 20
        ),
        cost_estimate=busy(25),
    )(partial.astype(BF16))


def tail_kernel(
    counts,
    gate_in,
    up_in,
    down_in,
    query_in,
    kv_in,
    proj_in,
    conv_b_in,
    conv_c_in,
    conv_x_in,
    conv_o_in,
    small_in,
    second_gu_in,
    second_down_in,
    gu_out,
    down_out,
    rest_out,
    a_own,
    a_other,
    a_sum,
    a_done,
    b_own,
    b_other,
    b_sum,
    b_done,
    c_own,
    c_other,
    c_got,
    own_sem,
    pair_send,
    pair_recv,
    c_own_sem,
    c_pair_send,
    c_pair_recv,
    c_send,
    c_recv,
    a_up_send,
    a_up_recv,
    a_back_send,
    a_back_recv,
    a_out_send,
    b_up_send,
    b_up_recv,
    b_back_send,
    b_back_recv,
    b_out_send,
    b_keep_sem,
    gu_recv,
    down_recv,
    rest_recv,
    second_send,
    second_recv,
):
    n_ctx, n_fsdp = counts
    section = lax.axis_index("section")
    place = lax.axis_index("ctx")
    group = lax.axis_index("fsdp")
    other = 1 - section
    a_chunks, a_rows, a_width = a_own.shape
    b_chunks, b_rows, b_width = b_own.shape
    half = gate_in.shape[0] // n_fsdp // 2
    subs = half // a_rows
    per_kind = n_fsdp * subs
    down_half = down_in.shape[0] // 2
    down_chunks = down_half // b_rows
    c_rows = c_own.shape[1]
    mixers = (query_in, kv_in, proj_in, conv_b_in, conv_c_in, conv_x_in, conv_o_in)
    n_mix = len(mixers)
    cut = 3 * half // b_rows
    c_parts = ((0, cut), (cut, c_rows // b_rows))
    ticks = a_chunks
    tail = 2 * (n_ctx - 1)

    barrier = pltpu.get_barrier_semaphore()
    for step in range(1, 2 * n_fsdp):
        flat = lax.rem(section * n_fsdp + group + step, 2 * n_fsdp)
        pl.semaphore_signal(
            barrier,
            inc=1,
            device_id={"section": flat // n_fsdp, "fsdp": lax.rem(flat, n_fsdp)},
            device_id_type=MESH,
        )

    @pl.when(place > 0)
    def _():
        pl.semaphore_signal(barrier, inc=1, device_id={"ctx": place - 1}, device_id_type=MESH)

    @pl.when(place < n_ctx - 1)
    def _():
        pl.semaphore_signal(barrier, inc=1, device_id={"ctx": place + 1}, device_id_type=MESH)

    at_edge = (place == 0) | (place == n_ctx - 1)

    @pl.when(at_edge)
    def _():
        pl.semaphore_wait(barrier, 2 * n_fsdp)

    @pl.when(jnp.logical_not(at_edge))
    def _():
        pl.semaphore_wait(barrier, 2 * n_fsdp + 1)

    def half_rows(owner, which):
        return pl.ds(pl.multiple_of(owner * (2 * half) + which * half, half), half)

    a_part, b_part = a_rows // 2, b_width // 2

    def a_at(buffer, k, way):
        return buffer.at[k, pl.ds(way * a_part, a_part)]

    def b_at(buffer, k, way):
        return buffer.at[k, :, pl.ds(way * b_part, b_part)]

    def opening(k, way):
        copies = []
        kind, rest = divmod(k, per_kind)
        owner, sub = divmod(rest, subs)
        source = (gate_in, up_in)[kind]
        spots = []
        for which in (section, other):
            start = owner * (2 * half) + which * half + sub * a_rows + way * a_part
            spots.append(source.at[pl.ds(pl.multiple_of(start, a_part), a_part)])
        spot = 2 * k + way
        copies.append((spots, a_at(a_own, k, way), a_at(a_other, k, way), spot))
        if k < down_chunks:
            spots = [
                down_in.at[
                    pl.ds(pl.multiple_of(which * down_half + k * b_rows, b_rows), b_rows),
                    pl.ds(way * b_part, b_part),
                ]
                for which in (section, other)
            ]
            copies.append((spots, b_at(b_own, k, way), b_at(b_other, k, way), 2 * a_chunks + spot))
        for (mine, theirs), own_dst, other_dst, spot in copies:
            pltpu.make_async_copy(mine, own_dst, own_sem.at[spot]).start()
            pltpu.make_async_remote_copy(
                src_ref=theirs,
                dst_ref=other_dst,
                send_sem=pair_send.at[spot],
                recv_sem=pair_recv.at[spot],
                device_id={"section": other},
                device_id_type=MESH,
            ).start()

    for k in range(a_chunks):
        for way in range(2):
            opening(k, way)
    c_local, c_pair = ([], []), ([], [])
    for kind, source in enumerate(mixers):
        part = 0 if kind < 3 else 1
        for owner in range(n_fsdp):
            index = owner * (n_mix + 1) + kind
            place_at = pl.ds(kind * half, half)
            c_local[part].append(
                pltpu.make_async_copy(
                    source.at[half_rows(owner, section)], c_own.at[owner, place_at], c_own_sem.at[index]
                )
            )
            c_pair[part].append(
                pltpu.make_async_remote_copy(
                    src_ref=source.at[half_rows(owner, other)],
                    dst_ref=c_other.at[owner, place_at],
                    send_sem=c_pair_send.at[index],
                    recv_sem=c_pair_recv.at[index],
                    device_id={"section": other},
                    device_id_type=MESH,
                )
            )
    for owner in range(n_fsdp):
        small_at = pl.ds(n_mix * half, c_rows - n_mix * half)
        index = owner * (n_mix + 1) + n_mix
        c_local[1].append(
            pltpu.make_async_copy(small_in.at[section], c_own.at[owner, small_at], c_own_sem.at[index])
        )
        c_pair[1].append(
            pltpu.make_async_remote_copy(
                src_ref=small_in.at[other],
                dst_ref=c_other.at[owner, small_at],
                send_sem=c_pair_send.at[index],
                recv_sem=c_pair_recv.at[index],
                device_id={"section": other},
                device_id_type=MESH,
            )
        )
    for part in range(2):
        for copy in c_pair[part]:
            copy.start()
        for copy in c_local[part]:
            copy.start()
    b_own[b_chunks - 1] = jnp.zeros((b_rows, b_width), BF16)
    _, beside, across, opposite = corners()

    def span(first, last):
        return pl.ds(first * b_rows, (last - first) * b_rows)

    def mixer_spans(part):
        first, last = c_parts[part]
        middle = (first + last) // 2
        return (first, middle, beside, across), (middle, last, across, beside)

    def mixer_copies(part):
        opening, onward = [], []
        for turn, (first, last, near, far) in enumerate(mixer_spans(part)):
            at = span(first, last)
            for slot, owner in ((0, opposite), (1, near)):
                opening.append(
                    to_side(
                        c_own.at[owner, at],
                        c_got.at[slot, at],
                        c_send.at[part, 3 * turn + slot],
                        c_recv.at[part, 3 * turn + slot],
                        near,
                    )
                )
            onward.append(
                to_side(
                    c_own.at[far, at],
                    c_got.at[2, at],
                    c_send.at[part, 3 * turn + 2],
                    c_recv.at[part, 3 * turn + 2],
                    far,
                )
            )
        return opening, onward

    def mixer_out(part):
        for copy in c_local[part]:
            copy.wait()
        for copy in c_pair[part]:
            copy.wait_recv()
        first, last = c_parts[part]
        size = last - first

        def add(index, carry):
            owner = index // size
            at = pl.ds(pl.multiple_of((first + lax.rem(index, size)) * b_rows, b_rows), b_rows)
            c_own[owner, at] = (c_own[owner, at].astype(F32) + c_other[owner, at].astype(F32)).astype(BF16)
            return carry

        lax.fori_loop(0, n_fsdp * size, add, 0)
        opening, _ = mixer_copies(part)
        for index in (0, 2, 1, 3):
            opening[index].start()

    def mixer_on(part):
        opening, onward = mixer_copies(part)
        for turn, (first, last, near, far) in enumerate(mixer_spans(part)):
            opening[2 * turn].wait_recv()

            def add(index, carry, far=far):
                at = pl.ds(pl.multiple_of(index * b_rows, b_rows), b_rows)
                c_own[far, at] = (c_own[far, at].astype(F32) + c_got[0, at].astype(F32)).astype(BF16)
                return carry

            lax.fori_loop(first, last, add, 0)
            onward[turn].start()

    def mixer_in(part):
        opening, onward = mixer_copies(part)
        for turn in range(2):
            opening[2 * turn + 1].wait_recv()
            onward[turn].wait_recv()
        first, last = c_parts[part]

        def add(index, carry):
            at = pl.ds(pl.multiple_of(index * b_rows, b_rows), b_rows)
            total = c_own[group, at].astype(F32) + c_got[1, at].astype(F32) + c_got[2, at].astype(F32)
            b_own[down_chunks + index] = total.astype(BF16)
            return carry

        lax.fori_loop(first, last, add, 0)

    strip = half // n_ctx

    def second_copies(remote):
        for index in range(n_ctx * n_fsdp * 2):
            source, kind = index // 2, index % 2
            turn, owner = source // n_fsdp, source % n_fsdp
            src = second_gu_in.at[turn, owner, kind]
            dst = gu_out.at[
                kind,
                pl.ds(pl.multiple_of(section * half + turn * strip, strip), strip),
                pl.ds(owner * a_width, a_width),
            ]
            if remote:
                pltpu.make_async_remote_copy(
                    src_ref=src,
                    dst_ref=dst,
                    send_sem=second_send.at[0],
                    recv_sem=second_recv,
                    device_id={"section": 1},
                    device_id_type=MESH,
                ).start()
            else:
                pltpu.make_async_copy(src, dst, second_send.at[0]).start()

    def second_start():
        down_at = down_out.at[pl.ds(pl.multiple_of(section * down_half, b_rows), down_half)]

        @pl.when(section == 1)
        def _():
            second_copies(False)
            pltpu.make_async_copy(second_down_in, down_at, second_send.at[1]).start()

        @pl.when(section == 0)
        def _():
            second_copies(True)
            pltpu.make_async_remote_copy(
                src_ref=second_down_in,
                dst_ref=down_at,
                send_sem=second_send.at[1],
                recv_sem=down_recv,
                device_id={"section": 1},
                device_id_type=MESH,
            ).start()

    def a_target(k, way):
        kind = k // per_kind
        rest = lax.rem(k, per_kind)
        owner = rest // subs
        sub = lax.rem(rest, subs)
        start = section * half + sub * a_rows + way * a_part
        spot = gu_out.at[
            kind,
            pl.ds(pl.multiple_of(start, a_part), a_part),
            pl.ds(pl.multiple_of(group * a_width, 128), a_width),
        ]
        return kind, owner, spot

    def hand_out(k, way):
        kind, owner, spot = a_target(k, way)
        is_mine = (section == 0) & (group == owner)
        slot = 2 * k + way
        a_ref, b_ref = a_at(a_done, k, way), b_at(b_done, k, way)
        lanes_at = pl.ds(way * b_part, b_part)

        @pl.when(is_mine)
        def _():
            pltpu.make_async_copy(a_ref, spot, a_out_send.at[slot]).start()

        @pl.when(jnp.logical_not(is_mine))
        def _():
            pltpu.make_async_remote_copy(
                src_ref=a_ref,
                dst_ref=spot,
                send_sem=a_out_send.at[slot],
                recv_sem=gu_recv.at[kind, section * n_fsdp + group],
                device_id={"section": 0, "fsdp": owner},
                device_id_type=MESH,
            ).start()

        @pl.when(k < down_chunks)
        def _():
            at = down_out.at[pl.ds(pl.multiple_of(section * down_half + k * b_rows, b_rows), b_rows), lanes_at]

            @pl.when(section == 0)
            def _():
                pltpu.make_async_copy(b_ref, at, b_out_send.at[slot]).start()

            @pl.when(section == 1)
            def _():
                pltpu.make_async_remote_copy(
                    src_ref=b_ref,
                    dst_ref=at,
                    send_sem=b_out_send.at[slot],
                    recv_sem=down_recv,
                    device_id={"section": 0},
                    device_id_type=MESH,
                ).start()

        @pl.when(k >= down_chunks)
        def _():
            at = rest_out.at[
                section, pl.ds(pl.multiple_of((k - down_chunks) * b_rows, b_rows), b_rows), lanes_at
            ]
            pltpu.make_async_copy(b_ref, at, b_keep_sem.at[slot]).start()
            pltpu.make_async_remote_copy(
                src_ref=b_ref,
                dst_ref=at,
                send_sem=b_out_send.at[slot],
                recv_sem=rest_recv,
                device_id={"section": other},
                device_id_type=MESH,
            ).start()

    def chain_copies(k, way, target, buffers, sems):
        slot = 2 * k + way
        return [
            pltpu.make_async_remote_copy(
                src_ref=at,
                dst_ref=at,
                send_sem=send.at[slot],
                recv_sem=recv.at[slot],
                device_id={"ctx": target},
                device_id_type=MESH,
            )
            for at, (send, recv) in zip((a_at(buffers[0], k, way), b_at(buffers[1], k, way)), sems)
        ]

    def up_copies(k, way, target):
        return chain_copies(
            k, way, target, (a_sum, b_sum), ((a_up_send, a_up_recv), (b_up_send, b_up_recv))
        )

    def back_copies(k, way, target):
        return chain_copies(
            k, way, target, (a_done, b_done), ((a_back_send, a_back_recv), (b_back_send, b_back_recv))
        )

    def a_load(buffer, k, way):
        return buffer[k, pl.ds(way * a_part, a_part)].astype(F32)

    def b_load(buffer, k, way):
        return buffer[k, :, pl.ds(way * b_part, b_part)].astype(F32)

    def a_store(buffer, k, way, value):
        buffer[k, pl.ds(way * a_part, a_part)] = value.astype(BF16)

    def b_store(buffer, k, way, value):
        buffer[k, :, pl.ds(way * b_part, b_part)] = value.astype(BF16)

    def own_terms(k, way):
        slot = 2 * k + way
        at = a_at(a_own, k, way)
        pltpu.make_async_copy(at, at, own_sem.at[slot]).wait()
        pltpu.make_async_copy(at, at, pair_recv.at[slot]).wait()

        @pl.when(k < down_chunks)
        def _():
            at = b_at(b_own, k, way)
            pltpu.make_async_copy(at, at, own_sem.at[2 * a_chunks + slot]).wait()
            pltpu.make_async_copy(at, at, pair_recv.at[2 * a_chunks + slot]).wait()
            b_store(b_own, k, way, b_load(b_own, k, way) + b_load(b_other, k, way))

        return a_load(a_own, k, way) + a_load(a_other, k, way), b_load(b_own, k, way)

    lanes = []
    for way in range(2):
        rank = place if way == 0 else n_ctx - 1 - place
        ahead = place + 1 if way == 0 else place - 1
        behind = place - 1 if way == 0 else place + 1
        lanes.append((way, rank, ahead, behind))

    def tick_step(tick, carry):
        events = (
            (1, mixer_out, 0),
            (3, mixer_out, 1),
            (6, mixer_on, 0),
            (down_chunks - 1, mixer_on, 1),
            (down_chunks, mixer_in, 0),
            (down_chunks + cut, mixer_in, 1),
        )
        for moment, action, part in events:

            @pl.when(tick == moment)
            def _(action=action, part=part):
                action(part)

        @pl.when(tick == 8)
        def _():
            second_start()

        for way, rank, ahead, behind in lanes:
            step = tick - rank
            k = jnp.clip(step, 0, ticks - 1)

            @pl.when((step >= 0) & (step < ticks))
            def _(k=k, way=way, rank=rank, ahead=ahead, behind=behind):
                a_term, b_term = own_terms(k, way)

                @pl.when(rank == 0)
                def _():
                    a_store(a_sum, k, way, a_term)
                    b_store(b_sum, k, way, b_term)

                @pl.when(rank > 0)
                def _():
                    for copy in up_copies(k, way, behind):
                        copy.wait_recv()

                @pl.when((rank > 0) & (rank < n_ctx - 1))
                def _():
                    a_store(a_sum, k, way, a_term + a_load(a_sum, k, way))
                    b_store(b_sum, k, way, b_term + b_load(b_sum, k, way))

                @pl.when(rank < n_ctx - 1)
                def _():
                    for copy in up_copies(k, way, ahead):
                        copy.start()

                @pl.when(rank == n_ctx - 1)
                def _():
                    a_store(a_done, k, way, a_term + a_load(a_sum, k, way))
                    b_store(b_done, k, way, b_term + b_load(b_sum, k, way))
                    for copy in back_copies(k, way, behind):
                        copy.start()
                    hand_out(k, way)

            late = tick - (tail - rank)
            j = jnp.clip(late, 0, ticks - 1)

            @pl.when((late >= 0) & (late < ticks) & (rank < n_ctx - 1))
            def _(j=j, way=way, rank=rank, ahead=ahead, behind=behind):
                for copy in back_copies(j, way, ahead):
                    copy.wait_recv()

                @pl.when(rank > 0)
                def _():
                    for copy in back_copies(j, way, behind):
                        copy.start()

                hand_out(j, way)

        return carry

    lax.fori_loop(0, ticks + tail, tick_step, 0)

    for part in range(2):
        for copy in c_pair[part]:
            copy.wait_send()
        opening, onward = mixer_copies(part)
        for copy in opening + onward:
            copy.wait_send()

    def settle(k, carry):
        for way, rank, ahead, behind in lanes:
            slot = 2 * k + way
            a_ref, b_ref = a_at(a_own, k, way), b_at(b_own, k, way)
            pltpu.make_async_copy(a_ref, a_ref, pair_send.at[slot]).wait()

            @pl.when(k < down_chunks)
            def _(b_ref=b_ref, slot=slot):
                pltpu.make_async_copy(b_ref, b_ref, pair_send.at[2 * a_chunks + slot]).wait()

            @pl.when(rank < n_ctx - 1)
            def _(k=k, way=way, ahead=ahead):
                for copy in up_copies(k, way, ahead):
                    copy.wait_send()

            @pl.when(rank > 0)
            def _(k=k, way=way, behind=behind):
                for copy in back_copies(k, way, behind):
                    copy.wait_send()

            pltpu.make_async_copy(a_ref, a_ref, a_out_send.at[slot]).wait()
            pltpu.make_async_copy(b_ref, b_ref, b_out_send.at[slot]).wait()

            @pl.when(k >= down_chunks)
            def _(b_ref=b_ref, slot=slot):
                pltpu.make_async_copy(b_ref, b_ref, b_keep_sem.at[slot]).wait()

        return carry

    lax.fori_loop(0, ticks, settle, 0)
    pltpu.make_async_copy(second_gu_in, second_gu_in, second_send.at[0]).wait()
    pltpu.make_async_copy(second_down_in, second_down_in, second_send.at[1]).wait()

    @pl.when(section == 0)
    def _():
        for kind in range(2):
            for source in range(2 * n_fsdp):

                @pl.when(group != source)
                def _(kind=kind, source=source):
                    region = gu_out.at[
                        kind,
                        pl.ds((source // n_fsdp) * half, half),
                        pl.ds((source % n_fsdp) * a_width, a_width),
                    ]
                    pltpu.make_async_copy(region, region, gu_recv.at[kind, source]).wait()

    @pl.when(section == 1)
    def _():
        pltpu.make_async_copy(second_gu_in, second_gu_in, second_recv).wait()

    region = down_out.at[pl.ds(pl.multiple_of(other * down_half, b_rows), down_half)]
    pltpu.make_async_copy(region, region, down_recv).wait()
    region = rest_out.at[other]
    pltpu.make_async_copy(region, region, rest_recv).wait()


def summed_gradients(first, mixers, small, second_gu, second_down):
    n_ctx, n_fsdp = lax.axis_size("ctx"), lax.axis_size("fsdp")
    gate, up, down = first
    half = gate.shape[0] // n_fsdp // 2
    a_rows, b_rows = half // 4, half * 3 // 8
    a_chunks = 2 * n_fsdp * 4
    a_width, b_width = gate.shape[1], down.shape[1]
    c_rows = len(mixers) * half + small.shape[1]
    down_chunks = down.shape[0] // 2 // b_rows
    b_chunks = down_chunks + c_rows // b_rows + 1
    assert a_chunks == b_chunks and c_rows % b_rows == 0
    rest = b_chunks - down_chunks
    dma = pltpu.SemaphoreType.DMA
    loads = 2 * (a_chunks + down_chunks)
    pieces = n_fsdp * (len(mixers) + 1)
    return pl.pallas_call(
        functools.partial(tail_kernel, (n_ctx, n_fsdp)),
        out_shape=(
            jax.ShapeDtypeStruct((2, 2 * half, n_fsdp * a_width), BF16),
            jax.ShapeDtypeStruct(down.shape, BF16),
            jax.ShapeDtypeStruct((2, rest * b_rows, b_width), BF16),
        ),
        in_specs=[pl.BlockSpec(memory_space=pl.ANY)] * (6 + len(mixers)),
        out_specs=[pl.BlockSpec(memory_space=pl.ANY)] * 3,
        scratch_shapes=[
            pltpu.VMEM((a_chunks, a_rows, a_width), BF16),
            pltpu.VMEM((a_chunks, a_rows, a_width), BF16),
            pltpu.VMEM((a_chunks, a_rows, a_width), BF16),
            pltpu.VMEM((a_chunks, a_rows, a_width), BF16),
            pltpu.VMEM((b_chunks, b_rows, b_width), BF16),
            pltpu.VMEM((down_chunks, b_rows, b_width), BF16),
            pltpu.VMEM((b_chunks, b_rows, b_width), BF16),
            pltpu.VMEM((b_chunks, b_rows, b_width), BF16),
            pltpu.VMEM((n_fsdp, c_rows, b_width), BF16),
            pltpu.VMEM((n_fsdp, c_rows, b_width), BF16),
            pltpu.VMEM((n_fsdp - 1, c_rows, b_width), BF16),
            dma((loads,)),
            dma((loads,)),
            dma((loads,)),
            dma((pieces,)),
            dma((pieces,)),
            dma((pieces,)),
            dma((2, 6)),
            dma((2, 6)),
            dma((2 * a_chunks,)),
            dma((2 * a_chunks,)),
            dma((2 * a_chunks,)),
            dma((2 * a_chunks,)),
            dma((2 * a_chunks,)),
            dma((2 * b_chunks,)),
            dma((2 * b_chunks,)),
            dma((2 * b_chunks,)),
            dma((2 * b_chunks,)),
            dma((2 * b_chunks,)),
            dma((2 * b_chunks,)),
            dma((2, 2 * n_fsdp)),
            dma,
            dma,
            dma((2,)),
            dma,
        ],
        compiler_params=pltpu.CompilerParams(
            collective_id=6, has_side_effects=True, vmem_limit_bytes=56 << 20
        ),
        cost_estimate=busy(160),
    )(gate, up, down, *mixers, small, second_gu, second_down)


def mixer_weights_kernel(count, first_in, second_in, first_out, second_out, send_sem, recv_sem, pair_send, pair_recv, own_sem):
    section = lax.axis_index("section")
    me = lax.axis_index("fsdp")
    other = 1 - section
    beside = me + 1 - 2 * lax.rem(me, 2)
    across = lax.rem(me + 2, count)
    opposite = lax.rem(beside + 2, count)
    rows = first_in.shape[0]
    half = rows // 2
    quarter = half // 2
    barrier = pltpu.get_barrier_semaphore()
    for target in ({"fsdp": beside}, {"fsdp": across}, {"section": other}):
        pl.semaphore_signal(barrier, inc=1, device_id=target, device_id_type=MESH)
    pl.semaphore_wait(barrier, 3)
    arrays = ((first_in, first_out), (second_in, second_out))

    def at_rows(owner, extra, size):
        return pl.ds(pl.multiple_of(owner * rows + extra, quarter), size)

    def remote(slot, sems, src, dst, target):
        return pltpu.make_async_remote_copy(
            src_ref=src,
            dst_ref=dst,
            send_sem=sems[0].at[slot],
            recv_sem=sems[1].at[slot],
            device_id=target,
            device_id_type=MESH,
        )

    hop, pair = (send_sem, recv_sem), (pair_send, pair_recv)
    waiting = []
    direct = []
    for index, (source, out) in enumerate(arrays):
        mine = source.at[pl.ds(pl.multiple_of(section * half, half), half)]
        spot = out.at[at_rows(me, section * half, half)]
        copies = [
            remote(index * 4, hop, mine, spot, {"fsdp": beside}),
            remote(index * 4 + 1, hop, mine, spot, {"fsdp": across}),
        ]
        for copy in copies:
            copy.start()
        direct.append(copies)
    own = [
        pltpu.make_async_copy(source, out.at[at_rows(me, 0, rows)], own_sem.at[index])
        for index, (source, out) in enumerate(arrays)
    ]
    for copy in own:
        copy.start()

    def arrived(owner, size, extra):
        return lambda out: out.at[at_rows(owner, section * half + extra, size)]

    onward = []
    for index, (source, out) in enumerate(arrays):
        direct[index][0].wait_recv()
        part = arrived(beside, quarter, 0)(out)
        onward.append(remote(index * 4 + 2, hop, part, part, {"fsdp": across}))
        onward[-1].start()
        whole = arrived(beside, half, 0)(out)
        waiting.append(remote(index * 4, pair, whole, whole, {"section": other}))
        waiting[-1].start()
        direct[index][1].wait_recv()
        part = arrived(across, quarter, quarter)(out)
        onward.append(remote(index * 4 + 3, hop, part, part, {"fsdp": beside}))
        onward[-1].start()
        whole = arrived(across, half, 0)(out)
        waiting.append(remote(index * 4 + 1, pair, whole, whole, {"section": other}))
        waiting[-1].start()
    for index, (source, out) in enumerate(arrays):
        for turn in range(2):
            onward[2 * index + turn].wait_recv()
            part = arrived(opposite, quarter, turn * quarter)(out)
            waiting.append(remote(index * 4 + 2 + turn, pair, part, part, {"section": other}))
            waiting[-1].start()
    for copy in own:
        copy.wait()
    for copies in direct:
        for copy in copies:
            copy.wait_send()
    for copy in onward:
        copy.wait_send()
    for copy in waiting:
        copy.wait()


def mixer_weights(first, second, collective_id):
    count = lax.axis_size("fsdp")
    dma = pltpu.SemaphoreType.DMA
    return pl.pallas_call(
        functools.partial(mixer_weights_kernel, count),
        out_shape=tuple(
            jax.ShapeDtypeStruct((count * w.shape[0], w.shape[1]), w.dtype) for w in (first, second)
        ),
        in_specs=[pl.BlockSpec(memory_space=pl.ANY)] * 2,
        out_specs=[pl.BlockSpec(memory_space=pl.ANY)] * 2,
        scratch_shapes=[dma((8,)), dma((8,)), dma((8,)), dma((8,)), dma((2,))],
        compiler_params=pltpu.CompilerParams(
            collective_id=collective_id, has_side_effects=True, vmem_limit_bytes=8 << 20
        ),
        cost_estimate=busy(45),
    )(first, second)


class Columns:
    def __init__(self, holder, sources, targets, send_sem, recv_sem, pair_send, pair_recv, own_sem):
        self.count = 4
        self.holder = holder
        self.section = lax.axis_index("section")
        self.me = lax.axis_index("fsdp")
        self.sources, self.targets = sources, targets
        self.sems = send_sem, recv_sem, pair_send, pair_recv, own_sem
        self.rows = sources[0].shape[0]
        self.wide = targets[0].shape[1]
        self.steps = [(step, kind) for step in range(1, self.count) for kind in range(2)]

    def at_rows(self, out, owner):
        return out.at[pl.ds(pl.multiple_of(owner * self.rows, self.rows), self.rows)]

    def at_columns(self, source, owner):
        return source.at[:, pl.ds(pl.multiple_of(owner * self.wide, 128), self.wide)]

    def crossing(self, step, kind):
        target = lax.rem(self.me + step, self.count)
        return to_side(
            self.at_columns(self.sources[kind], target),
            self.at_rows(self.targets[kind], self.me),
            self.sems[0].at[kind, step],
            self.sems[1].at[kind, step],
            target,
        )

    def handed(self, step, kind):
        if kind == 2:
            src, dst = self.sources[2], self.targets[2]
        else:
            origin = lax.rem(self.me + self.count - step, self.count)
            dst = self.at_rows(self.targets[kind], origin)
            src = self.at_columns(self.sources[kind], self.me) if step == 0 else dst
        return pltpu.make_async_remote_copy(
            src_ref=src,
            dst_ref=dst,
            send_sem=self.sems[2].at[kind, step],
            recv_sem=self.sems[3].at[kind, step],
            device_id={"section": 1 - self.section},
            device_id_type=MESH,
        )

    def kept(self, kind):
        if kind == 2:
            return pltpu.make_async_copy(self.sources[2], self.targets[2], self.sems[4].at[2])
        return pltpu.make_async_copy(
            self.at_columns(self.sources[kind], self.me),
            self.at_rows(self.targets[kind], self.me),
            self.sems[4].at[kind],
        )

    def start(self):
        @pl.when(self.section == self.holder)
        def _():
            for step, kind in self.steps:
                self.crossing(step, kind).start()
            for kind in range(3):
                self.handed(0, kind).start()
            for kind in range(3):
                self.kept(kind).start()

    def relay(self):
        @pl.when(self.section == self.holder)
        def _():
            for step, kind in self.steps:
                self.crossing(step, kind).wait_recv()
                self.handed(step, kind).start()

    def finish(self):
        every = [(0, kind) for kind in range(3)] + self.steps

        @pl.when(self.section == self.holder)
        def _():
            for kind in range(3):
                self.kept(kind).wait()
            for step, kind in self.steps:
                self.crossing(step, kind).wait_send()
            for step, kind in every:
                self.handed(step, kind).wait_send()

        @pl.when(self.section != self.holder)
        def _():
            for step, kind in every:
                self.handed(step, kind).wait_recv()


def column_weights_kernel(holder, *refs):
    section = lax.axis_index("section")
    _, beside, across, opposite = corners()
    barrier = pltpu.get_barrier_semaphore()
    for target in ({"fsdp": beside}, {"fsdp": across}, {"fsdp": opposite}, {"section": 1 - section}):
        pl.semaphore_signal(barrier, inc=1, device_id=target, device_id_type=MESH)
    pl.semaphore_wait(barrier, 4)
    columns = Columns(holder, refs[:3], refs[3:6], *refs[6:])
    columns.start()
    columns.relay()
    columns.finish()


def column_weights(gate, up, down, holder, collective_id):
    count = lax.axis_size("fsdp")
    assert count == 4
    dma = pltpu.SemaphoreType.DMA
    column = jax.ShapeDtypeStruct((count * gate.shape[0], gate.shape[1] // count), gate.dtype)
    return pl.pallas_call(
        functools.partial(column_weights_kernel, holder),
        out_shape=(column, column, jax.ShapeDtypeStruct(down.shape, down.dtype)),
        in_specs=[pl.BlockSpec(memory_space=pl.ANY)] * 3,
        out_specs=[pl.BlockSpec(memory_space=pl.ANY)] * 3,
        scratch_shapes=[dma((2, count)), dma((2, count)), dma((3, count)), dma((3, count)), dma((3,))],
        compiler_params=pltpu.CompilerParams(
            collective_id=collective_id, has_side_effects=True, vmem_limit_bytes=8 << 20
        ),
        cost_estimate=busy(40),
    )(gate, up, down)


class Chain:
    def __init__(self, count):
        self.count = count
        self.place = lax.axis_index("ctx")
        self.has_next = self.place < count - 1
        self.has_last = self.place > 0


def greet_mixed(chain, targets):
    barrier = pltpu.get_barrier_semaphore()
    for target in targets:
        pl.semaphore_signal(barrier, inc=1, device_id=target, device_id_type=MESH)

    @pl.when(chain.has_last)
    def _():
        pl.semaphore_signal(barrier, inc=1, device_id={"ctx": chain.place - 1}, device_id_type=MESH)

    @pl.when(chain.has_next)
    def _():
        pl.semaphore_signal(barrier, inc=1, device_id={"ctx": chain.place + 1}, device_id_type=MESH)

    inner = chain.has_last & chain.has_next

    @pl.when(inner)
    def _():
        pl.semaphore_wait(barrier, len(targets) + 2)

    @pl.when(jnp.logical_not(inner))
    def _():
        pl.semaphore_wait(barrier, len(targets) + 1)


def along(src, dst, send_sem, recv_sem, place):
    return pltpu.make_async_remote_copy(
        src_ref=src,
        dst_ref=dst,
        send_sem=send_sem,
        recv_sem=recv_sem,
        device_id={"ctx": place},
        device_id_type=MESH,
    )


def spread_heads(source, spread):
    rows = source.shape[0]
    low = lax.broadcasted_iota(jnp.int32, (rows, 128), 1) < 64
    for pair in range(source.shape[1] // 256):
        first = source[:, pair * 256 : pair * 256 + 128].astype(F32)
        second = source[:, pair * 256 + 128 : pair * 256 + 256].astype(F32)
        spread[4 * pair] = jnp.where(low, first, 0.0).astype(BF16)
        spread[4 * pair + 1] = jnp.where(low, pltpu.roll(first, 64, 1), 0.0).astype(BF16)
        spread[4 * pair + 2] = jnp.where(low, 0.0, pltpu.roll(second, 64, 1)).astype(BF16)
        spread[4 * pair + 3] = jnp.where(low, 0.0, second).astype(BF16)


def join_heads(spread, target):
    rows = target.shape[0]
    low = lax.broadcasted_iota(jnp.int32, (rows, 128), 1) < 64
    for pair in range(target.shape[1] // 256):
        parts = [spread(4 * pair + i).T for i in range(4)]
        target[:, pair * 256 : pair * 256 + 128] = jnp.where(low, parts[0], pltpu.roll(parts[1], 64, 1))
        target[:, pair * 256 + 128 : pair * 256 + 256] = jnp.where(low, pltpu.roll(parts[2], 64, 1), parts[3])


def mask_block(bias, length, place, block):
    rows = bias.shape[0]
    key_at = block * rows + lax.broadcasted_iota(jnp.int32, bias.shape, 0)
    query_at = place * rows + lax.broadcasted_iota(jnp.int32, bias.shape, 1)
    bias[...] = jnp.where((key_at <= query_at) & (key_at < length), 0.0, NEGATIVE)


def dot_right(left, right):
    return lax.dot_general(left, right, (((1,), (1,)), ((), ())), preferred_element_type=F32)


def dot_plain(left, right):
    return jnp.dot(left, right, preferred_element_type=F32)


def attend_kernel(
    n_ctx,
    length_ref,
    query,
    kv,
    d_block,
    gate_in,
    up_in,
    down_in,
    attended,
    log_total,
    kv_all,
    d_all,
    gate_out,
    up_out,
    down_out,
    spread,
    bias,
    peak,
    total,
    out_t,
    kv_send,
    kv_recv,
    d_send,
    d_recv,
    d_own,
    send_sem,
    recv_sem,
    pair_send,
    pair_recv,
    own_sem,
):
    chain = Chain(n_ctx)
    place = chain.place
    section = lax.axis_index("section")
    me, beside, across, opposite = corners()
    greet_mixed(
        chain,
        [{"fsdp": beside}, {"fsdp": across}, {"fsdp": opposite}, {"section": 1 - section}],
    )
    rows = query.shape[0]
    half_width = kv.shape[1] // 2

    def block_rows(block):
        return pl.ds(pl.multiple_of(block * rows, rows), rows)

    def upward(step, src):
        return along(
            src,
            kv_all.at[block_rows(place - step)],
            kv_send.at[step],
            kv_recv.at[step + 1],
            place + 1,
        )

    def arriving(step):
        at = kv_all.at[block_rows(place - step)]
        return along(at, at, kv_send.at[step], kv_recv.at[step], place)

    @pl.when(chain.has_next)
    def _():
        upward(0, kv).start()

    gather = SideGather(d_block, d_all, d_send, d_recv, d_own)
    gather.start()
    columns = Columns(
        1, (gate_in, up_in, down_in), (gate_out, up_out, down_out), send_sem, recv_sem, pair_send, pair_recv, own_sem
    )
    columns.start()
    kv_all[block_rows(place)] = kv[...]
    spread_heads(query, spread)
    peak[...] = jnp.full(peak.shape, NEGATIVE, F32)
    total[...] = jnp.zeros(total.shape, F32)
    out_t[...] = jnp.zeros(out_t.shape, F32)
    length = length_ref[0]
    scale = 64 ** (-0.5)

    def attend_block(block):
        mask_block(bias, length, place, block)
        for pair in range(half_width // 128):
            key = kv_all[block_rows(block), pair * 128 : pair * 128 + 128]
            value_t = kv_all[block_rows(block), half_width + pair * 128 : half_width + pair * 128 + 128].T
            for index in range(4):
                head = 4 * pair + index
                scores = dot_right(key, spread[head]) * scale + bias[...]
                before = peak[head]
                now = jnp.maximum(before, jnp.max(scores, axis=0, keepdims=True))
                weights = jnp.exp(scores - now)
                fade = jnp.exp(before - now)
                peak[head] = now
                total[head] = total[head] * fade + jnp.sum(weights, axis=0, keepdims=True)
                out_t[head] = out_t[head] * fade + dot_plain(value_t, weights.astype(BF16))

    attend_block(place)
    gather.relay()

    def step_on(step, carry):
        @pl.when(step <= place)
        def _():
            arriving(step).wait_recv()

            @pl.when(chain.has_next)
            def _():
                upward(step, kv_all.at[block_rows(place - step)]).start()

            attend_block(place - step)

        return carry

    lax.fori_loop(1, n_ctx, step_on, 0)
    join_heads(lambda head: out_t[head] / total[head], attended)
    for head in range(spread.shape[0]):
        log_total[head] = peak[head] + jnp.log(total[head])
    columns.relay()
    gather.finish()
    columns.finish()

    def settle(step, carry):
        @pl.when((step <= place) & chain.has_next)
        def _():
            upward(step, kv_all.at[block_rows(place - step)]).wait_send()

        return carry

    lax.fori_loop(0, n_ctx, settle, 0)


def attend(length, query, kv, d_block, gate, up, down, collective_id):
    n_ctx, count = lax.axis_size("ctx"), lax.axis_size("fsdp")
    rows, width = query.shape
    heads = width // 64
    dma = pltpu.SemaphoreType.DMA
    vmem = pl.BlockSpec(memory_space=pltpu.VMEM)
    hbm = pl.BlockSpec(memory_space=pl.ANY)
    column = jax.ShapeDtypeStruct((count * gate.shape[0], gate.shape[1] // count), gate.dtype)
    return pl.pallas_call(
        functools.partial(attend_kernel, n_ctx),
        out_shape=(
            jax.ShapeDtypeStruct((rows, width), F32),
            jax.ShapeDtypeStruct((heads, 1, rows), F32),
            jax.ShapeDtypeStruct((n_ctx * rows, kv.shape[1]), BF16),
            jax.ShapeDtypeStruct((count * rows, d_block.shape[1]), BF16),
            column,
            column,
            jax.ShapeDtypeStruct(down.shape, down.dtype),
        ),
        in_specs=[pl.BlockSpec(memory_space=pltpu.SMEM), vmem, vmem, vmem, hbm, hbm, hbm],
        out_specs=[vmem, vmem, vmem, vmem, hbm, hbm, hbm],
        scratch_shapes=[
            pltpu.VMEM((heads, rows, 128), BF16),
            pltpu.VMEM((rows, rows), F32),
            pltpu.VMEM((heads, 1, rows), F32),
            pltpu.VMEM((heads, 1, rows), F32),
            pltpu.VMEM((heads, 128, rows), F32),
            dma((n_ctx + 1,)),
            dma((n_ctx + 1,)),
            dma((4,)),
            dma((4,)),
            dma,
            dma((2, count)),
            dma((2, count)),
            dma((3, count)),
            dma((3, count)),
            dma((3,)),
        ],
        compiler_params=pltpu.CompilerParams(
            collective_id=collective_id, has_side_effects=True, vmem_limit_bytes=40 << 20
        ),
        cost_estimate=busy(50),
    )(length, query, kv, d_block, gate, up, down)


def attend_back_kernel(
    n_ctx,
    length_ref,
    query,
    kv_all,
    d_out,
    log_total,
    delta,
    blocks,
    d_query,
    d_kv,
    reduced_out,
    spread,
    d_spread,
    bias,
    d_query_t,
    term,
    leaving,
    coming,
    kv_send,
    kv_recv,
    beside_got,
    across_got,
    passed,
    passed_got,
    send_sem,
    recv_sem,
):
    chain = Chain(n_ctx)
    place = chain.place
    _, beside, across, _ = corners()
    greet_mixed(chain, [{"fsdp": beside}, {"fsdp": across}])
    rows = query.shape[0]
    half_width = kv_all.shape[1] // 2
    reduction = SideReduce(blocks, reduced_out, beside_got, across_got, passed, passed_got, send_sem, recv_sem)
    reduction.start()
    spread_heads(query, spread)
    spread_heads(d_out, d_spread)
    d_query_t[...] = jnp.zeros(d_query_t.shape, F32)
    length = length_ref[0]
    scale = 64 ** (-0.5)

    def downward(block):
        return along(leaving.at[block], coming.at[block], kv_send.at[block], kv_recv.at[block], place - 1)

    def step_on(block, carry):
        @pl.when(block <= place)
        def _():
            mask_block(bias, length, place, block)
            at = pl.ds(pl.multiple_of(block * rows, rows), rows)
            for pair in range(half_width // 128):
                lanes = slice(pair * 128, pair * 128 + 128)
                more = slice(half_width + pair * 128, half_width + pair * 128 + 128)
                key = kv_all[at, lanes]
                value = kv_all[at, more]
                key_t = key.T
                d_key = jnp.zeros((rows, 128), F32)
                d_value = jnp.zeros((rows, 128), F32)
                for index in range(4):
                    head = 4 * pair + index
                    scores = dot_right(key, spread[head]) * scale + bias[...]
                    prob = jnp.exp(scores - log_total[head])
                    d_prob = dot_right(value, d_spread[head])
                    d_scores = (prob * (d_prob - delta[head])).astype(BF16)
                    d_value = d_value + dot_plain(prob.astype(BF16), d_spread[head])
                    d_key = d_key + dot_plain(d_scores, spread[head])
                    d_query_t[head] = d_query_t[head] + dot_plain(key_t, d_scores)
                term[:, lanes] = d_key * scale
                term[:, more] = d_value

            @pl.when(chain.has_next)
            def _():
                along(
                    leaving.at[block], coming.at[block], kv_send.at[block], kv_recv.at[block], place
                ).wait_recv()
                term[...] = term[...] + coming[block].astype(F32)

            @pl.when(block < place)
            def _():
                leaving[block] = term[...].astype(BF16)
                downward(block).start()

            @pl.when(block == place)
            def _():
                d_kv[...] = term[...]

        @pl.when(block == 0)
        def _():
            reduction.relay()

        return carry

    lax.fori_loop(0, n_ctx, step_on, 0)
    join_heads(lambda head: d_query_t[head] * scale, d_query)
    reduction.finish()

    def settle(block, carry):
        @pl.when(block < place)
        def _():
            downward(block).wait_send()

        return carry

    lax.fori_loop(0, n_ctx, settle, 0)


def attend_back(length, query, kv_all, d_out, log_total, delta, blocks, collective_id):
    n_ctx = lax.axis_size("ctx")
    rows, width = query.shape
    heads = width // 64
    dma = pltpu.SemaphoreType.DMA
    vmem = pl.BlockSpec(memory_space=pltpu.VMEM)
    wide = jax.ShapeDtypeStruct((rows, width), F32)
    pair = pltpu.VMEM((2, rows // 2, blocks.shape[1]), BF16)
    return pl.pallas_call(
        functools.partial(attend_back_kernel, n_ctx),
        out_shape=(wide, jax.ShapeDtypeStruct((rows, kv_all.shape[1]), F32), wide),
        in_specs=[pl.BlockSpec(memory_space=pltpu.SMEM)] + [vmem] * 6,
        out_specs=[vmem] * 3,
        scratch_shapes=[
            pltpu.VMEM((heads, rows, 128), BF16),
            pltpu.VMEM((heads, rows, 128), BF16),
            pltpu.VMEM((rows, rows), F32),
            pltpu.VMEM((heads, 128, rows), F32),
            pltpu.VMEM((rows, kv_all.shape[1]), F32),
            pltpu.VMEM((n_ctx, rows, kv_all.shape[1]), BF16),
            pltpu.VMEM((n_ctx, rows, kv_all.shape[1]), BF16),
            dma((n_ctx,)),
            dma((n_ctx,)),
            pair,
            pair,
            pair,
            pair,
            dma((6,)),
            dma((6,)),
        ],
        compiler_params=pltpu.CompilerParams(
            collective_id=collective_id, has_side_effects=True, vmem_limit_bytes=56 << 20
        ),
        cost_estimate=busy(50),
    )(length, query, kv_all, d_out, log_total, delta, blocks)


def ffn_forward(residual, gain, w_gate, w_up, w_down):
    normed, inv_rms = norm_rows(residual)
    act = gathered((normed * gain).astype(BF16), 0)
    gate_pre = matmul(act, w_gate)
    up_pre = matmul(act, w_up)
    hidden = (jax.nn.silu(gate_pre) * up_pre).astype(BF16)
    return matmul(hidden, w_down).astype(BF16), (normed, inv_rms, act, gate_pre, up_pre, hidden)


def ffn_backward(d_all, kept, w_gate, w_up, w_down):
    _, _, act, gate_pre, up_pre, hidden = kept
    d_hidden = matmul_right(d_all, w_down)
    sigmoid = jax.nn.sigmoid(gate_pre)
    d_up = (d_hidden * gate_pre * sigmoid).astype(BF16)
    d_gate = (d_hidden * up_pre * sigmoid * (1.0 + gate_pre * (1.0 - sigmoid))).astype(BF16)
    terms = (matmul_right(d_gate, w_gate) + matmul_right(d_up, w_up)).astype(BF16)
    grads = (
        matmul_left(act, d_gate).astype(BF16),
        matmul_left(act, d_up).astype(BF16),
        matmul_left(hidden, d_all).astype(BF16),
    )
    return terms, grads


def ffn_norm_back(d_act, kept, gain):
    normed, inv_rms = kept[:2]
    return norm_back(d_act * gain, normed, inv_rms), jnp.sum(d_act * normed, axis=0)


def shards(
    inputs,
    cotangent,
    lengths,
    norm_gains,
    conv_in,
    conv_kernel,
    conv_out,
    attn_q,
    attn_k,
    attn_v,
    attn_out,
    head_gains,
    ffn_gate,
    ffn_up,
    ffn_down,
):
    micro, rows, width = inputs.shape
    section = lax.axis_index("section")
    group = lax.axis_index("fsdp")
    fsdp = lax.axis_size("fsdp")
    assert micro == lax.axis_size("section")
    head = head_gains.shape[1]
    q_width, kv_width = attn_q.shape[1], attn_k.shape[1]
    q_heads, kv_heads = q_width // head, kv_width // head
    positions = lax.axis_index("ctx") * rows + jnp.arange(rows)
    length = lax.dynamic_index_in_dim(lengths, group * micro + section, keepdims=False)
    mask = (positions < length).astype(F32)[:, None]

    def whole_rows(weight):
        half = weight.shape[0] // micro
        mine = lax.dynamic_slice_in_dim(weight, section * half, half, 0)
        return lax.all_gather(mine, ("fsdp", "section"), axis=0, tiled=True)

    part = ffn_gate.shape[1]
    in_full, out_full = mixer_weights(conv_in, conv_out, 2)
    gate1, up1, down1 = column_weights(ffn_gate[0], ffn_up[0], ffn_down[0], 0, 7)
    query_full, key_full, value_full, proj_full = (
        whole_rows(attn_q),
        whole_rows(attn_k),
        whole_rows(attn_v),
        whole_rows(attn_out),
    )

    x = lax.dynamic_index_in_dim(inputs, section, keepdims=False).astype(F32)
    normed0, inv0 = norm_rows(x)
    act1 = (normed0 * norm_gains[0]).astype(BF16)
    projected = matmul(act1, in_full)
    b_gate, c_gate, x_value = (
        projected[:, :width],
        projected[:, width : 2 * width],
        projected[:, 2 * width :],
    )
    b_product = (b_gate * x_value).astype(BF16)
    rim = passed_along(b_product[-2:], "ctx", 1)
    extended = jnp.concatenate([rim, b_product], axis=0).astype(F32)
    convolved = (
        conv_kernel[0] * extended[:-2]
        + conv_kernel[1] * extended[1:-1]
        + conv_kernel[2] * extended[2:]
    )
    z_low = (c_gate * convolved).astype(BF16)
    mixed = matmul(z_low, out_full)
    res1 = x + mixed
    terms1, kept1 = ffn_forward(res1, norm_gains[1], gate1, up1, down1)
    ffn1 = reduced(terms1, 1)
    h_low = (res1 + ffn1).astype(BF16)

    h = h_low.astype(F32)
    normed2, inv2 = norm_rows(h)
    act2 = (normed2 * norm_gains[2]).astype(BF16)
    q_normed, q_inv = norm_heads(matmul(act2, query_full), head)
    k_normed, k_inv = norm_heads(matmul(act2, key_full), head)
    q_gain = jnp.tile(head_gains[0], q_heads)
    k_gain = jnp.tile(head_gains[1], kv_heads)
    query = (q_normed * q_gain).astype(BF16)
    key = (k_normed * k_gain).astype(BF16)
    value = matmul(act2, value_full).astype(BF16)
    d_sum_low = (lax.dynamic_index_in_dim(cotangent, section, keepdims=False).astype(F32) * mask).astype(BF16)
    attended, log_total, kv_all, d_sum_all, gate2, up2, down2 = attend(
        length.reshape(1),
        query,
        jnp.concatenate([key, value], axis=1),
        d_sum_low,
        ffn_gate[0],
        ffn_up[0],
        ffn_down[0],
        3,
    )
    attended_low = attended.astype(BF16)
    attn_rows = matmul(attended_low, proj_full)
    res2 = h + attn_rows
    terms2, kept2 = ffn_forward(res2, norm_gains[3], gate2, up2, down2)

    d_sum = d_sum_low.astype(F32)
    d_terms2, grads2 = ffn_backward(d_sum_all, kept2, gate2, up2, down2)
    half = part // 2
    strip = half // lax.axis_size("ctx")

    def column_half(which):
        pieces = jnp.stack(grads2[:2]).reshape(2, fsdp, 2, half // strip, strip, -1)
        pieces = lax.dynamic_index_in_dim(pieces, which, 2, keepdims=False)
        return pieces.transpose(2, 1, 0, 3, 4).reshape(2 * fsdp * half, -1)

    def down_half(which):
        size = grads2[2].shape[0] // 2
        return lax.dynamic_slice_in_dim(grads2[2], which * size, size, 0)

    d_act3, got_gu, got_down = reduced_swapping(
        d_terms2, column_half(1 - section), down_half(1 - section), 8
    )
    d_ffn, gain3 = ffn_norm_back(d_act3, kept2, norm_gains[3])
    d_res2 = d_sum + d_ffn
    d_attn = d_res2.astype(BF16)
    grad_proj = matmul_left(attended_low, d_attn)
    d_att = matmul_right(d_attn, proj_full).astype(BF16)
    delta = jnp.sum((d_att.astype(F32) * attended).reshape(rows, q_heads, head), axis=-1)
    d_query, d_kv, ffn2 = attend_back(
        length.reshape(1), query, kv_all, d_att, log_total, delta.T.reshape(q_heads, 1, rows), terms2, 4
    )
    result = (res2 + ffn2) * mask

    def square(values):
        return jnp.sum(mask * values * values, axis=0, keepdims=True)

    squares = [square(v) for v in (x, mixed, ffn1, h, attn_rows, res2, ffn2, result)]
    second_gu, second_down = (
        lax.psum_scatter(
            (mine.astype(F32) + got.astype(F32)).astype(BF16), "ctx", scatter_dimension=0, tiled=True
        )
        for mine, got in ((column_half(section), got_gu), (down_half(section), got_down))
    )
    d_qn = rounded(d_query)
    grad_qgain = jnp.sum(jnp.sum(d_qn * q_normed, axis=0).reshape(q_heads, head), axis=0)
    d_qpre = norm_heads_back(d_qn * q_gain, q_normed, q_inv, head).astype(BF16)
    d_kn = rounded(d_kv[:, :kv_width])
    grad_kgain = jnp.sum(jnp.sum(d_kn * k_normed, axis=0).reshape(kv_heads, head), axis=0)
    d_kpre = norm_heads_back(d_kn * k_gain, k_normed, k_inv, head).astype(BF16)
    d_vpre = d_kv[:, kv_width:].astype(BF16)
    d_act2 = (
        matmul_right(d_qpre, query_full)
        + matmul_right(d_kpre, key_full)
        + matmul_right(d_vpre, value_full)
    )
    gain2 = jnp.sum(d_act2 * normed2, axis=0)
    d_h_low = (d_res2 + norm_back(d_act2 * norm_gains[2], normed2, inv2)).astype(BF16)

    d_h_all, second_gu = gathered_swapped(d_h_low, second_gu.reshape(fsdp, 2 * strip, -1), 5)
    second_gu = lax.all_gather(second_gu, "ctx", axis=0)
    second_down = lax.all_gather(second_down, "ctx", axis=0, tiled=True)
    d_terms1, grads1 = ffn_backward(d_h_all, kept1, gate1, up1, down1)
    d_ffn1, gain1 = ffn_norm_back(reduced(d_terms1, 1), kept1, norm_gains[1])
    d_ffn1, second_gu = lax.optimization_barrier((d_ffn1, second_gu))
    d_res1 = d_h_low.astype(F32) + d_ffn1
    d_mixed = d_res1.astype(BF16)
    grad_out = matmul_left(z_low, d_mixed)
    d_z = matmul_right(d_mixed, out_full)
    d_cgate = d_z * convolved
    d_conv = d_z * c_gate
    grad_kernel = jnp.stack(
        [
            jnp.sum(d_conv * extended[:-2], axis=0),
            jnp.sum(d_conv * extended[1:-1], axis=0),
            jnp.sum(d_conv * extended[2:], axis=0),
        ]
    )
    d_extended = (
        jnp.pad(d_conv * conv_kernel[0], ((0, 2), (0, 0)))
        + jnp.pad(d_conv * conv_kernel[1], ((1, 1), (0, 0)))
        + jnp.pad(d_conv * conv_kernel[2], ((2, 0), (0, 0)))
    )
    from_next, second_down = lax.optimization_barrier(
        (passed_along(d_extended[:2], "ctx", -1), second_down)
    )
    d_bproduct = rounded(d_extended[2:] + jnp.pad(from_next, ((rows - 2, 0), (0, 0))))
    d_projected = jnp.concatenate(
        [d_bproduct * x_value, d_cgate, d_bproduct * b_gate], axis=1
    ).astype(BF16)
    d_act1 = matmul_right(d_projected, in_full)
    gain0 = jnp.sum(d_act1 * normed0, axis=0)
    d_x = (d_res1 + norm_back(d_act1 * norm_gains[0], normed0, inv0)).astype(BF16)

    y_low = result.astype(BF16)
    is_first = section == 0
    other_end = swapped(jnp.where(is_first, y_low, d_x), "section")
    ends = jnp.where(is_first, jnp.stack([d_x, other_end]), jnp.stack([other_end, y_low]))[None]

    grad_parts = [
        matmul_left(act1, d_projected[:, i * width : (i + 1) * width]).astype(BF16) for i in range(3)
    ]
    mixers = [
        matmul_left(act2, d_qpre).astype(BF16),
        matmul_left(act2, jnp.concatenate([d_kpre, d_vpre], axis=1)).astype(BF16),
        grad_proj.astype(BF16),
    ] + grad_parts + [grad_out.astype(BF16)]

    small = jnp.concatenate(
        [gain0[None], gain1[None], gain2[None], gain3[None], grad_kernel]
        + [jnp.pad(grad[None], ((0, 0), (0, width - head))) for grad in (grad_qgain, grad_kgain)]
        + [jnp.zeros((7, width), F32)]
        + squares
        + [jnp.zeros((8, width), F32)]
    ).astype(BF16)
    small = small.reshape(2, 16, width)
    gu_sum, down_sum, rest_sum = summed_gradients(
        grads1,
        mixers,
        small,
        second_gu.reshape(-1, fsdp, 2, strip, second_gu.shape[-1]),
        second_down,
    )
    rest_sum = rest_sum.astype(F32)

    def block(index):
        rows_at = slice(index * half, (index + 1) * half)
        return rest_sum[:, rows_at].reshape(2 * half, width)

    attn_blocks = [block(i) for i in range(3)]
    conv_blocks = [block(3 + i) for i in range(4)]
    small_sum = rest_sum[0, 7 * half : 7 * half + 9]
    cut = width // fsdp
    mine = lax.dynamic_slice_in_dim(small_sum[:7], group * cut, cut, 1)
    head_cut = head // fsdp
    heads = lax.dynamic_slice_in_dim(small_sum[7:9], group * head_cut, head_cut, 1)
    square_cut = len(squares) // fsdp
    square_sum = jnp.sum(
        lax.dynamic_slice_in_dim(rest_sum[1, 7 * half : 7 * half + 8], group * square_cut, square_cut, 0), axis=1
    )
    token_total = jnp.sum(lengths).astype(F32) * width
    rms = jnp.sqrt(square_sum / token_total)
    return (
        ends,
        mine[:3],
        mine[3],
        jnp.concatenate(conv_blocks[:3], axis=1),
        mine[4:7],
        conv_blocks[3],
        attn_blocks[0],
        attn_blocks[1][:, :kv_width],
        attn_blocks[1][:, kv_width:],
        attn_blocks[2],
        heads,
        gu_sum[0][None].astype(F32),
        gu_sum[1][None].astype(F32),
        down_sum[None].astype(F32),
        rms,
    )


def solution(mesh):
    return jax.shard_map(
        shards,
        mesh=mesh,
        in_specs=(
            P("fsdp", "ctx", None),
            P("fsdp", "ctx", None),
            P(),
            P(),
            P("fsdp", None),
            P(),
            P("fsdp", None),
            P("fsdp", None),
            P("fsdp", None),
            P("fsdp", None),
            P("fsdp", None),
            P(),
            P("section", "fsdp", None),
            P("section", "fsdp", None),
            P("section", "fsdp", None),
        ),
        out_specs=(
            P("section", "fsdp", "ctx", None),
            P(None, "fsdp"),
            P("fsdp"),
            P("fsdp", None),
            P(None, "fsdp"),
            P("fsdp", None),
            P("fsdp", None),
            P("fsdp", None),
            P("fsdp", None),
            P("fsdp", None),
            P(None, "fsdp"),
            P("section", "fsdp", None),
            P("section", "fsdp", None),
            P("section", "fsdp", None),
            P("fsdp"),
        ),
        check_vma=False,
    )
```

```python
import functools

import jax
import jax.numpy as jnp
from jax import lax
from jax.experimental import pallas as pl
from jax.experimental.pallas import tpu as pltpu
from jax.sharding import PartitionSpec as P

EPSILON = 1e-05
NEGATIVE = -1e30
MESH = pl.DeviceIdType.MESH
F32 = jnp.float32
BF16 = jnp.bfloat16


def passed_along(block, axis, distance):
    devices = range(lax.axis_size(axis))
    route = [(i - distance, i) for i in devices if i - distance in devices]
    return lax.ppermute(block, axis, route)


def swapped(block, axis):
    return lax.ppermute(block, axis, [(0, 1), (1, 0)])


def rounded(values):
    return lax.optimization_barrier(values.astype(BF16)).astype(F32)


def matmul(left_op, right_op):
    return jnp.dot(left_op, right_op, preferred_element_type=F32)


def matmul_left(left_op, right_op):
    return lax.dot_general(left_op, right_op, (((0,), (0,)), ((), ())), preferred_element_type=F32)


def matmul_right(left_op, right_op):
    return lax.dot_general(left_op, right_op, (((1,), (1,)), ((), ())), preferred_element_type=F32)


def norm_rows(values):
    inv_rms = lax.rsqrt(jnp.mean(values * values, axis=-1, keepdims=True) + EPSILON)
    return (values * inv_rms, inv_rms)


def norm_back(dnormed, normed, inv_rms):
    return inv_rms * dnormed - normed * inv_rms * jnp.mean(dnormed * normed, axis=-1, keepdims=True)


def head_sums(values, head):
    heads = values.shape[1] // head
    owner = (jnp.arange(values.shape[1])[:, None] // head == jnp.arange(heads)[None, :]).astype(F32)
    sums = jnp.dot(values, owner, precision=lax.Precision.HIGHEST, preferred_element_type=F32)
    return jnp.dot(sums, owner.T, precision=lax.Precision.HIGHEST, preferred_element_type=F32)


def norm_heads(values, head):
    inv_rms = lax.rsqrt(head_sums(values * values, head) / head + EPSILON)
    return (values * inv_rms, inv_rms)


def norm_heads_back(dnormed, normed, inv_rms, head):
    return inv_rms * dnormed - normed * inv_rms * (head_sums(dnormed * normed, head) / head)


def busy(microseconds):
    return pl.CostEstimate(flops=int(microseconds), bytes_accessed=1 << 16, transcendentals=0)


def corners():
    me = lax.axis_index("fsdp")
    beside = me + 1 - 2 * lax.rem(me, 2)
    across = lax.rem(me + 2, 4)
    return me, beside, across, lax.rem(beside + 2, 4)


def greet_sides():
    _, beside, across, _ = corners()
    barrier = pltpu.get_barrier_semaphore()
    for target in (beside, across):
        pl.semaphore_signal(barrier, inc=1, device_id={"fsdp": target}, device_id_type=MESH)
    pl.semaphore_wait(barrier, 2)


def to_side(src, dst, send_sem, recv_sem, target):
    return pltpu.make_async_remote_copy(
        src_ref=src,
        dst_ref=dst,
        send_sem=send_sem,
        recv_sem=recv_sem,
        device_id={"fsdp": target},
        device_id_type=MESH,
    )


class SideGather:
    def __init__(self, block, whole, send_sem, recv_sem, own_sem):
        me, beside, across, _ = corners()
        rows = block.shape[0]
        half = rows // 2

        def part(owner, start, size):
            return whole.at[pl.ds(pl.multiple_of(owner * rows + start, half), size)]

        self.first = to_side(block, part(me, 0, rows), send_sem.at[0], recv_sem.at[0], beside)
        self.second = to_side(block, part(me, 0, rows), send_sem.at[1], recv_sem.at[1], across)
        at = part(beside, 0, half)
        self.third = to_side(at, at, send_sem.at[2], recv_sem.at[2], across)
        at = part(across, half, half)
        self.fourth = to_side(at, at, send_sem.at[3], recv_sem.at[3], beside)
        self.own = pltpu.make_async_copy(block, part(me, 0, rows), own_sem)

    def start(self):
        self.first.start()
        self.second.start()
        self.own.start()

    def relay(self):
        self.first.wait_recv()
        self.third.start()
        self.second.wait_recv()
        self.fourth.start()

    def finish(self):
        self.own.wait()
        self.first.wait_send()
        self.second.wait_send()
        self.third.wait()
        self.fourth.wait()


def gather_kernel(block, whole, send_sem, recv_sem, own_sem):
    greet_sides()
    gather = SideGather(block, whole, send_sem, recv_sem, own_sem)
    gather.start()
    gather.relay()
    gather.finish()


def gathered(array, collective_id):
    rows, width = array.shape
    assert lax.axis_size("fsdp") == 4
    dma = pltpu.SemaphoreType.DMA
    return pl.pallas_call(
        gather_kernel,
        out_shape=jax.ShapeDtypeStruct((4 * rows, width), array.dtype),
        in_specs=[pl.BlockSpec(memory_space=pltpu.VMEM)],
        out_specs=pl.BlockSpec(memory_space=pltpu.VMEM),
        scratch_shapes=[dma((4,)), dma((4,)), dma],
        compiler_params=pltpu.CompilerParams(
            collective_id=collective_id, has_side_effects=True, vmem_limit_bytes=8 << 20
        ),
        cost_estimate=busy(25),
    )(array)


def gather_swap_kernel(block, pieces, whole, swapped_out, send_sem, recv_sem, own_sem, cross_send, cross_recv, keep_sem):
    me, beside, across, opposite = corners()
    barrier = pltpu.get_barrier_semaphore()
    for target in (beside, across, opposite):
        pl.semaphore_signal(barrier, inc=1, device_id={"fsdp": target}, device_id_type=MESH)
    pl.semaphore_wait(barrier, 3)
    gather = SideGather(block, whole, send_sem, recv_sem, own_sem)
    gather.start()
    crossing = []
    for step in range(1, 4):
        target = lax.rem(me + step, 4)
        crossing.append(
            to_side(pieces.at[target], swapped_out.at[me], cross_send.at[step], cross_recv.at[step], target)
        )
        crossing[-1].start()
    keep = pltpu.make_async_copy(pieces.at[me], swapped_out.at[me], keep_sem)
    keep.start()
    gather.relay()
    gather.finish()
    keep.wait()
    for copy in crossing:
        copy.wait()


def gathered_swapped(array, pieces, collective_id):
    rows, width = array.shape
    dma = pltpu.SemaphoreType.DMA
    vmem = pl.BlockSpec(memory_space=pltpu.VMEM)
    hbm = pl.BlockSpec(memory_space=pl.ANY)
    return pl.pallas_call(
        gather_swap_kernel,
        out_shape=(
            jax.ShapeDtypeStruct((4 * rows, width), array.dtype),
            jax.ShapeDtypeStruct(pieces.shape, pieces.dtype),
        ),
        in_specs=[vmem, hbm],
        out_specs=[vmem, hbm],
        scratch_shapes=[dma((4,)), dma((4,)), dma, dma((4,)), dma((4,)), dma],
        compiler_params=pltpu.CompilerParams(
            collective_id=collective_id, has_side_effects=True, vmem_limit_bytes=8 << 20
        ),
        cost_estimate=busy(25),
    )(array, pieces)


class SideReduce:
    def __init__(self, blocks, total, beside_got, across_got, passed, passed_got, send_sem, recv_sem):
        self.refs = blocks, total, beside_got, across_got, passed, passed_got
        me, beside, across, opposite = corners()
        self.me, self.beside, self.across = me, beside, across
        self.copies = []
        for index, (turn, target, got) in enumerate(((0, beside, beside_got), (1, across, across_got))):
            for slot, owner in ((1, opposite), (0, target)):
                self.copies.append(
                    to_side(
                        blocks.at[self.part(owner, turn)],
                        got.at[slot],
                        send_sem.at[2 * index + slot],
                        recv_sem.at[2 * index + slot],
                        target,
                    )
                )
        self.onward = [
            to_side(passed.at[turn], passed_got.at[turn], send_sem.at[4 + turn], recv_sem.at[4 + turn], owner)
            for turn, owner in ((0, across), (1, beside))
        ]

    def part(self, owner, turn):
        half = self.refs[1].shape[0] // 2
        return pl.ds(pl.multiple_of(owner * 2 * half + turn * half, half), half)

    def start(self):
        for index in (0, 2, 1, 3):
            self.copies[index].start()

    def relay(self):
        blocks, _, beside_got, across_got, passed, _ = self.refs
        for turn, owner, index, got in ((0, self.across, 0, beside_got), (1, self.beside, 2, across_got)):
            self.copies[index].wait_recv()
            passed[turn] = (blocks[self.part(owner, turn)].astype(F32) + got[1].astype(F32)).astype(BF16)
            self.onward[turn].start()

    def finish(self):
        blocks, total, beside_got, across_got, _, passed_got = self.refs
        half = total.shape[0] // 2
        for turn, index, got in ((0, 1, beside_got), (1, 3, across_got)):
            self.copies[index].wait_recv()
            total[pl.ds(turn * half, half)] = blocks[self.part(self.me, turn)].astype(F32) + got[0].astype(F32)
        for turn in range(2):
            self.onward[turn].wait_recv()
            at = pl.ds(turn * half, half)
            total[at] = total[at] + passed_got[turn].astype(F32)
        for copy in self.copies + self.onward:
            copy.wait_send()


def reduce_kernel(blocks, total, beside_got, across_got, passed, passed_got, send_sem, recv_sem):
    greet_sides()
    reduction = SideReduce(blocks, total, beside_got, across_got, passed, passed_got, send_sem, recv_sem)
    reduction.start()
    reduction.relay()
    reduction.finish()


def reduce_pair_kernel(
    blocks,
    give_a,
    give_b,
    total,
    got_a,
    got_b,
    beside_got,
    across_got,
    passed,
    passed_got,
    send_sem,
    recv_sem,
    pair_send,
    pair_recv,
):
    other = {"section": 1 - lax.axis_index("section")}
    _, beside, across, _ = corners()
    barrier = pltpu.get_barrier_semaphore()
    for target in ({"fsdp": beside}, {"fsdp": across}, other):
        pl.semaphore_signal(barrier, inc=1, device_id=target, device_id_type=MESH)
    pl.semaphore_wait(barrier, 3)
    reduction = SideReduce(blocks, total, beside_got, across_got, passed, passed_got, send_sem, recv_sem)
    reduction.start()
    pairs = [
        pltpu.make_async_remote_copy(
            src_ref=src,
            dst_ref=dst,
            send_sem=pair_send.at[index],
            recv_sem=pair_recv.at[index],
            device_id=other,
            device_id_type=MESH,
        )
        for index, (src, dst) in enumerate(((give_a, got_a), (give_b, got_b)))
    ]
    for copy in pairs:
        copy.start()
    reduction.relay()
    reduction.finish()
    for copy in pairs:
        copy.wait()


def reduced_swapping(partial, give_a, give_b, collective_id):
    rows, width = partial.shape[0] // 4, partial.shape[1]
    dma = pltpu.SemaphoreType.DMA
    pair = pltpu.VMEM((2, rows // 2, width), BF16)
    vmem = pl.BlockSpec(memory_space=pltpu.VMEM)
    hbm = pl.BlockSpec(memory_space=pl.ANY)
    return pl.pallas_call(
        reduce_pair_kernel,
        out_shape=(
            jax.ShapeDtypeStruct((rows, width), F32),
            jax.ShapeDtypeStruct(give_a.shape, BF16),
            jax.ShapeDtypeStruct(give_b.shape, BF16),
        ),
        in_specs=[vmem, hbm, hbm],
        out_specs=[vmem, hbm, hbm],
        scratch_shapes=[pair, pair, pair, pair, dma((6,)), dma((6,)), dma((2,)), dma((2,))],
        compiler_params=pltpu.CompilerParams(
            collective_id=collective_id, has_side_effects=True, vmem_limit_bytes=16 << 20
        ),
        cost_estimate=busy(25),
    )(partial.astype(BF16), give_a, give_b)


def reduced(partial, collective_id):
    rows, width = partial.shape[0] // 4, partial.shape[1]
    assert lax.axis_size("fsdp") == 4
    dma = pltpu.SemaphoreType.DMA
    pair = pltpu.VMEM((2, rows // 2, width), BF16)
    return pl.pallas_call(
        reduce_kernel,
        out_shape=jax.ShapeDtypeStruct((rows, width), F32),
        in_specs=[pl.BlockSpec(memory_space=pltpu.VMEM)],
        out_specs=pl.BlockSpec(memory_space=pltpu.VMEM),
        scratch_shapes=[pair, pair, pair, pair, dma((6,)), dma((6,))],
        compiler_params=pltpu.CompilerParams(
            collective_id=collective_id, has_side_effects=True, vmem_limit_bytes=16 << 20
        ),
        cost_estimate=busy(25),
    )(partial.astype(BF16))


def tail_kernel(
    counts,
    gate_in,
    up_in,
    down_in,
    query_in,
    kv_in,
    proj_in,
    conv_b_in,
    conv_c_in,
    conv_x_in,
    conv_o_in,
    small_in,
    second_gu_in,
    second_down_in,
    gu_out,
    down_out,
    rest_out,
    a_own,
    a_other,
    a_sum,
    a_done,
    b_own,
    b_other,
    b_sum,
    b_done,
    c_own,
    c_other,
    c_got,
    own_sem,
    pair_send,
    pair_recv,
    c_own_sem,
    c_pair_send,
    c_pair_recv,
    c_send,
    c_recv,
    a_up_send,
    a_up_recv,
    a_back_send,
    a_back_recv,
    a_out_send,
    b_up_send,
    b_up_recv,
    b_back_send,
    b_back_recv,
    b_out_send,
    b_keep_sem,
    gu_recv,
    down_recv,
    rest_recv,
    second_send,
    second_recv,
):
    n_ctx, n_fsdp = counts
    section = lax.axis_index("section")
    place = lax.axis_index("ctx")
    group = lax.axis_index("fsdp")
    other = 1 - section
    a_chunks, a_rows, a_width = a_own.shape
    b_chunks, b_rows, b_width = b_own.shape
    half = gate_in.shape[0] // n_fsdp // 2
    subs = half // a_rows
    per_kind = n_fsdp * subs
    down_half = down_in.shape[0] // 2
    down_chunks = down_half // b_rows
    c_rows = c_own.shape[1]
    mixers = (query_in, kv_in, proj_in, conv_b_in, conv_c_in, conv_x_in, conv_o_in)
    n_mix = len(mixers)
    cut = 3 * half // b_rows
    c_parts = ((0, cut), (cut, c_rows // b_rows))
    ticks = a_chunks
    tail = 2 * (n_ctx - 1)

    barrier = pltpu.get_barrier_semaphore()
    for step in range(1, 2 * n_fsdp):
        flat = lax.rem(section * n_fsdp + group + step, 2 * n_fsdp)
        pl.semaphore_signal(
            barrier,
            inc=1,
            device_id={"section": flat // n_fsdp, "fsdp": lax.rem(flat, n_fsdp)},
            device_id_type=MESH,
        )

    @pl.when(place > 0)
    def _():
        pl.semaphore_signal(barrier, inc=1, device_id={"ctx": place - 1}, device_id_type=MESH)

    @pl.when(place < n_ctx - 1)
    def _():
        pl.semaphore_signal(barrier, inc=1, device_id={"ctx": place + 1}, device_id_type=MESH)

    at_edge = (place == 0) | (place == n_ctx - 1)

    @pl.when(at_edge)
    def _():
        pl.semaphore_wait(barrier, 2 * n_fsdp)

    @pl.when(jnp.logical_not(at_edge))
    def _():
        pl.semaphore_wait(barrier, 2 * n_fsdp + 1)

    def half_rows(owner, which):
        return pl.ds(pl.multiple_of(owner * (2 * half) + which * half, half), half)

    a_part, b_part = a_rows // 2, b_width // 2

    def a_at(buffer, k, way):
        return buffer.at[k, pl.ds(way * a_part, a_part)]

    def b_at(buffer, k, way):
        return buffer.at[k, :, pl.ds(way * b_part, b_part)]

    def opening(k, way):
        copies = []
        kind, rest = divmod(k, per_kind)
        owner, sub = divmod(rest, subs)
        source = (gate_in, up_in)[kind]
        spots = []
        for which in (section, other):
            start = owner * (2 * half) + which * half + sub * a_rows + way * a_part
            spots.append(source.at[pl.ds(pl.multiple_of(start, a_part), a_part)])
        spot = 2 * k + way
        copies.append((spots, a_at(a_own, k, way), a_at(a_other, k, way), spot))
        if k < down_chunks:
            spots = [
                down_in.at[
                    pl.ds(pl.multiple_of(which * down_half + k * b_rows, b_rows), b_rows),
                    pl.ds(way * b_part, b_part),
                ]
                for which in (section, other)
            ]
            copies.append((spots, b_at(b_own, k, way), b_at(b_other, k, way), 2 * a_chunks + spot))
        for (mine, theirs), own_dst, other_dst, spot in copies:
            pltpu.make_async_copy(mine, own_dst, own_sem.at[spot]).start()
            pltpu.make_async_remote_copy(
                src_ref=theirs,
                dst_ref=other_dst,
                send_sem=pair_send.at[spot],
                recv_sem=pair_recv.at[spot],
                device_id={"section": other},
                device_id_type=MESH,
            ).start()

    for k in range(a_chunks):
        for way in range(2):
            opening(k, way)
    c_local, c_pair = ([], []), ([], [])
    for kind, source in enumerate(mixers):
        part = 0 if kind < 3 else 1
        for owner in range(n_fsdp):
            index = owner * (n_mix + 1) + kind
            place_at = pl.ds(kind * half, half)
            c_local[part].append(
                pltpu.make_async_copy(
                    source.at[half_rows(owner, section)], c_own.at[owner, place_at], c_own_sem.at[index]
                )
            )
            c_pair[part].append(
                pltpu.make_async_remote_copy(
                    src_ref=source.at[half_rows(owner, other)],
                    dst_ref=c_other.at[owner, place_at],
                    send_sem=c_pair_send.at[index],
                    recv_sem=c_pair_recv.at[index],
                    device_id={"section": other},
                    device_id_type=MESH,
                )
            )
    for owner in range(n_fsdp):
        small_at = pl.ds(n_mix * half, c_rows - n_mix * half)
        index = owner * (n_mix + 1) + n_mix
        c_local[1].append(
            pltpu.make_async_copy(small_in.at[section], c_own.at[owner, small_at], c_own_sem.at[index])
        )
        c_pair[1].append(
            pltpu.make_async_remote_copy(
                src_ref=small_in.at[other],
                dst_ref=c_other.at[owner, small_at],
                send_sem=c_pair_send.at[index],
                recv_sem=c_pair_recv.at[index],
                device_id={"section": other},
                device_id_type=MESH,
            )
        )
    for part in range(2):
        for copy in c_pair[part]:
            copy.start()
        for copy in c_local[part]:
            copy.start()
    b_own[b_chunks - 1] = jnp.zeros((b_rows, b_width), BF16)
    _, beside, across, opposite = corners()

    def span(first, last):
        return pl.ds(first * b_rows, (last - first) * b_rows)

    def mixer_spans(part):
        first, last = c_parts[part]
        middle = (first + last) // 2
        return (first, middle, beside, across), (middle, last, across, beside)

    def mixer_copies(part):
        opening, onward = [], []
        for turn, (first, last, near, far) in enumerate(mixer_spans(part)):
            at = span(first, last)
            for slot, owner in ((0, opposite), (1, near)):
                opening.append(
                    to_side(
                        c_own.at[owner, at],
                        c_got.at[slot, at],
                        c_send.at[part, 3 * turn + slot],
                        c_recv.at[part, 3 * turn + slot],
                        near,
                    )
                )
            onward.append(
                to_side(
                    c_own.at[far, at],
                    c_got.at[2, at],
                    c_send.at[part, 3 * turn + 2],
                    c_recv.at[part, 3 * turn + 2],
                    far,
                )
            )
        return opening, onward

    def mixer_sum(part, owner):
        kinds = range(3) if part == 0 else range(3, n_mix + 1)
        first, last = c_parts[part]
        for kind in kinds:
            size = half if kind < n_mix else c_rows - n_mix * half
            at = c_own.at[owner, pl.ds(kind * half, size)]
            index = owner * (n_mix + 1) + kind
            pltpu.make_async_copy(at, at, c_own_sem.at[index]).wait()
            pltpu.make_async_copy(at, at, c_pair_recv.at[index]).wait()

        def add(index, carry):
            at = pl.ds(pl.multiple_of(index * b_rows, b_rows), b_rows)
            c_own[owner, at] = (c_own[owner, at].astype(F32) + c_other[owner, at].astype(F32)).astype(BF16)
            return carry

        lax.fori_loop(first, last, add, 0)

    def mixer_out(part):
        opening, _ = mixer_copies(part)
        for index in (0, 2, 1, 3):
            opening[index].start()

    def mixer_on(part):
        opening, onward = mixer_copies(part)
        for turn, (first, last, near, far) in enumerate(mixer_spans(part)):
            opening[2 * turn].wait_recv()

            def add(index, carry, far=far):
                at = pl.ds(pl.multiple_of(index * b_rows, b_rows), b_rows)
                c_own[far, at] = (c_own[far, at].astype(F32) + c_got[0, at].astype(F32)).astype(BF16)
                return carry

            lax.fori_loop(first, last, add, 0)
            onward[turn].start()

    def mixer_in(part):
        opening, onward = mixer_copies(part)
        for turn in range(2):
            opening[2 * turn + 1].wait_recv()
            onward[turn].wait_recv()
        first, last = c_parts[part]

        def add(index, carry):
            at = pl.ds(pl.multiple_of(index * b_rows, b_rows), b_rows)
            total = c_own[group, at].astype(F32) + c_got[1, at].astype(F32) + c_got[2, at].astype(F32)
            b_own[down_chunks + index] = total.astype(BF16)
            return carry

        lax.fori_loop(first, last, add, 0)

    strip = half // n_ctx

    def second_copies(remote):
        for index in range(n_ctx * n_fsdp * 2):
            source, kind = index // 2, index % 2
            turn, owner = source // n_fsdp, source % n_fsdp
            src = second_gu_in.at[turn, owner, kind]
            dst = gu_out.at[
                kind,
                pl.ds(pl.multiple_of(section * half + turn * strip, strip), strip),
                pl.ds(owner * a_width, a_width),
            ]
            if remote:
                pltpu.make_async_remote_copy(
                    src_ref=src,
                    dst_ref=dst,
                    send_sem=second_send.at[0],
                    recv_sem=second_recv,
                    device_id={"section": 1},
                    device_id_type=MESH,
                ).start()
            else:
                pltpu.make_async_copy(src, dst, second_send.at[0]).start()

    def second_start():
        down_at = down_out.at[pl.ds(pl.multiple_of(section * down_half, b_rows), down_half)]

        @pl.when(section == 1)
        def _():
            second_copies(False)
            pltpu.make_async_copy(second_down_in, down_at, second_send.at[1]).start()

        @pl.when(section == 0)
        def _():
            second_copies(True)
            pltpu.make_async_remote_copy(
                src_ref=second_down_in,
                dst_ref=down_at,
                send_sem=second_send.at[1],
                recv_sem=down_recv,
                device_id={"section": 1},
                device_id_type=MESH,
            ).start()

    def a_target(k, way):
        kind = k // per_kind
        rest = lax.rem(k, per_kind)
        owner = rest // subs
        sub = lax.rem(rest, subs)
        start = section * half + sub * a_rows + way * a_part
        spot = gu_out.at[
            kind,
            pl.ds(pl.multiple_of(start, a_part), a_part),
            pl.ds(pl.multiple_of(group * a_width, 128), a_width),
        ]
        return kind, owner, spot

    def hand_out(k, way):
        kind, owner, spot = a_target(k, way)
        is_mine = (section == 0) & (group == owner)
        slot = 2 * k + way
        a_ref, b_ref = a_at(a_done, k, way), b_at(b_done, k, way)
        lanes_at = pl.ds(way * b_part, b_part)

        @pl.when(is_mine)
        def _():
            pltpu.make_async_copy(a_ref, spot, a_out_send.at[slot]).start()

        @pl.when(jnp.logical_not(is_mine))
        def _():
            pltpu.make_async_remote_copy(
                src_ref=a_ref,
                dst_ref=spot,
                send_sem=a_out_send.at[slot],
                recv_sem=gu_recv.at[kind, section * n_fsdp + group],
                device_id={"section": 0, "fsdp": owner},
                device_id_type=MESH,
            ).start()

        @pl.when(k < down_chunks)
        def _():
            at = down_out.at[pl.ds(pl.multiple_of(section * down_half + k * b_rows, b_rows), b_rows), lanes_at]

            @pl.when(section == 0)
            def _():
                pltpu.make_async_copy(b_ref, at, b_out_send.at[slot]).start()

            @pl.when(section == 1)
            def _():
                pltpu.make_async_remote_copy(
                    src_ref=b_ref,
                    dst_ref=at,
                    send_sem=b_out_send.at[slot],
                    recv_sem=down_recv,
                    device_id={"section": 0},
                    device_id_type=MESH,
                ).start()

        @pl.when(k >= down_chunks)
        def _():
            at = rest_out.at[
                section, pl.ds(pl.multiple_of((k - down_chunks) * b_rows, b_rows), b_rows), lanes_at
            ]
            pltpu.make_async_copy(b_ref, at, b_keep_sem.at[slot]).start()
            pltpu.make_async_remote_copy(
                src_ref=b_ref,
                dst_ref=at,
                send_sem=b_out_send.at[slot],
                recv_sem=rest_recv,
                device_id={"section": other},
                device_id_type=MESH,
            ).start()

    def chain_copies(k, way, target, buffers, sems):
        slot = 2 * k + way
        return [
            pltpu.make_async_remote_copy(
                src_ref=at,
                dst_ref=at,
                send_sem=send.at[slot],
                recv_sem=recv.at[slot],
                device_id={"ctx": target},
                device_id_type=MESH,
            )
            for at, (send, recv) in zip((a_at(buffers[0], k, way), b_at(buffers[1], k, way)), sems)
        ]

    def up_copies(k, way, target):
        return chain_copies(
            k, way, target, (a_sum, b_sum), ((a_up_send, a_up_recv), (b_up_send, b_up_recv))
        )

    def back_copies(k, way, target):
        return chain_copies(
            k, way, target, (a_done, b_done), ((a_back_send, a_back_recv), (b_back_send, b_back_recv))
        )

    def a_load(buffer, k, way):
        return buffer[k, pl.ds(way * a_part, a_part)].astype(F32)

    def b_load(buffer, k, way):
        return buffer[k, :, pl.ds(way * b_part, b_part)].astype(F32)

    def a_store(buffer, k, way, value):
        buffer[k, pl.ds(way * a_part, a_part)] = value.astype(BF16)

    def b_store(buffer, k, way, value):
        buffer[k, :, pl.ds(way * b_part, b_part)] = value.astype(BF16)

    def own_terms(k, way):
        slot = 2 * k + way
        at = a_at(a_own, k, way)
        pltpu.make_async_copy(at, at, own_sem.at[slot]).wait()
        pltpu.make_async_copy(at, at, pair_recv.at[slot]).wait()

        @pl.when(k < down_chunks)
        def _():
            at = b_at(b_own, k, way)
            pltpu.make_async_copy(at, at, own_sem.at[2 * a_chunks + slot]).wait()
            pltpu.make_async_copy(at, at, pair_recv.at[2 * a_chunks + slot]).wait()
            b_store(b_own, k, way, b_load(b_own, k, way) + b_load(b_other, k, way))

        return a_load(a_own, k, way) + a_load(a_other, k, way), b_load(b_own, k, way)

    lanes = []
    for way in range(2):
        rank = place if way == 0 else n_ctx - 1 - place
        ahead = place + 1 if way == 0 else place - 1
        behind = place - 1 if way == 0 else place + 1
        lanes.append((way, rank, ahead, behind))

    def tick_step(tick, carry):
        for part, start in ((0, 2), (1, 6)):
            for owner in range(n_fsdp):

                @pl.when(tick == start + owner)
                def _(part=part, owner=owner):
                    mixer_sum(part, owner)

        events = (
            (5, mixer_out, 0),
            (9, mixer_out, 1),
            (10, mixer_on, 0),
            (down_chunks, mixer_in, 0),
            (16, mixer_on, 1),
            (down_chunks + cut, mixer_in, 1),
        )
        for moment, action, part in events:

            @pl.when(tick == moment)
            def _(action=action, part=part):
                action(part)

        for way, rank, ahead, behind in lanes:
            step = tick - 2 * rank
            k = jnp.clip(step, 0, ticks - 1)

            @pl.when((step >= 0) & (step < ticks))
            def _(k=k, way=way, rank=rank, ahead=ahead, behind=behind):
                a_term, b_term = own_terms(k, way)

                @pl.when(rank == 0)
                def _():
                    a_store(a_sum, k, way, a_term)
                    b_store(b_sum, k, way, b_term)

                @pl.when(rank > 0)
                def _():
                    for copy in up_copies(k, way, behind):
                        copy.wait_recv()

                @pl.when((rank > 0) & (rank < n_ctx - 1))
                def _():
                    a_store(a_sum, k, way, a_term + a_load(a_sum, k, way))
                    b_store(b_sum, k, way, b_term + b_load(b_sum, k, way))

                @pl.when(rank < n_ctx - 1)
                def _():
                    for copy in up_copies(k, way, ahead):
                        copy.start()

                @pl.when(rank == n_ctx - 1)
                def _():
                    a_store(a_done, k, way, a_term + a_load(a_sum, k, way))
                    b_store(b_done, k, way, b_term + b_load(b_sum, k, way))
                    for copy in back_copies(k, way, behind):
                        copy.start()
                    hand_out(k, way)

            late = tick - 2 * (tail - rank)
            j = jnp.clip(late, 0, ticks - 1)

            @pl.when((late >= 0) & (late < ticks) & (rank < n_ctx - 1))
            def _(j=j, way=way, rank=rank, ahead=ahead, behind=behind):
                for copy in back_copies(j, way, ahead):
                    copy.wait_recv()

                @pl.when(rank > 0)
                def _():
                    for copy in back_copies(j, way, behind):
                        copy.start()

                hand_out(j, way)

        return carry

    second_start()
    lax.fori_loop(0, ticks + 2 * tail, tick_step, 0)

    for part in range(2):
        for copy in c_pair[part]:
            copy.wait_send()
        opening, onward = mixer_copies(part)
        for copy in opening + onward:
            copy.wait_send()

    def settle(k, carry):
        for way, rank, ahead, behind in lanes:
            slot = 2 * k + way
            a_ref, b_ref = a_at(a_own, k, way), b_at(b_own, k, way)
            pltpu.make_async_copy(a_ref, a_ref, pair_send.at[slot]).wait()

            @pl.when(k < down_chunks)
            def _(b_ref=b_ref, slot=slot):
                pltpu.make_async_copy(b_ref, b_ref, pair_send.at[2 * a_chunks + slot]).wait()

            @pl.when(rank < n_ctx - 1)
            def _(k=k, way=way, ahead=ahead):
                for copy in up_copies(k, way, ahead):
                    copy.wait_send()

            @pl.when(rank > 0)
            def _(k=k, way=way, behind=behind):
                for copy in back_copies(k, way, behind):
                    copy.wait_send()

            pltpu.make_async_copy(a_ref, a_ref, a_out_send.at[slot]).wait()
            pltpu.make_async_copy(b_ref, b_ref, b_out_send.at[slot]).wait()

            @pl.when(k >= down_chunks)
            def _(b_ref=b_ref, slot=slot):
                pltpu.make_async_copy(b_ref, b_ref, b_keep_sem.at[slot]).wait()

        return carry

    lax.fori_loop(0, ticks, settle, 0)
    pltpu.make_async_copy(second_gu_in, second_gu_in, second_send.at[0]).wait()
    pltpu.make_async_copy(second_down_in, second_down_in, second_send.at[1]).wait()

    @pl.when(section == 0)
    def _():
        for kind in range(2):
            for source in range(2 * n_fsdp):

                @pl.when(group != source)
                def _(kind=kind, source=source):
                    region = gu_out.at[
                        kind,
                        pl.ds((source // n_fsdp) * half, half),
                        pl.ds((source % n_fsdp) * a_width, a_width),
                    ]
                    pltpu.make_async_copy(region, region, gu_recv.at[kind, source]).wait()

    @pl.when(section == 1)
    def _():
        pltpu.make_async_copy(second_gu_in, second_gu_in, second_recv).wait()

    region = down_out.at[pl.ds(pl.multiple_of(other * down_half, b_rows), down_half)]
    pltpu.make_async_copy(region, region, down_recv).wait()
    region = rest_out.at[other]
    pltpu.make_async_copy(region, region, rest_recv).wait()


def summed_gradients(first, mixers, small, second_gu, second_down):
    n_ctx, n_fsdp = lax.axis_size("ctx"), lax.axis_size("fsdp")
    gate, up, down = first
    half = gate.shape[0] // n_fsdp // 2
    a_rows, b_rows = half // 4, half * 3 // 8
    a_chunks = 2 * n_fsdp * 4
    a_width, b_width = gate.shape[1], down.shape[1]
    c_rows = len(mixers) * half + small.shape[1]
    down_chunks = down.shape[0] // 2 // b_rows
    b_chunks = down_chunks + c_rows // b_rows + 1
    assert a_chunks == b_chunks and c_rows % b_rows == 0
    rest = b_chunks - down_chunks
    dma = pltpu.SemaphoreType.DMA
    loads = 2 * (a_chunks + down_chunks)
    pieces = n_fsdp * (len(mixers) + 1)
    return pl.pallas_call(
        functools.partial(tail_kernel, (n_ctx, n_fsdp)),
        out_shape=(
            jax.ShapeDtypeStruct((2, 2 * half, n_fsdp * a_width), BF16),
            jax.ShapeDtypeStruct(down.shape, BF16),
            jax.ShapeDtypeStruct((2, rest * b_rows, b_width), BF16),
        ),
        in_specs=[pl.BlockSpec(memory_space=pl.ANY)] * (6 + len(mixers)),
        out_specs=[pl.BlockSpec(memory_space=pl.ANY)] * 3,
        scratch_shapes=[
            pltpu.VMEM((a_chunks, a_rows, a_width), BF16),
            pltpu.VMEM((a_chunks, a_rows, a_width), BF16),
            pltpu.VMEM((a_chunks, a_rows, a_width), BF16),
            pltpu.VMEM((a_chunks, a_rows, a_width), BF16),
            pltpu.VMEM((b_chunks, b_rows, b_width), BF16),
            pltpu.VMEM((down_chunks, b_rows, b_width), BF16),
            pltpu.VMEM((b_chunks, b_rows, b_width), BF16),
            pltpu.VMEM((b_chunks, b_rows, b_width), BF16),
            pltpu.VMEM((n_fsdp, c_rows, b_width), BF16),
            pltpu.VMEM((n_fsdp, c_rows, b_width), BF16),
            pltpu.VMEM((n_fsdp - 1, c_rows, b_width), BF16),
            dma((loads,)),
            dma((loads,)),
            dma((loads,)),
            dma((pieces,)),
            dma((pieces,)),
            dma((pieces,)),
            dma((2, 6)),
            dma((2, 6)),
            dma((2 * a_chunks,)),
            dma((2 * a_chunks,)),
            dma((2 * a_chunks,)),
            dma((2 * a_chunks,)),
            dma((2 * a_chunks,)),
            dma((2 * b_chunks,)),
            dma((2 * b_chunks,)),
            dma((2 * b_chunks,)),
            dma((2 * b_chunks,)),
            dma((2 * b_chunks,)),
            dma((2 * b_chunks,)),
            dma((2, 2 * n_fsdp)),
            dma,
            dma,
            dma((2,)),
            dma,
        ],
        compiler_params=pltpu.CompilerParams(
            collective_id=6, has_side_effects=True, vmem_limit_bytes=56 << 20
        ),
        cost_estimate=busy(160),
    )(gate, up, down, *mixers, small, second_gu, second_down)


class Columns:
    def __init__(self, holder, sources, targets, send_sem, recv_sem, pair_send, pair_recv, own_sem):
        self.count = 4
        self.holder = holder
        self.section = lax.axis_index("section")
        self.me = lax.axis_index("fsdp")
        self.sources, self.targets = sources, targets
        self.sems = send_sem, recv_sem, pair_send, pair_recv, own_sem
        self.rows = sources[0].shape[0]
        self.wide = targets[0].shape[1]
        self.steps = [(step, kind) for step in range(1, self.count) for kind in range(2)]

    def at_rows(self, out, owner):
        return out.at[pl.ds(pl.multiple_of(owner * self.rows, self.rows), self.rows)]

    def at_columns(self, source, owner):
        return source.at[:, pl.ds(pl.multiple_of(owner * self.wide, 128), self.wide)]

    def crossing(self, step, kind):
        target = lax.rem(self.me + step, self.count)
        return to_side(
            self.at_columns(self.sources[kind], target),
            self.at_rows(self.targets[kind], self.me),
            self.sems[0].at[kind, step],
            self.sems[1].at[kind, step],
            target,
        )

    def handed(self, step, kind):
        if kind == 2:
            src, dst = self.sources[2], self.targets[2]
        else:
            origin = lax.rem(self.me + self.count - step, self.count)
            dst = self.at_rows(self.targets[kind], origin)
            src = self.at_columns(self.sources[kind], self.me) if step == 0 else dst
        return pltpu.make_async_remote_copy(
            src_ref=src,
            dst_ref=dst,
            send_sem=self.sems[2].at[kind, step],
            recv_sem=self.sems[3].at[kind, step],
            device_id={"section": 1 - self.section},
            device_id_type=MESH,
        )

    def kept(self, kind):
        if kind == 2:
            return pltpu.make_async_copy(self.sources[2], self.targets[2], self.sems[4].at[2])
        return pltpu.make_async_copy(
            self.at_columns(self.sources[kind], self.me),
            self.at_rows(self.targets[kind], self.me),
            self.sems[4].at[kind],
        )

    def start(self):
        @pl.when(self.section == self.holder)
        def _():
            for step, kind in self.steps:
                self.crossing(step, kind).start()
            for kind in range(3):
                self.handed(0, kind).start()
            for kind in range(3):
                self.kept(kind).start()

    def relay(self):
        @pl.when(self.section == self.holder)
        def _():
            for step, kind in self.steps:
                self.crossing(step, kind).wait_recv()
                self.handed(step, kind).start()

    def arrive(self):
        every = [(0, kind) for kind in range(3)] + self.steps

        @pl.when(self.section == self.holder)
        def _():
            for kind in range(3):
                self.kept(kind).wait()

        @pl.when(self.section != self.holder)
        def _():
            for step, kind in every:
                self.handed(step, kind).wait_recv()

    def finish(self):
        every = [(0, kind) for kind in range(3)] + self.steps

        @pl.when(self.section == self.holder)
        def _():
            for step, kind in self.steps:
                self.crossing(step, kind).wait_send()
            for step, kind in every:
                self.handed(step, kind).wait_send()


class Chain:
    def __init__(self, count):
        self.count = count
        self.place = lax.axis_index("ctx")
        self.has_next = self.place < count - 1
        self.has_last = self.place > 0


def greet_mixed(chain, targets):
    barrier = pltpu.get_barrier_semaphore()
    for target in targets:
        pl.semaphore_signal(barrier, inc=1, device_id=target, device_id_type=MESH)

    @pl.when(chain.has_last)
    def _():
        pl.semaphore_signal(barrier, inc=1, device_id={"ctx": chain.place - 1}, device_id_type=MESH)

    @pl.when(chain.has_next)
    def _():
        pl.semaphore_signal(barrier, inc=1, device_id={"ctx": chain.place + 1}, device_id_type=MESH)

    inner = chain.has_last & chain.has_next

    @pl.when(inner)
    def _():
        pl.semaphore_wait(barrier, len(targets) + 2)

    @pl.when(jnp.logical_not(inner))
    def _():
        pl.semaphore_wait(barrier, len(targets) + 1)


def along(src, dst, send_sem, recv_sem, place):
    return pltpu.make_async_remote_copy(
        src_ref=src,
        dst_ref=dst,
        send_sem=send_sem,
        recv_sem=recv_sem,
        device_id={"ctx": place},
        device_id_type=MESH,
    )


def spread_heads(source, spread):
    rows = source.shape[0]
    low = lax.broadcasted_iota(jnp.int32, (rows, 128), 1) < 64
    for pair in range(source.shape[1] // 256):
        first = source[:, pair * 256 : pair * 256 + 128].astype(F32)
        second = source[:, pair * 256 + 128 : pair * 256 + 256].astype(F32)
        spread[4 * pair] = jnp.where(low, first, 0.0).astype(BF16)
        spread[4 * pair + 1] = jnp.where(low, pltpu.roll(first, 64, 1), 0.0).astype(BF16)
        spread[4 * pair + 2] = jnp.where(low, 0.0, pltpu.roll(second, 64, 1)).astype(BF16)
        spread[4 * pair + 3] = jnp.where(low, 0.0, second).astype(BF16)


def join_heads(spread, target):
    rows = target.shape[0]
    low = lax.broadcasted_iota(jnp.int32, (rows, 128), 1) < 64
    for pair in range(target.shape[1] // 256):
        parts = [spread(4 * pair + i).T for i in range(4)]
        target[:, pair * 256 : pair * 256 + 128] = jnp.where(low, parts[0], pltpu.roll(parts[1], 64, 1))
        target[:, pair * 256 + 128 : pair * 256 + 256] = jnp.where(low, pltpu.roll(parts[2], 64, 1), parts[3])


def mask_block(bias, length, place, block):
    rows = bias.shape[0]
    key_at = block * rows + lax.broadcasted_iota(jnp.int32, bias.shape, 0)
    query_at = place * rows + lax.broadcasted_iota(jnp.int32, bias.shape, 1)
    bias[...] = jnp.where((key_at <= query_at) & (key_at < length), 0.0, NEGATIVE)


def dot_right(left, right):
    return lax.dot_general(left, right, (((1,), (1,)), ((), ())), preferred_element_type=F32)


def dot_plain(left, right):
    return jnp.dot(left, right, preferred_element_type=F32)


def attend_kernel(
    n_ctx,
    length_ref,
    query,
    kv,
    d_block,
    gate_in,
    up_in,
    down_in,
    attended,
    log_total,
    kv_all,
    d_all,
    gate_out,
    up_out,
    down_out,
    w_gate,
    w_up,
    w_down,
    keep_sem,
    spread,
    bias,
    peak,
    total,
    out_t,
    kv_send,
    kv_recv,
    d_send,
    d_recv,
    d_own,
    send_sem,
    recv_sem,
    pair_send,
    pair_recv,
    own_sem,
):
    chain = Chain(n_ctx)
    place = chain.place
    section = lax.axis_index("section")
    me, beside, across, opposite = corners()
    greet_mixed(
        chain,
        [{"fsdp": beside}, {"fsdp": across}, {"fsdp": opposite}, {"section": 1 - section}],
    )
    rows = query.shape[0]
    half_width = kv.shape[1] // 2

    def block_rows(block):
        return pl.ds(pl.multiple_of(block * rows, rows), rows)

    def upward(step, src):
        return along(
            src,
            kv_all.at[block_rows(place - step)],
            kv_send.at[step],
            kv_recv.at[step + 1],
            place + 1,
        )

    def arriving(step):
        at = kv_all.at[block_rows(place - step)]
        return along(at, at, kv_send.at[step], kv_recv.at[step], place)

    @pl.when(chain.has_next)
    def _():
        upward(0, kv).start()

    gather = SideGather(d_block, d_all, d_send, d_recv, d_own)
    gather.start()
    columns = Columns(
        1, (gate_in, up_in, down_in), (w_gate, w_up, w_down), send_sem, recv_sem, pair_send, pair_recv, own_sem
    )
    columns.start()
    kv_all[block_rows(place)] = kv[...]
    spread_heads(query, spread)
    peak[...] = jnp.full(peak.shape, NEGATIVE, F32)
    total[...] = jnp.zeros(total.shape, F32)
    out_t[...] = jnp.zeros(out_t.shape, F32)
    length = length_ref[0]
    scale = 64 ** (-0.5)

    def attend_block(block):
        mask_block(bias, length, place, block)
        for pair in range(half_width // 128):
            key = kv_all[block_rows(block), pair * 128 : pair * 128 + 128]
            value_t = kv_all[block_rows(block), half_width + pair * 128 : half_width + pair * 128 + 128].T
            for index in range(4):
                head = 4 * pair + index
                scores = dot_right(key, spread[head]) * scale + bias[...]
                before = peak[head]
                now = jnp.maximum(before, jnp.max(scores, axis=0, keepdims=True))
                weights = jnp.exp(scores - now)
                fade = jnp.exp(before - now)
                peak[head] = now
                total[head] = total[head] * fade + jnp.sum(weights, axis=0, keepdims=True)
                out_t[head] = out_t[head] * fade + dot_plain(value_t, weights.astype(BF16))

    attend_block(place)
    gather.relay()

    def step_on(step, carry):
        @pl.when(step <= place)
        def _():
            arriving(step).wait_recv()

            @pl.when(chain.has_next)
            def _():
                upward(step, kv_all.at[block_rows(place - step)]).start()

            attend_block(place - step)

        return carry

    lax.fori_loop(1, n_ctx, step_on, 0)
    join_heads(lambda head: out_t[head] / total[head], attended)
    for head in range(spread.shape[0]):
        log_total[head] = peak[head] + jnp.log(total[head])
    columns.relay()
    columns.arrive()
    keeping = [
        pltpu.make_async_copy(src, dst, keep_sem.at[index])
        for index, (src, dst) in enumerate(((w_gate, gate_out), (w_up, up_out), (w_down, down_out)))
    ]
    for copy in keeping:
        copy.start()
    gather.finish()
    columns.finish()
    for copy in keeping:
        copy.wait()

    def settle(step, carry):
        @pl.when((step <= place) & chain.has_next)
        def _():
            upward(step, kv_all.at[block_rows(place - step)]).wait_send()

        return carry

    lax.fori_loop(0, n_ctx, settle, 0)


def attend(length, query, kv, d_block, gate, up, down, collective_id):
    n_ctx, count = lax.axis_size("ctx"), lax.axis_size("fsdp")
    rows, width = query.shape
    heads = width // 64
    dma = pltpu.SemaphoreType.DMA
    vmem = pl.BlockSpec(memory_space=pltpu.VMEM)
    hbm = pl.BlockSpec(memory_space=pl.ANY)
    column = jax.ShapeDtypeStruct((count * gate.shape[0], gate.shape[1] // count), gate.dtype)
    return pl.pallas_call(
        functools.partial(attend_kernel, n_ctx),
        out_shape=(
            jax.ShapeDtypeStruct((rows, width), F32),
            jax.ShapeDtypeStruct((heads, 1, rows), F32),
            jax.ShapeDtypeStruct((n_ctx * rows, kv.shape[1]), BF16),
            jax.ShapeDtypeStruct((count * rows, d_block.shape[1]), BF16),
            column,
            column,
            jax.ShapeDtypeStruct(down.shape, down.dtype),
        ),
        in_specs=[pl.BlockSpec(memory_space=pltpu.SMEM), vmem, vmem, vmem, hbm, hbm, hbm],
        out_specs=[vmem, vmem, vmem, vmem, hbm, hbm, hbm],
        scratch_shapes=[
            pltpu.VMEM(column.shape, BF16),
            pltpu.VMEM(column.shape, BF16),
            pltpu.VMEM(down.shape, BF16),
            dma((3,)),
            pltpu.VMEM((heads, rows, 128), BF16),
            pltpu.VMEM((rows, rows), F32),
            pltpu.VMEM((heads, 1, rows), F32),
            pltpu.VMEM((heads, 1, rows), F32),
            pltpu.VMEM((heads, 128, rows), F32),
            dma((n_ctx + 1,)),
            dma((n_ctx + 1,)),
            dma((4,)),
            dma((4,)),
            dma,
            dma((2, count)),
            dma((2, count)),
            dma((3, count)),
            dma((3, count)),
            dma((3,)),
        ],
        compiler_params=pltpu.CompilerParams(
            collective_id=collective_id, has_side_effects=True, vmem_limit_bytes=58 << 20
        ),
        cost_estimate=busy(50),
    )(length, query, kv, d_block, gate, up, down)


def attend_back_kernel(
    n_ctx,
    length_ref,
    query,
    kv_all,
    d_out,
    log_total,
    delta,
    blocks,
    d_query,
    d_kv,
    reduced_out,
    spread,
    d_spread,
    bias,
    d_query_t,
    term,
    leaving,
    coming,
    kv_send,
    kv_recv,
    beside_got,
    across_got,
    passed,
    passed_got,
    send_sem,
    recv_sem,
):
    chain = Chain(n_ctx)
    place = chain.place
    _, beside, across, _ = corners()
    greet_mixed(chain, [{"fsdp": beside}, {"fsdp": across}])
    rows = query.shape[0]
    half_width = kv_all.shape[1] // 2
    reduction = SideReduce(blocks, reduced_out, beside_got, across_got, passed, passed_got, send_sem, recv_sem)
    reduction.start()
    spread_heads(query, spread)
    spread_heads(d_out, d_spread)
    d_query_t[...] = jnp.zeros(d_query_t.shape, F32)
    length = length_ref[0]
    scale = 64 ** (-0.5)

    def downward(block):
        return along(leaving.at[block], coming.at[block], kv_send.at[block], kv_recv.at[block], place - 1)

    def step_on(block, carry):
        @pl.when(block <= place)
        def _():
            mask_block(bias, length, place, block)
            at = pl.ds(pl.multiple_of(block * rows, rows), rows)
            for pair in range(half_width // 128):
                lanes = slice(pair * 128, pair * 128 + 128)
                more = slice(half_width + pair * 128, half_width + pair * 128 + 128)
                key = kv_all[at, lanes]
                value = kv_all[at, more]
                key_t = key.T
                d_key = jnp.zeros((rows, 128), F32)
                d_value = jnp.zeros((rows, 128), F32)
                for index in range(4):
                    head = 4 * pair + index
                    scores = dot_right(key, spread[head]) * scale + bias[...]
                    prob = jnp.exp(scores - log_total[head])
                    d_prob = dot_right(value, d_spread[head])
                    d_scores = (prob * (d_prob - delta[head])).astype(BF16)
                    d_value = d_value + dot_plain(prob.astype(BF16), d_spread[head])
                    d_key = d_key + dot_plain(d_scores, spread[head])
                    d_query_t[head] = d_query_t[head] + dot_plain(key_t, d_scores)
                term[:, lanes] = d_key * scale
                term[:, more] = d_value

            @pl.when(chain.has_next)
            def _():
                along(
                    leaving.at[block], coming.at[block], kv_send.at[block], kv_recv.at[block], place
                ).wait_recv()
                term[...] = term[...] + coming[block].astype(F32)

            @pl.when(block < place)
            def _():
                leaving[block] = term[...].astype(BF16)
                downward(block).start()

            @pl.when(block == place)
            def _():
                d_kv[...] = term[...]

        @pl.when(block == 0)
        def _():
            reduction.relay()

        return carry

    lax.fori_loop(0, n_ctx, step_on, 0)
    join_heads(lambda head: d_query_t[head] * scale, d_query)
    reduction.finish()

    def settle(block, carry):
        @pl.when(block < place)
        def _():
            downward(block).wait_send()

        return carry

    lax.fori_loop(0, n_ctx, settle, 0)


def attend_back(length, query, kv_all, d_out, log_total, delta, blocks, collective_id):
    n_ctx = lax.axis_size("ctx")
    rows, width = query.shape
    heads = width // 64
    dma = pltpu.SemaphoreType.DMA
    vmem = pl.BlockSpec(memory_space=pltpu.VMEM)
    wide = jax.ShapeDtypeStruct((rows, width), F32)
    pair = pltpu.VMEM((2, rows // 2, blocks.shape[1]), BF16)
    return pl.pallas_call(
        functools.partial(attend_back_kernel, n_ctx),
        out_shape=(wide, jax.ShapeDtypeStruct((rows, kv_all.shape[1]), F32), wide),
        in_specs=[pl.BlockSpec(memory_space=pltpu.SMEM)] + [vmem] * 6,
        out_specs=[vmem] * 3,
        scratch_shapes=[
            pltpu.VMEM((heads, rows, 128), BF16),
            pltpu.VMEM((heads, rows, 128), BF16),
            pltpu.VMEM((rows, rows), F32),
            pltpu.VMEM((heads, 128, rows), F32),
            pltpu.VMEM((rows, kv_all.shape[1]), F32),
            pltpu.VMEM((n_ctx, rows, kv_all.shape[1]), BF16),
            pltpu.VMEM((n_ctx, rows, kv_all.shape[1]), BF16),
            dma((n_ctx,)),
            dma((n_ctx,)),
            pair,
            pair,
            pair,
            pair,
            dma((6,)),
            dma((6,)),
        ],
        compiler_params=pltpu.CompilerParams(
            collective_id=collective_id, has_side_effects=True, vmem_limit_bytes=56 << 20
        ),
        cost_estimate=busy(50),
    )(length, query, kv_all, d_out, log_total, delta, blocks)


class MixerGather:
    def __init__(self, sources, targets, send_sem, recv_sem, pair_send, pair_recv, own_sem):
        self.section = section = lax.axis_index("section")
        me, beside, across, opposite = corners()
        rows = sources[0].shape[0]
        half = rows // 2
        quarter = half // 2

        def at_rows(out, owner, extra, size):
            return out.at[pl.ds(pl.multiple_of(owner * rows + extra, quarter), size)]

        def pair(slot, at):
            return pltpu.make_async_remote_copy(
                src_ref=at,
                dst_ref=at,
                send_sem=pair_send.at[slot],
                recv_sem=pair_recv.at[slot],
                device_id={"section": 1 - section},
                device_id_type=MESH,
            )

        self.direct, self.onward, self.early, self.late, self.own = [], [], [], [], []
        start = section * half
        for index, (source, out) in enumerate(zip(sources, targets)):
            mine = source.at[pl.ds(pl.multiple_of(start, half), half)]
            spot = at_rows(out, me, start, half)
            slot = 4 * index
            self.direct.append(
                [
                    to_side(mine, spot, send_sem.at[slot], recv_sem.at[slot], beside),
                    to_side(mine, spot, send_sem.at[slot + 1], recv_sem.at[slot + 1], across),
                ]
            )
            passing = at_rows(out, beside, start, quarter), at_rows(out, across, start + quarter, quarter)
            self.onward.append(
                [
                    to_side(passing[0], passing[0], send_sem.at[slot + 2], recv_sem.at[slot + 2], across),
                    to_side(passing[1], passing[1], send_sem.at[slot + 3], recv_sem.at[slot + 3], beside),
                ]
            )
            self.early.append(
                [
                    pair(slot, at_rows(out, beside, start, half)),
                    pair(slot + 1, at_rows(out, across, start, half)),
                ]
            )
            self.late.append(
                [
                    pair(slot + 2, at_rows(out, opposite, start, quarter)),
                    pair(slot + 3, at_rows(out, opposite, start + quarter, quarter)),
                ]
            )
            self.own.append(pltpu.make_async_copy(source, at_rows(out, me, 0, rows), own_sem.at[index]))

    def start(self):
        for copies in self.direct:
            for copy in copies:
                copy.start()
        for copy in self.own:
            copy.start()

    def relay(self):
        for direct, onward, early in zip(self.direct, self.onward, self.early):
            for turn in range(2):
                direct[turn].wait_recv()
                onward[turn].start()
                early[turn].start()

    def relay_last(self):
        for onward, late in zip(self.onward, self.late):
            for turn in range(2):
                onward[turn].wait_recv()
                late[turn].start()

    def arrive(self, index):
        self.own[index].wait()
        for copy in self.early[index] + self.late[index]:
            copy.wait_recv()

    def finish(self):
        for group in (self.direct, self.onward, self.early, self.late):
            for copies in group:
                for copy in copies:
                    copy.wait_send()


def front_kernel(
    n_ctx,
    x_ref,
    gains,
    taps,
    conv_in,
    conv_out,
    gate_in,
    up_in,
    down_in,
    in_out,
    out_out,
    gate_out,
    up_out,
    down_out,
    projected,
    convolved,
    z_low,
    mixed,
    rim,
    act_all,
    w_in,
    w_out,
    w_gate,
    w_up,
    w_down,
    act1,
    act2,
    last_rows,
    rim_sem,
    mix_send,
    mix_recv,
    mix_pair_send,
    mix_pair_recv,
    mix_own,
    send_sem,
    recv_sem,
    pair_send,
    pair_recv,
    own_sem,
    act_send,
    act_recv,
    act_own,
    keep_sem,
):
    chain = Chain(n_ctx)
    section = lax.axis_index("section")
    _, beside, across, opposite = corners()
    greet_mixed(
        chain,
        [{"fsdp": beside}, {"fsdp": across}, {"fsdp": opposite}, {"section": 1 - section}],
    )
    mixers = MixerGather(
        (conv_in, conv_out), (w_in, w_out), mix_send, mix_recv, mix_pair_send, mix_pair_recv, mix_own
    )
    mixers.start()
    columns = Columns(
        0, (gate_in, up_in, down_in), (w_gate, w_up, w_down), send_sem, recv_sem, pair_send, pair_recv, own_sem
    )
    gather = SideGather(act2, act_all, act_send, act_recv, act_own)
    keeping = [
        pltpu.make_async_copy(src, dst, keep_sem.at[index])
        for index, (src, dst) in enumerate(
            ((w_in, in_out), (w_out, out_out), (w_gate, gate_out), (w_up, up_out), (w_down, down_out))
        )
    ]
    rows, width = x_ref.shape
    strip = 64

    def normalize(values, gain):
        inv_rms = lax.rsqrt(jnp.mean(values * values, axis=-1, keepdims=True) + EPSILON)
        return (values * inv_rms * gain).astype(BF16)

    def first_norm(index, carry):
        at = pl.ds(pl.multiple_of(index * strip, strip), strip)
        act1[at] = normalize(x_ref[at].astype(F32), gains[0:1])
        return carry

    lax.fori_loop(0, rows // strip, first_norm, 0)
    mixers.relay()
    columns.start()
    mixers.relay_last()
    mixers.arrive(0)
    keeping[0].start()
    wide = 512

    def project(index, carry):
        at = pl.ds(pl.multiple_of(index * wide, wide), wide)
        projected[:, at] = dot_plain(act1[...], w_in[:, at])
        return carry

    lax.fori_loop(0, projected.shape[1] // wide, project, 0)
    tail_at = pl.ds(rows - 16, 16)
    last_rows[...] = (projected[tail_at, :width] * projected[tail_at, 2 * width :]).astype(BF16)
    to_next = along(last_rows, rim, rim_sem.at[0], rim_sem.at[1], chain.place + 1)

    @pl.when(chain.has_next)
    def _():
        to_next.start()

    @pl.when(chain.has_last)
    def _():
        along(last_rows, rim, rim_sem.at[0], rim_sem.at[1], chain.place).wait_recv()

    @pl.when(jnp.logical_not(chain.has_last))
    def _():
        rim[...] = jnp.zeros(rim.shape, BF16)

    part = 128
    row_at = lax.broadcasted_iota(jnp.int32, (rows, part), 0)

    def convolve(index, carry):
        def lanes(offset):
            return pl.ds(pl.multiple_of(offset * width + index * part, part), part)

        product = (projected[:, lanes(0)] * projected[:, lanes(2)]).astype(BF16).astype(F32)
        edge = rim[:, lanes(0)].astype(F32)
        near, far = edge[15:16], edge[14:15]
        one = jnp.where(row_at >= 1, pltpu.roll(product, 1, 0), near)
        two = jnp.where(row_at >= 2, pltpu.roll(product, 2, 0), jnp.where(row_at == 1, near, far))
        tap = taps[:, lanes(0)]
        value = tap[0:1] * two + tap[1:2] * one + tap[2:3] * product
        convolved[:, lanes(0)] = value
        z_low[:, lanes(0)] = (projected[:, lanes(1)] * value).astype(BF16)
        return carry

    lax.fori_loop(0, width // part, convolve, 0)
    mixers.arrive(1)
    keeping[1].start()

    def mix(index, carry):
        at = pl.ds(pl.multiple_of(index * wide, wide), wide)
        mixed[:, at] = dot_plain(z_low[...], w_out[:, at])
        return carry

    lax.fori_loop(0, width // wide, mix, 0)

    def second_norm(index, carry):
        at = pl.ds(pl.multiple_of(index * strip, strip), strip)
        act2[at] = normalize(x_ref[at].astype(F32) + mixed[at], gains[1:2])
        return carry

    lax.fori_loop(0, rows // strip, second_norm, 0)
    gather.start()
    gather.relay()
    columns.relay()
    columns.arrive()
    for copy in keeping[2:]:
        copy.start()
    gather.finish()
    columns.finish()
    mixers.finish()

    @pl.when(chain.has_next)
    def _():
        to_next.wait_send()

    for copy in keeping:
        copy.wait()


def front(x_low, gains, taps, conv_in, conv_out, gate, up, down, collective_id):
    n_ctx, count = lax.axis_size("ctx"), lax.axis_size("fsdp")
    assert count == 4
    rows, width = x_low.shape
    dma = pltpu.SemaphoreType.DMA
    vmem = pl.BlockSpec(memory_space=pltpu.VMEM)
    hbm = pl.BlockSpec(memory_space=pl.ANY)

    def whole(weight):
        return (count * weight.shape[0], weight.shape[1])

    column = (count * gate.shape[0], gate.shape[1] // count)
    weights = [whole(conv_in), whole(conv_out), column, column, down.shape]
    return pl.pallas_call(
        functools.partial(front_kernel, n_ctx),
        out_shape=tuple(jax.ShapeDtypeStruct(shape, BF16) for shape in weights)
        + (
            jax.ShapeDtypeStruct((rows, conv_in.shape[1]), F32),
            jax.ShapeDtypeStruct((rows, width), F32),
            jax.ShapeDtypeStruct((rows, width), BF16),
            jax.ShapeDtypeStruct((rows, width), F32),
            jax.ShapeDtypeStruct((16, width), BF16),
            jax.ShapeDtypeStruct((count * rows, width), BF16),
        ),
        in_specs=[vmem] * 3 + [hbm] * 5,
        out_specs=[hbm] * 5 + [vmem] * 6,
        scratch_shapes=[pltpu.VMEM(shape, BF16) for shape in weights]
        + [
            pltpu.VMEM((rows, width), BF16),
            pltpu.VMEM((rows, width), BF16),
            pltpu.VMEM((16, width), BF16),
            dma((2,)),
            dma((8,)),
            dma((8,)),
            dma((8,)),
            dma((8,)),
            dma((2,)),
            dma((2, count)),
            dma((2, count)),
            dma((3, count)),
            dma((3, count)),
            dma((3,)),
            dma((4,)),
            dma((4,)),
            dma,
            dma((5,)),
        ],
        compiler_params=pltpu.CompilerParams(
            collective_id=collective_id, has_side_effects=True, vmem_limit_bytes=58 << 20
        ),
        cost_estimate=busy(70),
    )(x_low, gains, taps, conv_in, conv_out, gate, up, down)


def ffn_forward(act, w_gate, w_up, w_down):
    gate_pre = matmul(act, w_gate)
    up_pre = matmul(act, w_up)
    hidden = (jax.nn.silu(gate_pre) * up_pre).astype(BF16)
    return matmul(hidden, w_down).astype(BF16), (act, gate_pre, up_pre, hidden)


def ffn_backward(d_all, kept, w_gate, w_up, w_down):
    act, gate_pre, up_pre, hidden = kept
    d_hidden = matmul_right(d_all, w_down)
    sigmoid = jax.nn.sigmoid(gate_pre)
    d_up = (d_hidden * gate_pre * sigmoid).astype(BF16)
    d_gate = (d_hidden * up_pre * sigmoid * (1.0 + gate_pre * (1.0 - sigmoid))).astype(BF16)
    terms = (matmul_right(d_gate, w_gate) + matmul_right(d_up, w_up)).astype(BF16)
    grads = (
        matmul_left(act, d_gate).astype(BF16),
        matmul_left(act, d_up).astype(BF16),
        matmul_left(hidden, d_all).astype(BF16),
    )
    return terms, grads


def ffn_norm_back(d_act, residual, gain):
    normed, inv_rms = norm_rows(residual)
    return norm_back(d_act * gain, normed, inv_rms), jnp.sum(d_act * normed, axis=0)


def shards(
    inputs,
    cotangent,
    lengths,
    norm_gains,
    conv_in,
    conv_kernel,
    conv_out,
    attn_q,
    attn_k,
    attn_v,
    attn_out,
    head_gains,
    ffn_gate,
    ffn_up,
    ffn_down,
):
    micro, rows, width = inputs.shape
    section = lax.axis_index("section")
    group = lax.axis_index("fsdp")
    fsdp = lax.axis_size("fsdp")
    assert micro == lax.axis_size("section")
    head = head_gains.shape[1]
    q_width, kv_width = attn_q.shape[1], attn_k.shape[1]
    q_heads, kv_heads = q_width // head, kv_width // head
    positions = lax.axis_index("ctx") * rows + jnp.arange(rows)
    length = lax.dynamic_index_in_dim(lengths, group * micro + section, keepdims=False)
    mask = (positions < length).astype(F32)[:, None]

    def whole_rows(weight):
        half = weight.shape[0] // micro
        mine = lax.dynamic_slice_in_dim(weight, section * half, half, 0)
        return lax.all_gather(mine, ("fsdp", "section"), axis=0, tiled=True)

    part = ffn_gate.shape[1]
    query_full, key_full, value_full, proj_full = (
        whole_rows(attn_q),
        whole_rows(attn_k),
        whole_rows(attn_v),
        whole_rows(attn_out),
    )

    x_low = lax.dynamic_index_in_dim(inputs, section, keepdims=False)
    in_full, out_full, gate1, up1, down1, projected, convolved, z_low, mixed, rim, act_all1 = front(
        x_low, norm_gains, conv_kernel, conv_in, conv_out, ffn_gate[0], ffn_up[0], ffn_down[0], 2
    )
    x = x_low.astype(F32)
    res1 = x + mixed
    terms1, kept1 = ffn_forward(act_all1, gate1, up1, down1)
    ffn1 = reduced(terms1, 1)
    h_low = (res1 + ffn1).astype(BF16)

    h = h_low.astype(F32)
    normed2, inv2 = norm_rows(h)
    act2 = (normed2 * norm_gains[2]).astype(BF16)
    q_normed, q_inv = norm_heads(matmul(act2, query_full), head)
    k_normed, k_inv = norm_heads(matmul(act2, key_full), head)
    q_gain = jnp.tile(head_gains[0], q_heads)
    k_gain = jnp.tile(head_gains[1], kv_heads)
    query = (q_normed * q_gain).astype(BF16)
    key = (k_normed * k_gain).astype(BF16)
    value = matmul(act2, value_full).astype(BF16)
    d_sum_low = (lax.dynamic_index_in_dim(cotangent, section, keepdims=False).astype(F32) * mask).astype(BF16)
    attended, log_total, kv_all, d_sum_all, gate2, up2, down2 = attend(
        length.reshape(1),
        query,
        jnp.concatenate([key, value], axis=1),
        d_sum_low,
        ffn_gate[0],
        ffn_up[0],
        ffn_down[0],
        3,
    )
    attended_low = attended.astype(BF16)
    attn_rows = matmul(attended_low, proj_full)
    res2 = h + attn_rows
    normed3, _ = norm_rows(res2)
    act_all2 = gathered((normed3 * norm_gains[3]).astype(BF16), 0)
    terms2, kept2 = ffn_forward(act_all2, gate2, up2, down2)

    d_sum = d_sum_low.astype(F32)
    d_terms2, grads2 = ffn_backward(d_sum_all, kept2, gate2, up2, down2)
    half = part // 2
    strip = half // lax.axis_size("ctx")

    def column_half(which):
        pieces = jnp.stack(grads2[:2]).reshape(2, fsdp, 2, half // strip, strip, -1)
        pieces = lax.dynamic_index_in_dim(pieces, which, 2, keepdims=False)
        return pieces.transpose(2, 1, 0, 3, 4).reshape(2 * fsdp * half, -1)

    def down_half(which):
        size = grads2[2].shape[0] // 2
        return lax.dynamic_slice_in_dim(grads2[2], which * size, size, 0)

    d_act3, got_gu, got_down = reduced_swapping(
        d_terms2, column_half(1 - section), down_half(1 - section), 8
    )
    d_ffn, gain3 = ffn_norm_back(d_act3, res2, norm_gains[3])
    d_res2 = d_sum + d_ffn
    d_attn = d_res2.astype(BF16)
    grad_proj = matmul_left(attended_low, d_attn)
    d_att = matmul_right(d_attn, proj_full).astype(BF16)
    delta = jnp.sum((d_att.astype(F32) * attended).reshape(rows, q_heads, head), axis=-1)
    shared_terms = tuple(
        (mine.astype(F32) + got.astype(F32)).astype(BF16)
        for mine, got in ((column_half(section), got_gu), (down_half(section), got_down))
    )
    d_att, shared_terms = lax.optimization_barrier((d_att, shared_terms))
    d_query, d_kv, ffn2 = attend_back(
        length.reshape(1), query, kv_all, d_att, log_total, delta.T.reshape(q_heads, 1, rows), terms2, 4
    )
    result = (res2 + ffn2) * mask

    def square(values):
        return jnp.sum(mask * values * values, axis=0, keepdims=True)

    squares = [square(v) for v in (x, mixed, ffn1, h, attn_rows, res2, ffn2, result)]
    second_gu, second_down = (
        lax.psum_scatter(term, "ctx", scatter_dimension=0, tiled=True) for term in shared_terms
    )
    d_qn = rounded(d_query)
    grad_qgain = jnp.sum(jnp.sum(d_qn * q_normed, axis=0).reshape(q_heads, head), axis=0)
    d_qpre = norm_heads_back(d_qn * q_gain, q_normed, q_inv, head).astype(BF16)
    d_kn = rounded(d_kv[:, :kv_width])
    grad_kgain = jnp.sum(jnp.sum(d_kn * k_normed, axis=0).reshape(kv_heads, head), axis=0)
    d_kpre = norm_heads_back(d_kn * k_gain, k_normed, k_inv, head).astype(BF16)
    d_vpre = d_kv[:, kv_width:].astype(BF16)
    d_act2 = (
        matmul_right(d_qpre, query_full)
        + matmul_right(d_kpre, key_full)
        + matmul_right(d_vpre, value_full)
    )
    gain2 = jnp.sum(d_act2 * normed2, axis=0)
    d_h_low = (d_res2 + norm_back(d_act2 * norm_gains[2], normed2, inv2)).astype(BF16)

    d_h_all, second_gu = gathered_swapped(d_h_low, second_gu.reshape(fsdp, 2 * strip, -1), 5)
    second_gu = lax.all_gather(second_gu, "ctx", axis=0)
    second_down = lax.all_gather(second_down, "ctx", axis=0, tiled=True)
    d_terms1, grads1 = ffn_backward(d_h_all, kept1, gate1, up1, down1)
    d_ffn1, gain1 = ffn_norm_back(reduced(d_terms1, 1), res1, norm_gains[1])
    d_ffn1, second_gu = lax.optimization_barrier((d_ffn1, second_gu))
    d_res1 = d_h_low.astype(F32) + d_ffn1
    d_mixed = d_res1.astype(BF16)
    grad_out = matmul_left(z_low, d_mixed)
    normed0, inv0 = norm_rows(x)
    act1 = (normed0 * norm_gains[0]).astype(BF16)
    b_gate, c_gate, x_value = (
        projected[:, :width],
        projected[:, width : 2 * width],
        projected[:, 2 * width :],
    )
    extended = jnp.concatenate([rim[14:], (b_gate * x_value).astype(BF16)], axis=0).astype(F32)
    d_z = matmul_right(d_mixed, out_full)
    d_cgate = d_z * convolved
    d_conv = d_z * c_gate
    grad_kernel = jnp.stack(
        [
            jnp.sum(d_conv * extended[:-2], axis=0),
            jnp.sum(d_conv * extended[1:-1], axis=0),
            jnp.sum(d_conv * extended[2:], axis=0),
        ]
    )
    d_extended = (
        jnp.pad(d_conv * conv_kernel[0], ((0, 2), (0, 0)))
        + jnp.pad(d_conv * conv_kernel[1], ((1, 1), (0, 0)))
        + jnp.pad(d_conv * conv_kernel[2], ((2, 0), (0, 0)))
    )
    from_next, second_down = lax.optimization_barrier(
        (passed_along(d_extended[:2], "ctx", -1), second_down)
    )
    d_bproduct = rounded(d_extended[2:] + jnp.pad(from_next, ((rows - 2, 0), (0, 0))))
    d_projected = jnp.concatenate(
        [d_bproduct * x_value, d_cgate, d_bproduct * b_gate], axis=1
    ).astype(BF16)
    d_act1 = matmul_right(d_projected, in_full)
    gain0 = jnp.sum(d_act1 * normed0, axis=0)
    d_x = (d_res1 + norm_back(d_act1 * norm_gains[0], normed0, inv0)).astype(BF16)

    y_low = result.astype(BF16)
    is_first = section == 0
    other_end = swapped(jnp.where(is_first, y_low, d_x), "section")
    ends = jnp.where(is_first, jnp.stack([d_x, other_end]), jnp.stack([other_end, y_low]))[None]

    grad_parts = [
        matmul_left(act1, d_projected[:, i * width : (i + 1) * width]).astype(BF16) for i in range(3)
    ]
    mixers = [
        matmul_left(act2, d_qpre).astype(BF16),
        matmul_left(act2, jnp.concatenate([d_kpre, d_vpre], axis=1)).astype(BF16),
        grad_proj.astype(BF16),
    ] + grad_parts + [grad_out.astype(BF16)]

    small = jnp.concatenate(
        [gain0[None], gain1[None], gain2[None], gain3[None], grad_kernel]
        + [jnp.pad(grad[None], ((0, 0), (0, width - head))) for grad in (grad_qgain, grad_kgain)]
        + [jnp.zeros((7, width), F32)]
        + squares
        + [jnp.zeros((8, width), F32)]
    ).astype(BF16)
    small = small.reshape(2, 16, width)
    gu_sum, down_sum, rest_sum = summed_gradients(
        grads1,
        mixers,
        small,
        second_gu.reshape(-1, fsdp, 2, strip, second_gu.shape[-1]),
        second_down,
    )
    rest_sum = rest_sum.astype(F32)

    def block(index):
        rows_at = slice(index * half, (index + 1) * half)
        return rest_sum[:, rows_at].reshape(2 * half, width)

    attn_blocks = [block(i) for i in range(3)]
    conv_blocks = [block(3 + i) for i in range(4)]
    small_sum = rest_sum[0, 7 * half : 7 * half + 9]
    cut = width // fsdp
    mine = lax.dynamic_slice_in_dim(small_sum[:7], group * cut, cut, 1)
    head_cut = head // fsdp
    heads = lax.dynamic_slice_in_dim(small_sum[7:9], group * head_cut, head_cut, 1)
    square_cut = len(squares) // fsdp
    square_sum = jnp.sum(
        lax.dynamic_slice_in_dim(rest_sum[1, 7 * half : 7 * half + 8], group * square_cut, square_cut, 0), axis=1
    )
    token_total = jnp.sum(lengths).astype(F32) * width
    rms = jnp.sqrt(square_sum / token_total)
    return (
        ends,
        mine[:3],
        mine[3],
        jnp.concatenate(conv_blocks[:3], axis=1),
        mine[4:7],
        conv_blocks[3],
        attn_blocks[0],
        attn_blocks[1][:, :kv_width],
        attn_blocks[1][:, kv_width:],
        attn_blocks[2],
        heads,
        gu_sum[0][None].astype(F32),
        gu_sum[1][None].astype(F32),
        down_sum[None].astype(F32),
        rms,
    )


def solution(mesh):
    return jax.shard_map(
        shards,
        mesh=mesh,
        in_specs=(
            P("fsdp", "ctx", None),
            P("fsdp", "ctx", None),
            P(),
            P(),
            P("fsdp", None),
            P(),
            P("fsdp", None),
            P("fsdp", None),
            P("fsdp", None),
            P("fsdp", None),
            P("fsdp", None),
            P(),
            P("section", "fsdp", None),
            P("section", "fsdp", None),
            P("section", "fsdp", None),
        ),
        out_specs=(
            P("section", "fsdp", "ctx", None),
            P(None, "fsdp"),
            P("fsdp"),
            P("fsdp", None),
            P(None, "fsdp"),
            P("fsdp", None),
            P("fsdp", None),
            P("fsdp", None),
            P("fsdp", None),
            P("fsdp", None),
            P(None, "fsdp"),
            P("section", "fsdp", None),
            P("section", "fsdp", None),
            P("section", "fsdp", None),
            P("fsdp"),
        ),
        check_vma=False,
    )
```

```python
import functools

import jax
import jax.numpy as jnp
from jax import lax
from jax.experimental import pallas as pl
from jax.experimental.pallas import tpu as pltpu
from jax.sharding import PartitionSpec as P

EPSILON = 1e-05
NEGATIVE = -1e30
MESH = pl.DeviceIdType.MESH
F32 = jnp.float32
BF16 = jnp.bfloat16


def passed_along(block, axis, distance):
    devices = range(lax.axis_size(axis))
    route = [(i - distance, i) for i in devices if i - distance in devices]
    return lax.ppermute(block, axis, route)


def swapped(block, axis):
    return lax.ppermute(block, axis, [(0, 1), (1, 0)])


def rounded(values):
    return lax.optimization_barrier(values.astype(BF16)).astype(F32)


def matmul(left_op, right_op):
    return jnp.dot(left_op, right_op, preferred_element_type=F32)


def matmul_left(left_op, right_op):
    return lax.dot_general(left_op, right_op, (((0,), (0,)), ((), ())), preferred_element_type=F32)


def matmul_right(left_op, right_op):
    return lax.dot_general(left_op, right_op, (((1,), (1,)), ((), ())), preferred_element_type=F32)


def norm_rows(values):
    inv_rms = lax.rsqrt(jnp.mean(values * values, axis=-1, keepdims=True) + EPSILON)
    return (values * inv_rms, inv_rms)


def norm_back(dnormed, normed, inv_rms):
    return inv_rms * dnormed - normed * inv_rms * jnp.mean(dnormed * normed, axis=-1, keepdims=True)


def head_sums(values, head):
    heads = values.shape[1] // head
    owner = (jnp.arange(values.shape[1])[:, None] // head == jnp.arange(heads)[None, :]).astype(F32)
    sums = jnp.dot(values, owner, precision=lax.Precision.HIGHEST, preferred_element_type=F32)
    return jnp.dot(sums, owner.T, precision=lax.Precision.HIGHEST, preferred_element_type=F32)


def norm_heads(values, head):
    inv_rms = lax.rsqrt(head_sums(values * values, head) / head + EPSILON)
    return (values * inv_rms, inv_rms)


def norm_heads_back(dnormed, normed, inv_rms, head):
    return inv_rms * dnormed - normed * inv_rms * (head_sums(dnormed * normed, head) / head)


def busy(microseconds):
    return pl.CostEstimate(flops=int(microseconds), bytes_accessed=1 << 16, transcendentals=0)


def corners():
    me = lax.axis_index("fsdp")
    beside = me + 1 - 2 * lax.rem(me, 2)
    across = lax.rem(me + 2, 4)
    return me, beside, across, lax.rem(beside + 2, 4)


def greet_sides():
    _, beside, across, _ = corners()
    barrier = pltpu.get_barrier_semaphore()
    for target in (beside, across):
        pl.semaphore_signal(barrier, inc=1, device_id={"fsdp": target}, device_id_type=MESH)
    pl.semaphore_wait(barrier, 2)


def to_side(src, dst, send_sem, recv_sem, target):
    return pltpu.make_async_remote_copy(
        src_ref=src,
        dst_ref=dst,
        send_sem=send_sem,
        recv_sem=recv_sem,
        device_id={"fsdp": target},
        device_id_type=MESH,
    )


class SideGather:
    def __init__(self, block, whole, send_sem, recv_sem, own_sem):
        me, beside, across, _ = corners()
        rows = block.shape[0]
        half = rows // 2

        def part(owner, start, size):
            return whole.at[pl.ds(pl.multiple_of(owner * rows + start, half), size)]

        self.first = to_side(block, part(me, 0, rows), send_sem.at[0], recv_sem.at[0], beside)
        self.second = to_side(block, part(me, 0, rows), send_sem.at[1], recv_sem.at[1], across)
        at = part(beside, 0, half)
        self.third = to_side(at, at, send_sem.at[2], recv_sem.at[2], across)
        at = part(across, half, half)
        self.fourth = to_side(at, at, send_sem.at[3], recv_sem.at[3], beside)
        self.own = pltpu.make_async_copy(block, part(me, 0, rows), own_sem)

    def start(self):
        self.first.start()
        self.second.start()
        self.own.start()

    def relay(self):
        self.first.wait_recv()
        self.third.start()
        self.second.wait_recv()
        self.fourth.start()

    def finish(self):
        self.own.wait()
        self.first.wait_send()
        self.second.wait_send()
        self.third.wait()
        self.fourth.wait()


def gather_kernel(block, whole, send_sem, recv_sem, own_sem):
    greet_sides()
    gather = SideGather(block, whole, send_sem, recv_sem, own_sem)
    gather.start()
    gather.relay()
    gather.finish()


def gathered(array, collective_id):
    rows, width = array.shape
    assert lax.axis_size("fsdp") == 4
    dma = pltpu.SemaphoreType.DMA
    return pl.pallas_call(
        gather_kernel,
        out_shape=jax.ShapeDtypeStruct((4 * rows, width), array.dtype),
        in_specs=[pl.BlockSpec(memory_space=pltpu.VMEM)],
        out_specs=pl.BlockSpec(memory_space=pltpu.VMEM),
        scratch_shapes=[dma((4,)), dma((4,)), dma],
        compiler_params=pltpu.CompilerParams(
            collective_id=collective_id, has_side_effects=True, vmem_limit_bytes=8 << 20
        ),
        cost_estimate=busy(25),
    )(array)


def gather_swap_kernel(block, pieces, whole, swapped_out, send_sem, recv_sem, own_sem, cross_send, cross_recv, keep_sem):
    me, beside, across, opposite = corners()
    barrier = pltpu.get_barrier_semaphore()
    for target in (beside, across, opposite):
        pl.semaphore_signal(barrier, inc=1, device_id={"fsdp": target}, device_id_type=MESH)
    pl.semaphore_wait(barrier, 3)
    gather = SideGather(block, whole, send_sem, recv_sem, own_sem)
    gather.start()
    crossing = []
    for step in range(1, 4):
        target = lax.rem(me + step, 4)
        crossing.append(
            to_side(pieces.at[target], swapped_out.at[me], cross_send.at[step], cross_recv.at[step], target)
        )
        crossing[-1].start()
    keep = pltpu.make_async_copy(pieces.at[me], swapped_out.at[me], keep_sem)
    keep.start()
    gather.relay()
    gather.finish()
    keep.wait()
    for copy in crossing:
        copy.wait()


def gathered_swapped(array, pieces, collective_id):
    rows, width = array.shape
    dma = pltpu.SemaphoreType.DMA
    vmem = pl.BlockSpec(memory_space=pltpu.VMEM)
    hbm = pl.BlockSpec(memory_space=pl.ANY)
    return pl.pallas_call(
        gather_swap_kernel,
        out_shape=(
            jax.ShapeDtypeStruct((4 * rows, width), array.dtype),
            jax.ShapeDtypeStruct(pieces.shape, pieces.dtype),
        ),
        in_specs=[vmem, hbm],
        out_specs=[vmem, hbm],
        scratch_shapes=[dma((4,)), dma((4,)), dma, dma((4,)), dma((4,)), dma],
        compiler_params=pltpu.CompilerParams(
            collective_id=collective_id, has_side_effects=True, vmem_limit_bytes=8 << 20
        ),
        cost_estimate=busy(25),
    )(array, pieces)


class SideReduce:
    def __init__(self, blocks, total, beside_got, across_got, passed, passed_got, send_sem, recv_sem):
        self.refs = blocks, total, beside_got, across_got, passed, passed_got
        me, beside, across, opposite = corners()
        self.me, self.beside, self.across = me, beside, across
        self.copies = []
        for index, (turn, target, got) in enumerate(((0, beside, beside_got), (1, across, across_got))):
            for slot, owner in ((1, opposite), (0, target)):
                self.copies.append(
                    to_side(
                        blocks.at[self.part(owner, turn)],
                        got.at[slot],
                        send_sem.at[2 * index + slot],
                        recv_sem.at[2 * index + slot],
                        target,
                    )
                )
        self.onward = [
            to_side(passed.at[turn], passed_got.at[turn], send_sem.at[4 + turn], recv_sem.at[4 + turn], owner)
            for turn, owner in ((0, across), (1, beside))
        ]

    def part(self, owner, turn):
        half = self.refs[1].shape[0] // 2
        return pl.ds(pl.multiple_of(owner * 2 * half + turn * half, half), half)

    def start(self):
        for index in (0, 2, 1, 3):
            self.copies[index].start()

    def relay(self):
        blocks, _, beside_got, across_got, passed, _ = self.refs
        for turn, owner, index, got in ((0, self.across, 0, beside_got), (1, self.beside, 2, across_got)):
            self.copies[index].wait_recv()
            passed[turn] = (blocks[self.part(owner, turn)].astype(F32) + got[1].astype(F32)).astype(BF16)
            self.onward[turn].start()

    def finish(self):
        blocks, total, beside_got, across_got, _, passed_got = self.refs
        half = total.shape[0] // 2
        for turn, index, got in ((0, 1, beside_got), (1, 3, across_got)):
            self.copies[index].wait_recv()
            total[pl.ds(turn * half, half)] = blocks[self.part(self.me, turn)].astype(F32) + got[0].astype(F32)
        for turn in range(2):
            self.onward[turn].wait_recv()
            at = pl.ds(turn * half, half)
            total[at] = total[at] + passed_got[turn].astype(F32)
        for copy in self.copies + self.onward:
            copy.wait_send()


def reduce_kernel(blocks, total, beside_got, across_got, passed, passed_got, send_sem, recv_sem):
    greet_sides()
    reduction = SideReduce(blocks, total, beside_got, across_got, passed, passed_got, send_sem, recv_sem)
    reduction.start()
    reduction.relay()
    reduction.finish()


def reduce_pair_kernel(
    blocks,
    give_a,
    give_b,
    total,
    got_a,
    got_b,
    beside_got,
    across_got,
    passed,
    passed_got,
    send_sem,
    recv_sem,
    pair_send,
    pair_recv,
):
    other = {"section": 1 - lax.axis_index("section")}
    _, beside, across, _ = corners()
    barrier = pltpu.get_barrier_semaphore()
    for target in ({"fsdp": beside}, {"fsdp": across}, other):
        pl.semaphore_signal(barrier, inc=1, device_id=target, device_id_type=MESH)
    pl.semaphore_wait(barrier, 3)
    reduction = SideReduce(blocks, total, beside_got, across_got, passed, passed_got, send_sem, recv_sem)
    reduction.start()
    pairs = [
        pltpu.make_async_remote_copy(
            src_ref=src,
            dst_ref=dst,
            send_sem=pair_send.at[index],
            recv_sem=pair_recv.at[index],
            device_id=other,
            device_id_type=MESH,
        )
        for index, (src, dst) in enumerate(((give_a, got_a), (give_b, got_b)))
    ]
    for copy in pairs:
        copy.start()
    reduction.relay()
    reduction.finish()
    for copy in pairs:
        copy.wait()


def reduced_swapping(partial, give_a, give_b, collective_id):
    rows, width = partial.shape[0] // 4, partial.shape[1]
    dma = pltpu.SemaphoreType.DMA
    pair = pltpu.VMEM((2, rows // 2, width), BF16)
    vmem = pl.BlockSpec(memory_space=pltpu.VMEM)
    hbm = pl.BlockSpec(memory_space=pl.ANY)
    return pl.pallas_call(
        reduce_pair_kernel,
        out_shape=(
            jax.ShapeDtypeStruct((rows, width), F32),
            jax.ShapeDtypeStruct(give_a.shape, BF16),
            jax.ShapeDtypeStruct(give_b.shape, BF16),
        ),
        in_specs=[vmem, hbm, hbm],
        out_specs=[vmem, hbm, hbm],
        scratch_shapes=[pair, pair, pair, pair, dma((6,)), dma((6,)), dma((2,)), dma((2,))],
        compiler_params=pltpu.CompilerParams(
            collective_id=collective_id, has_side_effects=True, vmem_limit_bytes=16 << 20
        ),
        cost_estimate=busy(25),
    )(partial.astype(BF16), give_a, give_b)


def reduced(partial, collective_id):
    rows, width = partial.shape[0] // 4, partial.shape[1]
    assert lax.axis_size("fsdp") == 4
    dma = pltpu.SemaphoreType.DMA
    pair = pltpu.VMEM((2, rows // 2, width), BF16)
    return pl.pallas_call(
        reduce_kernel,
        out_shape=jax.ShapeDtypeStruct((rows, width), F32),
        in_specs=[pl.BlockSpec(memory_space=pltpu.VMEM)],
        out_specs=pl.BlockSpec(memory_space=pltpu.VMEM),
        scratch_shapes=[pair, pair, pair, pair, dma((6,)), dma((6,))],
        compiler_params=pltpu.CompilerParams(
            collective_id=collective_id, has_side_effects=True, vmem_limit_bytes=16 << 20
        ),
        cost_estimate=busy(25),
    )(partial.astype(BF16))


def tail_kernel(
    counts,
    gate_in,
    up_in,
    down_in,
    query_in,
    kv_in,
    proj_in,
    conv_b_in,
    conv_c_in,
    conv_x_in,
    conv_o_in,
    small_in,
    second_gu_in,
    second_down_in,
    gu_out,
    down_out,
    rest_out,
    a_own,
    a_other,
    a_sum,
    a_done,
    b_own,
    b_other,
    b_sum,
    b_done,
    c_own,
    c_other,
    c_got,
    own_sem,
    pair_send,
    pair_recv,
    c_own_sem,
    c_pair_send,
    c_pair_recv,
    c_send,
    c_recv,
    a_up_send,
    a_up_recv,
    a_back_send,
    a_back_recv,
    a_out_send,
    b_up_send,
    b_up_recv,
    b_back_send,
    b_back_recv,
    b_out_send,
    b_keep_sem,
    gu_recv,
    down_recv,
    rest_recv,
    second_send,
    second_recv,
):
    n_ctx, n_fsdp = counts
    section = lax.axis_index("section")
    place = lax.axis_index("ctx")
    group = lax.axis_index("fsdp")
    other = 1 - section
    a_chunks, a_rows, a_width = a_own.shape
    b_chunks, b_rows, b_width = b_own.shape
    half = gate_in.shape[0] // n_fsdp // 2
    subs = half // a_rows
    per_kind = n_fsdp * subs
    down_half = down_in.shape[0] // 2
    down_chunks = down_half // b_rows
    c_rows = c_own.shape[1]
    mixers = (query_in, kv_in, proj_in, conv_b_in, conv_c_in, conv_x_in, conv_o_in)
    n_mix = len(mixers)
    cut = 3 * half // b_rows
    c_parts = ((0, cut), (cut, c_rows // b_rows))
    paired = a_chunks // 2
    mix_chunks = b_chunks - down_chunks
    ticks = paired + mix_chunks // 2
    tail = 2 * (n_ctx - 1)

    barrier = pltpu.get_barrier_semaphore()
    for step in range(1, 2 * n_fsdp):
        flat = lax.rem(section * n_fsdp + group + step, 2 * n_fsdp)
        pl.semaphore_signal(
            barrier,
            inc=1,
            device_id={"section": flat // n_fsdp, "fsdp": lax.rem(flat, n_fsdp)},
            device_id_type=MESH,
        )

    @pl.when(place > 0)
    def _():
        pl.semaphore_signal(barrier, inc=1, device_id={"ctx": place - 1}, device_id_type=MESH)

    @pl.when(place < n_ctx - 1)
    def _():
        pl.semaphore_signal(barrier, inc=1, device_id={"ctx": place + 1}, device_id_type=MESH)

    at_edge = (place == 0) | (place == n_ctx - 1)

    @pl.when(at_edge)
    def _():
        pl.semaphore_wait(barrier, 2 * n_fsdp)

    @pl.when(jnp.logical_not(at_edge))
    def _():
        pl.semaphore_wait(barrier, 2 * n_fsdp + 1)

    def half_rows(owner, which):
        return pl.ds(pl.multiple_of(owner * (2 * half) + which * half, half), half)

    a_part, b_part = a_rows // 2, b_width // 2

    def a_at(buffer, k, way):
        return buffer.at[k, pl.ds(way * a_part, a_part)]

    def b_at(buffer, k, way):
        return buffer.at[k, :, pl.ds(way * b_part, b_part)]

    def opening(k, way):
        copies = []
        kind, rest = divmod(k, per_kind)
        owner, sub = divmod(rest, subs)
        source = (gate_in, up_in)[kind]
        spots = []
        for which in (section, other):
            start = owner * (2 * half) + which * half + sub * a_rows + way * a_part
            spots.append(source.at[pl.ds(pl.multiple_of(start, a_part), a_part)])
        spot = 2 * k + way
        copies.append((spots, a_at(a_own, k, way), a_at(a_other, k, way), spot))
        if k < down_chunks:
            spots = [
                down_in.at[
                    pl.ds(pl.multiple_of(which * down_half + k * b_rows, b_rows), b_rows),
                    pl.ds(way * b_part, b_part),
                ]
                for which in (section, other)
            ]
            copies.append((spots, b_at(b_own, k, way), b_at(b_other, k, way), 2 * a_chunks + spot))
        for (mine, theirs), own_dst, other_dst, spot in copies:
            pltpu.make_async_copy(mine, own_dst, own_sem.at[spot]).start()
            pltpu.make_async_remote_copy(
                src_ref=theirs,
                dst_ref=other_dst,
                send_sem=pair_send.at[spot],
                recv_sem=pair_recv.at[spot],
                device_id={"section": other},
                device_id_type=MESH,
            ).start()

    for k in range(a_chunks):
        for way in range(2):
            opening(k, way)
    c_local, c_pair = ([], []), ([], [])
    for kind, source in enumerate(mixers):
        part = 0 if kind < 3 else 1
        for owner in range(n_fsdp):
            index = owner * (n_mix + 1) + kind
            place_at = pl.ds(kind * half, half)
            c_local[part].append(
                pltpu.make_async_copy(
                    source.at[half_rows(owner, section)], c_own.at[owner, place_at], c_own_sem.at[index]
                )
            )
            c_pair[part].append(
                pltpu.make_async_remote_copy(
                    src_ref=source.at[half_rows(owner, other)],
                    dst_ref=c_other.at[owner, place_at],
                    send_sem=c_pair_send.at[index],
                    recv_sem=c_pair_recv.at[index],
                    device_id={"section": other},
                    device_id_type=MESH,
                )
            )
    for owner in range(n_fsdp):
        small_at = pl.ds(n_mix * half, c_rows - n_mix * half)
        index = owner * (n_mix + 1) + n_mix
        c_local[1].append(
            pltpu.make_async_copy(small_in.at[section], c_own.at[owner, small_at], c_own_sem.at[index])
        )
        c_pair[1].append(
            pltpu.make_async_remote_copy(
                src_ref=small_in.at[other],
                dst_ref=c_other.at[owner, small_at],
                send_sem=c_pair_send.at[index],
                recv_sem=c_pair_recv.at[index],
                device_id={"section": other},
                device_id_type=MESH,
            )
        )
    for part in range(2):
        for copy in c_pair[part]:
            copy.start()
        for copy in c_local[part]:
            copy.start()
    b_own[b_chunks - 1] = jnp.zeros((b_rows, b_width), BF16)
    _, beside, across, opposite = corners()

    def span(first, last):
        return pl.ds(first * b_rows, (last - first) * b_rows)

    def mixer_spans(part):
        first, last = c_parts[part]
        middle = (first + last) // 2
        return (first, middle, beside, across), (middle, last, across, beside)

    def mixer_copies(part):
        opening, onward = [], []
        for turn, (first, last, near, far) in enumerate(mixer_spans(part)):
            at = span(first, last)
            for slot, owner in ((0, opposite), (1, near)):
                opening.append(
                    to_side(
                        c_own.at[owner, at],
                        c_got.at[slot, at],
                        c_send.at[part, 3 * turn + slot],
                        c_recv.at[part, 3 * turn + slot],
                        near,
                    )
                )
            onward.append(
                to_side(
                    c_own.at[far, at],
                    c_got.at[2, at],
                    c_send.at[part, 3 * turn + 2],
                    c_recv.at[part, 3 * turn + 2],
                    far,
                )
            )
        return opening, onward

    def mixer_sum(part, owner):
        kinds = range(3) if part == 0 else range(3, n_mix + 1)
        first, last = c_parts[part]
        for kind in kinds:
            size = half if kind < n_mix else c_rows - n_mix * half
            at = c_own.at[owner, pl.ds(kind * half, size)]
            index = owner * (n_mix + 1) + kind
            pltpu.make_async_copy(at, at, c_own_sem.at[index]).wait()
            pltpu.make_async_copy(at, at, c_pair_recv.at[index]).wait()

        def add(index, carry):
            at = pl.ds(pl.multiple_of(index * b_rows, b_rows), b_rows)
            c_own[owner, at] = (c_own[owner, at].astype(F32) + c_other[owner, at].astype(F32)).astype(BF16)
            return carry

        lax.fori_loop(first, last, add, 0)

    def mixer_out(part):
        opening, _ = mixer_copies(part)
        for index in (0, 2, 1, 3):
            opening[index].start()

    def mixer_on(part):
        opening, onward = mixer_copies(part)
        for turn, (first, last, near, far) in enumerate(mixer_spans(part)):
            opening[2 * turn].wait_recv()

            def add(index, carry, far=far):
                at = pl.ds(pl.multiple_of(index * b_rows, b_rows), b_rows)
                c_own[far, at] = (c_own[far, at].astype(F32) + c_got[0, at].astype(F32)).astype(BF16)
                return carry

            lax.fori_loop(first, last, add, 0)
            onward[turn].start()

    def mixer_in(part):
        opening, onward = mixer_copies(part)
        for turn in range(2):
            opening[2 * turn + 1].wait_recv()
            onward[turn].wait_recv()
        first, last = c_parts[part]

        def add(index, carry):
            at = pl.ds(pl.multiple_of(index * b_rows, b_rows), b_rows)
            total = c_own[group, at].astype(F32) + c_got[1, at].astype(F32) + c_got[2, at].astype(F32)
            b_own[down_chunks + index] = total.astype(BF16)
            return carry

        lax.fori_loop(first, last, add, 0)

    strip = half // n_ctx

    def second_copies(remote):
        for index in range(n_ctx * n_fsdp * 2):
            source, kind = index // 2, index % 2
            turn, owner = source // n_fsdp, source % n_fsdp
            src = second_gu_in.at[turn, owner, kind]
            dst = gu_out.at[
                kind,
                pl.ds(pl.multiple_of(section * half + turn * strip, strip), strip),
                pl.ds(owner * a_width, a_width),
            ]
            if remote:
                pltpu.make_async_remote_copy(
                    src_ref=src,
                    dst_ref=dst,
                    send_sem=second_send.at[0],
                    recv_sem=second_recv,
                    device_id={"section": 1},
                    device_id_type=MESH,
                ).start()
            else:
                pltpu.make_async_copy(src, dst, second_send.at[0]).start()

    def second_start():
        down_at = down_out.at[pl.ds(pl.multiple_of(section * down_half, b_rows), down_half)]

        @pl.when(section == 1)
        def _():
            second_copies(False)
            pltpu.make_async_copy(second_down_in, down_at, second_send.at[1]).start()

        @pl.when(section == 0)
        def _():
            second_copies(True)
            pltpu.make_async_remote_copy(
                src_ref=second_down_in,
                dst_ref=down_at,
                send_sem=second_send.at[1],
                recv_sem=down_recv,
                device_id={"section": 1},
                device_id_type=MESH,
            ).start()

    def a_target(k, way):
        kind = k // per_kind
        rest = lax.rem(k, per_kind)
        owner = rest // subs
        sub = lax.rem(rest, subs)
        start = section * half + sub * a_rows + way * a_part
        spot = gu_out.at[
            kind,
            pl.ds(pl.multiple_of(start, a_part), a_part),
            pl.ds(pl.multiple_of(group * a_width, 128), a_width),
        ]
        return kind, owner, spot

    def a_hand_out(k, way):
        kind, owner, spot = a_target(k, way)
        is_mine = (section == 0) & (group == owner)
        slot = 2 * k + way
        a_ref = a_at(a_done, k, way)

        @pl.when(is_mine)
        def _():
            pltpu.make_async_copy(a_ref, spot, a_out_send.at[slot]).start()

        @pl.when(jnp.logical_not(is_mine))
        def _():
            pltpu.make_async_remote_copy(
                src_ref=a_ref,
                dst_ref=spot,
                send_sem=a_out_send.at[slot],
                recv_sem=gu_recv.at[kind, section * n_fsdp + group],
                device_id={"section": 0, "fsdp": owner},
                device_id_type=MESH,
            ).start()

    def down_hand_out(k, way):
        slot = 2 * k + way
        b_ref = b_at(b_done, k, way)
        at = down_out.at[
            pl.ds(pl.multiple_of(section * down_half + k * b_rows, b_rows), b_rows),
            pl.ds(way * b_part, b_part),
        ]

        @pl.when(section == 0)
        def _():
            pltpu.make_async_copy(b_ref, at, b_out_send.at[slot]).start()

        @pl.when(section == 1)
        def _():
            pltpu.make_async_remote_copy(
                src_ref=b_ref,
                dst_ref=at,
                send_sem=b_out_send.at[slot],
                recv_sem=down_recv,
                device_id={"section": 0},
                device_id_type=MESH,
            ).start()

    def mix_hand_out(k, way):
        slot = 2 * k + way
        b_ref = b_at(b_done, k, way)
        at = rest_out.at[
            section,
            pl.ds(pl.multiple_of((k - down_chunks) * b_rows, b_rows), b_rows),
            pl.ds(way * b_part, b_part),
        ]
        pltpu.make_async_copy(b_ref, at, b_keep_sem.at[slot]).start()
        pltpu.make_async_remote_copy(
            src_ref=b_ref,
            dst_ref=at,
            send_sem=b_out_send.at[slot],
            recv_sem=rest_recv,
            device_id={"section": other},
            device_id_type=MESH,
        ).start()

    def chain_copy(at, sems, slot, target):
        return pltpu.make_async_remote_copy(
            src_ref=at,
            dst_ref=at,
            send_sem=sems[0].at[slot],
            recv_sem=sems[1].at[slot],
            device_id={"ctx": target},
            device_id_type=MESH,
        )

    class Gates:
        hand_out = staticmethod(a_hand_out)

        @staticmethod
        def view(buffer, k, way):
            return a_at(buffer, k, way)

        own, sums, done = a_own, a_sum, a_done
        up, back = (a_up_send, a_up_recv), (a_back_send, a_back_recv)

        @staticmethod
        def term(k, way):
            slot = 2 * k + way
            at = a_at(a_own, k, way)
            pltpu.make_async_copy(at, at, own_sem.at[slot]).wait()
            pltpu.make_async_copy(at, at, pair_recv.at[slot]).wait()
            return at[...].astype(F32) + a_at(a_other, k, way)[...].astype(F32)

    class Downs:
        hand_out = staticmethod(down_hand_out)

        @staticmethod
        def view(buffer, k, way):
            return b_at(buffer, k, way)

        own, sums, done = b_own, b_sum, b_done
        up, back = (b_up_send, b_up_recv), (b_back_send, b_back_recv)

        @staticmethod
        def term(k, way):
            slot = 2 * a_chunks + 2 * k + way
            at = b_at(b_own, k, way)
            pltpu.make_async_copy(at, at, own_sem.at[slot]).wait()
            pltpu.make_async_copy(at, at, pair_recv.at[slot]).wait()
            return at[...].astype(F32) + b_at(b_other, k, way)[...].astype(F32)

    class Mixed(Downs):
        hand_out = staticmethod(mix_hand_out)

        @staticmethod
        def term(k, way):
            return b_at(b_own, k, way)[...].astype(F32)

    def upward(item, k, way, rank, ahead, behind):
        slot = 2 * k + way
        term = item.term(k, way)
        sums = item.view(item.sums, k, way)

        @pl.when(rank == 0)
        def _():
            sums[...] = term.astype(BF16)

        @pl.when(rank > 0)
        def _():
            chain_copy(sums, item.up, slot, behind).wait_recv()

        @pl.when((rank > 0) & (rank < n_ctx - 1))
        def _():
            sums[...] = (term + sums[...].astype(F32)).astype(BF16)

        @pl.when(rank < n_ctx - 1)
        def _():
            chain_copy(sums, item.up, slot, ahead).start()

        @pl.when(rank == n_ctx - 1)
        def _():
            done = item.view(item.done, k, way)
            done[...] = (term + sums[...].astype(F32)).astype(BF16)
            chain_copy(done, item.back, slot, behind).start()
            item.hand_out(k, way)

    def backward(item, k, way, rank, ahead, behind):
        slot = 2 * k + way
        done = item.view(item.done, k, way)
        chain_copy(done, item.back, slot, ahead).wait_recv()

        @pl.when(rank > 0)
        def _():
            chain_copy(done, item.back, slot, behind).start()

        item.hand_out(k, way)

    def on_step(action, step, active, *where):
        early = active & (step < paired)

        @pl.when(early)
        def _():
            at = jnp.clip(step, 0, paired - 1)
            for index in range(2):
                action(Gates, 2 * at + index, *where)

            @pl.when(lax.rem(at, 4) < 3)
            def _():
                action(Downs, 3 * (at // 4) + lax.rem(at, 4), *where)

        @pl.when(active & jnp.logical_not(early))
        def _():
            at = jnp.clip(step - paired, 0, mix_chunks // 2 - 1)
            for index in range(2):
                action(Mixed, down_chunks + 2 * at + index, *where)

    lanes = []
    for way in range(2):
        rank = place if way == 0 else n_ctx - 1 - place
        ahead = place + 1 if way == 0 else place - 1
        behind = place - 1 if way == 0 else place + 1
        lanes.append((way, rank, ahead, behind))

    def tick_step(tick, carry):
        for part, start in ((0, 1), (1, 5)):
            for owner in range(n_fsdp):

                @pl.when(tick == start + owner)
                def _(part=part, owner=owner):
                    mixer_sum(part, owner)

        events = (
            (4, mixer_out, 0),
            (8, mixer_out, 1),
            (9, mixer_on, 0),
            (13, mixer_on, 1),
            (paired - 1, mixer_in, 0),
            (paired + 3, mixer_in, 1),
        )
        for moment, action, part in events:

            @pl.when(tick == moment)
            def _(action=action, part=part):
                action(part)

        for way, rank, ahead, behind in lanes:
            step = tick - 2 * rank
            on_step(upward, step, (step >= 0) & (step < ticks), way, rank, ahead, behind)
            late = tick - 2 * (tail - rank)
            on_step(
                backward,
                late,
                (late >= 0) & (late < ticks) & (rank < n_ctx - 1),
                way,
                rank,
                ahead,
                behind,
            )

        return carry

    second_start()
    lax.fori_loop(0, ticks + 2 * tail, tick_step, 0)

    for part in range(2):
        for copy in c_pair[part]:
            copy.wait_send()
        opening, onward = mixer_copies(part)
        for copy in opening + onward:
            copy.wait_send()

    def settle(k, carry):
        for way, rank, ahead, behind in lanes:
            slot = 2 * k + way
            a_ref, b_ref = a_at(a_own, k, way), b_at(b_own, k, way)
            pltpu.make_async_copy(a_ref, a_ref, pair_send.at[slot]).wait()

            @pl.when(k < down_chunks)
            def _(b_ref=b_ref, slot=slot):
                pltpu.make_async_copy(b_ref, b_ref, pair_send.at[2 * a_chunks + slot]).wait()

            for item in (Gates, Mixed):

                @pl.when(rank < n_ctx - 1)
                def _(item=item, slot=slot, k=k, way=way, ahead=ahead):
                    chain_copy(item.view(item.sums, k, way), item.up, slot, ahead).wait_send()

                @pl.when(rank > 0)
                def _(item=item, slot=slot, k=k, way=way, behind=behind):
                    chain_copy(item.view(item.done, k, way), item.back, slot, behind).wait_send()

            pltpu.make_async_copy(a_ref, a_ref, a_out_send.at[slot]).wait()
            pltpu.make_async_copy(b_ref, b_ref, b_out_send.at[slot]).wait()

            @pl.when(k >= down_chunks)
            def _(b_ref=b_ref, slot=slot):
                pltpu.make_async_copy(b_ref, b_ref, b_keep_sem.at[slot]).wait()

        return carry

    lax.fori_loop(0, a_chunks, settle, 0)
    pltpu.make_async_copy(second_gu_in, second_gu_in, second_send.at[0]).wait()
    pltpu.make_async_copy(second_down_in, second_down_in, second_send.at[1]).wait()

    @pl.when(section == 0)
    def _():
        for kind in range(2):
            for source in range(2 * n_fsdp):

                @pl.when(group != source)
                def _(kind=kind, source=source):
                    region = gu_out.at[
                        kind,
                        pl.ds((source // n_fsdp) * half, half),
                        pl.ds((source % n_fsdp) * a_width, a_width),
                    ]
                    pltpu.make_async_copy(region, region, gu_recv.at[kind, source]).wait()

    @pl.when(section == 1)
    def _():
        pltpu.make_async_copy(second_gu_in, second_gu_in, second_recv).wait()

    region = down_out.at[pl.ds(pl.multiple_of(other * down_half, b_rows), down_half)]
    pltpu.make_async_copy(region, region, down_recv).wait()
    region = rest_out.at[other]
    pltpu.make_async_copy(region, region, rest_recv).wait()


def summed_gradients(first, mixers, small, second_gu, second_down):
    n_ctx, n_fsdp = lax.axis_size("ctx"), lax.axis_size("fsdp")
    gate, up, down = first
    half = gate.shape[0] // n_fsdp // 2
    a_rows, b_rows = half // 4, half * 3 // 8
    a_chunks = 2 * n_fsdp * 4
    a_width, b_width = gate.shape[1], down.shape[1]
    c_rows = len(mixers) * half + small.shape[1]
    down_chunks = down.shape[0] // 2 // b_rows
    b_chunks = down_chunks + c_rows // b_rows + 1
    assert a_chunks == b_chunks and c_rows % b_rows == 0
    assert down_chunks * 8 == a_chunks * 3 and (b_chunks - down_chunks) % 2 == 0
    rest = b_chunks - down_chunks
    dma = pltpu.SemaphoreType.DMA
    loads = 2 * (a_chunks + down_chunks)
    pieces = n_fsdp * (len(mixers) + 1)
    return pl.pallas_call(
        functools.partial(tail_kernel, (n_ctx, n_fsdp)),
        out_shape=(
            jax.ShapeDtypeStruct((2, 2 * half, n_fsdp * a_width), BF16),
            jax.ShapeDtypeStruct(down.shape, BF16),
            jax.ShapeDtypeStruct((2, rest * b_rows, b_width), BF16),
        ),
        in_specs=[pl.BlockSpec(memory_space=pl.ANY)] * (6 + len(mixers)),
        out_specs=[pl.BlockSpec(memory_space=pl.ANY)] * 3,
        scratch_shapes=[
            pltpu.VMEM((a_chunks, a_rows, a_width), BF16),
            pltpu.VMEM((a_chunks, a_rows, a_width), BF16),
            pltpu.VMEM((a_chunks, a_rows, a_width), BF16),
            pltpu.VMEM((a_chunks, a_rows, a_width), BF16),
            pltpu.VMEM((b_chunks, b_rows, b_width), BF16),
            pltpu.VMEM((down_chunks, b_rows, b_width), BF16),
            pltpu.VMEM((b_chunks, b_rows, b_width), BF16),
            pltpu.VMEM((b_chunks, b_rows, b_width), BF16),
            pltpu.VMEM((n_fsdp, c_rows, b_width), BF16),
            pltpu.VMEM((n_fsdp, c_rows, b_width), BF16),
            pltpu.VMEM((n_fsdp - 1, c_rows, b_width), BF16),
            dma((loads,)),
            dma((loads,)),
            dma((loads,)),
            dma((pieces,)),
            dma((pieces,)),
            dma((pieces,)),
            dma((2, 6)),
            dma((2, 6)),
            dma((2 * a_chunks,)),
            dma((2 * a_chunks,)),
            dma((2 * a_chunks,)),
            dma((2 * a_chunks,)),
            dma((2 * a_chunks,)),
            dma((2 * b_chunks,)),
            dma((2 * b_chunks,)),
            dma((2 * b_chunks,)),
            dma((2 * b_chunks,)),
            dma((2 * b_chunks,)),
            dma((2 * b_chunks,)),
            dma((2, 2 * n_fsdp)),
            dma,
            dma,
            dma((2,)),
            dma,
        ],
        compiler_params=pltpu.CompilerParams(
            collective_id=6, has_side_effects=True, vmem_limit_bytes=56 << 20
        ),
        cost_estimate=busy(160),
    )(gate, up, down, *mixers, small, second_gu, second_down)


class Columns:
    def __init__(self, holder, sources, targets, send_sem, recv_sem, pair_send, pair_recv, own_sem):
        self.count = 4
        self.holder = holder
        self.section = lax.axis_index("section")
        self.me = lax.axis_index("fsdp")
        self.sources, self.targets = sources, targets
        self.sems = send_sem, recv_sem, pair_send, pair_recv, own_sem
        self.rows = sources[0].shape[0]
        self.wide = targets[0].shape[1]
        self.steps = [(step, kind) for step in range(1, self.count) for kind in range(2)]

    def at_rows(self, out, owner):
        return out.at[pl.ds(pl.multiple_of(owner * self.rows, self.rows), self.rows)]

    def at_columns(self, source, owner):
        return source.at[:, pl.ds(pl.multiple_of(owner * self.wide, 128), self.wide)]

    def crossing(self, step, kind):
        target = lax.rem(self.me + step, self.count)
        return to_side(
            self.at_columns(self.sources[kind], target),
            self.at_rows(self.targets[kind], self.me),
            self.sems[0].at[kind, step],
            self.sems[1].at[kind, step],
            target,
        )

    def handed(self, step, kind):
        if kind == 2:
            src, dst = self.sources[2], self.targets[2]
        else:
            origin = lax.rem(self.me + self.count - step, self.count)
            dst = self.at_rows(self.targets[kind], origin)
            src = self.at_columns(self.sources[kind], self.me) if step == 0 else dst
        return pltpu.make_async_remote_copy(
            src_ref=src,
            dst_ref=dst,
            send_sem=self.sems[2].at[kind, step],
            recv_sem=self.sems[3].at[kind, step],
            device_id={"section": 1 - self.section},
            device_id_type=MESH,
        )

    def kept(self, kind):
        if kind == 2:
            return pltpu.make_async_copy(self.sources[2], self.targets[2], self.sems[4].at[2])
        return pltpu.make_async_copy(
            self.at_columns(self.sources[kind], self.me),
            self.at_rows(self.targets[kind], self.me),
            self.sems[4].at[kind],
        )

    def start(self):
        @pl.when(self.section == self.holder)
        def _():
            for step, kind in self.steps:
                self.crossing(step, kind).start()
            for kind in range(3):
                self.handed(0, kind).start()
            for kind in range(3):
                self.kept(kind).start()

    def relay(self):
        @pl.when(self.section == self.holder)
        def _():
            for step, kind in self.steps:
                self.crossing(step, kind).wait_recv()
                self.handed(step, kind).start()

    def arrive(self):
        every = [(0, kind) for kind in range(3)] + self.steps

        @pl.when(self.section == self.holder)
        def _():
            for kind in range(3):
                self.kept(kind).wait()

        @pl.when(self.section != self.holder)
        def _():
            for step, kind in every:
                self.handed(step, kind).wait_recv()

    def finish(self):
        every = [(0, kind) for kind in range(3)] + self.steps

        @pl.when(self.section == self.holder)
        def _():
            for step, kind in self.steps:
                self.crossing(step, kind).wait_send()
            for step, kind in every:
                self.handed(step, kind).wait_send()


class Chain:
    def __init__(self, count):
        self.count = count
        self.place = lax.axis_index("ctx")
        self.has_next = self.place < count - 1
        self.has_last = self.place > 0


def greet_mixed(chain, targets):
    barrier = pltpu.get_barrier_semaphore()
    for target in targets:
        pl.semaphore_signal(barrier, inc=1, device_id=target, device_id_type=MESH)

    @pl.when(chain.has_last)
    def _():
        pl.semaphore_signal(barrier, inc=1, device_id={"ctx": chain.place - 1}, device_id_type=MESH)

    @pl.when(chain.has_next)
    def _():
        pl.semaphore_signal(barrier, inc=1, device_id={"ctx": chain.place + 1}, device_id_type=MESH)

    inner = chain.has_last & chain.has_next

    @pl.when(inner)
    def _():
        pl.semaphore_wait(barrier, len(targets) + 2)

    @pl.when(jnp.logical_not(inner))
    def _():
        pl.semaphore_wait(barrier, len(targets) + 1)


def along(src, dst, send_sem, recv_sem, place):
    return pltpu.make_async_remote_copy(
        src_ref=src,
        dst_ref=dst,
        send_sem=send_sem,
        recv_sem=recv_sem,
        device_id={"ctx": place},
        device_id_type=MESH,
    )


def spread_heads(source, spread):
    rows = source.shape[0]
    low = lax.broadcasted_iota(jnp.int32, (rows, 128), 1) < 64
    for pair in range(source.shape[1] // 256):
        first = source[:, pair * 256 : pair * 256 + 128].astype(F32)
        second = source[:, pair * 256 + 128 : pair * 256 + 256].astype(F32)
        spread[4 * pair] = jnp.where(low, first, 0.0).astype(BF16)
        spread[4 * pair + 1] = jnp.where(low, pltpu.roll(first, 64, 1), 0.0).astype(BF16)
        spread[4 * pair + 2] = jnp.where(low, 0.0, pltpu.roll(second, 64, 1)).astype(BF16)
        spread[4 * pair + 3] = jnp.where(low, 0.0, second).astype(BF16)


def join_heads(spread, target):
    rows = target.shape[0]
    low = lax.broadcasted_iota(jnp.int32, (rows, 128), 1) < 64
    for pair in range(target.shape[1] // 256):
        parts = [spread(4 * pair + i).T for i in range(4)]
        target[:, pair * 256 : pair * 256 + 128] = jnp.where(low, parts[0], pltpu.roll(parts[1], 64, 1))
        target[:, pair * 256 + 128 : pair * 256 + 256] = jnp.where(low, pltpu.roll(parts[2], 64, 1), parts[3])


def mask_block(bias, length, place, block):
    rows = bias.shape[0]
    key_at = block * rows + lax.broadcasted_iota(jnp.int32, bias.shape, 0)
    query_at = place * rows + lax.broadcasted_iota(jnp.int32, bias.shape, 1)
    bias[...] = jnp.where((key_at <= query_at) & (key_at < length), 0.0, NEGATIVE)


def dot_right(left, right):
    return lax.dot_general(left, right, (((1,), (1,)), ((), ())), preferred_element_type=F32)


def dot_plain(left, right):
    return jnp.dot(left, right, preferred_element_type=F32)


def attend_kernel(
    n_ctx,
    length_ref,
    query,
    kv,
    d_block,
    gate_in,
    up_in,
    down_in,
    attended,
    log_total,
    kv_all,
    d_all,
    gate_out,
    up_out,
    down_out,
    w_gate,
    w_up,
    w_down,
    keep_sem,
    spread,
    bias,
    peak,
    total,
    out_t,
    kv_send,
    kv_recv,
    d_send,
    d_recv,
    d_own,
    send_sem,
    recv_sem,
    pair_send,
    pair_recv,
    own_sem,
):
    chain = Chain(n_ctx)
    place = chain.place
    section = lax.axis_index("section")
    me, beside, across, opposite = corners()
    greet_mixed(
        chain,
        [{"fsdp": beside}, {"fsdp": across}, {"fsdp": opposite}, {"section": 1 - section}],
    )
    rows = query.shape[0]
    half_width = kv.shape[1] // 2

    def block_rows(block):
        return pl.ds(pl.multiple_of(block * rows, rows), rows)

    def upward(step, src):
        return along(
            src,
            kv_all.at[block_rows(place - step)],
            kv_send.at[step],
            kv_recv.at[step + 1],
            place + 1,
        )

    def arriving(step):
        at = kv_all.at[block_rows(place - step)]
        return along(at, at, kv_send.at[step], kv_recv.at[step], place)

    @pl.when(chain.has_next)
    def _():
        upward(0, kv).start()

    gather = SideGather(d_block, d_all, d_send, d_recv, d_own)
    gather.start()
    columns = Columns(
        1, (gate_in, up_in, down_in), (w_gate, w_up, w_down), send_sem, recv_sem, pair_send, pair_recv, own_sem
    )
    columns.start()
    kv_all[block_rows(place)] = kv[...]
    spread_heads(query, spread)
    peak[...] = jnp.full(peak.shape, NEGATIVE, F32)
    total[...] = jnp.zeros(total.shape, F32)
    out_t[...] = jnp.zeros(out_t.shape, F32)
    length = length_ref[0]
    scale = 64 ** (-0.5)

    def attend_block(block):
        mask_block(bias, length, place, block)
        for pair in range(half_width // 128):
            key = kv_all[block_rows(block), pair * 128 : pair * 128 + 128]
            value_t = kv_all[block_rows(block), half_width + pair * 128 : half_width + pair * 128 + 128].T
            for index in range(4):
                head = 4 * pair + index
                scores = dot_right(key, spread[head]) * scale + bias[...]
                before = peak[head]
                now = jnp.maximum(before, jnp.max(scores, axis=0, keepdims=True))
                weights = jnp.exp(scores - now)
                fade = jnp.exp(before - now)
                peak[head] = now
                total[head] = total[head] * fade + jnp.sum(weights, axis=0, keepdims=True)
                out_t[head] = out_t[head] * fade + dot_plain(value_t, weights.astype(BF16))

    attend_block(place)
    gather.relay()

    def step_on(step, carry):
        @pl.when(step <= place)
        def _():
            arriving(step).wait_recv()

            @pl.when(chain.has_next)
            def _():
                upward(step, kv_all.at[block_rows(place - step)]).start()

            attend_block(place - step)

        return carry

    lax.fori_loop(1, n_ctx, step_on, 0)
    join_heads(lambda head: out_t[head] / total[head], attended)
    for head in range(spread.shape[0]):
        log_total[head] = peak[head] + jnp.log(total[head])
    columns.relay()
    columns.arrive()
    keeping = [
        pltpu.make_async_copy(src, dst, keep_sem.at[index])
        for index, (src, dst) in enumerate(((w_gate, gate_out), (w_up, up_out), (w_down, down_out)))
    ]
    for copy in keeping:
        copy.start()
    gather.finish()
    columns.finish()
    for copy in keeping:
        copy.wait()

    def settle(step, carry):
        @pl.when((step <= place) & chain.has_next)
        def _():
            upward(step, kv_all.at[block_rows(place - step)]).wait_send()

        return carry

    lax.fori_loop(0, n_ctx, settle, 0)


def attend(length, query, kv, d_block, gate, up, down, collective_id):
    n_ctx, count = lax.axis_size("ctx"), lax.axis_size("fsdp")
    rows, width = query.shape
    heads = width // 64
    dma = pltpu.SemaphoreType.DMA
    vmem = pl.BlockSpec(memory_space=pltpu.VMEM)
    hbm = pl.BlockSpec(memory_space=pl.ANY)
    column = jax.ShapeDtypeStruct((count * gate.shape[0], gate.shape[1] // count), gate.dtype)
    return pl.pallas_call(
        functools.partial(attend_kernel, n_ctx),
        out_shape=(
            jax.ShapeDtypeStruct((rows, width), F32),
            jax.ShapeDtypeStruct((heads, 1, rows), F32),
            jax.ShapeDtypeStruct((n_ctx * rows, kv.shape[1]), BF16),
            jax.ShapeDtypeStruct((count * rows, d_block.shape[1]), BF16),
            column,
            column,
            jax.ShapeDtypeStruct(down.shape, down.dtype),
        ),
        in_specs=[pl.BlockSpec(memory_space=pltpu.SMEM), vmem, vmem, vmem, hbm, hbm, hbm],
        out_specs=[vmem, vmem, vmem, vmem, hbm, hbm, hbm],
        scratch_shapes=[
            pltpu.VMEM(column.shape, BF16),
            pltpu.VMEM(column.shape, BF16),
            pltpu.VMEM(down.shape, BF16),
            dma((3,)),
            pltpu.VMEM((heads, rows, 128), BF16),
            pltpu.VMEM((rows, rows), F32),
            pltpu.VMEM((heads, 1, rows), F32),
            pltpu.VMEM((heads, 1, rows), F32),
            pltpu.VMEM((heads, 128, rows), F32),
            dma((n_ctx + 1,)),
            dma((n_ctx + 1,)),
            dma((4,)),
            dma((4,)),
            dma,
            dma((2, count)),
            dma((2, count)),
            dma((3, count)),
            dma((3, count)),
            dma((3,)),
        ],
        compiler_params=pltpu.CompilerParams(
            collective_id=collective_id, has_side_effects=True, vmem_limit_bytes=58 << 20
        ),
        cost_estimate=busy(50),
    )(length, query, kv, d_block, gate, up, down)


def attend_back_kernel(
    n_ctx,
    length_ref,
    query,
    kv_all,
    d_out,
    log_total,
    delta,
    blocks,
    d_query,
    d_kv,
    reduced_out,
    spread,
    d_spread,
    bias,
    d_query_t,
    term,
    leaving,
    coming,
    kv_send,
    kv_recv,
    beside_got,
    across_got,
    passed,
    passed_got,
    send_sem,
    recv_sem,
):
    chain = Chain(n_ctx)
    place = chain.place
    _, beside, across, _ = corners()
    greet_mixed(chain, [{"fsdp": beside}, {"fsdp": across}])
    rows = query.shape[0]
    half_width = kv_all.shape[1] // 2
    reduction = SideReduce(blocks, reduced_out, beside_got, across_got, passed, passed_got, send_sem, recv_sem)
    reduction.start()
    spread_heads(query, spread)
    spread_heads(d_out, d_spread)
    d_query_t[...] = jnp.zeros(d_query_t.shape, F32)
    length = length_ref[0]
    scale = 64 ** (-0.5)

    def downward(block):
        return along(leaving.at[block], coming.at[block], kv_send.at[block], kv_recv.at[block], place - 1)

    def step_on(block, carry):
        @pl.when(block <= place)
        def _():
            mask_block(bias, length, place, block)
            at = pl.ds(pl.multiple_of(block * rows, rows), rows)
            for pair in range(half_width // 128):
                lanes = slice(pair * 128, pair * 128 + 128)
                more = slice(half_width + pair * 128, half_width + pair * 128 + 128)
                key = kv_all[at, lanes]
                value = kv_all[at, more]
                key_t = key.T
                d_key = jnp.zeros((rows, 128), F32)
                d_value = jnp.zeros((rows, 128), F32)
                for index in range(4):
                    head = 4 * pair + index
                    scores = dot_right(key, spread[head]) * scale + bias[...]
                    prob = jnp.exp(scores - log_total[head])
                    d_prob = dot_right(value, d_spread[head])
                    d_scores = (prob * (d_prob - delta[head])).astype(BF16)
                    d_value = d_value + dot_plain(prob.astype(BF16), d_spread[head])
                    d_key = d_key + dot_plain(d_scores, spread[head])
                    d_query_t[head] = d_query_t[head] + dot_plain(key_t, d_scores)
                term[:, lanes] = d_key * scale
                term[:, more] = d_value

            @pl.when(chain.has_next)
            def _():
                along(
                    leaving.at[block], coming.at[block], kv_send.at[block], kv_recv.at[block], place
                ).wait_recv()
                term[...] = term[...] + coming[block].astype(F32)

            @pl.when(block < place)
            def _():
                leaving[block] = term[...].astype(BF16)
                downward(block).start()

            @pl.when(block == place)
            def _():
                d_kv[...] = term[...]

        @pl.when(block == 0)
        def _():
            reduction.relay()

        return carry

    lax.fori_loop(0, n_ctx, step_on, 0)
    join_heads(lambda head: d_query_t[head] * scale, d_query)
    reduction.finish()

    def settle(block, carry):
        @pl.when(block < place)
        def _():
            downward(block).wait_send()

        return carry

    lax.fori_loop(0, n_ctx, settle, 0)


def attend_back(length, query, kv_all, d_out, log_total, delta, blocks, collective_id):
    n_ctx = lax.axis_size("ctx")
    rows, width = query.shape
    heads = width // 64
    dma = pltpu.SemaphoreType.DMA
    vmem = pl.BlockSpec(memory_space=pltpu.VMEM)
    wide = jax.ShapeDtypeStruct((rows, width), F32)
    pair = pltpu.VMEM((2, rows // 2, blocks.shape[1]), BF16)
    return pl.pallas_call(
        functools.partial(attend_back_kernel, n_ctx),
        out_shape=(wide, jax.ShapeDtypeStruct((rows, kv_all.shape[1]), F32), wide),
        in_specs=[pl.BlockSpec(memory_space=pltpu.SMEM)] + [vmem] * 6,
        out_specs=[vmem] * 3,
        scratch_shapes=[
            pltpu.VMEM((heads, rows, 128), BF16),
            pltpu.VMEM((heads, rows, 128), BF16),
            pltpu.VMEM((rows, rows), F32),
            pltpu.VMEM((heads, 128, rows), F32),
            pltpu.VMEM((rows, kv_all.shape[1]), F32),
            pltpu.VMEM((n_ctx, rows, kv_all.shape[1]), BF16),
            pltpu.VMEM((n_ctx, rows, kv_all.shape[1]), BF16),
            dma((n_ctx,)),
            dma((n_ctx,)),
            pair,
            pair,
            pair,
            pair,
            dma((6,)),
            dma((6,)),
        ],
        compiler_params=pltpu.CompilerParams(
            collective_id=collective_id, has_side_effects=True, vmem_limit_bytes=56 << 20
        ),
        cost_estimate=busy(50),
    )(length, query, kv_all, d_out, log_total, delta, blocks)


class MixerGather:
    def __init__(self, sources, targets, send_sem, recv_sem, pair_send, pair_recv, own_sem):
        self.section = section = lax.axis_index("section")
        me, beside, across, opposite = corners()
        rows = sources[0].shape[0]
        half = rows // 2
        quarter = half // 2

        def at_rows(out, owner, extra, size):
            return out.at[pl.ds(pl.multiple_of(owner * rows + extra, quarter), size)]

        def pair(slot, at):
            return pltpu.make_async_remote_copy(
                src_ref=at,
                dst_ref=at,
                send_sem=pair_send.at[slot],
                recv_sem=pair_recv.at[slot],
                device_id={"section": 1 - section},
                device_id_type=MESH,
            )

        self.direct, self.onward, self.early, self.late, self.own = [], [], [], [], []
        start = section * half
        for index, (source, out) in enumerate(zip(sources, targets)):
            mine = source.at[pl.ds(pl.multiple_of(start, half), half)]
            spot = at_rows(out, me, start, half)
            slot = 4 * index
            self.direct.append(
                [
                    to_side(mine, spot, send_sem.at[slot], recv_sem.at[slot], beside),
                    to_side(mine, spot, send_sem.at[slot + 1], recv_sem.at[slot + 1], across),
                ]
            )
            passing = at_rows(out, beside, start, quarter), at_rows(out, across, start + quarter, quarter)
            self.onward.append(
                [
                    to_side(passing[0], passing[0], send_sem.at[slot + 2], recv_sem.at[slot + 2], across),
                    to_side(passing[1], passing[1], send_sem.at[slot + 3], recv_sem.at[slot + 3], beside),
                ]
            )
            self.early.append(
                [
                    pair(slot, at_rows(out, beside, start, half)),
                    pair(slot + 1, at_rows(out, across, start, half)),
                ]
            )
            self.late.append(
                [
                    pair(slot + 2, at_rows(out, opposite, start, quarter)),
                    pair(slot + 3, at_rows(out, opposite, start + quarter, quarter)),
                ]
            )
            self.own.append(pltpu.make_async_copy(source, at_rows(out, me, 0, rows), own_sem.at[index]))

    def start(self):
        for copies in self.direct:
            for copy in copies:
                copy.start()
        for copy in self.own:
            copy.start()

    def relay(self):
        for direct, onward, early in zip(self.direct, self.onward, self.early):
            for turn in range(2):
                direct[turn].wait_recv()
                onward[turn].start()
                early[turn].start()

    def relay_last(self):
        for onward, late in zip(self.onward, self.late):
            for turn in range(2):
                onward[turn].wait_recv()
                late[turn].start()

    def arrive(self, index):
        self.own[index].wait()
        for copy in self.early[index] + self.late[index]:
            copy.wait_recv()

    def finish(self):
        for group in (self.direct, self.onward, self.early, self.late):
            for copies in group:
                for copy in copies:
                    copy.wait_send()


def front_kernel(
    n_ctx,
    x_ref,
    gains,
    taps,
    conv_in,
    conv_out,
    gate_in,
    up_in,
    down_in,
    in_out,
    out_out,
    gate_out,
    up_out,
    down_out,
    projected,
    convolved,
    z_low,
    mixed,
    rim,
    act_all,
    w_in,
    w_out,
    w_gate,
    w_up,
    w_down,
    act1,
    act2,
    last_rows,
    rim_sem,
    mix_send,
    mix_recv,
    mix_pair_send,
    mix_pair_recv,
    mix_own,
    send_sem,
    recv_sem,
    pair_send,
    pair_recv,
    own_sem,
    act_send,
    act_recv,
    act_own,
    keep_sem,
):
    chain = Chain(n_ctx)
    section = lax.axis_index("section")
    _, beside, across, opposite = corners()
    greet_mixed(
        chain,
        [{"fsdp": beside}, {"fsdp": across}, {"fsdp": opposite}, {"section": 1 - section}],
    )
    mixers = MixerGather(
        (conv_in, conv_out), (w_in, w_out), mix_send, mix_recv, mix_pair_send, mix_pair_recv, mix_own
    )
    mixers.start()
    columns = Columns(
        0, (gate_in, up_in, down_in), (w_gate, w_up, w_down), send_sem, recv_sem, pair_send, pair_recv, own_sem
    )
    gather = SideGather(act2, act_all, act_send, act_recv, act_own)
    keeping = [
        pltpu.make_async_copy(src, dst, keep_sem.at[index])
        for index, (src, dst) in enumerate(
            ((w_in, in_out), (w_out, out_out), (w_gate, gate_out), (w_up, up_out), (w_down, down_out))
        )
    ]
    rows, width = x_ref.shape
    strip = 64

    def normalize(values, gain):
        inv_rms = lax.rsqrt(jnp.mean(values * values, axis=-1, keepdims=True) + EPSILON)
        return (values * inv_rms * gain).astype(BF16)

    def first_norm(index, carry):
        at = pl.ds(pl.multiple_of(index * strip, strip), strip)
        act1[at] = normalize(x_ref[at].astype(F32), gains[0:1])
        return carry

    lax.fori_loop(0, rows // strip, first_norm, 0)
    mixers.relay()
    columns.start()
    mixers.relay_last()
    mixers.arrive(0)
    keeping[0].start()
    wide = 512

    def project(index, carry):
        at = pl.ds(pl.multiple_of(index * wide, wide), wide)
        projected[:, at] = dot_plain(act1[...], w_in[:, at])
        return carry

    lax.fori_loop(0, projected.shape[1] // wide, project, 0)
    tail_at = pl.ds(rows - 16, 16)
    last_rows[...] = (projected[tail_at, :width] * projected[tail_at, 2 * width :]).astype(BF16)
    to_next = along(last_rows, rim, rim_sem.at[0], rim_sem.at[1], chain.place + 1)

    @pl.when(chain.has_next)
    def _():
        to_next.start()

    @pl.when(chain.has_last)
    def _():
        along(last_rows, rim, rim_sem.at[0], rim_sem.at[1], chain.place).wait_recv()

    @pl.when(jnp.logical_not(chain.has_last))
    def _():
        rim[...] = jnp.zeros(rim.shape, BF16)

    part = 128
    row_at = lax.broadcasted_iota(jnp.int32, (rows, part), 0)

    def convolve(index, carry):
        def lanes(offset):
            return pl.ds(pl.multiple_of(offset * width + index * part, part), part)

        product = (projected[:, lanes(0)] * projected[:, lanes(2)]).astype(BF16).astype(F32)
        edge = rim[:, lanes(0)].astype(F32)
        near, far = edge[15:16], edge[14:15]
        one = jnp.where(row_at >= 1, pltpu.roll(product, 1, 0), near)
        two = jnp.where(row_at >= 2, pltpu.roll(product, 2, 0), jnp.where(row_at == 1, near, far))
        tap = taps[:, lanes(0)]
        value = tap[0:1] * two + tap[1:2] * one + tap[2:3] * product
        convolved[:, lanes(0)] = value
        z_low[:, lanes(0)] = (projected[:, lanes(1)] * value).astype(BF16)
        return carry

    lax.fori_loop(0, width // part, convolve, 0)
    mixers.arrive(1)
    keeping[1].start()

    def mix(index, carry):
        at = pl.ds(pl.multiple_of(index * wide, wide), wide)
        mixed[:, at] = dot_plain(z_low[...], w_out[:, at])
        return carry

    lax.fori_loop(0, width // wide, mix, 0)

    def second_norm(index, carry):
        at = pl.ds(pl.multiple_of(index * strip, strip), strip)
        act2[at] = normalize(x_ref[at].astype(F32) + mixed[at], gains[1:2])
        return carry

    lax.fori_loop(0, rows // strip, second_norm, 0)
    gather.start()
    gather.relay()
    columns.relay()
    columns.arrive()
    for copy in keeping[2:]:
        copy.start()
    gather.finish()
    columns.finish()
    mixers.finish()

    @pl.when(chain.has_next)
    def _():
        to_next.wait_send()

    for copy in keeping:
        copy.wait()


def front(x_low, gains, taps, conv_in, conv_out, gate, up, down, collective_id):
    n_ctx, count = lax.axis_size("ctx"), lax.axis_size("fsdp")
    assert count == 4
    rows, width = x_low.shape
    dma = pltpu.SemaphoreType.DMA
    vmem = pl.BlockSpec(memory_space=pltpu.VMEM)
    hbm = pl.BlockSpec(memory_space=pl.ANY)

    def whole(weight):
        return (count * weight.shape[0], weight.shape[1])

    column = (count * gate.shape[0], gate.shape[1] // count)
    weights = [whole(conv_in), whole(conv_out), column, column, down.shape]
    return pl.pallas_call(
        functools.partial(front_kernel, n_ctx),
        out_shape=tuple(jax.ShapeDtypeStruct(shape, BF16) for shape in weights)
        + (
            jax.ShapeDtypeStruct((rows, conv_in.shape[1]), F32),
            jax.ShapeDtypeStruct((rows, width), F32),
            jax.ShapeDtypeStruct((rows, width), BF16),
            jax.ShapeDtypeStruct((rows, width), F32),
            jax.ShapeDtypeStruct((16, width), BF16),
            jax.ShapeDtypeStruct((count * rows, width), BF16),
        ),
        in_specs=[vmem] * 3 + [hbm] * 5,
        out_specs=[hbm] * 5 + [vmem] * 6,
        scratch_shapes=[pltpu.VMEM(shape, BF16) for shape in weights]
        + [
            pltpu.VMEM((rows, width), BF16),
            pltpu.VMEM((rows, width), BF16),
            pltpu.VMEM((16, width), BF16),
            dma((2,)),
            dma((8,)),
            dma((8,)),
            dma((8,)),
            dma((8,)),
            dma((2,)),
            dma((2, count)),
            dma((2, count)),
            dma((3, count)),
            dma((3, count)),
            dma((3,)),
            dma((4,)),
            dma((4,)),
            dma,
            dma((5,)),
        ],
        compiler_params=pltpu.CompilerParams(
            collective_id=collective_id, has_side_effects=True, vmem_limit_bytes=58 << 20
        ),
        cost_estimate=busy(70),
    )(x_low, gains, taps, conv_in, conv_out, gate, up, down)


def back_kernel(
    n_ctx,
    blocks,
    d_gate,
    d_up,
    x_ref,
    mixed,
    d_h,
    gains,
    taps,
    z_low,
    rim,
    act_in,
    hidden_in,
    d_all_in,
    w_in_in,
    w_out_in,
    projected_in,
    convolved_in,
    gate_grad,
    up_grad,
    down_grad,
    b_grad,
    c_grad,
    x_grad,
    o_grad,
    d_x,
    small,
    act,
    hidden,
    d_all,
    w_in,
    w_out,
    projected,
    convolved,
    load_sem,
    stage_wide,
    stage,
    stage_sem,
    beside_got,
    across_got,
    passed,
    passed_got,
    send_sem,
    recv_sem,
    d_act,
    d_res,
    d_mixed,
    d_conv,
    d_proj,
    act1,
    edge,
    next_edge,
    edge_sem,
):
    chain = Chain(n_ctx)
    _, beside, across, _ = corners()
    greet_mixed(chain, [{"fsdp": beside}, {"fsdp": across}])
    reduction = SideReduce(blocks, d_act, beside_got, across_got, passed, passed_got, send_sem, recv_sem)
    reduction.start()
    loads = [
        pltpu.make_async_copy(src, dst, load_sem.at[index])
        for index, (src, dst) in enumerate(
            (
                (act_in, act),
                (hidden_in, hidden),
                (d_all_in, d_all),
                (convolved_in, convolved),
                (projected_in, projected),
                (w_out_in, w_out),
                (w_in_in, w_in),
            )
        )
    ]
    for copy in loads:
        copy.start()
    rows, width = x_ref.shape
    wide = d_gate.shape[1]
    tile = 256
    small[...] = jnp.zeros(small.shape, F32)

    def weight_grad(left, right, at_right, target, staging, slot):
        count = left.shape[1] // tile

        def leaving(index, at):
            return pltpu.make_async_copy(staging.at[at], target.at[index], stage_sem.at[slot + at])

        def step(index, carry):
            at = lax.rem(index, 2)
            lanes = pl.ds(pl.multiple_of(index * tile, tile), tile)

            @pl.when(index >= 2)
            def _():
                leaving(lanes, at).wait()

            staging[at] = dot_plain(left[:, lanes].T, right[:, at_right]).astype(BF16)
            leaving(lanes, at).start()
            return carry

        lax.fori_loop(0, count, step, 0)
        for index in range(min(2, count)):
            leaving(pl.ds(0, tile), index).wait()

    loads[0].wait()
    weight_grad(act, d_gate, slice(None), gate_grad, stage_wide, 0)
    weight_grad(act, d_up, slice(None), up_grad, stage_wide, 0)
    reduction.relay()
    loads[1].wait()
    loads[2].wait()
    odd = hidden.shape[1] % tile

    weight_grad(hidden, d_all, slice(None), down_grad, stage, 2)
    if odd:
        last = hidden.shape[1] - odd
        stage[0, :odd] = dot_plain(hidden[:, last:].T, d_all[...]).astype(BF16)
        copy = pltpu.make_async_copy(stage.at[0, pl.ds(0, odd)], down_grad.at[pl.ds(last, odd)], stage_sem.at[2])
        copy.start()
        copy.wait()
    reduction.finish()
    strip = 64

    def norm_strip(at, values, gain, d_values, row):
        inv_rms = lax.rsqrt(jnp.mean(values * values, axis=-1, keepdims=True) + EPSILON)
        normed = values * inv_rms
        small[row : row + 1] = small[row : row + 1] + jnp.sum(d_values * normed, axis=0, keepdims=True)
        d_normed = d_values * gain
        return inv_rms * d_normed - normed * inv_rms * jnp.mean(d_normed * normed, axis=-1, keepdims=True)

    def second_norm(index, carry):
        at = pl.ds(pl.multiple_of(index * strip, strip), strip)
        x_rows = x_ref[at].astype(F32)
        value = d_h[at].astype(F32) + norm_strip(at, x_rows + mixed[at], gains[1:2], d_act[at], 1)
        d_res[at] = value
        d_mixed[at] = value.astype(BF16)
        inv_rms = lax.rsqrt(jnp.mean(x_rows * x_rows, axis=-1, keepdims=True) + EPSILON)
        act1[at] = (x_rows * inv_rms * gains[0:1]).astype(BF16)
        return carry

    lax.fori_loop(0, rows // strip, second_norm, 0)
    for index in range(3, 6):
        loads[index].wait()

    def to_z(index, carry):
        at = pl.ds(pl.multiple_of(index * tile, tile), tile)
        d_conv[:, at] = dot_right(d_mixed[...], w_out[at])
        return carry

    lax.fori_loop(0, width // tile, to_z, 0)
    part = 128
    row_at = lax.broadcasted_iota(jnp.int32, (rows, part), 0)

    def lanes_of(offset, index):
        return pl.ds(pl.multiple_of(offset * width + index * part, part), part)

    def convolve_back(index, carry):
        lanes = lanes_of(0, index)
        product = (projected[:, lanes] * projected[:, lanes_of(2, index)]).astype(BF16).astype(F32)
        before = rim[:, lanes].astype(F32)
        near, far = before[15:16], before[14:15]
        one = jnp.where(row_at >= 1, pltpu.roll(product, 1, 0), near)
        two = jnp.where(row_at >= 2, pltpu.roll(product, 2, 0), jnp.where(row_at == 1, near, far))
        d_z = d_conv[:, lanes]
        d_proj[:, lanes_of(1, index)] = (d_z * convolved[:, lanes]).astype(BF16)
        d_value = d_z * projected[:, lanes_of(1, index)]
        d_conv[:, lanes] = d_value
        for row, source in ((2, two), (3, one), (4, product)):
            small[row : row + 1, lanes] = jnp.sum(d_value * source, axis=0, keepdims=True)
        tap = taps[:, lanes]
        edge[0:1, lanes] = tap[0:1] * d_value[0:1]
        edge[1:2, lanes] = tap[0:1] * d_value[1:2] + tap[1:2] * d_value[0:1]
        return carry

    lax.fori_loop(0, width // part, convolve_back, 0)
    edge[2:8] = jnp.zeros((6, width), F32)
    to_last = along(edge, next_edge, edge_sem.at[0], edge_sem.at[1], chain.place - 1)

    @pl.when(chain.has_last)
    def _():
        to_last.start()

    weight_grad(z_low, d_mixed, slice(None), o_grad, stage, 2)

    @pl.when(chain.has_next)
    def _():
        along(edge, next_edge, edge_sem.at[0], edge_sem.at[1], chain.place).wait_recv()

    @pl.when(jnp.logical_not(chain.has_next))
    def _():
        next_edge[...] = jnp.zeros(next_edge.shape, F32)

    def products_back(index, carry):
        lanes = lanes_of(0, index)
        d_value = d_conv[:, lanes]
        tap = taps[:, lanes]
        after = next_edge[:, lanes]
        one = jnp.where(row_at < rows - 1, pltpu.roll(d_value, rows - 1, 0), 0.0)
        two = jnp.where(row_at < rows - 2, pltpu.roll(d_value, rows - 2, 0), 0.0)
        joined = tap[2:3] * d_value + tap[1:2] * one + tap[0:1] * two
        joined = joined + jnp.where(row_at == rows - 2, after[0:1], 0.0)
        joined = joined + jnp.where(row_at == rows - 1, after[1:2], 0.0)
        joined = joined.astype(BF16).astype(F32)
        d_proj[:, lanes] = (joined * projected[:, lanes_of(2, index)]).astype(BF16)
        d_proj[:, lanes_of(2, index)] = (joined * projected[:, lanes]).astype(BF16)
        return carry

    lax.fori_loop(0, width // part, products_back, 0)
    loads[6].wait()

    def to_act(index, carry):
        at = pl.ds(pl.multiple_of(index * tile, tile), tile)
        d_act[:, at] = dot_right(d_proj[...], w_in[at])
        return carry

    lax.fori_loop(0, width // tile, to_act, 0)
    for offset, target in enumerate((b_grad, c_grad, x_grad)):
        weight_grad(act1, d_proj, slice(offset * width, (offset + 1) * width), target, stage, 2)

    def first_norm(index, carry):
        at = pl.ds(pl.multiple_of(index * strip, strip), strip)
        value = d_res[at] + norm_strip(at, x_ref[at].astype(F32), gains[0:1], d_act[at], 0)
        d_x[at] = value.astype(BF16)
        return carry

    lax.fori_loop(0, rows // strip, first_norm, 0)

    @pl.when(chain.has_last)
    def _():
        to_last.wait_send()


def conv_back(blocks, d_gate, d_up, local, kept, collective_id):
    n_ctx = lax.axis_size("ctx")
    x_low = local[0]
    act, hidden = kept[0], kept[1]
    rows, width = x_low.shape
    wide = d_gate.shape[1]
    dma = pltpu.SemaphoreType.DMA
    vmem = pl.BlockSpec(memory_space=pltpu.VMEM)
    hbm = pl.BlockSpec(memory_space=pl.ANY)
    pair = pltpu.VMEM((2, rows // 2, width), BF16)
    square = jax.ShapeDtypeStruct((width, width), BF16)
    column = jax.ShapeDtypeStruct((width, wide), BF16)
    return pl.pallas_call(
        functools.partial(back_kernel, n_ctx),
        out_shape=(
            column,
            column,
            jax.ShapeDtypeStruct((wide, width), BF16),
            square,
            square,
            square,
            square,
            jax.ShapeDtypeStruct((rows, width), BF16),
            jax.ShapeDtypeStruct((8, width), F32),
        ),
        in_specs=[vmem] * (3 + len(local)) + [hbm] * len(kept),
        out_specs=[hbm] * 7 + [vmem] * 2,
        scratch_shapes=[pltpu.VMEM(k.shape, k.dtype) for k in kept]
        + [
            dma((7,)),
            pltpu.VMEM((2, 256, wide), BF16),
            pltpu.VMEM((2, 256, width), BF16),
            dma((4,)),
            pair,
            pair,
            pair,
            pair,
            dma((6,)),
            dma((6,)),
            pltpu.VMEM((rows, width), F32),
            pltpu.VMEM((rows, width), F32),
            pltpu.VMEM((rows, width), BF16),
            pltpu.VMEM((rows, width), F32),
            pltpu.VMEM((rows, 3 * width), BF16),
            pltpu.VMEM((rows, width), BF16),
            pltpu.VMEM((8, width), F32),
            pltpu.VMEM((8, width), F32),
            dma((2,)),
        ],
        compiler_params=pltpu.CompilerParams(
            collective_id=collective_id, has_side_effects=True, vmem_limit_bytes=58 << 20
        ),
        cost_estimate=busy(35),
    )(blocks, d_gate, d_up, *local, *kept)


def ffn_forward(act, w_gate, w_up, w_down):
    gate_pre = matmul(act, w_gate)
    up_pre = matmul(act, w_up)
    hidden = (jax.nn.silu(gate_pre) * up_pre).astype(BF16)
    return matmul(hidden, w_down).astype(BF16), (act, gate_pre, up_pre, hidden)


def ffn_backward(d_all, kept, w_gate, w_up, w_down):
    act, gate_pre, up_pre, hidden = kept
    d_hidden = matmul_right(d_all, w_down)
    sigmoid = jax.nn.sigmoid(gate_pre)
    d_up = (d_hidden * gate_pre * sigmoid).astype(BF16)
    d_gate = (d_hidden * up_pre * sigmoid * (1.0 + gate_pre * (1.0 - sigmoid))).astype(BF16)
    terms = (matmul_right(d_gate, w_gate) + matmul_right(d_up, w_up)).astype(BF16)
    return terms, d_gate, d_up


def ffn_weight_grads(d_all, kept, d_gate, d_up):
    act, _, _, hidden = kept
    return (
        matmul_left(act, d_gate).astype(BF16),
        matmul_left(act, d_up).astype(BF16),
        matmul_left(hidden, d_all).astype(BF16),
    )


def ffn_norm_back(d_act, residual, gain):
    normed, inv_rms = norm_rows(residual)
    return norm_back(d_act * gain, normed, inv_rms), jnp.sum(d_act * normed, axis=0)


def shards(
    inputs,
    cotangent,
    lengths,
    norm_gains,
    conv_in,
    conv_kernel,
    conv_out,
    attn_q,
    attn_k,
    attn_v,
    attn_out,
    head_gains,
    ffn_gate,
    ffn_up,
    ffn_down,
):
    micro, rows, width = inputs.shape
    section = lax.axis_index("section")
    group = lax.axis_index("fsdp")
    fsdp = lax.axis_size("fsdp")
    assert micro == lax.axis_size("section")
    head = head_gains.shape[1]
    q_width, kv_width = attn_q.shape[1], attn_k.shape[1]
    q_heads, kv_heads = q_width // head, kv_width // head
    positions = lax.axis_index("ctx") * rows + jnp.arange(rows)
    length = lax.dynamic_index_in_dim(lengths, group * micro + section, keepdims=False)
    mask = (positions < length).astype(F32)[:, None]

    def whole_rows(weight):
        half = weight.shape[0] // micro
        mine = lax.dynamic_slice_in_dim(weight, section * half, half, 0)
        return lax.all_gather(mine, ("fsdp", "section"), axis=0, tiled=True)

    part = ffn_gate.shape[1]
    attn_full = whole_rows(jnp.concatenate([attn_q, attn_k, attn_v, attn_out], axis=1))
    query_full, key_full, value_full, proj_full = (
        attn_full[:, :q_width],
        attn_full[:, q_width : q_width + kv_width],
        attn_full[:, q_width + kv_width : q_width + 2 * kv_width],
        attn_full[:, q_width + 2 * kv_width :],
    )

    x_low = lax.dynamic_index_in_dim(inputs, section, keepdims=False)
    in_full, out_full, gate1, up1, down1, projected, convolved, z_low, mixed, rim, act_all1 = front(
        x_low, norm_gains, conv_kernel, conv_in, conv_out, ffn_gate[0], ffn_up[0], ffn_down[0], 2
    )
    x = x_low.astype(F32)
    res1 = x + mixed
    terms1, kept1 = ffn_forward(act_all1, gate1, up1, down1)
    ffn1 = reduced(terms1, 1)
    h_low = (res1 + ffn1).astype(BF16)

    h = h_low.astype(F32)
    normed2, inv2 = norm_rows(h)
    act2 = (normed2 * norm_gains[2]).astype(BF16)
    q_normed, q_inv = norm_heads(matmul(act2, query_full), head)
    k_normed, k_inv = norm_heads(matmul(act2, key_full), head)
    q_gain = jnp.tile(head_gains[0], q_heads)
    k_gain = jnp.tile(head_gains[1], kv_heads)
    query = (q_normed * q_gain).astype(BF16)
    key = (k_normed * k_gain).astype(BF16)
    value = matmul(act2, value_full).astype(BF16)
    d_sum_low = (lax.dynamic_index_in_dim(cotangent, section, keepdims=False).astype(F32) * mask).astype(BF16)
    attended, log_total, kv_all, d_sum_all, gate2, up2, down2 = attend(
        length.reshape(1),
        query,
        jnp.concatenate([key, value], axis=1),
        d_sum_low,
        ffn_gate[0],
        ffn_up[0],
        ffn_down[0],
        3,
    )
    attended_low = attended.astype(BF16)
    attn_rows = matmul(attended_low, proj_full)
    res2 = h + attn_rows
    normed3, _ = norm_rows(res2)
    act_all2 = gathered((normed3 * norm_gains[3]).astype(BF16), 0)
    terms2, kept2 = ffn_forward(act_all2, gate2, up2, down2)

    d_sum = d_sum_low.astype(F32)
    d_terms2, d_gate2, d_up2 = ffn_backward(d_sum_all, kept2, gate2, up2, down2)
    grads2 = ffn_weight_grads(d_sum_all, kept2, d_gate2, d_up2)
    half = part // 2
    strip = half // lax.axis_size("ctx")

    def column_half(which):
        pieces = jnp.stack(grads2[:2]).reshape(2, fsdp, 2, half // strip, strip, -1)
        pieces = lax.dynamic_index_in_dim(pieces, which, 2, keepdims=False)
        return pieces.transpose(2, 1, 0, 3, 4).reshape(2 * fsdp * half, -1)

    def down_half(which):
        size = grads2[2].shape[0] // 2
        return lax.dynamic_slice_in_dim(grads2[2], which * size, size, 0)

    d_act3, got_gu, got_down = reduced_swapping(
        d_terms2, column_half(1 - section), down_half(1 - section), 8
    )
    d_ffn, gain3 = ffn_norm_back(d_act3, res2, norm_gains[3])
    d_res2 = d_sum + d_ffn
    d_attn = d_res2.astype(BF16)
    grad_proj = matmul_left(attended_low, d_attn)
    d_att = matmul_right(d_attn, proj_full).astype(BF16)
    delta = jnp.sum((d_att.astype(F32) * attended).reshape(rows, q_heads, head), axis=-1)
    shared_terms = tuple(
        (mine.astype(F32) + got.astype(F32)).astype(BF16)
        for mine, got in ((column_half(section), got_gu), (down_half(section), got_down))
    )
    d_att, shared_terms = lax.optimization_barrier((d_att, shared_terms))
    d_query, d_kv, ffn2 = attend_back(
        length.reshape(1), query, kv_all, d_att, log_total, delta.T.reshape(q_heads, 1, rows), terms2, 4
    )
    result = (res2 + ffn2) * mask

    def square(values):
        return jnp.sum(mask * values * values, axis=0, keepdims=True)

    squares = [square(v) for v in (x, mixed, ffn1, h, attn_rows, res2, ffn2, result)]
    second_gu, second_down = (
        lax.psum_scatter(term, "ctx", scatter_dimension=0, tiled=True) for term in shared_terms
    )
    d_qn = rounded(d_query)
    grad_qgain = jnp.sum(jnp.sum(d_qn * q_normed, axis=0).reshape(q_heads, head), axis=0)
    d_qpre = norm_heads_back(d_qn * q_gain, q_normed, q_inv, head).astype(BF16)
    d_kn = rounded(d_kv[:, :kv_width])
    grad_kgain = jnp.sum(jnp.sum(d_kn * k_normed, axis=0).reshape(kv_heads, head), axis=0)
    d_kpre = norm_heads_back(d_kn * k_gain, k_normed, k_inv, head).astype(BF16)
    d_vpre = d_kv[:, kv_width:].astype(BF16)
    d_act2 = (
        matmul_right(d_qpre, query_full)
        + matmul_right(d_kpre, key_full)
        + matmul_right(d_vpre, value_full)
    )
    gain2 = jnp.sum(d_act2 * normed2, axis=0)
    d_h_low = (d_res2 + norm_back(d_act2 * norm_gains[2], normed2, inv2)).astype(BF16)

    d_h_all, second_gu = gathered_swapped(d_h_low, second_gu.reshape(fsdp, 2 * strip, -1), 5)
    second_gu = lax.all_gather(second_gu, "ctx", axis=0)
    second_down = lax.all_gather(second_down, "ctx", axis=0, tiled=True)
    d_terms1, d_gate1, d_up1 = ffn_backward(d_h_all, kept1, gate1, up1, down1)
    attn_mixers = [
        matmul_left(act2, d_qpre).astype(BF16),
        matmul_left(act2, jnp.concatenate([d_kpre, d_vpre], axis=1)).astype(BF16),
        grad_proj.astype(BF16),
    ]
    *grads, d_x, conv_small = conv_back(
        d_terms1,
        d_gate1,
        d_up1,
        (x_low, mixed, d_h_low, norm_gains, conv_kernel, z_low, rim),
        (act_all1, kept1[3], d_h_all, in_full, out_full, projected, convolved),
        9,
    )

    y_low = result.astype(BF16)
    is_first = section == 0
    other_end = swapped(jnp.where(is_first, y_low, d_x), "section")
    ends = jnp.where(is_first, jnp.stack([d_x, other_end]), jnp.stack([other_end, y_low]))[None]

    small = jnp.concatenate(
        [conv_small[:2], gain2[None], gain3[None], conv_small[2:5]]
        + [jnp.pad(grad[None], ((0, 0), (0, width - head))) for grad in (grad_qgain, grad_kgain)]
        + [jnp.zeros((7, width), F32)]
        + squares
        + [jnp.zeros((8, width), F32)]
    ).astype(BF16)
    small = small.reshape(2, 16, width)
    gu_sum, down_sum, rest_sum = summed_gradients(
        grads[:3],
        attn_mixers + grads[3:],
        small,
        second_gu.reshape(-1, fsdp, 2, strip, second_gu.shape[-1]),
        second_down,
    )
    rest_sum = rest_sum.astype(F32)

    def block(index):
        rows_at = slice(index * half, (index + 1) * half)
        return rest_sum[:, rows_at].reshape(2 * half, width)

    attn_blocks = [block(i) for i in range(3)]
    conv_blocks = [block(3 + i) for i in range(4)]
    small_sum = rest_sum[0, 7 * half : 7 * half + 9]
    cut = width // fsdp
    mine = lax.dynamic_slice_in_dim(small_sum[:7], group * cut, cut, 1)
    head_cut = head // fsdp
    heads = lax.dynamic_slice_in_dim(small_sum[7:9], group * head_cut, head_cut, 1)
    square_cut = len(squares) // fsdp
    square_sum = jnp.sum(
        lax.dynamic_slice_in_dim(rest_sum[1, 7 * half : 7 * half + 8], group * square_cut, square_cut, 0), axis=1
    )
    token_total = jnp.sum(lengths).astype(F32) * width
    rms = jnp.sqrt(square_sum / token_total)
    return (
        ends,
        mine[:3],
        mine[3],
        jnp.concatenate(conv_blocks[:3], axis=1),
        mine[4:7],
        conv_blocks[3],
        attn_blocks[0],
        attn_blocks[1][:, :kv_width],
        attn_blocks[1][:, kv_width:],
        attn_blocks[2],
        heads,
        gu_sum[0][None].astype(F32),
        gu_sum[1][None].astype(F32),
        down_sum[None].astype(F32),
        rms,
    )


def solution(mesh):
    return jax.shard_map(
        shards,
        mesh=mesh,
        in_specs=(
            P("fsdp", "ctx", None),
            P("fsdp", "ctx", None),
            P(),
            P(),
            P("fsdp", None),
            P(),
            P("fsdp", None),
            P("fsdp", None),
            P("fsdp", None),
            P("fsdp", None),
            P("fsdp", None),
            P(),
            P("section", "fsdp", None),
            P("section", "fsdp", None),
            P("section", "fsdp", None),
        ),
        out_specs=(
            P("section", "fsdp", "ctx", None),
            P(None, "fsdp"),
            P("fsdp"),
            P("fsdp", None),
            P(None, "fsdp"),
            P("fsdp", None),
            P("fsdp", None),
            P("fsdp", None),
            P("fsdp", None),
            P("fsdp", None),
            P(None, "fsdp"),
            P("section", "fsdp", None),
            P("section", "fsdp", None),
            P("section", "fsdp", None),
            P("fsdp"),
        ),
        check_vma=False,
    )
```

```python
import functools

import jax
import jax.numpy as jnp
from jax import lax
from jax.experimental import pallas as pl
from jax.experimental.pallas import tpu as pltpu
from jax.sharding import PartitionSpec as P

EPSILON = 1e-05
NEGATIVE = -1e30
MESH = pl.DeviceIdType.MESH
F32 = jnp.float32
BF16 = jnp.bfloat16


def passed_along(block, axis, distance):
    devices = range(lax.axis_size(axis))
    route = [(i - distance, i) for i in devices if i - distance in devices]
    return lax.ppermute(block, axis, route)


def swapped(block, axis):
    return lax.ppermute(block, axis, [(0, 1), (1, 0)])


def rounded(values):
    return lax.optimization_barrier(values.astype(BF16)).astype(F32)


def matmul(left_op, right_op):
    return jnp.dot(left_op, right_op, preferred_element_type=F32)


def matmul_left(left_op, right_op):
    return lax.dot_general(left_op, right_op, (((0,), (0,)), ((), ())), preferred_element_type=F32)


def matmul_right(left_op, right_op):
    return lax.dot_general(left_op, right_op, (((1,), (1,)), ((), ())), preferred_element_type=F32)


def norm_rows(values):
    inv_rms = lax.rsqrt(jnp.mean(values * values, axis=-1, keepdims=True) + EPSILON)
    return (values * inv_rms, inv_rms)


def norm_back(dnormed, normed, inv_rms):
    return inv_rms * dnormed - normed * inv_rms * jnp.mean(dnormed * normed, axis=-1, keepdims=True)


def head_sums(values, head):
    heads = values.shape[1] // head
    owner = (jnp.arange(values.shape[1])[:, None] // head == jnp.arange(heads)[None, :]).astype(F32)
    sums = jnp.dot(values, owner, precision=lax.Precision.HIGHEST, preferred_element_type=F32)
    return jnp.dot(sums, owner.T, precision=lax.Precision.HIGHEST, preferred_element_type=F32)


def norm_heads(values, head):
    inv_rms = lax.rsqrt(head_sums(values * values, head) / head + EPSILON)
    return (values * inv_rms, inv_rms)


def norm_heads_back(dnormed, normed, inv_rms, head):
    return inv_rms * dnormed - normed * inv_rms * (head_sums(dnormed * normed, head) / head)


def busy(microseconds):
    return pl.CostEstimate(flops=int(microseconds), bytes_accessed=1 << 16, transcendentals=0)


def corners():
    me = lax.axis_index("fsdp")
    beside = me + 1 - 2 * lax.rem(me, 2)
    across = lax.rem(me + 2, 4)
    return me, beside, across, lax.rem(beside + 2, 4)


def greet_sides():
    _, beside, across, _ = corners()
    barrier = pltpu.get_barrier_semaphore()
    for target in (beside, across):
        pl.semaphore_signal(barrier, inc=1, device_id={"fsdp": target}, device_id_type=MESH)
    pl.semaphore_wait(barrier, 2)


def to_side(src, dst, send_sem, recv_sem, target):
    return pltpu.make_async_remote_copy(
        src_ref=src,
        dst_ref=dst,
        send_sem=send_sem,
        recv_sem=recv_sem,
        device_id={"fsdp": target},
        device_id_type=MESH,
    )


class SideGather:
    def __init__(self, block, whole, send_sem, recv_sem, own_sem):
        me, beside, across, _ = corners()
        rows = block.shape[0]
        half = rows // 2

        def part(owner, start, size):
            return whole.at[pl.ds(pl.multiple_of(owner * rows + start, half), size)]

        self.first = to_side(block, part(me, 0, rows), send_sem.at[0], recv_sem.at[0], beside)
        self.second = to_side(block, part(me, 0, rows), send_sem.at[1], recv_sem.at[1], across)
        at = part(beside, 0, half)
        self.third = to_side(at, at, send_sem.at[2], recv_sem.at[2], across)
        at = part(across, half, half)
        self.fourth = to_side(at, at, send_sem.at[3], recv_sem.at[3], beside)
        self.own = pltpu.make_async_copy(block, part(me, 0, rows), own_sem)

    def start(self):
        self.first.start()
        self.second.start()
        self.own.start()

    def relay(self):
        self.first.wait_recv()
        self.third.start()
        self.second.wait_recv()
        self.fourth.start()

    def finish(self):
        self.own.wait()
        self.first.wait_send()
        self.second.wait_send()
        self.third.wait()
        self.fourth.wait()


def gather_kernel(block, whole, send_sem, recv_sem, own_sem):
    greet_sides()
    gather = SideGather(block, whole, send_sem, recv_sem, own_sem)
    gather.start()
    gather.relay()
    gather.finish()


def gathered(array, collective_id):
    rows, width = array.shape
    assert lax.axis_size("fsdp") == 4
    dma = pltpu.SemaphoreType.DMA
    return pl.pallas_call(
        gather_kernel,
        out_shape=jax.ShapeDtypeStruct((4 * rows, width), array.dtype),
        in_specs=[pl.BlockSpec(memory_space=pltpu.VMEM)],
        out_specs=pl.BlockSpec(memory_space=pltpu.VMEM),
        scratch_shapes=[dma((4,)), dma((4,)), dma],
        compiler_params=pltpu.CompilerParams(
            collective_id=collective_id, has_side_effects=True, vmem_limit_bytes=8 << 20
        ),
        cost_estimate=busy(25),
    )(array)


def gather_swap_kernel(block, pieces, whole, swapped_out, send_sem, recv_sem, own_sem, cross_send, cross_recv, keep_sem):
    me, beside, across, opposite = corners()
    barrier = pltpu.get_barrier_semaphore()
    for target in (beside, across, opposite):
        pl.semaphore_signal(barrier, inc=1, device_id={"fsdp": target}, device_id_type=MESH)
    pl.semaphore_wait(barrier, 3)
    gather = SideGather(block, whole, send_sem, recv_sem, own_sem)
    gather.start()
    crossing = []
    for step in range(1, 4):
        target = lax.rem(me + step, 4)
        crossing.append(
            to_side(pieces.at[target], swapped_out.at[me], cross_send.at[step], cross_recv.at[step], target)
        )
        crossing[-1].start()
    keep = pltpu.make_async_copy(pieces.at[me], swapped_out.at[me], keep_sem)
    keep.start()
    gather.relay()
    gather.finish()
    keep.wait()
    for copy in crossing:
        copy.wait()


def gathered_swapped(array, pieces, collective_id):
    rows, width = array.shape
    dma = pltpu.SemaphoreType.DMA
    vmem = pl.BlockSpec(memory_space=pltpu.VMEM)
    hbm = pl.BlockSpec(memory_space=pl.ANY)
    return pl.pallas_call(
        gather_swap_kernel,
        out_shape=(
            jax.ShapeDtypeStruct((4 * rows, width), array.dtype),
            jax.ShapeDtypeStruct(pieces.shape, pieces.dtype),
        ),
        in_specs=[vmem, hbm],
        out_specs=[vmem, hbm],
        scratch_shapes=[dma((4,)), dma((4,)), dma, dma((4,)), dma((4,)), dma],
        compiler_params=pltpu.CompilerParams(
            collective_id=collective_id, has_side_effects=True, vmem_limit_bytes=8 << 20
        ),
        cost_estimate=busy(25),
    )(array, pieces)


class SideReduce:
    def __init__(self, blocks, total, beside_got, across_got, passed, passed_got, send_sem, recv_sem):
        self.refs = blocks, total, beside_got, across_got, passed, passed_got
        me, beside, across, opposite = corners()
        self.me, self.beside, self.across = me, beside, across
        self.copies = []
        for index, (turn, target, got) in enumerate(((0, beside, beside_got), (1, across, across_got))):
            for slot, owner in ((1, opposite), (0, target)):
                self.copies.append(
                    to_side(
                        blocks.at[self.part(owner, turn)],
                        got.at[slot],
                        send_sem.at[2 * index + slot],
                        recv_sem.at[2 * index + slot],
                        target,
                    )
                )
        self.onward = [
            to_side(passed.at[turn], passed_got.at[turn], send_sem.at[4 + turn], recv_sem.at[4 + turn], owner)
            for turn, owner in ((0, across), (1, beside))
        ]

    def part(self, owner, turn):
        half = self.refs[1].shape[0] // 2
        return pl.ds(pl.multiple_of(owner * 2 * half + turn * half, half), half)

    def start(self):
        for index in (0, 2, 1, 3):
            self.copies[index].start()

    def relay(self):
        blocks, _, beside_got, across_got, passed, _ = self.refs
        for turn, owner, index, got in ((0, self.across, 0, beside_got), (1, self.beside, 2, across_got)):
            self.copies[index].wait_recv()
            passed[turn] = (blocks[self.part(owner, turn)].astype(F32) + got[1].astype(F32)).astype(BF16)
            self.onward[turn].start()

    def finish(self):
        blocks, total, beside_got, across_got, _, passed_got = self.refs
        half = total.shape[0] // 2
        for turn, index, got in ((0, 1, beside_got), (1, 3, across_got)):
            self.copies[index].wait_recv()
            total[pl.ds(turn * half, half)] = blocks[self.part(self.me, turn)].astype(F32) + got[0].astype(F32)
        for turn in range(2):
            self.onward[turn].wait_recv()
            at = pl.ds(turn * half, half)
            total[at] = total[at] + passed_got[turn].astype(F32)
        for copy in self.copies + self.onward:
            copy.wait_send()


def reduce_kernel(blocks, total, beside_got, across_got, passed, passed_got, send_sem, recv_sem):
    greet_sides()
    reduction = SideReduce(blocks, total, beside_got, across_got, passed, passed_got, send_sem, recv_sem)
    reduction.start()
    reduction.relay()
    reduction.finish()


def reduced(partial, collective_id):
    rows, width = partial.shape[0] // 4, partial.shape[1]
    assert lax.axis_size("fsdp") == 4
    dma = pltpu.SemaphoreType.DMA
    pair = pltpu.VMEM((2, rows // 2, width), BF16)
    return pl.pallas_call(
        reduce_kernel,
        out_shape=jax.ShapeDtypeStruct((rows, width), F32),
        in_specs=[pl.BlockSpec(memory_space=pltpu.VMEM)],
        out_specs=pl.BlockSpec(memory_space=pltpu.VMEM),
        scratch_shapes=[pair, pair, pair, pair, dma((6,)), dma((6,))],
        compiler_params=pltpu.CompilerParams(
            collective_id=collective_id, has_side_effects=True, vmem_limit_bytes=16 << 20
        ),
        cost_estimate=busy(25),
    )(partial.astype(BF16))


def tail_kernel(
    counts,
    gate_in,
    up_in,
    down_in,
    query_in,
    kv_in,
    proj_in,
    conv_b_in,
    conv_c_in,
    conv_x_in,
    conv_o_in,
    small_in,
    second_gu_in,
    second_down_in,
    gu_out,
    down_out,
    rest_out,
    a_own,
    a_other,
    a_sum,
    a_done,
    b_own,
    b_other,
    b_sum,
    b_done,
    c_own,
    c_other,
    c_got,
    own_sem,
    pair_send,
    pair_recv,
    c_own_sem,
    c_pair_send,
    c_pair_recv,
    c_send,
    c_recv,
    a_up_send,
    a_up_recv,
    a_back_send,
    a_back_recv,
    a_out_send,
    b_up_send,
    b_up_recv,
    b_back_send,
    b_back_recv,
    b_out_send,
    b_keep_sem,
    gu_recv,
    down_recv,
    rest_recv,
    second_send,
    second_recv,
):
    n_ctx, n_fsdp = counts
    section = lax.axis_index("section")
    place = lax.axis_index("ctx")
    group = lax.axis_index("fsdp")
    other = 1 - section
    a_chunks, a_rows, a_width = a_own.shape
    b_chunks, b_rows, b_width = b_own.shape
    half = gate_in.shape[0] // n_fsdp // 2
    subs = half // a_rows
    per_kind = n_fsdp * subs
    down_half = down_in.shape[0] // 2
    down_chunks = down_half // b_rows
    c_rows = c_own.shape[1]
    mixers = (query_in, kv_in, proj_in, conv_b_in, conv_c_in, conv_x_in, conv_o_in)
    n_mix = len(mixers)
    cut = 3 * half // b_rows
    c_parts = ((0, cut), (cut, c_rows // b_rows))
    paired = a_chunks // 2
    mix_start = 2 * down_chunks
    mix_chunks = b_chunks - mix_start
    second = paired + down_chunks // 2
    ticks = second + mix_chunks // 2
    tail = 2 * (n_ctx - 1)

    barrier = pltpu.get_barrier_semaphore()
    for step in range(1, 2 * n_fsdp):
        flat = lax.rem(section * n_fsdp + group + step, 2 * n_fsdp)
        pl.semaphore_signal(
            barrier,
            inc=1,
            device_id={"section": flat // n_fsdp, "fsdp": lax.rem(flat, n_fsdp)},
            device_id_type=MESH,
        )

    @pl.when(place > 0)
    def _():
        pl.semaphore_signal(barrier, inc=1, device_id={"ctx": place - 1}, device_id_type=MESH)

    @pl.when(place < n_ctx - 1)
    def _():
        pl.semaphore_signal(barrier, inc=1, device_id={"ctx": place + 1}, device_id_type=MESH)

    at_edge = (place == 0) | (place == n_ctx - 1)

    @pl.when(at_edge)
    def _():
        pl.semaphore_wait(barrier, 2 * n_fsdp)

    @pl.when(jnp.logical_not(at_edge))
    def _():
        pl.semaphore_wait(barrier, 2 * n_fsdp + 1)

    def half_rows(owner, which):
        return pl.ds(pl.multiple_of(owner * (2 * half) + which * half, half), half)

    a_part, b_part = a_rows // 2, b_width // 2

    def a_at(buffer, k, way):
        return buffer.at[k, pl.ds(way * a_part, a_part)]

    def b_at(buffer, k, way):
        return buffer.at[k, :, pl.ds(way * b_part, b_part)]

    def opening(k, way):
        copies = []
        kind, rest = divmod(k, per_kind)
        owner, sub = divmod(rest, subs)
        source = (gate_in, up_in)[kind]
        spots = []
        for which in (section, other):
            start = owner * (2 * half) + which * half + sub * a_rows + way * a_part
            spots.append(source.at[pl.ds(pl.multiple_of(start, a_part), a_part)])
        spot = 2 * k + way
        copies.append((spots, a_at(a_own, k, way), a_at(a_other, k, way), spot))
        if k < down_chunks:
            spots = [
                down_in.at[
                    pl.ds(pl.multiple_of(which * down_half + k * b_rows, b_rows), b_rows),
                    pl.ds(way * b_part, b_part),
                ]
                for which in (section, other)
            ]
            copies.append((spots, b_at(b_own, k, way), b_at(b_other, k, way), 2 * a_chunks + spot))
        for (mine, theirs), own_dst, other_dst, spot in copies:
            pltpu.make_async_copy(mine, own_dst, own_sem.at[spot]).start()
            pltpu.make_async_remote_copy(
                src_ref=theirs,
                dst_ref=other_dst,
                send_sem=pair_send.at[spot],
                recv_sem=pair_recv.at[spot],
                device_id={"section": other},
                device_id_type=MESH,
            ).start()

    for k in range(a_chunks):
        for way in range(2):
            opening(k, way)
    for k in range(down_chunks):
        for way in range(2):
            pltpu.make_async_copy(
                second_down_in.at[pl.ds(k * b_rows, b_rows), pl.ds(way * b_part, b_part)],
                b_at(b_own, down_chunks + k, way),
                own_sem.at[2 * (a_chunks + down_chunks + k) + way],
            ).start()
    c_local, c_pair = ([], []), ([], [])
    for kind, source in enumerate(mixers):
        part = 0 if kind < 3 else 1
        for owner in range(n_fsdp):
            index = owner * (n_mix + 1) + kind
            place_at = pl.ds(kind * half, half)
            c_local[part].append(
                pltpu.make_async_copy(
                    source.at[half_rows(owner, section)], c_own.at[owner, place_at], c_own_sem.at[index]
                )
            )
            c_pair[part].append(
                pltpu.make_async_remote_copy(
                    src_ref=source.at[half_rows(owner, other)],
                    dst_ref=c_other.at[owner, place_at],
                    send_sem=c_pair_send.at[index],
                    recv_sem=c_pair_recv.at[index],
                    device_id={"section": other},
                    device_id_type=MESH,
                )
            )
    for owner in range(n_fsdp):
        small_at = pl.ds(n_mix * half, c_rows - n_mix * half)
        index = owner * (n_mix + 1) + n_mix
        c_local[1].append(
            pltpu.make_async_copy(small_in.at[section], c_own.at[owner, small_at], c_own_sem.at[index])
        )
        c_pair[1].append(
            pltpu.make_async_remote_copy(
                src_ref=small_in.at[other],
                dst_ref=c_other.at[owner, small_at],
                send_sem=c_pair_send.at[index],
                recv_sem=c_pair_recv.at[index],
                device_id={"section": other},
                device_id_type=MESH,
            )
        )
    for part in range(2):
        for copy in c_pair[part]:
            copy.start()
        for copy in c_local[part]:
            copy.start()
    b_own[b_chunks - 1] = jnp.zeros((b_rows, b_width), BF16)
    _, beside, across, opposite = corners()

    def span(first, last):
        return pl.ds(first * b_rows, (last - first) * b_rows)

    def mixer_spans(part):
        first, last = c_parts[part]
        middle = (first + last) // 2
        return (first, middle, beside, across), (middle, last, across, beside)

    def mixer_copies(part):
        opening, onward = [], []
        for turn, (first, last, near, far) in enumerate(mixer_spans(part)):
            at = span(first, last)
            for slot, owner in ((0, opposite), (1, near)):
                opening.append(
                    to_side(
                        c_own.at[owner, at],
                        c_got.at[slot, at],
                        c_send.at[part, 3 * turn + slot],
                        c_recv.at[part, 3 * turn + slot],
                        near,
                    )
                )
            onward.append(
                to_side(
                    c_own.at[far, at],
                    c_got.at[2, at],
                    c_send.at[part, 3 * turn + 2],
                    c_recv.at[part, 3 * turn + 2],
                    far,
                )
            )
        return opening, onward

    def mixer_sum(part, owner):
        kinds = range(3) if part == 0 else range(3, n_mix + 1)
        first, last = c_parts[part]
        for kind in kinds:
            size = half if kind < n_mix else c_rows - n_mix * half
            at = c_own.at[owner, pl.ds(kind * half, size)]
            index = owner * (n_mix + 1) + kind
            pltpu.make_async_copy(at, at, c_own_sem.at[index]).wait()
            pltpu.make_async_copy(at, at, c_pair_recv.at[index]).wait()

        def add(index, carry):
            at = pl.ds(pl.multiple_of(index * b_rows, b_rows), b_rows)
            c_own[owner, at] = (c_own[owner, at].astype(F32) + c_other[owner, at].astype(F32)).astype(BF16)
            return carry

        lax.fori_loop(first, last, add, 0)

    def mixer_out(part):
        opening, _ = mixer_copies(part)
        for index in (0, 2, 1, 3):
            opening[index].start()

    def mixer_on(part):
        opening, onward = mixer_copies(part)
        for turn, (first, last, near, far) in enumerate(mixer_spans(part)):
            opening[2 * turn].wait_recv()

            def add(index, carry, far=far):
                at = pl.ds(pl.multiple_of(index * b_rows, b_rows), b_rows)
                c_own[far, at] = (c_own[far, at].astype(F32) + c_got[0, at].astype(F32)).astype(BF16)
                return carry

            lax.fori_loop(first, last, add, 0)
            onward[turn].start()

    def mixer_in(part):
        opening, onward = mixer_copies(part)
        for turn in range(2):
            opening[2 * turn + 1].wait_recv()
            onward[turn].wait_recv()
        first, last = c_parts[part]

        def add(index, carry):
            at = pl.ds(pl.multiple_of(index * b_rows, b_rows), b_rows)
            total = c_own[group, at].astype(F32) + c_got[1, at].astype(F32) + c_got[2, at].astype(F32)
            b_own[mix_start + index] = total.astype(BF16)
            return carry

        lax.fori_loop(first, last, add, 0)

    strip = half // n_ctx

    def second_copies(remote):
        for index in range(n_ctx * n_fsdp * 2):
            source, kind = index // 2, index % 2
            turn, owner = source // n_fsdp, source % n_fsdp
            src = second_gu_in.at[turn, owner, kind]
            dst = gu_out.at[
                kind,
                pl.ds(pl.multiple_of(section * half + turn * strip, strip), strip),
                pl.ds(owner * a_width, a_width),
            ]
            if remote:
                pltpu.make_async_remote_copy(
                    src_ref=src,
                    dst_ref=dst,
                    send_sem=second_send.at[0],
                    recv_sem=second_recv,
                    device_id={"section": 1},
                    device_id_type=MESH,
                ).start()
            else:
                pltpu.make_async_copy(src, dst, second_send.at[0]).start()

    def second_start():
        @pl.when(section == 1)
        def _():
            second_copies(False)

        @pl.when(section == 0)
        def _():
            second_copies(True)

    def a_target(k, way):
        kind = k // per_kind
        rest = lax.rem(k, per_kind)
        owner = rest // subs
        sub = lax.rem(rest, subs)
        start = section * half + sub * a_rows + way * a_part
        spot = gu_out.at[
            kind,
            pl.ds(pl.multiple_of(start, a_part), a_part),
            pl.ds(pl.multiple_of(group * a_width, 128), a_width),
        ]
        return kind, owner, spot

    def a_hand_out(k, way):
        kind, owner, spot = a_target(k, way)
        is_mine = (section == 0) & (group == owner)
        slot = 2 * k + way
        a_ref = a_at(a_done, k, way)

        @pl.when(is_mine)
        def _():
            pltpu.make_async_copy(a_ref, spot, a_out_send.at[slot]).start()

        @pl.when(jnp.logical_not(is_mine))
        def _():
            pltpu.make_async_remote_copy(
                src_ref=a_ref,
                dst_ref=spot,
                send_sem=a_out_send.at[slot],
                recv_sem=gu_recv.at[kind, section * n_fsdp + group],
                device_id={"section": 0, "fsdp": owner},
                device_id_type=MESH,
            ).start()

    def down_hand_out(k, way, keeper):
        slot = 2 * k + way
        b_ref = b_at(b_done, k, way)
        index = k - keeper * down_chunks
        at = down_out.at[
            pl.ds(pl.multiple_of(section * down_half + index * b_rows, b_rows), b_rows),
            pl.ds(way * b_part, b_part),
        ]

        @pl.when(section == keeper)
        def _():
            pltpu.make_async_copy(b_ref, at, b_out_send.at[slot]).start()

        @pl.when(section != keeper)
        def _():
            pltpu.make_async_remote_copy(
                src_ref=b_ref,
                dst_ref=at,
                send_sem=b_out_send.at[slot],
                recv_sem=down_recv,
                device_id={"section": keeper},
                device_id_type=MESH,
            ).start()

    def mix_hand_out(k, way):
        slot = 2 * k + way
        b_ref = b_at(b_done, k, way)
        at = rest_out.at[
            section,
            pl.ds(pl.multiple_of((k - mix_start) * b_rows, b_rows), b_rows),
            pl.ds(way * b_part, b_part),
        ]
        pltpu.make_async_copy(b_ref, at, b_keep_sem.at[slot]).start()
        pltpu.make_async_remote_copy(
            src_ref=b_ref,
            dst_ref=at,
            send_sem=b_out_send.at[slot],
            recv_sem=rest_recv,
            device_id={"section": other},
            device_id_type=MESH,
        ).start()

    def chain_copy(at, sems, slot, target):
        return pltpu.make_async_remote_copy(
            src_ref=at,
            dst_ref=at,
            send_sem=sems[0].at[slot],
            recv_sem=sems[1].at[slot],
            device_id={"ctx": target},
            device_id_type=MESH,
        )

    class Gates:
        hand_out = staticmethod(a_hand_out)

        @staticmethod
        def view(buffer, k, way):
            return a_at(buffer, k, way)

        own, sums, done = a_own, a_sum, a_done
        up, back = (a_up_send, a_up_recv), (a_back_send, a_back_recv)

        @staticmethod
        def term(k, way):
            slot = 2 * k + way
            at = a_at(a_own, k, way)
            pltpu.make_async_copy(at, at, own_sem.at[slot]).wait()
            pltpu.make_async_copy(at, at, pair_recv.at[slot]).wait()
            return at[...].astype(F32) + a_at(a_other, k, way)[...].astype(F32)

    class Downs:
        @staticmethod
        def hand_out(k, way):
            down_hand_out(k, way, 0)

        @staticmethod
        def view(buffer, k, way):
            return b_at(buffer, k, way)

        own, sums, done = b_own, b_sum, b_done
        up, back = (b_up_send, b_up_recv), (b_back_send, b_back_recv)

        @staticmethod
        def term(k, way):
            slot = 2 * a_chunks + 2 * k + way
            at = b_at(b_own, k, way)
            pltpu.make_async_copy(at, at, own_sem.at[slot]).wait()
            pltpu.make_async_copy(at, at, pair_recv.at[slot]).wait()
            return at[...].astype(F32) + b_at(b_other, k, way)[...].astype(F32)

    class Seconds(Downs):
        @staticmethod
        def hand_out(k, way):
            down_hand_out(k, way, 1)

        @staticmethod
        def term(k, way):
            at = b_at(b_own, k, way)
            pltpu.make_async_copy(at, at, own_sem.at[2 * a_chunks + 2 * k + way]).wait()
            return at[...].astype(F32)

    class Mixed(Downs):
        hand_out = staticmethod(mix_hand_out)

        @staticmethod
        def term(k, way):
            return b_at(b_own, k, way)[...].astype(F32)

    def upward(item, k, way, rank, ahead, behind):
        slot = 2 * k + way
        term = item.term(k, way)
        sums = item.view(item.sums, k, way)

        @pl.when(rank == 0)
        def _():
            sums[...] = term.astype(BF16)

        @pl.when(rank > 0)
        def _():
            chain_copy(sums, item.up, slot, behind).wait_recv()

        @pl.when((rank > 0) & (rank < n_ctx - 1))
        def _():
            sums[...] = (term + sums[...].astype(F32)).astype(BF16)

        @pl.when(rank < n_ctx - 1)
        def _():
            chain_copy(sums, item.up, slot, ahead).start()

        @pl.when(rank == n_ctx - 1)
        def _():
            done = item.view(item.done, k, way)
            done[...] = (term + sums[...].astype(F32)).astype(BF16)
            chain_copy(done, item.back, slot, behind).start()
            item.hand_out(k, way)

    def backward(item, k, way, rank, ahead, behind):
        slot = 2 * k + way
        done = item.view(item.done, k, way)
        chain_copy(done, item.back, slot, ahead).wait_recv()

        @pl.when(rank > 0)
        def _():
            chain_copy(done, item.back, slot, behind).start()

        item.hand_out(k, way)

    def on_step(action, step, active, *where):
        early = active & (step < paired)

        @pl.when(early)
        def _():
            at = jnp.clip(step, 0, paired - 1)
            for index in range(2):
                action(Gates, 2 * at + index, *where)

            @pl.when(lax.rem(at, 4) < 3)
            def _():
                action(Downs, 3 * (at // 4) + lax.rem(at, 4), *where)

        @pl.when(active & (step >= paired) & (step < second))
        def _():
            at = jnp.clip(step - paired, 0, down_chunks // 2 - 1)
            for index in range(2):
                action(Seconds, down_chunks + 2 * at + index, *where)

        @pl.when(active & (step >= second))
        def _():
            at = jnp.clip(step - second, 0, mix_chunks // 2 - 1)
            for index in range(2):
                action(Mixed, mix_start + 2 * at + index, *where)

    lanes = []
    for way in range(2):
        rank = place if way == 0 else n_ctx - 1 - place
        ahead = place + 1 if way == 0 else place - 1
        behind = place - 1 if way == 0 else place + 1
        lanes.append((way, rank, ahead, behind))

    def tick_step(tick, carry):
        for part, start in ((0, 1), (1, 5)):
            for owner in range(n_fsdp):

                @pl.when(tick == start + owner)
                def _(part=part, owner=owner):
                    mixer_sum(part, owner)

        events = (
            (4, mixer_out, 0),
            (8, mixer_out, 1),
            (10, mixer_on, 0),
            (15, mixer_on, 1),
            (second - 1, mixer_in, 0),
            (second + 3, mixer_in, 1),
        )
        for moment, action, part in events:

            @pl.when(tick == moment)
            def _(action=action, part=part):
                action(part)

        for way, rank, ahead, behind in lanes:
            step = tick - 2 * rank
            on_step(upward, step, (step >= 0) & (step < ticks), way, rank, ahead, behind)
            late = tick - 2 * (tail - rank)
            on_step(
                backward,
                late,
                (late >= 0) & (late < ticks) & (rank < n_ctx - 1),
                way,
                rank,
                ahead,
                behind,
            )

        return carry

    second_start()
    lax.fori_loop(0, ticks + 2 * tail, tick_step, 0)

    for part in range(2):
        for copy in c_pair[part]:
            copy.wait_send()
        opening, onward = mixer_copies(part)
        for copy in opening + onward:
            copy.wait_send()

    def settle_item(item, k, out_send):
        for way, rank, ahead, behind in lanes:
            slot = 2 * k + way

            @pl.when(rank < n_ctx - 1)
            def _(slot=slot, way=way, ahead=ahead):
                chain_copy(item.view(item.sums, k, way), item.up, slot, ahead).wait_send()

            @pl.when(rank > 0)
            def _(slot=slot, way=way, behind=behind):
                chain_copy(item.view(item.done, k, way), item.back, slot, behind).wait_send()

            ref = item.view(item.own, k, way)
            pltpu.make_async_copy(ref, ref, out_send.at[slot]).wait()

    def settle_gates(k, carry):
        settle_item(Gates, k, a_out_send)
        for way in range(2):
            ref = a_at(a_own, k, way)
            pltpu.make_async_copy(ref, ref, pair_send.at[2 * k + way]).wait()
        return carry

    lax.fori_loop(0, a_chunks, settle_gates, 0)

    def settle_rest(k, carry):
        settle_item(Mixed, k, b_out_send)
        for way in range(2):
            ref = b_at(b_own, k, way)

            @pl.when(k < down_chunks)
            def _(ref=ref, way=way):
                pltpu.make_async_copy(ref, ref, pair_send.at[2 * a_chunks + 2 * k + way]).wait()

            @pl.when(k >= mix_start)
            def _(ref=ref, way=way):
                pltpu.make_async_copy(ref, ref, b_keep_sem.at[2 * k + way]).wait()

        return carry

    lax.fori_loop(0, b_chunks, settle_rest, 0)
    pltpu.make_async_copy(second_gu_in, second_gu_in, second_send.at[0]).wait()

    @pl.when(section == 0)
    def _():
        for kind in range(2):
            for source in range(2 * n_fsdp):

                @pl.when(group != source)
                def _(kind=kind, source=source):
                    region = gu_out.at[
                        kind,
                        pl.ds((source // n_fsdp) * half, half),
                        pl.ds((source % n_fsdp) * a_width, a_width),
                    ]
                    pltpu.make_async_copy(region, region, gu_recv.at[kind, source]).wait()

    @pl.when(section == 1)
    def _():
        pltpu.make_async_copy(second_gu_in, second_gu_in, second_recv).wait()

    region = down_out.at[pl.ds(pl.multiple_of(other * down_half, b_rows), down_half)]
    pltpu.make_async_copy(region, region, down_recv).wait()
    region = rest_out.at[other]
    pltpu.make_async_copy(region, region, rest_recv).wait()


def summed_gradients(first, mixers, small, second_gu, second_down):
    n_ctx, n_fsdp = lax.axis_size("ctx"), lax.axis_size("fsdp")
    gate, up, down = first
    half = gate.shape[0] // n_fsdp // 2
    a_rows, b_rows = half // 4, half * 3 // 8
    a_chunks = 2 * n_fsdp * 4
    a_width, b_width = gate.shape[1], down.shape[1]
    c_rows = len(mixers) * half + small.shape[1]
    down_chunks = down.shape[0] // 2 // b_rows
    b_chunks = 2 * down_chunks + c_rows // b_rows + 1
    assert c_rows % b_rows == 0 and b_chunks % 2 == 0 and down_chunks % 2 == 0
    assert down_chunks * 8 == a_chunks * 3
    rest = b_chunks - 2 * down_chunks
    dma = pltpu.SemaphoreType.DMA
    loads = 2 * (a_chunks + 2 * down_chunks)
    pieces = n_fsdp * (len(mixers) + 1)
    return pl.pallas_call(
        functools.partial(tail_kernel, (n_ctx, n_fsdp)),
        out_shape=(
            jax.ShapeDtypeStruct((2, 2 * half, n_fsdp * a_width), BF16),
            jax.ShapeDtypeStruct(down.shape, BF16),
            jax.ShapeDtypeStruct((2, rest * b_rows, b_width), BF16),
        ),
        in_specs=[pl.BlockSpec(memory_space=pl.ANY)] * (6 + len(mixers)),
        out_specs=[pl.BlockSpec(memory_space=pl.ANY)] * 3,
        scratch_shapes=[
            pltpu.VMEM((a_chunks, a_rows, a_width), BF16),
            pltpu.VMEM((a_chunks, a_rows, a_width), BF16),
            pltpu.VMEM((a_chunks, a_rows, a_width), BF16),
            pltpu.VMEM((a_chunks, a_rows, a_width), BF16),
            pltpu.VMEM((b_chunks, b_rows, b_width), BF16),
            pltpu.VMEM((down_chunks, b_rows, b_width), BF16),
            pltpu.VMEM((b_chunks, b_rows, b_width), BF16),
            pltpu.VMEM((b_chunks, b_rows, b_width), BF16),
            pltpu.VMEM((n_fsdp, c_rows, b_width), BF16),
            pltpu.VMEM((n_fsdp, c_rows, b_width), BF16),
            pltpu.VMEM((n_fsdp - 1, c_rows, b_width), BF16),
            dma((loads,)),
            dma((loads,)),
            dma((loads,)),
            dma((pieces,)),
            dma((pieces,)),
            dma((pieces,)),
            dma((2, 6)),
            dma((2, 6)),
            dma((2 * a_chunks,)),
            dma((2 * a_chunks,)),
            dma((2 * a_chunks,)),
            dma((2 * a_chunks,)),
            dma((2 * a_chunks,)),
            dma((2 * b_chunks,)),
            dma((2 * b_chunks,)),
            dma((2 * b_chunks,)),
            dma((2 * b_chunks,)),
            dma((2 * b_chunks,)),
            dma((2 * b_chunks,)),
            dma((2, 2 * n_fsdp)),
            dma,
            dma,
            dma((2,)),
            dma,
        ],
        compiler_params=pltpu.CompilerParams(
            collective_id=6, has_side_effects=True, vmem_limit_bytes=56 << 20
        ),
        cost_estimate=busy(160),
    )(gate, up, down, *mixers, small, second_gu, second_down)


class Columns:
    def __init__(self, holder, sources, targets, send_sem, recv_sem, pair_send, pair_recv, own_sem):
        self.count = 4
        self.holder = holder
        self.section = lax.axis_index("section")
        self.me = lax.axis_index("fsdp")
        self.sources, self.targets = sources, targets
        self.sems = send_sem, recv_sem, pair_send, pair_recv, own_sem
        self.rows = sources[0].shape[0]
        self.wide = targets[0].shape[1]
        self.steps = [(step, kind) for step in range(1, self.count) for kind in range(2)]

    def at_rows(self, out, owner):
        return out.at[pl.ds(pl.multiple_of(owner * self.rows, self.rows), self.rows)]

    def at_columns(self, source, owner):
        return source.at[:, pl.ds(pl.multiple_of(owner * self.wide, 128), self.wide)]

    def crossing(self, step, kind):
        target = lax.rem(self.me + step, self.count)
        return to_side(
            self.at_columns(self.sources[kind], target),
            self.at_rows(self.targets[kind], self.me),
            self.sems[0].at[kind, step],
            self.sems[1].at[kind, step],
            target,
        )

    def handed(self, step, kind):
        if kind == 2:
            src, dst = self.sources[2], self.targets[2]
        else:
            origin = lax.rem(self.me + self.count - step, self.count)
            dst = self.at_rows(self.targets[kind], origin)
            src = self.at_columns(self.sources[kind], self.me) if step == 0 else dst
        return pltpu.make_async_remote_copy(
            src_ref=src,
            dst_ref=dst,
            send_sem=self.sems[2].at[kind, step],
            recv_sem=self.sems[3].at[kind, step],
            device_id={"section": 1 - self.section},
            device_id_type=MESH,
        )

    def kept(self, kind):
        if kind == 2:
            return pltpu.make_async_copy(self.sources[2], self.targets[2], self.sems[4].at[2])
        return pltpu.make_async_copy(
            self.at_columns(self.sources[kind], self.me),
            self.at_rows(self.targets[kind], self.me),
            self.sems[4].at[kind],
        )

    def start(self):
        @pl.when(self.section == self.holder)
        def _():
            for step, kind in self.steps:
                self.crossing(step, kind).start()
            for kind in range(3):
                self.handed(0, kind).start()
            for kind in range(3):
                self.kept(kind).start()

    def relay(self):
        @pl.when(self.section == self.holder)
        def _():
            for step, kind in self.steps:
                self.crossing(step, kind).wait_recv()
                self.handed(step, kind).start()

    def arrive(self):
        every = [(0, kind) for kind in range(3)] + self.steps

        @pl.when(self.section == self.holder)
        def _():
            for kind in range(3):
                self.kept(kind).wait()

        @pl.when(self.section != self.holder)
        def _():
            for step, kind in every:
                self.handed(step, kind).wait_recv()

    def finish(self):
        every = [(0, kind) for kind in range(3)] + self.steps

        @pl.when(self.section == self.holder)
        def _():
            for step, kind in self.steps:
                self.crossing(step, kind).wait_send()
            for step, kind in every:
                self.handed(step, kind).wait_send()


class Chain:
    def __init__(self, count):
        self.count = count
        self.place = lax.axis_index("ctx")
        self.has_next = self.place < count - 1
        self.has_last = self.place > 0


def greet_mixed(chain, targets):
    barrier = pltpu.get_barrier_semaphore()
    for target in targets:
        pl.semaphore_signal(barrier, inc=1, device_id=target, device_id_type=MESH)

    @pl.when(chain.has_last)
    def _():
        pl.semaphore_signal(barrier, inc=1, device_id={"ctx": chain.place - 1}, device_id_type=MESH)

    @pl.when(chain.has_next)
    def _():
        pl.semaphore_signal(barrier, inc=1, device_id={"ctx": chain.place + 1}, device_id_type=MESH)

    inner = chain.has_last & chain.has_next

    @pl.when(inner)
    def _():
        pl.semaphore_wait(barrier, len(targets) + 2)

    @pl.when(jnp.logical_not(inner))
    def _():
        pl.semaphore_wait(barrier, len(targets) + 1)


def along(src, dst, send_sem, recv_sem, place):
    return pltpu.make_async_remote_copy(
        src_ref=src,
        dst_ref=dst,
        send_sem=send_sem,
        recv_sem=recv_sem,
        device_id={"ctx": place},
        device_id_type=MESH,
    )


def spread_heads(source, spread):
    rows = source.shape[0]
    low = lax.broadcasted_iota(jnp.int32, (rows, 128), 1) < 64
    for pair in range(source.shape[1] // 256):
        first = source[:, pair * 256 : pair * 256 + 128].astype(F32)
        second = source[:, pair * 256 + 128 : pair * 256 + 256].astype(F32)
        spread[4 * pair] = jnp.where(low, first, 0.0).astype(BF16)
        spread[4 * pair + 1] = jnp.where(low, pltpu.roll(first, 64, 1), 0.0).astype(BF16)
        spread[4 * pair + 2] = jnp.where(low, 0.0, pltpu.roll(second, 64, 1)).astype(BF16)
        spread[4 * pair + 3] = jnp.where(low, 0.0, second).astype(BF16)


def join_heads(spread, target):
    rows = target.shape[0]
    low = lax.broadcasted_iota(jnp.int32, (rows, 128), 1) < 64
    for pair in range(target.shape[1] // 256):
        parts = [spread(4 * pair + i).T for i in range(4)]
        target[:, pair * 256 : pair * 256 + 128] = jnp.where(low, parts[0], pltpu.roll(parts[1], 64, 1))
        target[:, pair * 256 + 128 : pair * 256 + 256] = jnp.where(low, pltpu.roll(parts[2], 64, 1), parts[3])


def mask_block(bias, length, place, block):
    rows = bias.shape[0]
    key_at = block * rows + lax.broadcasted_iota(jnp.int32, bias.shape, 0)
    query_at = place * rows + lax.broadcasted_iota(jnp.int32, bias.shape, 1)
    bias[...] = jnp.where((key_at <= query_at) & (key_at < length), 0.0, NEGATIVE)


def dot_right(left, right):
    return lax.dot_general(left, right, (((1,), (1,)), ((), ())), preferred_element_type=F32)


def dot_plain(left, right):
    return jnp.dot(left, right, preferred_element_type=F32)


def attend_kernel(
    n_ctx,
    length_ref,
    query,
    kv,
    d_block,
    gate_in,
    up_in,
    down_in,
    attended,
    log_total,
    kv_all,
    d_all,
    gate_out,
    up_out,
    down_out,
    w_gate,
    w_up,
    w_down,
    keep_sem,
    spread,
    bias,
    peak,
    total,
    out_t,
    kv_send,
    kv_recv,
    d_send,
    d_recv,
    d_own,
    send_sem,
    recv_sem,
    pair_send,
    pair_recv,
    own_sem,
):
    chain = Chain(n_ctx)
    place = chain.place
    section = lax.axis_index("section")
    me, beside, across, opposite = corners()
    greet_mixed(
        chain,
        [{"fsdp": beside}, {"fsdp": across}, {"fsdp": opposite}, {"section": 1 - section}],
    )
    rows = query.shape[0]
    half_width = kv.shape[1] // 2

    def block_rows(block):
        return pl.ds(pl.multiple_of(block * rows, rows), rows)

    def upward(step, src):
        return along(
            src,
            kv_all.at[block_rows(place - step)],
            kv_send.at[step],
            kv_recv.at[step + 1],
            place + 1,
        )

    def arriving(step):
        at = kv_all.at[block_rows(place - step)]
        return along(at, at, kv_send.at[step], kv_recv.at[step], place)

    @pl.when(chain.has_next)
    def _():
        upward(0, kv).start()

    gather = SideGather(d_block, d_all, d_send, d_recv, d_own)
    gather.start()
    columns = Columns(
        1, (gate_in, up_in, down_in), (w_gate, w_up, w_down), send_sem, recv_sem, pair_send, pair_recv, own_sem
    )
    columns.start()
    kv_all[block_rows(place)] = kv[...]
    spread_heads(query, spread)
    peak[...] = jnp.full(peak.shape, NEGATIVE, F32)
    total[...] = jnp.zeros(total.shape, F32)
    out_t[...] = jnp.zeros(out_t.shape, F32)
    length = length_ref[0]
    scale = 64 ** (-0.5)

    def attend_block(block):
        mask_block(bias, length, place, block)
        for pair in range(half_width // 128):
            key = kv_all[block_rows(block), pair * 128 : pair * 128 + 128]
            value_t = kv_all[block_rows(block), half_width + pair * 128 : half_width + pair * 128 + 128].T
            for index in range(4):
                head = 4 * pair + index
                scores = dot_right(key, spread[head]) * scale + bias[...]
                before = peak[head]
                now = jnp.maximum(before, jnp.max(scores, axis=0, keepdims=True))
                weights = jnp.exp(scores - now)
                fade = jnp.exp(before - now)
                peak[head] = now
                total[head] = total[head] * fade + jnp.sum(weights, axis=0, keepdims=True)
                out_t[head] = out_t[head] * fade + dot_plain(value_t, weights.astype(BF16))

    attend_block(place)
    gather.relay()

    def step_on(step, carry):
        @pl.when(step <= place)
        def _():
            arriving(step).wait_recv()

            @pl.when(chain.has_next)
            def _():
                upward(step, kv_all.at[block_rows(place - step)]).start()

            attend_block(place - step)

        return carry

    lax.fori_loop(1, n_ctx, step_on, 0)
    join_heads(lambda head: out_t[head] / total[head], attended)
    for head in range(spread.shape[0]):
        log_total[head] = peak[head] + jnp.log(total[head])
    columns.relay()
    columns.arrive()
    keeping = [
        pltpu.make_async_copy(src, dst, keep_sem.at[index])
        for index, (src, dst) in enumerate(((w_gate, gate_out), (w_up, up_out), (w_down, down_out)))
    ]
    for copy in keeping:
        copy.start()
    gather.finish()
    columns.finish()
    for copy in keeping:
        copy.wait()

    def settle(step, carry):
        @pl.when((step <= place) & chain.has_next)
        def _():
            upward(step, kv_all.at[block_rows(place - step)]).wait_send()

        return carry

    lax.fori_loop(0, n_ctx, settle, 0)


def attend(length, query, kv, d_block, gate, up, down, collective_id):
    n_ctx, count = lax.axis_size("ctx"), lax.axis_size("fsdp")
    rows, width = query.shape
    heads = width // 64
    dma = pltpu.SemaphoreType.DMA
    vmem = pl.BlockSpec(memory_space=pltpu.VMEM)
    hbm = pl.BlockSpec(memory_space=pl.ANY)
    column = jax.ShapeDtypeStruct((count * gate.shape[0], gate.shape[1] // count), gate.dtype)
    return pl.pallas_call(
        functools.partial(attend_kernel, n_ctx),
        out_shape=(
            jax.ShapeDtypeStruct((rows, width), F32),
            jax.ShapeDtypeStruct((heads, 1, rows), F32),
            jax.ShapeDtypeStruct((n_ctx * rows, kv.shape[1]), BF16),
            jax.ShapeDtypeStruct((count * rows, d_block.shape[1]), BF16),
            column,
            column,
            jax.ShapeDtypeStruct(down.shape, down.dtype),
        ),
        in_specs=[pl.BlockSpec(memory_space=pltpu.SMEM), vmem, vmem, vmem, hbm, hbm, hbm],
        out_specs=[vmem, vmem, vmem, vmem, hbm, hbm, hbm],
        scratch_shapes=[
            pltpu.VMEM(column.shape, BF16),
            pltpu.VMEM(column.shape, BF16),
            pltpu.VMEM(down.shape, BF16),
            dma((3,)),
            pltpu.VMEM((heads, rows, 128), BF16),
            pltpu.VMEM((rows, rows), F32),
            pltpu.VMEM((heads, 1, rows), F32),
            pltpu.VMEM((heads, 1, rows), F32),
            pltpu.VMEM((heads, 128, rows), F32),
            dma((n_ctx + 1,)),
            dma((n_ctx + 1,)),
            dma((4,)),
            dma((4,)),
            dma,
            dma((2, count)),
            dma((2, count)),
            dma((3, count)),
            dma((3, count)),
            dma((3,)),
        ],
        compiler_params=pltpu.CompilerParams(
            collective_id=collective_id, has_side_effects=True, vmem_limit_bytes=58 << 20
        ),
        cost_estimate=busy(50),
    )(length, query, kv, d_block, gate, up, down)


def attend_back_kernel(
    n_ctx,
    length_ref,
    query,
    kv_all,
    d_out,
    log_total,
    delta,
    blocks,
    d_query,
    d_kv,
    reduced_out,
    spread,
    d_spread,
    bias,
    d_query_t,
    term,
    leaving,
    coming,
    kv_send,
    kv_recv,
    beside_got,
    across_got,
    passed,
    passed_got,
    send_sem,
    recv_sem,
):
    chain = Chain(n_ctx)
    place = chain.place
    _, beside, across, _ = corners()
    greet_mixed(chain, [{"fsdp": beside}, {"fsdp": across}])
    rows = query.shape[0]
    half_width = kv_all.shape[1] // 2
    reduction = SideReduce(blocks, reduced_out, beside_got, across_got, passed, passed_got, send_sem, recv_sem)
    reduction.start()
    spread_heads(query, spread)
    spread_heads(d_out, d_spread)
    d_query_t[...] = jnp.zeros(d_query_t.shape, F32)
    length = length_ref[0]
    scale = 64 ** (-0.5)

    def downward(block):
        return along(leaving.at[block], coming.at[block], kv_send.at[block], kv_recv.at[block], place - 1)

    def step_on(block, carry):
        @pl.when(block <= place)
        def _():
            mask_block(bias, length, place, block)
            at = pl.ds(pl.multiple_of(block * rows, rows), rows)
            for pair in range(half_width // 128):
                lanes = slice(pair * 128, pair * 128 + 128)
                more = slice(half_width + pair * 128, half_width + pair * 128 + 128)
                key = kv_all[at, lanes]
                value = kv_all[at, more]
                key_t = key.T
                d_key = jnp.zeros((rows, 128), F32)
                d_value = jnp.zeros((rows, 128), F32)
                for index in range(4):
                    head = 4 * pair + index
                    scores = dot_right(key, spread[head]) * scale + bias[...]
                    prob = jnp.exp(scores - log_total[head])
                    d_prob = dot_right(value, d_spread[head])
                    d_scores = (prob * (d_prob - delta[head])).astype(BF16)
                    d_value = d_value + dot_plain(prob.astype(BF16), d_spread[head])
                    d_key = d_key + dot_plain(d_scores, spread[head])
                    d_query_t[head] = d_query_t[head] + dot_plain(key_t, d_scores)
                term[:, lanes] = d_key * scale
                term[:, more] = d_value

            @pl.when(chain.has_next)
            def _():
                along(
                    leaving.at[block], coming.at[block], kv_send.at[block], kv_recv.at[block], place
                ).wait_recv()
                term[...] = term[...] + coming[block].astype(F32)

            @pl.when(block < place)
            def _():
                leaving[block] = term[...].astype(BF16)
                downward(block).start()

            @pl.when(block == place)
            def _():
                d_kv[...] = term[...]

        @pl.when(block == 0)
        def _():
            reduction.relay()

        return carry

    lax.fori_loop(0, n_ctx, step_on, 0)
    join_heads(lambda head: d_query_t[head] * scale, d_query)
    reduction.finish()

    def settle(block, carry):
        @pl.when(block < place)
        def _():
            downward(block).wait_send()

        return carry

    lax.fori_loop(0, n_ctx, settle, 0)


def attend_back(length, query, kv_all, d_out, log_total, delta, blocks, collective_id):
    n_ctx = lax.axis_size("ctx")
    rows, width = query.shape
    heads = width // 64
    dma = pltpu.SemaphoreType.DMA
    vmem = pl.BlockSpec(memory_space=pltpu.VMEM)
    wide = jax.ShapeDtypeStruct((rows, width), F32)
    pair = pltpu.VMEM((2, rows // 2, blocks.shape[1]), BF16)
    return pl.pallas_call(
        functools.partial(attend_back_kernel, n_ctx),
        out_shape=(wide, jax.ShapeDtypeStruct((rows, kv_all.shape[1]), F32), wide),
        in_specs=[pl.BlockSpec(memory_space=pltpu.SMEM)] + [vmem] * 6,
        out_specs=[vmem] * 3,
        scratch_shapes=[
            pltpu.VMEM((heads, rows, 128), BF16),
            pltpu.VMEM((heads, rows, 128), BF16),
            pltpu.VMEM((rows, rows), F32),
            pltpu.VMEM((heads, 128, rows), F32),
            pltpu.VMEM((rows, kv_all.shape[1]), F32),
            pltpu.VMEM((n_ctx, rows, kv_all.shape[1]), BF16),
            pltpu.VMEM((n_ctx, rows, kv_all.shape[1]), BF16),
            dma((n_ctx,)),
            dma((n_ctx,)),
            pair,
            pair,
            pair,
            pair,
            dma((6,)),
            dma((6,)),
        ],
        compiler_params=pltpu.CompilerParams(
            collective_id=collective_id, has_side_effects=True, vmem_limit_bytes=56 << 20
        ),
        cost_estimate=busy(50),
    )(length, query, kv_all, d_out, log_total, delta, blocks)


class MixerGather:
    def __init__(self, sources, targets, send_sem, recv_sem, pair_send, pair_recv, own_sem):
        self.section = section = lax.axis_index("section")
        me, beside, across, opposite = corners()
        rows = sources[0].shape[0]
        half = rows // 2
        quarter = half // 2

        def at_rows(out, owner, extra, size):
            return out.at[pl.ds(pl.multiple_of(owner * rows + extra, quarter), size)]

        def pair(slot, at):
            return pltpu.make_async_remote_copy(
                src_ref=at,
                dst_ref=at,
                send_sem=pair_send.at[slot],
                recv_sem=pair_recv.at[slot],
                device_id={"section": 1 - section},
                device_id_type=MESH,
            )

        self.direct, self.onward, self.early, self.late, self.own = [], [], [], [], []
        start = section * half
        for index, (source, out) in enumerate(zip(sources, targets)):
            mine = source.at[pl.ds(pl.multiple_of(start, half), half)]
            spot = at_rows(out, me, start, half)
            slot = 4 * index
            self.direct.append(
                [
                    to_side(mine, spot, send_sem.at[slot], recv_sem.at[slot], beside),
                    to_side(mine, spot, send_sem.at[slot + 1], recv_sem.at[slot + 1], across),
                ]
            )
            passing = at_rows(out, beside, start, quarter), at_rows(out, across, start + quarter, quarter)
            self.onward.append(
                [
                    to_side(passing[0], passing[0], send_sem.at[slot + 2], recv_sem.at[slot + 2], across),
                    to_side(passing[1], passing[1], send_sem.at[slot + 3], recv_sem.at[slot + 3], beside),
                ]
            )
            self.early.append(
                [
                    pair(slot, at_rows(out, beside, start, half)),
                    pair(slot + 1, at_rows(out, across, start, half)),
                ]
            )
            self.late.append(
                [
                    pair(slot + 2, at_rows(out, opposite, start, quarter)),
                    pair(slot + 3, at_rows(out, opposite, start + quarter, quarter)),
                ]
            )
            self.own.append(pltpu.make_async_copy(source, at_rows(out, me, 0, rows), own_sem.at[index]))

    def start(self):
        for copies in self.direct:
            for copy in copies:
                copy.start()
        for copy in self.own:
            copy.start()

    def relay(self):
        for direct, onward, early in zip(self.direct, self.onward, self.early):
            for turn in range(2):
                direct[turn].wait_recv()
                onward[turn].start()
                early[turn].start()

    def relay_last(self):
        for onward, late in zip(self.onward, self.late):
            for turn in range(2):
                onward[turn].wait_recv()
                late[turn].start()

    def arrive(self, index):
        self.own[index].wait()
        for copy in self.early[index] + self.late[index]:
            copy.wait_recv()

    def finish(self):
        for group in (self.direct, self.onward, self.early, self.late):
            for copies in group:
                for copy in copies:
                    copy.wait_send()


def front_kernel(
    n_ctx,
    x_ref,
    gains,
    taps,
    conv_in,
    conv_out,
    gate_in,
    up_in,
    down_in,
    in_out,
    out_out,
    gate_out,
    up_out,
    down_out,
    projected,
    convolved,
    z_low,
    mixed,
    rim,
    act_all,
    w_in,
    w_out,
    w_gate,
    w_up,
    w_down,
    act1,
    act2,
    last_rows,
    rim_sem,
    mix_send,
    mix_recv,
    mix_pair_send,
    mix_pair_recv,
    mix_own,
    send_sem,
    recv_sem,
    pair_send,
    pair_recv,
    own_sem,
    act_send,
    act_recv,
    act_own,
    keep_sem,
):
    chain = Chain(n_ctx)
    section = lax.axis_index("section")
    _, beside, across, opposite = corners()
    greet_mixed(
        chain,
        [{"fsdp": beside}, {"fsdp": across}, {"fsdp": opposite}, {"section": 1 - section}],
    )
    mixers = MixerGather(
        (conv_in, conv_out), (w_in, w_out), mix_send, mix_recv, mix_pair_send, mix_pair_recv, mix_own
    )
    mixers.start()
    columns = Columns(
        0, (gate_in, up_in, down_in), (w_gate, w_up, w_down), send_sem, recv_sem, pair_send, pair_recv, own_sem
    )
    gather = SideGather(act2, act_all, act_send, act_recv, act_own)
    keeping = [
        pltpu.make_async_copy(src, dst, keep_sem.at[index])
        for index, (src, dst) in enumerate(
            ((w_in, in_out), (w_out, out_out), (w_gate, gate_out), (w_up, up_out), (w_down, down_out))
        )
    ]
    rows, width = x_ref.shape
    strip = 64

    def normalize(values, gain):
        inv_rms = lax.rsqrt(jnp.mean(values * values, axis=-1, keepdims=True) + EPSILON)
        return (values * inv_rms * gain).astype(BF16)

    def first_norm(index, carry):
        at = pl.ds(pl.multiple_of(index * strip, strip), strip)
        act1[at] = normalize(x_ref[at].astype(F32), gains[0:1])
        return carry

    lax.fori_loop(0, rows // strip, first_norm, 0)
    mixers.relay()
    columns.start()
    mixers.relay_last()
    mixers.arrive(0)
    keeping[0].start()
    wide = 512

    def project(index, carry):
        at = pl.ds(pl.multiple_of(index * wide, wide), wide)
        projected[:, at] = dot_plain(act1[...], w_in[:, at])
        return carry

    lax.fori_loop(0, projected.shape[1] // wide, project, 0)
    tail_at = pl.ds(rows - 16, 16)
    last_rows[...] = (projected[tail_at, :width] * projected[tail_at, 2 * width :]).astype(BF16)
    to_next = along(last_rows, rim, rim_sem.at[0], rim_sem.at[1], chain.place + 1)

    @pl.when(chain.has_next)
    def _():
        to_next.start()

    @pl.when(chain.has_last)
    def _():
        along(last_rows, rim, rim_sem.at[0], rim_sem.at[1], chain.place).wait_recv()

    @pl.when(jnp.logical_not(chain.has_last))
    def _():
        rim[...] = jnp.zeros(rim.shape, BF16)

    part = 128
    row_at = lax.broadcasted_iota(jnp.int32, (rows, part), 0)

    def convolve(index, carry):
        def lanes(offset):
            return pl.ds(pl.multiple_of(offset * width + index * part, part), part)

        product = (projected[:, lanes(0)] * projected[:, lanes(2)]).astype(BF16).astype(F32)
        edge = rim[:, lanes(0)].astype(F32)
        near, far = edge[15:16], edge[14:15]
        one = jnp.where(row_at >= 1, pltpu.roll(product, 1, 0), near)
        two = jnp.where(row_at >= 2, pltpu.roll(product, 2, 0), jnp.where(row_at == 1, near, far))
        tap = taps[:, lanes(0)]
        value = tap[0:1] * two + tap[1:2] * one + tap[2:3] * product
        convolved[:, lanes(0)] = value
        z_low[:, lanes(0)] = (projected[:, lanes(1)] * value).astype(BF16)
        return carry

    lax.fori_loop(0, width // part, convolve, 0)
    mixers.arrive(1)
    keeping[1].start()

    def mix(index, carry):
        at = pl.ds(pl.multiple_of(index * wide, wide), wide)
        mixed[:, at] = dot_plain(z_low[...], w_out[:, at])
        return carry

    lax.fori_loop(0, width // wide, mix, 0)

    def second_norm(index, carry):
        at = pl.ds(pl.multiple_of(index * strip, strip), strip)
        act2[at] = normalize(x_ref[at].astype(F32) + mixed[at], gains[1:2])
        return carry

    lax.fori_loop(0, rows // strip, second_norm, 0)
    gather.start()
    gather.relay()
    columns.relay()
    columns.arrive()
    for copy in keeping[2:]:
        copy.start()
    gather.finish()
    columns.finish()
    mixers.finish()

    @pl.when(chain.has_next)
    def _():
        to_next.wait_send()

    for copy in keeping:
        copy.wait()


def front(x_low, gains, taps, conv_in, conv_out, gate, up, down, collective_id):
    n_ctx, count = lax.axis_size("ctx"), lax.axis_size("fsdp")
    assert count == 4
    rows, width = x_low.shape
    dma = pltpu.SemaphoreType.DMA
    vmem = pl.BlockSpec(memory_space=pltpu.VMEM)
    hbm = pl.BlockSpec(memory_space=pl.ANY)

    def whole(weight):
        return (count * weight.shape[0], weight.shape[1])

    column = (count * gate.shape[0], gate.shape[1] // count)
    weights = [whole(conv_in), whole(conv_out), column, column, down.shape]
    return pl.pallas_call(
        functools.partial(front_kernel, n_ctx),
        out_shape=tuple(jax.ShapeDtypeStruct(shape, BF16) for shape in weights)
        + (
            jax.ShapeDtypeStruct((rows, conv_in.shape[1]), F32),
            jax.ShapeDtypeStruct((rows, width), F32),
            jax.ShapeDtypeStruct((rows, width), BF16),
            jax.ShapeDtypeStruct((rows, width), F32),
            jax.ShapeDtypeStruct((16, width), BF16),
            jax.ShapeDtypeStruct((count * rows, width), BF16),
        ),
        in_specs=[vmem] * 3 + [hbm] * 5,
        out_specs=[hbm] * 5 + [vmem] * 6,
        scratch_shapes=[pltpu.VMEM(shape, BF16) for shape in weights]
        + [
            pltpu.VMEM((rows, width), BF16),
            pltpu.VMEM((rows, width), BF16),
            pltpu.VMEM((16, width), BF16),
            dma((2,)),
            dma((8,)),
            dma((8,)),
            dma((8,)),
            dma((8,)),
            dma((2,)),
            dma((2, count)),
            dma((2, count)),
            dma((3, count)),
            dma((3, count)),
            dma((3,)),
            dma((4,)),
            dma((4,)),
            dma,
            dma((5,)),
        ],
        compiler_params=pltpu.CompilerParams(
            collective_id=collective_id, has_side_effects=True, vmem_limit_bytes=58 << 20
        ),
        cost_estimate=busy(70),
    )(x_low, gains, taps, conv_in, conv_out, gate, up, down)


def ffn_grads_kernel(
    blocks,
    d_gate,
    d_up,
    act_in,
    hidden_in,
    d_all_in,
    total,
    shared_gu,
    shared_down,
    act,
    hidden,
    d_all,
    load_sem,
    gu_all,
    gu_got,
    gu_sum,
    down_all,
    down_got,
    down_sum,
    keep_sem,
    beside_got,
    across_got,
    passed,
    passed_got,
    send_sem,
    recv_sem,
    pair_send,
    pair_recv,
):
    section = lax.axis_index("section")
    other = 1 - section
    _, beside, across, _ = corners()
    barrier = pltpu.get_barrier_semaphore()
    for target in ({"fsdp": beside}, {"fsdp": across}, {"section": other}):
        pl.semaphore_signal(barrier, inc=1, device_id=target, device_id_type=MESH)
    pl.semaphore_wait(barrier, 3)
    reduction = SideReduce(blocks, total, beside_got, across_got, passed, passed_got, send_sem, recv_sem)
    reduction.start()
    loads = [
        pltpu.make_async_copy(src, dst, load_sem.at[index])
        for index, (src, dst) in enumerate(((act_in, act), (hidden_in, hidden), (d_all_in, d_all)))
    ]
    for copy in loads:
        copy.start()
    tile = 256
    half = gu_got.shape[2]
    strips, owners, kinds, strip, _ = gu_sum.shape

    def gate_swap(kind, owner):
        start = owner * (2 * half) + other * half
        return pltpu.make_async_remote_copy(
            src_ref=gu_all.at[kind, pl.ds(pl.multiple_of(start, half), half)],
            dst_ref=gu_got.at[kind, owner],
            send_sem=pair_send.at[kind * owners + owner],
            recv_sem=pair_recv.at[kind * owners + owner],
            device_id={"section": other},
            device_id_type=MESH,
        )

    loads[0].wait()
    for kind, right in enumerate((d_gate, d_up)):

        def column(owner, carry, kind=kind, right=right):
            lanes = pl.ds(pl.multiple_of(owner * tile, tile), tile)
            gu_all[kind, lanes] = dot_plain(act[:, lanes].T, right[...]).astype(BF16)
            gate_swap(kind, owner).start()
            return carry

        lax.fori_loop(0, owners, column, 0)
    reduction.relay()
    for copy in loads[1:]:
        copy.wait()
    height = hidden.shape[1]

    def down_tile(index, carry):
        lanes = pl.ds(pl.multiple_of(index * tile, tile), tile)
        down_all[lanes] = dot_plain(hidden[:, lanes].T, d_all[...]).astype(BF16)
        return carry

    lax.fori_loop(0, height // tile, down_tile, 0)
    rest = height // tile * tile
    if rest < height:
        down_all[rest:] = dot_plain(hidden[:, rest:].T, d_all[...]).astype(BF16)
    down_half = height // 2
    down_swap = pltpu.make_async_remote_copy(
        src_ref=down_all.at[pl.ds(pl.multiple_of(other * down_half, 16), down_half)],
        dst_ref=down_got,
        send_sem=pair_send.at[kinds * owners],
        recv_sem=pair_recv.at[kinds * owners],
        device_id={"section": other},
        device_id_type=MESH,
    )
    down_swap.start()

    def join(index, carry):
        place = index // (owners * kinds)
        left = lax.rem(index, owners * kinds)
        owner, kind = left // kinds, lax.rem(left, kinds)

        @pl.when(place == 0)
        def _():
            gate_swap(kind, owner).wait_recv()

        mine = pl.ds(pl.multiple_of(owner * (2 * half) + section * half + place * strip, strip), strip)
        theirs = pl.ds(pl.multiple_of(place * strip, strip), strip)
        gu_sum[place, owner, kind] = (
            gu_all[kind, mine].astype(F32) + gu_got[kind, owner, theirs].astype(F32)
        ).astype(BF16)
        return carry

    lax.fori_loop(0, strips * owners * kinds, join, 0)
    keeping = [pltpu.make_async_copy(gu_sum, shared_gu, keep_sem.at[0])]
    keeping[0].start()
    down_swap.wait_recv()
    piece = 64

    def join_down(index, carry):
        theirs = pl.ds(pl.multiple_of(index * piece, piece), piece)
        mine = pl.ds(pl.multiple_of(section * down_half + index * piece, piece), piece)
        down_sum[theirs] = (down_all[mine].astype(F32) + down_got[theirs].astype(F32)).astype(BF16)
        return carry

    lax.fori_loop(0, down_half // piece, join_down, 0)
    keeping.append(pltpu.make_async_copy(down_sum, shared_down, keep_sem.at[1]))
    keeping[1].start()
    reduction.finish()

    def settle(index, carry):
        gate_swap(index // owners, lax.rem(index, owners)).wait_send()
        return carry

    lax.fori_loop(0, kinds * owners, settle, 0)
    down_swap.wait_send()
    for copy in keeping:
        copy.wait()


def ffn_grads(blocks, d_gate, d_up, act, hidden, d_all, collective_id):
    n_ctx, owners = lax.axis_size("ctx"), lax.axis_size("fsdp")
    rows, width = blocks.shape[0] // owners, blocks.shape[1]
    wide = d_gate.shape[1]
    half = width // owners // 2
    dma = pltpu.SemaphoreType.DMA
    vmem = pl.BlockSpec(memory_space=pltpu.VMEM)
    hbm = pl.BlockSpec(memory_space=pl.ANY)
    pair = pltpu.VMEM((2, rows // 2, width), BF16)
    summed = (n_ctx, owners, 2, half // n_ctx, wide)
    assert width // owners == 256 and wide // 2 % 64 == 0
    return pl.pallas_call(
        ffn_grads_kernel,
        out_shape=(
            jax.ShapeDtypeStruct((rows, width), F32),
            jax.ShapeDtypeStruct(summed, BF16),
            jax.ShapeDtypeStruct((wide // 2, width), BF16),
        ),
        in_specs=[vmem] * 3 + [hbm] * 3,
        out_specs=[vmem, hbm, hbm],
        scratch_shapes=[pltpu.VMEM(k.shape, BF16) for k in (act, hidden, d_all)]
        + [
            dma((3,)),
            pltpu.VMEM((2, width, wide), BF16),
            pltpu.VMEM((2, owners, half, wide), BF16),
            pltpu.VMEM(summed, BF16),
            pltpu.VMEM((wide, width), BF16),
            pltpu.VMEM((wide // 2, width), BF16),
            pltpu.VMEM((wide // 2, width), BF16),
            dma((2,)),
            pair,
            pair,
            pair,
            pair,
            dma((6,)),
            dma((6,)),
            dma((2 * owners + 1,)),
            dma((2 * owners + 1,)),
        ],
        compiler_params=pltpu.CompilerParams(
            collective_id=collective_id, has_side_effects=True, vmem_limit_bytes=58 << 20
        ),
        cost_estimate=busy(25),
    )(blocks, d_gate, d_up, act, hidden, d_all)


def back_kernel(
    n_ctx,
    blocks,
    d_gate,
    d_up,
    x_ref,
    mixed,
    d_h,
    gains,
    taps,
    z_low,
    rim,
    act_in,
    hidden_in,
    d_all_in,
    w_in_in,
    w_out_in,
    projected_in,
    convolved_in,
    gate_grad,
    up_grad,
    down_grad,
    b_grad,
    c_grad,
    x_grad,
    o_grad,
    d_x,
    small,
    act,
    hidden,
    d_all,
    w_in,
    w_out,
    projected,
    convolved,
    load_sem,
    stage_wide,
    stage,
    stage_sem,
    beside_got,
    across_got,
    passed,
    passed_got,
    send_sem,
    recv_sem,
    d_act,
    d_res,
    d_mixed,
    d_conv,
    d_proj,
    act1,
    edge,
    next_edge,
    edge_sem,
):
    chain = Chain(n_ctx)
    _, beside, across, _ = corners()
    greet_mixed(chain, [{"fsdp": beside}, {"fsdp": across}])
    reduction = SideReduce(blocks, d_act, beside_got, across_got, passed, passed_got, send_sem, recv_sem)
    reduction.start()
    loads = [
        pltpu.make_async_copy(src, dst, load_sem.at[index])
        for index, (src, dst) in enumerate(
            (
                (act_in, act),
                (hidden_in, hidden),
                (d_all_in, d_all),
                (convolved_in, convolved),
                (projected_in, projected),
                (w_out_in, w_out),
                (w_in_in, w_in),
            )
        )
    ]
    for copy in loads:
        copy.start()
    rows, width = x_ref.shape
    wide = d_gate.shape[1]
    tile = 256
    small[...] = jnp.zeros(small.shape, F32)

    def weight_grad(left, right, at_right, target, staging, slot):
        count = left.shape[1] // tile

        def leaving(index, at):
            return pltpu.make_async_copy(staging.at[at], target.at[index], stage_sem.at[slot + at])

        def step(index, carry):
            at = lax.rem(index, 2)
            lanes = pl.ds(pl.multiple_of(index * tile, tile), tile)

            @pl.when(index >= 2)
            def _():
                leaving(lanes, at).wait()

            staging[at] = dot_plain(left[:, lanes].T, right[:, at_right]).astype(BF16)
            leaving(lanes, at).start()
            return carry

        lax.fori_loop(0, count, step, 0)
        for index in range(min(2, count)):
            leaving(pl.ds(0, tile), index).wait()

    loads[0].wait()
    weight_grad(act, d_gate, slice(None), gate_grad, stage_wide, 0)
    weight_grad(act, d_up, slice(None), up_grad, stage_wide, 0)
    reduction.relay()
    loads[1].wait()
    loads[2].wait()
    odd = hidden.shape[1] % tile

    weight_grad(hidden, d_all, slice(None), down_grad, stage, 2)
    if odd:
        last = hidden.shape[1] - odd
        stage[0, :odd] = dot_plain(hidden[:, last:].T, d_all[...]).astype(BF16)
        copy = pltpu.make_async_copy(stage.at[0, pl.ds(0, odd)], down_grad.at[pl.ds(last, odd)], stage_sem.at[2])
        copy.start()
        copy.wait()
    reduction.finish()
    strip = 64

    def norm_strip(at, values, gain, d_values, row):
        inv_rms = lax.rsqrt(jnp.mean(values * values, axis=-1, keepdims=True) + EPSILON)
        normed = values * inv_rms
        small[row : row + 1] = small[row : row + 1] + jnp.sum(d_values * normed, axis=0, keepdims=True)
        d_normed = d_values * gain
        return inv_rms * d_normed - normed * inv_rms * jnp.mean(d_normed * normed, axis=-1, keepdims=True)

    def second_norm(index, carry):
        at = pl.ds(pl.multiple_of(index * strip, strip), strip)
        x_rows = x_ref[at].astype(F32)
        value = d_h[at].astype(F32) + norm_strip(at, x_rows + mixed[at], gains[1:2], d_act[at], 1)
        d_res[at] = value
        d_mixed[at] = value.astype(BF16)
        inv_rms = lax.rsqrt(jnp.mean(x_rows * x_rows, axis=-1, keepdims=True) + EPSILON)
        act1[at] = (x_rows * inv_rms * gains[0:1]).astype(BF16)
        return carry

    lax.fori_loop(0, rows // strip, second_norm, 0)
    for index in range(3, 6):
        loads[index].wait()

    def to_z(index, carry):
        at = pl.ds(pl.multiple_of(index * tile, tile), tile)
        d_conv[:, at] = dot_right(d_mixed[...], w_out[at])
        return carry

    lax.fori_loop(0, width // tile, to_z, 0)
    part = 128
    row_at = lax.broadcasted_iota(jnp.int32, (rows, part), 0)

    def lanes_of(offset, index):
        return pl.ds(pl.multiple_of(offset * width + index * part, part), part)

    def convolve_back(index, carry):
        lanes = lanes_of(0, index)
        product = (projected[:, lanes] * projected[:, lanes_of(2, index)]).astype(BF16).astype(F32)
        before = rim[:, lanes].astype(F32)
        near, far = before[15:16], before[14:15]
        one = jnp.where(row_at >= 1, pltpu.roll(product, 1, 0), near)
        two = jnp.where(row_at >= 2, pltpu.roll(product, 2, 0), jnp.where(row_at == 1, near, far))
        d_z = d_conv[:, lanes]
        d_proj[:, lanes_of(1, index)] = (d_z * convolved[:, lanes]).astype(BF16)
        d_value = d_z * projected[:, lanes_of(1, index)]
        d_conv[:, lanes] = d_value
        for row, source in ((2, two), (3, one), (4, product)):
            small[row : row + 1, lanes] = jnp.sum(d_value * source, axis=0, keepdims=True)
        tap = taps[:, lanes]
        edge[0:1, lanes] = tap[0:1] * d_value[0:1]
        edge[1:2, lanes] = tap[0:1] * d_value[1:2] + tap[1:2] * d_value[0:1]
        return carry

    lax.fori_loop(0, width // part, convolve_back, 0)
    edge[2:8] = jnp.zeros((6, width), F32)
    to_last = along(edge, next_edge, edge_sem.at[0], edge_sem.at[1], chain.place - 1)

    @pl.when(chain.has_last)
    def _():
        to_last.start()

    weight_grad(z_low, d_mixed, slice(None), o_grad, stage, 2)

    @pl.when(chain.has_next)
    def _():
        along(edge, next_edge, edge_sem.at[0], edge_sem.at[1], chain.place).wait_recv()

    @pl.when(jnp.logical_not(chain.has_next))
    def _():
        next_edge[...] = jnp.zeros(next_edge.shape, F32)

    def products_back(index, carry):
        lanes = lanes_of(0, index)
        d_value = d_conv[:, lanes]
        tap = taps[:, lanes]
        after = next_edge[:, lanes]
        one = jnp.where(row_at < rows - 1, pltpu.roll(d_value, rows - 1, 0), 0.0)
        two = jnp.where(row_at < rows - 2, pltpu.roll(d_value, rows - 2, 0), 0.0)
        joined = tap[2:3] * d_value + tap[1:2] * one + tap[0:1] * two
        joined = joined + jnp.where(row_at == rows - 2, after[0:1], 0.0)
        joined = joined + jnp.where(row_at == rows - 1, after[1:2], 0.0)
        joined = joined.astype(BF16).astype(F32)
        d_proj[:, lanes] = (joined * projected[:, lanes_of(2, index)]).astype(BF16)
        d_proj[:, lanes_of(2, index)] = (joined * projected[:, lanes]).astype(BF16)
        return carry

    lax.fori_loop(0, width // part, products_back, 0)
    loads[6].wait()

    def to_act(index, carry):
        at = pl.ds(pl.multiple_of(index * tile, tile), tile)
        d_act[:, at] = dot_right(d_proj[...], w_in[at])
        return carry

    lax.fori_loop(0, width // tile, to_act, 0)
    for offset, target in enumerate((b_grad, c_grad, x_grad)):
        weight_grad(act1, d_proj, slice(offset * width, (offset + 1) * width), target, stage, 2)

    def first_norm(index, carry):
        at = pl.ds(pl.multiple_of(index * strip, strip), strip)
        value = d_res[at] + norm_strip(at, x_ref[at].astype(F32), gains[0:1], d_act[at], 0)
        d_x[at] = value.astype(BF16)
        return carry

    lax.fori_loop(0, rows // strip, first_norm, 0)

    @pl.when(chain.has_last)
    def _():
        to_last.wait_send()


def conv_back(blocks, d_gate, d_up, local, kept, collective_id):
    n_ctx = lax.axis_size("ctx")
    x_low = local[0]
    act, hidden = kept[0], kept[1]
    rows, width = x_low.shape
    wide = d_gate.shape[1]
    dma = pltpu.SemaphoreType.DMA
    vmem = pl.BlockSpec(memory_space=pltpu.VMEM)
    hbm = pl.BlockSpec(memory_space=pl.ANY)
    pair = pltpu.VMEM((2, rows // 2, width), BF16)
    square = jax.ShapeDtypeStruct((width, width), BF16)
    column = jax.ShapeDtypeStruct((width, wide), BF16)
    return pl.pallas_call(
        functools.partial(back_kernel, n_ctx),
        out_shape=(
            column,
            column,
            jax.ShapeDtypeStruct((wide, width), BF16),
            square,
            square,
            square,
            square,
            jax.ShapeDtypeStruct((rows, width), BF16),
            jax.ShapeDtypeStruct((8, width), F32),
        ),
        in_specs=[vmem] * (3 + len(local)) + [hbm] * len(kept),
        out_specs=[hbm] * 7 + [vmem] * 2,
        scratch_shapes=[pltpu.VMEM(k.shape, k.dtype) for k in kept]
        + [
            dma((7,)),
            pltpu.VMEM((2, 256, wide), BF16),
            pltpu.VMEM((2, 256, width), BF16),
            dma((4,)),
            pair,
            pair,
            pair,
            pair,
            dma((6,)),
            dma((6,)),
            pltpu.VMEM((rows, width), F32),
            pltpu.VMEM((rows, width), F32),
            pltpu.VMEM((rows, width), BF16),
            pltpu.VMEM((rows, width), F32),
            pltpu.VMEM((rows, 3 * width), BF16),
            pltpu.VMEM((rows, width), BF16),
            pltpu.VMEM((8, width), F32),
            pltpu.VMEM((8, width), F32),
            dma((2,)),
        ],
        compiler_params=pltpu.CompilerParams(
            collective_id=collective_id, has_side_effects=True, vmem_limit_bytes=58 << 20
        ),
        cost_estimate=busy(35),
    )(blocks, d_gate, d_up, *local, *kept)


def ffn_forward(act, w_gate, w_up, w_down):
    gate_pre = matmul(act, w_gate)
    up_pre = matmul(act, w_up)
    hidden = (jax.nn.silu(gate_pre) * up_pre).astype(BF16)
    return matmul(hidden, w_down).astype(BF16), (act, gate_pre, up_pre, hidden)


def ffn_backward(d_all, kept, w_gate, w_up, w_down):
    act, gate_pre, up_pre, hidden = kept
    d_hidden = matmul_right(d_all, w_down)
    sigmoid = jax.nn.sigmoid(gate_pre)
    d_up = (d_hidden * gate_pre * sigmoid).astype(BF16)
    d_gate = (d_hidden * up_pre * sigmoid * (1.0 + gate_pre * (1.0 - sigmoid))).astype(BF16)
    terms = (matmul_right(d_gate, w_gate) + matmul_right(d_up, w_up)).astype(BF16)
    return terms, d_gate, d_up


def ffn_norm_back(d_act, residual, gain):
    normed, inv_rms = norm_rows(residual)
    return norm_back(d_act * gain, normed, inv_rms), jnp.sum(d_act * normed, axis=0)


def shards(
    inputs,
    cotangent,
    lengths,
    norm_gains,
    conv_in,
    conv_kernel,
    conv_out,
    attn_q,
    attn_k,
    attn_v,
    attn_out,
    head_gains,
    ffn_gate,
    ffn_up,
    ffn_down,
):
    micro, rows, width = inputs.shape
    section = lax.axis_index("section")
    group = lax.axis_index("fsdp")
    fsdp = lax.axis_size("fsdp")
    assert micro == lax.axis_size("section")
    head = head_gains.shape[1]
    q_width, kv_width = attn_q.shape[1], attn_k.shape[1]
    q_heads, kv_heads = q_width // head, kv_width // head
    positions = lax.axis_index("ctx") * rows + jnp.arange(rows)
    length = lax.dynamic_index_in_dim(lengths, group * micro + section, keepdims=False)
    mask = (positions < length).astype(F32)[:, None]

    def whole_rows(weight):
        share = weight.shape[0] // (micro * lax.axis_size("ctx"))
        start = (section * lax.axis_size("ctx") + lax.axis_index("ctx")) * share
        mine = lax.dynamic_slice_in_dim(weight, start, share, 0)
        return lax.all_gather(mine, ("fsdp", "section", "ctx"), axis=0, tiled=True)

    part = ffn_gate.shape[1]
    attn_full = whole_rows(jnp.concatenate([attn_q, attn_k, attn_v, attn_out], axis=1))
    query_full, key_full, value_full, proj_full = (
        attn_full[:, :q_width],
        attn_full[:, q_width : q_width + kv_width],
        attn_full[:, q_width + kv_width : q_width + 2 * kv_width],
        attn_full[:, q_width + 2 * kv_width :],
    )

    x_low = lax.dynamic_index_in_dim(inputs, section, keepdims=False)
    in_full, out_full, gate1, up1, down1, projected, convolved, z_low, mixed, rim, act_all1 = front(
        x_low, norm_gains, conv_kernel, conv_in, conv_out, ffn_gate[0], ffn_up[0], ffn_down[0], 2
    )
    x = x_low.astype(F32)
    res1 = x + mixed
    terms1, kept1 = ffn_forward(act_all1, gate1, up1, down1)
    ffn1 = reduced(terms1, 1)
    h_low = (res1 + ffn1).astype(BF16)

    h = h_low.astype(F32)
    normed2, inv2 = norm_rows(h)
    act2 = (normed2 * norm_gains[2]).astype(BF16)
    q_normed, q_inv = norm_heads(matmul(act2, query_full), head)
    k_normed, k_inv = norm_heads(matmul(act2, key_full), head)
    q_gain = jnp.tile(head_gains[0], q_heads)
    k_gain = jnp.tile(head_gains[1], kv_heads)
    query = (q_normed * q_gain).astype(BF16)
    key = (k_normed * k_gain).astype(BF16)
    value = matmul(act2, value_full).astype(BF16)
    d_sum_low = (lax.dynamic_index_in_dim(cotangent, section, keepdims=False).astype(F32) * mask).astype(BF16)
    attended, log_total, kv_all, d_sum_all, gate2, up2, down2 = attend(
        length.reshape(1),
        query,
        jnp.concatenate([key, value], axis=1),
        d_sum_low,
        ffn_gate[0],
        ffn_up[0],
        ffn_down[0],
        3,
    )
    attended_low = attended.astype(BF16)
    attn_rows = matmul(attended_low, proj_full)
    res2 = h + attn_rows
    normed3, _ = norm_rows(res2)
    act_all2 = gathered((normed3 * norm_gains[3]).astype(BF16), 0)
    terms2, kept2 = ffn_forward(act_all2, gate2, up2, down2)

    d_sum = d_sum_low.astype(F32)
    d_terms2, d_gate2, d_up2 = ffn_backward(d_sum_all, kept2, gate2, up2, down2)
    d_act3, shared_gu, shared_down = ffn_grads(
        d_terms2, d_gate2, d_up2, act_all2, kept2[3], d_sum_all, 8
    )
    d_ffn, gain3 = ffn_norm_back(d_act3, res2, norm_gains[3])
    d_res2 = d_sum + d_ffn
    d_attn = d_res2.astype(BF16)
    grad_proj = matmul_left(attended_low, d_attn)
    d_att = matmul_right(d_attn, proj_full).astype(BF16)
    delta = jnp.sum((d_att.astype(F32) * attended).reshape(rows, q_heads, head), axis=-1)
    d_query, d_kv, ffn2 = attend_back(
        length.reshape(1), query, kv_all, d_att, log_total, delta.T.reshape(q_heads, 1, rows), terms2, 4
    )
    result = (res2 + ffn2) * mask

    def square(values):
        return jnp.sum(mask * values * values, axis=0, keepdims=True)

    squares = [square(v) for v in (x, mixed, ffn1, h, attn_rows, res2, ffn2, result)]
    second_gu = lax.psum_scatter(
        shared_gu.reshape(-1, shared_gu.shape[-1]), "ctx", scatter_dimension=0, tiled=True
    )
    d_qn = rounded(d_query)
    grad_qgain = jnp.sum(jnp.sum(d_qn * q_normed, axis=0).reshape(q_heads, head), axis=0)
    d_qpre = norm_heads_back(d_qn * q_gain, q_normed, q_inv, head).astype(BF16)
    d_kn = rounded(d_kv[:, :kv_width])
    grad_kgain = jnp.sum(jnp.sum(d_kn * k_normed, axis=0).reshape(kv_heads, head), axis=0)
    d_kpre = norm_heads_back(d_kn * k_gain, k_normed, k_inv, head).astype(BF16)
    d_vpre = d_kv[:, kv_width:].astype(BF16)
    d_act2 = (
        matmul_right(d_qpre, query_full)
        + matmul_right(d_kpre, key_full)
        + matmul_right(d_vpre, value_full)
    )
    gain2 = jnp.sum(d_act2 * normed2, axis=0)
    d_h_low = (d_res2 + norm_back(d_act2 * norm_gains[2], normed2, inv2)).astype(BF16)

    d_h_all, second_gu = gathered_swapped(
        d_h_low, second_gu.reshape(fsdp, -1, second_gu.shape[-1]), 5
    )
    second_gu = lax.all_gather(second_gu, "ctx", axis=0)
    d_terms1, d_gate1, d_up1 = ffn_backward(d_h_all, kept1, gate1, up1, down1)
    attn_mixers = [
        matmul_left(act2, d_qpre).astype(BF16),
        matmul_left(act2, jnp.concatenate([d_kpre, d_vpre], axis=1)).astype(BF16),
        grad_proj.astype(BF16),
    ]
    *grads, d_x, conv_small = conv_back(
        d_terms1,
        d_gate1,
        d_up1,
        (x_low, mixed, d_h_low, norm_gains, conv_kernel, z_low, rim),
        (act_all1, kept1[3], d_h_all, in_full, out_full, projected, convolved),
        9,
    )

    half = ffn_gate.shape[1] // 2
    y_low = result.astype(BF16)
    is_first = section == 0
    other_end = swapped(jnp.where(is_first, y_low, d_x), "section")
    ends = jnp.where(is_first, jnp.stack([d_x, other_end]), jnp.stack([other_end, y_low]))[None]

    small = jnp.concatenate(
        [conv_small[:2], gain2[None], gain3[None], conv_small[2:5]]
        + [jnp.pad(grad[None], ((0, 0), (0, width - head))) for grad in (grad_qgain, grad_kgain)]
        + [jnp.zeros((7, width), F32)]
        + squares
        + [jnp.zeros((8, width), F32)]
    ).astype(BF16)
    small = small.reshape(2, 16, width)
    gu_sum, down_sum, rest_sum = summed_gradients(
        grads[:3],
        attn_mixers + grads[3:],
        small,
        second_gu.reshape(-1, fsdp, 2, second_gu.shape[2] // 2, second_gu.shape[-1]),
        shared_down,
    )
    rest_sum = rest_sum.astype(F32)

    def block(index):
        rows_at = slice(index * half, (index + 1) * half)
        return rest_sum[:, rows_at].reshape(2 * half, width)

    attn_blocks = [block(i) for i in range(3)]
    conv_blocks = [block(3 + i) for i in range(4)]
    small_sum = rest_sum[0, 7 * half : 7 * half + 9]
    cut = width // fsdp
    mine = lax.dynamic_slice_in_dim(small_sum[:7], group * cut, cut, 1)
    head_cut = head // fsdp
    heads = lax.dynamic_slice_in_dim(small_sum[7:9], group * head_cut, head_cut, 1)
    square_cut = len(squares) // fsdp
    square_sum = jnp.sum(
        lax.dynamic_slice_in_dim(rest_sum[1, 7 * half : 7 * half + 8], group * square_cut, square_cut, 0), axis=1
    )
    token_total = jnp.sum(lengths).astype(F32) * width
    rms = jnp.sqrt(square_sum / token_total)
    return (
        ends,
        mine[:3],
        mine[3],
        jnp.concatenate(conv_blocks[:3], axis=1),
        mine[4:7],
        conv_blocks[3],
        attn_blocks[0],
        attn_blocks[1][:, :kv_width],
        attn_blocks[1][:, kv_width:],
        attn_blocks[2],
        heads,
        gu_sum[0][None].astype(F32),
        gu_sum[1][None].astype(F32),
        down_sum[None].astype(F32),
        rms,
    )


def solution(mesh):
    return jax.shard_map(
        shards,
        mesh=mesh,
        in_specs=(
            P("fsdp", "ctx", None),
            P("fsdp", "ctx", None),
            P(),
            P(),
            P("fsdp", None),
            P(),
            P("fsdp", None),
            P("fsdp", None),
            P("fsdp", None),
            P("fsdp", None),
            P("fsdp", None),
            P(),
            P("section", "fsdp", None),
            P("section", "fsdp", None),
            P("section", "fsdp", None),
        ),
        out_specs=(
            P("section", "fsdp", "ctx", None),
            P(None, "fsdp"),
            P("fsdp"),
            P("fsdp", None),
            P(None, "fsdp"),
            P("fsdp", None),
            P("fsdp", None),
            P("fsdp", None),
            P("fsdp", None),
            P("fsdp", None),
            P(None, "fsdp"),
            P("section", "fsdp", None),
            P("section", "fsdp", None),
            P("section", "fsdp", None),
            P("fsdp"),
        ),
        check_vma=False,
    )
```

```python
import functools

import jax
import jax.numpy as jnp
from jax import lax
from jax.experimental import pallas as pl
from jax.experimental.pallas import tpu as pltpu
from jax.sharding import PartitionSpec as P

EPSILON = 1e-05
NEGATIVE = -1e30
MESH = pl.DeviceIdType.MESH
F32 = jnp.float32
BF16 = jnp.bfloat16


def passed_along(block, axis, distance):
    devices = range(lax.axis_size(axis))
    route = [(i - distance, i) for i in devices if i - distance in devices]
    return lax.ppermute(block, axis, route)


def swapped(block, axis):
    return lax.ppermute(block, axis, [(0, 1), (1, 0)])


def rounded(values):
    return lax.optimization_barrier(values.astype(BF16)).astype(F32)


def matmul(left_op, right_op):
    return jnp.dot(left_op, right_op, preferred_element_type=F32)


def matmul_left(left_op, right_op):
    return lax.dot_general(left_op, right_op, (((0,), (0,)), ((), ())), preferred_element_type=F32)


def matmul_right(left_op, right_op):
    return lax.dot_general(left_op, right_op, (((1,), (1,)), ((), ())), preferred_element_type=F32)


def norm_rows(values):
    inv_rms = lax.rsqrt(jnp.mean(values * values, axis=-1, keepdims=True) + EPSILON)
    return (values * inv_rms, inv_rms)


def norm_back(dnormed, normed, inv_rms):
    return inv_rms * dnormed - normed * inv_rms * jnp.mean(dnormed * normed, axis=-1, keepdims=True)


def head_sums(values, head):
    heads = values.shape[1] // head
    owner = (jnp.arange(values.shape[1])[:, None] // head == jnp.arange(heads)[None, :]).astype(F32)
    sums = jnp.dot(values, owner, precision=lax.Precision.HIGHEST, preferred_element_type=F32)
    return jnp.dot(sums, owner.T, precision=lax.Precision.HIGHEST, preferred_element_type=F32)


def norm_heads(values, head):
    inv_rms = lax.rsqrt(head_sums(values * values, head) / head + EPSILON)
    return (values * inv_rms, inv_rms)


def norm_heads_back(dnormed, normed, inv_rms, head):
    return inv_rms * dnormed - normed * inv_rms * (head_sums(dnormed * normed, head) / head)


def busy(microseconds):
    return pl.CostEstimate(flops=int(microseconds), bytes_accessed=1 << 16, transcendentals=0)


def corners():
    me = lax.axis_index("fsdp")
    beside = me + 1 - 2 * lax.rem(me, 2)
    across = lax.rem(me + 2, 4)
    return me, beside, across, lax.rem(beside + 2, 4)


def greet_sides():
    _, beside, across, _ = corners()
    barrier = pltpu.get_barrier_semaphore()
    for target in (beside, across):
        pl.semaphore_signal(barrier, inc=1, device_id={"fsdp": target}, device_id_type=MESH)
    pl.semaphore_wait(barrier, 2)


def to_side(src, dst, send_sem, recv_sem, target):
    return pltpu.make_async_remote_copy(
        src_ref=src,
        dst_ref=dst,
        send_sem=send_sem,
        recv_sem=recv_sem,
        device_id={"fsdp": target},
        device_id_type=MESH,
    )


class SideGather:
    def __init__(self, block, whole, send_sem, recv_sem, own_sem):
        me, beside, across, _ = corners()
        rows = block.shape[0]
        half = rows // 2

        def part(owner, start, size):
            return whole.at[pl.ds(pl.multiple_of(owner * rows + start, half), size)]

        self.first = to_side(block, part(me, 0, rows), send_sem.at[0], recv_sem.at[0], beside)
        self.second = to_side(block, part(me, 0, rows), send_sem.at[1], recv_sem.at[1], across)
        at = part(beside, 0, half)
        self.third = to_side(at, at, send_sem.at[2], recv_sem.at[2], across)
        at = part(across, half, half)
        self.fourth = to_side(at, at, send_sem.at[3], recv_sem.at[3], beside)
        self.own = pltpu.make_async_copy(block, part(me, 0, rows), own_sem)

    def start(self):
        self.first.start()
        self.second.start()
        self.own.start()

    def relay(self):
        self.first.wait_recv()
        self.third.start()
        self.second.wait_recv()
        self.fourth.start()

    def finish(self):
        self.own.wait()
        self.first.wait_send()
        self.second.wait_send()
        self.third.wait()
        self.fourth.wait()


def gather_kernel(block, whole, send_sem, recv_sem, own_sem):
    greet_sides()
    gather = SideGather(block, whole, send_sem, recv_sem, own_sem)
    gather.start()
    gather.relay()
    gather.finish()


def gathered(array, collective_id):
    rows, width = array.shape
    assert lax.axis_size("fsdp") == 4
    dma = pltpu.SemaphoreType.DMA
    return pl.pallas_call(
        gather_kernel,
        out_shape=jax.ShapeDtypeStruct((4 * rows, width), array.dtype),
        in_specs=[pl.BlockSpec(memory_space=pltpu.VMEM)],
        out_specs=pl.BlockSpec(memory_space=pltpu.VMEM),
        scratch_shapes=[dma((4,)), dma((4,)), dma],
        compiler_params=pltpu.CompilerParams(
            collective_id=collective_id, has_side_effects=True, vmem_limit_bytes=8 << 20
        ),
        cost_estimate=busy(25),
    )(array)


def gather_swap_kernel(block, pieces, whole, swapped_out, send_sem, recv_sem, own_sem, cross_send, cross_recv, keep_sem):
    me, beside, across, opposite = corners()
    barrier = pltpu.get_barrier_semaphore()
    for target in (beside, across, opposite):
        pl.semaphore_signal(barrier, inc=1, device_id={"fsdp": target}, device_id_type=MESH)
    pl.semaphore_wait(barrier, 3)
    gather = SideGather(block, whole, send_sem, recv_sem, own_sem)
    gather.start()
    crossing = []
    for step in range(1, 4):
        target = lax.rem(me + step, 4)
        crossing.append(
            to_side(pieces.at[target], swapped_out.at[me], cross_send.at[step], cross_recv.at[step], target)
        )
        crossing[-1].start()
    keep = pltpu.make_async_copy(pieces.at[me], swapped_out.at[me], keep_sem)
    keep.start()
    gather.relay()
    gather.finish()
    keep.wait()
    for copy in crossing:
        copy.wait()


def gathered_swapped(array, pieces, collective_id):
    rows, width = array.shape
    dma = pltpu.SemaphoreType.DMA
    vmem = pl.BlockSpec(memory_space=pltpu.VMEM)
    hbm = pl.BlockSpec(memory_space=pl.ANY)
    return pl.pallas_call(
        gather_swap_kernel,
        out_shape=(
            jax.ShapeDtypeStruct((4 * rows, width), array.dtype),
            jax.ShapeDtypeStruct(pieces.shape, pieces.dtype),
        ),
        in_specs=[vmem, hbm],
        out_specs=[vmem, hbm],
        scratch_shapes=[dma((4,)), dma((4,)), dma, dma((4,)), dma((4,)), dma],
        compiler_params=pltpu.CompilerParams(
            collective_id=collective_id, has_side_effects=True, vmem_limit_bytes=8 << 20
        ),
        cost_estimate=busy(25),
    )(array, pieces)


class SideReduce:
    def __init__(self, blocks, total, beside_got, across_got, passed, passed_got, send_sem, recv_sem):
        self.refs = blocks, total, beside_got, across_got, passed, passed_got
        me, beside, across, opposite = corners()
        self.me, self.beside, self.across = me, beside, across
        self.copies = []
        for index, (turn, target, got) in enumerate(((0, beside, beside_got), (1, across, across_got))):
            for slot, owner in ((1, opposite), (0, target)):
                self.copies.append(
                    to_side(
                        blocks.at[self.part(owner, turn)],
                        got.at[slot],
                        send_sem.at[2 * index + slot],
                        recv_sem.at[2 * index + slot],
                        target,
                    )
                )
        self.onward = [
            to_side(passed.at[turn], passed_got.at[turn], send_sem.at[4 + turn], recv_sem.at[4 + turn], owner)
            for turn, owner in ((0, across), (1, beside))
        ]

    def part(self, owner, turn):
        half = self.refs[1].shape[0] // 2
        return pl.ds(pl.multiple_of(owner * 2 * half + turn * half, half), half)

    def start(self):
        for index in (0, 2, 1, 3):
            self.copies[index].start()

    def relay(self):
        blocks, _, beside_got, across_got, passed, _ = self.refs
        for turn, owner, index, got in ((0, self.across, 0, beside_got), (1, self.beside, 2, across_got)):
            self.copies[index].wait_recv()
            passed[turn] = (blocks[self.part(owner, turn)].astype(F32) + got[1].astype(F32)).astype(BF16)
            self.onward[turn].start()

    def finish(self):
        blocks, total, beside_got, across_got, _, passed_got = self.refs
        half = total.shape[0] // 2
        for turn, index, got in ((0, 1, beside_got), (1, 3, across_got)):
            self.copies[index].wait_recv()
            total[pl.ds(turn * half, half)] = blocks[self.part(self.me, turn)].astype(F32) + got[0].astype(F32)
        for turn in range(2):
            self.onward[turn].wait_recv()
            at = pl.ds(turn * half, half)
            total[at] = total[at] + passed_got[turn].astype(F32)
        for copy in self.copies + self.onward:
            copy.wait_send()


def reduce_kernel(blocks, total, beside_got, across_got, passed, passed_got, send_sem, recv_sem):
    greet_sides()
    reduction = SideReduce(blocks, total, beside_got, across_got, passed, passed_got, send_sem, recv_sem)
    reduction.start()
    reduction.relay()
    reduction.finish()


def reduced(partial, collective_id):
    rows, width = partial.shape[0] // 4, partial.shape[1]
    assert lax.axis_size("fsdp") == 4
    dma = pltpu.SemaphoreType.DMA
    pair = pltpu.VMEM((2, rows // 2, width), BF16)
    return pl.pallas_call(
        reduce_kernel,
        out_shape=jax.ShapeDtypeStruct((rows, width), F32),
        in_specs=[pl.BlockSpec(memory_space=pltpu.VMEM)],
        out_specs=pl.BlockSpec(memory_space=pltpu.VMEM),
        scratch_shapes=[pair, pair, pair, pair, dma((6,)), dma((6,))],
        compiler_params=pltpu.CompilerParams(
            collective_id=collective_id, has_side_effects=True, vmem_limit_bytes=16 << 20
        ),
        cost_estimate=busy(25),
    )(partial.astype(BF16))


def tail_kernel(
    counts,
    gate_in,
    up_in,
    down_in,
    query_in,
    kv_in,
    proj_in,
    conv_b_in,
    conv_c_in,
    conv_x_in,
    conv_o_in,
    small_in,
    second_gu_in,
    second_down_in,
    gu_out,
    down_out,
    rest_out,
    a_own,
    a_other,
    a_sum,
    a_done,
    b_own,
    b_other,
    b_sum,
    b_done,
    c_own,
    c_other,
    c_got,
    own_sem,
    pair_send,
    pair_recv,
    c_own_sem,
    c_pair_send,
    c_pair_recv,
    c_send,
    c_recv,
    a_up_send,
    a_up_recv,
    a_back_send,
    a_back_recv,
    a_out_send,
    b_up_send,
    b_up_recv,
    b_back_send,
    b_back_recv,
    b_out_send,
    b_keep_sem,
    gu_recv,
    down_recv,
    rest_recv,
    second_send,
    second_recv,
):
    n_ctx, n_fsdp = counts
    section = lax.axis_index("section")
    place = lax.axis_index("ctx")
    group = lax.axis_index("fsdp")
    other = 1 - section
    a_chunks, a_rows, a_width = a_own.shape
    b_chunks, b_rows, b_width = b_own.shape
    half = gate_in.shape[0] // n_fsdp // 2
    subs = half // a_rows
    per_kind = n_fsdp * subs
    down_half = down_in.shape[0] // 2
    down_chunks = down_half // b_rows
    c_rows = c_own.shape[1]
    mixers = (query_in, kv_in, proj_in, conv_b_in, conv_c_in, conv_x_in, conv_o_in)
    n_mix = len(mixers)
    cut = 3 * half // b_rows
    c_parts = ((0, cut), (cut, c_rows // b_rows))
    paired = a_chunks // 2
    mix_start = 2 * down_chunks
    mix_chunks = b_chunks - mix_start
    second = paired + down_chunks // 2
    ticks = second + mix_chunks // 2
    tail = 2 * (n_ctx - 1)

    barrier = pltpu.get_barrier_semaphore()
    for step in range(1, 2 * n_fsdp):
        flat = lax.rem(section * n_fsdp + group + step, 2 * n_fsdp)
        pl.semaphore_signal(
            barrier,
            inc=1,
            device_id={"section": flat // n_fsdp, "fsdp": lax.rem(flat, n_fsdp)},
            device_id_type=MESH,
        )

    @pl.when(place > 0)
    def _():
        pl.semaphore_signal(barrier, inc=1, device_id={"ctx": place - 1}, device_id_type=MESH)

    @pl.when(place < n_ctx - 1)
    def _():
        pl.semaphore_signal(barrier, inc=1, device_id={"ctx": place + 1}, device_id_type=MESH)

    at_edge = (place == 0) | (place == n_ctx - 1)

    @pl.when(at_edge)
    def _():
        pl.semaphore_wait(barrier, 2 * n_fsdp)

    @pl.when(jnp.logical_not(at_edge))
    def _():
        pl.semaphore_wait(barrier, 2 * n_fsdp + 1)

    def half_rows(owner, which):
        return pl.ds(pl.multiple_of(owner * (2 * half) + which * half, half), half)

    a_part, b_part = a_rows // 2, b_width // 2

    def a_at(buffer, k, way):
        return buffer.at[k, pl.ds(way * a_part, a_part)]

    def b_at(buffer, k, way):
        return buffer.at[k, :, pl.ds(way * b_part, b_part)]

    def opening(k, way):
        copies = []
        kind, rest = divmod(k, per_kind)
        owner, sub = divmod(rest, subs)
        source = (gate_in, up_in)[kind]
        spots = []
        for which in (section, other):
            start = owner * (2 * half) + which * half + sub * a_rows + way * a_part
            spots.append(source.at[pl.ds(pl.multiple_of(start, a_part), a_part)])
        spot = 2 * k + way
        copies.append((spots, a_at(a_own, k, way), a_at(a_other, k, way), spot))
        if k < down_chunks:
            spots = [
                down_in.at[
                    pl.ds(pl.multiple_of(which * down_half + k * b_rows, b_rows), b_rows),
                    pl.ds(way * b_part, b_part),
                ]
                for which in (section, other)
            ]
            copies.append((spots, b_at(b_own, k, way), b_at(b_other, k, way), 2 * a_chunks + spot))
        for (mine, theirs), own_dst, other_dst, spot in copies:
            pltpu.make_async_copy(mine, own_dst, own_sem.at[spot]).start()
            pltpu.make_async_remote_copy(
                src_ref=theirs,
                dst_ref=other_dst,
                send_sem=pair_send.at[spot],
                recv_sem=pair_recv.at[spot],
                device_id={"section": other},
                device_id_type=MESH,
            ).start()

    for k in range(a_chunks):
        for way in range(2):
            opening(k, way)
    for k in range(down_chunks):
        for way in range(2):
            pltpu.make_async_copy(
                second_down_in.at[pl.ds(k * b_rows, b_rows), pl.ds(way * b_part, b_part)],
                b_at(b_own, down_chunks + k, way),
                own_sem.at[2 * (a_chunks + down_chunks + k) + way],
            ).start()
    c_local, c_pair = ([], []), ([], [])
    for kind, source in enumerate(mixers):
        part = 0 if kind < 3 else 1
        for owner in range(n_fsdp):
            index = owner * (n_mix + 1) + kind
            place_at = pl.ds(kind * half, half)
            c_local[part].append(
                pltpu.make_async_copy(
                    source.at[half_rows(owner, section)], c_own.at[owner, place_at], c_own_sem.at[index]
                )
            )
            c_pair[part].append(
                pltpu.make_async_remote_copy(
                    src_ref=source.at[half_rows(owner, other)],
                    dst_ref=c_other.at[owner, place_at],
                    send_sem=c_pair_send.at[index],
                    recv_sem=c_pair_recv.at[index],
                    device_id={"section": other},
                    device_id_type=MESH,
                )
            )
    for owner in range(n_fsdp):
        small_at = pl.ds(n_mix * half, c_rows - n_mix * half)
        index = owner * (n_mix + 1) + n_mix
        c_local[1].append(
            pltpu.make_async_copy(small_in.at[section], c_own.at[owner, small_at], c_own_sem.at[index])
        )
        c_pair[1].append(
            pltpu.make_async_remote_copy(
                src_ref=small_in.at[other],
                dst_ref=c_other.at[owner, small_at],
                send_sem=c_pair_send.at[index],
                recv_sem=c_pair_recv.at[index],
                device_id={"section": other},
                device_id_type=MESH,
            )
        )
    for part in range(2):
        for copy in c_pair[part]:
            copy.start()
        for copy in c_local[part]:
            copy.start()
    b_own[b_chunks - 1] = jnp.zeros((b_rows, b_width), BF16)
    _, beside, across, opposite = corners()

    def span(first, last):
        return pl.ds(first * b_rows, (last - first) * b_rows)

    def mixer_spans(part):
        first, last = c_parts[part]
        middle = (first + last) // 2
        return (first, middle, beside, across), (middle, last, across, beside)

    def mixer_copies(part):
        opening, onward = [], []
        for turn, (first, last, near, far) in enumerate(mixer_spans(part)):
            at = span(first, last)
            for slot, owner in ((0, opposite), (1, near)):
                opening.append(
                    to_side(
                        c_own.at[owner, at],
                        c_got.at[slot, at],
                        c_send.at[part, 3 * turn + slot],
                        c_recv.at[part, 3 * turn + slot],
                        near,
                    )
                )
            onward.append(
                to_side(
                    c_own.at[far, at],
                    c_got.at[2, at],
                    c_send.at[part, 3 * turn + 2],
                    c_recv.at[part, 3 * turn + 2],
                    far,
                )
            )
        return opening, onward

    def mixer_sum(part, owner):
        kinds = range(3) if part == 0 else range(3, n_mix + 1)
        first, last = c_parts[part]
        for kind in kinds:
            size = half if kind < n_mix else c_rows - n_mix * half
            at = c_own.at[owner, pl.ds(kind * half, size)]
            index = owner * (n_mix + 1) + kind
            pltpu.make_async_copy(at, at, c_own_sem.at[index]).wait()
            pltpu.make_async_copy(at, at, c_pair_recv.at[index]).wait()

        def add(index, carry):
            at = pl.ds(pl.multiple_of(index * b_rows, b_rows), b_rows)
            c_own[owner, at] = (c_own[owner, at].astype(F32) + c_other[owner, at].astype(F32)).astype(BF16)
            return carry

        lax.fori_loop(first, last, add, 0)

    def mixer_out(part):
        opening, _ = mixer_copies(part)
        for index in (0, 2, 1, 3):
            opening[index].start()

    def mixer_on(part):
        opening, onward = mixer_copies(part)
        for turn, (first, last, near, far) in enumerate(mixer_spans(part)):
            opening[2 * turn].wait_recv()

            def add(index, carry, far=far):
                at = pl.ds(pl.multiple_of(index * b_rows, b_rows), b_rows)
                c_own[far, at] = (c_own[far, at].astype(F32) + c_got[0, at].astype(F32)).astype(BF16)
                return carry

            lax.fori_loop(first, last, add, 0)
            onward[turn].start()

    def mixer_in(part):
        opening, onward = mixer_copies(part)
        for turn in range(2):
            opening[2 * turn + 1].wait_recv()
            onward[turn].wait_recv()
        first, last = c_parts[part]

        def add(index, carry):
            at = pl.ds(pl.multiple_of(index * b_rows, b_rows), b_rows)
            total = c_own[group, at].astype(F32) + c_got[1, at].astype(F32) + c_got[2, at].astype(F32)
            b_own[mix_start + index] = total.astype(BF16)
            return carry

        lax.fori_loop(first, last, add, 0)

    strip = half // n_ctx

    def second_copies(remote):
        for index in range(n_ctx * n_fsdp * 2):
            source, kind = index // 2, index % 2
            turn, owner = source // n_fsdp, source % n_fsdp
            src = second_gu_in.at[turn, owner, kind]
            dst = gu_out.at[
                kind,
                pl.ds(pl.multiple_of(section * half + turn * strip, strip), strip),
                pl.ds(owner * a_width, a_width),
            ]
            if remote:
                pltpu.make_async_remote_copy(
                    src_ref=src,
                    dst_ref=dst,
                    send_sem=second_send.at[0],
                    recv_sem=second_recv,
                    device_id={"section": 1},
                    device_id_type=MESH,
                ).start()
            else:
                pltpu.make_async_copy(src, dst, second_send.at[0]).start()

    def second_start():
        @pl.when(section == 1)
        def _():
            second_copies(False)

        @pl.when(section == 0)
        def _():
            second_copies(True)

    def a_target(k, way):
        kind = k // per_kind
        rest = lax.rem(k, per_kind)
        owner = rest // subs
        sub = lax.rem(rest, subs)
        start = section * half + sub * a_rows + way * a_part
        spot = gu_out.at[
            kind,
            pl.ds(pl.multiple_of(start, a_part), a_part),
            pl.ds(pl.multiple_of(group * a_width, 128), a_width),
        ]
        return kind, owner, spot

    def a_hand_out(k, way):
        kind, owner, spot = a_target(k, way)
        is_mine = (section == 0) & (group == owner)
        slot = 2 * k + way
        a_ref = a_at(a_done, k, way)

        @pl.when(is_mine)
        def _():
            pltpu.make_async_copy(a_ref, spot, a_out_send.at[slot]).start()

        @pl.when(jnp.logical_not(is_mine))
        def _():
            pltpu.make_async_remote_copy(
                src_ref=a_ref,
                dst_ref=spot,
                send_sem=a_out_send.at[slot],
                recv_sem=gu_recv.at[kind, section * n_fsdp + group],
                device_id={"section": 0, "fsdp": owner},
                device_id_type=MESH,
            ).start()

    def down_hand_out(k, way, keeper):
        slot = 2 * k + way
        b_ref = b_at(b_done, k, way)
        index = k - keeper * down_chunks
        at = down_out.at[
            pl.ds(pl.multiple_of(section * down_half + index * b_rows, b_rows), b_rows),
            pl.ds(way * b_part, b_part),
        ]

        @pl.when(section == keeper)
        def _():
            pltpu.make_async_copy(b_ref, at, b_out_send.at[slot]).start()

        @pl.when(section != keeper)
        def _():
            pltpu.make_async_remote_copy(
                src_ref=b_ref,
                dst_ref=at,
                send_sem=b_out_send.at[slot],
                recv_sem=down_recv,
                device_id={"section": keeper},
                device_id_type=MESH,
            ).start()

    def mix_hand_out(k, way):
        slot = 2 * k + way
        b_ref = b_at(b_done, k, way)
        at = rest_out.at[
            section,
            pl.ds(pl.multiple_of((k - mix_start) * b_rows, b_rows), b_rows),
            pl.ds(way * b_part, b_part),
        ]
        pltpu.make_async_copy(b_ref, at, b_keep_sem.at[slot]).start()
        pltpu.make_async_remote_copy(
            src_ref=b_ref,
            dst_ref=at,
            send_sem=b_out_send.at[slot],
            recv_sem=rest_recv,
            device_id={"section": other},
            device_id_type=MESH,
        ).start()

    def chain_copy(at, sems, slot, target):
        return pltpu.make_async_remote_copy(
            src_ref=at,
            dst_ref=at,
            send_sem=sems[0].at[slot],
            recv_sem=sems[1].at[slot],
            device_id={"ctx": target},
            device_id_type=MESH,
        )

    class Gates:
        hand_out = staticmethod(a_hand_out)

        @staticmethod
        def view(buffer, k, way):
            return a_at(buffer, k, way)

        own, sums, done = a_own, a_sum, a_done
        up, back = (a_up_send, a_up_recv), (a_back_send, a_back_recv)

        @staticmethod
        def term(k, way):
            slot = 2 * k + way
            at = a_at(a_own, k, way)
            pltpu.make_async_copy(at, at, own_sem.at[slot]).wait()
            pltpu.make_async_copy(at, at, pair_recv.at[slot]).wait()
            return at[...].astype(F32) + a_at(a_other, k, way)[...].astype(F32)

    class Downs:
        @staticmethod
        def hand_out(k, way):
            down_hand_out(k, way, 0)

        @staticmethod
        def view(buffer, k, way):
            return b_at(buffer, k, way)

        own, sums, done = b_own, b_sum, b_done
        up, back = (b_up_send, b_up_recv), (b_back_send, b_back_recv)

        @staticmethod
        def term(k, way):
            slot = 2 * a_chunks + 2 * k + way
            at = b_at(b_own, k, way)
            pltpu.make_async_copy(at, at, own_sem.at[slot]).wait()
            pltpu.make_async_copy(at, at, pair_recv.at[slot]).wait()
            return at[...].astype(F32) + b_at(b_other, k, way)[...].astype(F32)

    class Seconds(Downs):
        @staticmethod
        def hand_out(k, way):
            down_hand_out(k, way, 1)

        @staticmethod
        def term(k, way):
            at = b_at(b_own, k, way)
            pltpu.make_async_copy(at, at, own_sem.at[2 * a_chunks + 2 * k + way]).wait()
            return at[...].astype(F32)

    class Mixed(Downs):
        hand_out = staticmethod(mix_hand_out)

        @staticmethod
        def term(k, way):
            return b_at(b_own, k, way)[...].astype(F32)

    def upward(item, k, way, rank, ahead, behind):
        slot = 2 * k + way
        term = item.term(k, way)
        sums = item.view(item.sums, k, way)

        @pl.when(rank == 0)
        def _():
            sums[...] = term.astype(BF16)

        @pl.when(rank > 0)
        def _():
            chain_copy(sums, item.up, slot, behind).wait_recv()

        @pl.when((rank > 0) & (rank < n_ctx - 1))
        def _():
            sums[...] = (term + sums[...].astype(F32)).astype(BF16)

        @pl.when(rank < n_ctx - 1)
        def _():
            chain_copy(sums, item.up, slot, ahead).start()

        @pl.when(rank == n_ctx - 1)
        def _():
            done = item.view(item.done, k, way)
            done[...] = (term + sums[...].astype(F32)).astype(BF16)
            chain_copy(done, item.back, slot, behind).start()
            item.hand_out(k, way)

    def backward(item, k, way, rank, ahead, behind):
        slot = 2 * k + way
        done = item.view(item.done, k, way)
        chain_copy(done, item.back, slot, ahead).wait_recv()

        @pl.when(rank > 0)
        def _():
            chain_copy(done, item.back, slot, behind).start()

        item.hand_out(k, way)

    def on_step(action, step, active, *where):
        early = active & (step < paired)

        @pl.when(early)
        def _():
            at = jnp.clip(step, 0, paired - 1)
            for index in range(2):
                action(Gates, 2 * at + index, *where)

            @pl.when(lax.rem(at, 4) < 3)
            def _():
                action(Downs, 3 * (at // 4) + lax.rem(at, 4), *where)

        @pl.when(active & (step >= paired) & (step < second))
        def _():
            at = jnp.clip(step - paired, 0, down_chunks // 2 - 1)
            for index in range(2):
                action(Seconds, down_chunks + 2 * at + index, *where)

        @pl.when(active & (step >= second))
        def _():
            at = jnp.clip(step - second, 0, mix_chunks // 2 - 1)
            for index in range(2):
                action(Mixed, mix_start + 2 * at + index, *where)

    lanes = []
    for way in range(2):
        rank = place if way == 0 else n_ctx - 1 - place
        ahead = place + 1 if way == 0 else place - 1
        behind = place - 1 if way == 0 else place + 1
        lanes.append((way, rank, ahead, behind))

    def tick_step(tick, carry):
        for part, start in ((0, 1), (1, 5)):
            for owner in range(n_fsdp):

                @pl.when(tick == start + owner)
                def _(part=part, owner=owner):
                    mixer_sum(part, owner)

        events = (
            (4, mixer_out, 0),
            (8, mixer_out, 1),
            (10, mixer_on, 0),
            (15, mixer_on, 1),
            (second - 1, mixer_in, 0),
            (second + 3, mixer_in, 1),
        )
        for moment, action, part in events:

            @pl.when(tick == moment)
            def _(action=action, part=part):
                action(part)

        for way, rank, ahead, behind in lanes:
            step = tick - 2 * rank
            on_step(upward, step, (step >= 0) & (step < ticks), way, rank, ahead, behind)
            late = tick - 2 * (tail - rank)
            on_step(
                backward,
                late,
                (late >= 0) & (late < ticks) & (rank < n_ctx - 1),
                way,
                rank,
                ahead,
                behind,
            )

        return carry

    second_start()
    lax.fori_loop(0, ticks + 2 * tail, tick_step, 0)

    for part in range(2):
        for copy in c_pair[part]:
            copy.wait_send()
        opening, onward = mixer_copies(part)
        for copy in opening + onward:
            copy.wait_send()

    def settle_item(item, k, out_send):
        for way, rank, ahead, behind in lanes:
            slot = 2 * k + way

            @pl.when(rank < n_ctx - 1)
            def _(slot=slot, way=way, ahead=ahead):
                chain_copy(item.view(item.sums, k, way), item.up, slot, ahead).wait_send()

            @pl.when(rank > 0)
            def _(slot=slot, way=way, behind=behind):
                chain_copy(item.view(item.done, k, way), item.back, slot, behind).wait_send()

            ref = item.view(item.own, k, way)
            pltpu.make_async_copy(ref, ref, out_send.at[slot]).wait()

    def settle_gates(k, carry):
        settle_item(Gates, k, a_out_send)
        for way in range(2):
            ref = a_at(a_own, k, way)
            pltpu.make_async_copy(ref, ref, pair_send.at[2 * k + way]).wait()
        return carry

    lax.fori_loop(0, a_chunks, settle_gates, 0)

    def settle_rest(k, carry):
        settle_item(Mixed, k, b_out_send)
        for way in range(2):
            ref = b_at(b_own, k, way)

            @pl.when(k < down_chunks)
            def _(ref=ref, way=way):
                pltpu.make_async_copy(ref, ref, pair_send.at[2 * a_chunks + 2 * k + way]).wait()

            @pl.when(k >= mix_start)
            def _(ref=ref, way=way):
                pltpu.make_async_copy(ref, ref, b_keep_sem.at[2 * k + way]).wait()

        return carry

    lax.fori_loop(0, b_chunks, settle_rest, 0)
    pltpu.make_async_copy(second_gu_in, second_gu_in, second_send.at[0]).wait()

    @pl.when(section == 0)
    def _():
        for kind in range(2):
            for source in range(2 * n_fsdp):

                @pl.when(group != source)
                def _(kind=kind, source=source):
                    region = gu_out.at[
                        kind,
                        pl.ds((source // n_fsdp) * half, half),
                        pl.ds((source % n_fsdp) * a_width, a_width),
                    ]
                    pltpu.make_async_copy(region, region, gu_recv.at[kind, source]).wait()

    @pl.when(section == 1)
    def _():
        pltpu.make_async_copy(second_gu_in, second_gu_in, second_recv).wait()

    region = down_out.at[pl.ds(pl.multiple_of(other * down_half, b_rows), down_half)]
    pltpu.make_async_copy(region, region, down_recv).wait()
    region = rest_out.at[other]
    pltpu.make_async_copy(region, region, rest_recv).wait()


def summed_gradients(first, mixers, small, second_gu, second_down):
    n_ctx, n_fsdp = lax.axis_size("ctx"), lax.axis_size("fsdp")
    gate, up, down = first
    half = gate.shape[0] // n_fsdp // 2
    a_rows, b_rows = half // 4, half * 3 // 8
    a_chunks = 2 * n_fsdp * 4
    a_width, b_width = gate.shape[1], down.shape[1]
    c_rows = len(mixers) * half + small.shape[1]
    down_chunks = down.shape[0] // 2 // b_rows
    b_chunks = 2 * down_chunks + c_rows // b_rows + 1
    assert c_rows % b_rows == 0 and b_chunks % 2 == 0 and down_chunks % 2 == 0
    assert down_chunks * 8 == a_chunks * 3
    rest = b_chunks - 2 * down_chunks
    dma = pltpu.SemaphoreType.DMA
    loads = 2 * (a_chunks + 2 * down_chunks)
    pieces = n_fsdp * (len(mixers) + 1)
    return pl.pallas_call(
        functools.partial(tail_kernel, (n_ctx, n_fsdp)),
        out_shape=(
            jax.ShapeDtypeStruct((2, 2 * half, n_fsdp * a_width), BF16),
            jax.ShapeDtypeStruct(down.shape, BF16),
            jax.ShapeDtypeStruct((2, rest * b_rows, b_width), BF16),
        ),
        in_specs=[pl.BlockSpec(memory_space=pl.ANY)] * (6 + len(mixers)),
        out_specs=[pl.BlockSpec(memory_space=pl.ANY)] * 3,
        scratch_shapes=[
            pltpu.VMEM((a_chunks, a_rows, a_width), BF16),
            pltpu.VMEM((a_chunks, a_rows, a_width), BF16),
            pltpu.VMEM((a_chunks, a_rows, a_width), BF16),
            pltpu.VMEM((a_chunks, a_rows, a_width), BF16),
            pltpu.VMEM((b_chunks, b_rows, b_width), BF16),
            pltpu.VMEM((down_chunks, b_rows, b_width), BF16),
            pltpu.VMEM((b_chunks, b_rows, b_width), BF16),
            pltpu.VMEM((b_chunks, b_rows, b_width), BF16),
            pltpu.VMEM((n_fsdp, c_rows, b_width), BF16),
            pltpu.VMEM((n_fsdp, c_rows, b_width), BF16),
            pltpu.VMEM((n_fsdp - 1, c_rows, b_width), BF16),
            dma((loads,)),
            dma((loads,)),
            dma((loads,)),
            dma((pieces,)),
            dma((pieces,)),
            dma((pieces,)),
            dma((2, 6)),
            dma((2, 6)),
            dma((2 * a_chunks,)),
            dma((2 * a_chunks,)),
            dma((2 * a_chunks,)),
            dma((2 * a_chunks,)),
            dma((2 * a_chunks,)),
            dma((2 * b_chunks,)),
            dma((2 * b_chunks,)),
            dma((2 * b_chunks,)),
            dma((2 * b_chunks,)),
            dma((2 * b_chunks,)),
            dma((2 * b_chunks,)),
            dma((2, 2 * n_fsdp)),
            dma,
            dma,
            dma((2,)),
            dma,
        ],
        compiler_params=pltpu.CompilerParams(
            collective_id=6, has_side_effects=True, vmem_limit_bytes=56 << 20
        ),
        cost_estimate=busy(160),
    )(gate, up, down, *mixers, small, second_gu, second_down)


class Columns:
    def __init__(self, holder, sources, targets, send_sem, recv_sem, pair_send, pair_recv, own_sem):
        self.count = 4
        self.holder = holder
        self.section = lax.axis_index("section")
        self.me = lax.axis_index("fsdp")
        self.sources, self.targets = sources, targets
        self.sems = send_sem, recv_sem, pair_send, pair_recv, own_sem
        self.rows = sources[0].shape[0]
        self.wide = targets[0].shape[1]
        self.steps = [(step, kind) for step in range(1, self.count) for kind in range(2)]

    def at_rows(self, out, owner):
        return out.at[pl.ds(pl.multiple_of(owner * self.rows, self.rows), self.rows)]

    def at_columns(self, source, owner):
        return source.at[:, pl.ds(pl.multiple_of(owner * self.wide, 128), self.wide)]

    def crossing(self, step, kind):
        target = lax.rem(self.me + step, self.count)
        return to_side(
            self.at_columns(self.sources[kind], target),
            self.at_rows(self.targets[kind], self.me),
            self.sems[0].at[kind, step],
            self.sems[1].at[kind, step],
            target,
        )

    def handed(self, step, kind):
        if kind == 2:
            src, dst = self.sources[2], self.targets[2]
        else:
            origin = lax.rem(self.me + self.count - step, self.count)
            dst = self.at_rows(self.targets[kind], origin)
            src = self.at_columns(self.sources[kind], self.me) if step == 0 else dst
        return pltpu.make_async_remote_copy(
            src_ref=src,
            dst_ref=dst,
            send_sem=self.sems[2].at[kind, step],
            recv_sem=self.sems[3].at[kind, step],
            device_id={"section": 1 - self.section},
            device_id_type=MESH,
        )

    def kept(self, kind):
        if kind == 2:
            return pltpu.make_async_copy(self.sources[2], self.targets[2], self.sems[4].at[2])
        return pltpu.make_async_copy(
            self.at_columns(self.sources[kind], self.me),
            self.at_rows(self.targets[kind], self.me),
            self.sems[4].at[kind],
        )

    def start(self):
        @pl.when(self.section == self.holder)
        def _():
            for step, kind in self.steps:
                self.crossing(step, kind).start()
            for kind in range(3):
                self.handed(0, kind).start()
            for kind in range(3):
                self.kept(kind).start()

    def relay(self):
        @pl.when(self.section == self.holder)
        def _():
            for step, kind in self.steps:
                self.crossing(step, kind).wait_recv()
                self.handed(step, kind).start()

    def arrive(self):
        every = [(0, kind) for kind in range(3)] + self.steps

        @pl.when(self.section == self.holder)
        def _():
            for kind in range(3):
                self.kept(kind).wait()

        @pl.when(self.section != self.holder)
        def _():
            for step, kind in every:
                self.handed(step, kind).wait_recv()

    def finish(self):
        every = [(0, kind) for kind in range(3)] + self.steps

        @pl.when(self.section == self.holder)
        def _():
            for step, kind in self.steps:
                self.crossing(step, kind).wait_send()
            for step, kind in every:
                self.handed(step, kind).wait_send()


class SharedColumns(Columns):
    def __init__(self, *args):
        *args, plane_send, plane_recv = args
        super().__init__(*args)
        self.plane = plane_send, plane_recv
        place = lax.axis_index("ctx")
        self.odd = lax.rem(place, 2)
        self.partner = place + 1 - 2 * self.odd

    def passed_on(self, step, kind):
        at = self.at_rows(self.targets[kind], lax.rem(self.me + self.count - step, self.count))
        return pltpu.make_async_remote_copy(
            src_ref=at,
            dst_ref=at,
            send_sem=self.plane[0].at[kind, step],
            recv_sem=self.plane[1].at[kind, step],
            device_id={"ctx": self.partner},
            device_id_type=MESH,
        )

    def by_kind(self, action):
        for kind in range(2):

            @pl.when((self.section == self.holder) & (self.odd == kind))
            def _(kind=kind):
                for step in range(1, self.count):
                    action(step, kind)

    def start(self):
        self.by_kind(lambda step, kind: self.crossing(step, kind).start())

        @pl.when(self.section == self.holder)
        def _():
            for kind in range(3):
                self.handed(0, kind).start()
            for kind in range(3):
                self.kept(kind).start()

    def relay(self):
        def moved(step, kind):
            self.crossing(step, kind).wait_recv()
            self.passed_on(step, kind).start()
            self.handed(step, kind).start()

        self.by_kind(moved)

    def relay_passed(self):
        def passed(step, kind):
            self.passed_on(step, 1 - kind).wait_recv()
            self.handed(step, 1 - kind).start()

        self.by_kind(passed)

    def finish(self):
        def sent(step, kind):
            self.crossing(step, kind).wait_send()
            self.passed_on(step, kind).wait_send()

        self.by_kind(sent)
        every = [(0, kind) for kind in range(3)] + self.steps

        @pl.when(self.section == self.holder)
        def _():
            for step, kind in every:
                self.handed(step, kind).wait_send()


class Chain:
    def __init__(self, count):
        self.count = count
        self.place = lax.axis_index("ctx")
        self.has_next = self.place < count - 1
        self.has_last = self.place > 0


def greet_mixed(chain, targets):
    barrier = pltpu.get_barrier_semaphore()
    for target in targets:
        pl.semaphore_signal(barrier, inc=1, device_id=target, device_id_type=MESH)

    @pl.when(chain.has_last)
    def _():
        pl.semaphore_signal(barrier, inc=1, device_id={"ctx": chain.place - 1}, device_id_type=MESH)

    @pl.when(chain.has_next)
    def _():
        pl.semaphore_signal(barrier, inc=1, device_id={"ctx": chain.place + 1}, device_id_type=MESH)

    inner = chain.has_last & chain.has_next

    @pl.when(inner)
    def _():
        pl.semaphore_wait(barrier, len(targets) + 2)

    @pl.when(jnp.logical_not(inner))
    def _():
        pl.semaphore_wait(barrier, len(targets) + 1)


def along(src, dst, send_sem, recv_sem, place):
    return pltpu.make_async_remote_copy(
        src_ref=src,
        dst_ref=dst,
        send_sem=send_sem,
        recv_sem=recv_sem,
        device_id={"ctx": place},
        device_id_type=MESH,
    )


def spread_heads(source, spread):
    rows = source.shape[0]
    low = lax.broadcasted_iota(jnp.int32, (rows, 128), 1) < 64
    for pair in range(source.shape[1] // 256):
        first = source[:, pair * 256 : pair * 256 + 128].astype(F32)
        second = source[:, pair * 256 + 128 : pair * 256 + 256].astype(F32)
        spread[4 * pair] = jnp.where(low, first, 0.0).astype(BF16)
        spread[4 * pair + 1] = jnp.where(low, pltpu.roll(first, 64, 1), 0.0).astype(BF16)
        spread[4 * pair + 2] = jnp.where(low, 0.0, pltpu.roll(second, 64, 1)).astype(BF16)
        spread[4 * pair + 3] = jnp.where(low, 0.0, second).astype(BF16)


def join_heads(spread, target):
    rows = target.shape[0]
    low = lax.broadcasted_iota(jnp.int32, (rows, 128), 1) < 64
    for pair in range(target.shape[1] // 256):
        parts = [spread(4 * pair + i).T for i in range(4)]
        target[:, pair * 256 : pair * 256 + 128] = jnp.where(low, parts[0], pltpu.roll(parts[1], 64, 1))
        target[:, pair * 256 + 128 : pair * 256 + 256] = jnp.where(low, pltpu.roll(parts[2], 64, 1), parts[3])


def mask_block(bias, length, place, block):
    rows = bias.shape[0]
    key_at = block * rows + lax.broadcasted_iota(jnp.int32, bias.shape, 0)
    query_at = place * rows + lax.broadcasted_iota(jnp.int32, bias.shape, 1)
    bias[...] = jnp.where((key_at <= query_at) & (key_at < length), 0.0, NEGATIVE)


def dot_right(left, right):
    return lax.dot_general(left, right, (((1,), (1,)), ((), ())), preferred_element_type=F32)


def dot_plain(left, right):
    return jnp.dot(left, right, preferred_element_type=F32)


def attend_kernel(
    n_ctx,
    length_ref,
    query,
    kv,
    d_block,
    gate_in,
    up_in,
    down_in,
    attended,
    log_total,
    kv_all,
    d_all,
    gate_out,
    up_out,
    down_out,
    w_gate,
    w_up,
    w_down,
    keep_sem,
    spread,
    bias,
    peak,
    total,
    out_t,
    kv_send,
    kv_recv,
    d_send,
    d_recv,
    d_own,
    send_sem,
    recv_sem,
    pair_send,
    pair_recv,
    own_sem,
):
    chain = Chain(n_ctx)
    place = chain.place
    section = lax.axis_index("section")
    me, beside, across, opposite = corners()
    greet_mixed(
        chain,
        [{"fsdp": beside}, {"fsdp": across}, {"fsdp": opposite}, {"section": 1 - section}],
    )
    rows = query.shape[0]
    half_width = kv.shape[1] // 2

    def block_rows(block):
        return pl.ds(pl.multiple_of(block * rows, rows), rows)

    def upward(step, src):
        return along(
            src,
            kv_all.at[block_rows(place - step)],
            kv_send.at[step],
            kv_recv.at[step + 1],
            place + 1,
        )

    def arriving(step):
        at = kv_all.at[block_rows(place - step)]
        return along(at, at, kv_send.at[step], kv_recv.at[step], place)

    @pl.when(chain.has_next)
    def _():
        upward(0, kv).start()

    gather = SideGather(d_block, d_all, d_send, d_recv, d_own)
    gather.start()
    columns = Columns(
        1, (gate_in, up_in, down_in), (w_gate, w_up, w_down), send_sem, recv_sem, pair_send, pair_recv, own_sem
    )
    columns.start()
    kv_all[block_rows(place)] = kv[...]
    spread_heads(query, spread)
    peak[...] = jnp.full(peak.shape, NEGATIVE, F32)
    total[...] = jnp.zeros(total.shape, F32)
    out_t[...] = jnp.zeros(out_t.shape, F32)
    length = length_ref[0]
    scale = 64 ** (-0.5)

    def attend_block(block):
        mask_block(bias, length, place, block)
        for pair in range(half_width // 128):
            key = kv_all[block_rows(block), pair * 128 : pair * 128 + 128]
            value_t = kv_all[block_rows(block), half_width + pair * 128 : half_width + pair * 128 + 128].T
            for index in range(4):
                head = 4 * pair + index
                scores = dot_right(key, spread[head]) * scale + bias[...]
                before = peak[head]
                now = jnp.maximum(before, jnp.max(scores, axis=0, keepdims=True))
                weights = jnp.exp(scores - now)
                fade = jnp.exp(before - now)
                peak[head] = now
                total[head] = total[head] * fade + jnp.sum(weights, axis=0, keepdims=True)
                out_t[head] = out_t[head] * fade + dot_plain(value_t, weights.astype(BF16))

    attend_block(place)
    gather.relay()

    def step_on(step, carry):
        @pl.when(step <= place)
        def _():
            arriving(step).wait_recv()

            @pl.when(chain.has_next)
            def _():
                upward(step, kv_all.at[block_rows(place - step)]).start()

            attend_block(place - step)

        return carry

    lax.fori_loop(1, n_ctx, step_on, 0)
    join_heads(lambda head: out_t[head] / total[head], attended)
    for head in range(spread.shape[0]):
        log_total[head] = peak[head] + jnp.log(total[head])
    columns.relay()
    columns.arrive()
    keeping = [
        pltpu.make_async_copy(src, dst, keep_sem.at[index])
        for index, (src, dst) in enumerate(((w_gate, gate_out), (w_up, up_out), (w_down, down_out)))
    ]
    for copy in keeping:
        copy.start()
    gather.finish()
    columns.finish()
    for copy in keeping:
        copy.wait()

    def settle(step, carry):
        @pl.when((step <= place) & chain.has_next)
        def _():
            upward(step, kv_all.at[block_rows(place - step)]).wait_send()

        return carry

    lax.fori_loop(0, n_ctx, settle, 0)


def attend(length, query, kv, d_block, gate, up, down, collective_id):
    n_ctx, count = lax.axis_size("ctx"), lax.axis_size("fsdp")
    rows, width = query.shape
    heads = width // 64
    dma = pltpu.SemaphoreType.DMA
    vmem = pl.BlockSpec(memory_space=pltpu.VMEM)
    hbm = pl.BlockSpec(memory_space=pl.ANY)
    column = jax.ShapeDtypeStruct((count * gate.shape[0], gate.shape[1] // count), gate.dtype)
    return pl.pallas_call(
        functools.partial(attend_kernel, n_ctx),
        out_shape=(
            jax.ShapeDtypeStruct((rows, width), F32),
            jax.ShapeDtypeStruct((heads, 1, rows), F32),
            jax.ShapeDtypeStruct((n_ctx * rows, kv.shape[1]), BF16),
            jax.ShapeDtypeStruct((count * rows, d_block.shape[1]), BF16),
            column,
            column,
            jax.ShapeDtypeStruct(down.shape, down.dtype),
        ),
        in_specs=[pl.BlockSpec(memory_space=pltpu.SMEM), vmem, vmem, vmem, hbm, hbm, hbm],
        out_specs=[vmem, vmem, vmem, vmem, hbm, hbm, hbm],
        scratch_shapes=[
            pltpu.VMEM(column.shape, BF16),
            pltpu.VMEM(column.shape, BF16),
            pltpu.VMEM(down.shape, BF16),
            dma((3,)),
            pltpu.VMEM((heads, rows, 128), BF16),
            pltpu.VMEM((rows, rows), F32),
            pltpu.VMEM((heads, 1, rows), F32),
            pltpu.VMEM((heads, 1, rows), F32),
            pltpu.VMEM((heads, 128, rows), F32),
            dma((n_ctx + 1,)),
            dma((n_ctx + 1,)),
            dma((4,)),
            dma((4,)),
            dma,
            dma((2, count)),
            dma((2, count)),
            dma((3, count)),
            dma((3, count)),
            dma((3,)),
        ],
        compiler_params=pltpu.CompilerParams(
            collective_id=collective_id, has_side_effects=True, vmem_limit_bytes=58 << 20
        ),
        cost_estimate=busy(50),
    )(length, query, kv, d_block, gate, up, down)


def attend_back_kernel(
    n_ctx,
    length_ref,
    query,
    kv_all,
    d_out,
    log_total,
    delta,
    blocks,
    d_query,
    d_kv,
    reduced_out,
    spread,
    d_spread,
    bias,
    d_query_t,
    term,
    leaving,
    coming,
    kv_send,
    kv_recv,
    beside_got,
    across_got,
    passed,
    passed_got,
    send_sem,
    recv_sem,
):
    chain = Chain(n_ctx)
    place = chain.place
    _, beside, across, _ = corners()
    greet_mixed(chain, [{"fsdp": beside}, {"fsdp": across}])
    rows = query.shape[0]
    half_width = kv_all.shape[1] // 2
    reduction = SideReduce(blocks, reduced_out, beside_got, across_got, passed, passed_got, send_sem, recv_sem)
    reduction.start()
    spread_heads(query, spread)
    spread_heads(d_out, d_spread)
    d_query_t[...] = jnp.zeros(d_query_t.shape, F32)
    length = length_ref[0]
    scale = 64 ** (-0.5)

    def downward(block):
        return along(leaving.at[block], coming.at[block], kv_send.at[block], kv_recv.at[block], place - 1)

    def step_on(block, carry):
        @pl.when(block <= place)
        def _():
            mask_block(bias, length, place, block)
            at = pl.ds(pl.multiple_of(block * rows, rows), rows)
            for pair in range(half_width // 128):
                lanes = slice(pair * 128, pair * 128 + 128)
                more = slice(half_width + pair * 128, half_width + pair * 128 + 128)
                key = kv_all[at, lanes]
                value = kv_all[at, more]
                key_t = key.T
                d_key = jnp.zeros((rows, 128), F32)
                d_value = jnp.zeros((rows, 128), F32)
                for index in range(4):
                    head = 4 * pair + index
                    scores = dot_right(key, spread[head]) * scale + bias[...]
                    prob = jnp.exp(scores - log_total[head])
                    d_prob = dot_right(value, d_spread[head])
                    d_scores = (prob * (d_prob - delta[head])).astype(BF16)
                    d_value = d_value + dot_plain(prob.astype(BF16), d_spread[head])
                    d_key = d_key + dot_plain(d_scores, spread[head])
                    d_query_t[head] = d_query_t[head] + dot_plain(key_t, d_scores)
                term[:, lanes] = d_key * scale
                term[:, more] = d_value

            @pl.when(chain.has_next)
            def _():
                along(
                    leaving.at[block], coming.at[block], kv_send.at[block], kv_recv.at[block], place
                ).wait_recv()
                term[...] = term[...] + coming[block].astype(F32)

            @pl.when(block < place)
            def _():
                leaving[block] = term[...].astype(BF16)
                downward(block).start()

            @pl.when(block == place)
            def _():
                d_kv[...] = term[...]

        @pl.when(block == 0)
        def _():
            reduction.relay()

        return carry

    lax.fori_loop(0, n_ctx, step_on, 0)
    join_heads(lambda head: d_query_t[head] * scale, d_query)
    reduction.finish()

    def settle(block, carry):
        @pl.when(block < place)
        def _():
            downward(block).wait_send()

        return carry

    lax.fori_loop(0, n_ctx, settle, 0)


def attend_back(length, query, kv_all, d_out, log_total, delta, blocks, collective_id):
    n_ctx = lax.axis_size("ctx")
    rows, width = query.shape
    heads = width // 64
    dma = pltpu.SemaphoreType.DMA
    vmem = pl.BlockSpec(memory_space=pltpu.VMEM)
    wide = jax.ShapeDtypeStruct((rows, width), F32)
    pair = pltpu.VMEM((2, rows // 2, blocks.shape[1]), BF16)
    return pl.pallas_call(
        functools.partial(attend_back_kernel, n_ctx),
        out_shape=(wide, jax.ShapeDtypeStruct((rows, kv_all.shape[1]), F32), wide),
        in_specs=[pl.BlockSpec(memory_space=pltpu.SMEM)] + [vmem] * 6,
        out_specs=[vmem] * 3,
        scratch_shapes=[
            pltpu.VMEM((heads, rows, 128), BF16),
            pltpu.VMEM((heads, rows, 128), BF16),
            pltpu.VMEM((rows, rows), F32),
            pltpu.VMEM((heads, 128, rows), F32),
            pltpu.VMEM((rows, kv_all.shape[1]), F32),
            pltpu.VMEM((n_ctx, rows, kv_all.shape[1]), BF16),
            pltpu.VMEM((n_ctx, rows, kv_all.shape[1]), BF16),
            dma((n_ctx,)),
            dma((n_ctx,)),
            pair,
            pair,
            pair,
            pair,
            dma((6,)),
            dma((6,)),
        ],
        compiler_params=pltpu.CompilerParams(
            collective_id=collective_id, has_side_effects=True, vmem_limit_bytes=56 << 20
        ),
        cost_estimate=busy(50),
    )(length, query, kv_all, d_out, log_total, delta, blocks)


class MixerGather:
    def __init__(self, sources, targets, send_sem, recv_sem, pair_send, pair_recv, own_sem):
        self.section = section = lax.axis_index("section")
        me, beside, across, opposite = corners()
        rows = sources[0].shape[0]
        half = rows // 2
        quarter = half // 2

        def at_rows(out, owner, extra, size):
            return out.at[pl.ds(pl.multiple_of(owner * rows + extra, quarter), size)]

        def pair(slot, at):
            return pltpu.make_async_remote_copy(
                src_ref=at,
                dst_ref=at,
                send_sem=pair_send.at[slot],
                recv_sem=pair_recv.at[slot],
                device_id={"section": 1 - section},
                device_id_type=MESH,
            )

        self.direct, self.onward, self.early, self.late, self.own = [], [], [], [], []
        start = section * half
        for index, (source, out) in enumerate(zip(sources, targets)):
            mine = source.at[pl.ds(pl.multiple_of(start, half), half)]
            spot = at_rows(out, me, start, half)
            slot = 4 * index
            self.direct.append(
                [
                    to_side(mine, spot, send_sem.at[slot], recv_sem.at[slot], beside),
                    to_side(mine, spot, send_sem.at[slot + 1], recv_sem.at[slot + 1], across),
                ]
            )
            passing = at_rows(out, beside, start, quarter), at_rows(out, across, start + quarter, quarter)
            self.onward.append(
                [
                    to_side(passing[0], passing[0], send_sem.at[slot + 2], recv_sem.at[slot + 2], across),
                    to_side(passing[1], passing[1], send_sem.at[slot + 3], recv_sem.at[slot + 3], beside),
                ]
            )
            self.early.append(
                [
                    pair(slot, at_rows(out, beside, start, half)),
                    pair(slot + 1, at_rows(out, across, start, half)),
                ]
            )
            self.late.append(
                [
                    pair(slot + 2, at_rows(out, opposite, start, quarter)),
                    pair(slot + 3, at_rows(out, opposite, start + quarter, quarter)),
                ]
            )
            self.own.append(pltpu.make_async_copy(source, at_rows(out, me, 0, rows), own_sem.at[index]))

    def start(self):
        for copies in self.direct:
            for copy in copies:
                copy.start()
        for copy in self.own:
            copy.start()

    def relay(self):
        for direct, onward, early in zip(self.direct, self.onward, self.early):
            for turn in range(2):
                direct[turn].wait_recv()
                onward[turn].start()
                early[turn].start()

    def relay_last(self):
        for onward, late in zip(self.onward, self.late):
            for turn in range(2):
                onward[turn].wait_recv()
                late[turn].start()

    def arrive(self, index):
        self.own[index].wait()
        for copy in self.early[index] + self.late[index]:
            copy.wait_recv()

    def finish(self):
        for group in (self.direct, self.onward, self.early, self.late):
            for copies in group:
                for copy in copies:
                    copy.wait_send()


def front_kernel(
    n_ctx,
    x_ref,
    gains,
    taps,
    conv_in,
    conv_out,
    gate_in,
    up_in,
    down_in,
    in_out,
    out_out,
    gate_out,
    up_out,
    down_out,
    projected,
    convolved,
    z_low,
    mixed,
    rim,
    act_all,
    w_in,
    w_out,
    w_gate,
    w_up,
    w_down,
    act1,
    act2,
    last_rows,
    rim_sem,
    mix_send,
    mix_recv,
    mix_pair_send,
    mix_pair_recv,
    mix_own,
    send_sem,
    recv_sem,
    pair_send,
    pair_recv,
    own_sem,
    plane_send,
    plane_recv,
    act_send,
    act_recv,
    act_own,
    keep_sem,
):
    chain = Chain(n_ctx)
    section = lax.axis_index("section")
    _, beside, across, opposite = corners()
    greet_mixed(
        chain,
        [{"fsdp": beside}, {"fsdp": across}, {"fsdp": opposite}, {"section": 1 - section}],
    )
    mixers = MixerGather(
        (conv_in, conv_out), (w_in, w_out), mix_send, mix_recv, mix_pair_send, mix_pair_recv, mix_own
    )
    mixers.start()
    columns = SharedColumns(
        0,
        (gate_in, up_in, down_in),
        (w_gate, w_up, w_down),
        send_sem,
        recv_sem,
        pair_send,
        pair_recv,
        own_sem,
        plane_send,
        plane_recv,
    )
    gather = SideGather(act2, act_all, act_send, act_recv, act_own)
    keeping = [
        pltpu.make_async_copy(src, dst, keep_sem.at[index])
        for index, (src, dst) in enumerate(
            ((w_in, in_out), (w_out, out_out), (w_gate, gate_out), (w_up, up_out), (w_down, down_out))
        )
    ]
    rows, width = x_ref.shape
    strip = 64

    def normalize(values, gain):
        inv_rms = lax.rsqrt(jnp.mean(values * values, axis=-1, keepdims=True) + EPSILON)
        return (values * inv_rms * gain).astype(BF16)

    def first_norm(index, carry):
        at = pl.ds(pl.multiple_of(index * strip, strip), strip)
        act1[at] = normalize(x_ref[at].astype(F32), gains[0:1])
        return carry

    lax.fori_loop(0, rows // strip, first_norm, 0)
    mixers.relay()
    columns.start()
    mixers.relay_last()
    mixers.arrive(0)
    keeping[0].start()
    wide = 512

    def project(index, carry):
        at = pl.ds(pl.multiple_of(index * wide, wide), wide)
        projected[:, at] = dot_plain(act1[...], w_in[:, at])
        return carry

    lax.fori_loop(0, projected.shape[1] // wide, project, 0)
    tail_at = pl.ds(rows - 16, 16)
    last_rows[...] = (projected[tail_at, :width] * projected[tail_at, 2 * width :]).astype(BF16)
    to_next = along(last_rows, rim, rim_sem.at[0], rim_sem.at[1], chain.place + 1)

    @pl.when(chain.has_next)
    def _():
        to_next.start()

    @pl.when(chain.has_last)
    def _():
        along(last_rows, rim, rim_sem.at[0], rim_sem.at[1], chain.place).wait_recv()

    @pl.when(jnp.logical_not(chain.has_last))
    def _():
        rim[...] = jnp.zeros(rim.shape, BF16)

    part = 128
    row_at = lax.broadcasted_iota(jnp.int32, (rows, part), 0)

    def convolve(index, carry):
        def lanes(offset):
            return pl.ds(pl.multiple_of(offset * width + index * part, part), part)

        product = (projected[:, lanes(0)] * projected[:, lanes(2)]).astype(BF16).astype(F32)
        edge = rim[:, lanes(0)].astype(F32)
        near, far = edge[15:16], edge[14:15]
        one = jnp.where(row_at >= 1, pltpu.roll(product, 1, 0), near)
        two = jnp.where(row_at >= 2, pltpu.roll(product, 2, 0), jnp.where(row_at == 1, near, far))
        tap = taps[:, lanes(0)]
        value = tap[0:1] * two + tap[1:2] * one + tap[2:3] * product
        convolved[:, lanes(0)] = value
        z_low[:, lanes(0)] = (projected[:, lanes(1)] * value).astype(BF16)
        return carry

    lax.fori_loop(0, width // part, convolve, 0)
    mixers.arrive(1)
    keeping[1].start()

    def mix(index, carry):
        at = pl.ds(pl.multiple_of(index * wide, wide), wide)
        mixed[:, at] = dot_plain(z_low[...], w_out[:, at])
        return carry

    lax.fori_loop(0, width // wide, mix, 0)

    def second_norm(index, carry):
        at = pl.ds(pl.multiple_of(index * strip, strip), strip)
        act2[at] = normalize(x_ref[at].astype(F32) + mixed[at], gains[1:2])
        return carry

    lax.fori_loop(0, rows // strip, second_norm, 0)
    gather.start()
    columns.relay()
    gather.relay()
    columns.relay_passed()
    columns.arrive()
    for copy in keeping[2:]:
        copy.start()
    gather.finish()
    columns.finish()
    mixers.finish()

    @pl.when(chain.has_next)
    def _():
        to_next.wait_send()

    for copy in keeping:
        copy.wait()


def front(x_low, gains, taps, conv_in, conv_out, gate, up, down, collective_id):
    n_ctx, count = lax.axis_size("ctx"), lax.axis_size("fsdp")
    assert count == 4
    rows, width = x_low.shape
    dma = pltpu.SemaphoreType.DMA
    vmem = pl.BlockSpec(memory_space=pltpu.VMEM)
    hbm = pl.BlockSpec(memory_space=pl.ANY)

    def whole(weight):
        return (count * weight.shape[0], weight.shape[1])

    column = (count * gate.shape[0], gate.shape[1] // count)
    weights = [whole(conv_in), whole(conv_out), column, column, down.shape]
    return pl.pallas_call(
        functools.partial(front_kernel, n_ctx),
        out_shape=tuple(jax.ShapeDtypeStruct(shape, BF16) for shape in weights)
        + (
            jax.ShapeDtypeStruct((rows, conv_in.shape[1]), F32),
            jax.ShapeDtypeStruct((rows, width), F32),
            jax.ShapeDtypeStruct((rows, width), BF16),
            jax.ShapeDtypeStruct((rows, width), F32),
            jax.ShapeDtypeStruct((16, width), BF16),
            jax.ShapeDtypeStruct((count * rows, width), BF16),
        ),
        in_specs=[vmem] * 3 + [hbm] * 5,
        out_specs=[hbm] * 5 + [vmem] * 6,
        scratch_shapes=[pltpu.VMEM(shape, BF16) for shape in weights]
        + [
            pltpu.VMEM((rows, width), BF16),
            pltpu.VMEM((rows, width), BF16),
            pltpu.VMEM((16, width), BF16),
            dma((2,)),
            dma((8,)),
            dma((8,)),
            dma((8,)),
            dma((8,)),
            dma((2,)),
            dma((2, count)),
            dma((2, count)),
            dma((3, count)),
            dma((3, count)),
            dma((3,)),
            dma((2, count)),
            dma((2, count)),
            dma((4,)),
            dma((4,)),
            dma,
            dma((5,)),
        ],
        compiler_params=pltpu.CompilerParams(
            collective_id=collective_id, has_side_effects=True, vmem_limit_bytes=58 << 20
        ),
        cost_estimate=busy(70),
    )(x_low, gains, taps, conv_in, conv_out, gate, up, down)


def turn_kernel(
    act_block,
    w_gate_in,
    w_up_in,
    w_down_in,
    d_all_in,
    terms,
    total,
    shared_gu,
    shared_down,
    w_gate,
    w_up,
    w_down,
    d_all,
    load_sem,
    act,
    hidden,
    d_gate,
    d_up,
    blocks,
    act_send,
    act_recv,
    act_own,
    gu_all,
    gu_got,
    gu_sum,
    down_all,
    down_got,
    down_sum,
    keep_sem,
    beside_got,
    across_got,
    passed,
    passed_got,
    send_sem,
    recv_sem,
    pair_send,
    pair_recv,
):
    section = lax.axis_index("section")
    other = 1 - section
    _, beside, across, _ = corners()
    barrier = pltpu.get_barrier_semaphore()
    for target in ({"fsdp": beside}, {"fsdp": across}, {"section": other}):
        pl.semaphore_signal(barrier, inc=1, device_id=target, device_id_type=MESH)
    pl.semaphore_wait(barrier, 3)
    reduction = SideReduce(blocks, total, beside_got, across_got, passed, passed_got, send_sem, recv_sem)
    gather = SideGather(act_block, act, act_send, act_recv, act_own)
    gather.start()
    loads = [
        pltpu.make_async_copy(src, dst, load_sem.at[index])
        for index, (src, dst) in enumerate(
            ((w_gate_in, w_gate), (w_up_in, w_up), (d_all_in, d_all), (w_down_in, w_down))
        )
    ]
    for copy in loads:
        copy.start()
    me, _, _, opposite = corners()
    rows = act_block.shape[0]
    wide, width = w_down.shape
    lanes_wide, lanes_out = 384, 512

    def turn(owner):
        at = pl.ds(pl.multiple_of(owner * rows, rows), rows)

        def hidden_part(index, carry):
            lanes = pl.ds(pl.multiple_of(index * lanes_wide, 128), lanes_wide)
            gate_pre = dot_plain(act[at], w_gate[:, lanes])
            up_pre = dot_plain(act[at], w_up[:, lanes])
            d_hidden = dot_right(d_all[at], w_down[lanes])
            sigmoid = jax.nn.sigmoid(gate_pre)
            silu = gate_pre * sigmoid
            hidden[at, lanes] = (silu * up_pre).astype(BF16)
            d_up[at, lanes] = (d_hidden * silu).astype(BF16)
            d_gate[at, lanes] = (
                d_hidden * up_pre * sigmoid * (1.0 + gate_pre * (1.0 - sigmoid))
            ).astype(BF16)
            return carry

        lax.fori_loop(0, wide // lanes_wide, hidden_part, 0)

        def out_part(index, carry):
            lanes = pl.ds(pl.multiple_of(index * lanes_out, 128), lanes_out)
            terms[at, lanes] = dot_plain(hidden[at], w_down[:, lanes]).astype(BF16)
            blocks[at, lanes] = (
                dot_right(d_gate[at], w_gate[lanes]) + dot_right(d_up[at], w_up[lanes])
            ).astype(BF16)
            return carry

        lax.fori_loop(0, width // lanes_out, out_part, 0)

    gather.own.wait()
    for copy in loads:
        copy.wait()
    turn(me)
    gather.relay()
    turn(beside)
    turn(across)
    reduction.copies[1].start()
    reduction.copies[3].start()
    gather.third.wait_recv()
    gather.fourth.wait_recv()
    turn(opposite)
    reduction.copies[0].start()
    reduction.copies[2].start()
    tile = 256
    half = gu_got.shape[2]
    strips, owners, kinds, strip, _ = gu_sum.shape

    def gate_swap(kind, owner):
        start = owner * (2 * half) + other * half
        return pltpu.make_async_remote_copy(
            src_ref=gu_all.at[kind, pl.ds(pl.multiple_of(start, half), half)],
            dst_ref=gu_got.at[kind, owner],
            send_sem=pair_send.at[kind * owners + owner],
            recv_sem=pair_recv.at[kind * owners + owner],
            device_id={"section": other},
            device_id_type=MESH,
        )

    for kind, right in enumerate((d_gate, d_up)):

        def column(owner, carry, kind=kind, right=right):
            lanes = pl.ds(pl.multiple_of(owner * tile, tile), tile)
            gu_all[kind, lanes] = dot_plain(act[:, lanes].T, right[...]).astype(BF16)
            gate_swap(kind, owner).start()
            return carry

        lax.fori_loop(0, owners, column, 0)
    reduction.relay()
    height = hidden.shape[1]

    def down_tile(index, carry):
        lanes = pl.ds(pl.multiple_of(index * tile, tile), tile)
        down_all[lanes] = dot_plain(hidden[:, lanes].T, d_all[...]).astype(BF16)
        return carry

    lax.fori_loop(0, height // tile, down_tile, 0)
    rest = height // tile * tile
    if rest < height:
        down_all[rest:] = dot_plain(hidden[:, rest:].T, d_all[...]).astype(BF16)
    down_half = height // 2
    down_swap = pltpu.make_async_remote_copy(
        src_ref=down_all.at[pl.ds(pl.multiple_of(other * down_half, 16), down_half)],
        dst_ref=down_got,
        send_sem=pair_send.at[kinds * owners],
        recv_sem=pair_recv.at[kinds * owners],
        device_id={"section": other},
        device_id_type=MESH,
    )
    down_swap.start()

    def join(index, carry):
        place = index // (owners * kinds)
        left = lax.rem(index, owners * kinds)
        owner, kind = left // kinds, lax.rem(left, kinds)

        @pl.when(place == 0)
        def _():
            gate_swap(kind, owner).wait_recv()

        mine = pl.ds(pl.multiple_of(owner * (2 * half) + section * half + place * strip, strip), strip)
        theirs = pl.ds(pl.multiple_of(place * strip, strip), strip)
        gu_sum[place, owner, kind] = (
            gu_all[kind, mine].astype(F32) + gu_got[kind, owner, theirs].astype(F32)
        ).astype(BF16)
        return carry

    lax.fori_loop(0, strips * owners * kinds, join, 0)
    keeping = [pltpu.make_async_copy(gu_sum, shared_gu, keep_sem.at[0])]
    keeping[0].start()
    down_swap.wait_recv()
    piece = 64

    def join_down(index, carry):
        theirs = pl.ds(pl.multiple_of(index * piece, piece), piece)
        mine = pl.ds(pl.multiple_of(section * down_half + index * piece, piece), piece)
        down_sum[theirs] = (down_all[mine].astype(F32) + down_got[theirs].astype(F32)).astype(BF16)
        return carry

    lax.fori_loop(0, down_half // piece, join_down, 0)
    keeping.append(pltpu.make_async_copy(down_sum, shared_down, keep_sem.at[1]))
    keeping[1].start()
    reduction.finish()

    def settle(index, carry):
        gate_swap(index // owners, lax.rem(index, owners)).wait_send()
        return carry

    lax.fori_loop(0, kinds * owners, settle, 0)
    down_swap.wait_send()
    for copy in (gather.first, gather.second, gather.third, gather.fourth):
        copy.wait_send()
    for copy in keeping:
        copy.wait()


def ffn_turn(act_block, w_gate, w_up, w_down, d_all, collective_id):
    n_ctx, owners = lax.axis_size("ctx"), lax.axis_size("fsdp")
    rows, width = act_block.shape
    wide = w_gate.shape[1]
    half = width // owners // 2
    dma = pltpu.SemaphoreType.DMA
    vmem = pl.BlockSpec(memory_space=pltpu.VMEM)
    hbm = pl.BlockSpec(memory_space=pl.ANY)
    pair = pltpu.VMEM((2, rows // 2, width), BF16)
    summed = (n_ctx, owners, 2, half // n_ctx, wide)
    assert width // owners == 256 and wide // 2 % 64 == 0 and wide % 384 == 0
    whole = (owners * rows, width)
    columns = pltpu.VMEM((owners * rows, wide), BF16)
    return pl.pallas_call(
        turn_kernel,
        out_shape=(
            jax.ShapeDtypeStruct(whole, BF16),
            jax.ShapeDtypeStruct((rows, width), F32),
            jax.ShapeDtypeStruct(summed, BF16),
            jax.ShapeDtypeStruct((wide // 2, width), BF16),
        ),
        in_specs=[vmem] + [hbm] * 4,
        out_specs=[vmem, vmem, hbm, hbm],
        scratch_shapes=[pltpu.VMEM(k.shape, BF16) for k in (w_gate, w_up, w_down, d_all)]
        + [
            dma((4,)),
            pltpu.VMEM(whole, BF16),
            columns,
            columns,
            columns,
            pltpu.VMEM(whole, BF16),
            dma((4,)),
            dma((4,)),
            dma,
            pltpu.VMEM((2, width, wide), BF16),
            pltpu.VMEM((2, owners, half, wide), BF16),
            pltpu.VMEM(summed, BF16),
            pltpu.VMEM((wide, width), BF16),
            pltpu.VMEM((wide // 2, width), BF16),
            pltpu.VMEM((wide // 2, width), BF16),
            dma((2,)),
            pair,
            pair,
            pair,
            pair,
            dma((6,)),
            dma((6,)),
            dma((2 * owners + 1,)),
            dma((2 * owners + 1,)),
        ],
        compiler_params=pltpu.CompilerParams(
            collective_id=collective_id, has_side_effects=True, vmem_limit_bytes=58 << 20
        ),
        cost_estimate=busy(45),
    )(act_block, w_gate, w_up, w_down, d_all)


def back_kernel(
    n_ctx,
    blocks,
    d_gate,
    d_up,
    x_ref,
    mixed,
    d_h,
    gains,
    taps,
    z_low,
    rim,
    act_in,
    hidden_in,
    d_all_in,
    w_in_in,
    w_out_in,
    projected_in,
    convolved_in,
    gate_grad,
    up_grad,
    down_grad,
    b_grad,
    c_grad,
    x_grad,
    o_grad,
    d_x,
    small,
    act,
    hidden,
    d_all,
    w_in,
    w_out,
    projected,
    convolved,
    load_sem,
    stage_wide,
    stage,
    stage_sem,
    beside_got,
    across_got,
    passed,
    passed_got,
    send_sem,
    recv_sem,
    d_act,
    d_res,
    d_mixed,
    d_conv,
    d_proj,
    act1,
    edge,
    next_edge,
    edge_sem,
):
    chain = Chain(n_ctx)
    _, beside, across, _ = corners()
    greet_mixed(chain, [{"fsdp": beside}, {"fsdp": across}])
    reduction = SideReduce(blocks, d_act, beside_got, across_got, passed, passed_got, send_sem, recv_sem)
    reduction.start()
    loads = [
        pltpu.make_async_copy(src, dst, load_sem.at[index])
        for index, (src, dst) in enumerate(
            (
                (act_in, act),
                (hidden_in, hidden),
                (d_all_in, d_all),
                (convolved_in, convolved),
                (projected_in, projected),
                (w_out_in, w_out),
                (w_in_in, w_in),
            )
        )
    ]
    for copy in loads:
        copy.start()
    rows, width = x_ref.shape
    wide = d_gate.shape[1]
    tile = 256
    small[...] = jnp.zeros(small.shape, F32)

    def weight_grad(left, right, at_right, target, staging, slot):
        count = left.shape[1] // tile

        def leaving(index, at):
            return pltpu.make_async_copy(staging.at[at], target.at[index], stage_sem.at[slot + at])

        def step(index, carry):
            at = lax.rem(index, 2)
            lanes = pl.ds(pl.multiple_of(index * tile, tile), tile)

            @pl.when(index >= 2)
            def _():
                leaving(lanes, at).wait()

            staging[at] = dot_plain(left[:, lanes].T, right[:, at_right]).astype(BF16)
            leaving(lanes, at).start()
            return carry

        lax.fori_loop(0, count, step, 0)
        for index in range(min(2, count)):
            leaving(pl.ds(0, tile), index).wait()

    loads[0].wait()
    weight_grad(act, d_gate, slice(None), gate_grad, stage_wide, 0)
    weight_grad(act, d_up, slice(None), up_grad, stage_wide, 0)
    reduction.relay()
    loads[1].wait()
    loads[2].wait()
    odd = hidden.shape[1] % tile

    weight_grad(hidden, d_all, slice(None), down_grad, stage, 2)
    if odd:
        last = hidden.shape[1] - odd
        stage[0, :odd] = dot_plain(hidden[:, last:].T, d_all[...]).astype(BF16)
        copy = pltpu.make_async_copy(stage.at[0, pl.ds(0, odd)], down_grad.at[pl.ds(last, odd)], stage_sem.at[2])
        copy.start()
        copy.wait()
    reduction.finish()
    strip = 64

    def norm_strip(at, values, gain, d_values, row):
        inv_rms = lax.rsqrt(jnp.mean(values * values, axis=-1, keepdims=True) + EPSILON)
        normed = values * inv_rms
        small[row : row + 1] = small[row : row + 1] + jnp.sum(d_values * normed, axis=0, keepdims=True)
        d_normed = d_values * gain
        return inv_rms * d_normed - normed * inv_rms * jnp.mean(d_normed * normed, axis=-1, keepdims=True)

    def second_norm(index, carry):
        at = pl.ds(pl.multiple_of(index * strip, strip), strip)
        x_rows = x_ref[at].astype(F32)
        value = d_h[at].astype(F32) + norm_strip(at, x_rows + mixed[at], gains[1:2], d_act[at], 1)
        d_res[at] = value
        d_mixed[at] = value.astype(BF16)
        inv_rms = lax.rsqrt(jnp.mean(x_rows * x_rows, axis=-1, keepdims=True) + EPSILON)
        act1[at] = (x_rows * inv_rms * gains[0:1]).astype(BF16)
        return carry

    lax.fori_loop(0, rows // strip, second_norm, 0)
    for index in range(3, 6):
        loads[index].wait()

    def to_z(index, carry):
        at = pl.ds(pl.multiple_of(index * tile, tile), tile)
        d_conv[:, at] = dot_right(d_mixed[...], w_out[at])
        return carry

    lax.fori_loop(0, width // tile, to_z, 0)
    part = 128
    row_at = lax.broadcasted_iota(jnp.int32, (rows, part), 0)

    def lanes_of(offset, index):
        return pl.ds(pl.multiple_of(offset * width + index * part, part), part)

    def convolve_back(index, carry):
        lanes = lanes_of(0, index)
        product = (projected[:, lanes] * projected[:, lanes_of(2, index)]).astype(BF16).astype(F32)
        before = rim[:, lanes].astype(F32)
        near, far = before[15:16], before[14:15]
        one = jnp.where(row_at >= 1, pltpu.roll(product, 1, 0), near)
        two = jnp.where(row_at >= 2, pltpu.roll(product, 2, 0), jnp.where(row_at == 1, near, far))
        d_z = d_conv[:, lanes]
        d_proj[:, lanes_of(1, index)] = (d_z * convolved[:, lanes]).astype(BF16)
        d_value = d_z * projected[:, lanes_of(1, index)]
        d_conv[:, lanes] = d_value
        for row, source in ((2, two), (3, one), (4, product)):
            small[row : row + 1, lanes] = jnp.sum(d_value * source, axis=0, keepdims=True)
        tap = taps[:, lanes]
        edge[0:1, lanes] = tap[0:1] * d_value[0:1]
        edge[1:2, lanes] = tap[0:1] * d_value[1:2] + tap[1:2] * d_value[0:1]
        return carry

    lax.fori_loop(0, width // part, convolve_back, 0)
    edge[2:8] = jnp.zeros((6, width), F32)
    to_last = along(edge, next_edge, edge_sem.at[0], edge_sem.at[1], chain.place - 1)

    @pl.when(chain.has_last)
    def _():
        to_last.start()

    weight_grad(z_low, d_mixed, slice(None), o_grad, stage, 2)

    @pl.when(chain.has_next)
    def _():
        along(edge, next_edge, edge_sem.at[0], edge_sem.at[1], chain.place).wait_recv()

    @pl.when(jnp.logical_not(chain.has_next))
    def _():
        next_edge[...] = jnp.zeros(next_edge.shape, F32)

    def products_back(index, carry):
        lanes = lanes_of(0, index)
        d_value = d_conv[:, lanes]
        tap = taps[:, lanes]
        after = next_edge[:, lanes]
        one = jnp.where(row_at < rows - 1, pltpu.roll(d_value, rows - 1, 0), 0.0)
        two = jnp.where(row_at < rows - 2, pltpu.roll(d_value, rows - 2, 0), 0.0)
        joined = tap[2:3] * d_value + tap[1:2] * one + tap[0:1] * two
        joined = joined + jnp.where(row_at == rows - 2, after[0:1], 0.0)
        joined = joined + jnp.where(row_at == rows - 1, after[1:2], 0.0)
        joined = joined.astype(BF16).astype(F32)
        d_proj[:, lanes] = (joined * projected[:, lanes_of(2, index)]).astype(BF16)
        d_proj[:, lanes_of(2, index)] = (joined * projected[:, lanes]).astype(BF16)
        return carry

    lax.fori_loop(0, width // part, products_back, 0)
    loads[6].wait()

    def to_act(index, carry):
        at = pl.ds(pl.multiple_of(index * tile, tile), tile)
        d_act[:, at] = dot_right(d_proj[...], w_in[at])
        return carry

    lax.fori_loop(0, width // tile, to_act, 0)
    for offset, target in enumerate((b_grad, c_grad, x_grad)):
        weight_grad(act1, d_proj, slice(offset * width, (offset + 1) * width), target, stage, 2)

    def first_norm(index, carry):
        at = pl.ds(pl.multiple_of(index * strip, strip), strip)
        value = d_res[at] + norm_strip(at, x_ref[at].astype(F32), gains[0:1], d_act[at], 0)
        d_x[at] = value.astype(BF16)
        return carry

    lax.fori_loop(0, rows // strip, first_norm, 0)

    @pl.when(chain.has_last)
    def _():
        to_last.wait_send()


def conv_back(blocks, d_gate, d_up, local, kept, collective_id):
    n_ctx = lax.axis_size("ctx")
    x_low = local[0]
    act, hidden = kept[0], kept[1]
    rows, width = x_low.shape
    wide = d_gate.shape[1]
    dma = pltpu.SemaphoreType.DMA
    vmem = pl.BlockSpec(memory_space=pltpu.VMEM)
    hbm = pl.BlockSpec(memory_space=pl.ANY)
    pair = pltpu.VMEM((2, rows // 2, width), BF16)
    square = jax.ShapeDtypeStruct((width, width), BF16)
    column = jax.ShapeDtypeStruct((width, wide), BF16)
    return pl.pallas_call(
        functools.partial(back_kernel, n_ctx),
        out_shape=(
            column,
            column,
            jax.ShapeDtypeStruct((wide, width), BF16),
            square,
            square,
            square,
            square,
            jax.ShapeDtypeStruct((rows, width), BF16),
            jax.ShapeDtypeStruct((8, width), F32),
        ),
        in_specs=[vmem] * (3 + len(local)) + [hbm] * len(kept),
        out_specs=[hbm] * 7 + [vmem] * 2,
        scratch_shapes=[pltpu.VMEM(k.shape, k.dtype) for k in kept]
        + [
            dma((7,)),
            pltpu.VMEM((2, 256, wide), BF16),
            pltpu.VMEM((2, 256, width), BF16),
            dma((4,)),
            pair,
            pair,
            pair,
            pair,
            dma((6,)),
            dma((6,)),
            pltpu.VMEM((rows, width), F32),
            pltpu.VMEM((rows, width), F32),
            pltpu.VMEM((rows, width), BF16),
            pltpu.VMEM((rows, width), F32),
            pltpu.VMEM((rows, 3 * width), BF16),
            pltpu.VMEM((rows, width), BF16),
            pltpu.VMEM((8, width), F32),
            pltpu.VMEM((8, width), F32),
            dma((2,)),
        ],
        compiler_params=pltpu.CompilerParams(
            collective_id=collective_id, has_side_effects=True, vmem_limit_bytes=58 << 20
        ),
        cost_estimate=busy(35),
    )(blocks, d_gate, d_up, *local, *kept)


def ffn_forward(act, w_gate, w_up, w_down):
    gate_pre = matmul(act, w_gate)
    up_pre = matmul(act, w_up)
    hidden = (jax.nn.silu(gate_pre) * up_pre).astype(BF16)
    return matmul(hidden, w_down).astype(BF16), (act, gate_pre, up_pre, hidden)


def ffn_backward(d_all, kept, w_gate, w_up, w_down):
    act, gate_pre, up_pre, hidden = kept
    d_hidden = matmul_right(d_all, w_down)
    sigmoid = jax.nn.sigmoid(gate_pre)
    d_up = (d_hidden * gate_pre * sigmoid).astype(BF16)
    d_gate = (d_hidden * up_pre * sigmoid * (1.0 + gate_pre * (1.0 - sigmoid))).astype(BF16)
    terms = (matmul_right(d_gate, w_gate) + matmul_right(d_up, w_up)).astype(BF16)
    return terms, d_gate, d_up


def ffn_norm_back(d_act, residual, gain):
    normed, inv_rms = norm_rows(residual)
    return norm_back(d_act * gain, normed, inv_rms), jnp.sum(d_act * normed, axis=0)


def shards(
    inputs,
    cotangent,
    lengths,
    norm_gains,
    conv_in,
    conv_kernel,
    conv_out,
    attn_q,
    attn_k,
    attn_v,
    attn_out,
    head_gains,
    ffn_gate,
    ffn_up,
    ffn_down,
):
    micro, rows, width = inputs.shape
    section = lax.axis_index("section")
    group = lax.axis_index("fsdp")
    fsdp = lax.axis_size("fsdp")
    assert micro == lax.axis_size("section")
    head = head_gains.shape[1]
    q_width, kv_width = attn_q.shape[1], attn_k.shape[1]
    q_heads, kv_heads = q_width // head, kv_width // head
    positions = lax.axis_index("ctx") * rows + jnp.arange(rows)
    length = lax.dynamic_index_in_dim(lengths, group * micro + section, keepdims=False)
    mask = (positions < length).astype(F32)[:, None]

    def whole_rows(weight):
        share = weight.shape[0] // (micro * lax.axis_size("ctx"))
        start = (section * lax.axis_size("ctx") + lax.axis_index("ctx")) * share
        mine = lax.dynamic_slice_in_dim(weight, start, share, 0)
        return lax.all_gather(mine, ("fsdp", "section", "ctx"), axis=0, tiled=True)

    part = ffn_gate.shape[1]
    attn_full = whole_rows(jnp.concatenate([attn_q, attn_k, attn_v, attn_out], axis=1))
    query_full, key_full, value_full, proj_full = (
        attn_full[:, :q_width],
        attn_full[:, q_width : q_width + kv_width],
        attn_full[:, q_width + kv_width : q_width + 2 * kv_width],
        attn_full[:, q_width + 2 * kv_width :],
    )

    x_low = lax.dynamic_index_in_dim(inputs, section, keepdims=False)
    in_full, out_full, gate1, up1, down1, projected, convolved, z_low, mixed, rim, act_all1 = front(
        x_low, norm_gains, conv_kernel, conv_in, conv_out, ffn_gate[0], ffn_up[0], ffn_down[0], 2
    )
    x = x_low.astype(F32)
    res1 = x + mixed
    terms1, kept1 = ffn_forward(act_all1, gate1, up1, down1)
    ffn1 = reduced(terms1, 1)
    h_low = (res1 + ffn1).astype(BF16)

    h = h_low.astype(F32)
    normed2, inv2 = norm_rows(h)
    act2 = (normed2 * norm_gains[2]).astype(BF16)
    q_normed, q_inv = norm_heads(matmul(act2, query_full), head)
    k_normed, k_inv = norm_heads(matmul(act2, key_full), head)
    q_gain = jnp.tile(head_gains[0], q_heads)
    k_gain = jnp.tile(head_gains[1], kv_heads)
    query = (q_normed * q_gain).astype(BF16)
    key = (k_normed * k_gain).astype(BF16)
    value = matmul(act2, value_full).astype(BF16)
    d_sum_low = (lax.dynamic_index_in_dim(cotangent, section, keepdims=False).astype(F32) * mask).astype(BF16)
    attended, log_total, kv_all, d_sum_all, gate2, up2, down2 = attend(
        length.reshape(1),
        query,
        jnp.concatenate([key, value], axis=1),
        d_sum_low,
        ffn_gate[0],
        ffn_up[0],
        ffn_down[0],
        3,
    )
    attended_low = attended.astype(BF16)
    attn_rows = matmul(attended_low, proj_full)
    res2 = h + attn_rows
    normed3, _ = norm_rows(res2)
    terms2, d_act3, shared_gu, shared_down = ffn_turn(
        (normed3 * norm_gains[3]).astype(BF16), gate2, up2, down2, d_sum_all, 8
    )

    d_sum = d_sum_low.astype(F32)
    d_ffn, gain3 = ffn_norm_back(d_act3, res2, norm_gains[3])
    d_res2 = d_sum + d_ffn
    d_attn = d_res2.astype(BF16)
    grad_proj = matmul_left(attended_low, d_attn)
    d_att = matmul_right(d_attn, proj_full).astype(BF16)
    delta = jnp.sum((d_att.astype(F32) * attended).reshape(rows, q_heads, head), axis=-1)
    d_query, d_kv, ffn2 = attend_back(
        length.reshape(1), query, kv_all, d_att, log_total, delta.T.reshape(q_heads, 1, rows), terms2, 4
    )
    result = (res2 + ffn2) * mask

    def square(values):
        return jnp.sum(mask * values * values, axis=0, keepdims=True)

    squares = [square(v) for v in (x, mixed, ffn1, h, attn_rows, res2, ffn2, result)]
    second_gu = lax.psum_scatter(
        shared_gu.reshape(-1, shared_gu.shape[-1]), "ctx", scatter_dimension=0, tiled=True
    )
    d_qn = rounded(d_query)
    grad_qgain = jnp.sum(jnp.sum(d_qn * q_normed, axis=0).reshape(q_heads, head), axis=0)
    d_qpre = norm_heads_back(d_qn * q_gain, q_normed, q_inv, head).astype(BF16)
    d_kn = rounded(d_kv[:, :kv_width])
    grad_kgain = jnp.sum(jnp.sum(d_kn * k_normed, axis=0).reshape(kv_heads, head), axis=0)
    d_kpre = norm_heads_back(d_kn * k_gain, k_normed, k_inv, head).astype(BF16)
    d_vpre = d_kv[:, kv_width:].astype(BF16)
    d_act2 = (
        matmul_right(d_qpre, query_full)
        + matmul_right(d_kpre, key_full)
        + matmul_right(d_vpre, value_full)
    )
    gain2 = jnp.sum(d_act2 * normed2, axis=0)
    d_h_low = (d_res2 + norm_back(d_act2 * norm_gains[2], normed2, inv2)).astype(BF16)

    d_h_all, second_gu = gathered_swapped(
        d_h_low, second_gu.reshape(fsdp, -1, second_gu.shape[-1]), 5
    )
    second_gu = lax.all_gather(second_gu, "ctx", axis=0)
    d_terms1, d_gate1, d_up1 = ffn_backward(d_h_all, kept1, gate1, up1, down1)
    attn_mixers = [
        matmul_left(act2, d_qpre).astype(BF16),
        matmul_left(act2, jnp.concatenate([d_kpre, d_vpre], axis=1)).astype(BF16),
        grad_proj.astype(BF16),
    ]
    *grads, d_x, conv_small = conv_back(
        d_terms1,
        d_gate1,
        d_up1,
        (x_low, mixed, d_h_low, norm_gains, conv_kernel, z_low, rim),
        (act_all1, kept1[3], d_h_all, in_full, out_full, projected, convolved),
        9,
    )

    half = ffn_gate.shape[1] // 2
    y_low = result.astype(BF16)
    is_first = section == 0
    other_end = swapped(jnp.where(is_first, y_low, d_x), "section")
    ends = jnp.where(is_first, jnp.stack([d_x, other_end]), jnp.stack([other_end, y_low]))[None]

    small = jnp.concatenate(
        [conv_small[:2], gain2[None], gain3[None], conv_small[2:5]]
        + [jnp.pad(grad[None], ((0, 0), (0, width - head))) for grad in (grad_qgain, grad_kgain)]
        + [jnp.zeros((7, width), F32)]
        + squares
        + [jnp.zeros((8, width), F32)]
    ).astype(BF16)
    small = small.reshape(2, 16, width)
    gu_sum, down_sum, rest_sum = summed_gradients(
        grads[:3],
        attn_mixers + grads[3:],
        small,
        second_gu.reshape(-1, fsdp, 2, second_gu.shape[2] // 2, second_gu.shape[-1]),
        shared_down,
    )
    rest_sum = rest_sum.astype(F32)

    def block(index):
        rows_at = slice(index * half, (index + 1) * half)
        return rest_sum[:, rows_at].reshape(2 * half, width)

    attn_blocks = [block(i) for i in range(3)]
    conv_blocks = [block(3 + i) for i in range(4)]
    small_sum = rest_sum[0, 7 * half : 7 * half + 9]
    cut = width // fsdp
    mine = lax.dynamic_slice_in_dim(small_sum[:7], group * cut, cut, 1)
    head_cut = head // fsdp
    heads = lax.dynamic_slice_in_dim(small_sum[7:9], group * head_cut, head_cut, 1)
    square_cut = len(squares) // fsdp
    square_sum = jnp.sum(
        lax.dynamic_slice_in_dim(rest_sum[1, 7 * half : 7 * half + 8], group * square_cut, square_cut, 0), axis=1
    )
    token_total = jnp.sum(lengths).astype(F32) * width
    rms = jnp.sqrt(square_sum / token_total)
    return (
        ends,
        mine[:3],
        mine[3],
        jnp.concatenate(conv_blocks[:3], axis=1),
        mine[4:7],
        conv_blocks[3],
        attn_blocks[0],
        attn_blocks[1][:, :kv_width],
        attn_blocks[1][:, kv_width:],
        attn_blocks[2],
        heads,
        gu_sum[0][None].astype(F32),
        gu_sum[1][None].astype(F32),
        down_sum[None].astype(F32),
        rms,
    )


def solution(mesh):
    return jax.shard_map(
        shards,
        mesh=mesh,
        in_specs=(
            P("fsdp", "ctx", None),
            P("fsdp", "ctx", None),
            P(),
            P(),
            P("fsdp", None),
            P(),
            P("fsdp", None),
            P("fsdp", None),
            P("fsdp", None),
            P("fsdp", None),
            P("fsdp", None),
            P(),
            P("section", "fsdp", None),
            P("section", "fsdp", None),
            P("section", "fsdp", None),
        ),
        out_specs=(
            P("section", "fsdp", "ctx", None),
            P(None, "fsdp"),
            P("fsdp"),
            P("fsdp", None),
            P(None, "fsdp"),
            P("fsdp", None),
            P("fsdp", None),
            P("fsdp", None),
            P("fsdp", None),
            P("fsdp", None),
            P(None, "fsdp"),
            P("section", "fsdp", None),
            P("section", "fsdp", None),
            P("section", "fsdp", None),
            P("fsdp"),
        ),
        check_vma=False,
    )
```

```python
import functools

import jax
import jax.numpy as jnp
from jax import lax
from jax.experimental import pallas as pl
from jax.experimental.pallas import tpu as pltpu
from jax.sharding import PartitionSpec as P

EPSILON = 1e-05
NEGATIVE = -1e30
MESH = pl.DeviceIdType.MESH
F32 = jnp.float32
BF16 = jnp.bfloat16


def passed_along(block, axis, distance):
    devices = range(lax.axis_size(axis))
    route = [(i - distance, i) for i in devices if i - distance in devices]
    return lax.ppermute(block, axis, route)


def swapped(block, axis):
    return lax.ppermute(block, axis, [(0, 1), (1, 0)])


def rounded(values):
    return lax.optimization_barrier(values.astype(BF16)).astype(F32)


def matmul(left_op, right_op):
    return jnp.dot(left_op, right_op, preferred_element_type=F32)


def matmul_left(left_op, right_op):
    return lax.dot_general(left_op, right_op, (((0,), (0,)), ((), ())), preferred_element_type=F32)


def matmul_right(left_op, right_op):
    return lax.dot_general(left_op, right_op, (((1,), (1,)), ((), ())), preferred_element_type=F32)


def norm_rows(values):
    inv_rms = lax.rsqrt(jnp.mean(values * values, axis=-1, keepdims=True) + EPSILON)
    return (values * inv_rms, inv_rms)


def norm_back(dnormed, normed, inv_rms):
    return inv_rms * dnormed - normed * inv_rms * jnp.mean(dnormed * normed, axis=-1, keepdims=True)


def head_sums(values, head):
    heads = values.shape[1] // head
    owner = (jnp.arange(values.shape[1])[:, None] // head == jnp.arange(heads)[None, :]).astype(F32)
    sums = jnp.dot(values, owner, precision=lax.Precision.HIGHEST, preferred_element_type=F32)
    return jnp.dot(sums, owner.T, precision=lax.Precision.HIGHEST, preferred_element_type=F32)


def norm_heads(values, head):
    inv_rms = lax.rsqrt(head_sums(values * values, head) / head + EPSILON)
    return (values * inv_rms, inv_rms)


def norm_heads_back(dnormed, normed, inv_rms, head):
    return inv_rms * dnormed - normed * inv_rms * (head_sums(dnormed * normed, head) / head)


def busy(microseconds):
    return pl.CostEstimate(flops=int(microseconds), bytes_accessed=1 << 16, transcendentals=0)


def corners():
    me = lax.axis_index("fsdp")
    beside = me + 1 - 2 * lax.rem(me, 2)
    across = lax.rem(me + 2, 4)
    return me, beside, across, lax.rem(beside + 2, 4)


def greet_sides():
    _, beside, across, _ = corners()
    barrier = pltpu.get_barrier_semaphore()
    for target in (beside, across):
        pl.semaphore_signal(barrier, inc=1, device_id={"fsdp": target}, device_id_type=MESH)
    pl.semaphore_wait(barrier, 2)


def to_side(src, dst, send_sem, recv_sem, target):
    return pltpu.make_async_remote_copy(
        src_ref=src,
        dst_ref=dst,
        send_sem=send_sem,
        recv_sem=recv_sem,
        device_id={"fsdp": target},
        device_id_type=MESH,
    )


class SideGather:
    def __init__(self, block, whole, send_sem, recv_sem, own_sem):
        me, beside, across, _ = corners()
        rows = block.shape[0]
        half = rows // 2

        def part(owner, start, size):
            return whole.at[pl.ds(pl.multiple_of(owner * rows + start, half), size)]

        self.first = to_side(block, part(me, 0, rows), send_sem.at[0], recv_sem.at[0], beside)
        self.second = to_side(block, part(me, 0, rows), send_sem.at[1], recv_sem.at[1], across)
        at = part(beside, 0, half)
        self.third = to_side(at, at, send_sem.at[2], recv_sem.at[2], across)
        at = part(across, half, half)
        self.fourth = to_side(at, at, send_sem.at[3], recv_sem.at[3], beside)
        self.own = pltpu.make_async_copy(block, part(me, 0, rows), own_sem)

    def start(self):
        self.first.start()
        self.second.start()
        self.own.start()

    def relay(self):
        self.first.wait_recv()
        self.third.start()
        self.second.wait_recv()
        self.fourth.start()

    def finish(self):
        self.own.wait()
        self.first.wait_send()
        self.second.wait_send()
        self.third.wait()
        self.fourth.wait()


class SideReduce:
    def __init__(self, blocks, total, beside_got, across_got, passed, passed_got, send_sem, recv_sem):
        self.refs = blocks, total, beside_got, across_got, passed, passed_got
        me, beside, across, opposite = corners()
        self.me, self.beside, self.across = me, beside, across
        self.copies = []
        for index, (turn, target, got) in enumerate(((0, beside, beside_got), (1, across, across_got))):
            for slot, owner in ((1, opposite), (0, target)):
                self.copies.append(
                    to_side(
                        blocks.at[self.part(owner, turn)],
                        got.at[slot],
                        send_sem.at[2 * index + slot],
                        recv_sem.at[2 * index + slot],
                        target,
                    )
                )
        self.onward = [
            to_side(passed.at[turn], passed_got.at[turn], send_sem.at[4 + turn], recv_sem.at[4 + turn], owner)
            for turn, owner in ((0, across), (1, beside))
        ]

    def part(self, owner, turn):
        half = self.refs[1].shape[0] // 2
        return pl.ds(pl.multiple_of(owner * 2 * half + turn * half, half), half)

    def start(self):
        for index in (0, 2, 1, 3):
            self.copies[index].start()

    def relay(self):
        blocks, _, beside_got, across_got, passed, _ = self.refs
        for turn, owner, index, got in ((0, self.across, 0, beside_got), (1, self.beside, 2, across_got)):
            self.copies[index].wait_recv()
            passed[turn] = (blocks[self.part(owner, turn)].astype(F32) + got[1].astype(F32)).astype(BF16)
            self.onward[turn].start()

    def finish(self):
        blocks, total, beside_got, across_got, _, passed_got = self.refs
        half = total.shape[0] // 2
        for turn, index, got in ((0, 1, beside_got), (1, 3, across_got)):
            self.copies[index].wait_recv()
            total[pl.ds(turn * half, half)] = blocks[self.part(self.me, turn)].astype(F32) + got[0].astype(F32)
        for turn in range(2):
            self.onward[turn].wait_recv()
            at = pl.ds(turn * half, half)
            total[at] = total[at] + passed_got[turn].astype(F32)
        for copy in self.copies + self.onward:
            copy.wait_send()


def reduce_kernel(blocks, total, beside_got, across_got, passed, passed_got, send_sem, recv_sem):
    greet_sides()
    reduction = SideReduce(blocks, total, beside_got, across_got, passed, passed_got, send_sem, recv_sem)
    reduction.start()
    reduction.relay()
    reduction.finish()


def reduced(partial, collective_id):
    rows, width = partial.shape[0] // 4, partial.shape[1]
    assert lax.axis_size("fsdp") == 4
    dma = pltpu.SemaphoreType.DMA
    pair = pltpu.VMEM((2, rows // 2, width), BF16)
    return pl.pallas_call(
        reduce_kernel,
        out_shape=jax.ShapeDtypeStruct((rows, width), F32),
        in_specs=[pl.BlockSpec(memory_space=pltpu.VMEM)],
        out_specs=pl.BlockSpec(memory_space=pltpu.VMEM),
        scratch_shapes=[pair, pair, pair, pair, dma((6,)), dma((6,))],
        compiler_params=pltpu.CompilerParams(
            collective_id=collective_id, has_side_effects=True, vmem_limit_bytes=16 << 20
        ),
        cost_estimate=busy(25),
    )(partial.astype(BF16))


def tail_kernel(
    counts,
    gate_in,
    up_in,
    down_in,
    query_in,
    kv_in,
    proj_in,
    conv_b_in,
    conv_c_in,
    conv_x_in,
    conv_o_in,
    small_in,
    second_gu_in,
    second_down_in,
    gu_out,
    down_out,
    rest_out,
    a_own,
    a_other,
    a_sum,
    a_done,
    b_own,
    b_other,
    b_sum,
    b_done,
    c_own,
    c_other,
    c_got,
    own_sem,
    pair_send,
    pair_recv,
    c_own_sem,
    c_pair_send,
    c_pair_recv,
    c_send,
    c_recv,
    a_up_send,
    a_up_recv,
    a_back_send,
    a_back_recv,
    a_out_send,
    b_up_send,
    b_up_recv,
    b_back_send,
    b_back_recv,
    b_out_send,
    b_keep_sem,
    gu_recv,
    down_recv,
    rest_recv,
    second_send,
):
    n_ctx, n_fsdp = counts
    section = lax.axis_index("section")
    place = lax.axis_index("ctx")
    group = lax.axis_index("fsdp")
    other = 1 - section
    a_chunks, a_rows, a_width = a_own.shape
    b_chunks, b_rows, b_width = b_own.shape
    half = gate_in.shape[0] // n_fsdp // 2
    subs = half // a_rows
    per_kind = n_fsdp * subs
    down_half = down_in.shape[0] // 2
    down_chunks = down_half // b_rows
    c_rows = c_own.shape[1]
    mixers = (query_in, kv_in, proj_in, conv_b_in, conv_c_in, conv_x_in, conv_o_in)
    n_mix = len(mixers)
    cut = 3 * half // b_rows
    c_parts = ((0, cut), (cut, c_rows // b_rows))
    paired = a_chunks // 2
    mix_start = 2 * down_chunks
    mix_chunks = b_chunks - mix_start
    second = paired + down_chunks // 2
    ticks = second + mix_chunks // 2
    tail = 2 * (n_ctx - 1)

    barrier = pltpu.get_barrier_semaphore()
    for step in range(1, 2 * n_fsdp):
        flat = lax.rem(section * n_fsdp + group + step, 2 * n_fsdp)
        pl.semaphore_signal(
            barrier,
            inc=1,
            device_id={"section": flat // n_fsdp, "fsdp": lax.rem(flat, n_fsdp)},
            device_id_type=MESH,
        )

    @pl.when(place > 0)
    def _():
        pl.semaphore_signal(barrier, inc=1, device_id={"ctx": place - 1}, device_id_type=MESH)

    @pl.when(place < n_ctx - 1)
    def _():
        pl.semaphore_signal(barrier, inc=1, device_id={"ctx": place + 1}, device_id_type=MESH)

    at_edge = (place == 0) | (place == n_ctx - 1)

    @pl.when(at_edge)
    def _():
        pl.semaphore_wait(barrier, 2 * n_fsdp)

    @pl.when(jnp.logical_not(at_edge))
    def _():
        pl.semaphore_wait(barrier, 2 * n_fsdp + 1)

    def half_rows(owner, which):
        return pl.ds(pl.multiple_of(owner * (2 * half) + which * half, half), half)

    def a_at(buffer, k):
        return buffer.at[k]

    b_at = a_at

    def opening(k):
        copies = []
        kind, rest = divmod(k, per_kind)
        owner, sub = divmod(rest, subs)
        source = (gate_in, up_in)[kind]
        spots = []
        for which in (section, other):
            start = owner * (2 * half) + which * half + sub * a_rows
            spots.append(source.at[pl.ds(pl.multiple_of(start, a_rows), a_rows)])
        copies.append((spots, a_own.at[k], a_other.at[k], k))
        if k < down_chunks:
            spots = [
                down_in.at[pl.ds(pl.multiple_of(which * down_half + k * b_rows, b_rows), b_rows)]
                for which in (section, other)
            ]
            copies.append((spots, b_own.at[k], b_other.at[k], a_chunks + k))
        for (mine, theirs), own_dst, other_dst, spot in copies:
            pltpu.make_async_copy(mine, own_dst, own_sem.at[spot]).start()
            pltpu.make_async_remote_copy(
                src_ref=theirs,
                dst_ref=other_dst,
                send_sem=pair_send.at[spot],
                recv_sem=pair_recv.at[spot],
                device_id={"section": other},
                device_id_type=MESH,
            ).start()

    for k in range(a_chunks):
        opening(k)
    for k in range(down_chunks):
        pltpu.make_async_copy(
            second_down_in.at[pl.ds(k * b_rows, b_rows)],
            b_own.at[down_chunks + k],
            own_sem.at[a_chunks + down_chunks + k],
        ).start()
    c_local, c_pair = ([], []), ([], [])
    for kind, source in enumerate(mixers):
        part = 0 if kind < 3 else 1
        for owner in range(n_fsdp):
            index = owner * (n_mix + 1) + kind
            place_at = pl.ds(kind * half, half)
            c_local[part].append(
                pltpu.make_async_copy(
                    source.at[half_rows(owner, section)], c_own.at[owner, place_at], c_own_sem.at[index]
                )
            )
            c_pair[part].append(
                pltpu.make_async_remote_copy(
                    src_ref=source.at[half_rows(owner, other)],
                    dst_ref=c_other.at[owner, place_at],
                    send_sem=c_pair_send.at[index],
                    recv_sem=c_pair_recv.at[index],
                    device_id={"section": other},
                    device_id_type=MESH,
                )
            )
    for owner in range(n_fsdp):
        small_at = pl.ds(n_mix * half, c_rows - n_mix * half)
        index = owner * (n_mix + 1) + n_mix
        c_local[1].append(
            pltpu.make_async_copy(small_in.at[section], c_own.at[owner, small_at], c_own_sem.at[index])
        )
        c_pair[1].append(
            pltpu.make_async_remote_copy(
                src_ref=small_in.at[other],
                dst_ref=c_other.at[owner, small_at],
                send_sem=c_pair_send.at[index],
                recv_sem=c_pair_recv.at[index],
                device_id={"section": other},
                device_id_type=MESH,
            )
        )
    for part in range(2):
        for copy in c_pair[part]:
            copy.start()
        for copy in c_local[part]:
            copy.start()
    b_own[b_chunks - 1] = jnp.zeros((b_rows, b_width), BF16)
    _, beside, across, opposite = corners()

    def span(first, last):
        return pl.ds(first * b_rows, (last - first) * b_rows)

    def mixer_spans(part):
        first, last = c_parts[part]
        middle = (first + last) // 2
        return (first, middle, beside, across), (middle, last, across, beside)

    def mixer_copies(part):
        opening, onward = [], []
        for turn, (first, last, near, far) in enumerate(mixer_spans(part)):
            at = span(first, last)
            for slot, owner in ((0, opposite), (1, near)):
                opening.append(
                    to_side(
                        c_own.at[owner, at],
                        c_got.at[slot, at],
                        c_send.at[part, 3 * turn + slot],
                        c_recv.at[part, 3 * turn + slot],
                        near,
                    )
                )
            onward.append(
                to_side(
                    c_own.at[far, at],
                    c_got.at[2, at],
                    c_send.at[part, 3 * turn + 2],
                    c_recv.at[part, 3 * turn + 2],
                    far,
                )
            )
        return opening, onward

    def mixer_sum(part, owner):
        kinds = range(3) if part == 0 else range(3, n_mix + 1)
        first, last = c_parts[part]
        for kind in kinds:
            size = half if kind < n_mix else c_rows - n_mix * half
            at = c_own.at[owner, pl.ds(kind * half, size)]
            index = owner * (n_mix + 1) + kind
            pltpu.make_async_copy(at, at, c_own_sem.at[index]).wait()
            pltpu.make_async_copy(at, at, c_pair_recv.at[index]).wait()

        def add(index, carry):
            at = pl.ds(pl.multiple_of(index * b_rows, b_rows), b_rows)
            c_own[owner, at] = (c_own[owner, at].astype(F32) + c_other[owner, at].astype(F32)).astype(BF16)
            return carry

        lax.fori_loop(first, last, add, 0)

    def mixer_out(part):
        opening, _ = mixer_copies(part)
        for index in (0, 2, 1, 3):
            opening[index].start()

    def mixer_on(part):
        opening, onward = mixer_copies(part)
        for turn, (first, last, near, far) in enumerate(mixer_spans(part)):
            opening[2 * turn].wait_recv()

            def add(index, carry, far=far):
                at = pl.ds(pl.multiple_of(index * b_rows, b_rows), b_rows)
                c_own[far, at] = (c_own[far, at].astype(F32) + c_got[0, at].astype(F32)).astype(BF16)
                return carry

            lax.fori_loop(first, last, add, 0)
            onward[turn].start()

    def mixer_in(part):
        opening, onward = mixer_copies(part)
        for turn in range(2):
            opening[2 * turn + 1].wait_recv()
            onward[turn].wait_recv()
        first, last = c_parts[part]

        def add(index, carry):
            at = pl.ds(pl.multiple_of(index * b_rows, b_rows), b_rows)
            total = c_own[group, at].astype(F32) + c_got[1, at].astype(F32) + c_got[2, at].astype(F32)
            b_own[mix_start + index] = total.astype(BF16)
            return carry

        lax.fori_loop(first, last, add, 0)

    strip = half // n_ctx

    def second_start():
        for owner in range(n_fsdp):
            is_mine = (section == 1) & (group == owner)
            for index in range(2 * n_ctx):
                turn, kind = index // 2, index % 2
                src = second_gu_in.at[turn, owner, kind]
                dst = gu_out.at[
                    kind,
                    pl.ds(pl.multiple_of(section * half + turn * strip, strip), strip),
                    pl.ds(pl.multiple_of(group * a_width, 128), a_width),
                ]

                @pl.when(is_mine)
                def _(src=src, dst=dst):
                    pltpu.make_async_copy(src, dst, second_send.at[0]).start()

                @pl.when(jnp.logical_not(is_mine))
                def _(src=src, dst=dst, kind=kind, owner=owner):
                    pltpu.make_async_remote_copy(
                        src_ref=src,
                        dst_ref=dst,
                        send_sem=second_send.at[0],
                        recv_sem=gu_recv.at[kind, section * n_fsdp + group],
                        device_id={"section": 1, "fsdp": owner},
                        device_id_type=MESH,
                    ).start()

    def a_target(k):
        kind = k // per_kind
        rest = lax.rem(k, per_kind)
        owner = rest // subs
        sub = lax.rem(rest, subs)
        start = section * half + sub * a_rows
        spot = gu_out.at[
            kind,
            pl.ds(pl.multiple_of(start, a_rows), a_rows),
            pl.ds(pl.multiple_of(group * a_width, 128), a_width),
        ]
        return kind, owner, spot

    def a_hand_out(k):
        kind, owner, spot = a_target(k)
        is_mine = (section == 0) & (group == owner)
        slot = k
        a_ref = a_at(a_done, k)

        @pl.when(is_mine)
        def _():
            pltpu.make_async_copy(a_ref, spot, a_out_send.at[slot]).start()

        @pl.when(jnp.logical_not(is_mine))
        def _():
            pltpu.make_async_remote_copy(
                src_ref=a_ref,
                dst_ref=spot,
                send_sem=a_out_send.at[slot],
                recv_sem=gu_recv.at[kind, section * n_fsdp + group],
                device_id={"section": 0, "fsdp": owner},
                device_id_type=MESH,
            ).start()

    def down_hand_out(k, keeper):
        slot = k
        b_ref = b_at(b_done, k)
        index = k - keeper * down_chunks
        at = down_out.at[
            pl.ds(pl.multiple_of(section * down_half + index * b_rows, b_rows), b_rows),
        ]

        @pl.when(section == keeper)
        def _():
            pltpu.make_async_copy(b_ref, at, b_out_send.at[slot]).start()

        @pl.when(section != keeper)
        def _():
            pltpu.make_async_remote_copy(
                src_ref=b_ref,
                dst_ref=at,
                send_sem=b_out_send.at[slot],
                recv_sem=down_recv,
                device_id={"section": keeper},
                device_id_type=MESH,
            ).start()

    def mix_hand_out(k):
        slot = k
        b_ref = b_at(b_done, k)
        at = rest_out.at[
            section,
            pl.ds(pl.multiple_of((k - mix_start) * b_rows, b_rows), b_rows),
        ]
        pltpu.make_async_copy(b_ref, at, b_keep_sem.at[slot]).start()
        pltpu.make_async_remote_copy(
            src_ref=b_ref,
            dst_ref=at,
            send_sem=b_out_send.at[slot],
            recv_sem=rest_recv,
            device_id={"section": other},
            device_id_type=MESH,
        ).start()

    def chain_copy(at, sems, slot, target):
        return pltpu.make_async_remote_copy(
            src_ref=at,
            dst_ref=at,
            send_sem=sems[0].at[slot],
            recv_sem=sems[1].at[slot],
            device_id={"ctx": target},
            device_id_type=MESH,
        )

    class Gates:
        hand_out = staticmethod(a_hand_out)

        @staticmethod
        def view(buffer, k):
            return a_at(buffer, k)

        own, sums, done = a_own, a_sum, a_done
        up, back = (a_up_send, a_up_recv), (a_back_send, a_back_recv)

        @staticmethod
        def term(k):
            slot = k
            at = a_at(a_own, k)
            pltpu.make_async_copy(at, at, own_sem.at[slot]).wait()
            pltpu.make_async_copy(at, at, pair_recv.at[slot]).wait()
            return at[...].astype(F32) + a_at(a_other, k)[...].astype(F32)

    class Downs:
        @staticmethod
        def hand_out(k):
            down_hand_out(k, 0)

        @staticmethod
        def view(buffer, k):
            return b_at(buffer, k)

        own, sums, done = b_own, b_sum, b_done
        up, back = (b_up_send, b_up_recv), (b_back_send, b_back_recv)

        @staticmethod
        def term(k):
            slot = a_chunks + k
            at = b_at(b_own, k)
            pltpu.make_async_copy(at, at, own_sem.at[slot]).wait()
            pltpu.make_async_copy(at, at, pair_recv.at[slot]).wait()
            return at[...].astype(F32) + b_at(b_other, k)[...].astype(F32)

    class Seconds(Downs):
        @staticmethod
        def hand_out(k):
            down_hand_out(k, 1)

        @staticmethod
        def term(k):
            at = b_at(b_own, k)
            pltpu.make_async_copy(at, at, own_sem.at[a_chunks + k]).wait()
            return at[...].astype(F32)

    class Mixed(Downs):
        hand_out = staticmethod(mix_hand_out)

        @staticmethod
        def term(k):
            return b_at(b_own, k)[...].astype(F32)

    def upward(item, k, rank, ahead, behind):
        slot = k
        term = item.term(k)
        sums = item.view(item.sums, k)

        @pl.when(rank == 0)
        def _():
            sums[...] = term.astype(BF16)

        @pl.when(rank > 0)
        def _():
            chain_copy(sums, item.up, slot, behind).wait_recv()

        @pl.when((rank > 0) & (rank < n_ctx - 1))
        def _():
            sums[...] = (term + sums[...].astype(F32)).astype(BF16)

        @pl.when(rank < n_ctx - 1)
        def _():
            chain_copy(sums, item.up, slot, ahead).start()

        @pl.when(rank == n_ctx - 1)
        def _():
            done = item.view(item.done, k)
            done[...] = (term + sums[...].astype(F32)).astype(BF16)
            chain_copy(done, item.back, slot, behind).start()
            item.hand_out(k)

    def backward(item, k, rank, ahead, behind):
        slot = k
        done = item.view(item.done, k)
        chain_copy(done, item.back, slot, ahead).wait_recv()

        @pl.when(rank > 0)
        def _():
            chain_copy(done, item.back, slot, behind).start()

        item.hand_out(k)

    def on_step(action, step, active, way, *where):
        @pl.when(active & (step < paired))
        def _():
            at = jnp.clip(step, 0, paired - 1)
            action(Gates, 2 * at + way, *where)

            @pl.when(lax.rem(3 * at, 8) < 3)
            def _():
                action(Downs, 2 * (3 * at // 8) + way, *where)

        @pl.when(active & (step >= paired) & (step < second))
        def _():
            at = jnp.clip(step - paired, 0, down_chunks // 2 - 1)
            action(Seconds, down_chunks + 2 * at + way, *where)

        @pl.when(active & (step >= second))
        def _():
            at = jnp.clip(step - second, 0, mix_chunks // 2 - 1)
            action(Mixed, mix_start + 2 * at + way, *where)

    lanes = []
    for way in range(2):
        rank = place if way == 0 else n_ctx - 1 - place
        ahead = place + 1 if way == 0 else place - 1
        behind = place - 1 if way == 0 else place + 1
        lanes.append((way, rank, ahead, behind))

    def tick_step(tick, carry):
        for part, start in ((0, 1), (1, 5)):
            for owner in range(n_fsdp):

                @pl.when(tick == start + owner)
                def _(part=part, owner=owner):
                    mixer_sum(part, owner)

        events = (
            (4, mixer_out, 0),
            (8, mixer_out, 1),
            (10, mixer_on, 0),
            (15, mixer_on, 1),
            (second - 1, mixer_in, 0),
            (second + 3, mixer_in, 1),
        )
        for moment, action, part in events:

            @pl.when(tick == moment)
            def _(action=action, part=part):
                action(part)

        for way, rank, ahead, behind in lanes:
            step = tick - 2 * rank
            on_step(upward, step, (step >= 0) & (step < ticks), way, rank, ahead, behind)
            late = tick - 2 * (tail - rank)
            on_step(
                backward,
                late,
                (late >= 0) & (late < ticks) & (rank < n_ctx - 1),
                way,
                rank,
                ahead,
                behind,
            )

        return carry

    second_start()
    lax.fori_loop(0, ticks + 2 * tail, tick_step, 0)

    for part in range(2):
        for copy in c_pair[part]:
            copy.wait_send()
        opening, onward = mixer_copies(part)
        for copy in opening + onward:
            copy.wait_send()

    def settle_item(item, k, rank, ahead, behind, out_send):
        @pl.when(rank < n_ctx - 1)
        def _():
            chain_copy(item.view(item.sums, k), item.up, k, ahead).wait_send()

        @pl.when(rank > 0)
        def _():
            chain_copy(item.view(item.done, k), item.back, k, behind).wait_send()

        ref = item.view(item.own, k)
        pltpu.make_async_copy(ref, ref, out_send.at[k]).wait()

    def settle_gates(index, carry):
        for way, rank, ahead, behind in lanes:
            k = 2 * index + way
            settle_item(Gates, k, rank, ahead, behind, a_out_send)
            ref = a_own.at[k]
            pltpu.make_async_copy(ref, ref, pair_send.at[k]).wait()
        return carry

    lax.fori_loop(0, a_chunks // 2, settle_gates, 0)

    def settle_rest(index, carry):
        for way, rank, ahead, behind in lanes:
            k = 2 * index + way
            settle_item(Mixed, k, rank, ahead, behind, b_out_send)
            ref = b_own.at[k]

            @pl.when(k < down_chunks)
            def _(ref=ref, k=k):
                pltpu.make_async_copy(ref, ref, pair_send.at[a_chunks + k]).wait()

            @pl.when(k >= mix_start)
            def _(ref=ref, k=k):
                pltpu.make_async_copy(ref, ref, b_keep_sem.at[k]).wait()

        return carry

    lax.fori_loop(0, b_chunks // 2, settle_rest, 0)
    pltpu.make_async_copy(second_gu_in, second_gu_in, second_send.at[0]).wait()

    for kind in range(2):
        for source in range(2 * n_fsdp):

            @pl.when(section * n_fsdp + group != source)
            def _(kind=kind, source=source):
                region = gu_out.at[
                    kind,
                    pl.ds((source // n_fsdp) * half, half),
                    pl.ds((source % n_fsdp) * a_width, a_width),
                ]
                pltpu.make_async_copy(region, region, gu_recv.at[kind, source]).wait()

    region = down_out.at[pl.ds(pl.multiple_of(other * down_half, b_rows), down_half)]
    pltpu.make_async_copy(region, region, down_recv).wait()
    region = rest_out.at[other]
    pltpu.make_async_copy(region, region, rest_recv).wait()


def summed_gradients(first, mixers, small, second_gu, second_down):
    n_ctx, n_fsdp = lax.axis_size("ctx"), lax.axis_size("fsdp")
    gate, up, down = first
    half = gate.shape[0] // n_fsdp // 2
    a_rows, b_rows = half // 4, half * 3 // 8
    a_chunks = 2 * n_fsdp * 4
    a_width, b_width = gate.shape[1], down.shape[1]
    c_rows = len(mixers) * half + small.shape[1]
    down_chunks = down.shape[0] // 2 // b_rows
    b_chunks = 2 * down_chunks + c_rows // b_rows + 1
    assert c_rows % b_rows == 0 and b_chunks % 2 == 0 and down_chunks % 2 == 0
    assert down_chunks * 8 == a_chunks * 3
    rest = b_chunks - 2 * down_chunks
    dma = pltpu.SemaphoreType.DMA
    loads = a_chunks + 2 * down_chunks
    pieces = n_fsdp * (len(mixers) + 1)
    return pl.pallas_call(
        functools.partial(tail_kernel, (n_ctx, n_fsdp)),
        out_shape=(
            jax.ShapeDtypeStruct((2, 2 * half, n_fsdp * a_width), BF16),
            jax.ShapeDtypeStruct(down.shape, BF16),
            jax.ShapeDtypeStruct((2, rest * b_rows, b_width), BF16),
        ),
        in_specs=[pl.BlockSpec(memory_space=pl.ANY)] * (6 + len(mixers)),
        out_specs=[pl.BlockSpec(memory_space=pl.ANY)] * 3,
        scratch_shapes=[
            pltpu.VMEM((a_chunks, a_rows, a_width), BF16),
            pltpu.VMEM((a_chunks, a_rows, a_width), BF16),
            pltpu.VMEM((a_chunks, a_rows, a_width), BF16),
            pltpu.VMEM((a_chunks, a_rows, a_width), BF16),
            pltpu.VMEM((b_chunks, b_rows, b_width), BF16),
            pltpu.VMEM((down_chunks, b_rows, b_width), BF16),
            pltpu.VMEM((b_chunks, b_rows, b_width), BF16),
            pltpu.VMEM((b_chunks, b_rows, b_width), BF16),
            pltpu.VMEM((n_fsdp, c_rows, b_width), BF16),
            pltpu.VMEM((n_fsdp, c_rows, b_width), BF16),
            pltpu.VMEM((n_fsdp - 1, c_rows, b_width), BF16),
            dma((loads,)),
            dma((loads,)),
            dma((loads,)),
            dma((pieces,)),
            dma((pieces,)),
            dma((pieces,)),
            dma((2, 6)),
            dma((2, 6)),
            dma((a_chunks,)),
            dma((a_chunks,)),
            dma((a_chunks,)),
            dma((a_chunks,)),
            dma((a_chunks,)),
            dma((b_chunks,)),
            dma((b_chunks,)),
            dma((b_chunks,)),
            dma((b_chunks,)),
            dma((b_chunks,)),
            dma((b_chunks,)),
            dma((2, 2 * n_fsdp)),
            dma,
            dma,
            dma((2,)),
        ],
        compiler_params=pltpu.CompilerParams(
            collective_id=6, has_side_effects=True, vmem_limit_bytes=56 << 20
        ),
        cost_estimate=busy(160),
    )(gate, up, down, *mixers, small, second_gu, second_down)


class Columns:
    def __init__(self, holder, sources, targets, send_sem, recv_sem, pair_send, pair_recv, own_sem):
        self.count = 4
        self.holder = holder
        self.section = lax.axis_index("section")
        self.me = lax.axis_index("fsdp")
        self.sources, self.targets = sources, targets
        self.sems = send_sem, recv_sem, pair_send, pair_recv, own_sem
        self.rows = sources[0].shape[0]
        self.wide = targets[0].shape[1]
        self.steps = [(step, kind) for step in range(1, self.count) for kind in range(2)]

    def at_rows(self, out, owner):
        return out.at[pl.ds(pl.multiple_of(owner * self.rows, self.rows), self.rows)]

    def at_columns(self, source, owner):
        return source.at[:, pl.ds(pl.multiple_of(owner * self.wide, 128), self.wide)]

    def crossing(self, step, kind):
        target = lax.rem(self.me + step, self.count)
        return to_side(
            self.at_columns(self.sources[kind], target),
            self.at_rows(self.targets[kind], self.me),
            self.sems[0].at[kind, step],
            self.sems[1].at[kind, step],
            target,
        )

    def handed(self, step, kind):
        if kind == 2:
            src, dst = self.sources[2], self.targets[2]
        else:
            origin = lax.rem(self.me + self.count - step, self.count)
            dst = self.at_rows(self.targets[kind], origin)
            src = self.at_columns(self.sources[kind], self.me) if step == 0 else dst
        return pltpu.make_async_remote_copy(
            src_ref=src,
            dst_ref=dst,
            send_sem=self.sems[2].at[kind, step],
            recv_sem=self.sems[3].at[kind, step],
            device_id={"section": 1 - self.section},
            device_id_type=MESH,
        )

    def kept(self, kind):
        if kind == 2:
            return pltpu.make_async_copy(self.sources[2], self.targets[2], self.sems[4].at[2])
        return pltpu.make_async_copy(
            self.at_columns(self.sources[kind], self.me),
            self.at_rows(self.targets[kind], self.me),
            self.sems[4].at[kind],
        )

    def start(self):
        @pl.when(self.section == self.holder)
        def _():
            for step, kind in self.steps:
                self.crossing(step, kind).start()
            for kind in range(3):
                self.handed(0, kind).start()
            for kind in range(3):
                self.kept(kind).start()

    def relay(self):
        @pl.when(self.section == self.holder)
        def _():
            for step, kind in self.steps:
                self.crossing(step, kind).wait_recv()
                self.handed(step, kind).start()

    def arrive(self):
        every = [(0, kind) for kind in range(3)] + self.steps

        @pl.when(self.section == self.holder)
        def _():
            for kind in range(3):
                self.kept(kind).wait()

        @pl.when(self.section != self.holder)
        def _():
            for step, kind in every:
                self.handed(step, kind).wait_recv()

    def finish(self):
        every = [(0, kind) for kind in range(3)] + self.steps

        @pl.when(self.section == self.holder)
        def _():
            for step, kind in self.steps:
                self.crossing(step, kind).wait_send()
            for step, kind in every:
                self.handed(step, kind).wait_send()


class SharedColumns(Columns):
    def __init__(self, *args):
        *args, plane_send, plane_recv = args
        super().__init__(*args)
        self.plane = plane_send, plane_recv
        place = lax.axis_index("ctx")
        self.odd = lax.rem(place, 2)
        self.partner = place + 1 - 2 * self.odd

    def passed_on(self, step, kind):
        at = self.at_rows(self.targets[kind], lax.rem(self.me + self.count - step, self.count))
        return pltpu.make_async_remote_copy(
            src_ref=at,
            dst_ref=at,
            send_sem=self.plane[0].at[kind, step],
            recv_sem=self.plane[1].at[kind, step],
            device_id={"ctx": self.partner},
            device_id_type=MESH,
        )

    def by_kind(self, action):
        for kind in range(2):

            @pl.when((self.section == self.holder) & (self.odd == kind))
            def _(kind=kind):
                for step in range(1, self.count):
                    action(step, kind)

    def start(self):
        self.by_kind(lambda step, kind: self.crossing(step, kind).start())

        @pl.when(self.section == self.holder)
        def _():
            for kind in range(3):
                self.handed(0, kind).start()
            for kind in range(3):
                self.kept(kind).start()

    def relay(self):
        def moved(step, kind):
            self.crossing(step, kind).wait_recv()
            self.passed_on(step, kind).start()
            self.handed(step, kind).start()

        self.by_kind(moved)

    def relay_passed(self):
        def passed(step, kind):
            self.passed_on(step, 1 - kind).wait_recv()
            self.handed(step, 1 - kind).start()

        self.by_kind(passed)

    def finish(self):
        def sent(step, kind):
            self.crossing(step, kind).wait_send()
            self.passed_on(step, kind).wait_send()

        self.by_kind(sent)
        every = [(0, kind) for kind in range(3)] + self.steps

        @pl.when(self.section == self.holder)
        def _():
            for step, kind in every:
                self.handed(step, kind).wait_send()


class Chain:
    def __init__(self, count):
        self.count = count
        self.place = lax.axis_index("ctx")
        self.has_next = self.place < count - 1
        self.has_last = self.place > 0


def greet_mixed(chain, targets):
    barrier = pltpu.get_barrier_semaphore()
    for target in targets:
        pl.semaphore_signal(barrier, inc=1, device_id=target, device_id_type=MESH)

    @pl.when(chain.has_last)
    def _():
        pl.semaphore_signal(barrier, inc=1, device_id={"ctx": chain.place - 1}, device_id_type=MESH)

    @pl.when(chain.has_next)
    def _():
        pl.semaphore_signal(barrier, inc=1, device_id={"ctx": chain.place + 1}, device_id_type=MESH)

    inner = chain.has_last & chain.has_next

    @pl.when(inner)
    def _():
        pl.semaphore_wait(barrier, len(targets) + 2)

    @pl.when(jnp.logical_not(inner))
    def _():
        pl.semaphore_wait(barrier, len(targets) + 1)


def along(src, dst, send_sem, recv_sem, place):
    return pltpu.make_async_remote_copy(
        src_ref=src,
        dst_ref=dst,
        send_sem=send_sem,
        recv_sem=recv_sem,
        device_id={"ctx": place},
        device_id_type=MESH,
    )


def spread_heads(source, spread):
    rows = source.shape[0]
    low = lax.broadcasted_iota(jnp.int32, (rows, 128), 1) < 64
    for pair in range(source.shape[1] // 256):
        first = source[:, pair * 256 : pair * 256 + 128].astype(F32)
        second = source[:, pair * 256 + 128 : pair * 256 + 256].astype(F32)
        spread[4 * pair] = jnp.where(low, first, 0.0).astype(BF16)
        spread[4 * pair + 1] = jnp.where(low, pltpu.roll(first, 64, 1), 0.0).astype(BF16)
        spread[4 * pair + 2] = jnp.where(low, 0.0, pltpu.roll(second, 64, 1)).astype(BF16)
        spread[4 * pair + 3] = jnp.where(low, 0.0, second).astype(BF16)


def join_heads(spread, target):
    rows = target.shape[0]
    low = lax.broadcasted_iota(jnp.int32, (rows, 128), 1) < 64
    for pair in range(target.shape[1] // 256):
        parts = [spread(4 * pair + i).T for i in range(4)]
        target[:, pair * 256 : pair * 256 + 128] = jnp.where(low, parts[0], pltpu.roll(parts[1], 64, 1))
        target[:, pair * 256 + 128 : pair * 256 + 256] = jnp.where(low, pltpu.roll(parts[2], 64, 1), parts[3])


def mask_block(bias, length, place, block):
    rows = bias.shape[0]
    key_at = block * rows + lax.broadcasted_iota(jnp.int32, bias.shape, 0)
    query_at = place * rows + lax.broadcasted_iota(jnp.int32, bias.shape, 1)
    bias[...] = jnp.where((key_at <= query_at) & (key_at < length), 0.0, NEGATIVE)


def dot_right(left, right):
    return lax.dot_general(left, right, (((1,), (1,)), ((), ())), preferred_element_type=F32)


def dot_plain(left, right):
    return jnp.dot(left, right, preferred_element_type=F32)


def attend_kernel(
    n_ctx,
    length_ref,
    query,
    kv,
    d_block,
    gate_in,
    up_in,
    down_in,
    attended,
    log_total,
    kv_all,
    d_all,
    gate_out,
    up_out,
    down_out,
    w_gate,
    w_up,
    w_down,
    keep_sem,
    spread,
    bias,
    peak,
    total,
    out_t,
    kv_send,
    kv_recv,
    d_send,
    d_recv,
    d_own,
    send_sem,
    recv_sem,
    pair_send,
    pair_recv,
    own_sem,
):
    chain = Chain(n_ctx)
    place = chain.place
    section = lax.axis_index("section")
    me, beside, across, opposite = corners()
    greet_mixed(
        chain,
        [{"fsdp": beside}, {"fsdp": across}, {"fsdp": opposite}, {"section": 1 - section}],
    )
    rows = query.shape[0]
    half_width = kv.shape[1] // 2

    def block_rows(block):
        return pl.ds(pl.multiple_of(block * rows, rows), rows)

    def upward(step, src):
        return along(
            src,
            kv_all.at[block_rows(place - step)],
            kv_send.at[step],
            kv_recv.at[step + 1],
            place + 1,
        )

    def arriving(step):
        at = kv_all.at[block_rows(place - step)]
        return along(at, at, kv_send.at[step], kv_recv.at[step], place)

    @pl.when(chain.has_next)
    def _():
        upward(0, kv).start()

    gather = SideGather(d_block, d_all, d_send, d_recv, d_own)
    gather.start()
    columns = Columns(
        1, (gate_in, up_in, down_in), (w_gate, w_up, w_down), send_sem, recv_sem, pair_send, pair_recv, own_sem
    )
    columns.start()
    kv_all[block_rows(place)] = kv[...]
    spread_heads(query, spread)
    peak[...] = jnp.full(peak.shape, NEGATIVE, F32)
    total[...] = jnp.zeros(total.shape, F32)
    out_t[...] = jnp.zeros(out_t.shape, F32)
    length = length_ref[0]
    scale = 64 ** (-0.5)

    def attend_block(block):
        mask_block(bias, length, place, block)
        for pair in range(half_width // 128):
            key = kv_all[block_rows(block), pair * 128 : pair * 128 + 128]
            value_t = kv_all[block_rows(block), half_width + pair * 128 : half_width + pair * 128 + 128].T
            for index in range(4):
                head = 4 * pair + index
                scores = dot_right(key, spread[head]) * scale + bias[...]
                before = peak[head]
                now = jnp.maximum(before, jnp.max(scores, axis=0, keepdims=True))
                weights = jnp.exp(scores - now)
                fade = jnp.exp(before - now)
                peak[head] = now
                total[head] = total[head] * fade + jnp.sum(weights, axis=0, keepdims=True)
                out_t[head] = out_t[head] * fade + dot_plain(value_t, weights.astype(BF16))

    attend_block(place)
    gather.relay()

    def step_on(step, carry):
        @pl.when(step <= place)
        def _():
            arriving(step).wait_recv()

            @pl.when(chain.has_next)
            def _():
                upward(step, kv_all.at[block_rows(place - step)]).start()

            attend_block(place - step)

        return carry

    lax.fori_loop(1, n_ctx, step_on, 0)
    join_heads(lambda head: out_t[head] / total[head], attended)
    for head in range(spread.shape[0]):
        log_total[head] = peak[head] + jnp.log(total[head])
    columns.relay()
    columns.arrive()
    keeping = [
        pltpu.make_async_copy(src, dst, keep_sem.at[index])
        for index, (src, dst) in enumerate(((w_gate, gate_out), (w_up, up_out), (w_down, down_out)))
    ]
    for copy in keeping:
        copy.start()
    gather.finish()
    columns.finish()
    for copy in keeping:
        copy.wait()

    def settle(step, carry):
        @pl.when((step <= place) & chain.has_next)
        def _():
            upward(step, kv_all.at[block_rows(place - step)]).wait_send()

        return carry

    lax.fori_loop(0, n_ctx, settle, 0)


def attend(length, query, kv, d_block, gate, up, down, collective_id):
    n_ctx, count = lax.axis_size("ctx"), lax.axis_size("fsdp")
    rows, width = query.shape
    heads = width // 64
    dma = pltpu.SemaphoreType.DMA
    vmem = pl.BlockSpec(memory_space=pltpu.VMEM)
    hbm = pl.BlockSpec(memory_space=pl.ANY)
    column = jax.ShapeDtypeStruct((count * gate.shape[0], gate.shape[1] // count), gate.dtype)
    return pl.pallas_call(
        functools.partial(attend_kernel, n_ctx),
        out_shape=(
            jax.ShapeDtypeStruct((rows, width), F32),
            jax.ShapeDtypeStruct((heads, 1, rows), F32),
            jax.ShapeDtypeStruct((n_ctx * rows, kv.shape[1]), BF16),
            jax.ShapeDtypeStruct((count * rows, d_block.shape[1]), BF16),
            column,
            column,
            jax.ShapeDtypeStruct(down.shape, down.dtype),
        ),
        in_specs=[pl.BlockSpec(memory_space=pltpu.SMEM), vmem, vmem, vmem, hbm, hbm, hbm],
        out_specs=[vmem, vmem, vmem, vmem, hbm, hbm, hbm],
        scratch_shapes=[
            pltpu.VMEM(column.shape, BF16),
            pltpu.VMEM(column.shape, BF16),
            pltpu.VMEM(down.shape, BF16),
            dma((3,)),
            pltpu.VMEM((heads, rows, 128), BF16),
            pltpu.VMEM((rows, rows), F32),
            pltpu.VMEM((heads, 1, rows), F32),
            pltpu.VMEM((heads, 1, rows), F32),
            pltpu.VMEM((heads, 128, rows), F32),
            dma((n_ctx + 1,)),
            dma((n_ctx + 1,)),
            dma((4,)),
            dma((4,)),
            dma,
            dma((2, count)),
            dma((2, count)),
            dma((3, count)),
            dma((3, count)),
            dma((3,)),
        ],
        compiler_params=pltpu.CompilerParams(
            collective_id=collective_id, has_side_effects=True, vmem_limit_bytes=58 << 20
        ),
        cost_estimate=busy(50),
    )(length, query, kv, d_block, gate, up, down)


def attend_back_kernel(
    n_ctx,
    length_ref,
    query,
    kv_all,
    d_out,
    log_total,
    delta,
    blocks,
    d_query,
    d_kv,
    reduced_out,
    spread,
    d_spread,
    bias,
    d_query_t,
    term,
    leaving,
    coming,
    kv_send,
    kv_recv,
    beside_got,
    across_got,
    passed,
    passed_got,
    send_sem,
    recv_sem,
):
    chain = Chain(n_ctx)
    place = chain.place
    _, beside, across, _ = corners()
    greet_mixed(chain, [{"fsdp": beside}, {"fsdp": across}])
    rows = query.shape[0]
    half_width = kv_all.shape[1] // 2
    reduction = SideReduce(blocks, reduced_out, beside_got, across_got, passed, passed_got, send_sem, recv_sem)
    reduction.start()
    spread_heads(query, spread)
    spread_heads(d_out, d_spread)
    d_query_t[...] = jnp.zeros(d_query_t.shape, F32)
    length = length_ref[0]
    scale = 64 ** (-0.5)

    def downward(block):
        return along(leaving.at[block], coming.at[block], kv_send.at[block], kv_recv.at[block], place - 1)

    def step_on(block, carry):
        @pl.when(block <= place)
        def _():
            mask_block(bias, length, place, block)
            at = pl.ds(pl.multiple_of(block * rows, rows), rows)
            for pair in range(half_width // 128):
                lanes = slice(pair * 128, pair * 128 + 128)
                more = slice(half_width + pair * 128, half_width + pair * 128 + 128)
                key = kv_all[at, lanes]
                value = kv_all[at, more]
                key_t = key.T
                d_key = jnp.zeros((rows, 128), F32)
                d_value = jnp.zeros((rows, 128), F32)
                for index in range(4):
                    head = 4 * pair + index
                    scores = dot_right(key, spread[head]) * scale + bias[...]
                    prob = jnp.exp(scores - log_total[head])
                    d_prob = dot_right(value, d_spread[head])
                    d_scores = (prob * (d_prob - delta[head])).astype(BF16)
                    d_value = d_value + dot_plain(prob.astype(BF16), d_spread[head])
                    d_key = d_key + dot_plain(d_scores, spread[head])
                    d_query_t[head] = d_query_t[head] + dot_plain(key_t, d_scores)
                term[:, lanes] = d_key * scale
                term[:, more] = d_value

            @pl.when(chain.has_next)
            def _():
                along(
                    leaving.at[block], coming.at[block], kv_send.at[block], kv_recv.at[block], place
                ).wait_recv()
                term[...] = term[...] + coming[block].astype(F32)

            @pl.when(block < place)
            def _():
                leaving[block] = term[...].astype(BF16)
                downward(block).start()

            @pl.when(block == place)
            def _():
                d_kv[...] = term[...]

        @pl.when(block == 0)
        def _():
            reduction.relay()

        return carry

    lax.fori_loop(0, n_ctx, step_on, 0)
    join_heads(lambda head: d_query_t[head] * scale, d_query)
    reduction.finish()

    def settle(block, carry):
        @pl.when(block < place)
        def _():
            downward(block).wait_send()

        return carry

    lax.fori_loop(0, n_ctx, settle, 0)


def attend_back(length, query, kv_all, d_out, log_total, delta, blocks, collective_id):
    n_ctx = lax.axis_size("ctx")
    rows, width = query.shape
    heads = width // 64
    dma = pltpu.SemaphoreType.DMA
    vmem = pl.BlockSpec(memory_space=pltpu.VMEM)
    wide = jax.ShapeDtypeStruct((rows, width), F32)
    pair = pltpu.VMEM((2, rows // 2, blocks.shape[1]), BF16)
    return pl.pallas_call(
        functools.partial(attend_back_kernel, n_ctx),
        out_shape=(wide, jax.ShapeDtypeStruct((rows, kv_all.shape[1]), F32), wide),
        in_specs=[pl.BlockSpec(memory_space=pltpu.SMEM)] + [vmem] * 6,
        out_specs=[vmem] * 3,
        scratch_shapes=[
            pltpu.VMEM((heads, rows, 128), BF16),
            pltpu.VMEM((heads, rows, 128), BF16),
            pltpu.VMEM((rows, rows), F32),
            pltpu.VMEM((heads, 128, rows), F32),
            pltpu.VMEM((rows, kv_all.shape[1]), F32),
            pltpu.VMEM((n_ctx, rows, kv_all.shape[1]), BF16),
            pltpu.VMEM((n_ctx, rows, kv_all.shape[1]), BF16),
            dma((n_ctx,)),
            dma((n_ctx,)),
            pair,
            pair,
            pair,
            pair,
            dma((6,)),
            dma((6,)),
        ],
        compiler_params=pltpu.CompilerParams(
            collective_id=collective_id, has_side_effects=True, vmem_limit_bytes=56 << 20
        ),
        cost_estimate=busy(50),
    )(length, query, kv_all, d_out, log_total, delta, blocks)


class MixerGather:
    def __init__(self, sources, targets, send_sem, recv_sem, pair_send, pair_recv, own_sem):
        self.section = section = lax.axis_index("section")
        me, beside, across, opposite = corners()
        rows = sources[0].shape[0]
        half = rows // 2
        quarter = half // 2

        def at_rows(out, owner, extra, size):
            return out.at[pl.ds(pl.multiple_of(owner * rows + extra, quarter), size)]

        def pair(slot, at):
            return pltpu.make_async_remote_copy(
                src_ref=at,
                dst_ref=at,
                send_sem=pair_send.at[slot],
                recv_sem=pair_recv.at[slot],
                device_id={"section": 1 - section},
                device_id_type=MESH,
            )

        self.direct, self.onward, self.early, self.late, self.own = [], [], [], [], []
        start = section * half
        for index, (source, out) in enumerate(zip(sources, targets)):
            mine = source.at[pl.ds(pl.multiple_of(start, half), half)]
            spot = at_rows(out, me, start, half)
            slot = 4 * index
            self.direct.append(
                [
                    to_side(mine, spot, send_sem.at[slot], recv_sem.at[slot], beside),
                    to_side(mine, spot, send_sem.at[slot + 1], recv_sem.at[slot + 1], across),
                ]
            )
            passing = at_rows(out, beside, start, quarter), at_rows(out, across, start + quarter, quarter)
            self.onward.append(
                [
                    to_side(passing[0], passing[0], send_sem.at[slot + 2], recv_sem.at[slot + 2], across),
                    to_side(passing[1], passing[1], send_sem.at[slot + 3], recv_sem.at[slot + 3], beside),
                ]
            )
            self.early.append(
                [
                    pair(slot, at_rows(out, beside, start, half)),
                    pair(slot + 1, at_rows(out, across, start, half)),
                ]
            )
            self.late.append(
                [
                    pair(slot + 2, at_rows(out, opposite, start, quarter)),
                    pair(slot + 3, at_rows(out, opposite, start + quarter, quarter)),
                ]
            )
            self.own.append(pltpu.make_async_copy(source, at_rows(out, me, 0, rows), own_sem.at[index]))

    def start(self):
        for copies in self.direct:
            for copy in copies:
                copy.start()
        for copy in self.own:
            copy.start()

    def relay(self):
        for direct, onward, early in zip(self.direct, self.onward, self.early):
            for turn in range(2):
                direct[turn].wait_recv()
                onward[turn].start()
                early[turn].start()

    def relay_last(self):
        for onward, late in zip(self.onward, self.late):
            for turn in range(2):
                onward[turn].wait_recv()
                late[turn].start()

    def arrive(self, index):
        self.own[index].wait()
        for copy in self.early[index] + self.late[index]:
            copy.wait_recv()

    def finish(self):
        for group in (self.direct, self.onward, self.early, self.late):
            for copies in group:
                for copy in copies:
                    copy.wait_send()


def front_kernel(
    n_ctx,
    x_ref,
    gains,
    taps,
    conv_in,
    conv_out,
    gate_in,
    up_in,
    down_in,
    in_out,
    out_out,
    gate_out,
    up_out,
    down_out,
    projected,
    convolved,
    z_low,
    mixed,
    rim,
    act_all,
    w_in,
    w_out,
    w_gate,
    w_up,
    w_down,
    act1,
    act2,
    last_rows,
    rim_sem,
    mix_send,
    mix_recv,
    mix_pair_send,
    mix_pair_recv,
    mix_own,
    send_sem,
    recv_sem,
    pair_send,
    pair_recv,
    own_sem,
    plane_send,
    plane_recv,
    act_send,
    act_recv,
    act_own,
    keep_sem,
):
    chain = Chain(n_ctx)
    section = lax.axis_index("section")
    _, beside, across, opposite = corners()
    greet_mixed(
        chain,
        [{"fsdp": beside}, {"fsdp": across}, {"fsdp": opposite}, {"section": 1 - section}],
    )
    mixers = MixerGather(
        (conv_in, conv_out), (w_in, w_out), mix_send, mix_recv, mix_pair_send, mix_pair_recv, mix_own
    )
    mixers.start()
    columns = SharedColumns(
        0,
        (gate_in, up_in, down_in),
        (w_gate, w_up, w_down),
        send_sem,
        recv_sem,
        pair_send,
        pair_recv,
        own_sem,
        plane_send,
        plane_recv,
    )
    gather = SideGather(act2, act_all, act_send, act_recv, act_own)
    keeping = [
        pltpu.make_async_copy(src, dst, keep_sem.at[index])
        for index, (src, dst) in enumerate(
            ((w_in, in_out), (w_out, out_out), (w_gate, gate_out), (w_up, up_out), (w_down, down_out))
        )
    ]
    rows, width = x_ref.shape
    strip = 64

    def normalize(values, gain):
        inv_rms = lax.rsqrt(jnp.mean(values * values, axis=-1, keepdims=True) + EPSILON)
        return (values * inv_rms * gain).astype(BF16)

    def first_norm(index, carry):
        at = pl.ds(pl.multiple_of(index * strip, strip), strip)
        act1[at] = normalize(x_ref[at].astype(F32), gains[0:1])
        return carry

    lax.fori_loop(0, rows // strip, first_norm, 0)
    mixers.relay()
    columns.start()
    mixers.relay_last()
    mixers.arrive(0)
    keeping[0].start()
    wide = 512

    def project(index, carry):
        at = pl.ds(pl.multiple_of(index * wide, wide), wide)
        projected[:, at] = dot_plain(act1[...], w_in[:, at])
        return carry

    lax.fori_loop(0, projected.shape[1] // wide, project, 0)
    tail_at = pl.ds(rows - 16, 16)
    last_rows[...] = (projected[tail_at, :width] * projected[tail_at, 2 * width :]).astype(BF16)
    to_next = along(last_rows, rim, rim_sem.at[0], rim_sem.at[1], chain.place + 1)

    @pl.when(chain.has_next)
    def _():
        to_next.start()

    @pl.when(chain.has_last)
    def _():
        along(last_rows, rim, rim_sem.at[0], rim_sem.at[1], chain.place).wait_recv()

    @pl.when(jnp.logical_not(chain.has_last))
    def _():
        rim[...] = jnp.zeros(rim.shape, BF16)

    part = 128
    row_at = lax.broadcasted_iota(jnp.int32, (rows, part), 0)

    def convolve(index, carry):
        def lanes(offset):
            return pl.ds(pl.multiple_of(offset * width + index * part, part), part)

        product = (projected[:, lanes(0)] * projected[:, lanes(2)]).astype(BF16).astype(F32)
        edge = rim[:, lanes(0)].astype(F32)
        near, far = edge[15:16], edge[14:15]
        one = jnp.where(row_at >= 1, pltpu.roll(product, 1, 0), near)
        two = jnp.where(row_at >= 2, pltpu.roll(product, 2, 0), jnp.where(row_at == 1, near, far))
        tap = taps[:, lanes(0)]
        value = tap[0:1] * two + tap[1:2] * one + tap[2:3] * product
        convolved[:, lanes(0)] = value
        z_low[:, lanes(0)] = (projected[:, lanes(1)] * value).astype(BF16)
        return carry

    lax.fori_loop(0, width // part, convolve, 0)
    mixers.arrive(1)
    keeping[1].start()

    def mix(index, carry):
        at = pl.ds(pl.multiple_of(index * wide, wide), wide)
        mixed[:, at] = dot_plain(z_low[...], w_out[:, at])
        return carry

    lax.fori_loop(0, width // wide, mix, 0)

    def second_norm(index, carry):
        at = pl.ds(pl.multiple_of(index * strip, strip), strip)
        act2[at] = normalize(x_ref[at].astype(F32) + mixed[at], gains[1:2])
        return carry

    lax.fori_loop(0, rows // strip, second_norm, 0)
    gather.start()
    columns.relay()
    gather.relay()
    columns.relay_passed()
    columns.arrive()
    for copy in keeping[2:]:
        copy.start()
    gather.finish()
    columns.finish()
    mixers.finish()

    @pl.when(chain.has_next)
    def _():
        to_next.wait_send()

    for copy in keeping:
        copy.wait()


def front(x_low, gains, taps, conv_in, conv_out, gate, up, down, collective_id):
    n_ctx, count = lax.axis_size("ctx"), lax.axis_size("fsdp")
    assert count == 4
    rows, width = x_low.shape
    dma = pltpu.SemaphoreType.DMA
    vmem = pl.BlockSpec(memory_space=pltpu.VMEM)
    hbm = pl.BlockSpec(memory_space=pl.ANY)

    def whole(weight):
        return (count * weight.shape[0], weight.shape[1])

    column = (count * gate.shape[0], gate.shape[1] // count)
    weights = [whole(conv_in), whole(conv_out), column, column, down.shape]
    return pl.pallas_call(
        functools.partial(front_kernel, n_ctx),
        out_shape=tuple(jax.ShapeDtypeStruct(shape, BF16) for shape in weights)
        + (
            jax.ShapeDtypeStruct((rows, conv_in.shape[1]), F32),
            jax.ShapeDtypeStruct((rows, width), F32),
            jax.ShapeDtypeStruct((rows, width), BF16),
            jax.ShapeDtypeStruct((rows, width), F32),
            jax.ShapeDtypeStruct((16, width), BF16),
            jax.ShapeDtypeStruct((count * rows, width), BF16),
        ),
        in_specs=[vmem] * 3 + [hbm] * 5,
        out_specs=[hbm] * 5 + [vmem] * 6,
        scratch_shapes=[pltpu.VMEM(shape, BF16) for shape in weights]
        + [
            pltpu.VMEM((rows, width), BF16),
            pltpu.VMEM((rows, width), BF16),
            pltpu.VMEM((16, width), BF16),
            dma((2,)),
            dma((8,)),
            dma((8,)),
            dma((8,)),
            dma((8,)),
            dma((2,)),
            dma((2, count)),
            dma((2, count)),
            dma((3, count)),
            dma((3, count)),
            dma((3,)),
            dma((2, count)),
            dma((2, count)),
            dma((4,)),
            dma((4,)),
            dma,
            dma((5,)),
        ],
        compiler_params=pltpu.CompilerParams(
            collective_id=collective_id, has_side_effects=True, vmem_limit_bytes=58 << 20
        ),
        cost_estimate=busy(70),
    )(x_low, gains, taps, conv_in, conv_out, gate, up, down)


def turn_kernel(
    act_block,
    w_gate_in,
    w_up_in,
    w_down_in,
    d_all_in,
    terms,
    total,
    shared_gu,
    shared_down,
    w_gate,
    w_up,
    w_down,
    d_all,
    load_sem,
    act,
    hidden,
    d_gate,
    d_up,
    blocks,
    act_send,
    act_recv,
    act_own,
    gu_all,
    gu_got,
    gu_sum,
    down_all,
    down_got,
    down_sum,
    keep_sem,
    beside_got,
    across_got,
    passed,
    passed_got,
    send_sem,
    recv_sem,
    pair_send,
    pair_recv,
):
    section = lax.axis_index("section")
    other = 1 - section
    _, beside, across, _ = corners()
    barrier = pltpu.get_barrier_semaphore()
    for target in ({"fsdp": beside}, {"fsdp": across}, {"section": other}):
        pl.semaphore_signal(barrier, inc=1, device_id=target, device_id_type=MESH)
    pl.semaphore_wait(barrier, 3)
    reduction = SideReduce(blocks, total, beside_got, across_got, passed, passed_got, send_sem, recv_sem)
    gather = SideGather(act_block, act, act_send, act_recv, act_own)
    gather.start()
    loads = [
        pltpu.make_async_copy(src, dst, load_sem.at[index])
        for index, (src, dst) in enumerate(
            ((w_gate_in, w_gate), (w_up_in, w_up), (d_all_in, d_all), (w_down_in, w_down))
        )
    ]
    for copy in loads:
        copy.start()
    me, _, _, opposite = corners()
    rows = act_block.shape[0]
    wide, width = w_down.shape
    lanes_wide, lanes_out = 384, 1024

    def turn(owner):
        at = pl.ds(pl.multiple_of(owner * rows, rows), rows)

        def hidden_part(index, carry):
            lanes = pl.ds(pl.multiple_of(index * lanes_wide, 128), lanes_wide)
            gate_pre = dot_plain(act[at], w_gate[:, lanes])
            up_pre = dot_plain(act[at], w_up[:, lanes])
            d_hidden = dot_right(d_all[at], w_down[lanes])
            sigmoid = jax.nn.sigmoid(gate_pre)
            silu = gate_pre * sigmoid
            hidden[at, lanes] = (silu * up_pre).astype(BF16)
            d_up[at, lanes] = (d_hidden * silu).astype(BF16)
            d_gate[at, lanes] = (
                d_hidden * up_pre * sigmoid * (1.0 + gate_pre * (1.0 - sigmoid))
            ).astype(BF16)
            return carry

        lax.fori_loop(0, wide // lanes_wide, hidden_part, 0)

        def out_part(index, carry):
            lanes = pl.ds(pl.multiple_of(index * lanes_out, 128), lanes_out)
            terms[at, lanes] = dot_plain(hidden[at], w_down[:, lanes]).astype(BF16)
            blocks[at, lanes] = (
                dot_right(d_gate[at], w_gate[lanes]) + dot_right(d_up[at], w_up[lanes])
            ).astype(BF16)
            return carry

        lax.fori_loop(0, width // lanes_out, out_part, 0)

    gather.own.wait()
    for copy in loads:
        copy.wait()
    turn(me)
    gather.relay()
    turn(beside)
    turn(across)
    reduction.copies[1].start()
    reduction.copies[3].start()
    gather.third.wait_recv()
    gather.fourth.wait_recv()
    turn(opposite)
    reduction.copies[0].start()
    reduction.copies[2].start()
    tile = 256
    half = gu_got.shape[2]
    strips, owners, kinds, strip, _ = gu_sum.shape

    def gate_swap(kind, owner):
        start = owner * (2 * half) + other * half
        return pltpu.make_async_remote_copy(
            src_ref=gu_all.at[kind, pl.ds(pl.multiple_of(start, half), half)],
            dst_ref=gu_got.at[kind, owner],
            send_sem=pair_send.at[kind * owners + owner],
            recv_sem=pair_recv.at[kind * owners + owner],
            device_id={"section": other},
            device_id_type=MESH,
        )

    for kind, right in enumerate((d_gate, d_up)):

        def column(owner, carry, kind=kind, right=right):
            lanes = pl.ds(pl.multiple_of(owner * tile, tile), tile)
            gu_all[kind, lanes] = dot_plain(act[:, lanes].T, right[...]).astype(BF16)
            gate_swap(kind, owner).start()
            return carry

        lax.fori_loop(0, owners, column, 0)
    reduction.relay()
    height = hidden.shape[1]

    def down_tile(index, carry):
        lanes = pl.ds(pl.multiple_of(index * tile, tile), tile)
        down_all[lanes] = dot_plain(hidden[:, lanes].T, d_all[...]).astype(BF16)
        return carry

    lax.fori_loop(0, height // tile, down_tile, 0)
    rest = height // tile * tile
    if rest < height:
        down_all[rest:] = dot_plain(hidden[:, rest:].T, d_all[...]).astype(BF16)
    down_half = height // 2
    down_swap = pltpu.make_async_remote_copy(
        src_ref=down_all.at[pl.ds(pl.multiple_of(other * down_half, 16), down_half)],
        dst_ref=down_got,
        send_sem=pair_send.at[kinds * owners],
        recv_sem=pair_recv.at[kinds * owners],
        device_id={"section": other},
        device_id_type=MESH,
    )
    down_swap.start()

    def join(index, carry):
        place = index // (owners * kinds)
        left = lax.rem(index, owners * kinds)
        owner, kind = left // kinds, lax.rem(left, kinds)

        @pl.when(place == 0)
        def _():
            gate_swap(kind, owner).wait_recv()

        mine = pl.ds(pl.multiple_of(owner * (2 * half) + section * half + place * strip, strip), strip)
        theirs = pl.ds(pl.multiple_of(place * strip, strip), strip)
        gu_sum[place, owner, kind] = (
            gu_all[kind, mine].astype(F32) + gu_got[kind, owner, theirs].astype(F32)
        ).astype(BF16)
        return carry

    lax.fori_loop(0, strips * owners * kinds, join, 0)
    keeping = [pltpu.make_async_copy(gu_sum, shared_gu, keep_sem.at[0])]
    keeping[0].start()
    down_swap.wait_recv()
    piece = 64

    def join_down(index, carry):
        theirs = pl.ds(pl.multiple_of(index * piece, piece), piece)
        mine = pl.ds(pl.multiple_of(section * down_half + index * piece, piece), piece)
        down_sum[theirs] = (down_all[mine].astype(F32) + down_got[theirs].astype(F32)).astype(BF16)
        return carry

    lax.fori_loop(0, down_half // piece, join_down, 0)
    keeping.append(pltpu.make_async_copy(down_sum, shared_down, keep_sem.at[1]))
    keeping[1].start()
    reduction.finish()

    def settle(index, carry):
        gate_swap(index // owners, lax.rem(index, owners)).wait_send()
        return carry

    lax.fori_loop(0, kinds * owners, settle, 0)
    down_swap.wait_send()
    for copy in (gather.first, gather.second, gather.third, gather.fourth):
        copy.wait_send()
    for copy in keeping:
        copy.wait()


def ffn_turn(act_block, w_gate, w_up, w_down, d_all, collective_id):
    n_ctx, owners = lax.axis_size("ctx"), lax.axis_size("fsdp")
    rows, width = act_block.shape
    wide = w_gate.shape[1]
    half = width // owners // 2
    dma = pltpu.SemaphoreType.DMA
    vmem = pl.BlockSpec(memory_space=pltpu.VMEM)
    hbm = pl.BlockSpec(memory_space=pl.ANY)
    pair = pltpu.VMEM((2, rows // 2, width), BF16)
    summed = (n_ctx, owners, 2, half // n_ctx, wide)
    assert width // owners == 256 and wide // 2 % 64 == 0 and wide % 384 == 0
    whole = (owners * rows, width)
    columns = pltpu.VMEM((owners * rows, wide), BF16)
    return pl.pallas_call(
        turn_kernel,
        out_shape=(
            jax.ShapeDtypeStruct(whole, BF16),
            jax.ShapeDtypeStruct((rows, width), F32),
            jax.ShapeDtypeStruct(summed, BF16),
            jax.ShapeDtypeStruct((wide // 2, width), BF16),
        ),
        in_specs=[vmem] + [hbm] * 4,
        out_specs=[vmem, vmem, hbm, hbm],
        scratch_shapes=[pltpu.VMEM(k.shape, BF16) for k in (w_gate, w_up, w_down, d_all)]
        + [
            dma((4,)),
            pltpu.VMEM(whole, BF16),
            columns,
            columns,
            columns,
            pltpu.VMEM(whole, BF16),
            dma((4,)),
            dma((4,)),
            dma,
            pltpu.VMEM((2, width, wide), BF16),
            pltpu.VMEM((2, owners, half, wide), BF16),
            pltpu.VMEM(summed, BF16),
            pltpu.VMEM((wide, width), BF16),
            pltpu.VMEM((wide // 2, width), BF16),
            pltpu.VMEM((wide // 2, width), BF16),
            dma((2,)),
            pair,
            pair,
            pair,
            pair,
            dma((6,)),
            dma((6,)),
            dma((2 * owners + 1,)),
            dma((2 * owners + 1,)),
        ],
        compiler_params=pltpu.CompilerParams(
            collective_id=collective_id, has_side_effects=True, vmem_limit_bytes=58 << 20
        ),
        cost_estimate=busy(45),
    )(act_block, w_gate, w_up, w_down, d_all)


def back_kernel(
    n_ctx,
    x_ref,
    mixed,
    d_h,
    gains,
    taps,
    z_low,
    rim,
    act_qkv,
    d_query,
    d_key_value,
    attended,
    d_attended,
    gate_pre_in,
    up_pre_in,
    w_down_in,
    w_gate_in,
    w_up_in,
    act_in,
    hidden_in,
    w_in_in,
    w_out_in,
    projected_in,
    convolved_in,
    gate_grad,
    up_grad,
    down_grad,
    q_grad,
    kv_grad,
    proj_grad,
    b_grad,
    c_grad,
    x_grad,
    o_grad,
    d_x,
    small,
    w_down,
    w_gate,
    w_up,
    act,
    hidden,
    w_in,
    w_out,
    projected,
    convolved,
    load_sem,
    pre,
    pre_sem,
    d_all,
    d_gate,
    d_up,
    blocks,
    d_send,
    d_recv,
    d_own,
    stage_wide,
    stage,
    stage_sem,
    beside_got,
    across_got,
    passed,
    passed_got,
    send_sem,
    recv_sem,
    d_act,
    d_res,
    d_mixed,
    d_conv,
    d_proj,
    act1,
    edge,
    next_edge,
    edge_sem,
):
    chain = Chain(n_ctx)
    me, beside, across, opposite = corners()
    greet_mixed(chain, [{"fsdp": beside}, {"fsdp": across}])
    gather = SideGather(d_h, d_all, d_send, d_recv, d_own)
    gather.start()
    reduction = SideReduce(blocks, d_act, beside_got, across_got, passed, passed_got, send_sem, recv_sem)

    def fetch(owner, slot):
        at = pl.ds(pl.multiple_of(owner * x_ref.shape[0], x_ref.shape[0]), x_ref.shape[0])
        return [
            pltpu.make_async_copy(source.at[at], pre.at[slot, kind], pre_sem.at[slot, kind])
            for kind, source in enumerate((gate_pre_in, up_pre_in))
        ]

    loads = [
        pltpu.make_async_copy(src, dst, load_sem.at[index])
        for index, (src, dst) in enumerate(
            (
                (w_down_in, w_down),
                (w_gate_in, w_gate),
                (w_up_in, w_up),
                (act_in, act),
                (hidden_in, hidden),
                (convolved_in, convolved),
                (projected_in, projected),
                (w_out_in, w_out),
                (w_in_in, w_in),
            )
        )
    ]
    for copy in fetch(me, 0) + loads[:3] + fetch(beside, 1) + loads[3:]:
        copy.start()
    rows, width = x_ref.shape
    wide = w_gate.shape[1]
    tile = 256
    small[...] = jnp.zeros(small.shape, F32)

    def weight_grad(left, right, at_right, target, staging, slot):
        count = left.shape[1] // tile

        def leaving(index, at):
            return pltpu.make_async_copy(staging.at[at], target.at[index], stage_sem.at[slot + at])

        def step(index, carry):
            at = lax.rem(index, 2)
            lanes = pl.ds(pl.multiple_of(index * tile, tile), tile)

            @pl.when(index >= 2)
            def _():
                leaving(lanes, at).wait()

            staging[at] = dot_plain(left[:, lanes].T, right[:, at_right]).astype(BF16)
            leaving(lanes, at).start()
            return carry

        lax.fori_loop(0, count, step, 0)
        for index in range(min(2, count)):
            leaving(pl.ds(0, tile), index).wait()

    lanes_wide, lanes_out = 384, 512

    def turn(owner, slot, after):
        at = pl.ds(pl.multiple_of(owner * rows, rows), rows)
        for copy in fetch(owner, slot):
            copy.wait()

        def hidden_part(index, carry):
            lanes = pl.ds(pl.multiple_of(index * lanes_wide, 128), lanes_wide)
            gate_pre, up_pre = pre[slot, 0, :, lanes], pre[slot, 1, :, lanes]
            d_hidden = dot_right(d_all[at], w_down[lanes])
            sigmoid = jax.nn.sigmoid(gate_pre)
            d_up[at, lanes] = (d_hidden * gate_pre * sigmoid).astype(BF16)
            d_gate[at, lanes] = (
                d_hidden * up_pre * sigmoid * (1.0 + gate_pre * (1.0 - sigmoid))
            ).astype(BF16)
            return carry

        lax.fori_loop(0, wide // lanes_wide, hidden_part, 0)
        if after is not None:
            for copy in fetch(after, slot):
                copy.start()

        def out_part(index, carry):
            lanes = pl.ds(pl.multiple_of(index * lanes_out, 128), lanes_out)
            blocks[at, lanes] = (
                dot_right(d_gate[at], w_gate[lanes]) + dot_right(d_up[at], w_up[lanes])
            ).astype(BF16)
            return carry

        lax.fori_loop(0, width // lanes_out, out_part, 0)

    gather.own.wait()
    for copy in loads[:3]:
        copy.wait()
    turn(me, 0, across)
    for left, right, target in (
        (act_qkv, d_query, q_grad),
        (act_qkv, d_key_value, kv_grad),
        (attended, d_attended, proj_grad),
    ):
        weight_grad(left, right, slice(None), target, stage, 2)
    gather.relay()
    turn(beside, 1, opposite)
    turn(across, 0, None)
    reduction.copies[1].start()
    reduction.copies[3].start()
    gather.third.wait_recv()
    gather.fourth.wait_recv()
    turn(opposite, 1, None)
    reduction.copies[0].start()
    reduction.copies[2].start()
    loads[3].wait()
    weight_grad(act, d_gate, slice(None), gate_grad, stage_wide, 0)
    weight_grad(act, d_up, slice(None), up_grad, stage_wide, 0)
    reduction.relay()
    loads[4].wait()
    odd = hidden.shape[1] % tile

    weight_grad(hidden, d_all, slice(None), down_grad, stage, 2)
    if odd:
        last = hidden.shape[1] - odd
        stage[0, :odd] = dot_plain(hidden[:, last:].T, d_all[...]).astype(BF16)
        copy = pltpu.make_async_copy(stage.at[0, pl.ds(0, odd)], down_grad.at[pl.ds(last, odd)], stage_sem.at[2])
        copy.start()
        copy.wait()
    reduction.finish()
    strip = 64

    def norm_strip(at, values, gain, d_values, row):
        inv_rms = lax.rsqrt(jnp.mean(values * values, axis=-1, keepdims=True) + EPSILON)
        normed = values * inv_rms
        small[row : row + 1] = small[row : row + 1] + jnp.sum(d_values * normed, axis=0, keepdims=True)
        d_normed = d_values * gain
        return inv_rms * d_normed - normed * inv_rms * jnp.mean(d_normed * normed, axis=-1, keepdims=True)

    def second_norm(index, carry):
        at = pl.ds(pl.multiple_of(index * strip, strip), strip)
        x_rows = x_ref[at].astype(F32)
        value = d_h[at].astype(F32) + norm_strip(at, x_rows + mixed[at], gains[1:2], d_act[at], 1)
        d_res[at] = value
        d_mixed[at] = value.astype(BF16)
        inv_rms = lax.rsqrt(jnp.mean(x_rows * x_rows, axis=-1, keepdims=True) + EPSILON)
        act1[at] = (x_rows * inv_rms * gains[0:1]).astype(BF16)
        return carry

    lax.fori_loop(0, rows // strip, second_norm, 0)
    for index in range(5, 8):
        loads[index].wait()

    def to_z(index, carry):
        at = pl.ds(pl.multiple_of(index * tile, tile), tile)
        d_conv[:, at] = dot_right(d_mixed[...], w_out[at])
        return carry

    lax.fori_loop(0, width // tile, to_z, 0)
    part = 128
    row_at = lax.broadcasted_iota(jnp.int32, (rows, part), 0)

    def lanes_of(offset, index):
        return pl.ds(pl.multiple_of(offset * width + index * part, part), part)

    def convolve_back(index, carry):
        lanes = lanes_of(0, index)
        product = (projected[:, lanes] * projected[:, lanes_of(2, index)]).astype(BF16).astype(F32)
        before = rim[:, lanes].astype(F32)
        near, far = before[15:16], before[14:15]
        one = jnp.where(row_at >= 1, pltpu.roll(product, 1, 0), near)
        two = jnp.where(row_at >= 2, pltpu.roll(product, 2, 0), jnp.where(row_at == 1, near, far))
        d_z = d_conv[:, lanes]
        d_proj[:, lanes_of(1, index)] = (d_z * convolved[:, lanes]).astype(BF16)
        d_value = d_z * projected[:, lanes_of(1, index)]
        d_conv[:, lanes] = d_value
        for row, source in ((2, two), (3, one), (4, product)):
            small[row : row + 1, lanes] = jnp.sum(d_value * source, axis=0, keepdims=True)
        tap = taps[:, lanes]
        edge[0:1, lanes] = tap[0:1] * d_value[0:1]
        edge[1:2, lanes] = tap[0:1] * d_value[1:2] + tap[1:2] * d_value[0:1]
        return carry

    lax.fori_loop(0, width // part, convolve_back, 0)
    edge[2:8] = jnp.zeros((6, width), F32)
    to_last = along(edge, next_edge, edge_sem.at[0], edge_sem.at[1], chain.place - 1)

    @pl.when(chain.has_last)
    def _():
        to_last.start()

    weight_grad(z_low, d_mixed, slice(None), o_grad, stage, 2)

    @pl.when(chain.has_next)
    def _():
        along(edge, next_edge, edge_sem.at[0], edge_sem.at[1], chain.place).wait_recv()

    @pl.when(jnp.logical_not(chain.has_next))
    def _():
        next_edge[...] = jnp.zeros(next_edge.shape, F32)

    def products_back(index, carry):
        lanes = lanes_of(0, index)
        d_value = d_conv[:, lanes]
        tap = taps[:, lanes]
        after = next_edge[:, lanes]
        one = jnp.where(row_at < rows - 1, pltpu.roll(d_value, rows - 1, 0), 0.0)
        two = jnp.where(row_at < rows - 2, pltpu.roll(d_value, rows - 2, 0), 0.0)
        joined = tap[2:3] * d_value + tap[1:2] * one + tap[0:1] * two
        joined = joined + jnp.where(row_at == rows - 2, after[0:1], 0.0)
        joined = joined + jnp.where(row_at == rows - 1, after[1:2], 0.0)
        joined = joined.astype(BF16).astype(F32)
        d_proj[:, lanes] = (joined * projected[:, lanes_of(2, index)]).astype(BF16)
        d_proj[:, lanes_of(2, index)] = (joined * projected[:, lanes]).astype(BF16)
        return carry

    lax.fori_loop(0, width // part, products_back, 0)
    loads[8].wait()

    def to_act(index, carry):
        at = pl.ds(pl.multiple_of(index * tile, tile), tile)
        d_act[:, at] = dot_right(d_proj[...], w_in[at])
        return carry

    lax.fori_loop(0, width // tile, to_act, 0)
    for offset, target in enumerate((b_grad, c_grad, x_grad)):
        weight_grad(act1, d_proj, slice(offset * width, (offset + 1) * width), target, stage, 2)

    def first_norm(index, carry):
        at = pl.ds(pl.multiple_of(index * strip, strip), strip)
        value = d_res[at] + norm_strip(at, x_ref[at].astype(F32), gains[0:1], d_act[at], 0)
        d_x[at] = value.astype(BF16)
        return carry

    lax.fori_loop(0, rows // strip, first_norm, 0)
    for copy in (gather.first, gather.second, gather.third, gather.fourth):
        copy.wait_send()

    @pl.when(chain.has_last)
    def _():
        to_last.wait_send()


def conv_back(local, before, kept, collective_id):
    n_ctx = lax.axis_size("ctx")
    x_low = local[0]
    rows, width = x_low.shape
    wide = before[0].shape[1]
    assert wide % 384 == 0 and width % 512 == 0
    columns = pltpu.VMEM((4 * rows, wide), BF16)
    whole = pltpu.VMEM((4 * rows, width), BF16)
    dma = pltpu.SemaphoreType.DMA
    vmem = pl.BlockSpec(memory_space=pltpu.VMEM)
    hbm = pl.BlockSpec(memory_space=pl.ANY)
    pair = pltpu.VMEM((2, rows // 2, width), BF16)
    square = jax.ShapeDtypeStruct((width, width), BF16)
    column = jax.ShapeDtypeStruct((width, wide), BF16)
    return pl.pallas_call(
        functools.partial(back_kernel, n_ctx),
        out_shape=(
            column,
            column,
            jax.ShapeDtypeStruct((wide, width), BF16),
            square,
            square,
            square,
            square,
            square,
            square,
            square,
            jax.ShapeDtypeStruct((rows, width), BF16),
            jax.ShapeDtypeStruct((8, width), F32),
        ),
        in_specs=[vmem] * len(local) + [hbm] * (len(before) + len(kept)),
        out_specs=[hbm] * 10 + [vmem] * 2,
        scratch_shapes=[pltpu.VMEM(k.shape, k.dtype) for k in kept]
        + [
            dma((9,)),
            pltpu.VMEM((2, 2, rows, wide), F32),
            dma((2, 2)),
            whole,
            columns,
            columns,
            whole,
            dma((4,)),
            dma((4,)),
            dma,
            pltpu.VMEM((2, 256, wide), BF16),
            pltpu.VMEM((2, 256, width), BF16),
            dma((4,)),
            pair,
            pair,
            pair,
            pair,
            dma((6,)),
            dma((6,)),
            pltpu.VMEM((rows, width), F32),
            pltpu.VMEM((rows, width), F32),
            pltpu.VMEM((rows, width), BF16),
            pltpu.VMEM((rows, width), F32),
            pltpu.VMEM((rows, 3 * width), BF16),
            pltpu.VMEM((rows, width), BF16),
            pltpu.VMEM((8, width), F32),
            pltpu.VMEM((8, width), F32),
            dma((2,)),
        ],
        compiler_params=pltpu.CompilerParams(
            collective_id=collective_id, has_side_effects=True, vmem_limit_bytes=58 << 20
        ),
        cost_estimate=busy(55),
    )(*local, *before, *kept)


def ffn_forward(act, w_gate, w_up, w_down):
    gate_pre = matmul(act, w_gate)
    up_pre = matmul(act, w_up)
    hidden = (jax.nn.silu(gate_pre) * up_pre).astype(BF16)
    return matmul(hidden, w_down).astype(BF16), (act, gate_pre, up_pre, hidden)


def ffn_norm_back(d_act, residual, gain):
    normed, inv_rms = norm_rows(residual)
    return norm_back(d_act * gain, normed, inv_rms), jnp.sum(d_act * normed, axis=0)


def shards(
    inputs,
    cotangent,
    lengths,
    norm_gains,
    conv_in,
    conv_kernel,
    conv_out,
    attn_q,
    attn_k,
    attn_v,
    attn_out,
    head_gains,
    ffn_gate,
    ffn_up,
    ffn_down,
):
    micro, rows, width = inputs.shape
    section = lax.axis_index("section")
    group = lax.axis_index("fsdp")
    fsdp = lax.axis_size("fsdp")
    assert micro == lax.axis_size("section")
    head = head_gains.shape[1]
    q_width, kv_width = attn_q.shape[1], attn_k.shape[1]
    q_heads, kv_heads = q_width // head, kv_width // head
    positions = lax.axis_index("ctx") * rows + jnp.arange(rows)
    length = lax.dynamic_index_in_dim(lengths, group * micro + section, keepdims=False)
    mask = (positions < length).astype(F32)[:, None]

    def whole_rows(weight):
        share = weight.shape[0] // (micro * lax.axis_size("ctx"))
        start = (section * lax.axis_size("ctx") + lax.axis_index("ctx")) * share
        mine = lax.dynamic_slice_in_dim(weight, start, share, 0)
        return lax.all_gather(mine, ("fsdp", "section", "ctx"), axis=0, tiled=True)

    part = ffn_gate.shape[1]
    attn_full = whole_rows(jnp.concatenate([attn_q, attn_k, attn_v, attn_out], axis=1))
    query_full, key_full, value_full, proj_full = (
        attn_full[:, :q_width],
        attn_full[:, q_width : q_width + kv_width],
        attn_full[:, q_width + kv_width : q_width + 2 * kv_width],
        attn_full[:, q_width + 2 * kv_width :],
    )

    x_low = lax.dynamic_index_in_dim(inputs, section, keepdims=False)
    in_full, out_full, gate1, up1, down1, projected, convolved, z_low, mixed, rim, act_all1 = front(
        x_low, norm_gains, conv_kernel, conv_in, conv_out, ffn_gate[0], ffn_up[0], ffn_down[0], 2
    )
    x = x_low.astype(F32)
    res1 = x + mixed
    terms1, kept1 = ffn_forward(act_all1, gate1, up1, down1)
    ffn1 = reduced(terms1, 1)
    h_low = (res1 + ffn1).astype(BF16)

    h = h_low.astype(F32)
    normed2, inv2 = norm_rows(h)
    act2 = (normed2 * norm_gains[2]).astype(BF16)
    q_normed, q_inv = norm_heads(matmul(act2, query_full), head)
    k_normed, k_inv = norm_heads(matmul(act2, key_full), head)
    q_gain = jnp.tile(head_gains[0], q_heads)
    k_gain = jnp.tile(head_gains[1], kv_heads)
    query = (q_normed * q_gain).astype(BF16)
    key = (k_normed * k_gain).astype(BF16)
    value = matmul(act2, value_full).astype(BF16)
    d_sum_low = (lax.dynamic_index_in_dim(cotangent, section, keepdims=False).astype(F32) * mask).astype(BF16)
    attended, log_total, kv_all, d_sum_all, gate2, up2, down2 = attend(
        length.reshape(1),
        query,
        jnp.concatenate([key, value], axis=1),
        d_sum_low,
        ffn_gate[0],
        ffn_up[0],
        ffn_down[0],
        3,
    )
    attended_low = attended.astype(BF16)
    attn_rows = matmul(attended_low, proj_full)
    res2 = h + attn_rows
    normed3, _ = norm_rows(res2)
    terms2, d_act3, shared_gu, shared_down = ffn_turn(
        (normed3 * norm_gains[3]).astype(BF16), gate2, up2, down2, d_sum_all, 8
    )

    d_sum = d_sum_low.astype(F32)
    d_ffn, gain3 = ffn_norm_back(d_act3, res2, norm_gains[3])
    d_res2 = d_sum + d_ffn
    d_attn = d_res2.astype(BF16)
    d_att = matmul_right(d_attn, proj_full).astype(BF16)
    delta = jnp.sum((d_att.astype(F32) * attended).reshape(rows, q_heads, head), axis=-1)
    d_query, d_kv, ffn2 = attend_back(
        length.reshape(1), query, kv_all, d_att, log_total, delta.T.reshape(q_heads, 1, rows), terms2, 4
    )
    result = (res2 + ffn2) * mask

    def square(values):
        return jnp.sum(mask * values * values, axis=0, keepdims=True)

    squares = [square(v) for v in (x, mixed, ffn1, h, attn_rows, res2, ffn2, result)]
    second_gu = lax.psum_scatter(
        shared_gu.reshape(-1, shared_gu.shape[-1]), "ctx", scatter_dimension=0, tiled=True
    )
    d_qn = rounded(d_query)
    grad_qgain = jnp.sum(jnp.sum(d_qn * q_normed, axis=0).reshape(q_heads, head), axis=0)
    d_qpre = norm_heads_back(d_qn * q_gain, q_normed, q_inv, head).astype(BF16)
    d_kn = rounded(d_kv[:, :kv_width])
    grad_kgain = jnp.sum(jnp.sum(d_kn * k_normed, axis=0).reshape(kv_heads, head), axis=0)
    d_kpre = norm_heads_back(d_kn * k_gain, k_normed, k_inv, head).astype(BF16)
    d_vpre = d_kv[:, kv_width:].astype(BF16)
    d_act2 = (
        matmul_right(d_qpre, query_full)
        + matmul_right(d_kpre, key_full)
        + matmul_right(d_vpre, value_full)
    )
    gain2 = jnp.sum(d_act2 * normed2, axis=0)
    d_h_low = (d_res2 + norm_back(d_act2 * norm_gains[2], normed2, inv2)).astype(BF16)

    second_gu = lax.all_gather(second_gu, "ctx", axis=0)
    *grads, d_x, conv_small = conv_back(
        (
            x_low,
            mixed,
            d_h_low,
            norm_gains,
            conv_kernel,
            z_low,
            rim,
            act2,
            d_qpre,
            jnp.concatenate([d_kpre, d_vpre], axis=1),
            attended_low,
            d_attn,
        ),
        kept1[1:3],
        (down1, gate1, up1, act_all1, kept1[3], in_full, out_full, projected, convolved),
        9,
    )

    half = ffn_gate.shape[1] // 2
    y_low = result.astype(BF16)
    is_first = section == 0
    other_end = swapped(jnp.where(is_first, y_low, d_x), "section")
    ends = jnp.where(is_first, jnp.stack([d_x, other_end]), jnp.stack([other_end, y_low]))[None]

    small = jnp.concatenate(
        [conv_small[:2], gain2[None], gain3[None], conv_small[2:5]]
        + [jnp.pad(grad[None], ((0, 0), (0, width - head))) for grad in (grad_qgain, grad_kgain)]
        + [jnp.zeros((7, width), F32)]
        + squares
        + [jnp.zeros((8, width), F32)]
    ).astype(BF16)
    small = small.reshape(2, 16, width)
    gu_sum, down_sum, rest_sum = summed_gradients(
        grads[:3],
        grads[3:],
        small,
        second_gu.reshape((-1,) + shared_gu.shape[1:]),
        shared_down,
    )
    rest_sum = rest_sum.astype(F32)

    def block(index):
        rows_at = slice(index * half, (index + 1) * half)
        return rest_sum[:, rows_at].reshape(2 * half, width)

    attn_blocks = [block(i) for i in range(3)]
    conv_blocks = [block(3 + i) for i in range(4)]
    small_sum = rest_sum[0, 7 * half : 7 * half + 9]
    cut = width // fsdp
    mine = lax.dynamic_slice_in_dim(small_sum[:7], group * cut, cut, 1)
    head_cut = head // fsdp
    heads = lax.dynamic_slice_in_dim(small_sum[7:9], group * head_cut, head_cut, 1)
    square_cut = len(squares) // fsdp
    square_sum = jnp.sum(
        lax.dynamic_slice_in_dim(rest_sum[1, 7 * half : 7 * half + 8], group * square_cut, square_cut, 0), axis=1
    )
    token_total = jnp.sum(lengths).astype(F32) * width
    rms = jnp.sqrt(square_sum / token_total)
    return (
        ends,
        mine[:3],
        mine[3],
        jnp.concatenate(conv_blocks[:3], axis=1),
        mine[4:7],
        conv_blocks[3],
        attn_blocks[0],
        attn_blocks[1][:, :kv_width],
        attn_blocks[1][:, kv_width:],
        attn_blocks[2],
        heads,
        gu_sum[0][None].astype(F32),
        gu_sum[1][None].astype(F32),
        down_sum[None].astype(F32),
        rms,
    )


def solution(mesh):
    return jax.shard_map(
        shards,
        mesh=mesh,
        in_specs=(
            P("fsdp", "ctx", None),
            P("fsdp", "ctx", None),
            P(),
            P(),
            P("fsdp", None),
            P(),
            P("fsdp", None),
            P("fsdp", None),
            P("fsdp", None),
            P("fsdp", None),
            P("fsdp", None),
            P(),
            P("section", "fsdp", None),
            P("section", "fsdp", None),
            P("section", "fsdp", None),
        ),
        out_specs=(
            P("section", "fsdp", "ctx", None),
            P(None, "fsdp"),
            P("fsdp"),
            P("fsdp", None),
            P(None, "fsdp"),
            P("fsdp", None),
            P("fsdp", None),
            P("fsdp", None),
            P("fsdp", None),
            P("fsdp", None),
            P(None, "fsdp"),
            P("section", "fsdp", None),
            P("section", "fsdp", None),
            P("section", "fsdp", None),
            P("fsdp"),
        ),
        check_vma=False,
    )
```

```python
import functools

import jax
import jax.numpy as jnp
from jax import lax
from jax.experimental import pallas as pl
from jax.experimental.pallas import tpu as pltpu
from jax.sharding import PartitionSpec as P

EPSILON = 1e-05
NEGATIVE = -1e30
MESH = pl.DeviceIdType.MESH
F32 = jnp.float32
BF16 = jnp.bfloat16


def passed_along(block, axis, distance):
    devices = range(lax.axis_size(axis))
    route = [(i - distance, i) for i in devices if i - distance in devices]
    return lax.ppermute(block, axis, route)


def swapped(block, axis):
    return lax.ppermute(block, axis, [(0, 1), (1, 0)])


def rounded(values):
    return lax.optimization_barrier(values.astype(BF16)).astype(F32)


def matmul(left_op, right_op):
    return jnp.dot(left_op, right_op, preferred_element_type=F32)


def matmul_left(left_op, right_op):
    return lax.dot_general(left_op, right_op, (((0,), (0,)), ((), ())), preferred_element_type=F32)


def matmul_right(left_op, right_op):
    return lax.dot_general(left_op, right_op, (((1,), (1,)), ((), ())), preferred_element_type=F32)


def norm_rows(values):
    inv_rms = lax.rsqrt(jnp.mean(values * values, axis=-1, keepdims=True) + EPSILON)
    return (values * inv_rms, inv_rms)


def norm_back(dnormed, normed, inv_rms):
    return inv_rms * dnormed - normed * inv_rms * jnp.mean(dnormed * normed, axis=-1, keepdims=True)


def head_sums(values, head):
    heads = values.shape[1] // head
    owner = (jnp.arange(values.shape[1])[:, None] // head == jnp.arange(heads)[None, :]).astype(F32)
    sums = jnp.dot(values, owner, precision=lax.Precision.HIGHEST, preferred_element_type=F32)
    return jnp.dot(sums, owner.T, precision=lax.Precision.HIGHEST, preferred_element_type=F32)


def norm_heads(values, head):
    inv_rms = lax.rsqrt(head_sums(values * values, head) / head + EPSILON)
    return (values * inv_rms, inv_rms)


def norm_heads_back(dnormed, normed, inv_rms, head):
    return inv_rms * dnormed - normed * inv_rms * (head_sums(dnormed * normed, head) / head)


def busy(microseconds):
    return pl.CostEstimate(flops=int(microseconds), bytes_accessed=1 << 16, transcendentals=0)


def corners():
    me = lax.axis_index("fsdp")
    beside = me + 1 - 2 * lax.rem(me, 2)
    across = lax.rem(me + 2, 4)
    return me, beside, across, lax.rem(beside + 2, 4)


def greet_sides():
    _, beside, across, _ = corners()
    barrier = pltpu.get_barrier_semaphore()
    for target in (beside, across):
        pl.semaphore_signal(barrier, inc=1, device_id={"fsdp": target}, device_id_type=MESH)
    pl.semaphore_wait(barrier, 2)


def to_side(src, dst, send_sem, recv_sem, target):
    return pltpu.make_async_remote_copy(
        src_ref=src,
        dst_ref=dst,
        send_sem=send_sem,
        recv_sem=recv_sem,
        device_id={"fsdp": target},
        device_id_type=MESH,
    )


class SideGather:
    def __init__(self, block, whole, send_sem, recv_sem, own_sem):
        me, beside, across, _ = corners()
        rows = block.shape[0]
        half = rows // 2

        def part(owner, start, size):
            return whole.at[pl.ds(pl.multiple_of(owner * rows + start, half), size)]

        self.first = to_side(block, part(me, 0, rows), send_sem.at[0], recv_sem.at[0], beside)
        self.second = to_side(block, part(me, 0, rows), send_sem.at[1], recv_sem.at[1], across)
        at = part(beside, 0, half)
        self.third = to_side(at, at, send_sem.at[2], recv_sem.at[2], across)
        at = part(across, half, half)
        self.fourth = to_side(at, at, send_sem.at[3], recv_sem.at[3], beside)
        self.own = pltpu.make_async_copy(block, part(me, 0, rows), own_sem)

    def start(self):
        self.first.start()
        self.second.start()
        self.own.start()

    def relay(self):
        self.first.wait_recv()
        self.third.start()
        self.second.wait_recv()
        self.fourth.start()

    def finish(self):
        self.own.wait()
        self.first.wait_send()
        self.second.wait_send()
        self.third.wait()
        self.fourth.wait()


class SideReduce:
    def __init__(self, blocks, total, beside_got, across_got, passed, passed_got, send_sem, recv_sem):
        self.refs = blocks, total, beside_got, across_got, passed, passed_got
        me, beside, across, opposite = corners()
        self.me, self.beside, self.across = me, beside, across
        self.copies = []
        for index, (turn, target, got) in enumerate(((0, beside, beside_got), (1, across, across_got))):
            for slot, owner in ((1, opposite), (0, target)):
                self.copies.append(
                    to_side(
                        blocks.at[self.part(owner, turn)],
                        got.at[slot],
                        send_sem.at[2 * index + slot],
                        recv_sem.at[2 * index + slot],
                        target,
                    )
                )
        self.onward = [
            to_side(passed.at[turn], passed_got.at[turn], send_sem.at[4 + turn], recv_sem.at[4 + turn], owner)
            for turn, owner in ((0, across), (1, beside))
        ]

    def part(self, owner, turn):
        half = self.refs[1].shape[0] // 2
        return pl.ds(pl.multiple_of(owner * 2 * half + turn * half, half), half)

    def start(self):
        for index in (0, 2, 1, 3):
            self.copies[index].start()

    def relay(self):
        blocks, _, beside_got, across_got, passed, _ = self.refs
        for turn, owner, index, got in ((0, self.across, 0, beside_got), (1, self.beside, 2, across_got)):
            self.copies[index].wait_recv()
            passed[turn] = (blocks[self.part(owner, turn)].astype(F32) + got[1].astype(F32)).astype(BF16)
            self.onward[turn].start()

    def finish(self):
        blocks, total, beside_got, across_got, _, passed_got = self.refs
        half = total.shape[0] // 2
        for turn, index, got in ((0, 1, beside_got), (1, 3, across_got)):
            self.copies[index].wait_recv()
            total[pl.ds(turn * half, half)] = blocks[self.part(self.me, turn)].astype(F32) + got[0].astype(F32)
        for turn in range(2):
            self.onward[turn].wait_recv()
            at = pl.ds(turn * half, half)
            total[at] = total[at] + passed_got[turn].astype(F32)
        for copy in self.copies + self.onward:
            copy.wait_send()


def tail_kernel(
    counts,
    gate_in,
    up_in,
    down_in,
    query_in,
    kv_in,
    proj_in,
    conv_b_in,
    conv_c_in,
    conv_x_in,
    conv_o_in,
    small_in,
    second_gu_in,
    second_down_in,
    gu_out,
    down_out,
    rest_out,
    a_own,
    a_other,
    a_sum,
    a_done,
    b_own,
    b_other,
    b_sum,
    b_done,
    c_own,
    c_other,
    c_got,
    own_sem,
    pair_send,
    pair_recv,
    c_own_sem,
    c_pair_send,
    c_pair_recv,
    c_send,
    c_recv,
    a_up_send,
    a_up_recv,
    a_back_send,
    a_back_recv,
    a_out_send,
    b_up_send,
    b_up_recv,
    b_back_send,
    b_back_recv,
    b_out_send,
    b_keep_sem,
    gu_recv,
    down_recv,
    rest_recv,
    second_send,
):
    n_ctx, n_fsdp = counts
    section = lax.axis_index("section")
    place = lax.axis_index("ctx")
    group = lax.axis_index("fsdp")
    other = 1 - section
    a_chunks, a_rows, a_width = a_own.shape
    b_chunks, b_rows, b_width = b_own.shape
    half = gate_in.shape[0] // n_fsdp // 2
    subs = half // a_rows
    per_kind = n_fsdp * subs
    down_half = down_in.shape[0] // 2
    down_chunks = down_half // b_rows
    c_rows = c_own.shape[1]
    mixers = (query_in, kv_in, proj_in, conv_b_in, conv_c_in, conv_x_in, conv_o_in)
    n_mix = len(mixers)
    cut = 3 * half // b_rows
    c_parts = ((0, cut), (cut, c_rows // b_rows))
    paired = a_chunks // 2
    mix_start = 2 * down_chunks
    mix_chunks = b_chunks - mix_start
    second = paired + down_chunks // 2
    ticks = second + mix_chunks // 2
    tail = 2 * (n_ctx - 1)

    barrier = pltpu.get_barrier_semaphore()
    for step in range(1, 2 * n_fsdp):
        flat = lax.rem(section * n_fsdp + group + step, 2 * n_fsdp)
        pl.semaphore_signal(
            barrier,
            inc=1,
            device_id={"section": flat // n_fsdp, "fsdp": lax.rem(flat, n_fsdp)},
            device_id_type=MESH,
        )

    @pl.when(place > 0)
    def _():
        pl.semaphore_signal(barrier, inc=1, device_id={"ctx": place - 1}, device_id_type=MESH)

    @pl.when(place < n_ctx - 1)
    def _():
        pl.semaphore_signal(barrier, inc=1, device_id={"ctx": place + 1}, device_id_type=MESH)

    at_edge = (place == 0) | (place == n_ctx - 1)

    @pl.when(at_edge)
    def _():
        pl.semaphore_wait(barrier, 2 * n_fsdp)

    @pl.when(jnp.logical_not(at_edge))
    def _():
        pl.semaphore_wait(barrier, 2 * n_fsdp + 1)

    def half_rows(owner, which):
        return pl.ds(pl.multiple_of(owner * (2 * half) + which * half, half), half)

    def a_at(buffer, k):
        return buffer.at[k]

    b_at = a_at

    def opening(k):
        copies = []
        kind, rest = divmod(k, per_kind)
        owner, sub = divmod(rest, subs)
        source = (gate_in, up_in)[kind]
        spots = []
        for which in (section, other):
            start = owner * (2 * half) + which * half + sub * a_rows
            spots.append(source.at[pl.ds(pl.multiple_of(start, a_rows), a_rows)])
        copies.append((spots, a_own.at[k], a_other.at[k], k))
        if k < down_chunks:
            spots = [
                down_in.at[pl.ds(pl.multiple_of(which * down_half + k * b_rows, b_rows), b_rows)]
                for which in (section, other)
            ]
            copies.append((spots, b_own.at[k], b_other.at[k], a_chunks + k))
        for (mine, theirs), own_dst, other_dst, spot in copies:
            pltpu.make_async_copy(mine, own_dst, own_sem.at[spot]).start()
            pltpu.make_async_remote_copy(
                src_ref=theirs,
                dst_ref=other_dst,
                send_sem=pair_send.at[spot],
                recv_sem=pair_recv.at[spot],
                device_id={"section": other},
                device_id_type=MESH,
            ).start()

    for k in range(a_chunks):
        opening(k)
    for k in range(down_chunks):
        pltpu.make_async_copy(
            second_down_in.at[pl.ds(k * b_rows, b_rows)],
            b_own.at[down_chunks + k],
            own_sem.at[a_chunks + down_chunks + k],
        ).start()
    c_local, c_pair = ([], []), ([], [])
    for kind, source in enumerate(mixers):
        part = 0 if kind < 3 else 1
        for owner in range(n_fsdp):
            index = owner * (n_mix + 1) + kind
            place_at = pl.ds(kind * half, half)
            c_local[part].append(
                pltpu.make_async_copy(
                    source.at[half_rows(owner, section)], c_own.at[owner, place_at], c_own_sem.at[index]
                )
            )
            c_pair[part].append(
                pltpu.make_async_remote_copy(
                    src_ref=source.at[half_rows(owner, other)],
                    dst_ref=c_other.at[owner, place_at],
                    send_sem=c_pair_send.at[index],
                    recv_sem=c_pair_recv.at[index],
                    device_id={"section": other},
                    device_id_type=MESH,
                )
            )
    for owner in range(n_fsdp):
        small_at = pl.ds(n_mix * half, c_rows - n_mix * half)
        index = owner * (n_mix + 1) + n_mix
        c_local[1].append(
            pltpu.make_async_copy(small_in.at[section], c_own.at[owner, small_at], c_own_sem.at[index])
        )
        c_pair[1].append(
            pltpu.make_async_remote_copy(
                src_ref=small_in.at[other],
                dst_ref=c_other.at[owner, small_at],
                send_sem=c_pair_send.at[index],
                recv_sem=c_pair_recv.at[index],
                device_id={"section": other},
                device_id_type=MESH,
            )
        )
    for part in range(2):
        for copy in c_pair[part]:
            copy.start()
        for copy in c_local[part]:
            copy.start()
    b_own[b_chunks - 1] = jnp.zeros((b_rows, b_width), BF16)
    _, beside, across, opposite = corners()

    def span(first, last):
        return pl.ds(first * b_rows, (last - first) * b_rows)

    def mixer_spans(part):
        first, last = c_parts[part]
        middle = (first + last) // 2
        return (first, middle, beside, across), (middle, last, across, beside)

    def mixer_copies(part):
        opening, onward = [], []
        for turn, (first, last, near, far) in enumerate(mixer_spans(part)):
            at = span(first, last)
            for slot, owner in ((0, opposite), (1, near)):
                opening.append(
                    to_side(
                        c_own.at[owner, at],
                        c_got.at[slot, at],
                        c_send.at[part, 3 * turn + slot],
                        c_recv.at[part, 3 * turn + slot],
                        near,
                    )
                )
            onward.append(
                to_side(
                    c_own.at[far, at],
                    c_got.at[2, at],
                    c_send.at[part, 3 * turn + 2],
                    c_recv.at[part, 3 * turn + 2],
                    far,
                )
            )
        return opening, onward

    def mixer_sum(part, owner):
        kinds = range(3) if part == 0 else range(3, n_mix + 1)
        first, last = c_parts[part]
        for kind in kinds:
            size = half if kind < n_mix else c_rows - n_mix * half
            at = c_own.at[owner, pl.ds(kind * half, size)]
            index = owner * (n_mix + 1) + kind
            pltpu.make_async_copy(at, at, c_own_sem.at[index]).wait()
            pltpu.make_async_copy(at, at, c_pair_recv.at[index]).wait()

        def add(index, carry):
            at = pl.ds(pl.multiple_of(index * b_rows, b_rows), b_rows)
            c_own[owner, at] = (c_own[owner, at].astype(F32) + c_other[owner, at].astype(F32)).astype(BF16)
            return carry

        lax.fori_loop(first, last, add, 0)

    def mixer_out(part):
        opening, _ = mixer_copies(part)
        for index in (0, 2, 1, 3):
            opening[index].start()

    def mixer_on(part):
        opening, onward = mixer_copies(part)
        for turn, (first, last, near, far) in enumerate(mixer_spans(part)):
            opening[2 * turn].wait_recv()

            def add(index, carry, far=far):
                at = pl.ds(pl.multiple_of(index * b_rows, b_rows), b_rows)
                c_own[far, at] = (c_own[far, at].astype(F32) + c_got[0, at].astype(F32)).astype(BF16)
                return carry

            lax.fori_loop(first, last, add, 0)
            onward[turn].start()

    def mixer_in(part):
        opening, onward = mixer_copies(part)
        for turn in range(2):
            opening[2 * turn + 1].wait_recv()
            onward[turn].wait_recv()
        first, last = c_parts[part]

        def add(index, carry):
            at = pl.ds(pl.multiple_of(index * b_rows, b_rows), b_rows)
            total = c_own[group, at].astype(F32) + c_got[1, at].astype(F32) + c_got[2, at].astype(F32)
            b_own[mix_start + index] = total.astype(BF16)
            return carry

        lax.fori_loop(first, last, add, 0)

    strip = half // n_ctx

    def second_start():
        for owner in range(n_fsdp):
            is_mine = (section == 1) & (group == owner)
            for index in range(2 * n_ctx):
                turn, kind = index // 2, index % 2
                src = second_gu_in.at[turn, owner, kind]
                dst = gu_out.at[
                    kind,
                    pl.ds(pl.multiple_of(section * half + turn * strip, strip), strip),
                    pl.ds(pl.multiple_of(group * a_width, 128), a_width),
                ]

                @pl.when(is_mine)
                def _(src=src, dst=dst):
                    pltpu.make_async_copy(src, dst, second_send.at[0]).start()

                @pl.when(jnp.logical_not(is_mine))
                def _(src=src, dst=dst, kind=kind, owner=owner):
                    pltpu.make_async_remote_copy(
                        src_ref=src,
                        dst_ref=dst,
                        send_sem=second_send.at[0],
                        recv_sem=gu_recv.at[kind, section * n_fsdp + group],
                        device_id={"section": 1, "fsdp": owner},
                        device_id_type=MESH,
                    ).start()

    def a_target(k):
        kind = k // per_kind
        rest = lax.rem(k, per_kind)
        owner = rest // subs
        sub = lax.rem(rest, subs)
        start = section * half + sub * a_rows
        spot = gu_out.at[
            kind,
            pl.ds(pl.multiple_of(start, a_rows), a_rows),
            pl.ds(pl.multiple_of(group * a_width, 128), a_width),
        ]
        return kind, owner, spot

    def a_hand_out(k):
        kind, owner, spot = a_target(k)
        is_mine = (section == 0) & (group == owner)
        slot = k
        a_ref = a_at(a_done, k)

        @pl.when(is_mine)
        def _():
            pltpu.make_async_copy(a_ref, spot, a_out_send.at[slot]).start()

        @pl.when(jnp.logical_not(is_mine))
        def _():
            pltpu.make_async_remote_copy(
                src_ref=a_ref,
                dst_ref=spot,
                send_sem=a_out_send.at[slot],
                recv_sem=gu_recv.at[kind, section * n_fsdp + group],
                device_id={"section": 0, "fsdp": owner},
                device_id_type=MESH,
            ).start()

    def down_hand_out(k, keeper):
        slot = k
        b_ref = b_at(b_done, k)
        index = k - keeper * down_chunks
        at = down_out.at[
            pl.ds(pl.multiple_of(section * down_half + index * b_rows, b_rows), b_rows),
        ]

        @pl.when(section == keeper)
        def _():
            pltpu.make_async_copy(b_ref, at, b_out_send.at[slot]).start()

        @pl.when(section != keeper)
        def _():
            pltpu.make_async_remote_copy(
                src_ref=b_ref,
                dst_ref=at,
                send_sem=b_out_send.at[slot],
                recv_sem=down_recv,
                device_id={"section": keeper},
                device_id_type=MESH,
            ).start()

    def mix_hand_out(k):
        slot = k
        b_ref = b_at(b_done, k)
        at = rest_out.at[
            section,
            pl.ds(pl.multiple_of((k - mix_start) * b_rows, b_rows), b_rows),
        ]
        pltpu.make_async_copy(b_ref, at, b_keep_sem.at[slot]).start()
        pltpu.make_async_remote_copy(
            src_ref=b_ref,
            dst_ref=at,
            send_sem=b_out_send.at[slot],
            recv_sem=rest_recv,
            device_id={"section": other},
            device_id_type=MESH,
        ).start()

    def chain_copy(at, sems, slot, target):
        return pltpu.make_async_remote_copy(
            src_ref=at,
            dst_ref=at,
            send_sem=sems[0].at[slot],
            recv_sem=sems[1].at[slot],
            device_id={"ctx": target},
            device_id_type=MESH,
        )

    class Gates:
        hand_out = staticmethod(a_hand_out)

        @staticmethod
        def view(buffer, k):
            return a_at(buffer, k)

        own, sums, done = a_own, a_sum, a_done
        up, back = (a_up_send, a_up_recv), (a_back_send, a_back_recv)

        @staticmethod
        def term(k):
            slot = k
            at = a_at(a_own, k)
            pltpu.make_async_copy(at, at, own_sem.at[slot]).wait()
            pltpu.make_async_copy(at, at, pair_recv.at[slot]).wait()
            return at[...].astype(F32) + a_at(a_other, k)[...].astype(F32)

    class Downs:
        @staticmethod
        def hand_out(k):
            down_hand_out(k, 0)

        @staticmethod
        def view(buffer, k):
            return b_at(buffer, k)

        own, sums, done = b_own, b_sum, b_done
        up, back = (b_up_send, b_up_recv), (b_back_send, b_back_recv)

        @staticmethod
        def term(k):
            slot = a_chunks + k
            at = b_at(b_own, k)
            pltpu.make_async_copy(at, at, own_sem.at[slot]).wait()
            pltpu.make_async_copy(at, at, pair_recv.at[slot]).wait()
            return at[...].astype(F32) + b_at(b_other, k)[...].astype(F32)

    class Seconds(Downs):
        @staticmethod
        def hand_out(k):
            down_hand_out(k, 1)

        @staticmethod
        def term(k):
            at = b_at(b_own, k)
            pltpu.make_async_copy(at, at, own_sem.at[a_chunks + k]).wait()
            return at[...].astype(F32)

    class Mixed(Downs):
        hand_out = staticmethod(mix_hand_out)

        @staticmethod
        def term(k):
            return b_at(b_own, k)[...].astype(F32)

    def upward(item, k, rank, ahead, behind):
        slot = k
        term = item.term(k)
        sums = item.view(item.sums, k)

        @pl.when(rank == 0)
        def _():
            sums[...] = term.astype(BF16)

        @pl.when(rank > 0)
        def _():
            chain_copy(sums, item.up, slot, behind).wait_recv()

        @pl.when((rank > 0) & (rank < n_ctx - 1))
        def _():
            sums[...] = (term + sums[...].astype(F32)).astype(BF16)

        @pl.when(rank < n_ctx - 1)
        def _():
            chain_copy(sums, item.up, slot, ahead).start()

        @pl.when(rank == n_ctx - 1)
        def _():
            done = item.view(item.done, k)
            done[...] = (term + sums[...].astype(F32)).astype(BF16)
            chain_copy(done, item.back, slot, behind).start()
            item.hand_out(k)

    def backward(item, k, rank, ahead, behind):
        slot = k
        done = item.view(item.done, k)
        chain_copy(done, item.back, slot, ahead).wait_recv()

        @pl.when(rank > 0)
        def _():
            chain_copy(done, item.back, slot, behind).start()

        item.hand_out(k)

    def on_step(action, step, active, way, *where):
        @pl.when(active & (step < paired))
        def _():
            at = jnp.clip(step, 0, paired - 1)
            action(Gates, 2 * at + way, *where)

            @pl.when(lax.rem(3 * at, 8) < 3)
            def _():
                action(Downs, 2 * (3 * at // 8) + way, *where)

        @pl.when(active & (step >= paired) & (step < second))
        def _():
            at = jnp.clip(step - paired, 0, down_chunks // 2 - 1)
            action(Seconds, down_chunks + 2 * at + way, *where)

        @pl.when(active & (step >= second))
        def _():
            at = jnp.clip(step - second, 0, mix_chunks // 2 - 1)
            action(Mixed, mix_start + 2 * at + way, *where)

    lanes = []
    for way in range(2):
        rank = place if way == 0 else n_ctx - 1 - place
        ahead = place + 1 if way == 0 else place - 1
        behind = place - 1 if way == 0 else place + 1
        lanes.append((way, rank, ahead, behind))

    def tick_step(tick, carry):
        for part, start in ((0, 1), (1, 5)):
            for owner in range(n_fsdp):

                @pl.when(tick == start + owner)
                def _(part=part, owner=owner):
                    mixer_sum(part, owner)

        events = (
            (4, mixer_out, 0),
            (8, mixer_out, 1),
            (10, mixer_on, 0),
            (15, mixer_on, 1),
            (second - 1, mixer_in, 0),
            (second + 3, mixer_in, 1),
        )
        for moment, action, part in events:

            @pl.when(tick == moment)
            def _(action=action, part=part):
                action(part)

        for way, rank, ahead, behind in lanes:
            step = tick - 2 * rank
            on_step(upward, step, (step >= 0) & (step < ticks), way, rank, ahead, behind)
            late = tick - 2 * (tail - rank)
            on_step(
                backward,
                late,
                (late >= 0) & (late < ticks) & (rank < n_ctx - 1),
                way,
                rank,
                ahead,
                behind,
            )

        return carry

    second_start()
    lax.fori_loop(0, ticks + 2 * tail, tick_step, 0)

    for part in range(2):
        for copy in c_pair[part]:
            copy.wait_send()
        opening, onward = mixer_copies(part)
        for copy in opening + onward:
            copy.wait_send()

    def settle_item(item, k, rank, ahead, behind, out_send):
        @pl.when(rank < n_ctx - 1)
        def _():
            chain_copy(item.view(item.sums, k), item.up, k, ahead).wait_send()

        @pl.when(rank > 0)
        def _():
            chain_copy(item.view(item.done, k), item.back, k, behind).wait_send()

        ref = item.view(item.own, k)
        pltpu.make_async_copy(ref, ref, out_send.at[k]).wait()

    def settle_gates(index, carry):
        for way, rank, ahead, behind in lanes:
            k = 2 * index + way
            settle_item(Gates, k, rank, ahead, behind, a_out_send)
            ref = a_own.at[k]
            pltpu.make_async_copy(ref, ref, pair_send.at[k]).wait()
        return carry

    lax.fori_loop(0, a_chunks // 2, settle_gates, 0)

    def settle_rest(index, carry):
        for way, rank, ahead, behind in lanes:
            k = 2 * index + way
            settle_item(Mixed, k, rank, ahead, behind, b_out_send)
            ref = b_own.at[k]

            @pl.when(k < down_chunks)
            def _(ref=ref, k=k):
                pltpu.make_async_copy(ref, ref, pair_send.at[a_chunks + k]).wait()

            @pl.when(k >= mix_start)
            def _(ref=ref, k=k):
                pltpu.make_async_copy(ref, ref, b_keep_sem.at[k]).wait()

        return carry

    lax.fori_loop(0, b_chunks // 2, settle_rest, 0)
    pltpu.make_async_copy(second_gu_in, second_gu_in, second_send.at[0]).wait()

    for kind in range(2):
        for source in range(2 * n_fsdp):

            @pl.when(section * n_fsdp + group != source)
            def _(kind=kind, source=source):
                region = gu_out.at[
                    kind,
                    pl.ds((source // n_fsdp) * half, half),
                    pl.ds((source % n_fsdp) * a_width, a_width),
                ]
                pltpu.make_async_copy(region, region, gu_recv.at[kind, source]).wait()

    region = down_out.at[pl.ds(pl.multiple_of(other * down_half, b_rows), down_half)]
    pltpu.make_async_copy(region, region, down_recv).wait()
    region = rest_out.at[other]
    pltpu.make_async_copy(region, region, rest_recv).wait()


def summed_gradients(first, mixers, small, second_gu, second_down):
    n_ctx, n_fsdp = lax.axis_size("ctx"), lax.axis_size("fsdp")
    gate, up, down = first
    half = gate.shape[0] // n_fsdp // 2
    a_rows, b_rows = half // 4, half * 3 // 8
    a_chunks = 2 * n_fsdp * 4
    a_width, b_width = gate.shape[1], down.shape[1]
    c_rows = len(mixers) * half + small.shape[1]
    down_chunks = down.shape[0] // 2 // b_rows
    b_chunks = 2 * down_chunks + c_rows // b_rows + 1
    assert c_rows % b_rows == 0 and b_chunks % 2 == 0 and down_chunks % 2 == 0
    assert down_chunks * 8 == a_chunks * 3
    rest = b_chunks - 2 * down_chunks
    dma = pltpu.SemaphoreType.DMA
    loads = a_chunks + 2 * down_chunks
    pieces = n_fsdp * (len(mixers) + 1)
    return pl.pallas_call(
        functools.partial(tail_kernel, (n_ctx, n_fsdp)),
        out_shape=(
            jax.ShapeDtypeStruct((2, 2 * half, n_fsdp * a_width), BF16),
            jax.ShapeDtypeStruct(down.shape, BF16),
            jax.ShapeDtypeStruct((2, rest * b_rows, b_width), BF16),
        ),
        in_specs=[pl.BlockSpec(memory_space=pl.ANY)] * (6 + len(mixers)),
        out_specs=[pl.BlockSpec(memory_space=pl.ANY)] * 3,
        scratch_shapes=[
            pltpu.VMEM((a_chunks, a_rows, a_width), BF16),
            pltpu.VMEM((a_chunks, a_rows, a_width), BF16),
            pltpu.VMEM((a_chunks, a_rows, a_width), BF16),
            pltpu.VMEM((a_chunks, a_rows, a_width), BF16),
            pltpu.VMEM((b_chunks, b_rows, b_width), BF16),
            pltpu.VMEM((down_chunks, b_rows, b_width), BF16),
            pltpu.VMEM((b_chunks, b_rows, b_width), BF16),
            pltpu.VMEM((b_chunks, b_rows, b_width), BF16),
            pltpu.VMEM((n_fsdp, c_rows, b_width), BF16),
            pltpu.VMEM((n_fsdp, c_rows, b_width), BF16),
            pltpu.VMEM((n_fsdp - 1, c_rows, b_width), BF16),
            dma((loads,)),
            dma((loads,)),
            dma((loads,)),
            dma((pieces,)),
            dma((pieces,)),
            dma((pieces,)),
            dma((2, 6)),
            dma((2, 6)),
            dma((a_chunks,)),
            dma((a_chunks,)),
            dma((a_chunks,)),
            dma((a_chunks,)),
            dma((a_chunks,)),
            dma((b_chunks,)),
            dma((b_chunks,)),
            dma((b_chunks,)),
            dma((b_chunks,)),
            dma((b_chunks,)),
            dma((b_chunks,)),
            dma((2, 2 * n_fsdp)),
            dma,
            dma,
            dma((2,)),
        ],
        compiler_params=pltpu.CompilerParams(
            collective_id=6, has_side_effects=True, vmem_limit_bytes=56 << 20
        ),
        cost_estimate=busy(160),
    )(gate, up, down, *mixers, small, second_gu, second_down)


class Columns:
    def __init__(self, holder, sources, targets, send_sem, recv_sem, pair_send, pair_recv, own_sem):
        self.count = 4
        self.holder = holder
        self.section = lax.axis_index("section")
        self.me = lax.axis_index("fsdp")
        self.sources, self.targets = sources, targets
        self.sems = send_sem, recv_sem, pair_send, pair_recv, own_sem
        self.rows = sources[0].shape[0]
        self.wide = targets[0].shape[1]
        self.steps = [(step, kind) for step in range(1, self.count) for kind in range(2)]

    def at_rows(self, out, owner):
        return out.at[pl.ds(pl.multiple_of(owner * self.rows, self.rows), self.rows)]

    def at_columns(self, source, owner):
        return source.at[:, pl.ds(pl.multiple_of(owner * self.wide, 128), self.wide)]

    def crossing(self, step, kind):
        target = lax.rem(self.me + step, self.count)
        return to_side(
            self.at_columns(self.sources[kind], target),
            self.at_rows(self.targets[kind], self.me),
            self.sems[0].at[kind, step],
            self.sems[1].at[kind, step],
            target,
        )

    def handed(self, step, kind):
        if kind == 2:
            src, dst = self.sources[2], self.targets[2]
        else:
            origin = lax.rem(self.me + self.count - step, self.count)
            dst = self.at_rows(self.targets[kind], origin)
            src = self.at_columns(self.sources[kind], self.me) if step == 0 else dst
        return pltpu.make_async_remote_copy(
            src_ref=src,
            dst_ref=dst,
            send_sem=self.sems[2].at[kind, step],
            recv_sem=self.sems[3].at[kind, step],
            device_id={"section": 1 - self.section},
            device_id_type=MESH,
        )

    def kept(self, kind):
        if kind == 2:
            return pltpu.make_async_copy(self.sources[2], self.targets[2], self.sems[4].at[2])
        return pltpu.make_async_copy(
            self.at_columns(self.sources[kind], self.me),
            self.at_rows(self.targets[kind], self.me),
            self.sems[4].at[kind],
        )

    def start(self):
        @pl.when(self.section == self.holder)
        def _():
            for step, kind in self.steps:
                self.crossing(step, kind).start()
            for kind in range(3):
                self.handed(0, kind).start()
            for kind in range(3):
                self.kept(kind).start()

    def relay(self):
        @pl.when(self.section == self.holder)
        def _():
            for step, kind in self.steps:
                self.crossing(step, kind).wait_recv()
                self.handed(step, kind).start()

    def arrive(self):
        every = [(0, kind) for kind in range(3)] + self.steps

        @pl.when(self.section == self.holder)
        def _():
            for kind in range(3):
                self.kept(kind).wait()

        @pl.when(self.section != self.holder)
        def _():
            for step, kind in every:
                self.handed(step, kind).wait_recv()

    def finish(self):
        every = [(0, kind) for kind in range(3)] + self.steps

        @pl.when(self.section == self.holder)
        def _():
            for step, kind in self.steps:
                self.crossing(step, kind).wait_send()
            for step, kind in every:
                self.handed(step, kind).wait_send()


class SharedColumns(Columns):
    def __init__(self, *args):
        *args, plane_send, plane_recv = args
        super().__init__(*args)
        self.plane = plane_send, plane_recv
        place = lax.axis_index("ctx")
        self.odd = lax.rem(place, 2)
        self.partner = place + 1 - 2 * self.odd

    def passed_on(self, step, kind):
        at = self.at_rows(self.targets[kind], lax.rem(self.me + self.count - step, self.count))
        return pltpu.make_async_remote_copy(
            src_ref=at,
            dst_ref=at,
            send_sem=self.plane[0].at[kind, step],
            recv_sem=self.plane[1].at[kind, step],
            device_id={"ctx": self.partner},
            device_id_type=MESH,
        )

    def by_kind(self, action):
        for kind in range(2):

            @pl.when((self.section == self.holder) & (self.odd == kind))
            def _(kind=kind):
                for step in range(1, self.count):
                    action(step, kind)

    def start(self):
        self.by_kind(lambda step, kind: self.crossing(step, kind).start())

        @pl.when(self.section == self.holder)
        def _():
            for kind in range(3):
                self.handed(0, kind).start()
            for kind in range(3):
                self.kept(kind).start()

    def relay(self):
        def moved(step, kind):
            self.crossing(step, kind).wait_recv()
            self.passed_on(step, kind).start()
            self.handed(step, kind).start()

        self.by_kind(moved)

    def relay_passed(self):
        def passed(step, kind):
            self.passed_on(step, 1 - kind).wait_recv()
            self.handed(step, 1 - kind).start()

        self.by_kind(passed)

    def finish(self):
        def sent(step, kind):
            self.crossing(step, kind).wait_send()
            self.passed_on(step, kind).wait_send()

        self.by_kind(sent)
        every = [(0, kind) for kind in range(3)] + self.steps

        @pl.when(self.section == self.holder)
        def _():
            for step, kind in every:
                self.handed(step, kind).wait_send()


class Chain:
    def __init__(self, count):
        self.count = count
        self.place = lax.axis_index("ctx")
        self.has_next = self.place < count - 1
        self.has_last = self.place > 0


def greet_mixed(chain, targets):
    barrier = pltpu.get_barrier_semaphore()
    for target in targets:
        pl.semaphore_signal(barrier, inc=1, device_id=target, device_id_type=MESH)

    @pl.when(chain.has_last)
    def _():
        pl.semaphore_signal(barrier, inc=1, device_id={"ctx": chain.place - 1}, device_id_type=MESH)

    @pl.when(chain.has_next)
    def _():
        pl.semaphore_signal(barrier, inc=1, device_id={"ctx": chain.place + 1}, device_id_type=MESH)

    inner = chain.has_last & chain.has_next

    @pl.when(inner)
    def _():
        pl.semaphore_wait(barrier, len(targets) + 2)

    @pl.when(jnp.logical_not(inner))
    def _():
        pl.semaphore_wait(barrier, len(targets) + 1)


def along(src, dst, send_sem, recv_sem, place):
    return pltpu.make_async_remote_copy(
        src_ref=src,
        dst_ref=dst,
        send_sem=send_sem,
        recv_sem=recv_sem,
        device_id={"ctx": place},
        device_id_type=MESH,
    )


def spread_heads(source, spread):
    rows = source.shape[0]
    low = lax.broadcasted_iota(jnp.int32, (rows, 128), 1) < 64
    for pair in range(source.shape[1] // 256):
        first = source[:, pair * 256 : pair * 256 + 128].astype(F32)
        second = source[:, pair * 256 + 128 : pair * 256 + 256].astype(F32)
        spread[4 * pair] = jnp.where(low, first, 0.0).astype(BF16)
        spread[4 * pair + 1] = jnp.where(low, pltpu.roll(first, 64, 1), 0.0).astype(BF16)
        spread[4 * pair + 2] = jnp.where(low, 0.0, pltpu.roll(second, 64, 1)).astype(BF16)
        spread[4 * pair + 3] = jnp.where(low, 0.0, second).astype(BF16)


def join_heads(spread, target):
    rows = target.shape[0]
    low = lax.broadcasted_iota(jnp.int32, (rows, 128), 1) < 64
    for pair in range(target.shape[1] // 256):
        parts = [spread(4 * pair + i).T for i in range(4)]
        target[:, pair * 256 : pair * 256 + 128] = jnp.where(low, parts[0], pltpu.roll(parts[1], 64, 1))
        target[:, pair * 256 + 128 : pair * 256 + 256] = jnp.where(low, pltpu.roll(parts[2], 64, 1), parts[3])


def mask_block(bias, length, place, block):
    rows = bias.shape[0]
    key_at = block * rows + lax.broadcasted_iota(jnp.int32, bias.shape, 0)
    query_at = place * rows + lax.broadcasted_iota(jnp.int32, bias.shape, 1)
    bias[...] = jnp.where((key_at <= query_at) & (key_at < length), 0.0, NEGATIVE)


def dot_right(left, right):
    return lax.dot_general(left, right, (((1,), (1,)), ((), ())), preferred_element_type=F32)


def dot_plain(left, right):
    return jnp.dot(left, right, preferred_element_type=F32)


def attend_kernel(
    n_ctx,
    length_ref,
    query,
    kv,
    d_block,
    gate_in,
    up_in,
    down_in,
    attended,
    log_total,
    kv_all,
    d_all,
    gate_out,
    up_out,
    down_out,
    w_gate,
    w_up,
    w_down,
    keep_sem,
    spread,
    bias,
    peak,
    total,
    out_t,
    kv_send,
    kv_recv,
    d_send,
    d_recv,
    d_own,
    send_sem,
    recv_sem,
    pair_send,
    pair_recv,
    own_sem,
):
    chain = Chain(n_ctx)
    place = chain.place
    section = lax.axis_index("section")
    me, beside, across, opposite = corners()
    greet_mixed(
        chain,
        [{"fsdp": beside}, {"fsdp": across}, {"fsdp": opposite}, {"section": 1 - section}],
    )
    rows = query.shape[0]
    half_width = kv.shape[1] // 2

    def block_rows(block):
        return pl.ds(pl.multiple_of(block * rows, rows), rows)

    def upward(step, src):
        return along(
            src,
            kv_all.at[block_rows(place - step)],
            kv_send.at[step],
            kv_recv.at[step + 1],
            place + 1,
        )

    def arriving(step):
        at = kv_all.at[block_rows(place - step)]
        return along(at, at, kv_send.at[step], kv_recv.at[step], place)

    @pl.when(chain.has_next)
    def _():
        upward(0, kv).start()

    gather = SideGather(d_block, d_all, d_send, d_recv, d_own)
    gather.start()
    columns = Columns(
        1, (gate_in, up_in, down_in), (w_gate, w_up, w_down), send_sem, recv_sem, pair_send, pair_recv, own_sem
    )
    columns.start()
    kv_all[block_rows(place)] = kv[...]
    spread_heads(query, spread)
    peak[...] = jnp.full(peak.shape, NEGATIVE, F32)
    total[...] = jnp.zeros(total.shape, F32)
    out_t[...] = jnp.zeros(out_t.shape, F32)
    length = length_ref[0]
    scale = 64 ** (-0.5)

    def attend_block(block):
        mask_block(bias, length, place, block)
        for pair in range(half_width // 128):
            key = kv_all[block_rows(block), pair * 128 : pair * 128 + 128]
            value_t = kv_all[block_rows(block), half_width + pair * 128 : half_width + pair * 128 + 128].T
            for index in range(4):
                head = 4 * pair + index
                scores = dot_right(key, spread[head]) * scale + bias[...]
                before = peak[head]
                now = jnp.maximum(before, jnp.max(scores, axis=0, keepdims=True))
                weights = jnp.exp(scores - now)
                fade = jnp.exp(before - now)
                peak[head] = now
                total[head] = total[head] * fade + jnp.sum(weights, axis=0, keepdims=True)
                out_t[head] = out_t[head] * fade + dot_plain(value_t, weights.astype(BF16))

    attend_block(place)
    gather.relay()

    def step_on(step, carry):
        @pl.when(step <= place)
        def _():
            arriving(step).wait_recv()

            @pl.when(chain.has_next)
            def _():
                upward(step, kv_all.at[block_rows(place - step)]).start()

            attend_block(place - step)

        return carry

    lax.fori_loop(1, n_ctx, step_on, 0)
    join_heads(lambda head: out_t[head] / total[head], attended)
    for head in range(spread.shape[0]):
        log_total[head] = peak[head] + jnp.log(total[head])
    columns.relay()
    columns.arrive()
    keeping = [
        pltpu.make_async_copy(src, dst, keep_sem.at[index])
        for index, (src, dst) in enumerate(((w_gate, gate_out), (w_up, up_out), (w_down, down_out)))
    ]
    for copy in keeping:
        copy.start()
    gather.finish()
    columns.finish()
    for copy in keeping:
        copy.wait()

    def settle(step, carry):
        @pl.when((step <= place) & chain.has_next)
        def _():
            upward(step, kv_all.at[block_rows(place - step)]).wait_send()

        return carry

    lax.fori_loop(0, n_ctx, settle, 0)


def attend(length, query, kv, d_block, gate, up, down, collective_id):
    n_ctx, count = lax.axis_size("ctx"), lax.axis_size("fsdp")
    rows, width = query.shape
    heads = width // 64
    dma = pltpu.SemaphoreType.DMA
    vmem = pl.BlockSpec(memory_space=pltpu.VMEM)
    hbm = pl.BlockSpec(memory_space=pl.ANY)
    column = jax.ShapeDtypeStruct((count * gate.shape[0], gate.shape[1] // count), gate.dtype)
    return pl.pallas_call(
        functools.partial(attend_kernel, n_ctx),
        out_shape=(
            jax.ShapeDtypeStruct((rows, width), F32),
            jax.ShapeDtypeStruct((heads, 1, rows), F32),
            jax.ShapeDtypeStruct((n_ctx * rows, kv.shape[1]), BF16),
            jax.ShapeDtypeStruct((count * rows, d_block.shape[1]), BF16),
            column,
            column,
            jax.ShapeDtypeStruct(down.shape, down.dtype),
        ),
        in_specs=[pl.BlockSpec(memory_space=pltpu.SMEM), vmem, vmem, vmem, hbm, hbm, hbm],
        out_specs=[vmem, vmem, vmem, vmem, hbm, hbm, hbm],
        scratch_shapes=[
            pltpu.VMEM(column.shape, BF16),
            pltpu.VMEM(column.shape, BF16),
            pltpu.VMEM(down.shape, BF16),
            dma((3,)),
            pltpu.VMEM((heads, rows, 128), BF16),
            pltpu.VMEM((rows, rows), F32),
            pltpu.VMEM((heads, 1, rows), F32),
            pltpu.VMEM((heads, 1, rows), F32),
            pltpu.VMEM((heads, 128, rows), F32),
            dma((n_ctx + 1,)),
            dma((n_ctx + 1,)),
            dma((4,)),
            dma((4,)),
            dma,
            dma((2, count)),
            dma((2, count)),
            dma((3, count)),
            dma((3, count)),
            dma((3,)),
        ],
        compiler_params=pltpu.CompilerParams(
            collective_id=collective_id, has_side_effects=True, vmem_limit_bytes=58 << 20
        ),
        cost_estimate=busy(50),
    )(length, query, kv, d_block, gate, up, down)


def attend_back_kernel(
    n_ctx,
    length_ref,
    query,
    kv_all,
    d_out,
    log_total,
    delta,
    blocks,
    d_query,
    d_kv,
    reduced_out,
    spread,
    d_spread,
    bias,
    d_query_t,
    term,
    leaving,
    coming,
    kv_send,
    kv_recv,
    beside_got,
    across_got,
    passed,
    passed_got,
    send_sem,
    recv_sem,
):
    chain = Chain(n_ctx)
    place = chain.place
    _, beside, across, _ = corners()
    greet_mixed(chain, [{"fsdp": beside}, {"fsdp": across}])
    rows = query.shape[0]
    half_width = kv_all.shape[1] // 2
    reduction = SideReduce(blocks, reduced_out, beside_got, across_got, passed, passed_got, send_sem, recv_sem)
    reduction.start()
    spread_heads(query, spread)
    spread_heads(d_out, d_spread)
    d_query_t[...] = jnp.zeros(d_query_t.shape, F32)
    length = length_ref[0]
    scale = 64 ** (-0.5)

    def downward(block):
        return along(leaving.at[block], coming.at[block], kv_send.at[block], kv_recv.at[block], place - 1)

    def step_on(block, carry):
        @pl.when(block <= place)
        def _():
            mask_block(bias, length, place, block)
            at = pl.ds(pl.multiple_of(block * rows, rows), rows)
            for pair in range(half_width // 128):
                lanes = slice(pair * 128, pair * 128 + 128)
                more = slice(half_width + pair * 128, half_width + pair * 128 + 128)
                key = kv_all[at, lanes]
                value = kv_all[at, more]
                key_t = key.T
                d_key = jnp.zeros((rows, 128), F32)
                d_value = jnp.zeros((rows, 128), F32)
                for index in range(4):
                    head = 4 * pair + index
                    scores = dot_right(key, spread[head]) * scale + bias[...]
                    prob = jnp.exp(scores - log_total[head])
                    d_prob = dot_right(value, d_spread[head])
                    d_scores = (prob * (d_prob - delta[head])).astype(BF16)
                    d_value = d_value + dot_plain(prob.astype(BF16), d_spread[head])
                    d_key = d_key + dot_plain(d_scores, spread[head])
                    d_query_t[head] = d_query_t[head] + dot_plain(key_t, d_scores)
                term[:, lanes] = d_key * scale
                term[:, more] = d_value

            @pl.when(chain.has_next)
            def _():
                along(
                    leaving.at[block], coming.at[block], kv_send.at[block], kv_recv.at[block], place
                ).wait_recv()
                term[...] = term[...] + coming[block].astype(F32)

            @pl.when(block < place)
            def _():
                leaving[block] = term[...].astype(BF16)
                downward(block).start()

            @pl.when(block == place)
            def _():
                d_kv[...] = term[...]

        @pl.when(block == 0)
        def _():
            reduction.relay()

        return carry

    lax.fori_loop(0, n_ctx, step_on, 0)
    join_heads(lambda head: d_query_t[head] * scale, d_query)
    reduction.finish()

    def settle(block, carry):
        @pl.when(block < place)
        def _():
            downward(block).wait_send()

        return carry

    lax.fori_loop(0, n_ctx, settle, 0)


def attend_back(length, query, kv_all, d_out, log_total, delta, blocks, collective_id):
    n_ctx = lax.axis_size("ctx")
    rows, width = query.shape
    heads = width // 64
    dma = pltpu.SemaphoreType.DMA
    vmem = pl.BlockSpec(memory_space=pltpu.VMEM)
    wide = jax.ShapeDtypeStruct((rows, width), F32)
    pair = pltpu.VMEM((2, rows // 2, blocks.shape[1]), BF16)
    return pl.pallas_call(
        functools.partial(attend_back_kernel, n_ctx),
        out_shape=(wide, jax.ShapeDtypeStruct((rows, kv_all.shape[1]), F32), wide),
        in_specs=[pl.BlockSpec(memory_space=pltpu.SMEM)] + [vmem] * 6,
        out_specs=[vmem] * 3,
        scratch_shapes=[
            pltpu.VMEM((heads, rows, 128), BF16),
            pltpu.VMEM((heads, rows, 128), BF16),
            pltpu.VMEM((rows, rows), F32),
            pltpu.VMEM((heads, 128, rows), F32),
            pltpu.VMEM((rows, kv_all.shape[1]), F32),
            pltpu.VMEM((n_ctx, rows, kv_all.shape[1]), BF16),
            pltpu.VMEM((n_ctx, rows, kv_all.shape[1]), BF16),
            dma((n_ctx,)),
            dma((n_ctx,)),
            pair,
            pair,
            pair,
            pair,
            dma((6,)),
            dma((6,)),
        ],
        compiler_params=pltpu.CompilerParams(
            collective_id=collective_id, has_side_effects=True, vmem_limit_bytes=56 << 20
        ),
        cost_estimate=busy(50),
    )(length, query, kv_all, d_out, log_total, delta, blocks)


class MixerGather:
    def __init__(self, sources, targets, send_sem, recv_sem, pair_send, pair_recv, own_sem):
        self.section = section = lax.axis_index("section")
        me, beside, across, opposite = corners()
        rows = sources[0].shape[0]
        half = rows // 2
        quarter = half // 2

        def at_rows(out, owner, extra, size):
            return out.at[pl.ds(pl.multiple_of(owner * rows + extra, quarter), size)]

        def pair(slot, at):
            return pltpu.make_async_remote_copy(
                src_ref=at,
                dst_ref=at,
                send_sem=pair_send.at[slot],
                recv_sem=pair_recv.at[slot],
                device_id={"section": 1 - section},
                device_id_type=MESH,
            )

        self.direct, self.onward, self.early, self.late, self.own = [], [], [], [], []
        start = section * half
        for index, (source, out) in enumerate(zip(sources, targets)):
            mine = source.at[pl.ds(pl.multiple_of(start, half), half)]
            spot = at_rows(out, me, start, half)
            slot = 4 * index
            self.direct.append(
                [
                    to_side(mine, spot, send_sem.at[slot], recv_sem.at[slot], beside),
                    to_side(mine, spot, send_sem.at[slot + 1], recv_sem.at[slot + 1], across),
                ]
            )
            passing = at_rows(out, beside, start, quarter), at_rows(out, across, start + quarter, quarter)
            self.onward.append(
                [
                    to_side(passing[0], passing[0], send_sem.at[slot + 2], recv_sem.at[slot + 2], across),
                    to_side(passing[1], passing[1], send_sem.at[slot + 3], recv_sem.at[slot + 3], beside),
                ]
            )
            self.early.append(
                [
                    pair(slot, at_rows(out, beside, start, half)),
                    pair(slot + 1, at_rows(out, across, start, half)),
                ]
            )
            self.late.append(
                [
                    pair(slot + 2, at_rows(out, opposite, start, quarter)),
                    pair(slot + 3, at_rows(out, opposite, start + quarter, quarter)),
                ]
            )
            self.own.append(pltpu.make_async_copy(source, at_rows(out, me, 0, rows), own_sem.at[index]))

    def start(self):
        for copies in self.direct:
            for copy in copies:
                copy.start()
        for copy in self.own:
            copy.start()

    def relay(self):
        for direct, onward, early in zip(self.direct, self.onward, self.early):
            for turn in range(2):
                direct[turn].wait_recv()
                onward[turn].start()
                early[turn].start()

    def relay_last(self):
        for onward, late in zip(self.onward, self.late):
            for turn in range(2):
                onward[turn].wait_recv()
                late[turn].start()

    def arrive(self, index):
        self.own[index].wait()
        for copy in self.early[index] + self.late[index]:
            copy.wait_recv()

    def finish(self):
        for group in (self.direct, self.onward, self.early, self.late):
            for copies in group:
                for copy in copies:
                    copy.wait_send()


def front_kernel(
    n_ctx,
    x_ref,
    gains,
    taps,
    conv_in,
    conv_out,
    gate_in,
    up_in,
    down_in,
    in_out,
    out_out,
    gate_out,
    up_out,
    down_out,
    projected,
    convolved,
    z_low,
    mixed,
    rim,
    act_all,
    w_in,
    w_out,
    w_gate,
    w_up,
    w_down,
    act1,
    act2,
    last_rows,
    rim_sem,
    mix_send,
    mix_recv,
    mix_pair_send,
    mix_pair_recv,
    mix_own,
    send_sem,
    recv_sem,
    pair_send,
    pair_recv,
    own_sem,
    plane_send,
    plane_recv,
    act_send,
    act_recv,
    act_own,
    keep_sem,
):
    chain = Chain(n_ctx)
    section = lax.axis_index("section")
    _, beside, across, opposite = corners()
    greet_mixed(
        chain,
        [{"fsdp": beside}, {"fsdp": across}, {"fsdp": opposite}, {"section": 1 - section}],
    )
    mixers = MixerGather(
        (conv_in, conv_out), (w_in, w_out), mix_send, mix_recv, mix_pair_send, mix_pair_recv, mix_own
    )
    mixers.start()
    columns = SharedColumns(
        0,
        (gate_in, up_in, down_in),
        (w_gate, w_up, w_down),
        send_sem,
        recv_sem,
        pair_send,
        pair_recv,
        own_sem,
        plane_send,
        plane_recv,
    )
    gather = SideGather(act2, act_all, act_send, act_recv, act_own)
    keeping = [
        pltpu.make_async_copy(src, dst, keep_sem.at[index])
        for index, (src, dst) in enumerate(
            ((w_in, in_out), (w_out, out_out), (w_gate, gate_out), (w_up, up_out), (w_down, down_out))
        )
    ]
    rows, width = x_ref.shape
    strip = 64

    def normalize(values, gain):
        inv_rms = lax.rsqrt(jnp.mean(values * values, axis=-1, keepdims=True) + EPSILON)
        return (values * inv_rms * gain).astype(BF16)

    def first_norm(index, carry):
        at = pl.ds(pl.multiple_of(index * strip, strip), strip)
        act1[at] = normalize(x_ref[at].astype(F32), gains[0:1])
        return carry

    lax.fori_loop(0, rows // strip, first_norm, 0)
    mixers.relay()
    columns.start()
    mixers.relay_last()
    mixers.arrive(0)
    keeping[0].start()
    wide = 512

    def project(index, carry):
        at = pl.ds(pl.multiple_of(index * wide, wide), wide)
        projected[:, at] = dot_plain(act1[...], w_in[:, at])
        return carry

    lax.fori_loop(0, projected.shape[1] // wide, project, 0)
    tail_at = pl.ds(rows - 16, 16)
    last_rows[...] = (projected[tail_at, :width] * projected[tail_at, 2 * width :]).astype(BF16)
    to_next = along(last_rows, rim, rim_sem.at[0], rim_sem.at[1], chain.place + 1)

    @pl.when(chain.has_next)
    def _():
        to_next.start()

    @pl.when(chain.has_last)
    def _():
        along(last_rows, rim, rim_sem.at[0], rim_sem.at[1], chain.place).wait_recv()

    @pl.when(jnp.logical_not(chain.has_last))
    def _():
        rim[...] = jnp.zeros(rim.shape, BF16)

    part = 128
    row_at = lax.broadcasted_iota(jnp.int32, (rows, part), 0)

    def convolve(index, carry):
        def lanes(offset):
            return pl.ds(pl.multiple_of(offset * width + index * part, part), part)

        product = (projected[:, lanes(0)] * projected[:, lanes(2)]).astype(BF16).astype(F32)
        edge = rim[:, lanes(0)].astype(F32)
        near, far = edge[15:16], edge[14:15]
        one = jnp.where(row_at >= 1, pltpu.roll(product, 1, 0), near)
        two = jnp.where(row_at >= 2, pltpu.roll(product, 2, 0), jnp.where(row_at == 1, near, far))
        tap = taps[:, lanes(0)]
        value = tap[0:1] * two + tap[1:2] * one + tap[2:3] * product
        convolved[:, lanes(0)] = value
        z_low[:, lanes(0)] = (projected[:, lanes(1)] * value).astype(BF16)
        return carry

    lax.fori_loop(0, width // part, convolve, 0)
    mixers.arrive(1)
    keeping[1].start()

    def mix(index, carry):
        at = pl.ds(pl.multiple_of(index * wide, wide), wide)
        mixed[:, at] = dot_plain(z_low[...], w_out[:, at])
        return carry

    lax.fori_loop(0, width // wide, mix, 0)

    def second_norm(index, carry):
        at = pl.ds(pl.multiple_of(index * strip, strip), strip)
        act2[at] = normalize(x_ref[at].astype(F32) + mixed[at], gains[1:2])
        return carry

    lax.fori_loop(0, rows // strip, second_norm, 0)
    gather.start()
    columns.relay()
    gather.relay()
    columns.relay_passed()
    columns.arrive()
    for copy in keeping[2:]:
        copy.start()
    gather.finish()
    columns.finish()
    mixers.finish()

    @pl.when(chain.has_next)
    def _():
        to_next.wait_send()

    for copy in keeping:
        copy.wait()


def front(x_low, gains, taps, conv_in, conv_out, gate, up, down, collective_id):
    n_ctx, count = lax.axis_size("ctx"), lax.axis_size("fsdp")
    assert count == 4
    rows, width = x_low.shape
    dma = pltpu.SemaphoreType.DMA
    vmem = pl.BlockSpec(memory_space=pltpu.VMEM)
    hbm = pl.BlockSpec(memory_space=pl.ANY)

    def whole(weight):
        return (count * weight.shape[0], weight.shape[1])

    column = (count * gate.shape[0], gate.shape[1] // count)
    weights = [whole(conv_in), whole(conv_out), column, column, down.shape]
    return pl.pallas_call(
        functools.partial(front_kernel, n_ctx),
        out_shape=tuple(jax.ShapeDtypeStruct(shape, BF16) for shape in weights)
        + (
            jax.ShapeDtypeStruct((rows, conv_in.shape[1]), F32),
            jax.ShapeDtypeStruct((rows, width), F32),
            jax.ShapeDtypeStruct((rows, width), BF16),
            jax.ShapeDtypeStruct((rows, width), F32),
            jax.ShapeDtypeStruct((16, width), BF16),
            jax.ShapeDtypeStruct((count * rows, width), BF16),
        ),
        in_specs=[vmem] * 3 + [hbm] * 5,
        out_specs=[hbm] * 5 + [vmem] * 6,
        scratch_shapes=[pltpu.VMEM(shape, BF16) for shape in weights]
        + [
            pltpu.VMEM((rows, width), BF16),
            pltpu.VMEM((rows, width), BF16),
            pltpu.VMEM((16, width), BF16),
            dma((2,)),
            dma((8,)),
            dma((8,)),
            dma((8,)),
            dma((8,)),
            dma((2,)),
            dma((2, count)),
            dma((2, count)),
            dma((3, count)),
            dma((3, count)),
            dma((3,)),
            dma((2, count)),
            dma((2, count)),
            dma((4,)),
            dma((4,)),
            dma,
            dma((5,)),
        ],
        compiler_params=pltpu.CompilerParams(
            collective_id=collective_id, has_side_effects=True, vmem_limit_bytes=58 << 20
        ),
        cost_estimate=busy(70),
    )(x_low, gains, taps, conv_in, conv_out, gate, up, down)


def turn_kernel(
    act_block,
    w_gate_in,
    w_up_in,
    w_down_in,
    d_all_in,
    terms,
    total,
    shared_gu,
    shared_down,
    w_gate,
    w_up,
    w_down,
    d_all,
    load_sem,
    act,
    hidden,
    d_gate,
    d_up,
    blocks,
    act_send,
    act_recv,
    act_own,
    gu_all,
    gu_got,
    gu_sum,
    down_all,
    down_got,
    down_sum,
    keep_sem,
    beside_got,
    across_got,
    passed,
    passed_got,
    send_sem,
    recv_sem,
    pair_send,
    pair_recv,
):
    section = lax.axis_index("section")
    other = 1 - section
    _, beside, across, _ = corners()
    barrier = pltpu.get_barrier_semaphore()
    for target in ({"fsdp": beside}, {"fsdp": across}, {"section": other}):
        pl.semaphore_signal(barrier, inc=1, device_id=target, device_id_type=MESH)
    pl.semaphore_wait(barrier, 3)
    reduction = SideReduce(blocks, total, beside_got, across_got, passed, passed_got, send_sem, recv_sem)
    gather = SideGather(act_block, act, act_send, act_recv, act_own)
    gather.start()
    loads = [
        pltpu.make_async_copy(src, dst, load_sem.at[index])
        for index, (src, dst) in enumerate(
            ((w_gate_in, w_gate), (w_up_in, w_up), (d_all_in, d_all), (w_down_in, w_down))
        )
    ]
    for copy in loads:
        copy.start()
    me, _, _, opposite = corners()
    rows = act_block.shape[0]
    wide, width = w_down.shape
    lanes_wide, lanes_out = 384, 1024

    def turn(owner):
        at = pl.ds(pl.multiple_of(owner * rows, rows), rows)

        def hidden_part(index, carry):
            lanes = pl.ds(pl.multiple_of(index * lanes_wide, 128), lanes_wide)
            gate_pre = dot_plain(act[at], w_gate[:, lanes])
            up_pre = dot_plain(act[at], w_up[:, lanes])
            d_hidden = dot_right(d_all[at], w_down[lanes])
            sigmoid = jax.nn.sigmoid(gate_pre)
            silu = gate_pre * sigmoid
            hidden[at, lanes] = (silu * up_pre).astype(BF16)
            d_up[at, lanes] = (d_hidden * silu).astype(BF16)
            d_gate[at, lanes] = (
                d_hidden * up_pre * sigmoid * (1.0 + gate_pre * (1.0 - sigmoid))
            ).astype(BF16)
            return carry

        lax.fori_loop(0, wide // lanes_wide, hidden_part, 0)

        def out_part(index, carry):
            lanes = pl.ds(pl.multiple_of(index * lanes_out, 128), lanes_out)
            terms[at, lanes] = dot_plain(hidden[at], w_down[:, lanes]).astype(BF16)
            blocks[at, lanes] = (
                dot_right(d_gate[at], w_gate[lanes]) + dot_right(d_up[at], w_up[lanes])
            ).astype(BF16)
            return carry

        lax.fori_loop(0, width // lanes_out, out_part, 0)

    gather.own.wait()
    for copy in loads:
        copy.wait()
    turn(me)
    gather.relay()
    turn(beside)
    turn(across)
    reduction.copies[1].start()
    reduction.copies[3].start()
    gather.third.wait_recv()
    gather.fourth.wait_recv()
    turn(opposite)
    reduction.copies[0].start()
    reduction.copies[2].start()
    tile = 256
    half = gu_got.shape[2]
    strips, owners, kinds, strip, _ = gu_sum.shape

    def gate_swap(kind, owner):
        start = owner * (2 * half) + other * half
        return pltpu.make_async_remote_copy(
            src_ref=gu_all.at[kind, pl.ds(pl.multiple_of(start, half), half)],
            dst_ref=gu_got.at[kind, owner],
            send_sem=pair_send.at[kind * owners + owner],
            recv_sem=pair_recv.at[kind * owners + owner],
            device_id={"section": other},
            device_id_type=MESH,
        )

    for kind, right in enumerate((d_gate, d_up)):

        def column(owner, carry, kind=kind, right=right):
            lanes = pl.ds(pl.multiple_of(owner * tile, tile), tile)
            gu_all[kind, lanes] = dot_plain(act[:, lanes].T, right[...]).astype(BF16)
            gate_swap(kind, owner).start()
            return carry

        lax.fori_loop(0, owners, column, 0)
    reduction.relay()
    height = hidden.shape[1]

    def down_tile(index, carry):
        lanes = pl.ds(pl.multiple_of(index * tile, tile), tile)
        down_all[lanes] = dot_plain(hidden[:, lanes].T, d_all[...]).astype(BF16)
        return carry

    lax.fori_loop(0, height // tile, down_tile, 0)
    rest = height // tile * tile
    if rest < height:
        down_all[rest:] = dot_plain(hidden[:, rest:].T, d_all[...]).astype(BF16)
    down_half = height // 2
    down_swap = pltpu.make_async_remote_copy(
        src_ref=down_all.at[pl.ds(pl.multiple_of(other * down_half, 16), down_half)],
        dst_ref=down_got,
        send_sem=pair_send.at[kinds * owners],
        recv_sem=pair_recv.at[kinds * owners],
        device_id={"section": other},
        device_id_type=MESH,
    )
    down_swap.start()

    def join(index, carry):
        place = index // (owners * kinds)
        left = lax.rem(index, owners * kinds)
        owner, kind = left // kinds, lax.rem(left, kinds)

        @pl.when(place == 0)
        def _():
            gate_swap(kind, owner).wait_recv()

        mine = pl.ds(pl.multiple_of(owner * (2 * half) + section * half + place * strip, strip), strip)
        theirs = pl.ds(pl.multiple_of(place * strip, strip), strip)
        gu_sum[place, owner, kind] = (
            gu_all[kind, mine].astype(F32) + gu_got[kind, owner, theirs].astype(F32)
        ).astype(BF16)
        return carry

    lax.fori_loop(0, strips * owners * kinds, join, 0)
    keeping = [pltpu.make_async_copy(gu_sum, shared_gu, keep_sem.at[0])]
    keeping[0].start()
    down_swap.wait_recv()
    piece = 64

    def join_down(index, carry):
        theirs = pl.ds(pl.multiple_of(index * piece, piece), piece)
        mine = pl.ds(pl.multiple_of(section * down_half + index * piece, piece), piece)
        down_sum[theirs] = (down_all[mine].astype(F32) + down_got[theirs].astype(F32)).astype(BF16)
        return carry

    lax.fori_loop(0, down_half // piece, join_down, 0)
    keeping.append(pltpu.make_async_copy(down_sum, shared_down, keep_sem.at[1]))
    keeping[1].start()
    reduction.finish()

    def settle(index, carry):
        gate_swap(index // owners, lax.rem(index, owners)).wait_send()
        return carry

    lax.fori_loop(0, kinds * owners, settle, 0)
    down_swap.wait_send()
    for copy in (gather.first, gather.second, gather.third, gather.fourth):
        copy.wait_send()
    for copy in keeping:
        copy.wait()


def ffn_turn(act_block, w_gate, w_up, w_down, d_all, collective_id):
    n_ctx, owners = lax.axis_size("ctx"), lax.axis_size("fsdp")
    rows, width = act_block.shape
    wide = w_gate.shape[1]
    half = width // owners // 2
    dma = pltpu.SemaphoreType.DMA
    vmem = pl.BlockSpec(memory_space=pltpu.VMEM)
    hbm = pl.BlockSpec(memory_space=pl.ANY)
    pair = pltpu.VMEM((2, rows // 2, width), BF16)
    summed = (n_ctx, owners, 2, half // n_ctx, wide)
    assert width // owners == 256 and wide // 2 % 64 == 0 and wide % 384 == 0
    whole = (owners * rows, width)
    columns = pltpu.VMEM((owners * rows, wide), BF16)
    return pl.pallas_call(
        turn_kernel,
        out_shape=(
            jax.ShapeDtypeStruct(whole, BF16),
            jax.ShapeDtypeStruct((rows, width), F32),
            jax.ShapeDtypeStruct(summed, BF16),
            jax.ShapeDtypeStruct((wide // 2, width), BF16),
        ),
        in_specs=[vmem] + [hbm] * 4,
        out_specs=[vmem, vmem, hbm, hbm],
        scratch_shapes=[pltpu.VMEM(k.shape, BF16) for k in (w_gate, w_up, w_down, d_all)]
        + [
            dma((4,)),
            pltpu.VMEM(whole, BF16),
            columns,
            columns,
            columns,
            pltpu.VMEM(whole, BF16),
            dma((4,)),
            dma((4,)),
            dma,
            pltpu.VMEM((2, width, wide), BF16),
            pltpu.VMEM((2, owners, half, wide), BF16),
            pltpu.VMEM(summed, BF16),
            pltpu.VMEM((wide, width), BF16),
            pltpu.VMEM((wide // 2, width), BF16),
            pltpu.VMEM((wide // 2, width), BF16),
            dma((2,)),
            pair,
            pair,
            pair,
            pair,
            dma((6,)),
            dma((6,)),
            dma((2 * owners + 1,)),
            dma((2 * owners + 1,)),
        ],
        compiler_params=pltpu.CompilerParams(
            collective_id=collective_id, has_side_effects=True, vmem_limit_bytes=58 << 20
        ),
        cost_estimate=busy(45),
    )(act_block, w_gate, w_up, w_down, d_all)


def back_kernel(
    n_ctx,
    x_ref,
    mixed,
    d_h,
    gains,
    taps,
    z_low,
    rim,
    act_qkv,
    d_query,
    d_key_value,
    attended,
    d_attended,
    gate_pre_in,
    up_pre_in,
    w_down_in,
    w_gate_in,
    w_up_in,
    act_in,
    hidden_in,
    w_in_in,
    w_out_in,
    projected_in,
    convolved_in,
    gate_grad,
    up_grad,
    down_grad,
    q_grad,
    kv_grad,
    proj_grad,
    b_grad,
    c_grad,
    x_grad,
    o_grad,
    d_x,
    small,
    w_down,
    w_gate,
    w_up,
    act,
    hidden,
    w_in,
    w_out,
    projected,
    convolved,
    load_sem,
    pre,
    pre_sem,
    d_all,
    d_gate,
    d_up,
    blocks,
    d_send,
    d_recv,
    d_own,
    stage_wide,
    stage,
    stage_sem,
    beside_got,
    across_got,
    passed,
    passed_got,
    send_sem,
    recv_sem,
    d_act,
    d_res,
    d_mixed,
    d_conv,
    d_proj,
    act1,
    edge,
    next_edge,
    edge_sem,
):
    chain = Chain(n_ctx)
    me, beside, across, opposite = corners()
    greet_mixed(chain, [{"fsdp": beside}, {"fsdp": across}])
    gather = SideGather(d_h, d_all, d_send, d_recv, d_own)
    gather.start()
    reduction = SideReduce(blocks, d_act, beside_got, across_got, passed, passed_got, send_sem, recv_sem)

    def fetch(owner, slot):
        at = pl.ds(pl.multiple_of(owner * x_ref.shape[0], x_ref.shape[0]), x_ref.shape[0])
        return [
            pltpu.make_async_copy(source.at[at], pre.at[slot, kind], pre_sem.at[slot, kind])
            for kind, source in enumerate((gate_pre_in, up_pre_in))
        ]

    loads = [
        pltpu.make_async_copy(src, dst, load_sem.at[index])
        for index, (src, dst) in enumerate(
            (
                (w_down_in, w_down),
                (w_gate_in, w_gate),
                (w_up_in, w_up),
                (act_in, act),
                (hidden_in, hidden),
                (convolved_in, convolved),
                (projected_in, projected),
                (w_out_in, w_out),
                (w_in_in, w_in),
            )
        )
    ]
    for copy in fetch(me, 0) + loads[:3] + fetch(beside, 1) + loads[3:]:
        copy.start()
    rows, width = x_ref.shape
    wide = w_gate.shape[1]
    tile = 256
    small[...] = jnp.zeros(small.shape, F32)

    def weight_grad(left, right, at_right, target, staging, slot):
        count = left.shape[1] // tile

        def leaving(index, at):
            return pltpu.make_async_copy(staging.at[at], target.at[index], stage_sem.at[slot + at])

        def step(index, carry):
            at = lax.rem(index, 2)
            lanes = pl.ds(pl.multiple_of(index * tile, tile), tile)

            @pl.when(index >= 2)
            def _():
                leaving(lanes, at).wait()

            staging[at] = dot_plain(left[:, lanes].T, right[:, at_right]).astype(BF16)
            leaving(lanes, at).start()
            return carry

        lax.fori_loop(0, count, step, 0)
        for index in range(min(2, count)):
            leaving(pl.ds(0, tile), index).wait()

    lanes_wide, lanes_out = 384, 512

    def turn(owner, slot, after):
        at = pl.ds(pl.multiple_of(owner * rows, rows), rows)
        for copy in fetch(owner, slot):
            copy.wait()

        def hidden_part(index, carry):
            lanes = pl.ds(pl.multiple_of(index * lanes_wide, 128), lanes_wide)
            gate_pre, up_pre = pre[slot, 0, :, lanes], pre[slot, 1, :, lanes]
            d_hidden = dot_right(d_all[at], w_down[lanes])
            sigmoid = jax.nn.sigmoid(gate_pre)
            d_up[at, lanes] = (d_hidden * gate_pre * sigmoid).astype(BF16)
            d_gate[at, lanes] = (
                d_hidden * up_pre * sigmoid * (1.0 + gate_pre * (1.0 - sigmoid))
            ).astype(BF16)
            return carry

        lax.fori_loop(0, wide // lanes_wide, hidden_part, 0)
        if after is not None:
            for copy in fetch(after, slot):
                copy.start()

        def out_part(index, carry):
            lanes = pl.ds(pl.multiple_of(index * lanes_out, 128), lanes_out)
            blocks[at, lanes] = (
                dot_right(d_gate[at], w_gate[lanes]) + dot_right(d_up[at], w_up[lanes])
            ).astype(BF16)
            return carry

        lax.fori_loop(0, width // lanes_out, out_part, 0)

    gather.own.wait()
    for copy in loads[:3]:
        copy.wait()
    turn(me, 0, across)
    for left, right, target in (
        (act_qkv, d_query, q_grad),
        (act_qkv, d_key_value, kv_grad),
        (attended, d_attended, proj_grad),
    ):
        weight_grad(left, right, slice(None), target, stage, 2)
    gather.relay()
    turn(beside, 1, opposite)
    turn(across, 0, None)
    reduction.copies[1].start()
    reduction.copies[3].start()
    gather.third.wait_recv()
    gather.fourth.wait_recv()
    turn(opposite, 1, None)
    reduction.copies[0].start()
    reduction.copies[2].start()
    loads[3].wait()
    weight_grad(act, d_gate, slice(None), gate_grad, stage_wide, 0)
    weight_grad(act, d_up, slice(None), up_grad, stage_wide, 0)
    reduction.relay()
    loads[4].wait()
    odd = hidden.shape[1] % tile

    weight_grad(hidden, d_all, slice(None), down_grad, stage, 2)
    if odd:
        last = hidden.shape[1] - odd
        stage[0, :odd] = dot_plain(hidden[:, last:].T, d_all[...]).astype(BF16)
        copy = pltpu.make_async_copy(stage.at[0, pl.ds(0, odd)], down_grad.at[pl.ds(last, odd)], stage_sem.at[2])
        copy.start()
        copy.wait()
    reduction.finish()
    strip = 64

    def norm_strip(at, values, gain, d_values, row):
        inv_rms = lax.rsqrt(jnp.mean(values * values, axis=-1, keepdims=True) + EPSILON)
        normed = values * inv_rms
        small[row : row + 1] = small[row : row + 1] + jnp.sum(d_values * normed, axis=0, keepdims=True)
        d_normed = d_values * gain
        return inv_rms * d_normed - normed * inv_rms * jnp.mean(d_normed * normed, axis=-1, keepdims=True)

    def second_norm(index, carry):
        at = pl.ds(pl.multiple_of(index * strip, strip), strip)
        x_rows = x_ref[at].astype(F32)
        value = d_h[at].astype(F32) + norm_strip(at, x_rows + mixed[at], gains[1:2], d_act[at], 1)
        d_res[at] = value
        d_mixed[at] = value.astype(BF16)
        inv_rms = lax.rsqrt(jnp.mean(x_rows * x_rows, axis=-1, keepdims=True) + EPSILON)
        act1[at] = (x_rows * inv_rms * gains[0:1]).astype(BF16)
        return carry

    lax.fori_loop(0, rows // strip, second_norm, 0)
    for index in range(5, 8):
        loads[index].wait()

    def to_z(index, carry):
        at = pl.ds(pl.multiple_of(index * tile, tile), tile)
        d_conv[:, at] = dot_right(d_mixed[...], w_out[at])
        return carry

    lax.fori_loop(0, width // tile, to_z, 0)
    part = 128
    row_at = lax.broadcasted_iota(jnp.int32, (rows, part), 0)

    def lanes_of(offset, index):
        return pl.ds(pl.multiple_of(offset * width + index * part, part), part)

    def convolve_back(index, carry):
        lanes = lanes_of(0, index)
        product = (projected[:, lanes] * projected[:, lanes_of(2, index)]).astype(BF16).astype(F32)
        before = rim[:, lanes].astype(F32)
        near, far = before[15:16], before[14:15]
        one = jnp.where(row_at >= 1, pltpu.roll(product, 1, 0), near)
        two = jnp.where(row_at >= 2, pltpu.roll(product, 2, 0), jnp.where(row_at == 1, near, far))
        d_z = d_conv[:, lanes]
        d_proj[:, lanes_of(1, index)] = (d_z * convolved[:, lanes]).astype(BF16)
        d_value = d_z * projected[:, lanes_of(1, index)]
        d_conv[:, lanes] = d_value
        for row, source in ((2, two), (3, one), (4, product)):
            small[row : row + 1, lanes] = jnp.sum(d_value * source, axis=0, keepdims=True)
        tap = taps[:, lanes]
        edge[0:1, lanes] = tap[0:1] * d_value[0:1]
        edge[1:2, lanes] = tap[0:1] * d_value[1:2] + tap[1:2] * d_value[0:1]
        return carry

    lax.fori_loop(0, width // part, convolve_back, 0)
    edge[2:8] = jnp.zeros((6, width), F32)
    to_last = along(edge, next_edge, edge_sem.at[0], edge_sem.at[1], chain.place - 1)

    @pl.when(chain.has_last)
    def _():
        to_last.start()

    weight_grad(z_low, d_mixed, slice(None), o_grad, stage, 2)

    @pl.when(chain.has_next)
    def _():
        along(edge, next_edge, edge_sem.at[0], edge_sem.at[1], chain.place).wait_recv()

    @pl.when(jnp.logical_not(chain.has_next))
    def _():
        next_edge[...] = jnp.zeros(next_edge.shape, F32)

    def products_back(index, carry):
        lanes = lanes_of(0, index)
        d_value = d_conv[:, lanes]
        tap = taps[:, lanes]
        after = next_edge[:, lanes]
        one = jnp.where(row_at < rows - 1, pltpu.roll(d_value, rows - 1, 0), 0.0)
        two = jnp.where(row_at < rows - 2, pltpu.roll(d_value, rows - 2, 0), 0.0)
        joined = tap[2:3] * d_value + tap[1:2] * one + tap[0:1] * two
        joined = joined + jnp.where(row_at == rows - 2, after[0:1], 0.0)
        joined = joined + jnp.where(row_at == rows - 1, after[1:2], 0.0)
        joined = joined.astype(BF16).astype(F32)
        d_proj[:, lanes] = (joined * projected[:, lanes_of(2, index)]).astype(BF16)
        d_proj[:, lanes_of(2, index)] = (joined * projected[:, lanes]).astype(BF16)
        return carry

    lax.fori_loop(0, width // part, products_back, 0)
    loads[8].wait()

    def to_act(index, carry):
        at = pl.ds(pl.multiple_of(index * tile, tile), tile)
        d_act[:, at] = dot_right(d_proj[...], w_in[at])
        return carry

    lax.fori_loop(0, width // tile, to_act, 0)
    for offset, target in enumerate((b_grad, c_grad, x_grad)):
        weight_grad(act1, d_proj, slice(offset * width, (offset + 1) * width), target, stage, 2)

    def first_norm(index, carry):
        at = pl.ds(pl.multiple_of(index * strip, strip), strip)
        value = d_res[at] + norm_strip(at, x_ref[at].astype(F32), gains[0:1], d_act[at], 0)
        d_x[at] = value.astype(BF16)
        return carry

    lax.fori_loop(0, rows // strip, first_norm, 0)
    for copy in (gather.first, gather.second, gather.third, gather.fourth):
        copy.wait_send()

    @pl.when(chain.has_last)
    def _():
        to_last.wait_send()


def conv_back(local, before, kept, collective_id):
    n_ctx = lax.axis_size("ctx")
    x_low = local[0]
    rows, width = x_low.shape
    wide = before[0].shape[1]
    assert wide % 384 == 0 and width % 512 == 0
    columns = pltpu.VMEM((4 * rows, wide), BF16)
    whole = pltpu.VMEM((4 * rows, width), BF16)
    dma = pltpu.SemaphoreType.DMA
    vmem = pl.BlockSpec(memory_space=pltpu.VMEM)
    hbm = pl.BlockSpec(memory_space=pl.ANY)
    pair = pltpu.VMEM((2, rows // 2, width), BF16)
    square = jax.ShapeDtypeStruct((width, width), BF16)
    column = jax.ShapeDtypeStruct((width, wide), BF16)
    return pl.pallas_call(
        functools.partial(back_kernel, n_ctx),
        out_shape=(
            column,
            column,
            jax.ShapeDtypeStruct((wide, width), BF16),
            square,
            square,
            square,
            square,
            square,
            square,
            square,
            jax.ShapeDtypeStruct((rows, width), BF16),
            jax.ShapeDtypeStruct((8, width), F32),
        ),
        in_specs=[vmem] * len(local) + [hbm] * (len(before) + len(kept)),
        out_specs=[hbm] * 10 + [vmem] * 2,
        scratch_shapes=[pltpu.VMEM(k.shape, k.dtype) for k in kept]
        + [
            dma((9,)),
            pltpu.VMEM((2, 2, rows, wide), F32),
            dma((2, 2)),
            whole,
            columns,
            columns,
            whole,
            dma((4,)),
            dma((4,)),
            dma,
            pltpu.VMEM((2, 256, wide), BF16),
            pltpu.VMEM((2, 256, width), BF16),
            dma((4,)),
            pair,
            pair,
            pair,
            pair,
            dma((6,)),
            dma((6,)),
            pltpu.VMEM((rows, width), F32),
            pltpu.VMEM((rows, width), F32),
            pltpu.VMEM((rows, width), BF16),
            pltpu.VMEM((rows, width), F32),
            pltpu.VMEM((rows, 3 * width), BF16),
            pltpu.VMEM((rows, width), BF16),
            pltpu.VMEM((8, width), F32),
            pltpu.VMEM((8, width), F32),
            dma((2,)),
        ],
        compiler_params=pltpu.CompilerParams(
            collective_id=collective_id, has_side_effects=True, vmem_limit_bytes=58 << 20
        ),
        cost_estimate=busy(55),
    )(*local, *before, *kept)


def forward_kernel(
    act,
    w_gate_in,
    w_up_in,
    w_down_in,
    total,
    gate_out,
    up_out,
    hidden_out,
    w_gate,
    w_up,
    w_down,
    load_sem,
    pre,
    pre_sem,
    hidden,
    keep_sem,
    blocks,
    beside_got,
    across_got,
    passed,
    passed_got,
    send_sem,
    recv_sem,
):
    me, beside, across, opposite = corners()
    loads = [
        pltpu.make_async_copy(src, dst, load_sem.at[index])
        for index, (src, dst) in enumerate(((w_gate_in, w_gate), (w_up_in, w_up), (w_down_in, w_down)))
    ]
    for copy in loads:
        copy.start()
    greet_sides()
    reduction = SideReduce(blocks, total, beside_got, across_got, passed, passed_got, send_sem, recv_sem)
    rows = total.shape[0]
    wide, width = w_down.shape
    lanes_wide, lanes_out = 384, 1024

    def at_rows(owner):
        return pl.ds(pl.multiple_of(owner * rows, rows), rows)

    def leaving(owner, slot):
        return [
            pltpu.make_async_copy(pre.at[slot, kind], out.at[at_rows(owner)], pre_sem.at[slot, kind])
            for kind, out in enumerate((gate_out, up_out))
        ]

    def turn(owner, slot, before):
        at = at_rows(owner)
        if before is not None:
            for copy in leaving(before, slot):
                copy.wait()

        def hidden_part(index, carry):
            lanes = pl.ds(pl.multiple_of(index * lanes_wide, 128), lanes_wide)
            gate_pre = dot_plain(act[at], w_gate[:, lanes])
            up_pre = dot_plain(act[at], w_up[:, lanes])
            pre[slot, 0, :, lanes] = gate_pre
            pre[slot, 1, :, lanes] = up_pre
            hidden[at, lanes] = (gate_pre * jax.nn.sigmoid(gate_pre) * up_pre).astype(BF16)
            return carry

        lax.fori_loop(0, wide // lanes_wide, hidden_part, 0)
        for copy in leaving(owner, slot):
            copy.start()

        def out_part(index, carry):
            lanes = pl.ds(pl.multiple_of(index * lanes_out, 128), lanes_out)
            blocks[at, lanes] = dot_plain(hidden[at], w_down[:, lanes]).astype(BF16)
            return carry

        lax.fori_loop(0, width // lanes_out, out_part, 0)

    for copy in loads:
        copy.wait()
    turn(opposite, 0, None)
    reduction.copies[0].start()
    reduction.copies[2].start()
    turn(beside, 1, None)
    reduction.copies[1].start()
    turn(across, 0, opposite)
    reduction.copies[3].start()
    reduction.relay()
    turn(me, 1, beside)
    keep = pltpu.make_async_copy(hidden, hidden_out, keep_sem)
    keep.start()
    reduction.finish()
    for copy in leaving(across, 0) + leaving(me, 1) + [keep]:
        copy.wait()


def ffn_forward(act, w_gate, w_up, w_down, collective_id):
    count = lax.axis_size("fsdp")
    rows, width = act.shape[0] // count, act.shape[1]
    wide = w_gate.shape[1]
    assert count == 4 and wide % 384 == 0 and width % 1024 == 0
    dma = pltpu.SemaphoreType.DMA
    vmem = pl.BlockSpec(memory_space=pltpu.VMEM)
    hbm = pl.BlockSpec(memory_space=pl.ANY)
    pair = pltpu.VMEM((2, rows // 2, width), BF16)
    column = jax.ShapeDtypeStruct((count * rows, wide), F32)
    return pl.pallas_call(
        forward_kernel,
        out_shape=(
            jax.ShapeDtypeStruct((rows, width), F32),
            column,
            column,
            jax.ShapeDtypeStruct((count * rows, wide), BF16),
        ),
        in_specs=[vmem] + [hbm] * 3,
        out_specs=[vmem] + [hbm] * 3,
        scratch_shapes=[pltpu.VMEM(w.shape, BF16) for w in (w_gate, w_up, w_down)]
        + [
            dma((3,)),
            pltpu.VMEM((2, 2, rows, wide), F32),
            dma((2, 2)),
            pltpu.VMEM((count * rows, wide), BF16),
            dma,
            pltpu.VMEM((count * rows, width), BF16),
            pair,
            pair,
            pair,
            pair,
            dma((6,)),
            dma((6,)),
        ],
        compiler_params=pltpu.CompilerParams(
            collective_id=collective_id, has_side_effects=True, vmem_limit_bytes=58 << 20
        ),
        cost_estimate=busy(25),
    )(act, w_gate, w_up, w_down)


def ffn_norm_back(d_act, residual, gain):
    normed, inv_rms = norm_rows(residual)
    return norm_back(d_act * gain, normed, inv_rms), jnp.sum(d_act * normed, axis=0)


def shards(
    inputs,
    cotangent,
    lengths,
    norm_gains,
    conv_in,
    conv_kernel,
    conv_out,
    attn_q,
    attn_k,
    attn_v,
    attn_out,
    head_gains,
    ffn_gate,
    ffn_up,
    ffn_down,
):
    micro, rows, width = inputs.shape
    section = lax.axis_index("section")
    group = lax.axis_index("fsdp")
    fsdp = lax.axis_size("fsdp")
    assert micro == lax.axis_size("section")
    head = head_gains.shape[1]
    q_width, kv_width = attn_q.shape[1], attn_k.shape[1]
    q_heads, kv_heads = q_width // head, kv_width // head
    positions = lax.axis_index("ctx") * rows + jnp.arange(rows)
    length = lax.dynamic_index_in_dim(lengths, group * micro + section, keepdims=False)
    mask = (positions < length).astype(F32)[:, None]

    def whole_rows(weight):
        share = weight.shape[0] // (micro * lax.axis_size("ctx"))
        start = (section * lax.axis_size("ctx") + lax.axis_index("ctx")) * share
        mine = lax.dynamic_slice_in_dim(weight, start, share, 0)
        return lax.all_gather(mine, ("fsdp", "section", "ctx"), axis=0, tiled=True)

    part = ffn_gate.shape[1]
    attn_full = whole_rows(jnp.concatenate([attn_q, attn_k, attn_v, attn_out], axis=1))
    query_full, key_full, value_full, proj_full = (
        attn_full[:, :q_width],
        attn_full[:, q_width : q_width + kv_width],
        attn_full[:, q_width + kv_width : q_width + 2 * kv_width],
        attn_full[:, q_width + 2 * kv_width :],
    )

    x_low = lax.dynamic_index_in_dim(inputs, section, keepdims=False)
    in_full, out_full, gate1, up1, down1, projected, convolved, z_low, mixed, rim, act_all1 = front(
        x_low, norm_gains, conv_kernel, conv_in, conv_out, ffn_gate[0], ffn_up[0], ffn_down[0], 2
    )
    x = x_low.astype(F32)
    res1 = x + mixed
    ffn1, gate_pre1, up_pre1, hidden1 = ffn_forward(act_all1, gate1, up1, down1, 1)
    h_low = (res1 + ffn1).astype(BF16)

    h = h_low.astype(F32)
    normed2, inv2 = norm_rows(h)
    act2 = (normed2 * norm_gains[2]).astype(BF16)
    q_normed, q_inv = norm_heads(matmul(act2, query_full), head)
    k_normed, k_inv = norm_heads(matmul(act2, key_full), head)
    q_gain = jnp.tile(head_gains[0], q_heads)
    k_gain = jnp.tile(head_gains[1], kv_heads)
    query = (q_normed * q_gain).astype(BF16)
    key = (k_normed * k_gain).astype(BF16)
    value = matmul(act2, value_full).astype(BF16)
    d_sum_low = (lax.dynamic_index_in_dim(cotangent, section, keepdims=False).astype(F32) * mask).astype(BF16)
    attended, log_total, kv_all, d_sum_all, gate2, up2, down2 = attend(
        length.reshape(1),
        query,
        jnp.concatenate([key, value], axis=1),
        d_sum_low,
        ffn_gate[0],
        ffn_up[0],
        ffn_down[0],
        3,
    )
    attended_low = attended.astype(BF16)
    attn_rows = matmul(attended_low, proj_full)
    res2 = h + attn_rows
    normed3, _ = norm_rows(res2)
    terms2, d_act3, shared_gu, shared_down = ffn_turn(
        (normed3 * norm_gains[3]).astype(BF16), gate2, up2, down2, d_sum_all, 8
    )

    d_sum = d_sum_low.astype(F32)
    d_ffn, gain3 = ffn_norm_back(d_act3, res2, norm_gains[3])
    d_res2 = d_sum + d_ffn
    d_attn = d_res2.astype(BF16)
    d_att = matmul_right(d_attn, proj_full).astype(BF16)
    delta = jnp.sum((d_att.astype(F32) * attended).reshape(rows, q_heads, head), axis=-1)
    d_query, d_kv, ffn2 = attend_back(
        length.reshape(1), query, kv_all, d_att, log_total, delta.T.reshape(q_heads, 1, rows), terms2, 4
    )
    result = (res2 + ffn2) * mask

    def square(values):
        return jnp.sum(mask * values * values, axis=0, keepdims=True)

    squares = [square(v) for v in (x, mixed, ffn1, h, attn_rows, res2, ffn2, result)]
    d_query, shared_gu = lax.optimization_barrier((d_query, shared_gu))
    second_gu = lax.psum(shared_gu.reshape(-1, shared_gu.shape[-1]), "ctx")
    d_qn = rounded(d_query)
    grad_qgain = jnp.sum(jnp.sum(d_qn * q_normed, axis=0).reshape(q_heads, head), axis=0)
    d_qpre = norm_heads_back(d_qn * q_gain, q_normed, q_inv, head).astype(BF16)
    d_kn = rounded(d_kv[:, :kv_width])
    grad_kgain = jnp.sum(jnp.sum(d_kn * k_normed, axis=0).reshape(kv_heads, head), axis=0)
    d_kpre = norm_heads_back(d_kn * k_gain, k_normed, k_inv, head).astype(BF16)
    d_vpre = d_kv[:, kv_width:].astype(BF16)
    d_act2 = (
        matmul_right(d_qpre, query_full)
        + matmul_right(d_kpre, key_full)
        + matmul_right(d_vpre, value_full)
    )
    gain2 = jnp.sum(d_act2 * normed2, axis=0)
    d_h_low = (d_res2 + norm_back(d_act2 * norm_gains[2], normed2, inv2)).astype(BF16)

    *grads, d_x, conv_small = conv_back(
        (
            x_low,
            mixed,
            d_h_low,
            norm_gains,
            conv_kernel,
            z_low,
            rim,
            act2,
            d_qpre,
            jnp.concatenate([d_kpre, d_vpre], axis=1),
            attended_low,
            d_attn,
        ),
        (gate_pre1, up_pre1),
        (down1, gate1, up1, act_all1, hidden1, in_full, out_full, projected, convolved),
        9,
    )

    half = ffn_gate.shape[1] // 2
    y_low = result.astype(BF16)
    is_first = section == 0
    other_end = swapped(jnp.where(is_first, y_low, d_x), "section")
    ends = jnp.where(is_first, jnp.stack([d_x, other_end]), jnp.stack([other_end, y_low]))[None]

    small = jnp.concatenate(
        [conv_small[:2], gain2[None], gain3[None], conv_small[2:5]]
        + [jnp.pad(grad[None], ((0, 0), (0, width - head))) for grad in (grad_qgain, grad_kgain)]
        + [jnp.zeros((7, width), F32)]
        + squares
        + [jnp.zeros((8, width), F32)]
    ).astype(BF16)
    small = small.reshape(2, 16, width)
    gu_sum, down_sum, rest_sum = summed_gradients(
        grads[:3],
        grads[3:],
        small,
        second_gu.reshape((-1,) + shared_gu.shape[1:]),
        shared_down,
    )
    rest_sum = rest_sum.astype(F32)

    def block(index):
        rows_at = slice(index * half, (index + 1) * half)
        return rest_sum[:, rows_at].reshape(2 * half, width)

    attn_blocks = [block(i) for i in range(3)]
    conv_blocks = [block(3 + i) for i in range(4)]
    small_sum = rest_sum[0, 7 * half : 7 * half + 9]
    cut = width // fsdp
    mine = lax.dynamic_slice_in_dim(small_sum[:7], group * cut, cut, 1)
    head_cut = head // fsdp
    heads = lax.dynamic_slice_in_dim(small_sum[7:9], group * head_cut, head_cut, 1)
    square_cut = len(squares) // fsdp
    square_sum = jnp.sum(
        lax.dynamic_slice_in_dim(rest_sum[1, 7 * half : 7 * half + 8], group * square_cut, square_cut, 0), axis=1
    )
    token_total = jnp.sum(lengths).astype(F32) * width
    rms = jnp.sqrt(square_sum / token_total)
    return (
        ends,
        mine[:3],
        mine[3],
        jnp.concatenate(conv_blocks[:3], axis=1),
        mine[4:7],
        conv_blocks[3],
        attn_blocks[0],
        attn_blocks[1][:, :kv_width],
        attn_blocks[1][:, kv_width:],
        attn_blocks[2],
        heads,
        gu_sum[0][None].astype(F32),
        gu_sum[1][None].astype(F32),
        down_sum[None].astype(F32),
        rms,
    )


def solution(mesh):
    return jax.shard_map(
        shards,
        mesh=mesh,
        in_specs=(
            P("fsdp", "ctx", None),
            P("fsdp", "ctx", None),
            P(),
            P(),
            P("fsdp", None),
            P(),
            P("fsdp", None),
            P("fsdp", None),
            P("fsdp", None),
            P("fsdp", None),
            P("fsdp", None),
            P(),
            P("section", "fsdp", None),
            P("section", "fsdp", None),
            P("section", "fsdp", None),
        ),
        out_specs=(
            P("section", "fsdp", "ctx", None),
            P(None, "fsdp"),
            P("fsdp"),
            P("fsdp", None),
            P(None, "fsdp"),
            P("fsdp", None),
            P("fsdp", None),
            P("fsdp", None),
            P("fsdp", None),
            P("fsdp", None),
            P(None, "fsdp"),
            P("section", "fsdp", None),
            P("section", "fsdp", None),
            P("section", "fsdp", None),
            P("fsdp"),
        ),
        check_vma=False,
    )
```
